32 devices in a mesh: dp: 4 (over y, core), row: 2 (over x), col: 4 (over z).
Axes of the slice: x: 2, y: 2, z: 4, core: 2. Of those that a mesh axis runs over, the one named last changes fastest.
Arguments:
- x_prompt: bfloat16 [4, 1024, 1536], P('dp', 'col', 'row'), may hold values from -6 to 6
- x_cont: bfloat16 [4, 8, 128, 1536], P('dp', 'col', None, 'row'), may hold values from -6 to 6
- teacher_prompt: bfloat16 [4, 1024, 1536], P('dp', 'col', 'row'), may hold values from -12 to 12
- teacher_cont: bfloat16 [4, 8, 128, 1536], P('dp', 'col', None, 'row'), may hold values from -12 to 12
- segment_ids: int32 [4, 1024], P('dp'), may hold values from 0 to 3, never falling along the last dimension, each value on 1 to 512 neighbouring positions
- offsets: int32 [4, 8], P('dp'), may hold values from 1 to 1024
- prompt_valid: int32 [4, 1024], P('dp', 'col'), may hold values from 0 to 1
- cont_valid: int32 [4, 8, 128], P('dp', 'col'), may hold values from 0 to 1, as said below
- first_gain: bfloat16 [1536], P('row'), may hold values from 0.5 to 1.5
- w_query: bfloat16 [1536, 1536], P('row', 'col'), may hold values from -0.15625 to 0.15625
- w_key: bfloat16 [1536, 1536], P('row', 'col'), may hold values from -0.15625 to 0.15625
- w_value: bfloat16 [1536, 1536], P('row', 'col'), may hold values from -0.15625 to 0.15625
- w_outgate: bfloat16 [1536, 1536], P('row', 'col'), may hold values from -0.15625 to 0.15625
- w_forget: bfloat16 [1536, 24], P('row', 'col'), may hold values from -0.15625 to 0.15625
- forget_bias: float32 [24], P('col'), may hold values from 2.5 to 7.5
- w_out: bfloat16 [1536, 1536], P('col', 'row'), may hold values from -1.75 to 1.75
- second_gain: bfloat16 [1536], P('row'), may hold values from 0.5 to 1.5
- w_gate: bfloat16 [1536, 4096], P('row', 'col'), may hold values from -0.15625 to 0.15625
- w_up: bfloat16 [1536, 4096], P('row', 'col'), may hold values from -0.15625 to 0.15625
- w_down: bfloat16 [4096, 1536], P('col', 'row'), may hold values from -0.09375 to 0.09375
Outputs:
- loss: float32 [], replicated
- grad_prompt: float32 [4, 1024, 1536], P('dp', 'col', 'row')
- grad_cont: float32 [4, 8, 128, 1536], P('dp', 'col', None, 'row')
- grad_first_gain: float32 [1536], P('row')
- grad_query: float32 [1536, 1536], P('row', 'col')
- grad_key: float32 [1536, 1536], P('row', 'col')
- grad_value: float32 [1536, 1536], P('row', 'col')
- grad_outgate: float32 [1536, 1536], P('row', 'col')
- grad_forget: float32 [1536, 24], P('row', 'col')
- grad_forget_bias: float32 [24], P('col')
- grad_out: float32 [1536, 1536], P('col', 'row')
- grad_second_gain: float32 [1536], P('row')
- grad_gate: float32 [1536, 4096], P('row', 'col')
- grad_up: float32 [1536, 4096], P('row', 'col')
- grad_down: float32 [4096, 1536], P('col', 'row')
The draws below stay inside these ranges and needn't reach their ends.
Inputs may be any that keep to these rules, and one draw needn't show every extreme that they name: `segment_ids`: within a group the document numbers never fall, each document has 1 to 512 positions. `cont_valid`: the first token of every continuation is valid.
All inputs are finite; a program needn't handle non-finite values.
Results may differ from the reference program's by a relative error of at most 0.024.
Values may be sent and summed in bfloat16 or wider, within the bound.
A program may use at most 256 MiB of HBM per device.

```python
import math
from functools import partial
import jax
import jax.numpy as jnp
import numpy as np
from jax import lax

D = 1536
HEADS = 24
HEAD_DIM = 64
FF = 4096
PROMPT = 1024
CONTS = 8
CLEN = 128
GROUPS = 4


def teacher_base(key, shape):
    feature = jnp.arange(D, dtype=jnp.float32) / D
    spread = 1.0 + 2.0 * feature
    base = jnp.clip(jax.random.normal(key, shape, jnp.float32), -4.0, 4.0)
    return base * spread


def draw_teacher_prompt(key, part):
    return teacher_base(jax.random.fold_in(key, 11), (GROUPS, PROMPT, D)).astype(jnp.bfloat16)


def draw_teacher_cont(key, part):
    return teacher_base(jax.random.fold_in(key, 12), (GROUPS, CONTS, CLEN, D)).astype(jnp.bfloat16)


def draw_prompt_valid(key, part):
    group_index = jnp.arange(GROUPS, dtype=jnp.int32)[:, None]
    position = jnp.arange(PROMPT, dtype=jnp.int32)[None, :]
    threshold = 250 + 350 * group_index // GROUPS + 350 * position // PROMPT
    drawn_rolls = jax.random.randint(jax.random.fold_in(key, 21), (GROUPS, PROMPT), 0, 1000)
    return (drawn_rolls < threshold).astype(jnp.int32)


def draw_cont_valid(key, part):
    group_index = jnp.arange(GROUPS, dtype=jnp.int32)[:, None, None]
    cont_index = jnp.arange(CONTS, dtype=jnp.int32)[None, :, None]
    cont_step = jnp.arange(CLEN, dtype=jnp.int32)[None, None, :]
    threshold = 250 + 350 * group_index // GROUPS + 350 * cont_index // CONTS
    drawn_rolls = jax.random.randint(jax.random.fold_in(key, 22), (GROUPS, CONTS, CLEN), 0, 1000)
    return jnp.where(cont_step == 0, 1, (drawn_rolls < threshold).astype(jnp.int32)).astype(jnp.int32)


def place_ends(array, key, least, high):
    longest = array.shape.index(max(array.shape))
    spots = []
    for shift in (0, 1):
        where = [jax.random.randint(jax.random.fold_in(key, axis), (), 0, length) for axis, length in enumerate(array.shape)]
        where[longest] = (where[longest] + shift) % array.shape[longest]
        spots.append(tuple(where))
    return array.at[spots[0]].set(least).at[spots[1]].set(high)


def block_scale(own_key, extent, cuts, smallest, top_value):
    def one(dim, shards_of):
        steps = jax.random.uniform(jax.random.fold_in(jax.random.fold_in(own_key, 6), dim), (shards_of,), jnp.float32, smallest / len(cuts), top_value / len(cuts))
        return jnp.repeat(jnp.exp(steps), extent[dim] // shards_of).reshape((-1,) + (1,) * (len(extent) - dim - 1))

    gain = one(*cuts[0])
    for cut in cuts[1:]:
        gain = gain * one(*cut)
    return gain


def split_up(number_of, total, reach, lean):
    loads = [(1 << 20) // math.isqrt(rank ** lean) + 1 for rank in range(2, number_of + 1)]
    surplus, holding = total - reach - (number_of - 1), [1] * (number_of - 1)
    while surplus > 0:
        candidates = [i for i in range(number_of - 1) if holding[i] < reach]
        pool, budget = sum([loads[i] for i in candidates]), surplus
        for i in candidates:
            extra = min(reach - holding[i], max(1, budget * loads[i] // pool), surplus)
            holding[i] = holding[i] + extra
            surplus = surplus - extra
    return np.array([reach] + holding)


def ragged_sizes(own_key, number_of, total, limit, slope):
    if number_of == 2:
        one = jax.random.randint(own_key, (), max(1, total - limit), min(limit, total - 1) + 1)
        return jnp.stack([one, total - one])
    lengths = jnp.asarray(split_up(number_of, total, limit, slope), jnp.int32)
    twos = (number_of - 1) // 2
    source_of, sink = lengths[1:1 + 2 * twos:2], lengths[2:2 + 2 * twos:2]
    slack = jnp.minimum(source_of - 1, limit - sink)
    moved = jax.random.randint(jax.random.fold_in(own_key, 1), (twos,), 0, 1 << 20) % (slack + 1)
    lengths = lengths.at[1:1 + 2 * twos:2].set(source_of - moved).at[2:2 + 2 * twos:2].set(sink + moved)
    return lengths[jax.random.permutation(jax.random.fold_in(own_key, 2), number_of)]


def noise(key, shape, deviation, limit, split=(), kind=jnp.bfloat16):
    values = deviation * jax.random.normal(key, shape, jnp.float32)
    if split:
        values = values * block_scale(key, shape, split, -0.22, 0.18)
    return jnp.clip(values, -limit, limit).astype(kind)


def setup_inputs(seed: int = 0) -> dict:
    seeds = jax.random.split(jax.random.key(seed), 21)
    x_prompt = noise(seeds[0], (GROUPS, PROMPT, D), 1.0, 6.0, ((0, 4), (1, 4), (2, 2)))
    x_cont = noise(seeds[1], (GROUPS, CONTS, CLEN, D), 1.0, 6.0, ((0, 4), (1, 4), (3, 2)))
    teacher_prompt = draw_teacher_prompt(jax.random.fold_in(seeds[20], 71), 0)
    teacher_cont = draw_teacher_cont(jax.random.fold_in(seeds[20], 71), 0)
    segment_ids = jax.vmap(lambda own: jnp.searchsorted(jnp.cumsum(ragged_sizes(own, 4, PROMPT, PROMPT // 2, 0)), jnp.arange(PROMPT), side="right"))(jax.random.split(seeds[4], GROUPS)).reshape((GROUPS, PROMPT)).astype(jnp.int32)
    offsets = place_ends(jax.random.randint(seeds[5], (GROUPS, CONTS), 1, PROMPT + 1), jax.random.fold_in(seeds[5], 1), 1, PROMPT).astype(jnp.int32)
    prompt_valid = draw_prompt_valid(jax.random.fold_in(seeds[20], 71), 0)
    cont_valid = draw_cont_valid(jax.random.fold_in(seeds[20], 71), 0)
    first_gain = jnp.clip(1.0 + 0.1 * jax.random.normal(seeds[8], (D,), jnp.float32), 0.5, 1.5).astype(jnp.bfloat16)
    w_query = noise(seeds[9], (D, D), D ** -0.5, 0.15625, ((0, 2), (1, 4)))
    w_key = noise(seeds[10], (D, D), D ** -0.5, 0.15625, ((0, 2), (1, 4)))
    w_value = noise(seeds[11], (D, D), D ** -0.5, 0.15625, ((0, 2), (1, 4)))
    w_outgate = noise(seeds[12], (D, D), D ** -0.5, 0.15625, ((0, 2), (1, 4)))
    w_forget = noise(seeds[13], (D, HEADS), D ** -0.5, 0.15625, ((0, 2), (1, 4)))
    forget_bias = jnp.clip(2.5 + 5.0 * jax.random.uniform(seeds[14], (HEADS,), jnp.float32) ** block_scale(seeds[14], (HEADS,), ((0, 4),), -0.2, 0.2), 2.5, 7.5)
    w_out = noise(seeds[15], (D, D), (max(D // 128, 4)) ** -0.5, 1.75, ((0, 4), (1, 2)))
    second_gain = jnp.clip(1.0 + 0.1 * jax.random.normal(seeds[16], (D,), jnp.float32), 0.5, 1.5).astype(jnp.bfloat16)
    w_gate = noise(seeds[17], (D, FF), D ** -0.5, 0.15625, ((0, 2), (1, 4)))
    w_up = noise(seeds[18], (D, FF), D ** -0.5, 0.15625, ((0, 2), (1, 4)))
    w_down = noise(seeds[19], (FF, D), FF ** -0.5, 0.09375, ((0, 4), (1, 2)))
    return {"x_prompt": x_prompt, "x_cont": x_cont, "teacher_prompt": teacher_prompt, "teacher_cont": teacher_cont, "segment_ids": segment_ids, "offsets": offsets, "prompt_valid": prompt_valid, "cont_valid": cont_valid, "first_gain": first_gain, "w_query": w_query, "w_key": w_key, "w_value": w_value, "w_outgate": w_outgate, "w_forget": w_forget, "forget_bias": forget_bias, "w_out": w_out, "second_gain": second_gain, "w_gate": w_gate, "w_up": w_up, "w_down": w_down}


@jax.custom_vjp
def low(v):
    return lax.optimization_barrier(v.astype(jnp.bfloat16)).astype(jnp.float32)

@jax.custom_vjp
def low_back(v):
    return v

def low_keep(v):
    return (low(v), None)

def low_pass(kept, grad):
    return (grad,)

def back_keep(v):
    return (v, None)

def back_low(kept, grad):
    return (low(grad),)
low.defvjp(low_keep, low_pass)
low_back.defvjp(back_keep, back_low)
epsilon = 1e-06
highest = lax.Precision.HIGHEST
masked = -1e+30

def product(left_op, right_op):
    return jnp.dot(left_op, right_op, precision=highest)

def normalize(inputs, gain_vec):
    return inputs * lax.rsqrt(lax.optimization_barrier(jnp.mean(inputs * inputs, axis=-1, keepdims=True)) + epsilon) * gain_vec

def attend_head(segment_row, offset_row, pieces):
    query_prompt, key_prompt, value_prompt, cum_prompt, query_cont, key_cont, value_cont, cum_cont = pieces
    score_scale = HEAD_DIM ** (-0.5)
    position = jnp.arange(PROMPT, dtype=jnp.int32)
    same_doc = segment_row[None, :] == segment_row[:, None]
    allowed = (position[None, :] <= position[:, None]) & same_doc
    scores = low_back(product(query_prompt, key_prompt.T) * score_scale + cum_prompt[:, None] - cum_prompt[None, :])
    attn_probs = low(jax.nn.softmax(jnp.where(allowed, scores, masked), axis=-1))
    out_prompt = product(attn_probs, value_prompt)
    last_doc = segment_row[offset_row - 1]
    far_ok = (position[None, :] < offset_row[:, None]) & (segment_row[None, :] == last_doc[:, None])
    cont_step = jnp.arange(CLEN, dtype=jnp.int32)
    near_ok = cont_step[None, :] <= cont_step[:, None]
    far_scores = jnp.einsum('jqd,kd->jqk', query_cont, key_prompt, precision=highest) * score_scale + cum_cont[:, :, None] - cum_prompt[None, None, :]
    near_scores = jnp.einsum('jqd,jkd->jqk', query_cont, key_cont, precision=highest) * score_scale + cum_cont[:, :, None] - cum_cont[:, None, :]
    joined = low_back(jnp.concatenate([far_scores, near_scores], axis=-1))
    allowed_cont = jnp.concatenate([jnp.broadcast_to(far_ok[:, None, :], far_scores.shape), jnp.broadcast_to(near_ok[None], near_scores.shape)], axis=-1)
    probs_cont = low(jax.nn.softmax(jnp.where(allowed_cont, joined, masked), axis=-1))
    out_cont = jnp.einsum('jqk,kd->jqd', probs_cont[..., :PROMPT], value_prompt, precision=highest) + jnp.einsum('jqk,jkd->jqd', probs_cont[..., PROMPT:], value_cont, precision=highest)
    return (out_prompt, out_cont)

def group_error(weights, prompt_rows, cont_rows, teacher, validity, segment_row, offset_row):
    gain_one, w_query, w_key, w_value, w_outgate, w_forget, forget_bias, w_out, gain_two, w_gate, w_up, w_down = weights
    tokens = jnp.concatenate([prompt_rows, cont_rows.reshape(CONTS * CLEN, D)], axis=0)
    normed = low(normalize(tokens, gain_one))
    query_rows = low_back(low(product(normed, w_query)))
    key_rows = low_back(low(product(normed, w_key)))
    value_rows = low_back(low(product(normed, w_value)))
    gate_logit = low_back(product(normed, w_outgate))
    forget_lin = low_back(low(product(normed, w_forget)))
    log_keep = jax.nn.log_sigmoid(forget_lin + forget_bias)
    cum_prompt = jnp.cumsum(log_keep[:PROMPT], axis=0)
    cum_cont = cum_prompt[offset_row - 1][:, None, :] + jnp.cumsum(log_keep[PROMPT:].reshape(CONTS, CLEN, HEADS), axis=1)

    def split_prompt(matrix):
        return matrix[:PROMPT].reshape(PROMPT, HEADS, HEAD_DIM).transpose(1, 0, 2)

    def split_cont(matrix):
        return matrix[PROMPT:].reshape(CONTS, CLEN, HEADS, HEAD_DIM).transpose(2, 0, 1, 3)
    pieces = (split_prompt(query_rows), split_prompt(key_rows), split_prompt(value_rows), cum_prompt.T, split_cont(query_rows), split_cont(key_rows), split_cont(value_rows), cum_cont.transpose(2, 0, 1))
    out_prompt, out_cont = lax.map(jax.checkpoint(partial(attend_head, segment_row, offset_row)), pieces)
    attended = jnp.concatenate([out_prompt.transpose(1, 0, 2).reshape(PROMPT, D), out_cont.transpose(1, 2, 0, 3).reshape(CONTS * CLEN, D)], axis=0)
    attended = low_back(attended)
    gated = low(attended * jax.nn.sigmoid(gate_logit))
    residual = tokens + low_back(product(gated, w_out))
    normed_two = low(normalize(residual, gain_two))
    gate_rows = low_back(product(normed_two, w_gate))
    up_rows = low_back(product(normed_two, w_up))
    hidden = low(jax.nn.silu(gate_rows) * up_rows)
    result_rows = residual + low_back(product(hidden, w_down))
    return 0.5 * jnp.sum(validity[:, None] * (result_rows - teacher) ** 2)

def reference(x_prompt, x_cont, teacher_prompt, teacher_cont, segment_ids, offsets, prompt_valid, cont_valid, first_gain, w_query, w_key, w_value, w_outgate, w_forget, forget_bias, w_out, second_gain, w_gate, w_up, w_down):
    weights = tuple((weight_in.astype(jnp.float32) for weight_in in (first_gain, w_query, w_key, w_value, w_outgate, w_forget, forget_bias, w_out, second_gain, w_gate, w_up, w_down)))
    valid_count = jnp.sum(prompt_valid.astype(jnp.float32)) + jnp.sum(cont_valid.astype(jnp.float32))

    def one_group(carried, group_data):
        totals, error_sum = carried
        prompt_in, cont_in, teach_prompt, teach_cont, segment_row, offset_row, valid_prompt, valid_cont = group_data
        teacher = jnp.concatenate([teach_prompt.astype(jnp.float32), teach_cont.reshape(CONTS * CLEN, D).astype(jnp.float32)], axis=0)
        validity = jnp.concatenate([valid_prompt.astype(jnp.float32), valid_cont.reshape(CONTS * CLEN).astype(jnp.float32)], axis=0)

        def error_of(weight_set, prompt_rows, cont_rows):
            return group_error(weight_set, prompt_rows, cont_rows, teacher, validity, segment_row, offset_row)
        group_err, pullback = jax.vjp(error_of, weights, prompt_in.astype(jnp.float32), cont_in.astype(jnp.float32))
        group_grads, grad_prompt_one, grad_cont_one = pullback(jnp.ones((), jnp.float32))
        totals = jax.tree.map(jnp.add, totals, group_grads)
        return ((totals, error_sum + group_err), (grad_prompt_one, grad_cont_one))
    zero_grads = tuple((jnp.zeros_like(weight_in) for weight_in in weights))
    (totals, error_sum), (grad_prompt, grad_cont) = lax.scan(one_group, (zero_grads, jnp.zeros((), jnp.float32)), (x_prompt, x_cont, teacher_prompt, teacher_cont, segment_ids, offsets, prompt_valid, cont_valid))
    grad_scale = GROUPS * (PROMPT + CONTS * CLEN) / valid_count
    loss_value = error_sum / (D * valid_count)
    return (loss_value, grad_prompt * grad_scale, grad_cont * grad_scale, totals[0] * grad_scale, totals[1] * grad_scale, totals[2] * grad_scale, totals[3] * grad_scale, totals[4] * grad_scale, totals[5] * grad_scale, totals[6] * grad_scale, totals[7] * grad_scale, totals[8] * grad_scale, totals[9] * grad_scale, totals[10] * grad_scale, totals[11] * grad_scale)
```

```python
import functools
import itertools

import jax
import jax.numpy as jnp
from jax import lax
from jax.experimental import pallas as pl
from jax.experimental.pallas import tpu as pltpu
from jax.sharding import Mesh, PartitionSpec as P

D = 1536
HEADS = 24
HEAD_DIM = 64
PROMPT = 1024
CONTS = 8
CLEN = 128


epsilon = 1e-06
highest = lax.Precision.HIGHEST
masked = -1e30


def matmul(left_op, right_op):
    return jnp.dot(left_op, right_op, preferred_element_type=jnp.float32)


def by_transpose(left_op, right_op):
    return lax.dot_general(
        left_op, right_op, (((1,), (1,)), ((), ())), preferred_element_type=jnp.float32
    )


def inner_rows(left_op, right_op):
    return lax.dot_general(
        left_op, right_op, (((0,), (0,)), ((), ())), preferred_element_type=jnp.float32
    )


def feature_total(partial_sum):
    return lax.psum(partial_sum, "row")


def group_rows(local_rows):
    return lax.all_gather(local_rows, "col", axis=0, tiled=True)


def token_sums(partial_rows):
    return lax.psum_scatter(
        partial_rows.astype(jnp.bfloat16), "col", scatter_dimension=0, tiled=True
    ).astype(jnp.float32)


def row_partials(partial_rows, col_count, blocks, quarter):
    shaped = partial_rows.reshape(
        col_count, blocks, lax.axis_size("row"), quarter, partial_rows.shape[-1]
    )
    return lax.psum_scatter(
        shaped.astype(jnp.bfloat16), "row", scatter_dimension=2, tiled=True
    ).astype(jnp.float32)


def head_rows(own_rows):
    gathered = lax.all_gather(own_rows, "row", axis=2, tiled=True)
    return gathered.reshape(-1, gathered.shape[-1])


def norm_forward(tokens, gain_vec):
    row_total = feature_total(jnp.sum(tokens * tokens, axis=-1))
    factor = lax.rsqrt(row_total / D + epsilon)
    scaled = tokens * factor[:, None]
    return (factor, scaled, (scaled * gain_vec).astype(jnp.bfloat16))


def norm_backward(grad_normed, factor, scaled, gain_vec):
    grad_scaled = grad_normed * gain_vec
    row_total = feature_total(jnp.sum(grad_scaled * scaled, axis=-1))
    gain_grad = jnp.sum(grad_normed * scaled, axis=0)
    return (gain_grad, factor[:, None] * (grad_scaled - scaled * (row_total / D)[:, None]))


def log_total(scores):
    row_top = jnp.max(scores, axis=-1, keepdims=True)
    return row_top + jnp.log(jnp.sum(jnp.exp(scores - row_top), axis=-1, keepdims=True))


def prompt_scores(queries, key_rows, cum_query, cum_key, allowed):
    raw_scores = jnp.einsum("qhd,khd->hqk", queries, key_rows, preferred_element_type=jnp.float32)
    raw_scores = raw_scores * HEAD_DIM ** (-0.5) + cum_query.T[:, :, None] - cum_key.T[:, None, :]
    return jnp.where(allowed[None], raw_scores, masked)


def cont_scores(queries, key_rows, key_cont, cum_query, cum_key, cum_cont, far_ok, near_ok):
    score_scale = HEAD_DIM ** (-0.5)
    query_cum = cum_query.transpose(0, 2, 1)[:, :, :, None]
    far_scores = jnp.einsum("jqhd,khd->jhqk", queries, key_rows, preferred_element_type=jnp.float32)
    far_scores = far_scores * score_scale + query_cum - cum_key.T[None, :, None, :]
    near_scores = jnp.einsum(
        "jqhd,jkhd->jhqk", queries, key_cont, preferred_element_type=jnp.float32
    )
    near_scores = near_scores * score_scale + query_cum - cum_cont.transpose(0, 2, 1)[:, :, None, :]
    far_scores = jnp.where(far_ok[:, None, None, :], far_scores, masked)
    near_scores = jnp.where(near_ok[None, None], near_scores, masked)
    return jnp.concatenate([far_scores, near_scores], axis=-1)


def wide_body(
    x_prompt,
    x_cont,
    teacher_prompt,
    teacher_cont,
    segment_ids,
    offsets,
    prompt_valid,
    cont_valid,
    first_gain,
    w_query,
    w_key,
    w_value,
    w_outgate,
    w_forget,
    forget_bias,
    w_out,
    second_gain,
    w_gate,
    w_up,
    w_down,
):
    row_count = lax.axis_size("row")
    col_count = lax.axis_size("col")
    row_index = lax.axis_index("row")
    local_prompt = x_prompt.shape[1]
    local_conts = x_cont.shape[1]
    quarter = CLEN // row_count
    local_tokens = local_prompt + local_conts * CLEN
    blocks = local_tokens // CLEN
    prompt_blocks = local_prompt // CLEN
    heads_here = w_forget.shape[1]
    width_here = heads_here * HEAD_DIM
    units_here = w_gate.shape[1]
    score_scale = HEAD_DIM ** (-0.5)
    w_project = jnp.concatenate([w_query, w_key, w_value, w_outgate], axis=1)
    w_hidden = jnp.concatenate([w_gate, w_up], axis=1)
    gain_one = first_gain.astype(jnp.float32)
    gain_two = second_gain.astype(jnp.float32)
    position = jnp.arange(PROMPT, dtype=jnp.int32)
    cont_step = jnp.arange(CLEN, dtype=jnp.int32)
    own_step = row_index * quarter + jnp.arange(quarter, dtype=jnp.int32)
    near_ok = cont_step[None, :] <= own_step[:, None]
    own_position = lax.dynamic_index_in_dim(
        position.reshape(col_count, prompt_blocks, row_count, quarter), row_index, 2, keepdims=False
    ).reshape(-1)

    def own_prompt_part(matrix):
        return matrix[:, :prompt_blocks, 0]

    def one_group(carried, group_data):
        (
            acc_project,
            acc_forget,
            acc_bias,
            acc_out,
            acc_hidden,
            acc_down,
            acc_gain_one,
            acc_gain_two,
            error_sum,
            count_sum,
        ) = carried
        (
            prompt_in,
            cont_in,
            teach_prompt,
            teach_cont,
            segment_row,
            offset_row,
            valid_prompt,
            valid_cont,
        ) = group_data
        tokens = jnp.concatenate(
            [prompt_in, cont_in.reshape(local_conts * CLEN, -1)], axis=0
        ).astype(jnp.float32)
        teacher = jnp.concatenate(
            [teach_prompt, teach_cont.reshape(local_conts * CLEN, -1)], axis=0
        ).astype(jnp.float32)
        validity = jnp.concatenate([valid_prompt, valid_cont.reshape(-1)], axis=0).astype(
            jnp.float32
        )
        branch_mask = position[None, :] == offset_row[:, None] - 1
        branch_hot = branch_mask.astype(jnp.float32)
        last_doc = jnp.sum(jnp.where(branch_mask, segment_row[None, :], 0), axis=1)
        far_ok = (position[None, :] < offset_row[:, None]) & (
            segment_row[None, :] == last_doc[:, None]
        )
        own_doc = lax.dynamic_index_in_dim(
            segment_row.reshape(col_count, prompt_blocks, row_count, quarter),
            row_index,
            2,
            keepdims=False,
        ).reshape(-1)
        prompt_ok = (position[None, :] <= own_position[:, None]) & (
            segment_row[None, :] == own_doc[:, None]
        )
        factor_one, scaled_one, normed_one = norm_forward(tokens, gain_one)
        normed_all = group_rows(normed_one)
        project_part = matmul(normed_all, w_project).reshape(
            col_count, blocks, row_count, quarter, 4 * width_here
        )
        forget_part = matmul(normed_all, w_forget).reshape(
            col_count, blocks, row_count, quarter, heads_here
        )
        own_project, own_forget = (
            lax.psum_scatter(project_part, "row", scatter_dimension=2, tiled=True),
            lax.psum_scatter(forget_part, "row", scatter_dimension=2, tiled=True),
        )
        own_query = own_project[..., :width_here].astype(jnp.bfloat16)
        own_kv = own_project[..., width_here : 3 * width_here].astype(jnp.bfloat16)
        gate_logit = own_project[..., 3 * width_here :]
        kv_all, forget_all = (
            lax.all_gather(own_kv, "row", axis=2, tiled=True),
            lax.all_gather(own_forget.astype(jnp.bfloat16), "row", axis=2, tiled=True),
        )
        kv_all = kv_all.reshape(col_count, local_tokens, 2 * width_here)
        pre_gate = (
            forget_all.reshape(col_count, local_tokens, heads_here).astype(jnp.float32)
            + forget_bias
        )
        log_keep = jax.nn.log_sigmoid(pre_gate)
        cum_prompt = jnp.cumsum(log_keep[:, :local_prompt].reshape(PROMPT, heads_here), axis=0)
        branch_cum = jnp.dot(branch_hot, cum_prompt, precision=highest)
        cum_cont = branch_cum[:, None, :] + jnp.cumsum(
            log_keep[:, local_prompt:].reshape(CONTS, CLEN, heads_here), axis=1
        )
        kv_prompt = kv_all[:, :local_prompt].reshape(PROMPT, 2, heads_here, HEAD_DIM)
        key_prompt = kv_prompt[:, 0]
        value_prompt = kv_prompt[:, 1]
        kv_cont = kv_all[:, local_prompt:].reshape(CONTS, CLEN, 2, heads_here, HEAD_DIM)
        key_cont = kv_cont[:, :, 0]
        value_cont = kv_cont[:, :, 1]
        cum_query_prompt = lax.dynamic_index_in_dim(
            cum_prompt.reshape(col_count, prompt_blocks, row_count, quarter, heads_here),
            row_index,
            2,
            keepdims=False,
        ).reshape(-1, heads_here)
        cum_query_cont = lax.dynamic_index_in_dim(
            cum_cont.reshape(CONTS, row_count, quarter, heads_here), row_index, 1, keepdims=False
        )
        query_prompt = own_prompt_part(own_query).reshape(-1, heads_here, HEAD_DIM)
        query_cont = own_query[:, prompt_blocks:, 0].reshape(CONTS, quarter, heads_here, HEAD_DIM)
        scores_prompt = prompt_scores(
            query_prompt, key_prompt, cum_query_prompt, cum_prompt, prompt_ok
        )
        total_prompt = log_total(scores_prompt)
        probs_prompt = jnp.exp(scores_prompt - total_prompt).astype(jnp.bfloat16)
        out_prompt = jnp.einsum(
            "hqk,khd->qhd", probs_prompt, value_prompt, preferred_element_type=jnp.float32
        )
        scores_cont = cont_scores(
            query_cont, key_prompt, key_cont, cum_query_cont, cum_prompt, cum_cont, far_ok, near_ok
        )
        total_cont = log_total(scores_cont)
        probs_cont = jnp.exp(scores_cont - total_cont).astype(jnp.bfloat16)
        out_cont = jnp.einsum(
            "jhqk,khd->jqhd",
            probs_cont[..., :PROMPT],
            value_prompt,
            preferred_element_type=jnp.float32,
        )
        out_cont = out_cont + jnp.einsum(
            "jhqk,jkhd->jqhd",
            probs_cont[..., PROMPT:],
            value_cont,
            preferred_element_type=jnp.float32,
        )
        attended = jnp.concatenate(
            [
                out_prompt.reshape(col_count, prompt_blocks, 1, quarter, width_here),
                out_cont.reshape(col_count, local_conts, 1, quarter, width_here),
            ],
            axis=1,
        )
        gate_sig = jax.nn.sigmoid(gate_logit)
        gated = (attended * gate_sig).astype(jnp.bfloat16)
        gated_all = head_rows(gated)
        residual = tokens + token_sums(matmul(gated_all, w_out))
        factor_two, scaled_two, normed_two = norm_forward(residual, gain_two)
        normed_two_all = group_rows(normed_two)
        hidden_own = row_partials(matmul(normed_two_all, w_hidden), col_count, blocks, quarter)
        gate_rows = hidden_own[..., :units_here]
        up_rows = hidden_own[..., units_here:]
        gate_sig_two = jax.nn.sigmoid(gate_rows)
        silu_rows = gate_rows * gate_sig_two
        hidden_all = head_rows((silu_rows * up_rows).astype(jnp.bfloat16))
        result_rows = residual + token_sums(matmul(hidden_all, w_down))
        deviation = result_rows - teacher
        group_err = 0.5 * jnp.sum(validity[:, None] * deviation * deviation)
        grad_result = validity[:, None] * deviation
        grad_result_all = group_rows(grad_result.astype(jnp.bfloat16))
        grad_down_w = inner_rows(hidden_all, grad_result_all)
        grad_hid = row_partials(by_transpose(grad_result_all, w_down), col_count, blocks, quarter)
        grad_gate = grad_hid * up_rows * gate_sig_two * (1.0 + gate_rows * (1.0 - gate_sig_two))
        grad_up = grad_hid * silu_rows
        grad_hidden_all = head_rows(
            jnp.concatenate([grad_gate, grad_up], axis=-1).astype(jnp.bfloat16)
        )
        grad_hidden_w = inner_rows(normed_two_all, grad_hidden_all)
        grad_normed_two = token_sums(by_transpose(grad_hidden_all, w_hidden))
        gain_two_grad, grad_residual = norm_backward(
            grad_normed_two, factor_two, scaled_two, gain_two
        )
        grad_residual = grad_residual + grad_result
        grad_residual_all = group_rows(grad_residual.astype(jnp.bfloat16))
        grad_out_w = inner_rows(gated_all, grad_residual_all)
        grad_gated = row_partials(
            by_transpose(grad_residual_all, w_out), col_count, blocks, quarter
        )
        grad_attended = (grad_gated * gate_sig).astype(jnp.bfloat16)
        grad_logit = (grad_gated * attended * gate_sig * (1.0 - gate_sig)).astype(jnp.bfloat16)
        grad_att_prompt = own_prompt_part(grad_attended).reshape(-1, heads_here, HEAD_DIM)
        grad_att_cont = grad_attended[:, prompt_blocks:, 0].reshape(
            CONTS, quarter, heads_here, HEAD_DIM
        )
        again_prompt = jnp.exp(
            prompt_scores(query_prompt, key_prompt, cum_query_prompt, cum_prompt, prompt_ok)
            - total_prompt
        )
        grad_prob_prompt = jnp.einsum(
            "qhd,khd->hqk", grad_att_prompt, value_prompt, preferred_element_type=jnp.float32
        )
        grad_score_prompt = (
            again_prompt
            * (grad_prob_prompt - jnp.sum(again_prompt * grad_prob_prompt, axis=-1, keepdims=True))
        ).astype(jnp.bfloat16)
        again_prompt_b = again_prompt.astype(jnp.bfloat16)
        grad_query_prompt = (
            jnp.einsum(
                "hqk,khd->qhd", grad_score_prompt, key_prompt, preferred_element_type=jnp.float32
            )
            * score_scale
        )
        grad_key_prompt = (
            jnp.einsum(
                "hqk,qhd->khd", grad_score_prompt, query_prompt, preferred_element_type=jnp.float32
            )
            * score_scale
        )
        grad_value_prompt = jnp.einsum(
            "hqk,qhd->khd", again_prompt_b, grad_att_prompt, preferred_element_type=jnp.float32
        )
        cum_grad_query_p = jnp.sum(grad_score_prompt, axis=-1, dtype=jnp.float32).T
        cum_grad_key_p = -jnp.sum(grad_score_prompt, axis=1, dtype=jnp.float32).T
        again_cont = jnp.exp(
            cont_scores(
                query_cont,
                key_prompt,
                key_cont,
                cum_query_cont,
                cum_prompt,
                cum_cont,
                far_ok,
                near_ok,
            )
            - total_cont
        )
        grad_prob_cont = jnp.concatenate(
            [
                jnp.einsum(
                    "jqhd,khd->jhqk",
                    grad_att_cont,
                    value_prompt,
                    preferred_element_type=jnp.float32,
                ),
                jnp.einsum(
                    "jqhd,jkhd->jhqk", grad_att_cont, value_cont, preferred_element_type=jnp.float32
                ),
            ],
            axis=-1,
        )
        grad_score_cont = (
            again_cont
            * (grad_prob_cont - jnp.sum(again_cont * grad_prob_cont, axis=-1, keepdims=True))
        ).astype(jnp.bfloat16)
        again_cont_b = again_cont.astype(jnp.bfloat16)
        far_grad = grad_score_cont[..., :PROMPT]
        near_grad = grad_score_cont[..., PROMPT:]
        grad_query_cont = (
            jnp.einsum("jhqk,khd->jqhd", far_grad, key_prompt, preferred_element_type=jnp.float32)
            + jnp.einsum("jhqk,jkhd->jqhd", near_grad, key_cont, preferred_element_type=jnp.float32)
        ) * score_scale
        grad_key_far = (
            jnp.einsum("jhqk,jqhd->khd", far_grad, query_cont, preferred_element_type=jnp.float32)
            * score_scale
        )
        grad_key_near = (
            jnp.einsum("jhqk,jqhd->jkhd", near_grad, query_cont, preferred_element_type=jnp.float32)
            * score_scale
        )
        grad_value_far = jnp.einsum(
            "jhqk,jqhd->khd",
            again_cont_b[..., :PROMPT],
            grad_att_cont,
            preferred_element_type=jnp.float32,
        )
        grad_value_near = jnp.einsum(
            "jhqk,jqhd->jkhd",
            again_cont_b[..., PROMPT:],
            grad_att_cont,
            preferred_element_type=jnp.float32,
        )
        cum_grad_query_c = jnp.sum(grad_score_cont, axis=-1, dtype=jnp.float32).transpose(0, 2, 1)
        cum_grad_key_far = -jnp.sum(far_grad, axis=(0, 2), dtype=jnp.float32).T
        cum_grad_key_near = -jnp.sum(near_grad, axis=2, dtype=jnp.float32).transpose(0, 2, 1)
        kv_grad_prompt = jnp.stack(
            [grad_key_prompt + grad_key_far, grad_value_prompt + grad_value_far], axis=1
        ).reshape(col_count, local_prompt, 2 * width_here)
        kv_grad_cont = jnp.stack([grad_key_near, grad_value_near], axis=2).reshape(
            col_count, local_conts * CLEN, 2 * width_here
        )
        kv_grad_part = jnp.concatenate([kv_grad_prompt, kv_grad_cont], axis=1)
        query_place = lax.dynamic_update_slice_in_dim(
            jnp.zeros((col_count, prompt_blocks, row_count, quarter, heads_here), jnp.float32),
            cum_grad_query_p.reshape(col_count, prompt_blocks, 1, quarter, heads_here),
            row_index,
            axis=2,
        ).reshape(PROMPT, heads_here)
        cont_place = lax.dynamic_update_slice_in_dim(
            jnp.zeros((CONTS, row_count, quarter, heads_here), jnp.float32),
            cum_grad_query_c.reshape(CONTS, 1, quarter, heads_here),
            row_index,
            axis=1,
        ).reshape(CONTS, CLEN, heads_here)
        cum_grad_part = jnp.concatenate(
            [
                (cum_grad_key_p + cum_grad_key_far + query_place).reshape(
                    col_count, local_prompt, heads_here
                ),
                (cum_grad_key_near + cont_place).reshape(col_count, local_conts * CLEN, heads_here),
            ],
            axis=1,
        )
        kv_grad_full, cum_grad_full = lax.psum((kv_grad_part, cum_grad_part), "row")
        cum_grad_cont = cum_grad_full[:, local_prompt:].reshape(CONTS, CLEN, heads_here)
        cum_grad_prompt = cum_grad_full[:, :local_prompt].reshape(PROMPT, heads_here)
        cum_grad_prompt = cum_grad_prompt + jnp.dot(
            branch_hot.T, jnp.sum(cum_grad_cont, axis=1), precision=highest
        )
        log_grad_prompt = lax.cumsum(cum_grad_prompt, axis=0, reverse=True)
        log_grad_cont = lax.cumsum(cum_grad_cont, axis=1, reverse=True)
        log_grad = jnp.concatenate(
            [
                log_grad_prompt.reshape(col_count, local_prompt, heads_here),
                log_grad_cont.reshape(col_count, local_conts * CLEN, heads_here),
            ],
            axis=1,
        )
        pre_grad = log_grad * jax.nn.sigmoid(-pre_gate)
        bias_grad = jnp.sum(pre_grad, axis=(0, 1))
        forget_grad_b = pre_grad.reshape(-1, heads_here).astype(jnp.bfloat16)
        query_grad_own = jnp.concatenate(
            [
                grad_query_prompt.reshape(col_count, prompt_blocks, 1, quarter, width_here),
                grad_query_cont.reshape(col_count, local_conts, 1, quarter, width_here),
            ],
            axis=1,
        )
        qg_grad_all = head_rows(
            jnp.concatenate([query_grad_own.astype(jnp.bfloat16), grad_logit], axis=-1)
        )
        kv_grad_rows = kv_grad_full.reshape(-1, 2 * width_here).astype(jnp.bfloat16)
        project_grad_rows = jnp.concatenate(
            [qg_grad_all[:, :width_here], kv_grad_rows, qg_grad_all[:, width_here:]], axis=-1
        )
        grad_project_w = inner_rows(normed_all, project_grad_rows)
        grad_forget_w = inner_rows(normed_all, forget_grad_b)
        grad_normed_one = token_sums(
            by_transpose(project_grad_rows, w_project) + by_transpose(forget_grad_b, w_forget)
        )
        gain_one_grad, grad_tokens = norm_backward(
            grad_normed_one, factor_one, scaled_one, gain_one
        )
        grad_tokens = grad_tokens + grad_residual
        grad_prompt_one = grad_tokens[:local_prompt]
        grad_cont_one = grad_tokens[local_prompt:].reshape(local_conts, CLEN, -1)
        group_count = jnp.sum(validity) * (row_index == 0).astype(jnp.float32)
        new_carry = (
            acc_project + grad_project_w,
            acc_forget + grad_forget_w,
            acc_bias + bias_grad,
            acc_out + grad_out_w,
            acc_hidden + grad_hidden_w,
            acc_down + grad_down_w,
            acc_gain_one + gain_one_grad,
            acc_gain_two + gain_two_grad,
            error_sum + group_err,
            count_sum + group_count,
        )
        return (new_carry, (grad_prompt_one, grad_cont_one))

    start = (
        jnp.zeros(w_project.shape, jnp.float32),
        jnp.zeros(w_forget.shape, jnp.float32),
        jnp.zeros(forget_bias.shape, jnp.float32),
        jnp.zeros(w_out.shape, jnp.float32),
        jnp.zeros(w_hidden.shape, jnp.float32),
        jnp.zeros(w_down.shape, jnp.float32),
        jnp.zeros(first_gain.shape, jnp.float32),
        jnp.zeros(second_gain.shape, jnp.float32),
        jnp.zeros((), jnp.float32),
        jnp.zeros((), jnp.float32),
    )
    finished, (grad_prompt, grad_cont) = lax.scan(
        one_group,
        start,
        (
            x_prompt,
            x_cont,
            teacher_prompt,
            teacher_cont,
            segment_ids,
            offsets,
            prompt_valid,
            cont_valid,
        ),
    )
    (
        acc_project,
        acc_forget,
        acc_bias,
        acc_out,
        acc_hidden,
        acc_down,
        acc_gain_one,
        acc_gain_two,
        error_sum,
        count_sum,
    ) = finished
    acc_project, acc_forget, acc_bias, acc_out, acc_hidden, acc_down = (
        lax.psum(acc_project.astype(jnp.bfloat16), "dp").astype(jnp.float32),
        lax.psum(acc_forget.astype(jnp.bfloat16), "dp").astype(jnp.float32),
        lax.psum(acc_bias.astype(jnp.bfloat16), "dp").astype(jnp.float32),
        lax.psum(acc_out.astype(jnp.bfloat16), "dp").astype(jnp.float32),
        lax.psum(acc_hidden.astype(jnp.bfloat16), "dp").astype(jnp.float32),
        lax.psum(acc_down.astype(jnp.bfloat16), "dp").astype(jnp.float32),
    )
    gain_one_total, gain_two_total = lax.psum((acc_gain_one, acc_gain_two), ("dp", "col"))
    error_total, count_total = lax.psum((error_sum, count_sum), ("dp", "row", "col"))
    grad_scale = x_prompt.shape[0] * lax.axis_size("dp") * (PROMPT + CONTS * CLEN) / count_total
    loss_value = error_total / (D * count_total)
    width_here = w_query.shape[1]
    units_here = w_gate.shape[1]
    return (
        loss_value,
        grad_prompt * grad_scale,
        grad_cont * grad_scale,
        gain_one_total * grad_scale,
        acc_project[:, :width_here] * grad_scale,
        acc_project[:, width_here : 2 * width_here] * grad_scale,
        acc_project[:, 2 * width_here : 3 * width_here] * grad_scale,
        acc_project[:, 3 * width_here :] * grad_scale,
        acc_forget * grad_scale,
        acc_bias * grad_scale,
        acc_out * grad_scale,
        gain_two_total * grad_scale,
        acc_hidden[:, :units_here] * grad_scale,
        acc_hidden[:, units_here:] * grad_scale,
        acc_down * grad_scale,
    )


AX = ("yo", "y", "c", "x", "zh", "zl")
FAR_PIECE = 18
DOC_LANE = 36
UNIT_LANE = 40
NEVER = 1e12
LANES = 128
BF = jnp.bfloat16
F32 = jnp.float32


class Ring:
    def __init__(self, sizes):
        self.sizes = sizes
        self.zl_count = sizes["zl"]
        self.offsets = [(dy, dz) for dy in range(2) for dz in range(self.zl_count)]
        self.back = [
            self.offsets.index(((-dy) % 2, (-dz) % self.zl_count)) for dy, dz in self.offsets
        ]

    def pairs(self, target, source_ok=None):
        ranges = [range(self.sizes[a]) for a in AX]
        number = {}
        for place, coords in enumerate(itertools.product(*ranges)):
            number[coords] = place
        out = []
        for coords in number:
            here = dict(zip(AX, coords))
            if source_ok is not None and not source_ok(here):
                continue
            there = dict(here, **target(here))
            out.append((number[coords], number[tuple(there[a] for a in AX)]))
        return out

    def move(self, value, target, source_ok=None):
        return lax.ppermute(value, AX, self.pairs(target, source_ok))

    def swap(self, value, axis, source_ok=None):
        return self.move(value, lambda h: {axis: 1 - h[axis]}, source_ok)

    def to_peer(self, value, k):
        dy, dz = self.offsets[k]
        return self.move(
            value, lambda h: {"y": (h["y"] + dy) % 2, "zl": (h["zl"] + dz) % self.zl_count}
        )

    def to_group(self, value, flip):
        return self.move(
            value,
            lambda h: {
                "y": h["zh"],
                "c": h["x"] ^ flip,
                "x": h["y"],
                "zh": h["c"],
            },
        )

    def from_group(self, value, flip):
        return self.move(
            value,
            lambda h: {"y": h["x"], "c": h["zh"], "x": h["c"] ^ flip, "zh": h["y"]},
        )

    def total(self, value):
        for axis in ("c", "y", "x", "zh"):
            value = value + self.swap(value, axis)
        if self.zl_count == 2:
            value = value + self.swap(value, "zl")
        elif self.zl_count > 2:
            value = lax.psum(value, "zl")
        if self.sizes["yo"] > 1:
            value = lax.psum(value, "yo")
        return value

    def gather(self, rows):
        return [rows] + [self.to_peer(rows, k) for k in range(1, len(self.offsets))]

    def scatter_sum(self, partial_of):
        arrived = []
        for k in range(1, len(self.offsets)):
            arrived.append(self.to_peer(partial_of(self.back[k]).astype(BF), k))
        total = partial_of(0)
        for part in arrived:
            total = total + part.astype(F32)
        return total


def nt_dot(left_op, right_op):
    return lax.dot_general(
        left_op, right_op, (((1,), (1,)), ((), ())), preferred_element_type=F32
    )


def tn_dot(left_op, right_op):
    return lax.dot_general(
        left_op, right_op, (((0,), (0,)), ((), ())), preferred_element_type=F32
    )


def nn_dot(left_op, right_op):
    return jnp.dot(left_op, right_op, preferred_element_type=F32)


def split_pieces(values, shift, heads):
    high = values.astype(BF).astype(F32)
    rest = values - high
    mid = rest.astype(BF).astype(F32)
    low = (rest - mid).astype(BF).astype(F32)
    out = None
    for place, piece in enumerate((high, mid, low)):
        amount = shift + place * heads
        moved = pltpu.roll(piece, amount, 1) if amount else piece
        out = moved if out is None else out + moved
    return out


def head_lanes(shape, head, heads):
    lane = lax.broadcasted_iota(jnp.int32, shape, len(shape) - 1)
    keep = lane >= DOC_LANE
    for place in range(3):
        keep = keep | (lane == place * heads + head) | (lane == FAR_PIECE + place * heads + head)
    return keep


def half_lanes(shape, half):
    lane = lax.broadcasted_iota(jnp.int32, shape, len(shape) - 1)
    return (lane >= HEAD_DIM * half) & (lane < HEAD_DIM * (half + 1))


def near_visible(rows):
    key_row = lax.broadcasted_iota(jnp.int32, (rows, rows), 0)
    query_row = lax.broadcasted_iota(jnp.int32, (rows, rows), 1)
    same = (key_row // CLEN) == (query_row // CLEN)
    return same & (key_row <= query_row)


def fill_keys(
    keys, flag, far_own, far_there, kv_near, cum_far, cum_near, far_base, near_base, far_rows, heads
):
    slots = heads // 2

    @pl.when(pl.program_id(0) == 0)
    def _():
        aug = (far_base[...].astype(F32) + split_pieces(-cum_far[...], FAR_PIECE, heads)).astype(BF)
        for s in range(slots):
            keys[s, :far_rows, LANES:] = aug

        @pl.when(flag[0] == 0)
        def _():
            for s in range(slots):
                keys[s, :far_rows, :LANES] = far_own[s][:, :LANES]

        @pl.when(flag[0] != 0)
        def _():
            for s in range(slots):
                keys[s, :far_rows, :LANES] = far_there[s][:, :LANES]

    aug = (near_base[...].astype(F32) + split_pieces(-cum_near[...], FAR_PIECE, heads)).astype(BF)
    for s in range(slots):
        keys[s, far_rows:, :LANES] = kv_near[s][:, :LANES]
        keys[s, far_rows:, LANES:] = aug


def attend_kernel(
    heads,
    flag,
    qg_a,
    qg_b,
    qg_c,
    near_a,
    near_b,
    near_c,
    own_a,
    own_b,
    own_c,
    there_a,
    there_b,
    there_c,
    cum_near,
    cum_far,
    q_base,
    near_base,
    far_base,
    gated_ref,
    att_ref,
    log_ref,
    keys,
    vals,
):
    qg = (qg_a, qg_b, qg_c)
    kv_near = (near_a, near_b, near_c)
    far_own = (own_a, own_b, own_c)
    far_there = (there_a, there_b, there_c)
    rows = qg_a.shape[0]
    far_rows = own_a.shape[0]
    slots = heads // 2
    fill_keys(
        keys,
        flag,
        far_own,
        far_there,
        kv_near,
        cum_far,
        cum_near,
        far_base,
        near_base,
        far_rows,
        heads,
    )

    @pl.when(pl.program_id(0) == 0)
    def _():
        def fill(source):
            for s in range(slots):
                moved = source[s][:, LANES:].T
                for half in range(2):
                    vals[2 * s + half, :HEAD_DIM, :far_rows] = moved[
                        HEAD_DIM * half : HEAD_DIM * (half + 1)
                    ]

        @pl.when(flag[0] == 0)
        def _():
            fill(far_own)

        @pl.when(flag[0] != 0)
        def _():
            fill(far_there)

        for h in range(heads):
            vals[h, HEAD_DIM:, :] = jnp.ones((16, far_rows + rows), BF)

    for s in range(slots):
        moved = kv_near[s][:, LANES:].T
        for half in range(2):
            vals[2 * s + half, :HEAD_DIM, far_rows:] = moved[
                HEAD_DIM * half : HEAD_DIM * (half + 1)
            ]
    q_aug = (q_base[...].astype(F32) + split_pieces(cum_near[...], 0, heads)).astype(BF)
    visible = near_visible(rows)
    outs = []
    logs = []
    for h in range(heads):
        s, half = h // 2, h % 2
        query = qg[s][:, :LANES]
        query = jnp.where(half_lanes(query.shape, half), query * BF(HEAD_DIM**-0.5), BF(0))
        aug = jnp.where(head_lanes(q_aug.shape, h, heads), q_aug, BF(0))
        q_cat = jnp.concatenate([query, aug], axis=1)
        far = nt_dot(keys[s, :far_rows], q_cat)
        near = jnp.where(visible, nt_dot(keys[s, far_rows:], q_cat), -NEVER)
        top = jnp.maximum(
            jnp.max(far, axis=0, keepdims=True), jnp.max(near, axis=0, keepdims=True)
        )
        far_p = jnp.exp(far - top).astype(BF)
        near_p = jnp.exp(near - top).astype(BF)
        out = nn_dot(vals[h, :, :far_rows], far_p) + nn_dot(vals[h, :, far_rows:], near_p)
        total = out[HEAD_DIM : HEAD_DIM + 1]
        outs.append(out[:HEAD_DIM] / total)
        logs.append(top + jnp.log(total))
    att = jnp.concatenate(outs, axis=0).T
    att_ref[...] = att
    for s in range(slots):
        gate = qg[s][:, LANES:].astype(F32)
        cols = slice(s * LANES, (s + 1) * LANES)
        gated_ref[:, cols] = (att[:, cols] * jax.nn.sigmoid(gate)).astype(BF)
    log_rows = jnp.concatenate(logs + [jnp.zeros((LANES - heads, rows), F32)], axis=0)
    log_ref[...] = log_rows.T


def row_block(rows, cols, place=0):
    return pl.BlockSpec((rows, cols), lambda i: (i, place))


def whole_block(rows, cols):
    return pl.BlockSpec((rows, cols), lambda i: (0, 0))


def slot_inputs(flag, projects, kv_there, rows):
    far_rows = projects[0].shape[0]
    specs_in = [pl.BlockSpec(memory_space=pltpu.SMEM)]
    for spec in (
        row_block(rows, 2 * LANES),
        row_block(rows, 2 * LANES, 1),
        pl.BlockSpec((far_rows, 2 * LANES), lambda i: (0, 1)),
        whole_block(far_rows, 2 * LANES),
    ):
        specs_in += [spec] * len(projects)
    return specs_in, [flag, *projects, *projects, *projects, *kv_there]


def cum_specs(rows, far_rows):
    return [
        row_block(rows, LANES),
        whole_block(far_rows, LANES),
        row_block(rows, LANES),
        row_block(rows, LANES),
        whole_block(far_rows, LANES),
    ]


def attend(flag, projects, kv_there, cum_near, cum_far, q_base, near_base, far_base, rows, heads):
    total = projects[0].shape[0]
    width = heads * HEAD_DIM
    steps = total // rows
    flops = 2 * total * (total + rows) * heads * 384
    slot_specs, slot_values = slot_inputs(flag, projects, kv_there, rows)
    return pl.pallas_call(
        functools.partial(attend_kernel, heads),
        grid=(steps,),
        out_shape=(
            jax.ShapeDtypeStruct((total, width), BF),
            jax.ShapeDtypeStruct((total, width), F32),
            jax.ShapeDtypeStruct((total, LANES), F32),
        ),
        in_specs=slot_specs + cum_specs(rows, total),
        out_specs=(row_block(rows, width), row_block(rows, width), row_block(rows, LANES)),
        scratch_shapes=[
            pltpu.VMEM((heads // 2, total + rows, 2 * LANES), BF),
            pltpu.VMEM((heads, HEAD_DIM + 16, total + rows), BF),
        ],
        compiler_params=pltpu.CompilerParams(vmem_limit_bytes=48 << 20),
        cost_estimate=pl.CostEstimate(
            flops=flops, bytes_accessed=total * width * 20, transcendentals=total * total * heads
        ),
    )(*slot_values, cum_near, cum_far, q_base, near_base, far_base)


def attend_back_kernel(
    heads,
    flag,
    qg_a,
    qg_b,
    qg_c,
    near_a,
    near_b,
    near_c,
    own_a,
    own_b,
    own_c,
    there_a,
    there_b,
    there_c,
    cum_near,
    cum_far,
    q_base,
    near_base,
    far_base,
    grad_ref,
    att_ref,
    log_ref,
    dqg_ref,
    near_ref,
    far_ref,
    row_ref,
    near_col,
    far_col,
    keys,
    vals,
):
    qg = (qg_a, qg_b, qg_c)
    kv_near = (near_a, near_b, near_c)
    far_own = (own_a, own_b, own_c)
    far_there = (there_a, there_b, there_c)
    rows = qg_a.shape[0]
    far_rows = own_a.shape[0]
    slots = heads // 2
    fill_keys(
        keys,
        flag,
        far_own,
        far_there,
        kv_near,
        cum_far,
        cum_near,
        far_base,
        near_base,
        far_rows,
        heads,
    )

    @pl.when(pl.program_id(0) == 0)
    def _():
        lane = lax.broadcasted_iota(jnp.int32, (far_rows + rows, LANES), 1)
        ones = (lane < 3).astype(F32).astype(BF)
        for s in range(slots):
            vals[s, :, LANES:] = ones

        @pl.when(flag[0] == 0)
        def _():
            for s in range(slots):
                vals[s, :far_rows, :LANES] = far_own[s][:, LANES:]

        @pl.when(flag[0] != 0)
        def _():
            for s in range(slots):
                vals[s, :far_rows, :LANES] = far_there[s][:, LANES:]

        far_ref[...] = jnp.zeros(far_ref.shape, F32)
        far_col[...] = jnp.zeros(far_col.shape, F32)

    for s in range(slots):
        vals[s, far_rows:, :LANES] = kv_near[s][:, LANES:]
    q_aug = (q_base[...].astype(F32) + split_pieces(cum_near[...] - log_ref[...], 0, heads)).astype(
        BF
    )
    visible = near_visible(rows)
    lane = lax.broadcasted_iota(jnp.int32, (rows, LANES), 1)
    row_total = jnp.zeros((rows, LANES), F32)
    col_total = jnp.zeros((rows, LANES), F32)
    for s in range(slots):
        cols = slice(s * LANES, (s + 1) * LANES)
        kcols = slice(2 * s * LANES, (2 * s + 1) * LANES)
        vcols = slice((2 * s + 1) * LANES, (2 * s + 2) * LANES)
        gate_sig = jax.nn.sigmoid(qg[s][:, LANES:].astype(F32))
        grad = grad_ref[:, cols].astype(F32)
        att = att_ref[:, cols]
        grad_att = (grad * gate_sig).astype(BF)
        dqg_ref[:, vcols] = (grad * att * gate_sig * (1.0 - gate_sig)).astype(BF)
        weighed = grad_att.astype(F32) * att
        dq_total = jnp.zeros((rows, LANES), F32)
        dk_near = jnp.zeros((rows, LANES), F32)
        dv_near = jnp.zeros((rows, LANES), F32)
        for half in range(2):
            h = 2 * s + half
            mine = half_lanes((rows, LANES), half)
            query = jnp.where(mine, qg[s][:, :LANES] * BF(HEAD_DIM**-0.5), BF(0))
            aug = jnp.where(head_lanes(q_aug.shape, h, heads), q_aug, BF(0))
            q_cat = jnp.concatenate([query, aug], axis=1)
            ga = jnp.where(mine, grad_att, BF(0))
            delta = -jnp.sum(jnp.where(mine, weighed, 0.0), axis=1, keepdims=True)
            high = delta.astype(BF).astype(F32)
            mid = (delta - high).astype(BF).astype(F32)
            low = delta - high - mid
            d_aug = jnp.where(
                lane == 0, high, jnp.where(lane == 1, mid, jnp.where(lane == 2, low, 0.0))
            ).astype(BF)
            ga_cat = jnp.concatenate([ga, d_aug], axis=1)
            for part in range(2):
                span = slice(0, far_rows) if part == 0 else slice(far_rows, far_rows + rows)
                prob = jnp.exp(nt_dot(keys[s, span], q_cat))
                if part == 1:
                    prob = jnp.where(visible, prob, 0.0)
                ds = (prob * nt_dot(vals[s, span], ga_cat)).astype(BF)
                dv = nn_dot(prob.astype(BF), ga)
                dk = nn_dot(ds, q_cat)
                dq = tn_dot(ds, keys[s, span])
                dq_total += jnp.where(mine, dq[:, :LANES], 0.0)
                row_total += jnp.where(lane == h, dq[:, LANES:], 0.0)
                if part == 0:
                    far_ref[:, kcols] += dk[:, :LANES]
                    far_ref[:, vcols] += dv
                    far_col[...] += dk[:, LANES:]
                else:
                    dk_near += dk[:, :LANES]
                    dv_near += dv
                    col_total += dk[:, LANES:]
        dqg_ref[:, kcols] = (dq_total * HEAD_DIM**-0.5).astype(BF)
        near_ref[:, kcols] = dk_near
        near_ref[:, vcols] = dv_near
    row_ref[...] = row_total
    near_col[...] = col_total


def attend_back(
    flag,
    projects,
    kv_there,
    cum_near,
    cum_far,
    q_base,
    near_base,
    far_base,
    grad,
    att,
    logs,
    rows,
    heads,
):
    total = projects[0].shape[0]
    width = heads * HEAD_DIM
    steps = total // rows
    flops = 2 * total * (total + rows) * heads * 1152
    slot_specs, slot_values = slot_inputs(flag, projects, kv_there, rows)
    return pl.pallas_call(
        functools.partial(attend_back_kernel, heads),
        grid=(steps,),
        out_shape=(
            jax.ShapeDtypeStruct((total, 2 * width), BF),
            jax.ShapeDtypeStruct((total, 2 * width), F32),
            jax.ShapeDtypeStruct((total, 2 * width), F32),
            jax.ShapeDtypeStruct((total, LANES), F32),
            jax.ShapeDtypeStruct((total, LANES), F32),
            jax.ShapeDtypeStruct((total, LANES), F32),
        ),
        in_specs=slot_specs
        + cum_specs(rows, total)
        + [row_block(rows, width), row_block(rows, width), row_block(rows, LANES)],
        out_specs=(
            row_block(rows, 2 * width),
            row_block(rows, 2 * width),
            whole_block(total, 2 * width),
            row_block(rows, LANES),
            row_block(rows, LANES),
            whole_block(total, LANES),
        ),
        scratch_shapes=[
            pltpu.VMEM((heads // 2, total + rows, 2 * LANES), BF),
            pltpu.VMEM((heads // 2, total + rows, 2 * LANES), BF),
        ],
        compiler_params=pltpu.CompilerParams(vmem_limit_bytes=56 << 20),
        cost_estimate=pl.CostEstimate(
            flops=flops, bytes_accessed=total * width * 40, transcendentals=total * total * heads
        ),
    )(*slot_values, cum_near, cum_far, q_base, near_base, far_base, grad, att, logs)


def full_norm(tokens, gain_vec):
    factor = lax.rsqrt(jnp.mean(tokens * tokens, axis=-1, keepdims=True) + epsilon)
    scaled = tokens * factor
    return factor, scaled, (scaled * gain_vec).astype(BF)


def full_norm_back(grad_normed, factor, scaled, gain_vec):
    e = grad_normed * gain_vec
    mean = jnp.mean(e * scaled, axis=-1, keepdims=True)
    return jnp.sum(grad_normed * scaled, axis=0), factor * (e - scaled * mean)


MESH_ID = pl.DeviceIdType.MESH


class Here:
    def __init__(self, ring):
        self.ring = ring
        self.at = {a: lax.axis_index(a) for a in AX}

    def other(self, axis):
        return {axis: 1 - self.at[axis]}

    def peer(self, k):
        dy, dz = self.ring.offsets[k]
        return {
            "y": lax.rem(self.at["y"] + dy, 2),
            "zl": lax.rem(self.at["zl"] + dz, self.ring.zl_count),
        }

    def greet(self, targets, extra=()):
        barrier = pltpu.get_barrier_semaphore()
        for target in targets:
            pl.semaphore_signal(barrier, inc=1, device_id=target, device_id_type=MESH_ID)
        count = len(targets)
        for target, away in extra:
            @pl.when(away)
            def _():
                pl.semaphore_signal(barrier, inc=1, device_id=target, device_id_type=MESH_ID)

            count = count + away.astype(jnp.int32)
        pl.semaphore_wait(barrier, count)


def remote(src, dst, send_sem, recv_sem, target):
    return pltpu.make_async_remote_copy(
        src_ref=src,
        dst_ref=dst,
        send_sem=send_sem,
        recv_sem=recv_sem,
        device_id=target,
        device_id_type=MESH_ID,
    )


def last_kernel(
    ring,
    grads_in,
    weight_in,
    normed_in,
    tokens_in,
    residual_in,
    gain_in,
    hid_in,
    down_in,
    out_first_in,
    out_mid_in,
    back_out,
    proj_out,
    gate_out,
    up_out,
    down_out,
    out_out,
    gain_out,
    grads,
    weight,
    normed,
    tokens,
    residual,
    rs_send,
    rs_land,
    total,
    c_send,
    c_land,
    kept,
    x_send,
    x_land,
    z_send,
    z_land,
    final,
    blocks,
    gain_sum,
    gain_nat,
    gain_land,
    load_sem,
    local_sem,
    y_send_sem,
    y_recv_sem,
    c2_send_sem,
    c2_recv_sem,
    rs_send_sem,
    rs_recv_sem,
    c_send_sem,
    c_recv_sem,
    x_send_sem,
    x_recv_sem,
    z_send_sem,
    z_recv_sem,
    back_send_sem,
    back_recv_sem,
    gain_send_sem,
    gain_recv_sem,
):
    here = Here(ring)
    y, c, x, zh = (here.at[a] for a in ("y", "c", "x", "zh"))
    local, features = tokens.shape
    part = features // 4
    slot_w = 4 * LANES
    slots = z_count = 3
    units = down_in.shape[0]
    owner = zh == y
    peers = len(ring.offsets)

    loads = [
        pltpu.make_async_copy(a, b, load_sem.at[i])
        for i, (a, b) in enumerate(
            (
                (grads_in, grads),
                (weight_in, weight),
                (normed_in, normed),
                (tokens_in, tokens),
                (residual_in, residual),
            )
        )
    ]
    for copy in loads:
        copy.start()

    def back_target(flip):
        return {"y": x, "c": zh, "x": c ^ flip, "zh": y}

    def back_away(flip):
        return ~((x == y) & (zh == c) & ((c ^ flip) == x) & (zh == y))

    def back_from_away(flip):
        return ~((zh == y) & ((x ^ flip) == c) & (y == x) & (c == zh))

    here.greet(
        [here.peer(k) for k in range(1, peers)]
        + [here.other("c"), here.other("x"), here.other("zh")],
        [(back_target(f), back_away(f)) for f in range(2)]
        + [({"y": zh, "c": x ^ f, "x": y, "zh": c}, back_from_away(f)) for f in range(2)],
    )

    row0 = pl.multiple_of(c * part, part)

    def rows_of(ref, col, width):
        return ref.at[pl.ds(row0, part), pl.ds(pl.multiple_of(col, LANES), width)]

    def cols_of(ref, row, height):
        return ref.at[pl.ds(pl.multiple_of(row, LANES), height), pl.ds(row0, part)]

    pieces = [
        (hid_in.at[:, :units], rows_of(gate_out, y * units, units)),
        (hid_in.at[:, units:], rows_of(up_out, y * units, units)),
        (down_in, cols_of(down_out, y * units, units)),
        (out_first_in, cols_of(out_out, 2 * LANES * y, LANES)),
    ]
    own_pieces = [
        pltpu.make_async_copy(src, dst, local_sem.at[i]) for i, (src, dst) in enumerate(pieces)
    ]
    y_pieces = [
        remote(src, dst, y_send_sem.at[i], y_recv_sem.at[i], here.other("y"))
        for i, (src, dst) in enumerate(pieces)
    ]
    mid_dst = cols_of(out_out, LANES, LANES)
    own_mid = pltpu.make_async_copy(out_mid_in, mid_dst, local_sem.at[4])
    y_mid = remote(out_mid_in, mid_dst, y_send_sem.at[4], y_recv_sem.at[4], here.other("y"))

    loads[0].wait()
    loads[1].wait()
    tiles = 3
    tile_w = features // tiles

    def partial_rows(chunk_no, store):
        def step(i, carry):
            cols = pl.ds(pl.multiple_of(i * tile_w, LANES), tile_w)
            store(
                cols,
                nt_dot(grads[chunk_no * local : (chunk_no + 1) * local, :], weight[cols, :]),
            )
            return carry

        lax.fori_loop(0, tiles, step, 0)

    rs = []
    for k in range(1, peers):

        def store_out(cols, value, k=k):
            rs_send[k - 1, :, cols] = value.astype(BF)

        partial_rows(ring.back[k], store_out)
        copy = remote(
            rs_send.at[k - 1],
            rs_land.at[k - 1],
            rs_send_sem.at[k - 1],
            rs_recv_sem.at[k - 1],
            here.peer(k),
        )
        copy.start()
        rs.append(copy)
    for copy in own_pieces + y_pieces:
        copy.start()

    @pl.when(owner)
    def _():
        own_mid.start()
        y_mid.start()

    loads[2].wait()
    tile_r = LANES
    per_part = part // tile_r

    def weight_tile(first, i):
        cols = pl.ds(pl.multiple_of(first + i * tile_r, LANES), tile_r)
        return tn_dot(normed[:, cols], grads[:, : slots * slot_w])

    def c_step(i, carry):
        rows = pl.ds(pl.multiple_of(i * tile_r, tile_r), tile_r)
        c_send[rows, :] = weight_tile(2 * part, i).astype(BF)
        return carry

    lax.fori_loop(0, 2 * per_part, c_step, 0)
    c_copy = remote(c_send, c_land, c_send_sem, c_recv_sem, here.other("c"))
    c_copy.start()

    def store_own(cols, value):
        total[:, cols] = value

    partial_rows(0, store_own)
    c_copy.wait_recv()

    def x_step(i, carry):
        rows = pl.ds(pl.multiple_of(i * tile_r, tile_r), tile_r)
        land = pl.ds(pl.multiple_of(part + i * tile_r, tile_r), tile_r)
        value = weight_tile(part, i) + c_land[land, :].astype(F32)
        for s in range(slots):
            x_send[s, rows, :] = value[:, s * slot_w : (s + 1) * slot_w].astype(BF)
        return carry

    lax.fori_loop(0, per_part, x_step, 0)
    x_copies = {}
    for s in (2, 1, 0):
        x_copies[s] = remote(
            x_send.at[s], x_land.at[s], x_send_sem.at[s], x_recv_sem.at[s], here.other("x")
        )
        x_copies[s].start()

    def own_step(i, carry):
        rows = pl.ds(pl.multiple_of(i * tile_r, tile_r), tile_r)
        value = weight_tile(0, i) + c_land[rows, :].astype(F32)
        for s in range(slots):
            kept[s, rows, :] = value[:, s * slot_w : (s + 1) * slot_w]
        return carry

    lax.fori_loop(0, per_part, own_step, 0)

    loads[3].wait()
    loads[4].wait()
    for copy in rs:
        copy.wait_recv()
    gain_sum[...] = jnp.zeros(gain_sum.shape, F32)
    tile_n = 32

    def norm_step(i, carry):
        rows = pl.ds(pl.multiple_of(i * tile_n, tile_n), tile_n)
        tok = tokens[rows, :].astype(F32)
        grad = total[rows, :]
        for k in range(peers - 1):
            grad = grad + rs_land[k, rows, :].astype(F32)
        factor = lax.rsqrt(jnp.mean(tok * tok, axis=-1, keepdims=True) + epsilon)
        scaled_tok = tok * factor
        e = grad * gain_in[...]
        mean = jnp.mean(e * scaled_tok, axis=-1, keepdims=True)
        out = factor * (e - scaled_tok * mean) + residual[rows, :]
        weighed = jnp.sum(grad * scaled_tok, axis=0, keepdims=True)
        for i in range(4):
            blocks[i, rows, :] = out[:, i * part : (i + 1) * part].astype(BF)
            gain_sum[i, 0:1, :] += weighed[:, i * part : (i + 1) * part]
        return carry

    lax.fori_loop(0, local // tile_n, norm_step, 0)

    def block_no(half, low_high):
        return (half ^ x) + 2 * (low_high ^ c)

    def back_copy(flip, p):
        return remote(
            blocks.at[block_no(c ^ flip, p)],
            back_out.at[c, :, p * part : (p + 1) * part],
            back_send_sem.at[flip, p],
            back_recv_sem.at[flip, p],
            back_target(flip),
        )

    def back_own(flip, p):
        return pltpu.make_async_copy(
            blocks.at[block_no(c ^ flip, p)],
            back_out.at[c, :, p * part : (p + 1) * part],
            local_sem.at[5 + p],
        )

    for f in range(2):

        @pl.when(back_away(f))
        def _():
            for p in range(2):
                back_copy(f, p).start()

        @pl.when(~back_away(f))
        def _():
            for p in range(2):
                back_own(f, p).start()

    z_copies = {}
    for s in (2, 1, 0):
        x_copies[s].wait_recv()
        kept[s] += x_land[s].astype(F32)
        if s == 2:
            z_send[0] = kept[2].astype(BF)
            z_copies[0] = remote(
                z_send.at[0], z_land.at[0], z_send_sem.at[0], z_recv_sem.at[0], here.other("zh")
            )
            z_copies[0].start()
        if s == 1:
            z_copies[1] = remote(
                z_send.at[1], z_land.at[1], z_send_sem.at[1], z_recv_sem.at[1], here.other("zh")
            )

            @pl.when(~owner)
            def _():
                z_send[1] = kept[1].astype(BF)
                z_copies[1].start()

    for copy in own_pieces:
        copy.wait()
    for copy in y_pieces:
        copy.wait_recv()

    @pl.when(owner)
    def _():
        own_mid.wait()

    @pl.when(~owner)
    def _():
        y_mid.wait_recv()

    c2 = []
    for i, view in enumerate(
        (
            gate_out.at[pl.ds(row0, part), :],
            up_out.at[pl.ds(row0, part), :],
            down_out.at[:, pl.ds(row0, part)],
            out_out.at[:, pl.ds(row0, part)],
        )
    ):
        copy = remote(view, view, c2_send_sem.at[i], c2_recv_sem.at[i], here.other("c"))
        copy.start()
        c2.append(copy)

    for i in range(4):
        gain_nat[0, i] = gain_sum[block_no(i // 2, i % 2)]
    for place, axis in enumerate(("c", "y", "x", "zl", "zh")):
        copy = remote(
            gain_nat.at[place],
            gain_land.at[place],
            gain_send_sem.at[place],
            gain_recv_sem.at[place],
            here.other(axis),
        )
        copy.start()
        copy.wait_recv()
        gain_nat[place + 1] = gain_nat[place] + gain_land[place]
        copy.wait_send()
    gain_copy = pltpu.make_async_copy(gain_nat.at[5], gain_out, local_sem.at[7])
    gain_copy.start()

    z_copies[0].wait_recv()
    final[0] = (kept[0] + z_land[0].astype(F32)).astype(BF)

    @pl.when(owner)
    def _():
        z_copies[1].wait_recv()
        final[1] = (kept[1] + z_land[1].astype(F32)).astype(BF)

    first_dst = rows_of(proj_out, 2 * y * slot_w, slot_w)
    mid_proj = rows_of(proj_out, slot_w, slot_w)
    own_first = pltpu.make_async_copy(final.at[0], first_dst, local_sem.at[8])
    own_second = pltpu.make_async_copy(final.at[1], mid_proj, local_sem.at[9])
    y_first = remote(final.at[0], first_dst, y_send_sem.at[5], y_recv_sem.at[5], here.other("y"))
    y_second = remote(final.at[1], mid_proj, y_send_sem.at[6], y_recv_sem.at[6], here.other("y"))
    y_first.start()
    own_first.start()

    @pl.when(owner)
    def _():
        y_second.start()
        own_second.start()

    own_first.wait()
    y_first.wait_recv()

    @pl.when(owner)
    def _():
        own_second.wait()

    @pl.when(~owner)
    def _():
        y_second.wait_recv()

    view = proj_out.at[pl.ds(row0, part), :]
    copy = remote(view, view, c2_send_sem.at[4], c2_recv_sem.at[4], here.other("c"))
    copy.start()
    c2.append(copy)

    for copy in c2:
        copy.wait()
    for f in range(2):

        @pl.when(back_away(f))
        def _():
            for p in range(2):
                back_copy(f, p).wait()

        @pl.when(~back_away(f))
        def _():
            for p in range(2):
                back_own(f, p).wait()

    gain_copy.wait()
    for copy in rs + [c_copy, x_copies[0], x_copies[1], x_copies[2], z_copies[0], y_first]:
        copy.wait_send()
    for copy in y_pieces:
        copy.wait_send()

    @pl.when(owner)
    def _():
        y_mid.wait_send()
        y_second.wait_send()

    @pl.when(~owner)
    def _():
        z_copies[1].wait_send()


def last_step(ring, grads, weight, normed, tokens, residual, gain, hid, down, out_first, out_mid):
    local, features = tokens.shape
    rows = grads.shape[0]
    part = features // 4
    half = features // 2
    units = down.shape[0]
    peers = len(ring.offsets)
    slot_w = 4 * LANES
    any_spec = pl.BlockSpec(memory_space=pl.ANY)
    dma = pltpu.SemaphoreType.DMA
    return pl.pallas_call(
        functools.partial(last_kernel, ring),
        out_shape=(
            jax.ShapeDtypeStruct((2, local, half), BF),
            jax.ShapeDtypeStruct((half, 3 * slot_w), BF),
            jax.ShapeDtypeStruct((half, 2 * units), BF),
            jax.ShapeDtypeStruct((half, 2 * units), BF),
            jax.ShapeDtypeStruct((2 * units, half), BF),
            jax.ShapeDtypeStruct((3 * LANES, half), BF),
            jax.ShapeDtypeStruct((4, 8, part), F32),
        ),
        in_specs=[any_spec] * 5 + [pl.BlockSpec(memory_space=pltpu.VMEM)] + [any_spec] * 4,
        out_specs=[any_spec] * 7,
        scratch_shapes=[
            pltpu.VMEM(grads.shape, BF),
            pltpu.VMEM(weight.shape, BF),
            pltpu.VMEM(normed.shape, BF),
            pltpu.VMEM(tokens.shape, BF),
            pltpu.VMEM(residual.shape, F32),
            pltpu.VMEM((peers - 1, local, features), BF),
            pltpu.VMEM((peers - 1, local, features), BF),
            pltpu.VMEM((local, features), F32),
            pltpu.VMEM((half, 3 * slot_w), BF),
            pltpu.VMEM((half, 3 * slot_w), BF),
            pltpu.VMEM((3, part, slot_w), F32),
            pltpu.VMEM((3, part, slot_w), BF),
            pltpu.VMEM((3, part, slot_w), BF),
            pltpu.VMEM((2, part, slot_w), BF),
            pltpu.VMEM((2, part, slot_w), BF),
            pltpu.VMEM((2, part, slot_w), BF),
            pltpu.VMEM((4, local, part), BF),
            pltpu.VMEM((4, 8, part), F32),
            pltpu.VMEM((6, 4, 8, part), F32),
            pltpu.VMEM((5, 4, 8, part), F32),
            dma((5,)),
            dma((10,)),
            dma((7,)),
            dma((7,)),
            dma((5,)),
            dma((5,)),
            dma((peers - 1,)),
            dma((peers - 1,)),
            dma,
            dma,
            dma((3,)),
            dma((3,)),
            dma((2,)),
            dma((2,)),
            dma((2, 2)),
            dma((2, 2)),
            dma((5,)),
            dma((5,)),
        ],
        compiler_params=pltpu.CompilerParams(
            collective_id=1, has_side_effects=True, vmem_limit_bytes=58 << 20
        ),
        cost_estimate=pl.CostEstimate(
            flops=4 * rows * features * 3 * slot_w, bytes_accessed=40 << 20, transcendentals=0
        ),
    )(grads, weight, normed, tokens, residual, gain, hid, down, out_first, out_mid)


def ring_body(
    ring,
    x_prompt,
    x_cont,
    teacher_prompt,
    teacher_cont,
    segment_ids,
    offsets,
    prompt_valid,
    cont_valid,
    first_gain,
    w_query,
    w_key,
    w_value,
    w_outgate,
    w_forget,
    forget_bias,
    w_out,
    second_gain,
    w_gate,
    w_up,
    w_down,
):
    y = lax.axis_index("y")
    c = lax.axis_index("c")
    x = lax.axis_index("x")
    zh = lax.axis_index("zh")
    zl = lax.axis_index("zl")
    zl_count = ring.zl_count
    local = x_prompt.shape[1]
    half_d = x_prompt.shape[2]
    part_d = half_d // 2
    local_conts = x_cont.shape[1]
    heads = w_forget.shape[1]
    units_here = w_gate.shape[1]
    half_units = units_here // 2
    width = heads * HEAD_DIM
    slots = heads // 2
    pair_unit = PROMPT // CLEN
    chunk_units = local // CLEN
    peers = len(ring.offsets)
    owner = zh == y

    def by_x(own, other):
        return jnp.where(x == c, own, other)

    def regroup(prompt_rows, cont_rows):
        cont_rows = cont_rows.reshape(local_conts * CLEN, half_d)
        first = jnp.where(x == 0, prompt_rows, cont_rows)
        second = jnp.where(x == 0, cont_rows, prompt_rows)
        return ring.to_group(first, 0), ring.to_group(second, 1)

    def feature_order(own, other):
        def cut(value, place):
            low = value[..., :part_d]
            high = value[..., part_d:]
            return jnp.where(c == place, low, high)

        return jnp.concatenate([cut(own, 0), cut(other, 0), cut(own, 1), cut(other, 1)], axis=-1)

    def natural_order(value):
        pieces = [value[..., i * part_d : (i + 1) * part_d] for i in range(4)]
        own_low = jnp.where(c == 0, pieces[0], pieces[2])
        own_high = jnp.where(c == 0, pieces[2], pieces[0])
        other_low = jnp.where(c == 0, pieces[1], pieces[3])
        other_high = jnp.where(c == 0, pieces[3], pieces[1])
        return own_low, own_high, other_low, other_high

    got_a, got_b = regroup(x_prompt[0], x_cont[0])
    own_valid = jnp.where(x == 0, prompt_valid.reshape(-1), cont_valid.reshape(-1))
    small_in = jnp.concatenate([own_valid, segment_ids.reshape(-1), offsets.reshape(-1)])
    small_len = small_in.shape[0]
    small_pad = -small_len % LANES
    small = ring.to_group(
        jnp.concatenate([small_in, jnp.zeros((small_pad,), jnp.int32)]).reshape(-1, LANES), 0
    ).reshape(-1)
    validity = small[:local].astype(F32)
    segment_row = small[local : local + PROMPT]
    offset_row = small[local + PROMPT : local + PROMPT + CONTS]
    tokens_b = feature_order(by_x(got_a, got_b), by_x(got_b, got_a))
    tokens = tokens_b.astype(F32)

    packed = jnp.concatenate(
        [
            w_forget.T.astype(F32),
            first_gain[None].astype(F32),
            second_gain[None].astype(F32),
            jnp.pad(forget_bias, (0, half_d - heads))[None],
        ],
        axis=0,
    )
    packed_there = ring.swap(packed, "zh")
    own_x = jnp.stack(
        [jnp.where(zh == 0, packed, packed_there), jnp.where(zh == 0, packed_there, packed)]
    )
    other_x = ring.swap(own_x, "x")
    both_x = feature_order(own_x, other_x)
    gain_one = both_x[0, heads]
    gain_two = both_x[0, heads + 1]

    def head_slots(value):
        first = jnp.where(y == 0, value[:, 0:2], value[:, 4:6])
        slot_a = jnp.where(zh == 0, first[0], first[1])
        slot_c = jnp.where(zh == 0, first[1], first[0])
        slot_b = jnp.where(y == 0, value[0, 2:4], value[1, 2:4])
        return jnp.concatenate([slot_a, slot_b, slot_c], axis=0)

    forget_t = head_slots(both_x[:, :heads]).astype(BF)
    bias_all = own_x[:, heads + 2, :heads]
    bias_row = head_slots(bias_all[:, :, None])[:, 0]
    bias_row = jnp.concatenate([bias_row, jnp.zeros((LANES - heads,), F32)])[None]
    w_forget_all = jnp.concatenate(
        [forget_t, jnp.zeros((LANES - heads, forget_t.shape[1]), BF)], axis=0
    ).T

    def rows_part(value):
        return lax.dynamic_slice_in_dim(value, c * part_d, part_d, 0)

    def cols_part(value):
        return lax.dynamic_slice_in_dim(value, c * part_d, part_d, 1)

    projections = [rows_part(w) for w in (w_query, w_outgate, w_key, w_value)]
    first_pairs = jnp.concatenate(
        [lax.dynamic_slice_in_dim(w, 2 * LANES * y, LANES, 1) for w in projections], axis=1
    )
    mid_pairs = jnp.concatenate([w[:, LANES : 2 * LANES] for w in projections], axis=1)
    third_pairs = ring.swap(first_pairs, "zh")
    mid_there = ring.swap(mid_pairs, "zh", lambda h: h["zh"] == h["y"])
    mid_pairs = jnp.where(owner, mid_pairs, mid_there)

    def whole_features(part):
        half = jnp.concatenate([part, ring.swap(part, "x")], axis=0)
        return jnp.concatenate([half, ring.swap(half, "c")], axis=0)

    w_slots = [whole_features(part) for part in (first_pairs, mid_pairs, third_pairs)]
    w_slots[0] = jnp.concatenate([w_slots[0], w_forget_all], axis=1)
    third_pairs, w_out, w_down, w_gate, w_up = lax.optimization_barrier(
        (third_pairs, w_out, w_down, w_gate, w_up)
    )

    out_part = cols_part(w_out)
    down_part = lax.dynamic_slice_in_dim(cols_part(w_down), y * half_units, half_units, 0)
    first_rows = lax.dynamic_slice_in_dim(out_part, 2 * LANES * y, LANES, 0)
    mid_rows = out_part[LANES : 2 * LANES]
    there = ring.swap(jnp.concatenate([first_rows, down_part], axis=0), "zh")
    mid_rows_there = ring.swap(mid_rows, "zh", lambda h: h["zh"] == h["y"])
    mid_rows = jnp.where(owner, mid_rows, mid_rows_there)
    back_part = jnp.concatenate(
        [first_rows, mid_rows, there[:LANES], down_part, there[LANES:]], axis=0
    )
    back_half = jnp.concatenate([back_part, ring.swap(back_part, "x")], axis=1)
    back_all = jnp.concatenate([back_half, ring.swap(back_half, "c")], axis=1)
    w_out_all = back_all[:width]
    w_down_all = back_all[width:]

    hidden_part = jnp.concatenate(
        [
            lax.dynamic_slice_in_dim(rows_part(w), y * half_units, half_units, 1)
            for w in (w_gate, w_up)
        ],
        axis=1,
    )
    hidden_part = jnp.concatenate([hidden_part, ring.swap(hidden_part, "zh")], axis=1)
    hidden_half = jnp.concatenate([hidden_part, ring.swap(hidden_part, "x")], axis=0)
    w_hidden = jnp.concatenate([hidden_half, ring.swap(hidden_half, "c")], axis=0)

    def chunk(value, k):
        return value[k * local : (k + 1) * local]

    dy_all = jnp.array([o[0] for o in ring.offsets], jnp.int32)
    dz_all = jnp.array([o[1] for o in ring.offsets], jnp.int32)
    places = ((y - dy_all) % 2) * zl_count + (zl - dz_all) % zl_count
    unit_no = (places[:, None] * chunk_units + jnp.arange(chunk_units, dtype=jnp.int32)).reshape(-1)
    natural = jnp.arange(pair_unit, dtype=jnp.int32)
    pick = unit_no[:, None] == natural[None, :]
    step = jnp.arange(CLEN, dtype=jnp.int32)
    row_pos = (unit_no[:, None] * CLEN + step[None, :]).reshape(-1)
    seg_rel = jnp.sum(
        jnp.where(pick[:, :, None], segment_row.reshape(1, pair_unit, CLEN), 0), axis=1
    )
    offs_rel = jnp.sum(jnp.where(pick, offset_row[None, :], 0), axis=1)
    last_rel = jnp.sum(
        jnp.where(
            jnp.arange(PROMPT, dtype=jnp.int32)[None, :] == offs_rel[:, None] - 1,
            segment_row[None, :],
            0,
        ),
        axis=1,
    )
    limit = jnp.where(c == 0, unit_no * CLEN, offs_rel)
    doc_row = jnp.where(c == 0, seg_rel, last_rel[:, None]).reshape(-1, 1)
    seg_col = seg_rel.reshape(-1, 1)
    lane = jnp.arange(LANES, dtype=jnp.int32)[None, :]
    unit_col = jnp.repeat(natural, CLEN)[:, None]
    pieces = 3 * heads
    is_doc = (lane >= DOC_LANE) & (lane < DOC_LANE + 4)
    is_unit = (lane >= UNIT_LANE) & (lane < UNIT_LANE + pair_unit)
    limit_lane = jnp.pad(limit, (UNIT_LANE, LANES - UNIT_LANE - pair_unit))[None, :]
    q_base = jnp.where(
        (lane >= FAR_PIECE) & (lane < FAR_PIECE + pieces),
        1.0,
        jnp.where(
            (is_doc & (doc_row != lane - DOC_LANE)) | (is_unit & (unit_col == lane - UNIT_LANE)),
            -NEVER,
            0.0,
        ),
    ).astype(BF)
    near_base = jnp.where(
        (lane < pieces) | (is_doc & (doc_row == lane - DOC_LANE)), 1.0, 0.0
    ).astype(BF)
    far_base = jnp.where(
        (lane < pieces)
        | (is_doc & (seg_col == lane - DOC_LANE))
        | (is_unit & (row_pos[:, None] >= limit_lane)),
        1.0,
        0.0,
    ).astype(BF)
    tri = (step[:, None] >= step[None, :]).astype(F32)
    earlier = (unit_no[None, :] < unit_no[:, None]).astype(F32)
    later = (unit_no[None, :] > unit_no[:, None]).astype(F32)
    hot = (row_pos[None, :] == limit[:, None] - 1).astype(F32)
    cont_hot = (row_pos[None, :] == offs_rel[:, None] - 1).astype(F32)

    factor_one, scaled_one, normed_one = full_norm(tokens, gain_one)
    normed_all = jnp.concatenate(ring.gather(normed_one), axis=0)
    normed_all, teacher_prompt, teacher_cont = lax.optimization_barrier(
        (normed_all, teacher_prompt, teacher_cont)
    )
    projects = [nn_dot(normed_all, w).astype(BF) for w in w_slots]
    kv_there = [ring.swap(p[:, 2 * LANES :], "c") for p in projects]
    forget_own = projects[0][:, 4 * LANES :]
    forget_far = jnp.where(c == 0, forget_own, kv_there[0][:, 2 * LANES :])
    flag = c.astype(jnp.int32).reshape(1)
    teach_a, teach_b = regroup(teacher_prompt[0], teacher_cont[0])
    head_lane = lane < heads

    def keep_log(lin):
        return jnp.where(head_lane, jax.nn.log_sigmoid(lin.astype(F32) + bias_row), 0.0)

    def within(values, matrix):
        return jnp.einsum(
            "ts,ush->uth", matrix, values.reshape(pair_unit, CLEN, LANES), precision=highest
        )

    far_within = within(keep_log(forget_far), tri)
    far_prefix = jnp.dot(earlier, far_within[:, -1], precision=highest)
    cum_far = (far_within + far_prefix[:, None]).reshape(-1, LANES)
    own_base = jnp.dot(hot, cum_far, precision=highest)
    cum_near = (within(keep_log(forget_own), tri) + own_base[:, None]).reshape(-1, LANES)
    gated, attended, logs = attend(
        flag, projects, kv_there, cum_near, cum_far, q_base, near_base, far_base, local, heads
    )
    residual = tokens + ring.scatter_sum(lambda k: nn_dot(chunk(gated, k), w_out_all))
    factor_two, scaled_two, normed_two = full_norm(residual, gain_two)
    normed_two_all = jnp.concatenate(ring.gather(normed_two), axis=0)
    gate_up = nn_dot(normed_two_all, w_hidden)

    def split_units(value):
        gate_rows = jnp.concatenate(
            [value[:, :half_units], value[:, 2 * half_units : 3 * half_units]], axis=1
        )
        up_rows = jnp.concatenate(
            [value[:, half_units : 2 * half_units], value[:, 3 * half_units :]], axis=1
        )
        return gate_rows, up_rows

    gate_rows, up_rows = split_units(gate_up)
    gate_sig = jax.nn.sigmoid(gate_rows)
    silu_rows = gate_rows * gate_sig
    hidden = (silu_rows * up_rows).astype(BF)
    result = residual + ring.scatter_sum(lambda k: nn_dot(chunk(hidden, k), w_down_all))

    teacher = feature_order(by_x(teach_a, teach_b), by_x(teach_b, teach_a)).astype(F32)
    deviation = result - teacher
    grad_result = validity[:, None] * deviation
    error_own = 0.5 * jnp.sum(grad_result * deviation)
    count_own = jnp.sum(validity)
    grad_result_all = jnp.concatenate(ring.gather(grad_result.astype(BF)), axis=0)
    grad_hid = nt_dot(grad_result_all, w_down_all)
    grad_gate = (grad_hid * up_rows * gate_sig * (1.0 + gate_rows * (1.0 - gate_sig))).astype(BF)
    grad_up = (grad_hid * silu_rows).astype(BF)
    grad_gate_up = jnp.concatenate(
        [
            grad_gate[:, :half_units],
            grad_up[:, :half_units],
            grad_gate[:, half_units:],
            grad_up[:, half_units:],
        ],
        axis=1,
    )
    grad_normed_two = ring.scatter_sum(lambda k: nt_dot(chunk(grad_gate_up, k), w_hidden))
    grad_down_w = tn_dot(hidden, grad_result_all)
    grad_hidden_w = tn_dot(normed_two_all, grad_gate_up)
    gain_two_grad, grad_residual = full_norm_back(
        grad_normed_two, factor_two, scaled_two, gain_two
    )
    grad_residual = grad_residual + grad_result
    grad_residual_all = jnp.concatenate(ring.gather(grad_residual.astype(BF)), axis=0)
    grad_gated = nt_dot(grad_residual_all, w_out_all)
    grad_out_w = tn_dot(gated, grad_residual_all)
    dqg, dkv_near, dkv_far, row_sum, near_sum, far_sum = attend_back(
        flag,
        projects,
        kv_there,
        cum_near,
        cum_far,
        q_base,
        near_base,
        far_base,
        grad_gated,
        attended,
        logs,
        local,
        heads,
    )
    prompt_here = c == 0

    def at_lane(value, first):
        return jnp.pad(value[:, first : first + heads], ((0, 0), (0, LANES - heads)))

    cum_grad = row_sum - at_lane(near_sum, FAR_PIECE)
    unit_total = jnp.sum(cum_grad.reshape(pair_unit, CLEN, LANES), axis=1)
    far_own = at_lane(far_sum, FAR_PIECE)
    dkv_there = ring.swap(dkv_far.astype(BF), "c")
    sums_there = ring.swap(jnp.concatenate([far_own, unit_total], axis=0), "c")
    dkv = jnp.where(prompt_here, dkv_near + dkv_far + dkv_there.astype(F32), dkv_near).astype(BF)
    total_rows = far_own.shape[0]
    prompt_cum = (
        cum_grad
        - far_own
        - sums_there[:total_rows]
        + jnp.dot(cont_hot.T, sums_there[total_rows:], precision=highest)
    )
    cum_grad = jnp.where(prompt_here, prompt_cum, cum_grad)
    log_within = within(cum_grad, tri.T)
    log_suffix = jnp.where(prompt_here, jnp.dot(later, log_within[:, 0], precision=highest), 0.0)
    log_grad = (log_within + log_suffix[:, None]).reshape(-1, LANES)
    pre_grad = jnp.where(
        head_lane, log_grad * jax.nn.sigmoid(-(forget_own.astype(F32) + bias_row)), 0.0
    )
    bias_grad = jnp.sum(pre_grad, axis=0)
    grad_slots = []
    for s in range(slots):
        cols = slice(2 * s * LANES, 2 * (s + 1) * LANES)
        grad_slots.append(jnp.concatenate([dqg[:, cols], dkv[:, cols]], axis=1))
    forget_b = pre_grad.astype(BF)
    project_grad = jnp.concatenate(grad_slots + [forget_b], axis=1)
    w_project = jnp.concatenate(
        [w_slots[0][:, : 4 * LANES], w_slots[1], w_slots[2], w_forget_all], axis=1
    )
    forget_gw = tn_dot(forget_b, normed_all)[:heads]

    def low(value):
        return lax.reduce_precision(value, 8, 7).astype(BF)

    def outer_sum(value):
        if ring.sizes["yo"] > 1:
            return lax.psum(low(value), "yo").astype(F32)
        return value

    def fold(value, axis, dim):
        size = value.shape[dim] // 2
        mine = lax.slice_in_dim(value, 0, size, axis=dim)
        theirs = lax.slice_in_dim(value, size, 2 * size, axis=dim)
        return mine + ring.swap(theirs.astype(BF), axis).astype(F32)

    def reduce_core_x(value, dim):
        return fold(fold(value, "c", dim), "x", dim)

    def both_parts(value, dim):
        other = ring.swap(value, "c")
        return jnp.concatenate(
            [jnp.where(c == 0, value, other), jnp.where(c == 0, other, value)], axis=dim
        )

    def reduce_pairs(first, mid, third, dim):
        first = first + ring.swap(third.astype(BF), "zh").astype(F32)
        mid = mid + ring.swap(mid.astype(BF), "zh", lambda h: h["zh"] != h["y"]).astype(F32)
        first = low(outer_sum(first))
        mid = low(outer_sum(mid))
        other = ring.swap(first, "y")
        mid_other = ring.swap(mid, "y", lambda h: h["zh"] == h["y"])
        mid = jnp.where(owner, mid, mid_other)
        pair_low = jnp.where(y == 0, first, other)
        pair_high = jnp.where(y == 0, other, first)
        return [both_parts(v, dim) for v in (pair_low, mid, pair_high)]

    def edge_sums(first, mid, third):
        first = first + ring.swap(third.astype(BF), "zh").astype(F32)
        mid = mid + ring.swap(mid.astype(BF), "zh", lambda h: h["zh"] != h["y"]).astype(F32)
        return low(outer_sum(first)), low(outer_sum(mid))

    down_mine = low(outer_sum(fold(reduce_core_x(grad_down_w, 1), "zh", 0)))
    hid_mine = low(outer_sum(fold(reduce_core_x(grad_hidden_w, 0), "zh", 1)))
    out_w = reduce_core_x(grad_out_w, 1)
    out_first, out_mid = edge_sums(*[out_w[s * LANES : (s + 1) * LANES] for s in range(slots)])
    rows_back, proj_all, gate_all, up_all, down_all, out_all, gain_all = last_step(
        ring,
        project_grad,
        w_project,
        normed_all,
        tokens_b,
        grad_residual,
        gain_one[None],
        hid_mine,
        down_mine,
        out_first,
        out_mid,
    )
    gain_one_sum = gain_all[:, 0].reshape(-1)
    projection_grads = [
        jnp.concatenate(
            [proj_all[:, (4 * s + i) * LANES : (4 * s + i + 1) * LANES] for s in range(slots)],
            axis=1,
        )
        for i in range(4)
    ]
    forget_w = reduce_core_x(forget_gw, 1)
    forget_grad = jnp.concatenate(
        reduce_pairs(forget_w[0:2], forget_w[2:4], forget_w[4:6], 1), axis=0
    ).T

    def all_features(value):
        own_low, own_high, other_low, other_high = natural_order(value)
        own = jnp.concatenate([own_low, own_high], axis=-1)
        other = jnp.concatenate([other_low, other_high], axis=-1)
        return jnp.concatenate(
            [jnp.where(x == 0, own, other), jnp.where(x == 0, other, own)], axis=-1
        )

    def place_heads(value):
        slot_a, slot_b, slot_c = value[0:2], value[2:4], value[4:6]
        blank = jnp.zeros_like(slot_a)
        rows_out = []
        for high in range(2):
            is_own = zh == high
            edge = jnp.where(is_own, slot_a, slot_c)
            mid = jnp.where(y == high, slot_b, blank)
            quarter = jnp.concatenate(
                [jnp.where(y == 0, edge, blank), mid, jnp.where(y == 1, edge, blank)], axis=0
            )
            for low_z in range(zl_count):
                rows_out.append(jnp.where(zl == low_z, quarter, jnp.zeros_like(quarter)))
        return jnp.concatenate(rows_out, axis=0)

    bias_place = place_heads(bias_grad[:heads, None])[:, 0]
    scalars = jnp.concatenate([error_own[None], count_own[None], bias_place])
    sums = ring.total(jnp.pad(scalars, (0, LANES - scalars.shape[0]))[None])[0]
    gain_two_sum = ring.total(all_features(gain_two_grad).reshape(-1, LANES)).reshape(-1)
    error_total = sums[0]
    count_total = sums[1]
    groups = ring.sizes["yo"] * ring.sizes["y"] * ring.sizes["c"]
    grad_scale = groups * (PROMPT + CONTS * CLEN) / count_total
    loss_value = error_total / (D * count_total)

    def own_half(value):
        return lax.dynamic_slice_in_dim(value, x * half_d, half_d, value.ndim - 1)

    quarter_no = zh * zl_count + zl
    bias_out = lax.dynamic_slice_in_dim(sums, 2 + quarter_no * heads, heads, 0)

    def scaled(value):
        return value.astype(F32) * grad_scale

    return (
        loss_value,
        scaled(rows_back[0])[None],
        scaled(rows_back[1]).reshape(1, local_conts, CLEN, half_d),
        scaled(own_half(gain_one_sum)),
        scaled(projection_grads[0]),
        scaled(projection_grads[2]),
        scaled(projection_grads[3]),
        scaled(projection_grads[1]),
        scaled(forget_grad),
        scaled(bias_out),
        scaled(out_all),
        scaled(own_half(gain_two_sum)),
        scaled(gate_all),
        scaled(up_all),
        scaled(down_all),
    )


def specs(dp, row, col):
    in_specs = (
        P(dp, col, row),
        P(dp, col, None, row),
        P(dp, col, row),
        P(dp, col, None, row),
        P(dp, None),
        P(dp, None),
        P(dp, col),
        P(dp, col, None),
        P(row),
        P(row, col),
        P(row, col),
        P(row, col),
        P(row, col),
        P(row, col),
        P(col),
        P(col, row),
        P(row),
        P(row, col),
        P(row, col),
        P(col, row),
    )
    out_specs = (
        P(),
        P(dp, col, row),
        P(dp, col, None, row),
        P(row),
        P(row, col),
        P(row, col),
        P(row, col),
        P(row, col),
        P(row, col),
        P(col),
        P(col, row),
        P(row),
        P(row, col),
        P(row, col),
        P(col, row),
    )
    return in_specs, out_specs


def solution(mesh):
    dp, row, col = mesh.shape["dp"], mesh.shape["row"], mesh.shape["col"]
    heads = HEADS // col
    if dp == 4 and row == 2 and col % 2 == 0 and heads == 6:
        sizes = {"yo": dp // 4, "y": 2, "c": 2, "x": 2, "zh": 2, "zl": col // 2}
        ring_mesh = Mesh(mesh.devices.reshape([sizes[a] for a in AX]), AX)
        in_specs, out_specs = specs(("yo", "y", "c"), "x", ("zh", "zl"))
        step = functools.partial(ring_body, Ring(sizes))
        return jax.shard_map(
            step, mesh=ring_mesh, in_specs=in_specs, out_specs=out_specs, check_vma=False
        )
    in_specs, out_specs = specs("dp", "row", "col")
    return jax.shard_map(
        wide_body, mesh=mesh, in_specs=in_specs, out_specs=out_specs, check_vma=False
    )
```

```python
import functools
import itertools

import jax
import jax.numpy as jnp
from jax import lax
from jax.experimental import pallas as pl
from jax.experimental.pallas import tpu as pltpu
from jax.sharding import Mesh, PartitionSpec as P

D = 1536
HEADS = 24
HEAD_DIM = 64
PROMPT = 1024
CONTS = 8
CLEN = 128


epsilon = 1e-06
highest = lax.Precision.HIGHEST
masked = -1e30


def matmul(left_op, right_op):
    return jnp.dot(left_op, right_op, preferred_element_type=jnp.float32)


def by_transpose(left_op, right_op):
    return lax.dot_general(
        left_op, right_op, (((1,), (1,)), ((), ())), preferred_element_type=jnp.float32
    )


def inner_rows(left_op, right_op):
    return lax.dot_general(
        left_op, right_op, (((0,), (0,)), ((), ())), preferred_element_type=jnp.float32
    )


def feature_total(partial_sum):
    return lax.psum(partial_sum, "row")


def group_rows(local_rows):
    return lax.all_gather(local_rows, "col", axis=0, tiled=True)


def token_sums(partial_rows):
    return lax.psum_scatter(
        partial_rows.astype(jnp.bfloat16), "col", scatter_dimension=0, tiled=True
    ).astype(jnp.float32)


def row_partials(partial_rows, col_count, blocks, quarter):
    shaped = partial_rows.reshape(
        col_count, blocks, lax.axis_size("row"), quarter, partial_rows.shape[-1]
    )
    return lax.psum_scatter(
        shaped.astype(jnp.bfloat16), "row", scatter_dimension=2, tiled=True
    ).astype(jnp.float32)


def head_rows(own_rows):
    gathered = lax.all_gather(own_rows, "row", axis=2, tiled=True)
    return gathered.reshape(-1, gathered.shape[-1])


def norm_forward(tokens, gain_vec):
    row_total = feature_total(jnp.sum(tokens * tokens, axis=-1))
    factor = lax.rsqrt(row_total / D + epsilon)
    scaled = tokens * factor[:, None]
    return (factor, scaled, (scaled * gain_vec).astype(jnp.bfloat16))


def norm_backward(grad_normed, factor, scaled, gain_vec):
    grad_scaled = grad_normed * gain_vec
    row_total = feature_total(jnp.sum(grad_scaled * scaled, axis=-1))
    gain_grad = jnp.sum(grad_normed * scaled, axis=0)
    return (gain_grad, factor[:, None] * (grad_scaled - scaled * (row_total / D)[:, None]))


def log_total(scores):
    row_top = jnp.max(scores, axis=-1, keepdims=True)
    return row_top + jnp.log(jnp.sum(jnp.exp(scores - row_top), axis=-1, keepdims=True))


def prompt_scores(queries, key_rows, cum_query, cum_key, allowed):
    raw_scores = jnp.einsum("qhd,khd->hqk", queries, key_rows, preferred_element_type=jnp.float32)
    raw_scores = raw_scores * HEAD_DIM ** (-0.5) + cum_query.T[:, :, None] - cum_key.T[:, None, :]
    return jnp.where(allowed[None], raw_scores, masked)


def cont_scores(queries, key_rows, key_cont, cum_query, cum_key, cum_cont, far_ok, near_ok):
    score_scale = HEAD_DIM ** (-0.5)
    query_cum = cum_query.transpose(0, 2, 1)[:, :, :, None]
    far_scores = jnp.einsum("jqhd,khd->jhqk", queries, key_rows, preferred_element_type=jnp.float32)
    far_scores = far_scores * score_scale + query_cum - cum_key.T[None, :, None, :]
    near_scores = jnp.einsum(
        "jqhd,jkhd->jhqk", queries, key_cont, preferred_element_type=jnp.float32
    )
    near_scores = near_scores * score_scale + query_cum - cum_cont.transpose(0, 2, 1)[:, :, None, :]
    far_scores = jnp.where(far_ok[:, None, None, :], far_scores, masked)
    near_scores = jnp.where(near_ok[None, None], near_scores, masked)
    return jnp.concatenate([far_scores, near_scores], axis=-1)


def wide_body(
    x_prompt,
    x_cont,
    teacher_prompt,
    teacher_cont,
    segment_ids,
    offsets,
    prompt_valid,
    cont_valid,
    first_gain,
    w_query,
    w_key,
    w_value,
    w_outgate,
    w_forget,
    forget_bias,
    w_out,
    second_gain,
    w_gate,
    w_up,
    w_down,
):
    row_count = lax.axis_size("row")
    col_count = lax.axis_size("col")
    row_index = lax.axis_index("row")
    local_prompt = x_prompt.shape[1]
    local_conts = x_cont.shape[1]
    quarter = CLEN // row_count
    local_tokens = local_prompt + local_conts * CLEN
    blocks = local_tokens // CLEN
    prompt_blocks = local_prompt // CLEN
    heads_here = w_forget.shape[1]
    width_here = heads_here * HEAD_DIM
    units_here = w_gate.shape[1]
    score_scale = HEAD_DIM ** (-0.5)
    w_project = jnp.concatenate([w_query, w_key, w_value, w_outgate], axis=1)
    w_hidden = jnp.concatenate([w_gate, w_up], axis=1)
    gain_one = first_gain.astype(jnp.float32)
    gain_two = second_gain.astype(jnp.float32)
    position = jnp.arange(PROMPT, dtype=jnp.int32)
    cont_step = jnp.arange(CLEN, dtype=jnp.int32)
    own_step = row_index * quarter + jnp.arange(quarter, dtype=jnp.int32)
    near_ok = cont_step[None, :] <= own_step[:, None]
    own_position = lax.dynamic_index_in_dim(
        position.reshape(col_count, prompt_blocks, row_count, quarter), row_index, 2, keepdims=False
    ).reshape(-1)

    def own_prompt_part(matrix):
        return matrix[:, :prompt_blocks, 0]

    def one_group(carried, group_data):
        (
            acc_project,
            acc_forget,
            acc_bias,
            acc_out,
            acc_hidden,
            acc_down,
            acc_gain_one,
            acc_gain_two,
            error_sum,
            count_sum,
        ) = carried
        (
            prompt_in,
            cont_in,
            teach_prompt,
            teach_cont,
            segment_row,
            offset_row,
            valid_prompt,
            valid_cont,
        ) = group_data
        tokens = jnp.concatenate(
            [prompt_in, cont_in.reshape(local_conts * CLEN, -1)], axis=0
        ).astype(jnp.float32)
        teacher = jnp.concatenate(
            [teach_prompt, teach_cont.reshape(local_conts * CLEN, -1)], axis=0
        ).astype(jnp.float32)
        validity = jnp.concatenate([valid_prompt, valid_cont.reshape(-1)], axis=0).astype(
            jnp.float32
        )
        branch_mask = position[None, :] == offset_row[:, None] - 1
        branch_hot = branch_mask.astype(jnp.float32)
        last_doc = jnp.sum(jnp.where(branch_mask, segment_row[None, :], 0), axis=1)
        far_ok = (position[None, :] < offset_row[:, None]) & (
            segment_row[None, :] == last_doc[:, None]
        )
        own_doc = lax.dynamic_index_in_dim(
            segment_row.reshape(col_count, prompt_blocks, row_count, quarter),
            row_index,
            2,
            keepdims=False,
        ).reshape(-1)
        prompt_ok = (position[None, :] <= own_position[:, None]) & (
            segment_row[None, :] == own_doc[:, None]
        )
        factor_one, scaled_one, normed_one = norm_forward(tokens, gain_one)
        normed_all = group_rows(normed_one)
        project_part = matmul(normed_all, w_project).reshape(
            col_count, blocks, row_count, quarter, 4 * width_here
        )
        forget_part = matmul(normed_all, w_forget).reshape(
            col_count, blocks, row_count, quarter, heads_here
        )
        own_project, own_forget = (
            lax.psum_scatter(project_part, "row", scatter_dimension=2, tiled=True),
            lax.psum_scatter(forget_part, "row", scatter_dimension=2, tiled=True),
        )
        own_query = own_project[..., :width_here].astype(jnp.bfloat16)
        own_kv = own_project[..., width_here : 3 * width_here].astype(jnp.bfloat16)
        gate_logit = own_project[..., 3 * width_here :]
        kv_all, forget_all = (
            lax.all_gather(own_kv, "row", axis=2, tiled=True),
            lax.all_gather(own_forget.astype(jnp.bfloat16), "row", axis=2, tiled=True),
        )
        kv_all = kv_all.reshape(col_count, local_tokens, 2 * width_here)
        pre_gate = (
            forget_all.reshape(col_count, local_tokens, heads_here).astype(jnp.float32)
            + forget_bias
        )
        log_keep = jax.nn.log_sigmoid(pre_gate)
        cum_prompt = jnp.cumsum(log_keep[:, :local_prompt].reshape(PROMPT, heads_here), axis=0)
        branch_cum = jnp.dot(branch_hot, cum_prompt, precision=highest)
        cum_cont = branch_cum[:, None, :] + jnp.cumsum(
            log_keep[:, local_prompt:].reshape(CONTS, CLEN, heads_here), axis=1
        )
        kv_prompt = kv_all[:, :local_prompt].reshape(PROMPT, 2, heads_here, HEAD_DIM)
        key_prompt = kv_prompt[:, 0]
        value_prompt = kv_prompt[:, 1]
        kv_cont = kv_all[:, local_prompt:].reshape(CONTS, CLEN, 2, heads_here, HEAD_DIM)
        key_cont = kv_cont[:, :, 0]
        value_cont = kv_cont[:, :, 1]
        cum_query_prompt = lax.dynamic_index_in_dim(
            cum_prompt.reshape(col_count, prompt_blocks, row_count, quarter, heads_here),
            row_index,
            2,
            keepdims=False,
        ).reshape(-1, heads_here)
        cum_query_cont = lax.dynamic_index_in_dim(
            cum_cont.reshape(CONTS, row_count, quarter, heads_here), row_index, 1, keepdims=False
        )
        query_prompt = own_prompt_part(own_query).reshape(-1, heads_here, HEAD_DIM)
        query_cont = own_query[:, prompt_blocks:, 0].reshape(CONTS, quarter, heads_here, HEAD_DIM)
        scores_prompt = prompt_scores(
            query_prompt, key_prompt, cum_query_prompt, cum_prompt, prompt_ok
        )
        total_prompt = log_total(scores_prompt)
        probs_prompt = jnp.exp(scores_prompt - total_prompt).astype(jnp.bfloat16)
        out_prompt = jnp.einsum(
            "hqk,khd->qhd", probs_prompt, value_prompt, preferred_element_type=jnp.float32
        )
        scores_cont = cont_scores(
            query_cont, key_prompt, key_cont, cum_query_cont, cum_prompt, cum_cont, far_ok, near_ok
        )
        total_cont = log_total(scores_cont)
        probs_cont = jnp.exp(scores_cont - total_cont).astype(jnp.bfloat16)
        out_cont = jnp.einsum(
            "jhqk,khd->jqhd",
            probs_cont[..., :PROMPT],
            value_prompt,
            preferred_element_type=jnp.float32,
        )
        out_cont = out_cont + jnp.einsum(
            "jhqk,jkhd->jqhd",
            probs_cont[..., PROMPT:],
            value_cont,
            preferred_element_type=jnp.float32,
        )
        attended = jnp.concatenate(
            [
                out_prompt.reshape(col_count, prompt_blocks, 1, quarter, width_here),
                out_cont.reshape(col_count, local_conts, 1, quarter, width_here),
            ],
            axis=1,
        )
        gate_sig = jax.nn.sigmoid(gate_logit)
        gated = (attended * gate_sig).astype(jnp.bfloat16)
        gated_all = head_rows(gated)
        residual = tokens + token_sums(matmul(gated_all, w_out))
        factor_two, scaled_two, normed_two = norm_forward(residual, gain_two)
        normed_two_all = group_rows(normed_two)
        hidden_own = row_partials(matmul(normed_two_all, w_hidden), col_count, blocks, quarter)
        gate_rows = hidden_own[..., :units_here]
        up_rows = hidden_own[..., units_here:]
        gate_sig_two = jax.nn.sigmoid(gate_rows)
        silu_rows = gate_rows * gate_sig_two
        hidden_all = head_rows((silu_rows * up_rows).astype(jnp.bfloat16))
        result_rows = residual + token_sums(matmul(hidden_all, w_down))
        deviation = result_rows - teacher
        group_err = 0.5 * jnp.sum(validity[:, None] * deviation * deviation)
        grad_result = validity[:, None] * deviation
        grad_result_all = group_rows(grad_result.astype(jnp.bfloat16))
        grad_down_w = inner_rows(hidden_all, grad_result_all)
        grad_hid = row_partials(by_transpose(grad_result_all, w_down), col_count, blocks, quarter)
        grad_gate = grad_hid * up_rows * gate_sig_two * (1.0 + gate_rows * (1.0 - gate_sig_two))
        grad_up = grad_hid * silu_rows
        grad_hidden_all = head_rows(
            jnp.concatenate([grad_gate, grad_up], axis=-1).astype(jnp.bfloat16)
        )
        grad_hidden_w = inner_rows(normed_two_all, grad_hidden_all)
        grad_normed_two = token_sums(by_transpose(grad_hidden_all, w_hidden))
        gain_two_grad, grad_residual = norm_backward(
            grad_normed_two, factor_two, scaled_two, gain_two
        )
        grad_residual = grad_residual + grad_result
        grad_residual_all = group_rows(grad_residual.astype(jnp.bfloat16))
        grad_out_w = inner_rows(gated_all, grad_residual_all)
        grad_gated = row_partials(
            by_transpose(grad_residual_all, w_out), col_count, blocks, quarter
        )
        grad_attended = (grad_gated * gate_sig).astype(jnp.bfloat16)
        grad_logit = (grad_gated * attended * gate_sig * (1.0 - gate_sig)).astype(jnp.bfloat16)
        grad_att_prompt = own_prompt_part(grad_attended).reshape(-1, heads_here, HEAD_DIM)
        grad_att_cont = grad_attended[:, prompt_blocks:, 0].reshape(
            CONTS, quarter, heads_here, HEAD_DIM
        )
        again_prompt = jnp.exp(
            prompt_scores(query_prompt, key_prompt, cum_query_prompt, cum_prompt, prompt_ok)
            - total_prompt
        )
        grad_prob_prompt = jnp.einsum(
            "qhd,khd->hqk", grad_att_prompt, value_prompt, preferred_element_type=jnp.float32
        )
        grad_score_prompt = (
            again_prompt
            * (grad_prob_prompt - jnp.sum(again_prompt * grad_prob_prompt, axis=-1, keepdims=True))
        ).astype(jnp.bfloat16)
        again_prompt_b = again_prompt.astype(jnp.bfloat16)
        grad_query_prompt = (
            jnp.einsum(
                "hqk,khd->qhd", grad_score_prompt, key_prompt, preferred_element_type=jnp.float32
            )
            * score_scale
        )
        grad_key_prompt = (
            jnp.einsum(
                "hqk,qhd->khd", grad_score_prompt, query_prompt, preferred_element_type=jnp.float32
            )
            * score_scale
        )
        grad_value_prompt = jnp.einsum(
            "hqk,qhd->khd", again_prompt_b, grad_att_prompt, preferred_element_type=jnp.float32
        )
        cum_grad_query_p = jnp.sum(grad_score_prompt, axis=-1, dtype=jnp.float32).T
        cum_grad_key_p = -jnp.sum(grad_score_prompt, axis=1, dtype=jnp.float32).T
        again_cont = jnp.exp(
            cont_scores(
                query_cont,
                key_prompt,
                key_cont,
                cum_query_cont,
                cum_prompt,
                cum_cont,
                far_ok,
                near_ok,
            )
            - total_cont
        )
        grad_prob_cont = jnp.concatenate(
            [
                jnp.einsum(
                    "jqhd,khd->jhqk",
                    grad_att_cont,
                    value_prompt,
                    preferred_element_type=jnp.float32,
                ),
                jnp.einsum(
                    "jqhd,jkhd->jhqk", grad_att_cont, value_cont, preferred_element_type=jnp.float32
                ),
            ],
            axis=-1,
        )
        grad_score_cont = (
            again_cont
            * (grad_prob_cont - jnp.sum(again_cont * grad_prob_cont, axis=-1, keepdims=True))
        ).astype(jnp.bfloat16)
        again_cont_b = again_cont.astype(jnp.bfloat16)
        far_grad = grad_score_cont[..., :PROMPT]
        near_grad = grad_score_cont[..., PROMPT:]
        grad_query_cont = (
            jnp.einsum("jhqk,khd->jqhd", far_grad, key_prompt, preferred_element_type=jnp.float32)
            + jnp.einsum("jhqk,jkhd->jqhd", near_grad, key_cont, preferred_element_type=jnp.float32)
        ) * score_scale
        grad_key_far = (
            jnp.einsum("jhqk,jqhd->khd", far_grad, query_cont, preferred_element_type=jnp.float32)
            * score_scale
        )
        grad_key_near = (
            jnp.einsum("jhqk,jqhd->jkhd", near_grad, query_cont, preferred_element_type=jnp.float32)
            * score_scale
        )
        grad_value_far = jnp.einsum(
            "jhqk,jqhd->khd",
            again_cont_b[..., :PROMPT],
            grad_att_cont,
            preferred_element_type=jnp.float32,
        )
        grad_value_near = jnp.einsum(
            "jhqk,jqhd->jkhd",
            again_cont_b[..., PROMPT:],
            grad_att_cont,
            preferred_element_type=jnp.float32,
        )
        cum_grad_query_c = jnp.sum(grad_score_cont, axis=-1, dtype=jnp.float32).transpose(0, 2, 1)
        cum_grad_key_far = -jnp.sum(far_grad, axis=(0, 2), dtype=jnp.float32).T
        cum_grad_key_near = -jnp.sum(near_grad, axis=2, dtype=jnp.float32).transpose(0, 2, 1)
        kv_grad_prompt = jnp.stack(
            [grad_key_prompt + grad_key_far, grad_value_prompt + grad_value_far], axis=1
        ).reshape(col_count, local_prompt, 2 * width_here)
        kv_grad_cont = jnp.stack([grad_key_near, grad_value_near], axis=2).reshape(
            col_count, local_conts * CLEN, 2 * width_here
        )
        kv_grad_part = jnp.concatenate([kv_grad_prompt, kv_grad_cont], axis=1)
        query_place = lax.dynamic_update_slice_in_dim(
            jnp.zeros((col_count, prompt_blocks, row_count, quarter, heads_here), jnp.float32),
            cum_grad_query_p.reshape(col_count, prompt_blocks, 1, quarter, heads_here),
            row_index,
            axis=2,
        ).reshape(PROMPT, heads_here)
        cont_place = lax.dynamic_update_slice_in_dim(
            jnp.zeros((CONTS, row_count, quarter, heads_here), jnp.float32),
            cum_grad_query_c.reshape(CONTS, 1, quarter, heads_here),
            row_index,
            axis=1,
        ).reshape(CONTS, CLEN, heads_here)
        cum_grad_part = jnp.concatenate(
            [
                (cum_grad_key_p + cum_grad_key_far + query_place).reshape(
                    col_count, local_prompt, heads_here
                ),
                (cum_grad_key_near + cont_place).reshape(col_count, local_conts * CLEN, heads_here),
            ],
            axis=1,
        )
        kv_grad_full, cum_grad_full = lax.psum((kv_grad_part, cum_grad_part), "row")
        cum_grad_cont = cum_grad_full[:, local_prompt:].reshape(CONTS, CLEN, heads_here)
        cum_grad_prompt = cum_grad_full[:, :local_prompt].reshape(PROMPT, heads_here)
        cum_grad_prompt = cum_grad_prompt + jnp.dot(
            branch_hot.T, jnp.sum(cum_grad_cont, axis=1), precision=highest
        )
        log_grad_prompt = lax.cumsum(cum_grad_prompt, axis=0, reverse=True)
        log_grad_cont = lax.cumsum(cum_grad_cont, axis=1, reverse=True)
        log_grad = jnp.concatenate(
            [
                log_grad_prompt.reshape(col_count, local_prompt, heads_here),
                log_grad_cont.reshape(col_count, local_conts * CLEN, heads_here),
            ],
            axis=1,
        )
        pre_grad = log_grad * jax.nn.sigmoid(-pre_gate)
        bias_grad = jnp.sum(pre_grad, axis=(0, 1))
        forget_grad_b = pre_grad.reshape(-1, heads_here).astype(jnp.bfloat16)
        query_grad_own = jnp.concatenate(
            [
                grad_query_prompt.reshape(col_count, prompt_blocks, 1, quarter, width_here),
                grad_query_cont.reshape(col_count, local_conts, 1, quarter, width_here),
            ],
            axis=1,
        )
        qg_grad_all = head_rows(
            jnp.concatenate([query_grad_own.astype(jnp.bfloat16), grad_logit], axis=-1)
        )
        kv_grad_rows = kv_grad_full.reshape(-1, 2 * width_here).astype(jnp.bfloat16)
        project_grad_rows = jnp.concatenate(
            [qg_grad_all[:, :width_here], kv_grad_rows, qg_grad_all[:, width_here:]], axis=-1
        )
        grad_project_w = inner_rows(normed_all, project_grad_rows)
        grad_forget_w = inner_rows(normed_all, forget_grad_b)
        grad_normed_one = token_sums(
            by_transpose(project_grad_rows, w_project) + by_transpose(forget_grad_b, w_forget)
        )
        gain_one_grad, grad_tokens = norm_backward(
            grad_normed_one, factor_one, scaled_one, gain_one
        )
        grad_tokens = grad_tokens + grad_residual
        grad_prompt_one = grad_tokens[:local_prompt]
        grad_cont_one = grad_tokens[local_prompt:].reshape(local_conts, CLEN, -1)
        group_count = jnp.sum(validity) * (row_index == 0).astype(jnp.float32)
        new_carry = (
            acc_project + grad_project_w,
            acc_forget + grad_forget_w,
            acc_bias + bias_grad,
            acc_out + grad_out_w,
            acc_hidden + grad_hidden_w,
            acc_down + grad_down_w,
            acc_gain_one + gain_one_grad,
            acc_gain_two + gain_two_grad,
            error_sum + group_err,
            count_sum + group_count,
        )
        return (new_carry, (grad_prompt_one, grad_cont_one))

    start = (
        jnp.zeros(w_project.shape, jnp.float32),
        jnp.zeros(w_forget.shape, jnp.float32),
        jnp.zeros(forget_bias.shape, jnp.float32),
        jnp.zeros(w_out.shape, jnp.float32),
        jnp.zeros(w_hidden.shape, jnp.float32),
        jnp.zeros(w_down.shape, jnp.float32),
        jnp.zeros(first_gain.shape, jnp.float32),
        jnp.zeros(second_gain.shape, jnp.float32),
        jnp.zeros((), jnp.float32),
        jnp.zeros((), jnp.float32),
    )
    finished, (grad_prompt, grad_cont) = lax.scan(
        one_group,
        start,
        (
            x_prompt,
            x_cont,
            teacher_prompt,
            teacher_cont,
            segment_ids,
            offsets,
            prompt_valid,
            cont_valid,
        ),
    )
    (
        acc_project,
        acc_forget,
        acc_bias,
        acc_out,
        acc_hidden,
        acc_down,
        acc_gain_one,
        acc_gain_two,
        error_sum,
        count_sum,
    ) = finished
    acc_project, acc_forget, acc_bias, acc_out, acc_hidden, acc_down = (
        lax.psum(acc_project.astype(jnp.bfloat16), "dp").astype(jnp.float32),
        lax.psum(acc_forget.astype(jnp.bfloat16), "dp").astype(jnp.float32),
        lax.psum(acc_bias.astype(jnp.bfloat16), "dp").astype(jnp.float32),
        lax.psum(acc_out.astype(jnp.bfloat16), "dp").astype(jnp.float32),
        lax.psum(acc_hidden.astype(jnp.bfloat16), "dp").astype(jnp.float32),
        lax.psum(acc_down.astype(jnp.bfloat16), "dp").astype(jnp.float32),
    )
    gain_one_total, gain_two_total = lax.psum((acc_gain_one, acc_gain_two), ("dp", "col"))
    error_total, count_total = lax.psum((error_sum, count_sum), ("dp", "row", "col"))
    grad_scale = x_prompt.shape[0] * lax.axis_size("dp") * (PROMPT + CONTS * CLEN) / count_total
    loss_value = error_total / (D * count_total)
    width_here = w_query.shape[1]
    units_here = w_gate.shape[1]
    return (
        loss_value,
        grad_prompt * grad_scale,
        grad_cont * grad_scale,
        gain_one_total * grad_scale,
        acc_project[:, :width_here] * grad_scale,
        acc_project[:, width_here : 2 * width_here] * grad_scale,
        acc_project[:, 2 * width_here : 3 * width_here] * grad_scale,
        acc_project[:, 3 * width_here :] * grad_scale,
        acc_forget * grad_scale,
        acc_bias * grad_scale,
        acc_out * grad_scale,
        gain_two_total * grad_scale,
        acc_hidden[:, :units_here] * grad_scale,
        acc_hidden[:, units_here:] * grad_scale,
        acc_down * grad_scale,
    )


AX = ("yo", "y", "c", "x", "zh", "zl")
FAR_PIECE = 18
DOC_LANE = 36
UNIT_LANE = 40
NEVER = 1e12
LANES = 128
BF = jnp.bfloat16
F32 = jnp.float32


class Ring:
    def __init__(self, sizes):
        self.sizes = sizes
        self.zl_count = sizes["zl"]
        self.offsets = [(dy, dz) for dy in range(2) for dz in range(self.zl_count)]
        self.back = [
            self.offsets.index(((-dy) % 2, (-dz) % self.zl_count)) for dy, dz in self.offsets
        ]

    def pairs(self, target, source_ok=None):
        ranges = [range(self.sizes[a]) for a in AX]
        number = {}
        for place, coords in enumerate(itertools.product(*ranges)):
            number[coords] = place
        out = []
        for coords in number:
            here = dict(zip(AX, coords))
            if source_ok is not None and not source_ok(here):
                continue
            there = dict(here, **target(here))
            out.append((number[coords], number[tuple(there[a] for a in AX)]))
        return out

    def move(self, value, target, source_ok=None):
        return lax.ppermute(value, AX, self.pairs(target, source_ok))

    def swap(self, value, axis, source_ok=None):
        return self.move(value, lambda h: {axis: 1 - h[axis]}, source_ok)

    def to_peer(self, value, k):
        dy, dz = self.offsets[k]
        return self.move(
            value, lambda h: {"y": (h["y"] + dy) % 2, "zl": (h["zl"] + dz) % self.zl_count}
        )

    def to_group(self, value, flip):
        return self.move(
            value,
            lambda h: {
                "y": h["zh"],
                "c": h["x"] ^ flip,
                "x": h["y"],
                "zh": h["c"],
            },
        )

    def from_group(self, value, flip):
        return self.move(
            value,
            lambda h: {"y": h["x"], "c": h["zh"], "x": h["c"] ^ flip, "zh": h["y"]},
        )

    def total(self, value):
        for axis in ("c", "y", "x", "zh"):
            value = value + self.swap(value, axis)
        if self.zl_count == 2:
            value = value + self.swap(value, "zl")
        elif self.zl_count > 2:
            value = lax.psum(value, "zl")
        if self.sizes["yo"] > 1:
            value = lax.psum(value, "yo")
        return value

    def gather(self, rows):
        return [rows] + [self.to_peer(rows, k) for k in range(1, len(self.offsets))]

    def scatter_sum(self, partial_of):
        arrived = []
        for k in range(1, len(self.offsets)):
            arrived.append(self.to_peer(partial_of(self.back[k]).astype(BF), k))
        total = partial_of(0)
        for part in arrived:
            total = total + part.astype(F32)
        return total


def nt_dot(left_op, right_op):
    return lax.dot_general(
        left_op, right_op, (((1,), (1,)), ((), ())), preferred_element_type=F32
    )


def tn_dot(left_op, right_op):
    return lax.dot_general(
        left_op, right_op, (((0,), (0,)), ((), ())), preferred_element_type=F32
    )


def nn_dot(left_op, right_op):
    return jnp.dot(left_op, right_op, preferred_element_type=F32)


def split_pieces(values, shift, heads):
    high = values.astype(BF).astype(F32)
    rest = values - high
    mid = rest.astype(BF).astype(F32)
    low = (rest - mid).astype(BF).astype(F32)
    out = None
    for place, piece in enumerate((high, mid, low)):
        amount = shift + place * heads
        moved = pltpu.roll(piece, amount, 1) if amount else piece
        out = moved if out is None else out + moved
    return out


def head_lanes(shape, head, heads):
    lane = lax.broadcasted_iota(jnp.int32, shape, len(shape) - 1)
    keep = lane >= DOC_LANE
    for place in range(3):
        keep = keep | (lane == place * heads + head) | (lane == FAR_PIECE + place * heads + head)
    return keep


def half_lanes(shape, half):
    lane = lax.broadcasted_iota(jnp.int32, shape, len(shape) - 1)
    return (lane >= HEAD_DIM * half) & (lane < HEAD_DIM * (half + 1))


def near_visible(rows):
    key_row = lax.broadcasted_iota(jnp.int32, (rows, rows), 0)
    query_row = lax.broadcasted_iota(jnp.int32, (rows, rows), 1)
    same = (key_row // CLEN) == (query_row // CLEN)
    return same & (key_row <= query_row)


def fill_keys(
    keys, flag, far_own, far_there, kv_near, cum_far, cum_near, far_base, near_base, far_rows, heads
):
    slots = heads // 2

    @pl.when(pl.program_id(0) == 0)
    def _():
        aug = (far_base[...].astype(F32) + split_pieces(-cum_far[...], FAR_PIECE, heads)).astype(BF)
        for s in range(slots):
            keys[s, :far_rows, LANES:] = aug

        @pl.when(flag[0] == 0)
        def _():
            for s in range(slots):
                keys[s, :far_rows, :LANES] = far_own[s][:, :LANES]

        @pl.when(flag[0] != 0)
        def _():
            for s in range(slots):
                keys[s, :far_rows, :LANES] = far_there[s][:, :LANES]

    aug = (near_base[...].astype(F32) + split_pieces(-cum_near[...], FAR_PIECE, heads)).astype(BF)
    for s in range(slots):
        keys[s, far_rows:, :LANES] = kv_near[s][:, :LANES]
        keys[s, far_rows:, LANES:] = aug


def attend_kernel(
    heads,
    flag,
    qg_a,
    qg_b,
    qg_c,
    near_a,
    near_b,
    near_c,
    own_a,
    own_b,
    own_c,
    there_a,
    there_b,
    there_c,
    cum_near,
    cum_far,
    q_base,
    near_base,
    far_base,
    gated_ref,
    att_ref,
    log_ref,
    keys,
    vals,
):
    qg = (qg_a, qg_b, qg_c)
    kv_near = (near_a, near_b, near_c)
    far_own = (own_a, own_b, own_c)
    far_there = (there_a, there_b, there_c)
    rows = qg_a.shape[0]
    far_rows = own_a.shape[0]
    slots = heads // 2
    fill_keys(
        keys,
        flag,
        far_own,
        far_there,
        kv_near,
        cum_far,
        cum_near,
        far_base,
        near_base,
        far_rows,
        heads,
    )

    @pl.when(pl.program_id(0) == 0)
    def _():
        def fill(source):
            for s in range(slots):
                moved = source[s][:, LANES:].T
                for half in range(2):
                    vals[2 * s + half, :HEAD_DIM, :far_rows] = moved[
                        HEAD_DIM * half : HEAD_DIM * (half + 1)
                    ]

        @pl.when(flag[0] == 0)
        def _():
            fill(far_own)

        @pl.when(flag[0] != 0)
        def _():
            fill(far_there)

        for h in range(heads):
            vals[h, HEAD_DIM:, :] = jnp.ones((16, far_rows + rows), BF)

    for s in range(slots):
        moved = kv_near[s][:, LANES:].T
        for half in range(2):
            vals[2 * s + half, :HEAD_DIM, far_rows:] = moved[
                HEAD_DIM * half : HEAD_DIM * (half + 1)
            ]
    q_aug = (q_base[...].astype(F32) + split_pieces(cum_near[...], 0, heads)).astype(BF)
    visible = near_visible(rows)
    outs = []
    logs = []
    for h in range(heads):
        s, half = h // 2, h % 2
        query = qg[s][:, :LANES]
        query = jnp.where(half_lanes(query.shape, half), query * BF(HEAD_DIM**-0.5), BF(0))
        aug = jnp.where(head_lanes(q_aug.shape, h, heads), q_aug, BF(0))
        q_cat = jnp.concatenate([query, aug], axis=1)
        far = nt_dot(keys[s, :far_rows], q_cat)
        near = jnp.where(visible, nt_dot(keys[s, far_rows:], q_cat), -NEVER)
        top = jnp.maximum(
            jnp.max(far, axis=0, keepdims=True), jnp.max(near, axis=0, keepdims=True)
        )
        far_p = jnp.exp(far - top).astype(BF)
        near_p = jnp.exp(near - top).astype(BF)
        out = nn_dot(vals[h, :, :far_rows], far_p) + nn_dot(vals[h, :, far_rows:], near_p)
        total = out[HEAD_DIM : HEAD_DIM + 1]
        outs.append(out[:HEAD_DIM] / total)
        logs.append(top + jnp.log(total))
    att = jnp.concatenate(outs, axis=0).T
    att_ref[...] = att
    for s in range(slots):
        gate = qg[s][:, LANES:].astype(F32)
        cols = slice(s * LANES, (s + 1) * LANES)
        gated_ref[:, cols] = (att[:, cols] * jax.nn.sigmoid(gate)).astype(BF)
    log_rows = jnp.concatenate(logs + [jnp.zeros((LANES - heads, rows), F32)], axis=0)
    log_ref[...] = log_rows.T


def row_block(rows, cols, place=0):
    return pl.BlockSpec((rows, cols), lambda i: (i, place))


def whole_block(rows, cols):
    return pl.BlockSpec((rows, cols), lambda i: (0, 0))


def slot_inputs(flag, projects, kv_there, rows):
    far_rows = projects[0].shape[0]
    specs_in = [pl.BlockSpec(memory_space=pltpu.SMEM)]
    for spec in (
        row_block(rows, 2 * LANES),
        row_block(rows, 2 * LANES, 1),
        pl.BlockSpec((far_rows, 2 * LANES), lambda i: (0, 1)),
        whole_block(far_rows, 2 * LANES),
    ):
        specs_in += [spec] * len(projects)
    return specs_in, [flag, *projects, *projects, *projects, *kv_there]


def cum_specs(rows, far_rows):
    return [
        row_block(rows, LANES),
        whole_block(far_rows, LANES),
        row_block(rows, LANES),
        row_block(rows, LANES),
        whole_block(far_rows, LANES),
    ]


def attend(flag, projects, kv_there, cum_near, cum_far, q_base, near_base, far_base, rows, heads):
    total = projects[0].shape[0]
    width = heads * HEAD_DIM
    steps = total // rows
    flops = 2 * total * (total + rows) * heads * 384
    slot_specs, slot_values = slot_inputs(flag, projects, kv_there, rows)
    return pl.pallas_call(
        functools.partial(attend_kernel, heads),
        grid=(steps,),
        out_shape=(
            jax.ShapeDtypeStruct((total, width), BF),
            jax.ShapeDtypeStruct((total, width), F32),
            jax.ShapeDtypeStruct((total, LANES), F32),
        ),
        in_specs=slot_specs + cum_specs(rows, total),
        out_specs=(row_block(rows, width), row_block(rows, width), row_block(rows, LANES)),
        scratch_shapes=[
            pltpu.VMEM((heads // 2, total + rows, 2 * LANES), BF),
            pltpu.VMEM((heads, HEAD_DIM + 16, total + rows), BF),
        ],
        compiler_params=pltpu.CompilerParams(vmem_limit_bytes=48 << 20),
        cost_estimate=pl.CostEstimate(
            flops=flops, bytes_accessed=total * width * 20, transcendentals=total * total * heads
        ),
    )(*slot_values, cum_near, cum_far, q_base, near_base, far_base)


def attend_back_kernel(
    heads,
    flag,
    qg_a,
    qg_b,
    qg_c,
    near_a,
    near_b,
    near_c,
    own_a,
    own_b,
    own_c,
    there_a,
    there_b,
    there_c,
    cum_near,
    cum_far,
    q_base,
    near_base,
    far_base,
    grad_ref,
    att_ref,
    log_ref,
    dqg_ref,
    near_ref,
    far_ref,
    row_ref,
    near_col,
    far_col,
    keys,
    vals,
):
    qg = (qg_a, qg_b, qg_c)
    kv_near = (near_a, near_b, near_c)
    far_own = (own_a, own_b, own_c)
    far_there = (there_a, there_b, there_c)
    rows = qg_a.shape[0]
    far_rows = own_a.shape[0]
    slots = heads // 2
    fill_keys(
        keys,
        flag,
        far_own,
        far_there,
        kv_near,
        cum_far,
        cum_near,
        far_base,
        near_base,
        far_rows,
        heads,
    )

    @pl.when(pl.program_id(0) == 0)
    def _():
        lane = lax.broadcasted_iota(jnp.int32, (far_rows + rows, LANES), 1)
        ones = (lane < 3).astype(F32).astype(BF)
        for s in range(slots):
            vals[s, :, LANES:] = ones

        @pl.when(flag[0] == 0)
        def _():
            for s in range(slots):
                vals[s, :far_rows, :LANES] = far_own[s][:, LANES:]

        @pl.when(flag[0] != 0)
        def _():
            for s in range(slots):
                vals[s, :far_rows, :LANES] = far_there[s][:, LANES:]

        far_ref[...] = jnp.zeros(far_ref.shape, F32)
        far_col[...] = jnp.zeros(far_col.shape, F32)

    for s in range(slots):
        vals[s, far_rows:, :LANES] = kv_near[s][:, LANES:]
    q_aug = (q_base[...].astype(F32) + split_pieces(cum_near[...] - log_ref[...], 0, heads)).astype(
        BF
    )
    visible = near_visible(rows)
    lane = lax.broadcasted_iota(jnp.int32, (rows, LANES), 1)
    row_total = jnp.zeros((rows, LANES), F32)
    col_total = jnp.zeros((rows, LANES), F32)
    for s in range(slots):
        cols = slice(s * LANES, (s + 1) * LANES)
        kcols = slice(2 * s * LANES, (2 * s + 1) * LANES)
        vcols = slice((2 * s + 1) * LANES, (2 * s + 2) * LANES)
        gate_sig = jax.nn.sigmoid(qg[s][:, LANES:].astype(F32))
        grad = grad_ref[:, cols].astype(F32)
        att = att_ref[:, cols]
        grad_att = (grad * gate_sig).astype(BF)
        dqg_ref[:, vcols] = (grad * att * gate_sig * (1.0 - gate_sig)).astype(BF)
        weighed = grad_att.astype(F32) * att
        dq_total = jnp.zeros((rows, LANES), F32)
        dk_near = jnp.zeros((rows, LANES), F32)
        dv_near = jnp.zeros((rows, LANES), F32)
        for half in range(2):
            h = 2 * s + half
            mine = half_lanes((rows, LANES), half)
            query = jnp.where(mine, qg[s][:, :LANES] * BF(HEAD_DIM**-0.5), BF(0))
            aug = jnp.where(head_lanes(q_aug.shape, h, heads), q_aug, BF(0))
            q_cat = jnp.concatenate([query, aug], axis=1)
            ga = jnp.where(mine, grad_att, BF(0))
            delta = -jnp.sum(jnp.where(mine, weighed, 0.0), axis=1, keepdims=True)
            high = delta.astype(BF).astype(F32)
            mid = (delta - high).astype(BF).astype(F32)
            low = delta - high - mid
            d_aug = jnp.where(
                lane == 0, high, jnp.where(lane == 1, mid, jnp.where(lane == 2, low, 0.0))
            ).astype(BF)
            ga_cat = jnp.concatenate([ga, d_aug], axis=1)
            for part in range(2):
                span = slice(0, far_rows) if part == 0 else slice(far_rows, far_rows + rows)
                prob = jnp.exp(nt_dot(keys[s, span], q_cat))
                if part == 1:
                    prob = jnp.where(visible, prob, 0.0)
                ds = (prob * nt_dot(vals[s, span], ga_cat)).astype(BF)
                dv = nn_dot(prob.astype(BF), ga)
                dk = nn_dot(ds, q_cat)
                dq = tn_dot(ds, keys[s, span])
                dq_total += jnp.where(mine, dq[:, :LANES], 0.0)
                row_total += jnp.where(lane == h, dq[:, LANES:], 0.0)
                if part == 0:
                    far_ref[:, kcols] += dk[:, :LANES]
                    far_ref[:, vcols] += dv
                    far_col[...] += dk[:, LANES:]
                else:
                    dk_near += dk[:, :LANES]
                    dv_near += dv
                    col_total += dk[:, LANES:]
        dqg_ref[:, kcols] = (dq_total * HEAD_DIM**-0.5).astype(BF)
        near_ref[:, kcols] = dk_near
        near_ref[:, vcols] = dv_near
    row_ref[...] = row_total
    near_col[...] = col_total


def attend_back(
    flag,
    projects,
    kv_there,
    cum_near,
    cum_far,
    q_base,
    near_base,
    far_base,
    grad,
    att,
    logs,
    rows,
    heads,
):
    total = projects[0].shape[0]
    width = heads * HEAD_DIM
    steps = total // rows
    flops = 2 * total * (total + rows) * heads * 1152
    slot_specs, slot_values = slot_inputs(flag, projects, kv_there, rows)
    return pl.pallas_call(
        functools.partial(attend_back_kernel, heads),
        grid=(steps,),
        out_shape=(
            jax.ShapeDtypeStruct((total, 2 * width), BF),
            jax.ShapeDtypeStruct((total, 2 * width), F32),
            jax.ShapeDtypeStruct((total, 2 * width), F32),
            jax.ShapeDtypeStruct((total, LANES), F32),
            jax.ShapeDtypeStruct((total, LANES), F32),
            jax.ShapeDtypeStruct((total, LANES), F32),
        ),
        in_specs=slot_specs
        + cum_specs(rows, total)
        + [row_block(rows, width), row_block(rows, width), row_block(rows, LANES)],
        out_specs=(
            row_block(rows, 2 * width),
            row_block(rows, 2 * width),
            whole_block(total, 2 * width),
            row_block(rows, LANES),
            row_block(rows, LANES),
            whole_block(total, LANES),
        ),
        scratch_shapes=[
            pltpu.VMEM((heads // 2, total + rows, 2 * LANES), BF),
            pltpu.VMEM((heads // 2, total + rows, 2 * LANES), BF),
        ],
        compiler_params=pltpu.CompilerParams(vmem_limit_bytes=56 << 20),
        cost_estimate=pl.CostEstimate(
            flops=flops, bytes_accessed=total * width * 40, transcendentals=total * total * heads
        ),
    )(*slot_values, cum_near, cum_far, q_base, near_base, far_base, grad, att, logs)


def full_norm(tokens, gain_vec):
    factor = lax.rsqrt(jnp.mean(tokens * tokens, axis=-1, keepdims=True) + epsilon)
    scaled = tokens * factor
    return factor, scaled, (scaled * gain_vec).astype(BF)


def full_norm_back(grad_normed, factor, scaled, gain_vec):
    e = grad_normed * gain_vec
    mean = jnp.mean(e * scaled, axis=-1, keepdims=True)
    return jnp.sum(grad_normed * scaled, axis=0), factor * (e - scaled * mean)


MESH_ID = pl.DeviceIdType.MESH


class Here:
    def __init__(self, ring):
        self.ring = ring
        self.at = {a: lax.axis_index(a) for a in AX}

    def other(self, axis):
        return {axis: 1 - self.at[axis]}

    def peer(self, k):
        dy, dz = self.ring.offsets[k]
        return {
            "y": lax.rem(self.at["y"] + dy, 2),
            "zl": lax.rem(self.at["zl"] + dz, self.ring.zl_count),
        }

    def group_to(self, flip):
        at = self.at
        return {"y": at["zh"], "c": at["x"] ^ flip, "x": at["y"], "zh": at["c"]}

    def group_from(self, flip):
        at = self.at
        return {"y": at["x"], "c": at["zh"], "x": at["c"] ^ flip, "zh": at["y"]}

    def group_away(self):
        at = self.at
        return ~((at["y"] == at["zh"]) & (at["y"] == at["x"]) & (at["y"] == at["c"]))

    def greet_group(self, targets):
        away = self.group_away()
        self.greet(
            targets + [self.group_to(1), self.group_from(1)],
            [(self.group_to(0), away), (self.group_from(0), away)],
        )

    def greet(self, targets, extra=()):
        barrier = pltpu.get_barrier_semaphore()
        for target in targets:
            pl.semaphore_signal(barrier, inc=1, device_id=target, device_id_type=MESH_ID)
        count = len(targets)
        for target, away in extra:
            @pl.when(away)
            def _():
                pl.semaphore_signal(barrier, inc=1, device_id=target, device_id_type=MESH_ID)

            count = count + away.astype(jnp.int32)
        pl.semaphore_wait(barrier, count)


def remote(src, dst, send_sem, recv_sem, target):
    return pltpu.make_async_remote_copy(
        src_ref=src,
        dst_ref=dst,
        send_sem=send_sem,
        recv_sem=recv_sem,
        device_id=target,
        device_id_type=MESH_ID,
    )


def last_kernel(
    ring,
    grads_in,
    weight_in,
    normed_in,
    tokens_in,
    residual_in,
    gain_in,
    forget_w,
    hid_in,
    down_in,
    out_first_in,
    out_mid_in,
    back_out,
    proj_out,
    gate_out,
    up_out,
    down_out,
    out_out,
    gain_out,
    grads,
    weight,
    normed,
    tokens,
    residual,
    rs_send,
    rs_land,
    total,
    c_send,
    c_land,
    kept,
    x_send,
    x_land,
    z_send,
    z_land,
    final,
    blocks,
    gain_sum,
    gain_nat,
    gain_land,
    load_sem,
    local_sem,
    y_send_sem,
    y_recv_sem,
    c2_send_sem,
    c2_recv_sem,
    rs_send_sem,
    rs_recv_sem,
    c_send_sem,
    c_recv_sem,
    x_send_sem,
    x_recv_sem,
    z_send_sem,
    z_recv_sem,
    back_send_sem,
    back_recv_sem,
    gain_send_sem,
    gain_recv_sem,
):
    here = Here(ring)
    y, c, x, zh = (here.at[a] for a in ("y", "c", "x", "zh"))
    local, features = tokens.shape
    part = features // 4
    slot_w = 4 * LANES
    slots = z_count = 3
    units = down_in.shape[0]
    owner = zh == y
    peers = len(ring.offsets)

    loads = [
        pltpu.make_async_copy(a, b, load_sem.at[i])
        for i, (a, b) in enumerate(
            (
                (grads_in, grads),
                (weight_in, weight),
                (normed_in, normed),
                (tokens_in, tokens),
                (residual_in, residual),
            )
        )
    ]
    for copy in loads:
        copy.start()

    away = here.group_away()
    here.greet_group(
        [here.peer(k) for k in range(1, peers)]
        + [here.other("c"), here.other("x"), here.other("zh")]
    )

    row0 = pl.multiple_of(c * part, part)

    def rows_of(ref, col, width):
        return ref.at[pl.ds(row0, part), pl.ds(pl.multiple_of(col, LANES), width)]

    def cols_of(ref, row, height):
        return ref.at[pl.ds(pl.multiple_of(row, LANES), height), pl.ds(row0, part)]

    pieces = [
        (hid_in.at[:, :units], rows_of(gate_out, y * units, units)),
        (hid_in.at[:, units:], rows_of(up_out, y * units, units)),
        (down_in, cols_of(down_out, y * units, units)),
        (out_first_in, cols_of(out_out, 2 * LANES * y, LANES)),
    ]
    own_pieces = [
        pltpu.make_async_copy(src, dst, local_sem.at[i]) for i, (src, dst) in enumerate(pieces)
    ]
    y_pieces = [
        remote(src, dst, y_send_sem.at[i], y_recv_sem.at[i], here.other("y"))
        for i, (src, dst) in enumerate(pieces)
    ]
    mid_dst = cols_of(out_out, LANES, LANES)
    own_mid = pltpu.make_async_copy(out_mid_in, mid_dst, local_sem.at[4])
    y_mid = remote(out_mid_in, mid_dst, y_send_sem.at[4], y_recv_sem.at[4], here.other("y"))

    loads[0].wait()
    loads[1].wait()
    tiles = 3
    tile_w = features // tiles

    def partial_rows(chunk_no, store):
        def step(i, carry):
            cols = pl.ds(pl.multiple_of(i * tile_w, LANES), tile_w)
            store(
                cols,
                nt_dot(grads[chunk_no * local : (chunk_no + 1) * local, :slot_w], weight[0, cols, :])
                + nt_dot(
                    grads[chunk_no * local : (chunk_no + 1) * local, slot_w : 2 * slot_w],
                    weight[1, cols, :],
                )
                + nt_dot(
                    grads[chunk_no * local : (chunk_no + 1) * local, 2 * slot_w : 3 * slot_w],
                    weight[2, cols, :],
                )
                + nn_dot(
                    grads[chunk_no * local : (chunk_no + 1) * local, 3 * slot_w :],
                    forget_w[:, cols],
                ),
            )
            return carry

        lax.fori_loop(0, tiles, step, 0)

    rs = []
    for k in range(1, peers):

        def store_out(cols, value, k=k):
            rs_send[k - 1, :, cols] = value.astype(BF)

        partial_rows(ring.back[k], store_out)
        copy = remote(
            rs_send.at[k - 1],
            rs_land.at[k - 1],
            rs_send_sem.at[k - 1],
            rs_recv_sem.at[k - 1],
            here.peer(k),
        )
        copy.start()
        rs.append(copy)
    for copy in own_pieces + y_pieces:
        copy.start()

    @pl.when(owner)
    def _():
        own_mid.start()
        y_mid.start()

    loads[2].wait()
    tile_r = LANES
    per_part = part // tile_r

    def weight_tile(first, i):
        cols = pl.ds(pl.multiple_of(first + i * tile_r, LANES), tile_r)
        return tn_dot(normed[:, cols], grads[:, : slots * slot_w])

    def c_step(i, carry):
        rows = pl.ds(pl.multiple_of(i * tile_r, tile_r), tile_r)
        c_send[rows, :] = weight_tile(2 * part, i).astype(BF)
        return carry

    lax.fori_loop(0, 2 * per_part, c_step, 0)
    c_copy = remote(c_send, c_land, c_send_sem, c_recv_sem, here.other("c"))
    c_copy.start()

    def store_own(cols, value):
        total[:, cols] = value

    partial_rows(0, store_own)
    c_copy.wait_recv()

    def x_step(i, carry):
        rows = pl.ds(pl.multiple_of(i * tile_r, tile_r), tile_r)
        land = pl.ds(pl.multiple_of(part + i * tile_r, tile_r), tile_r)
        value = weight_tile(part, i) + c_land[land, :].astype(F32)
        for s in range(slots):
            x_send[s, rows, :] = value[:, s * slot_w : (s + 1) * slot_w].astype(BF)
        return carry

    lax.fori_loop(0, per_part, x_step, 0)
    x_copies = {}
    for s in (2, 1, 0):
        x_copies[s] = remote(
            x_send.at[s], x_land.at[s], x_send_sem.at[s], x_recv_sem.at[s], here.other("x")
        )
        x_copies[s].start()

    def own_step(i, carry):
        rows = pl.ds(pl.multiple_of(i * tile_r, tile_r), tile_r)
        value = weight_tile(0, i) + c_land[rows, :].astype(F32)
        for s in range(slots):
            kept[s, rows, :] = value[:, s * slot_w : (s + 1) * slot_w]
        return carry

    lax.fori_loop(0, per_part, own_step, 0)

    loads[3].wait()
    loads[4].wait()
    for copy in rs:
        copy.wait_recv()
    gain_sum[...] = jnp.zeros(gain_sum.shape, F32)
    tile_n = 32

    def norm_step(i, carry):
        rows = pl.ds(pl.multiple_of(i * tile_n, tile_n), tile_n)
        tok = tokens[rows, :].astype(F32)
        grad = total[rows, :]
        for k in range(peers - 1):
            grad = grad + rs_land[k, rows, :].astype(F32)
        factor = lax.rsqrt(jnp.mean(tok * tok, axis=-1, keepdims=True) + epsilon)
        scaled_tok = tok * factor
        e = grad * gain_in[...]
        mean = jnp.mean(e * scaled_tok, axis=-1, keepdims=True)
        out = factor * (e - scaled_tok * mean) + residual[rows, :]
        weighed = jnp.sum(grad * scaled_tok, axis=0, keepdims=True)
        for i in range(4):
            blocks[i, rows, :] = out[:, i * part : (i + 1) * part].astype(BF)
            gain_sum[i, 0:1, :] += weighed[:, i * part : (i + 1) * part]
        return carry

    lax.fori_loop(0, local // tile_n, norm_step, 0)

    def block_no(half, low_high):
        return (half ^ x) + 2 * (low_high ^ c)

    def back_copy(flip, p):
        return remote(
            blocks.at[block_no(c ^ flip, p)],
            back_out.at[c, :, p * part : (p + 1) * part],
            back_send_sem.at[flip, p],
            back_recv_sem.at[flip, p],
            here.group_from(flip),
        )

    def back_own(flip, p):
        return pltpu.make_async_copy(
            blocks.at[block_no(c ^ flip, p)],
            back_out.at[c, :, p * part : (p + 1) * part],
            local_sem.at[5 + p],
        )

    for p in range(2):
        back_copy(1, p).start()

    @pl.when(away)
    def _():
        for p in range(2):
            back_copy(0, p).start()

    @pl.when(~away)
    def _():
        for p in range(2):
            back_own(0, p).start()

    z_copies = {}
    for s in (2, 1, 0):
        x_copies[s].wait_recv()
        kept[s] += x_land[s].astype(F32)
        if s == 2:
            z_send[0] = kept[2].astype(BF)
            z_copies[0] = remote(
                z_send.at[0], z_land.at[0], z_send_sem.at[0], z_recv_sem.at[0], here.other("zh")
            )
            z_copies[0].start()
        if s == 1:
            z_copies[1] = remote(
                z_send.at[1], z_land.at[1], z_send_sem.at[1], z_recv_sem.at[1], here.other("zh")
            )

            @pl.when(~owner)
            def _():
                z_send[1] = kept[1].astype(BF)
                z_copies[1].start()

    for copy in own_pieces:
        copy.wait()
    for copy in y_pieces:
        copy.wait_recv()

    @pl.when(owner)
    def _():
        own_mid.wait()

    @pl.when(~owner)
    def _():
        y_mid.wait_recv()

    c2 = []
    for i, view in enumerate(
        (
            gate_out.at[pl.ds(row0, part), :],
            up_out.at[pl.ds(row0, part), :],
            down_out.at[:, pl.ds(row0, part)],
            out_out.at[:, pl.ds(row0, part)],
        )
    ):
        copy = remote(view, view, c2_send_sem.at[i], c2_recv_sem.at[i], here.other("c"))
        copy.start()
        c2.append(copy)

    for i in range(4):
        gain_nat[0, i] = gain_sum[block_no(i // 2, i % 2)]
    for place, axis in enumerate(("c", "y", "x", "zl", "zh")):
        copy = remote(
            gain_nat.at[place],
            gain_land.at[place],
            gain_send_sem.at[place],
            gain_recv_sem.at[place],
            here.other(axis),
        )
        copy.start()
        copy.wait_recv()
        gain_nat[place + 1] = gain_nat[place] + gain_land[place]
        copy.wait_send()
    gain_copy = pltpu.make_async_copy(gain_nat.at[5], gain_out, local_sem.at[7])
    gain_copy.start()

    z_copies[0].wait_recv()
    final[0] = (kept[0] + z_land[0].astype(F32)).astype(BF)

    @pl.when(owner)
    def _():
        z_copies[1].wait_recv()
        final[1] = (kept[1] + z_land[1].astype(F32)).astype(BF)

    first_dst = rows_of(proj_out, 2 * y * slot_w, slot_w)
    mid_proj = rows_of(proj_out, slot_w, slot_w)
    own_first = pltpu.make_async_copy(final.at[0], first_dst, local_sem.at[8])
    own_second = pltpu.make_async_copy(final.at[1], mid_proj, local_sem.at[9])
    y_first = remote(final.at[0], first_dst, y_send_sem.at[5], y_recv_sem.at[5], here.other("y"))
    y_second = remote(final.at[1], mid_proj, y_send_sem.at[6], y_recv_sem.at[6], here.other("y"))
    y_first.start()
    own_first.start()

    @pl.when(owner)
    def _():
        y_second.start()
        own_second.start()

    own_first.wait()
    y_first.wait_recv()

    @pl.when(owner)
    def _():
        own_second.wait()

    @pl.when(~owner)
    def _():
        y_second.wait_recv()

    view = proj_out.at[pl.ds(row0, part), :]
    copy = remote(view, view, c2_send_sem.at[4], c2_recv_sem.at[4], here.other("c"))
    copy.start()
    c2.append(copy)

    for copy in c2:
        copy.wait()
    for p in range(2):
        back_copy(1, p).wait()

    @pl.when(away)
    def _():
        for p in range(2):
            back_copy(0, p).wait()

    @pl.when(~away)
    def _():
        for p in range(2):
            back_own(0, p).wait()

    gain_copy.wait()
    for copy in rs + [c_copy, x_copies[0], x_copies[1], x_copies[2], z_copies[0], y_first]:
        copy.wait_send()
    for copy in y_pieces:
        copy.wait_send()

    @pl.when(owner)
    def _():
        y_mid.wait_send()
        y_second.wait_send()

    @pl.when(~owner)
    def _():
        z_copies[1].wait_send()


def last_step(
    ring, grads, weight, normed, tokens, residual, gain, forget_w, hid, down, out_first, out_mid
):
    local, features = tokens.shape
    rows = grads.shape[0]
    part = features // 4
    half = features // 2
    units = down.shape[0]
    peers = len(ring.offsets)
    slot_w = 4 * LANES
    any_spec = pl.BlockSpec(memory_space=pl.ANY)
    dma = pltpu.SemaphoreType.DMA
    return pl.pallas_call(
        functools.partial(last_kernel, ring),
        out_shape=(
            jax.ShapeDtypeStruct((2, local, half), BF),
            jax.ShapeDtypeStruct((half, 3 * slot_w), BF),
            jax.ShapeDtypeStruct((half, 2 * units), BF),
            jax.ShapeDtypeStruct((half, 2 * units), BF),
            jax.ShapeDtypeStruct((2 * units, half), BF),
            jax.ShapeDtypeStruct((3 * LANES, half), BF),
            jax.ShapeDtypeStruct((4, 8, part), F32),
        ),
        in_specs=[any_spec] * 5 + [pl.BlockSpec(memory_space=pltpu.VMEM)] * 2 + [any_spec] * 4,
        out_specs=[any_spec] * 7,
        scratch_shapes=[
            pltpu.VMEM(grads.shape, BF),
            pltpu.VMEM(weight.shape, BF),
            pltpu.VMEM(normed.shape, BF),
            pltpu.VMEM(tokens.shape, BF),
            pltpu.VMEM(residual.shape, F32),
            pltpu.VMEM((peers - 1, local, features), BF),
            pltpu.VMEM((peers - 1, local, features), BF),
            pltpu.VMEM((local, features), F32),
            pltpu.VMEM((half, 3 * slot_w), BF),
            pltpu.VMEM((half, 3 * slot_w), BF),
            pltpu.VMEM((3, part, slot_w), F32),
            pltpu.VMEM((3, part, slot_w), BF),
            pltpu.VMEM((3, part, slot_w), BF),
            pltpu.VMEM((2, part, slot_w), BF),
            pltpu.VMEM((2, part, slot_w), BF),
            pltpu.VMEM((2, part, slot_w), BF),
            pltpu.VMEM((4, local, part), BF),
            pltpu.VMEM((4, 8, part), F32),
            pltpu.VMEM((6, 4, 8, part), F32),
            pltpu.VMEM((5, 4, 8, part), F32),
            dma((5,)),
            dma((10,)),
            dma((7,)),
            dma((7,)),
            dma((5,)),
            dma((5,)),
            dma((peers - 1,)),
            dma((peers - 1,)),
            dma,
            dma,
            dma((3,)),
            dma((3,)),
            dma((2,)),
            dma((2,)),
            dma((2, 2)),
            dma((2, 2)),
            dma((5,)),
            dma((5,)),
        ],
        compiler_params=pltpu.CompilerParams(
            collective_id=1, has_side_effects=True, vmem_limit_bytes=58 << 20
        ),
        cost_estimate=pl.CostEstimate(
            flops=4 * rows * features * 3 * slot_w, bytes_accessed=40 << 20, transcendentals=0
        ),
    )(grads, weight, normed, tokens, residual, gain, forget_w, hid, down, out_first, out_mid)


def middle_kernel(
    ring,
    gated_in,
    w_out_in,
    hid_own_in,
    hid_there_in,
    w_down_in,
    tokens_in,
    teach_prompt_in,
    teach_cont_in,
    valid_ref,
    gain_ref,
    gated_grad,
    residual_grad,
    mixed_grads,
    hid_kept,
    hid_there,
    down_kept,
    down_there,
    error_ref,
    gain_grad,
    gated,
    w_out,
    w_hidden,
    w_down,
    tokens,
    teacher,
    mixed,
    total,
    result_grad,
    normed,
    hidden,
    gate_up,
    result_all,
    mixed_all,
    rs_send,
    rs_land,
    c_down_send,
    c_down_land,
    c_hid_send,
    c_hid_land,
    x_down_send,
    x_hid_send,
    down_sum,
    hid_sum,
    gg_stage,
    load_sem,
    wx_send,
    wx_recv,
    wc_send,
    wc_recv,
    wz_send,
    wz_recv,
    group_send,
    group_recv,
    out_sem,
    rs_send_sem,
    rs_recv_sem,
    ag_send_sem,
    ag_recv_sem,
    c_send_sem,
    c_recv_sem,
    x_send_sem,
    x_recv_sem,
):
    here = Here(ring)
    local, features = tokens.shape
    rows_all = gated.shape[0]
    width = gated.shape[1]
    units = hidden.shape[1]
    half_units = units // 2
    part = features // 4
    peers = len(ring.offsets)
    order = list(range(peers - 1, 0, -1))
    y, c, x = (here.at[a] for a in ("y", "c", "x"))
    down_view = w_down_in.at[
        pl.ds(pl.multiple_of(y * half_units, half_units), half_units),
        pl.ds(pl.multiple_of(c * part, part), part),
    ]

    loads = [
        pltpu.make_async_copy(a, b, load_sem.at[i])
        for i, (a, b) in enumerate(
            (
                (hid_own_in, w_hidden.at[0:part, 0:units]),
                (hid_there_in, w_hidden.at[0:part, units:]),
                (gated_in, gated),
                (w_out_in, w_out),
                (tokens_in, tokens),
                (down_view, w_down.at[0:half_units, 0:part]),
            )
        )
    ]
    for copy in loads:
        copy.start()
    here.greet_group(
        [here.peer(k) for k in range(1, peers)]
        + [here.other("c"), here.other("x"), here.other("zh")]
    )

    z_down = remote(
        down_view, w_down.at[half_units:, 0:part], wz_send, wz_recv, here.other("zh")
    )
    z_down.start()

    def hid_x_copy(i):
        cols = slice(i * units, (i + 1) * units)
        return remote(
            w_hidden.at[0:part, cols],
            w_hidden.at[part : 2 * part, cols],
            wx_send.at[i],
            wx_recv.at[i],
            here.other("x"),
        )

    def hid_c_copy(i):
        cols = slice(i * units, (i + 1) * units)
        return remote(
            w_hidden.at[0 : 2 * part, cols],
            w_hidden.at[2 * part :, cols],
            wc_send.at[i],
            wc_recv.at[i],
            here.other("c"),
        )

    for i in range(2):
        loads[i].wait()
        hid_x_copy(i).start()

    def teach_copies(flip, rows_in, remote_copy):
        kind = x ^ flip
        out = []
        for p in range(2):
            block = (x ^ y) + 2 * (kind ^ p)
            dst = teacher.at[:, pl.ds(pl.multiple_of(block * part, part), part)]
            src = rows_in.at[:, p * part : (p + 1) * part]
            if remote_copy:
                out.append(
                    remote(
                        src, dst, group_send.at[flip, p], group_recv.at[flip, p], here.group_to(flip)
                    )
                )
            else:
                out.append(pltpu.make_async_copy(src, dst, load_sem.at[6 + p]))
        return out

    away = here.group_away()

    def on_teacher(flip, here_too, what):
        for kind, rows_in in ((0, teach_prompt_in), (1, teach_cont_in)):
            mine = (x ^ flip) == kind
            if flip == 1:

                @pl.when(mine)
                def _():
                    for copy in teach_copies(1, rows_in, True):
                        what(copy)

            else:

                @pl.when(mine & away)
                def _():
                    for copy in teach_copies(0, rows_in, True):
                        what(copy)

                if here_too:

                    @pl.when(mine & ~away)
                    def _():
                        for copy in teach_copies(0, rows_in, False):
                            what(copy)

    def teacher_arrival(flip):
        for p in range(2):
            remote(
                teach_prompt_in.at[:, p * part : (p + 1) * part],
                teacher.at[:, p * part : (p + 1) * part],
                group_send.at[flip, p],
                group_recv.at[flip, p],
                here.group_to(flip),
            ).wait_recv()

    def chunk(k):
        return slice(k * local, (k + 1) * local)

    def tiled(count, size, step):
        def body(i, carry):
            step(pl.ds(pl.multiple_of(i * size, size), size))
            return carry

        lax.fori_loop(0, count, body, 0)

    def rs_copy(phase, j):
        return remote(
            rs_send.at[j - 1],
            rs_land.at[j - 1],
            rs_send_sem.at[phase, j - 1],
            rs_recv_sem.at[phase, j - 1],
            here.peer(j),
        )

    def ag_copy(phase, buffer, k):
        return remote(
            buffer.at[chunk(0)],
            buffer.at[chunk(k)],
            ag_send_sem.at[phase, k - 1],
            ag_recv_sem.at[phase, k - 1],
            here.peer(k),
        )

    wide = 512
    wide_count = features // wide

    def send_partial(phase, k, left, right, transposed):
        def step(cols):
            if transposed:
                value = nt_dot(left, right[cols, :])
            else:
                value = nn_dot(left, right[:, cols])
            if k == 0:
                total[:, cols] = value
            else:
                rs_send[ring.back[k] - 1, :, cols] = value.astype(BF)

        if k != 0 and phase > 0:
            rs_copy(phase - 1, ring.back[k]).wait_send()
        tiled(wide_count, wide, step)
        if k != 0:
            rs_copy(phase, ring.back[k]).start()

    def row_tiles(step):
        tiled(local // 32, 32, step)

    def summed(rows):
        value = total[rows, :]
        for j in range(1, peers):
            value = value + rs_land[j - 1, rows, :].astype(F32)
        return value

    loads[2].wait()
    loads[3].wait()
    for k in order + [0]:
        send_partial(0, k, gated[chunk(k), :], w_out, False)
    loads[4].wait()
    loads[5].wait()
    z_down.wait_recv()
    down_x_copy = remote(
        w_down.at[:, 0:part],
        w_down.at[:, part : 2 * part],
        wx_send.at[2],
        wx_recv.at[2],
        here.other("x"),
    )
    down_x_copy.start()
    for j in range(1, peers):
        rs_copy(0, j).wait_recv()

    def second_norm(rows):
        value = tokens[rows, :].astype(F32) + summed(rows)
        mixed[rows, :] = value
        factor = lax.rsqrt(jnp.mean(value * value, axis=-1, keepdims=True) + epsilon)
        normed[rows, :] = (value * factor * gain_ref[...]).astype(BF)

    row_tiles(second_norm)
    for k in order:
        ag_copy(0, normed, k).start()

    for i in range(2):
        hid_x_copy(i).wait_recv()
        hid_c_copy(i).start()
    for f in range(2):
        on_teacher(f, True, lambda copy: copy.start())
    for i in range(2):
        hid_c_copy(i).wait_recv()
    down_x_copy.wait_recv()
    down_c_copy = remote(
        w_down.at[:, 0 : 2 * part],
        w_down.at[:, 2 * part :],
        wc_send.at[2],
        wc_recv.at[2],
        here.other("c"),
    )
    down_c_copy.start()
    tile_u = 256
    per_half = half_units // tile_u

    def forward_chunk(k):
        left = normed[chunk(k), :]

        def step(i, carry):
            half = i // per_half
            sub = lax.rem(i, per_half)
            gate_at = pl.multiple_of(half * units + sub * tile_u, tile_u)
            up_at = pl.multiple_of(half * units + half_units + sub * tile_u, tile_u)
            gate = nn_dot(left, w_hidden[:, pl.ds(gate_at, tile_u)])
            up = nn_dot(left, w_hidden[:, pl.ds(up_at, tile_u)])
            gate_up[chunk(k), pl.ds(gate_at, tile_u)] = gate.astype(BF)
            gate_up[chunk(k), pl.ds(up_at, tile_u)] = up.astype(BF)
            hidden[chunk(k), pl.ds(pl.multiple_of(i * tile_u, tile_u), tile_u)] = (
                gate * jax.nn.sigmoid(gate) * up
            ).astype(BF)
            return carry

        lax.fori_loop(0, 2 * per_half, step, 0)
        if k == 0:
            down_c_copy.wait_recv()
        send_partial(1, k, hidden[chunk(k), :], w_down, False)

    forward_chunk(0)
    for k in range(1, peers):
        ag_copy(0, normed, k).wait_recv()
        forward_chunk(k)
    teacher_arrival(1)

    @pl.when(away)
    def _():
        teacher_arrival(0)

    @pl.when(~away)
    def _():
        for kind, rows_in in ((0, teach_prompt_in), (1, teach_cont_in)):

            @pl.when(x == kind)
            def _():
                for copy in teach_copies(0, rows_in, False):
                    copy.wait()

    for j in range(1, peers):
        rs_copy(1, j).wait_recv()
    error_ref[...] = jnp.zeros(error_ref.shape, F32)
    gain_grad[...] = jnp.zeros(gain_grad.shape, F32)

    def loss_rows(rows):
        deviation = mixed[rows, :] + summed(rows) - teacher[rows, :].astype(F32)
        grad = valid_ref[rows, :] * deviation
        result_grad[rows, :] = grad
        result_all[rows, :] = grad.astype(BF)
        error_ref[0:1, :] += 0.5 * jnp.sum(grad * deviation, axis=0, keepdims=True)

    row_tiles(loss_rows)
    for k in order:
        ag_copy(1, result_all, k).start()

    def backward_chunk(k):
        left = result_all[chunk(k), :]

        def step(i, carry):
            half = i // per_half
            sub = lax.rem(i, per_half)
            gate_at = pl.multiple_of(half * units + sub * tile_u, tile_u)
            up_at = pl.multiple_of(half * units + half_units + sub * tile_u, tile_u)
            grad = nt_dot(left, w_down[pl.ds(pl.multiple_of(i * tile_u, tile_u), tile_u), :])
            gate = gate_up[chunk(k), pl.ds(gate_at, tile_u)].astype(F32)
            up = gate_up[chunk(k), pl.ds(up_at, tile_u)].astype(F32)
            sig = jax.nn.sigmoid(gate)
            gate_up[chunk(k), pl.ds(gate_at, tile_u)] = (
                grad * up * sig * (1.0 + gate * (1.0 - sig))
            ).astype(BF)
            gate_up[chunk(k), pl.ds(up_at, tile_u)] = (grad * gate * sig).astype(BF)
            return carry

        lax.fori_loop(0, 2 * per_half, step, 0)
        send_partial(2, k, gate_up[chunk(k), :], w_hidden, True)

    backward_chunk(0)
    for k in range(1, peers):
        ag_copy(1, result_all, k).wait_recv()
        backward_chunk(k)

    unit_tile = 256

    def down_tile(units_at, cols):
        return tn_dot(hidden[:, units_at], result_all[:, cols])

    def down_c(units_at):
        c_down_send[units_at, :] = down_tile(units_at, slice(2 * part, features)).astype(BF)

    tiled(units // unit_tile, unit_tile, down_c)
    c_down = remote(c_down_send, c_down_land, c_send_sem.at[0], c_recv_sem.at[0], here.other("c"))
    c_down.start()
    feature_tile = 128

    def hid_tile(first, at):
        cols = pl.ds(pl.multiple_of(first + at.start, feature_tile), feature_tile)
        return tn_dot(normed[:, cols], gate_up[...])

    def hid_c(at):
        c_hid_send[at, :] = hid_tile(2 * part, at).astype(BF)

    tiled(2 * part // feature_tile, feature_tile, hid_c)
    c_hid = remote(c_hid_send, c_hid_land, c_send_sem.at[1], c_recv_sem.at[1], here.other("c"))
    c_hid.start()
    c_down.wait_recv()

    def down_x(units_at):
        value = down_tile(units_at, slice(part, 2 * part))
        x_down_send[units_at, :] = (value + c_down_land[units_at, part:].astype(F32)).astype(BF)

    tiled(units // unit_tile, unit_tile, down_x)
    x_down = remote(x_down_send, down_there, x_send_sem.at[0], x_recv_sem.at[0], here.other("x"))
    x_down.start()

    for j in range(1, peers):
        rs_copy(2, j).wait_recv()

    def norm_back(rows):
        value = mixed[rows, :]
        factor = lax.rsqrt(jnp.mean(value * value, axis=-1, keepdims=True) + epsilon)
        scaled_rows = value * factor
        grad = summed(rows)
        e = grad * gain_ref[...]
        mean = jnp.mean(e * scaled_rows, axis=-1, keepdims=True)
        out = result_grad[rows, :] + factor * (e - scaled_rows * mean)
        result_grad[rows, :] = out
        mixed_all[rows, :] = out.astype(BF)
        gain_grad[0:1, :] += jnp.sum(grad * scaled_rows, axis=0, keepdims=True)

    row_tiles(norm_back)
    for k in order:
        ag_copy(2, mixed_all, k).start()
    residual_copy = pltpu.make_async_copy(result_grad, residual_grad, out_sem.at[0])
    residual_copy.start()

    c_hid.wait_recv()

    def hid_x(at):
        land = pl.ds(pl.multiple_of(part + at.start, feature_tile), feature_tile)
        x_hid_send[at, :] = (hid_tile(part, at) + c_hid_land[land, :].astype(F32)).astype(BF)

    tiled(part // feature_tile, feature_tile, hid_x)
    x_hid = remote(x_hid_send, hid_there, x_send_sem.at[1], x_recv_sem.at[1], here.other("x"))
    x_hid.start()

    def gated_chunk(k):
        gg_stage[chunk(k), :] = nt_dot(mixed_all[chunk(k), :], w_out[...])

    gated_chunk(0)

    def down_own(units_at):
        value = down_tile(units_at, slice(0, part))
        down_sum[units_at, :] = value + c_down_land[units_at, :part].astype(F32)

    tiled(units // unit_tile, unit_tile, down_own)

    def hid_own(at):
        hid_sum[at, :] = hid_tile(0, at) + c_hid_land[at, :].astype(F32)

    tiled(part // feature_tile, feature_tile, hid_own)
    sums_out = [
        pltpu.make_async_copy(down_sum, down_kept, out_sem.at[1]),
        pltpu.make_async_copy(hid_sum, hid_kept, out_sem.at[2]),
    ]
    for copy in sums_out:
        copy.start()
    for k in range(1, peers):
        ag_copy(2, mixed_all, k).wait_recv()
        gated_chunk(k)
    finals = [
        pltpu.make_async_copy(gg_stage, gated_grad, out_sem.at[3]),
        pltpu.make_async_copy(mixed_all, mixed_grads, out_sem.at[4]),
    ]
    for copy in finals:
        copy.start()
    for k in range(1, peers):
        rs_copy(2, k).wait_send()
        for phase, buffer in enumerate((normed, result_all, mixed_all)):
            ag_copy(phase, buffer, k).wait_send()
    c_down.wait_send()
    c_hid.wait_send()
    z_down.wait_send()
    for i in range(2):
        hid_x_copy(i).wait_send()
        hid_c_copy(i).wait_send()
        on_teacher(i, False, lambda copy: copy.wait_send())
    down_x_copy.wait_send()
    down_c_copy.wait_send()
    x_down.wait()
    x_hid.wait()
    residual_copy.wait()
    for copy in sums_out + finals:
        copy.wait()


def middle_step(
    ring,
    gated,
    w_out,
    hid_own,
    hid_there,
    w_down,
    tokens,
    teach_prompt,
    teach_cont,
    valid,
    gain,
):
    rows, width = gated.shape
    local, features = tokens.shape
    units = w_down.shape[0]
    part = features // 4
    peers = len(ring.offsets)
    any_spec = pl.BlockSpec(memory_space=pl.ANY)
    vmem_spec = pl.BlockSpec(memory_space=pltpu.VMEM)
    dma = pltpu.SemaphoreType.DMA
    return pl.pallas_call(
        functools.partial(middle_kernel, ring),
        out_shape=(
            jax.ShapeDtypeStruct((rows, width), F32),
            jax.ShapeDtypeStruct((local, features), F32),
            jax.ShapeDtypeStruct((rows, features), BF),
            jax.ShapeDtypeStruct((part, 2 * units), F32),
            jax.ShapeDtypeStruct((part, 2 * units), BF),
            jax.ShapeDtypeStruct((units, part), F32),
            jax.ShapeDtypeStruct((units, part), BF),
            jax.ShapeDtypeStruct((8, features), F32),
            jax.ShapeDtypeStruct((8, features), F32),
        ),
        in_specs=[any_spec] * 8 + [vmem_spec] * 2,
        out_specs=[any_spec] * 7 + [vmem_spec] * 2,
        scratch_shapes=[
            pltpu.VMEM(gated.shape, BF),
            pltpu.VMEM(w_out.shape, BF),
            pltpu.VMEM((features, 2 * units), BF),
            pltpu.VMEM((units, features), BF),
            pltpu.VMEM(tokens.shape, BF),
            pltpu.VMEM(tokens.shape, BF),
            pltpu.VMEM(tokens.shape, F32),
            pltpu.VMEM(tokens.shape, F32),
            pltpu.VMEM(tokens.shape, F32),
            pltpu.VMEM((rows, features), BF),
            pltpu.VMEM((rows, units), BF),
            pltpu.VMEM((rows, 2 * units), BF),
            pltpu.VMEM((rows, features), BF),
            pltpu.VMEM((rows, features), BF),
            pltpu.VMEM((peers - 1, local, features), BF),
            pltpu.VMEM((peers - 1, local, features), BF),
            pltpu.VMEM((units, 2 * part), BF),
            pltpu.VMEM((units, 2 * part), BF),
            pltpu.VMEM((2 * part, 2 * units), BF),
            pltpu.VMEM((2 * part, 2 * units), BF),
            pltpu.VMEM((units, part), BF),
            pltpu.VMEM((part, 2 * units), BF),
            pltpu.VMEM((units, part), F32),
            pltpu.VMEM((part, 2 * units), F32),
            pltpu.VMEM((rows, width), F32),
            dma((8,)),
            dma((3,)),
            dma((3,)),
            dma((3,)),
            dma((3,)),
            dma,
            dma,
            dma((2, 2)),
            dma((2, 2)),
            dma((5,)),
            dma((3, peers - 1)),
            dma((3, peers - 1)),
            dma((3, peers - 1)),
            dma((3, peers - 1)),
            dma((2,)),
            dma((2,)),
            dma((2,)),
            dma((2,)),
        ],
        compiler_params=pltpu.CompilerParams(
            collective_id=2, has_side_effects=True, vmem_limit_bytes=63 << 20
        ),
        cost_estimate=pl.CostEstimate(
            flops=6 * rows * features * (3 * units + width),
            bytes_accessed=60 << 20,
            transcendentals=0,
        ),
    )(
        gated,
        w_out,
        hid_own,
        hid_there,
        w_down,
        tokens,
        teach_prompt,
        teach_cont,
        valid,
        gain,
    )


def first_kernel(
    ring,
    prompt_in,
    cont_in,
    small_in,
    ints_in,
    wq_in,
    wg_in,
    wk_in,
    wv_in,
    w_out_in,
    tokens_out,
    normed_out,
    slots_out,
    w_out_all,
    small_out,
    gains_out,
    forget_w_out,
    ints_out,
    proj_a,
    proj_b,
    proj_c,
    forget_own,
    there_a,
    there_b,
    there_c,
    forget_there,
    tokens,
    normed,
    slot_w,
    project,
    forget,
    small,
    small_x,
    feats,
    forget_f,
    forget_w,
    group_send,
    group_recv,
    ints_send,
    ints_recv,
    small_send,
    small_recv,
    own_sem,
    z_send,
    z_recv,
    x_send,
    x_recv,
    c_send,
    c_recv,
    ag_send,
    ag_recv,
    kv_send,
    kv_recv,
    out_sem,
):
    here = Here(ring)
    y, c, x, zh = (here.at[a] for a in ("y", "c", "x", "zh"))
    local, features = tokens.shape
    part = features // 4
    half = features // 2
    peers = len(ring.offsets)
    owner = zh == y
    row0 = pl.multiple_of(c * part, part)
    first0 = pl.multiple_of(2 * LANES * y, LANES)
    sources = (wq_in, wg_in, wk_in, wv_in)

    here.greet_group([here.peer(k) for k in range(1, peers)] + [here.other(a) for a in "cx"] + [here.other("zh")])

    def group_copies(flip, rows_in, remote_copy):
        kind = x ^ flip
        out = []
        for p in range(2):
            block = (x ^ y) + 2 * (kind ^ p)
            dst = tokens.at[:, pl.ds(pl.multiple_of(block * part, part), part)]
            src = rows_in.at[:, p * part : (p + 1) * part]
            if remote_copy:
                out.append(
                    remote(
                        src, dst, group_send.at[flip, p], group_recv.at[flip, p], here.group_to(flip)
                    )
                )
            else:
                out.append(pltpu.make_async_copy(src, dst, own_sem.at[12 + p]))
        return out

    def ints_copy():
        return remote(ints_in, ints_out, ints_send, ints_recv, here.group_to(0))

    def ints_own():
        return pltpu.make_async_copy(ints_in, ints_out, own_sem.at[14])

    away = here.group_away()

    def on_group(flip, what):
        for kind, rows_in in ((0, prompt_in), (1, cont_in)):
            mine = (x ^ flip) == kind
            if flip == 1:

                @pl.when(mine)
                def _():
                    for copy in group_copies(flip, rows_in, True):
                        what(copy)

            else:

                @pl.when(mine & away)
                def _():
                    for copy in group_copies(flip, rows_in, True):
                        what(copy)

                @pl.when(mine & ~away)
                def _():
                    for copy in group_copies(flip, rows_in, False):
                        what(copy)

    for f in range(2):
        on_group(f, lambda copy: copy.start())

    @pl.when(away)
    def _():
        ints_copy().start()

    @pl.when(~away)
    def _():
        ints_own().start()

    own_small = pltpu.make_async_copy(small_in, small.at[0], own_sem.at[15])
    own_small.start()
    small_z = remote(small_in, small.at[1], small_send.at[0], small_recv.at[0], here.other("zh"))
    small_z.start()

    def own_piece(i, s):
        start = first0 if s == 0 else LANES
        return pltpu.make_async_copy(
            sources[i].at[pl.ds(row0, part), pl.ds(start, LANES)],
            slot_w.at[s, 0:part, i * LANES : (i + 1) * LANES],
            own_sem.at[4 * s + i],
        )

    for i in range(4):
        own_piece(i, 0).start()

    @pl.when(owner)
    def _():
        for i in range(4):
            own_piece(i, 1).start()

    own_out = [
        pltpu.make_async_copy(
            w_out_in.at[pl.ds(first0, LANES), pl.ds(row0, part)],
            w_out_all.at[0:LANES, 0:part],
            own_sem.at[8],
        ),
        pltpu.make_async_copy(
            w_out_in.at[LANES : 2 * LANES, pl.ds(row0, part)],
            w_out_all.at[LANES : 2 * LANES, 0:part],
            own_sem.at[9],
        ),
    ]
    own_out[0].start()

    @pl.when(owner)
    def _():
        own_out[1].start()

    own_small.wait()
    small_z.wait_recv()
    small_over_x = remote(small, small_x, small_send.at[1], small_recv.at[1], here.other("x"))
    small_over_x.start()

    def x_copy(s):
        return remote(
            slot_w.at[s, 0:part],
            slot_w.at[s, part : 2 * part],
            x_send.at[s],
            x_recv.at[s],
            here.other("x"),
        )

    def c_copy(s):
        return remote(
            slot_w.at[s, 0:half],
            slot_w.at[s, half:features],
            c_send.at[s],
            c_recv.at[s],
            here.other("c"),
        )

    for i in range(4):
        own_piece(i, 0).wait()
    x_copy(0).start()
    small_over_x.wait_recv()
    for z in range(2):
        for place in range(2):
            at = pl.multiple_of((c ^ place) * part, part)
            feats[z, :, 2 * place * part : (2 * place + 1) * part] = small[z, :, pl.ds(at, part)]
            feats[z, :, (2 * place + 1) * part : (2 * place + 2) * part] = small_x[
                z, :, pl.ds(at, part)
            ]
    forget_f[...] = jnp.zeros(forget_f.shape, F32)
    for z, rows in ((0, slice(0, 2)), (1, slice(4, 6))):
        forget_f[rows, :] = jnp.where(y == 0, feats[z, 8:10, :], feats[z, 12:14, :])
    forget_f[2:4, :] = jnp.where(owner, feats[0, 10:12, :], feats[1, 10:12, :])
    forget_w[...] = jnp.zeros(forget_w.shape, BF)
    forget_w[0:16, :] = forget_f[...].astype(BF)

    for f in range(2):
        for p in range(2):
            pass

    def arrived(copy):
        if hasattr(copy, "wait_recv"):
            copy.wait_recv()

    def group_arrival(flip):
        for p in range(2):
            remote(
                prompt_in.at[:, p * part : (p + 1) * part],
                tokens.at[:, p * part : (p + 1) * part],
                group_send.at[flip, p],
                group_recv.at[flip, p],
                here.group_to(flip),
            ).wait_recv()

    group_arrival(1)

    @pl.when(away)
    def _():
        group_arrival(0)

    @pl.when(~away)
    def _():
        for kind, rows_in in ((0, prompt_in), (1, cont_in)):

            @pl.when(x == kind)
            def _():
                for copy in group_copies(0, rows_in, False):
                    copy.wait()

    def z_piece(i, s):
        start = first0 if s == 2 else LANES
        return remote(
            sources[i].at[pl.ds(row0, part), pl.ds(start, LANES)],
            slot_w.at[s, 0:part, i * LANES : (i + 1) * LANES],
            z_send.at[s, i],
            z_recv.at[s, i],
            here.other("zh"),
        )

    for i in range(4):
        z_piece(i, 2).start()

    @pl.when(owner)
    def _():
        for i in range(4):
            z_piece(i, 1).start()

    z_out = [
        remote(
            w_out_in.at[pl.ds(first0, LANES), pl.ds(row0, part)],
            w_out_all.at[2 * LANES : 3 * LANES, 0:part],
            z_send.at[0, 0],
            z_recv.at[0, 0],
            here.other("zh"),
        ),
        remote(
            w_out_in.at[LANES : 2 * LANES, pl.ds(row0, part)],
            w_out_all.at[LANES : 2 * LANES, 0:part],
            z_send.at[0, 1],
            z_recv.at[0, 1],
            here.other("zh"),
        ),
    ]
    z_out[0].start()

    @pl.when(owner)
    def _():
        z_out[1].start()

    def norm_rows(i, carry):
        rows = pl.ds(pl.multiple_of(i * 32, 32), 32)
        value = tokens[rows, :].astype(F32)
        factor = lax.rsqrt(jnp.mean(value * value, axis=-1, keepdims=True) + epsilon)
        normed[rows, :] = (value * factor * feats[0, 0:1, :]).astype(BF)
        return carry

    lax.fori_loop(0, local // 32, norm_rows, 0)

    def ag_copy(k):
        return remote(
            normed.at[0:local],
            normed.at[k * local : (k + 1) * local],
            ag_send.at[k - 1],
            ag_recv.at[k - 1],
            here.peer(k),
        )

    for k in range(peers - 1, 0, -1):
        ag_copy(k).start()

    outs = [
        pltpu.make_async_copy(tokens, tokens_out, out_sem.at[0]),
        pltpu.make_async_copy(small, small_out, out_sem.at[1]),
        pltpu.make_async_copy(feats.at[0], gains_out, out_sem.at[2]),
        pltpu.make_async_copy(forget_w, forget_w_out, out_sem.at[3]),
    ]
    for copy in outs:
        copy.start()

    x_copy(0).wait_recv()
    c_copy(0).start()
    for i in range(4):
        z_piece(i, 2).wait_recv()
    x_copy(2).start()

    @pl.when(owner)
    def _():
        for i in range(4):
            own_piece(i, 1).wait()

    @pl.when(~owner)
    def _():
        for i in range(4):
            z_piece(i, 1).wait_recv()

    x_copy(1).start()

    projects = (proj_a, proj_b, proj_c)
    theres = (there_a, there_b, there_c)

    def chunk(k):
        return slice(k * local, (k + 1) * local)

    def kv_copy(k, s):
        return remote(
            project.at[s, chunk(k), 2 * LANES :],
            theres[s].at[chunk(k)],
            kv_send.at[k, s],
            kv_recv.at[k, s],
            here.other("c"),
        )

    def forget_copy(k):
        return remote(
            forget.at[chunk(k)],
            forget_there.at[chunk(k)],
            kv_send.at[k, 3],
            kv_recv.at[k, 3],
            here.other("c"),
        )

    def project_chunk(k, s):
        project[s, chunk(k), :] = nn_dot(normed[chunk(k), :], slot_w[s]).astype(BF)
        kv_copy(k, s).start()

    def forget_chunk(k):
        forget[chunk(k), :] = nt_dot(normed[chunk(k), :], forget_w[...]).astype(BF)
        forget_copy(k).start()

    c_copy(0).wait_recv()
    forget_chunk(0)
    project_chunk(0, 0)
    for k in range(1, peers):
        ag_copy(k).wait_recv()
        forget_chunk(k)
        project_chunk(k, 0)
    normed_copy = pltpu.make_async_copy(normed, normed_out, out_sem.at[4])
    normed_copy.start()
    for s in (2, 1):
        x_copy(s).wait_recv()
        c_copy(s).start()
    own_out[0].wait()
    z_out[0].wait_recv()

    @pl.when(owner)
    def _():
        own_out[1].wait()

    @pl.when(~owner)
    def _():
        z_out[1].wait_recv()

    x_out = remote(
        w_out_all.at[:, 0:part],
        w_out_all.at[:, part : 2 * part],
        x_send.at[3],
        x_recv.at[3],
        here.other("x"),
    )
    x_out.start()
    for s in (2, 1):
        c_copy(s).wait_recv()
        for k in range(peers):
            project_chunk(k, s)
    slots_copy = pltpu.make_async_copy(slot_w, slots_out, out_sem.at[5])
    slots_copy.start()
    finals = [
        pltpu.make_async_copy(project.at[s], projects[s], out_sem.at[6 + s]) for s in range(3)
    ] + [pltpu.make_async_copy(forget, forget_own, out_sem.at[9])]
    for copy in finals:
        copy.start()
    x_out.wait_recv()
    c_out = remote(
        w_out_all.at[:, 0:half],
        w_out_all.at[:, half:features],
        c_send.at[3],
        c_recv.at[3],
        here.other("c"),
    )
    c_out.start()

    on_group(1, lambda copy: copy.wait_send())

    @pl.when(away)
    def _():
        ints_copy().wait()
        for kind, rows_in in ((0, prompt_in), (1, cont_in)):

            @pl.when(x == kind)
            def _():
                for copy in group_copies(0, rows_in, True):
                    copy.wait_send()

    @pl.when(~away)
    def _():
        ints_own().wait()

    small_z.wait_send()
    small_over_x.wait_send()
    for i in range(4):
        z_piece(i, 2).wait_send()
    z_out[0].wait_send()

    @pl.when(owner)
    def _():
        for i in range(4):
            z_piece(i, 1).wait_send()
        z_out[1].wait_send()

    for s in range(3):
        x_copy(s).wait_send()
        c_copy(s).wait_send()
    x_out.wait_send()
    for k in range(1, peers):
        ag_copy(k).wait_send()
    for k in range(peers):
        for s in range(3):
            kv_copy(k, s).wait()
        forget_copy(k).wait()
    c_out.wait()
    for copy in outs + finals + [normed_copy, slots_copy]:
        copy.wait()


def first_step(ring, prompt, cont, small, ints, wq, wg, wk, wv, w_out):
    local, half = prompt.shape
    features = 2 * half
    part = half // 2
    peers = len(ring.offsets)
    rows = peers * local
    slot = 4 * LANES
    any_spec = pl.BlockSpec(memory_space=pl.ANY)
    dma = pltpu.SemaphoreType.DMA
    shapes = [
        ((local, features), BF),
        ((rows, features), BF),
        ((3, features, slot), BF),
        ((3 * LANES, features), BF),
        ((2, 16, half), F32),
        ((16, features), F32),
        ((LANES, features), BF),
        (ints.shape, jnp.int32),
        ((rows, slot), BF),
        ((rows, slot), BF),
        ((rows, slot), BF),
        ((rows, LANES), BF),
        ((rows, 2 * LANES), BF),
        ((rows, 2 * LANES), BF),
        ((rows, 2 * LANES), BF),
        ((rows, LANES), BF),
    ]
    return pl.pallas_call(
        functools.partial(first_kernel, ring),
        out_shape=tuple(jax.ShapeDtypeStruct(*s) for s in shapes),
        in_specs=[any_spec] * 9,
        out_specs=[any_spec] * len(shapes),
        scratch_shapes=[
            pltpu.VMEM((local, features), BF),
            pltpu.VMEM((rows, features), BF),
            pltpu.VMEM((3, features, slot), BF),
            pltpu.VMEM((3, rows, slot), BF),
            pltpu.VMEM((rows, LANES), BF),
            pltpu.VMEM((2, 16, half), F32),
            pltpu.VMEM((2, 16, half), F32),
            pltpu.VMEM((2, 16, features), F32),
            pltpu.VMEM((16, features), F32),
            pltpu.VMEM((LANES, features), BF),
            dma((2, 2)),
            dma((2, 2)),
            dma,
            dma,
            dma((2,)),
            dma((2,)),
            dma((16,)),
            dma((3, 4)),
            dma((3, 4)),
            dma((4,)),
            dma((4,)),
            dma((4,)),
            dma((4,)),
            dma((peers - 1,)),
            dma((peers - 1,)),
            dma((peers, 4)),
            dma((peers, 4)),
            dma((10,)),
        ],
        compiler_params=pltpu.CompilerParams(
            collective_id=3, has_side_effects=True, vmem_limit_bytes=48 << 20
        ),
        cost_estimate=pl.CostEstimate(
            flops=2 * rows * features * 3 * slot, bytes_accessed=40 << 20, transcendentals=0
        ),
    )(prompt, cont, small, ints, wq, wg, wk, wv, w_out)


def ring_body(
    ring,
    x_prompt,
    x_cont,
    teacher_prompt,
    teacher_cont,
    segment_ids,
    offsets,
    prompt_valid,
    cont_valid,
    first_gain,
    w_query,
    w_key,
    w_value,
    w_outgate,
    w_forget,
    forget_bias,
    w_out,
    second_gain,
    w_gate,
    w_up,
    w_down,
):
    y = lax.axis_index("y")
    c = lax.axis_index("c")
    x = lax.axis_index("x")
    zh = lax.axis_index("zh")
    zl = lax.axis_index("zl")
    zl_count = ring.zl_count
    local = x_prompt.shape[1]
    half_d = x_prompt.shape[2]
    part_d = half_d // 2
    local_conts = x_cont.shape[1]
    heads = w_forget.shape[1]
    units_here = w_gate.shape[1]
    half_units = units_here // 2
    width = heads * HEAD_DIM
    slots = heads // 2
    pair_unit = PROMPT // CLEN
    chunk_units = local // CLEN
    peers = len(ring.offsets)
    owner = zh == y

    def by_x(own, other):
        return jnp.where(x == c, own, other)

    def natural_order(value):
        pieces = [value[..., i * part_d : (i + 1) * part_d] for i in range(4)]
        own_low = jnp.where(c == 0, pieces[0], pieces[2])
        own_high = jnp.where(c == 0, pieces[2], pieces[0])
        other_low = jnp.where(c == 0, pieces[1], pieces[3])
        other_high = jnp.where(c == 0, pieces[3], pieces[1])
        return own_low, own_high, other_low, other_high

    own_valid = jnp.where(x == 0, prompt_valid.reshape(-1), cont_valid.reshape(-1))
    small_in = jnp.concatenate([own_valid, segment_ids.reshape(-1), offsets.reshape(-1)])
    int_rows = 16
    ints = jnp.pad(small_in, (0, int_rows * LANES - small_in.shape[0])).reshape(int_rows, LANES)
    packed = jnp.concatenate(
        [
            first_gain[None].astype(F32),
            second_gain[None].astype(F32),
            jnp.pad(forget_bias, (0, half_d - heads))[None],
            jnp.zeros((5, half_d), F32),
            w_forget.T.astype(F32),
            jnp.zeros((8 - heads, half_d), F32),
        ],
        axis=0,
    )
    (
        tokens_b,
        normed_all,
        w_slots,
        w_out_all,
        small_all,
        gains,
        w_forget_rows,
        ints,
        proj_a,
        proj_b,
        proj_c,
        forget_own,
        there_a,
        there_b,
        there_c,
        forget_there,
    ) = first_step(
        ring,
        x_prompt[0],
        x_cont.reshape(local_conts * CLEN, half_d),
        packed,
        ints,
        w_query,
        w_outgate,
        w_key,
        w_value,
        w_out,
    )
    projects = [proj_a, proj_b, proj_c]
    kv_there = [there_a, there_b, there_c]
    ints = ints.reshape(-1)
    validity = ints[:local].astype(F32)
    segment_row = ints[local : local + PROMPT]
    offset_row = ints[local + PROMPT : local + PROMPT + CONTS]
    gain_one = gains[0]
    gain_two = gains[1]

    def head_slots(value):
        first = jnp.where(y == 0, value[:, 0:2], value[:, 4:6])
        slot_a = jnp.where(zh == 0, first[0], first[1])
        slot_c = jnp.where(zh == 0, first[1], first[0])
        slot_b = jnp.where(y == 0, value[0, 2:4], value[1, 2:4])
        return jnp.concatenate([slot_a, slot_b, slot_c], axis=0)

    bias_all = small_all[:, 2, :heads]
    bias_all = jnp.stack(
        [
            jnp.where(zh == 0, bias_all[0], bias_all[1]),
            jnp.where(zh == 0, bias_all[1], bias_all[0]),
        ]
    )
    bias_row = head_slots(bias_all[:, :, None])[:, 0]
    bias_row = jnp.concatenate([bias_row, jnp.zeros((LANES - heads,), F32)])[None]

    proj_a, w_gate, w_up = lax.optimization_barrier((proj_a, w_gate, w_up))
    projects[0] = proj_a
    hid_own = jnp.concatenate(
        [
            lax.dynamic_slice(w, (c * part_d, y * half_units), (part_d, half_units))
            for w in (w_gate, w_up)
        ],
        axis=1,
    )
    hid_there_w = ring.swap(hid_own, "zh")

    dy_all = jnp.array([o[0] for o in ring.offsets], jnp.int32)
    dz_all = jnp.array([o[1] for o in ring.offsets], jnp.int32)
    places = ((y - dy_all) % 2) * zl_count + (zl - dz_all) % zl_count
    unit_no = (places[:, None] * chunk_units + jnp.arange(chunk_units, dtype=jnp.int32)).reshape(-1)
    natural = jnp.arange(pair_unit, dtype=jnp.int32)
    pick = unit_no[:, None] == natural[None, :]
    step = jnp.arange(CLEN, dtype=jnp.int32)
    row_pos = (unit_no[:, None] * CLEN + step[None, :]).reshape(-1)
    seg_rel = jnp.sum(
        jnp.where(pick[:, :, None], segment_row.reshape(1, pair_unit, CLEN), 0), axis=1
    )
    offs_rel = jnp.sum(jnp.where(pick, offset_row[None, :], 0), axis=1)
    last_rel = jnp.sum(
        jnp.where(
            jnp.arange(PROMPT, dtype=jnp.int32)[None, :] == offs_rel[:, None] - 1,
            segment_row[None, :],
            0,
        ),
        axis=1,
    )
    limit = jnp.where(c == 0, unit_no * CLEN, offs_rel)
    doc_row = jnp.where(c == 0, seg_rel, last_rel[:, None]).reshape(-1, 1)
    seg_col = seg_rel.reshape(-1, 1)
    lane = jnp.arange(LANES, dtype=jnp.int32)[None, :]
    unit_col = jnp.repeat(natural, CLEN)[:, None]
    pieces = 3 * heads
    is_doc = (lane >= DOC_LANE) & (lane < DOC_LANE + 4)
    is_unit = (lane >= UNIT_LANE) & (lane < UNIT_LANE + pair_unit)
    limit_lane = jnp.pad(limit, (UNIT_LANE, LANES - UNIT_LANE - pair_unit))[None, :]
    q_base = jnp.where(
        (lane >= FAR_PIECE) & (lane < FAR_PIECE + pieces),
        1.0,
        jnp.where(
            (is_doc & (doc_row != lane - DOC_LANE)) | (is_unit & (unit_col == lane - UNIT_LANE)),
            -NEVER,
            0.0,
        ),
    ).astype(BF)
    near_base = jnp.where(
        (lane < pieces) | (is_doc & (doc_row == lane - DOC_LANE)), 1.0, 0.0
    ).astype(BF)
    far_base = jnp.where(
        (lane < pieces)
        | (is_doc & (seg_col == lane - DOC_LANE))
        | (is_unit & (row_pos[:, None] >= limit_lane)),
        1.0,
        0.0,
    ).astype(BF)
    tri = (step[:, None] >= step[None, :]).astype(F32)
    earlier = (unit_no[None, :] < unit_no[:, None]).astype(F32)
    later = (unit_no[None, :] > unit_no[:, None]).astype(F32)
    hot = (row_pos[None, :] == limit[:, None] - 1).astype(F32)
    cont_hot = (row_pos[None, :] == offs_rel[:, None] - 1).astype(F32)

    forget_far = jnp.where(c == 0, forget_own, forget_there)
    flag = c.astype(jnp.int32).reshape(1)
    head_lane = lane < heads

    def keep_log(lin):
        return jnp.where(head_lane, jax.nn.log_sigmoid(lin.astype(F32) + bias_row), 0.0)

    def within(values, matrix):
        return jnp.einsum(
            "ts,ush->uth", matrix, values.reshape(pair_unit, CLEN, LANES), precision=highest
        )

    far_within = within(keep_log(forget_far), tri)
    far_prefix = jnp.dot(earlier, far_within[:, -1], precision=highest)
    cum_far = (far_within + far_prefix[:, None]).reshape(-1, LANES)
    own_base = jnp.dot(hot, cum_far, precision=highest)
    cum_near = (within(keep_log(forget_own), tri) + own_base[:, None]).reshape(-1, LANES)
    gated, attended, logs = attend(
        flag, projects, kv_there, cum_near, cum_far, q_base, near_base, far_base, local, heads
    )
    (
        grad_gated,
        grad_residual,
        grad_residual_all,
        hid_kept,
        hid_there,
        down_kept,
        down_there,
        error_rows,
        gain_two_rows,
    ) = middle_step(
        ring,
        gated,
        w_out_all,
        hid_own,
        hid_there_w,
        w_down,
        tokens_b,
        teacher_prompt[0],
        teacher_cont.reshape(local_conts * CLEN, half_d),
        validity[:, None],
        gain_two[None],
    )
    error_own = jnp.sum(error_rows)
    count_own = jnp.sum(validity)
    gain_two_grad = gain_two_rows[0]
    grad_out_w = tn_dot(gated, grad_residual_all)
    dqg, dkv_near, dkv_far, row_sum, near_sum, far_sum = attend_back(
        flag,
        projects,
        kv_there,
        cum_near,
        cum_far,
        q_base,
        near_base,
        far_base,
        grad_gated,
        attended,
        logs,
        local,
        heads,
    )
    prompt_here = c == 0

    def at_lane(value, first):
        return jnp.pad(value[:, first : first + heads], ((0, 0), (0, LANES - heads)))

    cum_grad = row_sum - at_lane(near_sum, FAR_PIECE)
    unit_total = jnp.sum(cum_grad.reshape(pair_unit, CLEN, LANES), axis=1)
    far_own = at_lane(far_sum, FAR_PIECE)
    dkv_there = ring.swap(dkv_far.astype(BF), "c")
    sums_there = ring.swap(jnp.concatenate([far_own, unit_total], axis=0), "c")
    dkv = jnp.where(prompt_here, dkv_near + dkv_far + dkv_there.astype(F32), dkv_near).astype(BF)
    total_rows = far_own.shape[0]
    prompt_cum = (
        cum_grad
        - far_own
        - sums_there[:total_rows]
        + jnp.dot(cont_hot.T, sums_there[total_rows:], precision=highest)
    )
    cum_grad = jnp.where(prompt_here, prompt_cum, cum_grad)
    log_within = within(cum_grad, tri.T)
    log_suffix = jnp.where(prompt_here, jnp.dot(later, log_within[:, 0], precision=highest), 0.0)
    log_grad = (log_within + log_suffix[:, None]).reshape(-1, LANES)
    pre_grad = jnp.where(
        head_lane, log_grad * jax.nn.sigmoid(-(forget_own.astype(F32) + bias_row)), 0.0
    )
    bias_grad = jnp.sum(pre_grad, axis=0)
    grad_slots = []
    for s in range(slots):
        cols = slice(2 * s * LANES, 2 * (s + 1) * LANES)
        grad_slots.append(jnp.concatenate([dqg[:, cols], dkv[:, cols]], axis=1))
    forget_b = pre_grad.astype(BF)
    project_grad = jnp.concatenate(grad_slots + [forget_b], axis=1)
    forget_gw = tn_dot(forget_b, normed_all)[:heads]

    def low(value):
        return lax.reduce_precision(value, 8, 7).astype(BF)

    def outer_sum(value):
        if ring.sizes["yo"] > 1:
            return lax.psum(low(value), "yo").astype(F32)
        return value

    def fold(value, axis, dim):
        size = value.shape[dim] // 2
        mine = lax.slice_in_dim(value, 0, size, axis=dim)
        theirs = lax.slice_in_dim(value, size, 2 * size, axis=dim)
        return mine + ring.swap(theirs.astype(BF), axis).astype(F32)

    def reduce_core_x(value, dim):
        return fold(fold(value, "c", dim), "x", dim)

    def both_parts(value, dim):
        other = ring.swap(value, "c")
        return jnp.concatenate(
            [jnp.where(c == 0, value, other), jnp.where(c == 0, other, value)], axis=dim
        )

    def reduce_pairs(first, mid, third, dim):
        first = first + ring.swap(third.astype(BF), "zh").astype(F32)
        mid = mid + ring.swap(mid.astype(BF), "zh", lambda h: h["zh"] != h["y"]).astype(F32)
        first = low(outer_sum(first))
        mid = low(outer_sum(mid))
        other = ring.swap(first, "y")
        mid_other = ring.swap(mid, "y", lambda h: h["zh"] == h["y"])
        mid = jnp.where(owner, mid, mid_other)
        pair_low = jnp.where(y == 0, first, other)
        pair_high = jnp.where(y == 0, other, first)
        return [both_parts(v, dim) for v in (pair_low, mid, pair_high)]

    def edge_sums(first, mid, third):
        first = first + ring.swap(third.astype(BF), "zh").astype(F32)
        mid = mid + ring.swap(mid.astype(BF), "zh", lambda h: h["zh"] != h["y"]).astype(F32)
        return low(outer_sum(first)), low(outer_sum(mid))

    down_mine = low(outer_sum(fold(down_kept + down_there.astype(F32), "zh", 0)))
    hid_mine = low(outer_sum(fold(hid_kept + hid_there.astype(F32), "zh", 1)))
    out_w = reduce_core_x(grad_out_w, 1)
    out_first, out_mid = edge_sums(*[out_w[s * LANES : (s + 1) * LANES] for s in range(slots)])
    rows_back, proj_all, gate_all, up_all, down_all, out_all, gain_all = last_step(
        ring,
        project_grad,
        w_slots,
        normed_all,
        tokens_b,
        grad_residual,
        gain_one[None],
        w_forget_rows,
        hid_mine,
        down_mine,
        out_first,
        out_mid,
    )
    gain_one_sum = gain_all[:, 0].reshape(-1)
    projection_grads = [
        jnp.concatenate(
            [proj_all[:, (4 * s + i) * LANES : (4 * s + i + 1) * LANES] for s in range(slots)],
            axis=1,
        )
        for i in range(4)
    ]
    forget_w = reduce_core_x(forget_gw, 1)
    forget_grad = jnp.concatenate(
        reduce_pairs(forget_w[0:2], forget_w[2:4], forget_w[4:6], 1), axis=0
    ).T

    def all_features(value):
        own_low, own_high, other_low, other_high = natural_order(value)
        own = jnp.concatenate([own_low, own_high], axis=-1)
        other = jnp.concatenate([other_low, other_high], axis=-1)
        return jnp.concatenate(
            [jnp.where(x == 0, own, other), jnp.where(x == 0, other, own)], axis=-1
        )

    def place_heads(value):
        slot_a, slot_b, slot_c = value[0:2], value[2:4], value[4:6]
        blank = jnp.zeros_like(slot_a)
        rows_out = []
        for high in range(2):
            is_own = zh == high
            edge = jnp.where(is_own, slot_a, slot_c)
            mid = jnp.where(y == high, slot_b, blank)
            quarter = jnp.concatenate(
                [jnp.where(y == 0, edge, blank), mid, jnp.where(y == 1, edge, blank)], axis=0
            )
            for low_z in range(zl_count):
                rows_out.append(jnp.where(zl == low_z, quarter, jnp.zeros_like(quarter)))
        return jnp.concatenate(rows_out, axis=0)

    bias_place = place_heads(bias_grad[:heads, None])[:, 0]
    scalars = jnp.concatenate([error_own[None], count_own[None], bias_place])
    sums = ring.total(jnp.pad(scalars, (0, LANES - scalars.shape[0]))[None])[0]
    gain_two_sum = ring.total(all_features(gain_two_grad).reshape(-1, LANES)).reshape(-1)
    error_total = sums[0]
    count_total = sums[1]
    groups = ring.sizes["yo"] * ring.sizes["y"] * ring.sizes["c"]
    grad_scale = groups * (PROMPT + CONTS * CLEN) / count_total
    loss_value = error_total / (D * count_total)

    def own_half(value):
        return lax.dynamic_slice_in_dim(value, x * half_d, half_d, value.ndim - 1)

    quarter_no = zh * zl_count + zl
    bias_out = lax.dynamic_slice_in_dim(sums, 2 + quarter_no * heads, heads, 0)

    def scaled(value):
        return value.astype(F32) * grad_scale

    return (
        loss_value,
        scaled(rows_back[0])[None],
        scaled(rows_back[1]).reshape(1, local_conts, CLEN, half_d),
        scaled(own_half(gain_one_sum)),
        scaled(projection_grads[0]),
        scaled(projection_grads[2]),
        scaled(projection_grads[3]),
        scaled(projection_grads[1]),
        scaled(forget_grad),
        scaled(bias_out),
        scaled(out_all),
        scaled(own_half(gain_two_sum)),
        scaled(gate_all),
        scaled(up_all),
        scaled(down_all),
    )


def specs(dp, row, col):
    in_specs = (
        P(dp, col, row),
        P(dp, col, None, row),
        P(dp, col, row),
        P(dp, col, None, row),
        P(dp, None),
        P(dp, None),
        P(dp, col),
        P(dp, col, None),
        P(row),
        P(row, col),
        P(row, col),
        P(row, col),
        P(row, col),
        P(row, col),
        P(col),
        P(col, row),
        P(row),
        P(row, col),
        P(row, col),
        P(col, row),
    )
    out_specs = (
        P(),
        P(dp, col, row),
        P(dp, col, None, row),
        P(row),
        P(row, col),
        P(row, col),
        P(row, col),
        P(row, col),
        P(row, col),
        P(col),
        P(col, row),
        P(row),
        P(row, col),
        P(row, col),
        P(col, row),
    )
    return in_specs, out_specs


def solution(mesh):
    dp, row, col = mesh.shape["dp"], mesh.shape["row"], mesh.shape["col"]
    heads = HEADS // col
    if dp == 4 and row == 2 and col % 2 == 0 and heads == 6:
        sizes = {"yo": dp // 4, "y": 2, "c": 2, "x": 2, "zh": 2, "zl": col // 2}
        ring_mesh = Mesh(mesh.devices.reshape([sizes[a] for a in AX]), AX)
        in_specs, out_specs = specs(("yo", "y", "c"), "x", ("zh", "zl"))
        step = functools.partial(ring_body, Ring(sizes))
        return jax.shard_map(
            step, mesh=ring_mesh, in_specs=in_specs, out_specs=out_specs, check_vma=False
        )
    in_specs, out_specs = specs("dp", "row", "col")
    return jax.shard_map(
        wide_body, mesh=mesh, in_specs=in_specs, out_specs=out_specs, check_vma=False
    )
```

```python
import functools
import itertools

import jax
import jax.numpy as jnp
from jax import lax
from jax.experimental import pallas as pl
from jax.experimental.pallas import tpu as pltpu
from jax.sharding import Mesh, PartitionSpec as P

D = 1536
HEADS = 24
HEAD_DIM = 64
PROMPT = 1024
CONTS = 8
CLEN = 128


epsilon = 1e-06
highest = lax.Precision.HIGHEST
masked = -1e30


def matmul(left_op, right_op):
    return jnp.dot(left_op, right_op, preferred_element_type=jnp.float32)


def by_transpose(left_op, right_op):
    return lax.dot_general(
        left_op, right_op, (((1,), (1,)), ((), ())), preferred_element_type=jnp.float32
    )


def inner_rows(left_op, right_op):
    return lax.dot_general(
        left_op, right_op, (((0,), (0,)), ((), ())), preferred_element_type=jnp.float32
    )


def feature_total(partial_sum):
    return lax.psum(partial_sum, "row")


def group_rows(local_rows):
    return lax.all_gather(local_rows, "col", axis=0, tiled=True)


def token_sums(partial_rows):
    return lax.psum_scatter(
        partial_rows.astype(jnp.bfloat16), "col", scatter_dimension=0, tiled=True
    ).astype(jnp.float32)


def row_partials(partial_rows, col_count, blocks, quarter):
    shaped = partial_rows.reshape(
        col_count, blocks, lax.axis_size("row"), quarter, partial_rows.shape[-1]
    )
    return lax.psum_scatter(
        shaped.astype(jnp.bfloat16), "row", scatter_dimension=2, tiled=True
    ).astype(jnp.float32)


def head_rows(own_rows):
    gathered = lax.all_gather(own_rows, "row", axis=2, tiled=True)
    return gathered.reshape(-1, gathered.shape[-1])


def norm_forward(tokens, gain_vec):
    row_total = feature_total(jnp.sum(tokens * tokens, axis=-1))
    factor = lax.rsqrt(row_total / D + epsilon)
    scaled = tokens * factor[:, None]
    return (factor, scaled, (scaled * gain_vec).astype(jnp.bfloat16))


def norm_backward(grad_normed, factor, scaled, gain_vec):
    grad_scaled = grad_normed * gain_vec
    row_total = feature_total(jnp.sum(grad_scaled * scaled, axis=-1))
    gain_grad = jnp.sum(grad_normed * scaled, axis=0)
    return (gain_grad, factor[:, None] * (grad_scaled - scaled * (row_total / D)[:, None]))


def log_total(scores):
    row_top = jnp.max(scores, axis=-1, keepdims=True)
    return row_top + jnp.log(jnp.sum(jnp.exp(scores - row_top), axis=-1, keepdims=True))


def prompt_scores(queries, key_rows, cum_query, cum_key, allowed):
    raw_scores = jnp.einsum("qhd,khd->hqk", queries, key_rows, preferred_element_type=jnp.float32)
    raw_scores = raw_scores * HEAD_DIM ** (-0.5) + cum_query.T[:, :, None] - cum_key.T[:, None, :]
    return jnp.where(allowed[None], raw_scores, masked)


def cont_scores(queries, key_rows, key_cont, cum_query, cum_key, cum_cont, far_ok, near_ok):
    score_scale = HEAD_DIM ** (-0.5)
    query_cum = cum_query.transpose(0, 2, 1)[:, :, :, None]
    far_scores = jnp.einsum("jqhd,khd->jhqk", queries, key_rows, preferred_element_type=jnp.float32)
    far_scores = far_scores * score_scale + query_cum - cum_key.T[None, :, None, :]
    near_scores = jnp.einsum(
        "jqhd,jkhd->jhqk", queries, key_cont, preferred_element_type=jnp.float32
    )
    near_scores = near_scores * score_scale + query_cum - cum_cont.transpose(0, 2, 1)[:, :, None, :]
    far_scores = jnp.where(far_ok[:, None, None, :], far_scores, masked)
    near_scores = jnp.where(near_ok[None, None], near_scores, masked)
    return jnp.concatenate([far_scores, near_scores], axis=-1)


def wide_body(
    x_prompt,
    x_cont,
    teacher_prompt,
    teacher_cont,
    segment_ids,
    offsets,
    prompt_valid,
    cont_valid,
    first_gain,
    w_query,
    w_key,
    w_value,
    w_outgate,
    w_forget,
    forget_bias,
    w_out,
    second_gain,
    w_gate,
    w_up,
    w_down,
):
    row_count = lax.axis_size("row")
    col_count = lax.axis_size("col")
    row_index = lax.axis_index("row")
    local_prompt = x_prompt.shape[1]
    local_conts = x_cont.shape[1]
    quarter = CLEN // row_count
    local_tokens = local_prompt + local_conts * CLEN
    blocks = local_tokens // CLEN
    prompt_blocks = local_prompt // CLEN
    heads_here = w_forget.shape[1]
    width_here = heads_here * HEAD_DIM
    units_here = w_gate.shape[1]
    score_scale = HEAD_DIM ** (-0.5)
    w_project = jnp.concatenate([w_query, w_key, w_value, w_outgate], axis=1)
    w_hidden = jnp.concatenate([w_gate, w_up], axis=1)
    gain_one = first_gain.astype(jnp.float32)
    gain_two = second_gain.astype(jnp.float32)
    position = jnp.arange(PROMPT, dtype=jnp.int32)
    cont_step = jnp.arange(CLEN, dtype=jnp.int32)
    own_step = row_index * quarter + jnp.arange(quarter, dtype=jnp.int32)
    near_ok = cont_step[None, :] <= own_step[:, None]
    own_position = lax.dynamic_index_in_dim(
        position.reshape(col_count, prompt_blocks, row_count, quarter), row_index, 2, keepdims=False
    ).reshape(-1)

    def own_prompt_part(matrix):
        return matrix[:, :prompt_blocks, 0]

    def one_group(carried, group_data):
        (
            acc_project,
            acc_forget,
            acc_bias,
            acc_out,
            acc_hidden,
            acc_down,
            acc_gain_one,
            acc_gain_two,
            error_sum,
            count_sum,
        ) = carried
        (
            prompt_in,
            cont_in,
            teach_prompt,
            teach_cont,
            segment_row,
            offset_row,
            valid_prompt,
            valid_cont,
        ) = group_data
        tokens = jnp.concatenate(
            [prompt_in, cont_in.reshape(local_conts * CLEN, -1)], axis=0
        ).astype(jnp.float32)
        teacher = jnp.concatenate(
            [teach_prompt, teach_cont.reshape(local_conts * CLEN, -1)], axis=0
        ).astype(jnp.float32)
        validity = jnp.concatenate([valid_prompt, valid_cont.reshape(-1)], axis=0).astype(
            jnp.float32
        )
        branch_mask = position[None, :] == offset_row[:, None] - 1
        branch_hot = branch_mask.astype(jnp.float32)
        last_doc = jnp.sum(jnp.where(branch_mask, segment_row[None, :], 0), axis=1)
        far_ok = (position[None, :] < offset_row[:, None]) & (
            segment_row[None, :] == last_doc[:, None]
        )
        own_doc = lax.dynamic_index_in_dim(
            segment_row.reshape(col_count, prompt_blocks, row_count, quarter),
            row_index,
            2,
            keepdims=False,
        ).reshape(-1)
        prompt_ok = (position[None, :] <= own_position[:, None]) & (
            segment_row[None, :] == own_doc[:, None]
        )
        factor_one, scaled_one, normed_one = norm_forward(tokens, gain_one)
        normed_all = group_rows(normed_one)
        project_part = matmul(normed_all, w_project).reshape(
            col_count, blocks, row_count, quarter, 4 * width_here
        )
        forget_part = matmul(normed_all, w_forget).reshape(
            col_count, blocks, row_count, quarter, heads_here
        )
        own_project, own_forget = (
            lax.psum_scatter(project_part, "row", scatter_dimension=2, tiled=True),
            lax.psum_scatter(forget_part, "row", scatter_dimension=2, tiled=True),
        )
        own_query = own_project[..., :width_here].astype(jnp.bfloat16)
        own_kv = own_project[..., width_here : 3 * width_here].astype(jnp.bfloat16)
        gate_logit = own_project[..., 3 * width_here :]
        kv_all, forget_all = (
            lax.all_gather(own_kv, "row", axis=2, tiled=True),
            lax.all_gather(own_forget.astype(jnp.bfloat16), "row", axis=2, tiled=True),
        )
        kv_all = kv_all.reshape(col_count, local_tokens, 2 * width_here)
        pre_gate = (
            forget_all.reshape(col_count, local_tokens, heads_here).astype(jnp.float32)
            + forget_bias
        )
        log_keep = jax.nn.log_sigmoid(pre_gate)
        cum_prompt = jnp.cumsum(log_keep[:, :local_prompt].reshape(PROMPT, heads_here), axis=0)
        branch_cum = jnp.dot(branch_hot, cum_prompt, precision=highest)
        cum_cont = branch_cum[:, None, :] + jnp.cumsum(
            log_keep[:, local_prompt:].reshape(CONTS, CLEN, heads_here), axis=1
        )
        kv_prompt = kv_all[:, :local_prompt].reshape(PROMPT, 2, heads_here, HEAD_DIM)
        key_prompt = kv_prompt[:, 0]
        value_prompt = kv_prompt[:, 1]
        kv_cont = kv_all[:, local_prompt:].reshape(CONTS, CLEN, 2, heads_here, HEAD_DIM)
        key_cont = kv_cont[:, :, 0]
        value_cont = kv_cont[:, :, 1]
        cum_query_prompt = lax.dynamic_index_in_dim(
            cum_prompt.reshape(col_count, prompt_blocks, row_count, quarter, heads_here),
            row_index,
            2,
            keepdims=False,
        ).reshape(-1, heads_here)
        cum_query_cont = lax.dynamic_index_in_dim(
            cum_cont.reshape(CONTS, row_count, quarter, heads_here), row_index, 1, keepdims=False
        )
        query_prompt = own_prompt_part(own_query).reshape(-1, heads_here, HEAD_DIM)
        query_cont = own_query[:, prompt_blocks:, 0].reshape(CONTS, quarter, heads_here, HEAD_DIM)
        scores_prompt = prompt_scores(
            query_prompt, key_prompt, cum_query_prompt, cum_prompt, prompt_ok
        )
        total_prompt = log_total(scores_prompt)
        probs_prompt = jnp.exp(scores_prompt - total_prompt).astype(jnp.bfloat16)
        out_prompt = jnp.einsum(
            "hqk,khd->qhd", probs_prompt, value_prompt, preferred_element_type=jnp.float32
        )
        scores_cont = cont_scores(
            query_cont, key_prompt, key_cont, cum_query_cont, cum_prompt, cum_cont, far_ok, near_ok
        )
        total_cont = log_total(scores_cont)
        probs_cont = jnp.exp(scores_cont - total_cont).astype(jnp.bfloat16)
        out_cont = jnp.einsum(
            "jhqk,khd->jqhd",
            probs_cont[..., :PROMPT],
            value_prompt,
            preferred_element_type=jnp.float32,
        )
        out_cont = out_cont + jnp.einsum(
            "jhqk,jkhd->jqhd",
            probs_cont[..., PROMPT:],
            value_cont,
            preferred_element_type=jnp.float32,
        )
        attended = jnp.concatenate(
            [
                out_prompt.reshape(col_count, prompt_blocks, 1, quarter, width_here),
                out_cont.reshape(col_count, local_conts, 1, quarter, width_here),
            ],
            axis=1,
        )
        gate_sig = jax.nn.sigmoid(gate_logit)
        gated = (attended * gate_sig).astype(jnp.bfloat16)
        gated_all = head_rows(gated)
        residual = tokens + token_sums(matmul(gated_all, w_out))
        factor_two, scaled_two, normed_two = norm_forward(residual, gain_two)
        normed_two_all = group_rows(normed_two)
        hidden_own = row_partials(matmul(normed_two_all, w_hidden), col_count, blocks, quarter)
        gate_rows = hidden_own[..., :units_here]
        up_rows = hidden_own[..., units_here:]
        gate_sig_two = jax.nn.sigmoid(gate_rows)
        silu_rows = gate_rows * gate_sig_two
        hidden_all = head_rows((silu_rows * up_rows).astype(jnp.bfloat16))
        result_rows = residual + token_sums(matmul(hidden_all, w_down))
        deviation = result_rows - teacher
        group_err = 0.5 * jnp.sum(validity[:, None] * deviation * deviation)
        grad_result = validity[:, None] * deviation
        grad_result_all = group_rows(grad_result.astype(jnp.bfloat16))
        grad_down_w = inner_rows(hidden_all, grad_result_all)
        grad_hid = row_partials(by_transpose(grad_result_all, w_down), col_count, blocks, quarter)
        grad_gate = grad_hid * up_rows * gate_sig_two * (1.0 + gate_rows * (1.0 - gate_sig_two))
        grad_up = grad_hid * silu_rows
        grad_hidden_all = head_rows(
            jnp.concatenate([grad_gate, grad_up], axis=-1).astype(jnp.bfloat16)
        )
        grad_hidden_w = inner_rows(normed_two_all, grad_hidden_all)
        grad_normed_two = token_sums(by_transpose(grad_hidden_all, w_hidden))
        gain_two_grad, grad_residual = norm_backward(
            grad_normed_two, factor_two, scaled_two, gain_two
        )
        grad_residual = grad_residual + grad_result
        grad_residual_all = group_rows(grad_residual.astype(jnp.bfloat16))
        grad_out_w = inner_rows(gated_all, grad_residual_all)
        grad_gated = row_partials(
            by_transpose(grad_residual_all, w_out), col_count, blocks, quarter
        )
        grad_attended = (grad_gated * gate_sig).astype(jnp.bfloat16)
        grad_logit = (grad_gated * attended * gate_sig * (1.0 - gate_sig)).astype(jnp.bfloat16)
        grad_att_prompt = own_prompt_part(grad_attended).reshape(-1, heads_here, HEAD_DIM)
        grad_att_cont = grad_attended[:, prompt_blocks:, 0].reshape(
            CONTS, quarter, heads_here, HEAD_DIM
        )
        again_prompt = jnp.exp(
            prompt_scores(query_prompt, key_prompt, cum_query_prompt, cum_prompt, prompt_ok)
            - total_prompt
        )
        grad_prob_prompt = jnp.einsum(
            "qhd,khd->hqk", grad_att_prompt, value_prompt, preferred_element_type=jnp.float32
        )
        grad_score_prompt = (
            again_prompt
            * (grad_prob_prompt - jnp.sum(again_prompt * grad_prob_prompt, axis=-1, keepdims=True))
        ).astype(jnp.bfloat16)
        again_prompt_b = again_prompt.astype(jnp.bfloat16)
        grad_query_prompt = (
            jnp.einsum(
                "hqk,khd->qhd", grad_score_prompt, key_prompt, preferred_element_type=jnp.float32
            )
            * score_scale
        )
        grad_key_prompt = (
            jnp.einsum(
                "hqk,qhd->khd", grad_score_prompt, query_prompt, preferred_element_type=jnp.float32
            )
            * score_scale
        )
        grad_value_prompt = jnp.einsum(
            "hqk,qhd->khd", again_prompt_b, grad_att_prompt, preferred_element_type=jnp.float32
        )
        cum_grad_query_p = jnp.sum(grad_score_prompt, axis=-1, dtype=jnp.float32).T
        cum_grad_key_p = -jnp.sum(grad_score_prompt, axis=1, dtype=jnp.float32).T
        again_cont = jnp.exp(
            cont_scores(
                query_cont,
                key_prompt,
                key_cont,
                cum_query_cont,
                cum_prompt,
                cum_cont,
                far_ok,
                near_ok,
            )
            - total_cont
        )
        grad_prob_cont = jnp.concatenate(
            [
                jnp.einsum(
                    "jqhd,khd->jhqk",
                    grad_att_cont,
                    value_prompt,
                    preferred_element_type=jnp.float32,
                ),
                jnp.einsum(
                    "jqhd,jkhd->jhqk", grad_att_cont, value_cont, preferred_element_type=jnp.float32
                ),
            ],
            axis=-1,
        )
        grad_score_cont = (
            again_cont
            * (grad_prob_cont - jnp.sum(again_cont * grad_prob_cont, axis=-1, keepdims=True))
        ).astype(jnp.bfloat16)
        again_cont_b = again_cont.astype(jnp.bfloat16)
        far_grad = grad_score_cont[..., :PROMPT]
        near_grad = grad_score_cont[..., PROMPT:]
        grad_query_cont = (
            jnp.einsum("jhqk,khd->jqhd", far_grad, key_prompt, preferred_element_type=jnp.float32)
            + jnp.einsum("jhqk,jkhd->jqhd", near_grad, key_cont, preferred_element_type=jnp.float32)
        ) * score_scale
        grad_key_far = (
            jnp.einsum("jhqk,jqhd->khd", far_grad, query_cont, preferred_element_type=jnp.float32)
            * score_scale
        )
        grad_key_near = (
            jnp.einsum("jhqk,jqhd->jkhd", near_grad, query_cont, preferred_element_type=jnp.float32)
            * score_scale
        )
        grad_value_far = jnp.einsum(
            "jhqk,jqhd->khd",
            again_cont_b[..., :PROMPT],
            grad_att_cont,
            preferred_element_type=jnp.float32,
        )
        grad_value_near = jnp.einsum(
            "jhqk,jqhd->jkhd",
            again_cont_b[..., PROMPT:],
            grad_att_cont,
            preferred_element_type=jnp.float32,
        )
        cum_grad_query_c = jnp.sum(grad_score_cont, axis=-1, dtype=jnp.float32).transpose(0, 2, 1)
        cum_grad_key_far = -jnp.sum(far_grad, axis=(0, 2), dtype=jnp.float32).T
        cum_grad_key_near = -jnp.sum(near_grad, axis=2, dtype=jnp.float32).transpose(0, 2, 1)
        kv_grad_prompt = jnp.stack(
            [grad_key_prompt + grad_key_far, grad_value_prompt + grad_value_far], axis=1
        ).reshape(col_count, local_prompt, 2 * width_here)
        kv_grad_cont = jnp.stack([grad_key_near, grad_value_near], axis=2).reshape(
            col_count, local_conts * CLEN, 2 * width_here
        )
        kv_grad_part = jnp.concatenate([kv_grad_prompt, kv_grad_cont], axis=1)
        query_place = lax.dynamic_update_slice_in_dim(
            jnp.zeros((col_count, prompt_blocks, row_count, quarter, heads_here), jnp.float32),
            cum_grad_query_p.reshape(col_count, prompt_blocks, 1, quarter, heads_here),
            row_index,
            axis=2,
        ).reshape(PROMPT, heads_here)
        cont_place = lax.dynamic_update_slice_in_dim(
            jnp.zeros((CONTS, row_count, quarter, heads_here), jnp.float32),
            cum_grad_query_c.reshape(CONTS, 1, quarter, heads_here),
            row_index,
            axis=1,
        ).reshape(CONTS, CLEN, heads_here)
        cum_grad_part = jnp.concatenate(
            [
                (cum_grad_key_p + cum_grad_key_far + query_place).reshape(
                    col_count, local_prompt, heads_here
                ),
                (cum_grad_key_near + cont_place).reshape(col_count, local_conts * CLEN, heads_here),
            ],
            axis=1,
        )
        kv_grad_full, cum_grad_full = lax.psum((kv_grad_part, cum_grad_part), "row")
        cum_grad_cont = cum_grad_full[:, local_prompt:].reshape(CONTS, CLEN, heads_here)
        cum_grad_prompt = cum_grad_full[:, :local_prompt].reshape(PROMPT, heads_here)
        cum_grad_prompt = cum_grad_prompt + jnp.dot(
            branch_hot.T, jnp.sum(cum_grad_cont, axis=1), precision=highest
        )
        log_grad_prompt = lax.cumsum(cum_grad_prompt, axis=0, reverse=True)
        log_grad_cont = lax.cumsum(cum_grad_cont, axis=1, reverse=True)
        log_grad = jnp.concatenate(
            [
                log_grad_prompt.reshape(col_count, local_prompt, heads_here),
                log_grad_cont.reshape(col_count, local_conts * CLEN, heads_here),
            ],
            axis=1,
        )
        pre_grad = log_grad * jax.nn.sigmoid(-pre_gate)
        bias_grad = jnp.sum(pre_grad, axis=(0, 1))
        forget_grad_b = pre_grad.reshape(-1, heads_here).astype(jnp.bfloat16)
        query_grad_own = jnp.concatenate(
            [
                grad_query_prompt.reshape(col_count, prompt_blocks, 1, quarter, width_here),
                grad_query_cont.reshape(col_count, local_conts, 1, quarter, width_here),
            ],
            axis=1,
        )
        qg_grad_all = head_rows(
            jnp.concatenate([query_grad_own.astype(jnp.bfloat16), grad_logit], axis=-1)
        )
        kv_grad_rows = kv_grad_full.reshape(-1, 2 * width_here).astype(jnp.bfloat16)
        project_grad_rows = jnp.concatenate(
            [qg_grad_all[:, :width_here], kv_grad_rows, qg_grad_all[:, width_here:]], axis=-1
        )
        grad_project_w = inner_rows(normed_all, project_grad_rows)
        grad_forget_w = inner_rows(normed_all, forget_grad_b)
        grad_normed_one = token_sums(
            by_transpose(project_grad_rows, w_project) + by_transpose(forget_grad_b, w_forget)
        )
        gain_one_grad, grad_tokens = norm_backward(
            grad_normed_one, factor_one, scaled_one, gain_one
        )
        grad_tokens = grad_tokens + grad_residual
        grad_prompt_one = grad_tokens[:local_prompt]
        grad_cont_one = grad_tokens[local_prompt:].reshape(local_conts, CLEN, -1)
        group_count = jnp.sum(validity) * (row_index == 0).astype(jnp.float32)
        new_carry = (
            acc_project + grad_project_w,
            acc_forget + grad_forget_w,
            acc_bias + bias_grad,
            acc_out + grad_out_w,
            acc_hidden + grad_hidden_w,
            acc_down + grad_down_w,
            acc_gain_one + gain_one_grad,
            acc_gain_two + gain_two_grad,
            error_sum + group_err,
            count_sum + group_count,
        )
        return (new_carry, (grad_prompt_one, grad_cont_one))

    start = (
        jnp.zeros(w_project.shape, jnp.float32),
        jnp.zeros(w_forget.shape, jnp.float32),
        jnp.zeros(forget_bias.shape, jnp.float32),
        jnp.zeros(w_out.shape, jnp.float32),
        jnp.zeros(w_hidden.shape, jnp.float32),
        jnp.zeros(w_down.shape, jnp.float32),
        jnp.zeros(first_gain.shape, jnp.float32),
        jnp.zeros(second_gain.shape, jnp.float32),
        jnp.zeros((), jnp.float32),
        jnp.zeros((), jnp.float32),
    )
    finished, (grad_prompt, grad_cont) = lax.scan(
        one_group,
        start,
        (
            x_prompt,
            x_cont,
            teacher_prompt,
            teacher_cont,
            segment_ids,
            offsets,
            prompt_valid,
            cont_valid,
        ),
    )
    (
        acc_project,
        acc_forget,
        acc_bias,
        acc_out,
        acc_hidden,
        acc_down,
        acc_gain_one,
        acc_gain_two,
        error_sum,
        count_sum,
    ) = finished
    acc_project, acc_forget, acc_bias, acc_out, acc_hidden, acc_down = (
        lax.psum(acc_project.astype(jnp.bfloat16), "dp").astype(jnp.float32),
        lax.psum(acc_forget.astype(jnp.bfloat16), "dp").astype(jnp.float32),
        lax.psum(acc_bias.astype(jnp.bfloat16), "dp").astype(jnp.float32),
        lax.psum(acc_out.astype(jnp.bfloat16), "dp").astype(jnp.float32),
        lax.psum(acc_hidden.astype(jnp.bfloat16), "dp").astype(jnp.float32),
        lax.psum(acc_down.astype(jnp.bfloat16), "dp").astype(jnp.float32),
    )
    gain_one_total, gain_two_total = lax.psum((acc_gain_one, acc_gain_two), ("dp", "col"))
    error_total, count_total = lax.psum((error_sum, count_sum), ("dp", "row", "col"))
    grad_scale = x_prompt.shape[0] * lax.axis_size("dp") * (PROMPT + CONTS * CLEN) / count_total
    loss_value = error_total / (D * count_total)
    width_here = w_query.shape[1]
    units_here = w_gate.shape[1]
    return (
        loss_value,
        grad_prompt * grad_scale,
        grad_cont * grad_scale,
        gain_one_total * grad_scale,
        acc_project[:, :width_here] * grad_scale,
        acc_project[:, width_here : 2 * width_here] * grad_scale,
        acc_project[:, 2 * width_here : 3 * width_here] * grad_scale,
        acc_project[:, 3 * width_here :] * grad_scale,
        acc_forget * grad_scale,
        acc_bias * grad_scale,
        acc_out * grad_scale,
        gain_two_total * grad_scale,
        acc_hidden[:, :units_here] * grad_scale,
        acc_hidden[:, units_here:] * grad_scale,
        acc_down * grad_scale,
    )


AX = ("yo", "y", "c", "x", "zh", "zl")
FAR_PIECE = 18
DOC_LANE = 36
UNIT_LANE = 40
NEVER = 1e12
LANES = 128
BF = jnp.bfloat16
F32 = jnp.float32


class Ring:
    def __init__(self, sizes):
        self.sizes = sizes
        self.zl_count = sizes["zl"]
        self.offsets = [(dy, dz) for dy in range(2) for dz in range(self.zl_count)]
        self.back = [
            self.offsets.index(((-dy) % 2, (-dz) % self.zl_count)) for dy, dz in self.offsets
        ]

    def pairs(self, target, source_ok=None):
        ranges = [range(self.sizes[a]) for a in AX]
        number = {}
        for place, coords in enumerate(itertools.product(*ranges)):
            number[coords] = place
        out = []
        for coords in number:
            here = dict(zip(AX, coords))
            if source_ok is not None and not source_ok(here):
                continue
            there = dict(here, **target(here))
            out.append((number[coords], number[tuple(there[a] for a in AX)]))
        return out

    def move(self, value, target, source_ok=None):
        return lax.ppermute(value, AX, self.pairs(target, source_ok))

    def swap(self, value, axis, source_ok=None):
        return self.move(value, lambda h: {axis: 1 - h[axis]}, source_ok)

    def to_peer(self, value, k):
        dy, dz = self.offsets[k]
        return self.move(
            value, lambda h: {"y": (h["y"] + dy) % 2, "zl": (h["zl"] + dz) % self.zl_count}
        )

    def to_group(self, value, flip):
        return self.move(
            value,
            lambda h: {
                "y": h["zh"],
                "c": h["x"] ^ flip,
                "x": h["y"],
                "zh": h["c"],
            },
        )

    def from_group(self, value, flip):
        return self.move(
            value,
            lambda h: {"y": h["x"], "c": h["zh"], "x": h["c"] ^ flip, "zh": h["y"]},
        )

    def total(self, value):
        for axis in ("c", "y", "x", "zh"):
            value = value + self.swap(value, axis)
        if self.zl_count == 2:
            value = value + self.swap(value, "zl")
        elif self.zl_count > 2:
            value = lax.psum(value, "zl")
        if self.sizes["yo"] > 1:
            value = lax.psum(value, "yo")
        return value

    def gather(self, rows):
        return [rows] + [self.to_peer(rows, k) for k in range(1, len(self.offsets))]

    def scatter_sum(self, partial_of):
        arrived = []
        for k in range(1, len(self.offsets)):
            arrived.append(self.to_peer(partial_of(self.back[k]).astype(BF), k))
        total = partial_of(0)
        for part in arrived:
            total = total + part.astype(F32)
        return total


def nt_dot(left_op, right_op):
    return lax.dot_general(
        left_op, right_op, (((1,), (1,)), ((), ())), preferred_element_type=F32
    )


def tn_dot(left_op, right_op):
    return lax.dot_general(
        left_op, right_op, (((0,), (0,)), ((), ())), preferred_element_type=F32
    )


def nn_dot(left_op, right_op):
    return jnp.dot(left_op, right_op, preferred_element_type=F32)


def split_pieces(values, shift, heads):
    high = values.astype(BF).astype(F32)
    rest = values - high
    mid = rest.astype(BF).astype(F32)
    low = (rest - mid).astype(BF).astype(F32)
    out = None
    for place, piece in enumerate((high, mid, low)):
        amount = shift + place * heads
        moved = pltpu.roll(piece, amount, 1) if amount else piece
        out = moved if out is None else out + moved
    return out


def head_lanes(shape, head, heads):
    lane = lax.broadcasted_iota(jnp.int32, shape, len(shape) - 1)
    keep = lane >= DOC_LANE
    for place in range(3):
        keep = keep | (lane == place * heads + head) | (lane == FAR_PIECE + place * heads + head)
    return keep


def half_lanes(shape, half):
    lane = lax.broadcasted_iota(jnp.int32, shape, len(shape) - 1)
    return (lane >= HEAD_DIM * half) & (lane < HEAD_DIM * (half + 1))


def near_visible(rows):
    key_row = lax.broadcasted_iota(jnp.int32, (rows, rows), 0)
    query_row = lax.broadcasted_iota(jnp.int32, (rows, rows), 1)
    same = (key_row // CLEN) == (query_row // CLEN)
    return same & (key_row <= query_row)


def fill_keys(
    keys, flag, far_own, far_there, kv_near, cum_far, cum_near, far_base, near_base, far_rows, heads
):
    slots = heads // 2

    @pl.when(pl.program_id(0) == 0)
    def _():
        aug = (far_base[...].astype(F32) + split_pieces(-cum_far[...], FAR_PIECE, heads)).astype(BF)
        for s in range(slots):
            keys[s, :far_rows, LANES:] = aug

        @pl.when(flag[0] == 0)
        def _():
            for s in range(slots):
                keys[s, :far_rows, :LANES] = far_own[s][:, :LANES]

        @pl.when(flag[0] != 0)
        def _():
            for s in range(slots):
                keys[s, :far_rows, :LANES] = far_there[s][:, :LANES]

    aug = (near_base[...].astype(F32) + split_pieces(-cum_near[...], FAR_PIECE, heads)).astype(BF)
    for s in range(slots):
        keys[s, far_rows:, :LANES] = kv_near[s][:, :LANES]
        keys[s, far_rows:, LANES:] = aug


def attend_kernel(
    heads,
    flag,
    qg_a,
    qg_b,
    qg_c,
    near_a,
    near_b,
    near_c,
    own_a,
    own_b,
    own_c,
    there_a,
    there_b,
    there_c,
    cum_near,
    cum_far,
    q_base,
    near_base,
    far_base,
    gated_ref,
    att_ref,
    log_ref,
    keys,
    vals,
):
    qg = (qg_a, qg_b, qg_c)
    kv_near = (near_a, near_b, near_c)
    far_own = (own_a, own_b, own_c)
    far_there = (there_a, there_b, there_c)
    rows = qg_a.shape[0]
    far_rows = own_a.shape[0]
    slots = heads // 2
    fill_keys(
        keys,
        flag,
        far_own,
        far_there,
        kv_near,
        cum_far,
        cum_near,
        far_base,
        near_base,
        far_rows,
        heads,
    )

    @pl.when(pl.program_id(0) == 0)
    def _():
        def fill(source):
            for s in range(slots):
                moved = source[s][:, LANES:].T
                for half in range(2):
                    vals[2 * s + half, :HEAD_DIM, :far_rows] = moved[
                        HEAD_DIM * half : HEAD_DIM * (half + 1)
                    ]

        @pl.when(flag[0] == 0)
        def _():
            fill(far_own)

        @pl.when(flag[0] != 0)
        def _():
            fill(far_there)

        for h in range(heads):
            vals[h, HEAD_DIM:, :] = jnp.ones((16, far_rows + rows), BF)

    for s in range(slots):
        moved = kv_near[s][:, LANES:].T
        for half in range(2):
            vals[2 * s + half, :HEAD_DIM, far_rows:] = moved[
                HEAD_DIM * half : HEAD_DIM * (half + 1)
            ]
    q_aug = (q_base[...].astype(F32) + split_pieces(cum_near[...], 0, heads)).astype(BF)
    visible = near_visible(rows)
    outs = []
    logs = []
    for h in range(heads):
        s, half = h // 2, h % 2
        query = qg[s][:, :LANES]
        query = jnp.where(half_lanes(query.shape, half), query * BF(HEAD_DIM**-0.5), BF(0))
        aug = jnp.where(head_lanes(q_aug.shape, h, heads), q_aug, BF(0))
        q_cat = jnp.concatenate([query, aug], axis=1)
        far = nt_dot(keys[s, :far_rows], q_cat)
        near = jnp.where(visible, nt_dot(keys[s, far_rows:], q_cat), -NEVER)
        top = jnp.maximum(
            jnp.max(far, axis=0, keepdims=True), jnp.max(near, axis=0, keepdims=True)
        )
        far_p = jnp.exp(far - top).astype(BF)
        near_p = jnp.exp(near - top).astype(BF)
        out = nn_dot(vals[h, :, :far_rows], far_p) + nn_dot(vals[h, :, far_rows:], near_p)
        total = out[HEAD_DIM : HEAD_DIM + 1]
        outs.append(out[:HEAD_DIM] / total)
        logs.append(top + jnp.log(total))
    att = jnp.concatenate(outs, axis=0).T
    att_ref[...] = att
    for s in range(slots):
        gate = qg[s][:, LANES:].astype(F32)
        cols = slice(s * LANES, (s + 1) * LANES)
        gated_ref[:, cols] = (att[:, cols] * jax.nn.sigmoid(gate)).astype(BF)
    log_rows = jnp.concatenate(logs + [jnp.zeros((LANES - heads, rows), F32)], axis=0)
    log_ref[...] = log_rows.T


def row_block(rows, cols, place=0):
    return pl.BlockSpec((rows, cols), lambda i: (i, place))


def whole_block(rows, cols):
    return pl.BlockSpec((rows, cols), lambda i: (0, 0))


def slot_inputs(flag, projects, kv_there, rows):
    far_rows = projects[0].shape[0]
    specs_in = [pl.BlockSpec(memory_space=pltpu.SMEM)]
    for spec in (
        row_block(rows, 2 * LANES),
        row_block(rows, 2 * LANES, 1),
        pl.BlockSpec((far_rows, 2 * LANES), lambda i: (0, 1)),
        whole_block(far_rows, 2 * LANES),
    ):
        specs_in += [spec] * len(projects)
    return specs_in, [flag, *projects, *projects, *projects, *kv_there]


def cum_specs(rows, far_rows):
    return [
        row_block(rows, LANES),
        whole_block(far_rows, LANES),
        row_block(rows, LANES),
        row_block(rows, LANES),
        whole_block(far_rows, LANES),
    ]


def attend(flag, projects, kv_there, cum_near, cum_far, q_base, near_base, far_base, rows, heads):
    total = projects[0].shape[0]
    width = heads * HEAD_DIM
    steps = total // rows
    flops = 2 * total * (total + rows) * heads * 384
    slot_specs, slot_values = slot_inputs(flag, projects, kv_there, rows)
    return pl.pallas_call(
        functools.partial(attend_kernel, heads),
        grid=(steps,),
        out_shape=(
            jax.ShapeDtypeStruct((total, width), BF),
            jax.ShapeDtypeStruct((total, width), F32),
            jax.ShapeDtypeStruct((total, LANES), F32),
        ),
        in_specs=slot_specs + cum_specs(rows, total),
        out_specs=(row_block(rows, width), row_block(rows, width), row_block(rows, LANES)),
        scratch_shapes=[
            pltpu.VMEM((heads // 2, total + rows, 2 * LANES), BF),
            pltpu.VMEM((heads, HEAD_DIM + 16, total + rows), BF),
        ],
        compiler_params=pltpu.CompilerParams(vmem_limit_bytes=48 << 20),
        cost_estimate=pl.CostEstimate(
            flops=flops, bytes_accessed=total * width * 20, transcendentals=total * total * heads
        ),
    )(*slot_values, cum_near, cum_far, q_base, near_base, far_base)


def attend_back_kernel(
    heads,
    flag,
    qg_a,
    qg_b,
    qg_c,
    near_a,
    near_b,
    near_c,
    own_a,
    own_b,
    own_c,
    there_a,
    there_b,
    there_c,
    cum_near,
    cum_far,
    q_base,
    near_base,
    far_base,
    grad_ref,
    att_ref,
    log_ref,
    dqg_ref,
    near_ref,
    far_out,
    row_ref,
    near_col,
    far_col,
    keys,
    vals,
    far_ref,
):
    qg = (qg_a, qg_b, qg_c)
    kv_near = (near_a, near_b, near_c)
    far_own = (own_a, own_b, own_c)
    far_there = (there_a, there_b, there_c)
    rows = qg_a.shape[0]
    far_rows = own_a.shape[0]
    slots = heads // 2
    fill_keys(
        keys,
        flag,
        far_own,
        far_there,
        kv_near,
        cum_far,
        cum_near,
        far_base,
        near_base,
        far_rows,
        heads,
    )

    @pl.when(pl.program_id(0) == 0)
    def _():
        lane = lax.broadcasted_iota(jnp.int32, (far_rows + rows, LANES), 1)
        ones = (lane < 3).astype(F32).astype(BF)
        for s in range(slots):
            vals[s, :, LANES:] = ones

        @pl.when(flag[0] == 0)
        def _():
            for s in range(slots):
                vals[s, :far_rows, :LANES] = far_own[s][:, LANES:]

        @pl.when(flag[0] != 0)
        def _():
            for s in range(slots):
                vals[s, :far_rows, :LANES] = far_there[s][:, LANES:]

        far_ref[...] = jnp.zeros(far_ref.shape, F32)
        far_col[...] = jnp.zeros(far_col.shape, F32)

    for s in range(slots):
        vals[s, far_rows:, :LANES] = kv_near[s][:, LANES:]
    q_aug = (q_base[...].astype(F32) + split_pieces(cum_near[...] - log_ref[...], 0, heads)).astype(
        BF
    )
    visible = near_visible(rows)
    lane = lax.broadcasted_iota(jnp.int32, (rows, LANES), 1)
    row_total = jnp.zeros((rows, LANES), F32)
    col_total = jnp.zeros((rows, LANES), F32)
    for s in range(slots):
        cols = slice(s * LANES, (s + 1) * LANES)
        kcols = slice(2 * s * LANES, (2 * s + 1) * LANES)
        vcols = slice((2 * s + 1) * LANES, (2 * s + 2) * LANES)
        gate_sig = jax.nn.sigmoid(qg[s][:, LANES:].astype(F32))
        grad = grad_ref[:, cols].astype(F32)
        att = att_ref[:, cols]
        grad_att = (grad * gate_sig).astype(BF)
        dqg_ref[:, vcols] = (grad * att * gate_sig * (1.0 - gate_sig)).astype(BF)
        weighed = grad_att.astype(F32) * att
        dq_total = jnp.zeros((rows, LANES), F32)
        dk_near = jnp.zeros((rows, LANES), F32)
        dv_near = jnp.zeros((rows, LANES), F32)
        for half in range(2):
            h = 2 * s + half
            mine = half_lanes((rows, LANES), half)
            query = jnp.where(mine, qg[s][:, :LANES] * BF(HEAD_DIM**-0.5), BF(0))
            aug = jnp.where(head_lanes(q_aug.shape, h, heads), q_aug, BF(0))
            q_cat = jnp.concatenate([query, aug], axis=1)
            ga = jnp.where(mine, grad_att, BF(0))
            delta = -jnp.sum(jnp.where(mine, weighed, 0.0), axis=1, keepdims=True)
            high = delta.astype(BF).astype(F32)
            mid = (delta - high).astype(BF).astype(F32)
            low = delta - high - mid
            d_aug = jnp.where(
                lane == 0, high, jnp.where(lane == 1, mid, jnp.where(lane == 2, low, 0.0))
            ).astype(BF)
            ga_cat = jnp.concatenate([ga, d_aug], axis=1)
            for part in range(2):
                span = slice(0, far_rows) if part == 0 else slice(far_rows, far_rows + rows)
                prob = jnp.exp(nt_dot(keys[s, span], q_cat))
                if part == 1:
                    prob = jnp.where(visible, prob, 0.0)
                ds = (prob * nt_dot(vals[s, span], ga_cat)).astype(BF)
                dv = nn_dot(prob.astype(BF), ga)
                dk = nn_dot(ds, q_cat)
                dq = tn_dot(ds, keys[s, span])
                dq_total += jnp.where(mine, dq[:, :LANES], 0.0)
                row_total += jnp.where(lane == h, dq[:, LANES:], 0.0)
                if part == 0:
                    far_ref[:, kcols] += dk[:, :LANES]
                    far_ref[:, vcols] += dv
                    far_col[...] += dk[:, LANES:]
                else:
                    dk_near += dk[:, :LANES]
                    dv_near += dv
                    col_total += dk[:, LANES:]
        dqg_ref[:, kcols] = (dq_total * HEAD_DIM**-0.5).astype(BF)
        near_ref[:, kcols] = dk_near
        near_ref[:, vcols] = dv_near
    row_ref[...] = row_total
    near_col[...] = col_total

    @pl.when(pl.program_id(0) == pl.num_programs(0) - 1)
    def _():
        far_out[...] = far_ref[...].astype(BF)


def attend_back(
    flag,
    projects,
    kv_there,
    cum_near,
    cum_far,
    q_base,
    near_base,
    far_base,
    grad,
    att,
    logs,
    rows,
    heads,
):
    total = projects[0].shape[0]
    width = heads * HEAD_DIM
    steps = total // rows
    flops = 2 * total * (total + rows) * heads * 1152
    slot_specs, slot_values = slot_inputs(flag, projects, kv_there, rows)
    return pl.pallas_call(
        functools.partial(attend_back_kernel, heads),
        grid=(steps,),
        out_shape=(
            jax.ShapeDtypeStruct((total, 2 * width), BF),
            jax.ShapeDtypeStruct((total, 2 * width), F32),
            jax.ShapeDtypeStruct((total, 2 * width), BF),
            jax.ShapeDtypeStruct((total, LANES), F32),
            jax.ShapeDtypeStruct((total, LANES), F32),
            jax.ShapeDtypeStruct((total, LANES), F32),
        ),
        in_specs=slot_specs
        + cum_specs(rows, total)
        + [row_block(rows, width), row_block(rows, width), row_block(rows, LANES)],
        out_specs=(
            row_block(rows, 2 * width),
            row_block(rows, 2 * width),
            whole_block(total, 2 * width),
            row_block(rows, LANES),
            row_block(rows, LANES),
            whole_block(total, LANES),
        ),
        scratch_shapes=[
            pltpu.VMEM((heads // 2, total + rows, 2 * LANES), BF),
            pltpu.VMEM((heads // 2, total + rows, 2 * LANES), BF),
            pltpu.VMEM((total, 2 * width), F32),
        ],
        compiler_params=pltpu.CompilerParams(vmem_limit_bytes=56 << 20),
        cost_estimate=pl.CostEstimate(
            flops=flops, bytes_accessed=total * width * 40, transcendentals=total * total * heads
        ),
    )(*slot_values, cum_near, cum_far, q_base, near_base, far_base, grad, att, logs)


def full_norm(tokens, gain_vec):
    factor = lax.rsqrt(jnp.mean(tokens * tokens, axis=-1, keepdims=True) + epsilon)
    scaled = tokens * factor
    return factor, scaled, (scaled * gain_vec).astype(BF)


def full_norm_back(grad_normed, factor, scaled, gain_vec):
    e = grad_normed * gain_vec
    mean = jnp.mean(e * scaled, axis=-1, keepdims=True)
    return jnp.sum(grad_normed * scaled, axis=0), factor * (e - scaled * mean)


MESH_ID = pl.DeviceIdType.MESH


class Here:
    def __init__(self, ring):
        self.ring = ring
        self.at = {a: lax.axis_index(a) for a in AX}

    def other(self, axis):
        return {axis: 1 - self.at[axis]}

    def peer(self, k):
        dy, dz = self.ring.offsets[k]
        return {
            "y": lax.rem(self.at["y"] + dy, 2),
            "zl": lax.rem(self.at["zl"] + dz, self.ring.zl_count),
        }

    def group_to(self, flip):
        at = self.at
        return {"y": at["zh"], "c": at["x"] ^ flip, "x": at["y"], "zh": at["c"]}

    def group_from(self, flip):
        at = self.at
        return {"y": at["x"], "c": at["zh"], "x": at["c"] ^ flip, "zh": at["y"]}

    def group_away(self):
        at = self.at
        return ~((at["y"] == at["zh"]) & (at["y"] == at["x"]) & (at["y"] == at["c"]))

    def greet_group(self, targets):
        away = self.group_away()
        self.greet(
            targets + [self.group_to(1), self.group_from(1)],
            [(self.group_to(0), away), (self.group_from(0), away)],
        )

    def greet(self, targets, extra=()):
        barrier = pltpu.get_barrier_semaphore()
        for target in targets:
            pl.semaphore_signal(barrier, inc=1, device_id=target, device_id_type=MESH_ID)
        count = len(targets)
        for target, away in extra:
            @pl.when(away)
            def _():
                pl.semaphore_signal(barrier, inc=1, device_id=target, device_id_type=MESH_ID)

            count = count + away.astype(jnp.int32)
        pl.semaphore_wait(barrier, count)


def remote(src, dst, send_sem, recv_sem, target):
    return pltpu.make_async_remote_copy(
        src_ref=src,
        dst_ref=dst,
        send_sem=send_sem,
        recv_sem=recv_sem,
        device_id=target,
        device_id_type=MESH_ID,
    )


def last_kernel(
    ring,
    heads,
    dqg_in,
    near_in,
    far_in,
    row_in,
    near_col_in,
    far_col_in,
    weight_in,
    normed_in,
    gated_in,
    mixed_in,
    tokens_in,
    residual_in,
    hid_in,
    down_in,
    gain_ref,
    forget_w,
    sig_ref,
    hot_ref,
    error_ref,
    gain_two_ref,
    valid_ref,
    back_out,
    proj_out,
    gate_out,
    up_out,
    down_out,
    out_out,
    small_out,
    grads,
    near,
    far_own,
    far_land,
    row_sum,
    near_col,
    far_col,
    far_col_land,
    cum,
    tot_send,
    tot_land,
    weight,
    normed,
    gated,
    mixed,
    tokens,
    residual,
    rs_send,
    rs_land,
    total,
    c_send,
    c_land,
    kept,
    x_send,
    x_land,
    z_send,
    z_land,
    final,
    kept_f,
    xf_send,
    xf_land,
    zf_send,
    zf_land,
    final_f,
    yf_land,
    full_f,
    co_send,
    co_land,
    kept_o,
    xo_send,
    xo_land,
    zo_send,
    zo_land,
    final_o,
    blocks,
    gain_sum,
    gain_nat,
    gain_land,
    load_sem,
    local_sem,
    swap_send_sem,
    swap_recv_sem,
    y_send_sem,
    y_recv_sem,
    c2_send_sem,
    c2_recv_sem,
    rs_send_sem,
    rs_recv_sem,
    c_send_sem,
    c_recv_sem,
    x_send_sem,
    x_recv_sem,
    z_send_sem,
    z_recv_sem,
    back_send_sem,
    back_recv_sem,
    gain_send_sem,
    gain_recv_sem,
):
    here = Here(ring)
    y, c, x, zh, zl = (here.at[a] for a in ("y", "c", "x", "zh", "zl"))
    local, features = tokens.shape
    rows_all = normed.shape[0]
    part = features // 4
    slot_w = 4 * LANES
    slots = heads // 2
    all_w = slots * slot_w
    units = down_in.shape[0]
    owner = zh == y
    peers = len(ring.offsets)
    away = here.group_away()
    all_loads = [
        (row_in, row_sum),
        (near_col_in, near_col),
        (far_col_in, far_col),
        (far_in, far_own),
        (near_in, near),
    ]
    for s in range(slots):
        all_loads.append(
            (
                dqg_in.at[:, 2 * s * LANES : 2 * (s + 1) * LANES],
                grads.at[:, s * slot_w : s * slot_w + 2 * LANES],
            )
        )
    all_loads += [
        (normed_in, normed),
        (weight_in, weight),
        (gated_in, gated),
        (mixed_in, mixed),
        (tokens_in, tokens),
        (residual_in, residual),
    ]
    loads = [
        pltpu.make_async_copy(a, b, load_sem.at[i]) for i, (a, b) in enumerate(all_loads)
    ]
    for copy in loads:
        copy.start()
    load_row, load_near_col, load_far_col, load_far, load_near = loads[:5]
    load_dqg = loads[5 : 5 + slots]
    load_normed, load_weight, load_gated, load_mixed, load_tokens, load_residual = loads[5 + slots :]

    here.greet_group(
        [here.peer(k) for k in range(1, peers)]
        + [here.other("c"), here.other("x"), here.other("zh")]
    )
    far_swap = remote(
        far_in, far_land, swap_send_sem.at[0], swap_recv_sem.at[0], here.other("c")
    )
    far_swap.start()
    col_swap = remote(
        far_col_in, far_col_land, swap_send_sem.at[1], swap_recv_sem.at[1], here.other("c")
    )
    col_swap.start()

    lane = lax.broadcasted_iota(jnp.int32, (CLEN, LANES), 1)
    head_lane = lane < heads
    all_units = rows_all // CLEN
    chunk_units = local // CLEN

    def unit_rows(u):
        return slice(u * CLEN, (u + 1) * CLEN)

    load_row.wait()
    load_near_col.wait()
    for u in range(all_units):
        value = row_sum[unit_rows(u), :] - pltpu.roll(
            near_col[unit_rows(u), :], LANES - FAR_PIECE, 1
        )
        value = jnp.where(head_lane, value, 0.0)
        cum[unit_rows(u), :] = value
        tot_send[u : u + 1, :] = jnp.sum(value, axis=0, keepdims=True)
    tot_swap = remote(
        tot_send.at[:all_units],
        tot_land.at[:all_units],
        swap_send_sem.at[2],
        swap_recv_sem.at[2],
        here.other("c"),
    )
    tot_swap.start()

    load_gated.wait()
    load_mixed.wait()
    out_rows = slots * LANES

    def out_tile(s, cols):
        return tn_dot(gated[:, s * LANES : (s + 1) * LANES], mixed[:, cols])

    for s in range(slots):
        co_send[s * LANES : (s + 1) * LANES, :] = out_tile(
            s, slice(2 * part, features)
        ).astype(BF)
    co_copy = remote(co_send, co_land, c_send_sem.at[1], c_recv_sem.at[1], here.other("c"))
    co_copy.start()

    load_far.wait()
    load_near.wait()
    for copy in load_dqg:
        copy.wait()
    far_swap.wait_recv()
    on_prompt = jnp.where(c == 0, 1.0, 0.0)

    def merge(i, carry):
        rows = pl.ds(pl.multiple_of(i * CLEN, CLEN), CLEN)
        value = near[rows, :] + on_prompt * (
            far_own[rows, :].astype(F32) + far_land[rows, :].astype(F32)
        )
        value = value.astype(BF)
        for s in range(slots):
            grads[rows, s * slot_w + 2 * LANES : (s + 1) * slot_w] = value[
                :, 2 * s * LANES : 2 * (s + 1) * LANES
            ]
        return carry

    lax.fori_loop(0, all_units, merge, 0)
    load_far_col.wait()
    col_swap.wait_recv()
    tot_swap.wait_recv()

    @pl.when(c == 0)
    def _():
        for u in range(all_units):
            both = far_col[unit_rows(u), :] + far_col_land[unit_rows(u), :]
            value = cum[unit_rows(u), :] - jnp.where(
                head_lane, pltpu.roll(both, LANES - FAR_PIECE, 1), 0.0
            )
            for j in range(all_units):
                value = value + hot_ref[unit_rows(u), j : j + 1] * tot_land[j : j + 1, :]
            cum[unit_rows(u), :] = value

    step_row = lax.broadcasted_iota(jnp.int32, (CLEN, CLEN), 0)
    step_col = lax.broadcasted_iota(jnp.int32, (CLEN, CLEN), 1)
    tri_back = (step_col >= step_row).astype(F32)
    for u in range(all_units):
        value = jnp.dot(
            tri_back,
            cum[unit_rows(u), :],
            precision=highest,
            preferred_element_type=F32,
        )
        cum[unit_rows(u), :] = value
        tot_send[all_units + u : all_units + u + 1, :] = value[0:1, :]
    places = []
    for dy, dz in ring.offsets:
        place = lax.rem(y + 2 - dy, 2) * ring.zl_count + lax.rem(
            zl + ring.zl_count - dz, ring.zl_count
        )
        for i in range(chunk_units):
            places.append(place * chunk_units + i)
    bias = jnp.zeros((1, LANES), F32)
    for u in range(all_units):
        suffix = jnp.zeros((1, LANES), F32)
        for other in range(all_units):
            if other != u:
                seen = jnp.where((places[other] > places[u]) & (c == 0), 1.0, 0.0)
                suffix = suffix + seen * tot_send[all_units + other : all_units + other + 1, :]
        value = (cum[unit_rows(u), :] + suffix) * sig_ref[unit_rows(u), :]
        grads[unit_rows(u), all_w:] = value.astype(BF)
        bias = bias + jnp.sum(value, axis=0, keepdims=True)

    load_normed.wait()
    tile_r = LANES
    per_part = part // tile_r

    def weight_tile(first, i):
        cols = pl.ds(pl.multiple_of(first + i * tile_r, LANES), tile_r)
        return tn_dot(normed[:, cols], grads[...])

    def c_step(i, carry):
        rows = pl.ds(pl.multiple_of(i * tile_r, tile_r), tile_r)
        c_send[rows, :] = weight_tile(2 * part, i).astype(BF)
        return carry

    lax.fori_loop(0, 2 * per_part, c_step, 0)
    c_copy = remote(c_send, c_land, c_send_sem.at[0], c_recv_sem.at[0], here.other("c"))
    c_copy.start()

    load_weight.wait()
    tiles = 3
    tile_w = features // tiles

    def partial_rows(chunk_no, store):
        rows = slice(chunk_no * local, (chunk_no + 1) * local)

        def step(i, carry):
            cols = pl.ds(pl.multiple_of(i * tile_w, LANES), tile_w)
            value = nn_dot(grads[rows, all_w:], forget_w[:, cols])
            for s in range(slots):
                value = value + nt_dot(
                    grads[rows, s * slot_w : (s + 1) * slot_w], weight[s, cols, :]
                )
            store(cols, value)
            return carry

        lax.fori_loop(0, tiles, step, 0)

    rs = []
    for k in range(peers - 1, 0, -1):

        def store_out(cols, value, k=k):
            rs_send[k - 1, :, cols] = value.astype(BF)

        partial_rows(ring.back[k], store_out)
        copy = remote(
            rs_send.at[k - 1],
            rs_land.at[k - 1],
            rs_send_sem.at[k - 1],
            rs_recv_sem.at[k - 1],
            here.peer(k),
        )
        copy.start()
        rs.append(copy)

    c_copy.wait_recv()

    def x_step(i, carry):
        rows = pl.ds(pl.multiple_of(i * tile_r, tile_r), tile_r)
        land = pl.ds(pl.multiple_of(part + i * tile_r, tile_r), tile_r)
        value = weight_tile(part, i) + c_land[land, :].astype(F32)
        for s in range(slots):
            x_send[s, rows, :] = value[:, s * slot_w : (s + 1) * slot_w].astype(BF)
        xf_send[rows, :] = value[:, all_w:].astype(BF)
        return carry

    lax.fori_loop(0, per_part, x_step, 0)
    x_copies = {}
    for s in (2, 1, 0):
        x_copies[s] = remote(
            x_send.at[s], x_land.at[s], x_send_sem.at[s], x_recv_sem.at[s], here.other("x")
        )
        x_copies[s].start()
    xf_copy = remote(xf_send, xf_land, x_send_sem.at[3], x_recv_sem.at[3], here.other("x"))
    xf_copy.start()
    co_copy.wait_recv()
    for s in range(slots):
        rows = slice(s * LANES, (s + 1) * LANES)
        xo_send[rows, :] = (
            out_tile(s, slice(part, 2 * part)) + co_land[rows, part:].astype(F32)
        ).astype(BF)
    xo_copy = remote(xo_send, xo_land, x_send_sem.at[4], x_recv_sem.at[4], here.other("x"))
    xo_copy.start()

    def own_step(i, carry):
        rows = pl.ds(pl.multiple_of(i * tile_r, tile_r), tile_r)
        value = weight_tile(0, i) + c_land[rows, :].astype(F32)
        for s in range(slots):
            kept[s, rows, :] = value[:, s * slot_w : (s + 1) * slot_w]
        kept_f[rows, :] = value[:, all_w:]
        return carry

    lax.fori_loop(0, per_part, own_step, 0)
    for s in range(slots):
        rows = slice(s * LANES, (s + 1) * LANES)
        kept_o[rows, :] = out_tile(s, slice(0, part)) + co_land[rows, :part].astype(F32)

    def store_own(cols, value):
        total[:, cols] = value

    partial_rows(0, store_own)

    def z_copy(i, src, dst):
        return remote(src, dst, z_send_sem.at[i], z_recv_sem.at[i], here.other("zh"))

    z_first = z_copy(0, z_send.at[0], z_land.at[0])
    z_mid = z_copy(1, z_send.at[1], z_land.at[1])
    z_forget = z_copy(2, zf_send, zf_land)
    zo_first = z_copy(3, zo_send.at[0], zo_land.at[0])
    zo_mid = z_copy(4, zo_send.at[1], zo_land.at[1])
    x_copies[2].wait_recv()
    z_send[0] = (kept[2] + x_land[2].astype(F32)).astype(BF)
    z_first.start()

    load_tokens.wait()
    load_residual.wait()
    for copy in rs:
        copy.wait_recv()
    gain_sum[...] = jnp.zeros(gain_sum.shape, F32)
    tile_n = 32

    def norm_step(i, carry):
        rows = pl.ds(pl.multiple_of(i * tile_n, tile_n), tile_n)
        tok = tokens[rows, :].astype(F32)
        grad = total[rows, :]
        for k in range(peers - 1):
            grad = grad + rs_land[k, rows, :].astype(F32)
        factor = lax.rsqrt(jnp.mean(tok * tok, axis=-1, keepdims=True) + epsilon)
        scaled_tok = tok * factor
        e = grad * gain_ref[...]
        mean = jnp.mean(e * scaled_tok, axis=-1, keepdims=True)
        out = factor * (e - scaled_tok * mean) + residual[rows, :]
        weighed = jnp.sum(grad * scaled_tok, axis=0, keepdims=True)
        for b in range(4):
            blocks[b, rows, :] = out[:, b * part : (b + 1) * part].astype(BF)
            gain_sum[b, 0:1, :] += weighed[:, b * part : (b + 1) * part]
        return carry

    lax.fori_loop(0, local // tile_n, norm_step, 0)

    def block_no(half, low_high):
        return (half ^ x) + 2 * (low_high ^ c)

    def back_copy(flip, p):
        return remote(
            blocks.at[block_no(c ^ flip, p)],
            back_out.at[c, :, p * part : (p + 1) * part],
            back_send_sem.at[flip, p],
            back_recv_sem.at[flip, p],
            here.group_from(flip),
        )

    def back_own(flip, p):
        return pltpu.make_async_copy(
            blocks.at[block_no(c ^ flip, p)],
            back_out.at[c, :, p * part : (p + 1) * part],
            local_sem.at[5 + p],
        )

    for p in range(2):
        back_copy(1, p).start()

    @pl.when(away)
    def _():
        for p in range(2):
            back_copy(0, p).start()

    @pl.when(~away)
    def _():
        for p in range(2):
            back_own(0, p).start()

    row0 = pl.multiple_of(c * part, part)

    def rows_of(ref, col, width):
        return ref.at[pl.ds(row0, part), pl.ds(pl.multiple_of(col, LANES), width)]

    def cols_of(ref, row, height):
        return ref.at[pl.ds(pl.multiple_of(row, LANES), height), pl.ds(row0, part)]

    def y_copy(i, src, dst):
        return remote(src, dst, y_send_sem.at[i], y_recv_sem.at[i], here.other("y"))

    pieces = [
        (hid_in.at[:, :units], rows_of(gate_out, y * units, units)),
        (hid_in.at[:, units:], rows_of(up_out, y * units, units)),
        (down_in, cols_of(down_out, y * units, units)),
    ]
    own_pieces = [
        pltpu.make_async_copy(src, dst, local_sem.at[i]) for i, (src, dst) in enumerate(pieces)
    ]
    y_pieces = [y_copy(i, src, dst) for i, (src, dst) in enumerate(pieces)]
    for copy in own_pieces + y_pieces:
        copy.start()

    x_copies[1].wait_recv()

    @pl.when(~owner)
    def _():
        z_send[1] = (kept[1] + x_land[1].astype(F32)).astype(BF)
        z_mid.start()

    x_copies[0].wait_recv()
    kept[0] += x_land[0].astype(F32)
    xf_copy.wait_recv()
    kept_f[...] += xf_land[...].astype(F32)
    zf_send[...] = kept_f[...].astype(BF)
    z_forget.start()
    xo_copy.wait_recv()
    kept_o[...] += xo_land[...].astype(F32)
    zo_send[0] = kept_o[2 * LANES :, :].astype(BF)
    zo_first.start()

    @pl.when(~owner)
    def _():
        zo_send[1] = kept_o[LANES : 2 * LANES, :].astype(BF)
        zo_mid.start()

    first_dst = rows_of(proj_out, 2 * y * slot_w, slot_w)
    mid_dst = rows_of(proj_out, slot_w, slot_w)
    out_first_dst = cols_of(out_out, 2 * LANES * y, LANES)
    out_mid_dst = cols_of(out_out, LANES, LANES)
    y_first = y_copy(3, final.at[0], first_dst)
    y_mid = y_copy(4, final.at[1], mid_dst)
    y_forget = y_copy(5, final_f, yf_land)
    yo_first = y_copy(6, final_o.at[0], out_first_dst)
    yo_mid = y_copy(7, final_o.at[1], out_mid_dst)
    own_first = pltpu.make_async_copy(final.at[0], first_dst, local_sem.at[8])
    own_mid = pltpu.make_async_copy(final.at[1], mid_dst, local_sem.at[9])
    own_out_first = pltpu.make_async_copy(final_o.at[0], out_first_dst, local_sem.at[10])
    own_out_mid = pltpu.make_async_copy(final_o.at[1], out_mid_dst, local_sem.at[11])
    own_forget = pltpu.make_async_copy(
        full_f, proj_out.at[pl.ds(row0, part), all_w : all_w + LANES], local_sem.at[12]
    )
    z_first.wait_recv()
    final[0] = (kept[0] + z_land[0].astype(F32)).astype(BF)
    y_first.start()
    own_first.start()

    @pl.when(owner)
    def _():
        z_mid.wait_recv()
        final[1] = (kept[1] + x_land[1].astype(F32) + z_land[1].astype(F32)).astype(BF)
        y_mid.start()
        own_mid.start()

    z_forget.wait_recv()
    f_lane = lax.broadcasted_iota(jnp.int32, (part, LANES), 1)
    there_f = zf_land[...].astype(F32)
    edge = jnp.where(f_lane < 2, kept_f[...] + pltpu.roll(there_f, LANES - 4, 1), 0.0)
    edge = jnp.where(y == 0, edge, pltpu.roll(edge, 4, 1))
    mid_f = jnp.where((f_lane >= 2) & (f_lane < 4) & owner, kept_f[...] + there_f, 0.0)
    final_f[...] = (edge + mid_f).astype(BF)
    y_forget.start()
    zo_first.wait_recv()
    final_o[0] = (kept_o[:LANES, :] + zo_land[0].astype(F32)).astype(BF)
    yo_first.start()
    own_out_first.start()

    @pl.when(owner)
    def _():
        zo_mid.wait_recv()
        final_o[1] = (kept_o[LANES : 2 * LANES, :] + zo_land[1].astype(F32)).astype(BF)
        yo_mid.start()
        own_out_mid.start()

    for copy in own_pieces:
        copy.wait()
    for copy in y_pieces:
        copy.wait_recv()
    c2 = []

    def hand_over(i, view):
        copy = remote(view, view, c2_send_sem.at[i], c2_recv_sem.at[i], here.other("c"))
        copy.start()
        c2.append(copy)

    hand_over(0, gate_out.at[pl.ds(row0, part), :])
    hand_over(1, up_out.at[pl.ds(row0, part), :])
    hand_over(2, down_out.at[:, pl.ds(row0, part)])

    for b in range(4):
        gain_sum[b, 1:2, :] = gain_two_ref[0:1, b * part : (b + 1) * part]
    for b in range(4):
        gain_nat[0, b] = gain_sum[block_no(b // 2, b % 2)]
    wide_lane = lax.broadcasted_iota(jnp.int32, (1, part), 1)
    scalars = jnp.where(
        wide_lane == 0, jnp.sum(error_ref[0:1, :], axis=1, keepdims=True), 0.0
    ) + jnp.where(wide_lane == 1, jnp.sum(valid_ref[...], axis=0, keepdims=True), 0.0)
    small_lane = lax.broadcasted_iota(jnp.int32, (1, LANES), 1)
    for j in range(heads):
        if j < 2:
            quarter, head = zh, 4 * y + j
        elif j < 4:
            quarter, head = y, j
        else:
            quarter, head = 1 - zh, 4 * y + j - 4
        dest = 2 + (quarter * ring.zl_count + zl) * heads + head
        value = jnp.sum(jnp.where(small_lane == j, bias, 0.0), axis=1, keepdims=True)
        scalars = scalars + jnp.where(wide_lane == dest, value, 0.0)
    gain_nat[0, 0, 2:3, :] = scalars
    for place, axis in enumerate(("c", "y", "x", "zl", "zh")):
        copy = remote(
            gain_nat.at[place],
            gain_land.at[place],
            gain_send_sem.at[place],
            gain_recv_sem.at[place],
            here.other(axis),
        )
        copy.start()
        copy.wait_recv()
        gain_nat[place + 1] = gain_nat[place] + gain_land[place]
        copy.wait_send()
    gain_copy = pltpu.make_async_copy(gain_nat.at[5], small_out, local_sem.at[7])
    gain_copy.start()

    y_forget.wait_recv()
    full_f[...] = final_f[...] + yf_land[...]
    own_forget.start()
    own_first.wait()
    y_first.wait_recv()
    own_out_first.wait()
    yo_first.wait_recv()
    own_forget.wait()

    @pl.when(owner)
    def _():
        own_mid.wait()
        own_out_mid.wait()

    @pl.when(~owner)
    def _():
        y_mid.wait_recv()
        yo_mid.wait_recv()

    hand_over(3, out_out.at[:, pl.ds(row0, part)])
    hand_over(4, proj_out.at[pl.ds(row0, part), :])

    for copy in c2:
        copy.wait()
    for p in range(2):
        back_copy(1, p).wait()

    @pl.when(away)
    def _():
        for p in range(2):
            back_copy(0, p).wait()

    @pl.when(~away)
    def _():
        for p in range(2):
            back_own(0, p).wait()

    gain_copy.wait()
    for copy in rs + [c_copy, co_copy, x_copies[0], x_copies[1], x_copies[2], xf_copy, xo_copy]:
        copy.wait_send()
    for copy in [far_swap, col_swap, tot_swap, z_first, z_forget, zo_first]:
        copy.wait_send()
    for copy in y_pieces + [y_first, y_forget, yo_first]:
        copy.wait_send()

    @pl.when(owner)
    def _():
        y_mid.wait_send()
        yo_mid.wait_send()

    @pl.when(~owner)
    def _():
        z_mid.wait_send()
        zo_mid.wait_send()


def last_step(ring, heads, large, small):
    near = large[1]
    rows = near.shape[0]
    weight, normed, gated = large[6:9]
    tokens = large[10]
    units = large[13].shape[0]
    local, features = tokens.shape
    part = features // 4
    half = features // 2
    peers = len(ring.offsets)
    slot_w = 4 * LANES
    slots = heads // 2
    all_w = slots * slot_w
    any_spec = pl.BlockSpec(memory_space=pl.ANY)
    dma = pltpu.SemaphoreType.DMA
    vmem = pltpu.VMEM
    return pl.pallas_call(
        functools.partial(last_kernel, ring, heads),
        out_shape=(
            jax.ShapeDtypeStruct((2, local, half), BF),
            jax.ShapeDtypeStruct((half, all_w + LANES), BF),
            jax.ShapeDtypeStruct((half, 2 * units), BF),
            jax.ShapeDtypeStruct((half, 2 * units), BF),
            jax.ShapeDtypeStruct((2 * units, half), BF),
            jax.ShapeDtypeStruct((slots * LANES, half), BF),
            jax.ShapeDtypeStruct((4, 8, part), F32),
        ),
        in_specs=[any_spec] * len(large) + [pl.BlockSpec(memory_space=vmem)] * len(small),
        out_specs=[any_spec] * 7,
        scratch_shapes=[
            vmem((rows, all_w + LANES), BF),
            vmem(near.shape, F32),
            vmem(near.shape, BF),
            vmem(near.shape, BF),
            vmem((rows, LANES), F32),
            vmem((rows, LANES), F32),
            vmem((rows, LANES), F32),
            vmem((rows, LANES), F32),
            vmem((rows, LANES), F32),
            vmem((2 * (rows // CLEN), LANES), F32),
            vmem((2 * (rows // CLEN), LANES), F32),
            vmem(weight.shape, BF),
            vmem(normed.shape, BF),
            vmem(gated.shape, BF),
            vmem(normed.shape, BF),
            vmem(tokens.shape, BF),
            vmem(tokens.shape, F32),
            vmem((peers - 1, local, features), BF),
            vmem((peers - 1, local, features), BF),
            vmem((local, features), F32),
            vmem((half, all_w + LANES), BF),
            vmem((half, all_w + LANES), BF),
            vmem((slots, part, slot_w), F32),
            vmem((slots, part, slot_w), BF),
            vmem((slots, part, slot_w), BF),
            vmem((2, part, slot_w), BF),
            vmem((2, part, slot_w), BF),
            vmem((2, part, slot_w), BF),
            vmem((part, LANES), F32),
            vmem((part, LANES), BF),
            vmem((part, LANES), BF),
            vmem((part, LANES), BF),
            vmem((part, LANES), BF),
            vmem((part, LANES), BF),
            vmem((part, LANES), BF),
            vmem((part, LANES), BF),
            vmem((slots * LANES, half), BF),
            vmem((slots * LANES, half), BF),
            vmem((slots * LANES, part), F32),
            vmem((slots * LANES, part), BF),
            vmem((slots * LANES, part), BF),
            vmem((2, LANES, part), BF),
            vmem((2, LANES, part), BF),
            vmem((2, LANES, part), BF),
            vmem((4, local, part), BF),
            vmem((4, 8, part), F32),
            vmem((6, 4, 8, part), F32),
            vmem((5, 4, 8, part), F32),
            dma((11 + slots,)),
            dma((13,)),
            dma((3,)),
            dma((3,)),
            dma((8,)),
            dma((8,)),
            dma((5,)),
            dma((5,)),
            dma((peers - 1,)),
            dma((peers - 1,)),
            dma((2,)),
            dma((2,)),
            dma((5,)),
            dma((5,)),
            dma((5,)),
            dma((5,)),
            dma((2, 2)),
            dma((2, 2)),
            dma((5,)),
            dma((5,)),
        ],
        compiler_params=pltpu.CompilerParams(
            collective_id=1, has_side_effects=True, vmem_limit_bytes=63 << 20
        ),
        cost_estimate=pl.CostEstimate(
            flops=4 * rows * features * all_w, bytes_accessed=40 << 20, transcendentals=0
        ),
    )(*large, *small)


def middle_kernel(
    ring,
    gated_in,
    w_out_in,
    hid_own_in,
    hid_there_in,
    w_down_in,
    tokens_in,
    teach_prompt_in,
    teach_cont_in,
    valid_ref,
    gain_ref,
    gated_grad,
    residual_grad,
    mixed_grads,
    hid_kept,
    hid_there,
    down_kept,
    down_there,
    error_ref,
    gain_grad,
    gated,
    w_out,
    w_hidden,
    w_down,
    tokens,
    teacher,
    mixed,
    total,
    result_grad,
    normed,
    hidden,
    gate_up,
    result_all,
    mixed_all,
    rs_send,
    rs_land,
    c_down_send,
    c_down_land,
    c_hid_send,
    c_hid_land,
    x_down_send,
    x_hid_send,
    down_sum,
    hid_sum,
    gg_stage,
    load_sem,
    wx_send,
    wx_recv,
    wc_send,
    wc_recv,
    wz_send,
    wz_recv,
    group_send,
    group_recv,
    out_sem,
    rs_send_sem,
    rs_recv_sem,
    ag_send_sem,
    ag_recv_sem,
    c_send_sem,
    c_recv_sem,
    x_send_sem,
    x_recv_sem,
):
    here = Here(ring)
    local, features = tokens.shape
    rows_all = gated.shape[0]
    width = gated.shape[1]
    units = hidden.shape[1]
    half_units = units // 2
    part = features // 4
    peers = len(ring.offsets)
    order = list(range(peers - 1, 0, -1))
    y, c, x = (here.at[a] for a in ("y", "c", "x"))
    down_view = w_down_in.at[
        pl.ds(pl.multiple_of(y * half_units, half_units), half_units),
        pl.ds(pl.multiple_of(c * part, part), part),
    ]

    loads = [
        pltpu.make_async_copy(a, b, load_sem.at[i])
        for i, (a, b) in enumerate(
            (
                (hid_own_in, w_hidden.at[0:part, 0:units]),
                (hid_there_in, w_hidden.at[0:part, units:]),
                (gated_in, gated),
                (w_out_in, w_out),
                (tokens_in, tokens),
                (down_view, w_down.at[0:half_units, 0:part]),
            )
        )
    ]
    for copy in loads:
        copy.start()
    here.greet_group(
        [here.peer(k) for k in range(1, peers)]
        + [here.other("c"), here.other("x"), here.other("zh")]
    )

    z_down = remote(
        down_view, w_down.at[half_units:, 0:part], wz_send, wz_recv, here.other("zh")
    )
    z_down.start()

    def hid_x_copy(i):
        cols = slice(i * units, (i + 1) * units)
        return remote(
            w_hidden.at[0:part, cols],
            w_hidden.at[part : 2 * part, cols],
            wx_send.at[i],
            wx_recv.at[i],
            here.other("x"),
        )

    def hid_c_copy(i):
        cols = slice(i * units, (i + 1) * units)
        return remote(
            w_hidden.at[0 : 2 * part, cols],
            w_hidden.at[2 * part :, cols],
            wc_send.at[i],
            wc_recv.at[i],
            here.other("c"),
        )

    for i in range(2):
        loads[i].wait()
        hid_x_copy(i).start()

    def teach_copies(flip, rows_in, remote_copy):
        kind = x ^ flip
        out = []
        for p in range(2):
            block = (x ^ y) + 2 * (kind ^ p)
            dst = teacher.at[:, pl.ds(pl.multiple_of(block * part, part), part)]
            src = rows_in.at[:, p * part : (p + 1) * part]
            if remote_copy:
                out.append(
                    remote(
                        src, dst, group_send.at[flip, p], group_recv.at[flip, p], here.group_to(flip)
                    )
                )
            else:
                out.append(pltpu.make_async_copy(src, dst, load_sem.at[6 + p]))
        return out

    away = here.group_away()

    def on_teacher(flip, here_too, what):
        for kind, rows_in in ((0, teach_prompt_in), (1, teach_cont_in)):
            mine = (x ^ flip) == kind
            if flip == 1:

                @pl.when(mine)
                def _():
                    for copy in teach_copies(1, rows_in, True):
                        what(copy)

            else:

                @pl.when(mine & away)
                def _():
                    for copy in teach_copies(0, rows_in, True):
                        what(copy)

                if here_too:

                    @pl.when(mine & ~away)
                    def _():
                        for copy in teach_copies(0, rows_in, False):
                            what(copy)

    def teacher_arrival(flip):
        for p in range(2):
            remote(
                teach_prompt_in.at[:, p * part : (p + 1) * part],
                teacher.at[:, p * part : (p + 1) * part],
                group_send.at[flip, p],
                group_recv.at[flip, p],
                here.group_to(flip),
            ).wait_recv()

    def chunk(k):
        return slice(k * local, (k + 1) * local)

    def tiled(count, size, step):
        def body(i, carry):
            step(pl.ds(pl.multiple_of(i * size, size), size))
            return carry

        lax.fori_loop(0, count, body, 0)

    def rs_copy(phase, j):
        return remote(
            rs_send.at[j - 1],
            rs_land.at[j - 1],
            rs_send_sem.at[phase, j - 1],
            rs_recv_sem.at[phase, j - 1],
            here.peer(j),
        )

    def ag_copy(phase, buffer, k):
        return remote(
            buffer.at[chunk(0)],
            buffer.at[chunk(k)],
            ag_send_sem.at[phase, k - 1],
            ag_recv_sem.at[phase, k - 1],
            here.peer(k),
        )

    wide = 512
    wide_count = features // wide

    def send_partial(phase, k, left, right, transposed):
        def step(cols):
            if transposed:
                value = nt_dot(left, right[cols, :])
            else:
                value = nn_dot(left, right[:, cols])
            if k == 0:
                total[:, cols] = value
            else:
                rs_send[ring.back[k] - 1, :, cols] = value.astype(BF)

        if k != 0 and phase > 0:
            rs_copy(phase - 1, ring.back[k]).wait_send()
        tiled(wide_count, wide, step)
        if k != 0:
            rs_copy(phase, ring.back[k]).start()

    def row_tiles(step):
        tiled(local // 32, 32, step)

    def summed(rows):
        value = total[rows, :]
        for j in range(1, peers):
            value = value + rs_land[j - 1, rows, :].astype(F32)
        return value

    loads[2].wait()
    loads[3].wait()
    for k in order + [0]:
        send_partial(0, k, gated[chunk(k), :], w_out, False)
    loads[4].wait()
    loads[5].wait()
    z_down.wait_recv()
    down_x_copy = remote(
        w_down.at[:, 0:part],
        w_down.at[:, part : 2 * part],
        wx_send.at[2],
        wx_recv.at[2],
        here.other("x"),
    )
    down_x_copy.start()
    for j in range(1, peers):
        rs_copy(0, j).wait_recv()

    def second_norm(rows):
        value = tokens[rows, :].astype(F32) + summed(rows)
        mixed[rows, :] = value
        factor = lax.rsqrt(jnp.mean(value * value, axis=-1, keepdims=True) + epsilon)
        normed[rows, :] = (value * factor * gain_ref[...]).astype(BF)

    row_tiles(second_norm)
    for k in order:
        ag_copy(0, normed, k).start()

    for i in range(2):
        hid_x_copy(i).wait_recv()
        hid_c_copy(i).start()
    for f in range(2):
        on_teacher(f, True, lambda copy: copy.start())
    for i in range(2):
        hid_c_copy(i).wait_recv()
    down_x_copy.wait_recv()
    down_c_copy = remote(
        w_down.at[:, 0 : 2 * part],
        w_down.at[:, 2 * part :],
        wc_send.at[2],
        wc_recv.at[2],
        here.other("c"),
    )
    down_c_copy.start()
    tile_u = 256
    per_half = half_units // tile_u

    def forward_chunk(k):
        left = normed[chunk(k), :]

        def step(i, carry):
            half = i // per_half
            sub = lax.rem(i, per_half)
            gate_at = pl.multiple_of(half * units + sub * tile_u, tile_u)
            up_at = pl.multiple_of(half * units + half_units + sub * tile_u, tile_u)
            gate = nn_dot(left, w_hidden[:, pl.ds(gate_at, tile_u)])
            up = nn_dot(left, w_hidden[:, pl.ds(up_at, tile_u)])
            gate_up[chunk(k), pl.ds(gate_at, tile_u)] = gate.astype(BF)
            gate_up[chunk(k), pl.ds(up_at, tile_u)] = up.astype(BF)
            hidden[chunk(k), pl.ds(pl.multiple_of(i * tile_u, tile_u), tile_u)] = (
                gate * jax.nn.sigmoid(gate) * up
            ).astype(BF)
            return carry

        lax.fori_loop(0, 2 * per_half, step, 0)
        if k == 0:
            down_c_copy.wait_recv()
        send_partial(1, k, hidden[chunk(k), :], w_down, False)

    forward_chunk(0)
    for k in range(1, peers):
        ag_copy(0, normed, k).wait_recv()
        forward_chunk(k)
    teacher_arrival(1)

    @pl.when(away)
    def _():
        teacher_arrival(0)

    @pl.when(~away)
    def _():
        for kind, rows_in in ((0, teach_prompt_in), (1, teach_cont_in)):

            @pl.when(x == kind)
            def _():
                for copy in teach_copies(0, rows_in, False):
                    copy.wait()

    for j in range(1, peers):
        rs_copy(1, j).wait_recv()
    error_ref[...] = jnp.zeros(error_ref.shape, F32)
    gain_grad[...] = jnp.zeros(gain_grad.shape, F32)

    def loss_rows(rows):
        deviation = mixed[rows, :] + summed(rows) - teacher[rows, :].astype(F32)
        grad = valid_ref[rows, :] * deviation
        result_grad[rows, :] = grad
        result_all[rows, :] = grad.astype(BF)
        error_ref[0:1, :] += 0.5 * jnp.sum(grad * deviation, axis=0, keepdims=True)

    row_tiles(loss_rows)
    for k in order:
        ag_copy(1, result_all, k).start()

    def backward_chunk(k):
        left = result_all[chunk(k), :]

        def step(i, carry):
            half = i // per_half
            sub = lax.rem(i, per_half)
            gate_at = pl.multiple_of(half * units + sub * tile_u, tile_u)
            up_at = pl.multiple_of(half * units + half_units + sub * tile_u, tile_u)
            grad = nt_dot(left, w_down[pl.ds(pl.multiple_of(i * tile_u, tile_u), tile_u), :])
            gate = gate_up[chunk(k), pl.ds(gate_at, tile_u)].astype(F32)
            up = gate_up[chunk(k), pl.ds(up_at, tile_u)].astype(F32)
            sig = jax.nn.sigmoid(gate)
            gate_up[chunk(k), pl.ds(gate_at, tile_u)] = (
                grad * up * sig * (1.0 + gate * (1.0 - sig))
            ).astype(BF)
            gate_up[chunk(k), pl.ds(up_at, tile_u)] = (grad * gate * sig).astype(BF)
            return carry

        lax.fori_loop(0, 2 * per_half, step, 0)
        send_partial(2, k, gate_up[chunk(k), :], w_hidden, True)

    backward_chunk(0)
    for k in range(1, peers):
        ag_copy(1, result_all, k).wait_recv()
        backward_chunk(k)

    unit_tile = 256

    def down_tile(units_at, cols):
        return tn_dot(hidden[:, units_at], result_all[:, cols])

    def down_c(units_at):
        c_down_send[units_at, :] = down_tile(units_at, slice(2 * part, features)).astype(BF)

    tiled(units // unit_tile, unit_tile, down_c)
    c_down = remote(c_down_send, c_down_land, c_send_sem.at[0], c_recv_sem.at[0], here.other("c"))
    c_down.start()
    feature_tile = 128

    def hid_tile(first, at):
        cols = pl.ds(pl.multiple_of(first + at.start, feature_tile), feature_tile)
        return tn_dot(normed[:, cols], gate_up[...])

    def hid_c(at):
        c_hid_send[at, :] = hid_tile(2 * part, at).astype(BF)

    tiled(2 * part // feature_tile, feature_tile, hid_c)
    c_hid = remote(c_hid_send, c_hid_land, c_send_sem.at[1], c_recv_sem.at[1], here.other("c"))
    c_hid.start()
    c_down.wait_recv()

    def down_x(units_at):
        value = down_tile(units_at, slice(part, 2 * part))
        x_down_send[units_at, :] = (value + c_down_land[units_at, part:].astype(F32)).astype(BF)

    tiled(units // unit_tile, unit_tile, down_x)
    x_down = remote(x_down_send, down_there, x_send_sem.at[0], x_recv_sem.at[0], here.other("x"))
    x_down.start()

    for j in range(1, peers):
        rs_copy(2, j).wait_recv()

    def norm_back(rows):
        value = mixed[rows, :]
        factor = lax.rsqrt(jnp.mean(value * value, axis=-1, keepdims=True) + epsilon)
        scaled_rows = value * factor
        grad = summed(rows)
        e = grad * gain_ref[...]
        mean = jnp.mean(e * scaled_rows, axis=-1, keepdims=True)
        out = result_grad[rows, :] + factor * (e - scaled_rows * mean)
        result_grad[rows, :] = out
        mixed_all[rows, :] = out.astype(BF)
        gain_grad[0:1, :] += jnp.sum(grad * scaled_rows, axis=0, keepdims=True)

    row_tiles(norm_back)
    for k in order:
        ag_copy(2, mixed_all, k).start()
    residual_copy = pltpu.make_async_copy(result_grad, residual_grad, out_sem.at[0])
    residual_copy.start()

    c_hid.wait_recv()

    def hid_x(at):
        land = pl.ds(pl.multiple_of(part + at.start, feature_tile), feature_tile)
        x_hid_send[at, :] = (hid_tile(part, at) + c_hid_land[land, :].astype(F32)).astype(BF)

    tiled(part // feature_tile, feature_tile, hid_x)
    x_hid = remote(x_hid_send, hid_there, x_send_sem.at[1], x_recv_sem.at[1], here.other("x"))
    x_hid.start()

    def gated_chunk(k):
        gg_stage[chunk(k), :] = nt_dot(mixed_all[chunk(k), :], w_out[...])

    gated_chunk(0)

    def down_own(units_at):
        value = down_tile(units_at, slice(0, part))
        down_sum[units_at, :] = value + c_down_land[units_at, :part].astype(F32)

    tiled(units // unit_tile, unit_tile, down_own)

    def hid_own(at):
        hid_sum[at, :] = hid_tile(0, at) + c_hid_land[at, :].astype(F32)

    tiled(part // feature_tile, feature_tile, hid_own)
    sums_out = [
        pltpu.make_async_copy(down_sum, down_kept, out_sem.at[1]),
        pltpu.make_async_copy(hid_sum, hid_kept, out_sem.at[2]),
    ]
    for copy in sums_out:
        copy.start()
    for k in range(1, peers):
        ag_copy(2, mixed_all, k).wait_recv()
        gated_chunk(k)
    finals = [
        pltpu.make_async_copy(gg_stage, gated_grad, out_sem.at[3]),
        pltpu.make_async_copy(mixed_all, mixed_grads, out_sem.at[4]),
    ]
    for copy in finals:
        copy.start()
    for k in range(1, peers):
        rs_copy(2, k).wait_send()
        for phase, buffer in enumerate((normed, result_all, mixed_all)):
            ag_copy(phase, buffer, k).wait_send()
    c_down.wait_send()
    c_hid.wait_send()
    z_down.wait_send()
    for i in range(2):
        hid_x_copy(i).wait_send()
        hid_c_copy(i).wait_send()
        on_teacher(i, False, lambda copy: copy.wait_send())
    down_x_copy.wait_send()
    down_c_copy.wait_send()
    x_down.wait()
    x_hid.wait()
    residual_copy.wait()
    for copy in sums_out + finals:
        copy.wait()


def middle_step(
    ring,
    gated,
    w_out,
    hid_own,
    hid_there,
    w_down,
    tokens,
    teach_prompt,
    teach_cont,
    valid,
    gain,
):
    rows, width = gated.shape
    local, features = tokens.shape
    units = w_down.shape[0]
    part = features // 4
    peers = len(ring.offsets)
    any_spec = pl.BlockSpec(memory_space=pl.ANY)
    vmem_spec = pl.BlockSpec(memory_space=pltpu.VMEM)
    dma = pltpu.SemaphoreType.DMA
    return pl.pallas_call(
        functools.partial(middle_kernel, ring),
        out_shape=(
            jax.ShapeDtypeStruct((rows, width), F32),
            jax.ShapeDtypeStruct((local, features), F32),
            jax.ShapeDtypeStruct((rows, features), BF),
            jax.ShapeDtypeStruct((part, 2 * units), F32),
            jax.ShapeDtypeStruct((part, 2 * units), BF),
            jax.ShapeDtypeStruct((units, part), F32),
            jax.ShapeDtypeStruct((units, part), BF),
            jax.ShapeDtypeStruct((8, features), F32),
            jax.ShapeDtypeStruct((8, features), F32),
        ),
        in_specs=[any_spec] * 8 + [vmem_spec] * 2,
        out_specs=[any_spec] * 7 + [vmem_spec] * 2,
        scratch_shapes=[
            pltpu.VMEM(gated.shape, BF),
            pltpu.VMEM(w_out.shape, BF),
            pltpu.VMEM((features, 2 * units), BF),
            pltpu.VMEM((units, features), BF),
            pltpu.VMEM(tokens.shape, BF),
            pltpu.VMEM(tokens.shape, BF),
            pltpu.VMEM(tokens.shape, F32),
            pltpu.VMEM(tokens.shape, F32),
            pltpu.VMEM(tokens.shape, F32),
            pltpu.VMEM((rows, features), BF),
            pltpu.VMEM((rows, units), BF),
            pltpu.VMEM((rows, 2 * units), BF),
            pltpu.VMEM((rows, features), BF),
            pltpu.VMEM((rows, features), BF),
            pltpu.VMEM((peers - 1, local, features), BF),
            pltpu.VMEM((peers - 1, local, features), BF),
            pltpu.VMEM((units, 2 * part), BF),
            pltpu.VMEM((units, 2 * part), BF),
            pltpu.VMEM((2 * part, 2 * units), BF),
            pltpu.VMEM((2 * part, 2 * units), BF),
            pltpu.VMEM((units, part), BF),
            pltpu.VMEM((part, 2 * units), BF),
            pltpu.VMEM((units, part), F32),
            pltpu.VMEM((part, 2 * units), F32),
            pltpu.VMEM((rows, width), F32),
            dma((8,)),
            dma((3,)),
            dma((3,)),
            dma((3,)),
            dma((3,)),
            dma,
            dma,
            dma((2, 2)),
            dma((2, 2)),
            dma((5,)),
            dma((3, peers - 1)),
            dma((3, peers - 1)),
            dma((3, peers - 1)),
            dma((3, peers - 1)),
            dma((2,)),
            dma((2,)),
            dma((2,)),
            dma((2,)),
        ],
        compiler_params=pltpu.CompilerParams(
            collective_id=2, has_side_effects=True, vmem_limit_bytes=63 << 20
        ),
        cost_estimate=pl.CostEstimate(
            flops=6 * rows * features * (3 * units + width),
            bytes_accessed=60 << 20,
            transcendentals=0,
        ),
    )(
        gated,
        w_out,
        hid_own,
        hid_there,
        w_down,
        tokens,
        teach_prompt,
        teach_cont,
        valid,
        gain,
    )


def first_kernel(
    ring,
    prompt_in,
    cont_in,
    small_in,
    ints_in,
    wq_in,
    wg_in,
    wk_in,
    wv_in,
    w_out_in,
    tokens_out,
    normed_out,
    slots_out,
    w_out_all,
    small_out,
    gains_out,
    forget_w_out,
    ints_out,
    proj_a,
    proj_b,
    proj_c,
    forget_own,
    there_a,
    there_b,
    there_c,
    forget_there,
    tokens,
    normed,
    slot_w,
    project,
    forget,
    small,
    small_x,
    feats,
    forget_f,
    forget_w,
    group_send,
    group_recv,
    ints_send,
    ints_recv,
    small_send,
    small_recv,
    own_sem,
    z_send,
    z_recv,
    x_send,
    x_recv,
    c_send,
    c_recv,
    ag_send,
    ag_recv,
    kv_send,
    kv_recv,
    out_sem,
):
    here = Here(ring)
    y, c, x, zh = (here.at[a] for a in ("y", "c", "x", "zh"))
    local, features = tokens.shape
    part = features // 4
    half = features // 2
    peers = len(ring.offsets)
    owner = zh == y
    row0 = pl.multiple_of(c * part, part)
    first0 = pl.multiple_of(2 * LANES * y, LANES)
    sources = (wq_in, wg_in, wk_in, wv_in)

    here.greet_group([here.peer(k) for k in range(1, peers)] + [here.other(a) for a in "cx"] + [here.other("zh")])

    def group_copies(flip, rows_in, remote_copy):
        kind = x ^ flip
        out = []
        for p in range(2):
            block = (x ^ y) + 2 * (kind ^ p)
            dst = tokens.at[:, pl.ds(pl.multiple_of(block * part, part), part)]
            src = rows_in.at[:, p * part : (p + 1) * part]
            if remote_copy:
                out.append(
                    remote(
                        src, dst, group_send.at[flip, p], group_recv.at[flip, p], here.group_to(flip)
                    )
                )
            else:
                out.append(pltpu.make_async_copy(src, dst, own_sem.at[12 + p]))
        return out

    def ints_copy():
        return remote(ints_in, ints_out, ints_send, ints_recv, here.group_to(0))

    def ints_own():
        return pltpu.make_async_copy(ints_in, ints_out, own_sem.at[14])

    away = here.group_away()

    def on_group(flip, what):
        for kind, rows_in in ((0, prompt_in), (1, cont_in)):
            mine = (x ^ flip) == kind
            if flip == 1:

                @pl.when(mine)
                def _():
                    for copy in group_copies(flip, rows_in, True):
                        what(copy)

            else:

                @pl.when(mine & away)
                def _():
                    for copy in group_copies(flip, rows_in, True):
                        what(copy)

                @pl.when(mine & ~away)
                def _():
                    for copy in group_copies(flip, rows_in, False):
                        what(copy)

    for f in range(2):
        on_group(f, lambda copy: copy.start())

    @pl.when(away)
    def _():
        ints_copy().start()

    @pl.when(~away)
    def _():
        ints_own().start()

    own_small = pltpu.make_async_copy(small_in, small.at[0], own_sem.at[15])
    own_small.start()
    small_z = remote(small_in, small.at[1], small_send.at[0], small_recv.at[0], here.other("zh"))
    small_z.start()

    def own_piece(i, s):
        start = first0 if s == 0 else LANES
        return pltpu.make_async_copy(
            sources[i].at[pl.ds(row0, part), pl.ds(start, LANES)],
            slot_w.at[s, 0:part, i * LANES : (i + 1) * LANES],
            own_sem.at[4 * s + i],
        )

    for i in range(4):
        own_piece(i, 0).start()

    @pl.when(owner)
    def _():
        for i in range(4):
            own_piece(i, 1).start()

    own_out = [
        pltpu.make_async_copy(
            w_out_in.at[pl.ds(first0, LANES), pl.ds(row0, part)],
            w_out_all.at[0:LANES, 0:part],
            own_sem.at[8],
        ),
        pltpu.make_async_copy(
            w_out_in.at[LANES : 2 * LANES, pl.ds(row0, part)],
            w_out_all.at[LANES : 2 * LANES, 0:part],
            own_sem.at[9],
        ),
    ]
    own_out[0].start()

    @pl.when(owner)
    def _():
        own_out[1].start()

    own_small.wait()
    small_z.wait_recv()
    small_over_x = remote(small, small_x, small_send.at[1], small_recv.at[1], here.other("x"))
    small_over_x.start()

    def x_copy(s):
        return remote(
            slot_w.at[s, 0:part],
            slot_w.at[s, part : 2 * part],
            x_send.at[s],
            x_recv.at[s],
            here.other("x"),
        )

    def c_copy(s):
        return remote(
            slot_w.at[s, 0:half],
            slot_w.at[s, half:features],
            c_send.at[s],
            c_recv.at[s],
            here.other("c"),
        )

    for i in range(4):
        own_piece(i, 0).wait()
    x_copy(0).start()
    small_over_x.wait_recv()
    for z in range(2):
        for place in range(2):
            at = pl.multiple_of((c ^ place) * part, part)
            feats[z, :, 2 * place * part : (2 * place + 1) * part] = small[z, :, pl.ds(at, part)]
            feats[z, :, (2 * place + 1) * part : (2 * place + 2) * part] = small_x[
                z, :, pl.ds(at, part)
            ]
    forget_f[...] = jnp.zeros(forget_f.shape, F32)
    for z, rows in ((0, slice(0, 2)), (1, slice(4, 6))):
        forget_f[rows, :] = jnp.where(y == 0, feats[z, 8:10, :], feats[z, 12:14, :])
    forget_f[2:4, :] = jnp.where(owner, feats[0, 10:12, :], feats[1, 10:12, :])
    forget_w[...] = jnp.zeros(forget_w.shape, BF)
    forget_w[0:16, :] = forget_f[...].astype(BF)

    for f in range(2):
        for p in range(2):
            pass

    def arrived(copy):
        if hasattr(copy, "wait_recv"):
            copy.wait_recv()

    def group_arrival(flip):
        for p in range(2):
            remote(
                prompt_in.at[:, p * part : (p + 1) * part],
                tokens.at[:, p * part : (p + 1) * part],
                group_send.at[flip, p],
                group_recv.at[flip, p],
                here.group_to(flip),
            ).wait_recv()

    group_arrival(1)

    @pl.when(away)
    def _():
        group_arrival(0)

    @pl.when(~away)
    def _():
        for kind, rows_in in ((0, prompt_in), (1, cont_in)):

            @pl.when(x == kind)
            def _():
                for copy in group_copies(0, rows_in, False):
                    copy.wait()

    def z_piece(i, s):
        start = first0 if s == 2 else LANES
        return remote(
            sources[i].at[pl.ds(row0, part), pl.ds(start, LANES)],
            slot_w.at[s, 0:part, i * LANES : (i + 1) * LANES],
            z_send.at[s, i],
            z_recv.at[s, i],
            here.other("zh"),
        )

    for i in range(4):
        z_piece(i, 2).start()

    @pl.when(owner)
    def _():
        for i in range(4):
            z_piece(i, 1).start()

    z_out = [
        remote(
            w_out_in.at[pl.ds(first0, LANES), pl.ds(row0, part)],
            w_out_all.at[2 * LANES : 3 * LANES, 0:part],
            z_send.at[0, 0],
            z_recv.at[0, 0],
            here.other("zh"),
        ),
        remote(
            w_out_in.at[LANES : 2 * LANES, pl.ds(row0, part)],
            w_out_all.at[LANES : 2 * LANES, 0:part],
            z_send.at[0, 1],
            z_recv.at[0, 1],
            here.other("zh"),
        ),
    ]
    z_out[0].start()

    @pl.when(owner)
    def _():
        z_out[1].start()

    def norm_rows(i, carry):
        rows = pl.ds(pl.multiple_of(i * 32, 32), 32)
        value = tokens[rows, :].astype(F32)
        factor = lax.rsqrt(jnp.mean(value * value, axis=-1, keepdims=True) + epsilon)
        normed[rows, :] = (value * factor * feats[0, 0:1, :]).astype(BF)
        return carry

    lax.fori_loop(0, local // 32, norm_rows, 0)

    def ag_copy(k):
        return remote(
            normed.at[0:local],
            normed.at[k * local : (k + 1) * local],
            ag_send.at[k - 1],
            ag_recv.at[k - 1],
            here.peer(k),
        )

    for k in range(peers - 1, 0, -1):
        ag_copy(k).start()

    outs = [
        pltpu.make_async_copy(tokens, tokens_out, out_sem.at[0]),
        pltpu.make_async_copy(small, small_out, out_sem.at[1]),
        pltpu.make_async_copy(feats.at[0], gains_out, out_sem.at[2]),
        pltpu.make_async_copy(forget_w, forget_w_out, out_sem.at[3]),
    ]
    for copy in outs:
        copy.start()

    x_copy(0).wait_recv()
    c_copy(0).start()
    for i in range(4):
        z_piece(i, 2).wait_recv()
    x_copy(2).start()

    @pl.when(owner)
    def _():
        for i in range(4):
            own_piece(i, 1).wait()

    @pl.when(~owner)
    def _():
        for i in range(4):
            z_piece(i, 1).wait_recv()

    x_copy(1).start()

    projects = (proj_a, proj_b, proj_c)
    theres = (there_a, there_b, there_c)

    def chunk(k):
        return slice(k * local, (k + 1) * local)

    def kv_copy(k, s):
        return remote(
            project.at[s, chunk(k), 2 * LANES :],
            theres[s].at[chunk(k)],
            kv_send.at[k, s],
            kv_recv.at[k, s],
            here.other("c"),
        )

    def forget_copy(k):
        return remote(
            forget.at[chunk(k)],
            forget_there.at[chunk(k)],
            kv_send.at[k, 3],
            kv_recv.at[k, 3],
            here.other("c"),
        )

    def project_chunk(k, s):
        project[s, chunk(k), :] = nn_dot(normed[chunk(k), :], slot_w[s]).astype(BF)
        kv_copy(k, s).start()

    def forget_chunk(k):
        forget[chunk(k), :] = nt_dot(normed[chunk(k), :], forget_w[...]).astype(BF)
        forget_copy(k).start()

    c_copy(0).wait_recv()
    forget_chunk(0)
    project_chunk(0, 0)
    for k in range(1, peers):
        ag_copy(k).wait_recv()
        forget_chunk(k)
        project_chunk(k, 0)
    normed_copy = pltpu.make_async_copy(normed, normed_out, out_sem.at[4])
    normed_copy.start()
    for s in (2, 1):
        x_copy(s).wait_recv()
        c_copy(s).start()
    own_out[0].wait()
    z_out[0].wait_recv()

    @pl.when(owner)
    def _():
        own_out[1].wait()

    @pl.when(~owner)
    def _():
        z_out[1].wait_recv()

    x_out = remote(
        w_out_all.at[:, 0:part],
        w_out_all.at[:, part : 2 * part],
        x_send.at[3],
        x_recv.at[3],
        here.other("x"),
    )
    x_out.start()
    for s in (2, 1):
        c_copy(s).wait_recv()
        for k in range(peers):
            project_chunk(k, s)
    slots_copy = pltpu.make_async_copy(slot_w, slots_out, out_sem.at[5])
    slots_copy.start()
    finals = [
        pltpu.make_async_copy(project.at[s], projects[s], out_sem.at[6 + s]) for s in range(3)
    ] + [pltpu.make_async_copy(forget, forget_own, out_sem.at[9])]
    for copy in finals:
        copy.start()
    x_out.wait_recv()
    c_out = remote(
        w_out_all.at[:, 0:half],
        w_out_all.at[:, half:features],
        c_send.at[3],
        c_recv.at[3],
        here.other("c"),
    )
    c_out.start()

    on_group(1, lambda copy: copy.wait_send())

    @pl.when(away)
    def _():
        ints_copy().wait()
        for kind, rows_in in ((0, prompt_in), (1, cont_in)):

            @pl.when(x == kind)
            def _():
                for copy in group_copies(0, rows_in, True):
                    copy.wait_send()

    @pl.when(~away)
    def _():
        ints_own().wait()

    small_z.wait_send()
    small_over_x.wait_send()
    for i in range(4):
        z_piece(i, 2).wait_send()
    z_out[0].wait_send()

    @pl.when(owner)
    def _():
        for i in range(4):
            z_piece(i, 1).wait_send()
        z_out[1].wait_send()

    for s in range(3):
        x_copy(s).wait_send()
        c_copy(s).wait_send()
    x_out.wait_send()
    for k in range(1, peers):
        ag_copy(k).wait_send()
    for k in range(peers):
        for s in range(3):
            kv_copy(k, s).wait()
        forget_copy(k).wait()
    c_out.wait()
    for copy in outs + finals + [normed_copy, slots_copy]:
        copy.wait()


def first_step(ring, prompt, cont, small, ints, wq, wg, wk, wv, w_out):
    local, half = prompt.shape
    features = 2 * half
    part = half // 2
    peers = len(ring.offsets)
    rows = peers * local
    slot = 4 * LANES
    any_spec = pl.BlockSpec(memory_space=pl.ANY)
    dma = pltpu.SemaphoreType.DMA
    shapes = [
        ((local, features), BF),
        ((rows, features), BF),
        ((3, features, slot), BF),
        ((3 * LANES, features), BF),
        ((2, 16, half), F32),
        ((16, features), F32),
        ((LANES, features), BF),
        (ints.shape, jnp.int32),
        ((rows, slot), BF),
        ((rows, slot), BF),
        ((rows, slot), BF),
        ((rows, LANES), BF),
        ((rows, 2 * LANES), BF),
        ((rows, 2 * LANES), BF),
        ((rows, 2 * LANES), BF),
        ((rows, LANES), BF),
    ]
    return pl.pallas_call(
        functools.partial(first_kernel, ring),
        out_shape=tuple(jax.ShapeDtypeStruct(*s) for s in shapes),
        in_specs=[any_spec] * 9,
        out_specs=[any_spec] * len(shapes),
        scratch_shapes=[
            pltpu.VMEM((local, features), BF),
            pltpu.VMEM((rows, features), BF),
            pltpu.VMEM((3, features, slot), BF),
            pltpu.VMEM((3, rows, slot), BF),
            pltpu.VMEM((rows, LANES), BF),
            pltpu.VMEM((2, 16, half), F32),
            pltpu.VMEM((2, 16, half), F32),
            pltpu.VMEM((2, 16, features), F32),
            pltpu.VMEM((16, features), F32),
            pltpu.VMEM((LANES, features), BF),
            dma((2, 2)),
            dma((2, 2)),
            dma,
            dma,
            dma((2,)),
            dma((2,)),
            dma((16,)),
            dma((3, 4)),
            dma((3, 4)),
            dma((4,)),
            dma((4,)),
            dma((4,)),
            dma((4,)),
            dma((peers - 1,)),
            dma((peers - 1,)),
            dma((peers, 4)),
            dma((peers, 4)),
            dma((10,)),
        ],
        compiler_params=pltpu.CompilerParams(
            collective_id=3, has_side_effects=True, vmem_limit_bytes=48 << 20
        ),
        cost_estimate=pl.CostEstimate(
            flops=2 * rows * features * 3 * slot, bytes_accessed=40 << 20, transcendentals=0
        ),
    )(prompt, cont, small, ints, wq, wg, wk, wv, w_out)


def ring_body(
    ring,
    x_prompt,
    x_cont,
    teacher_prompt,
    teacher_cont,
    segment_ids,
    offsets,
    prompt_valid,
    cont_valid,
    first_gain,
    w_query,
    w_key,
    w_value,
    w_outgate,
    w_forget,
    forget_bias,
    w_out,
    second_gain,
    w_gate,
    w_up,
    w_down,
):
    y = lax.axis_index("y")
    c = lax.axis_index("c")
    x = lax.axis_index("x")
    zh = lax.axis_index("zh")
    zl = lax.axis_index("zl")
    zl_count = ring.zl_count
    local = x_prompt.shape[1]
    half_d = x_prompt.shape[2]
    part_d = half_d // 2
    local_conts = x_cont.shape[1]
    heads = w_forget.shape[1]
    units_here = w_gate.shape[1]
    half_units = units_here // 2
    width = heads * HEAD_DIM
    slots = heads // 2
    pair_unit = PROMPT // CLEN
    chunk_units = local // CLEN
    own_valid = jnp.where(x == 0, prompt_valid.reshape(-1), cont_valid.reshape(-1))
    small_in = jnp.concatenate([own_valid, segment_ids.reshape(-1), offsets.reshape(-1)])
    int_rows = 16
    ints = jnp.pad(small_in, (0, int_rows * LANES - small_in.shape[0])).reshape(int_rows, LANES)
    packed = jnp.concatenate(
        [
            first_gain[None].astype(F32),
            second_gain[None].astype(F32),
            jnp.pad(forget_bias, (0, half_d - heads))[None],
            jnp.zeros((5, half_d), F32),
            w_forget.T.astype(F32),
            jnp.zeros((8 - heads, half_d), F32),
        ],
        axis=0,
    )
    (
        tokens_b,
        normed_all,
        w_slots,
        w_out_all,
        small_all,
        gains,
        w_forget_rows,
        ints,
        proj_a,
        proj_b,
        proj_c,
        forget_own,
        there_a,
        there_b,
        there_c,
        forget_there,
    ) = first_step(
        ring,
        x_prompt[0],
        x_cont.reshape(local_conts * CLEN, half_d),
        packed,
        ints,
        w_query,
        w_outgate,
        w_key,
        w_value,
        w_out,
    )
    projects = [proj_a, proj_b, proj_c]
    kv_there = [there_a, there_b, there_c]
    ints = ints.reshape(-1)
    validity = ints[:local].astype(F32)
    segment_row = ints[local : local + PROMPT]
    offset_row = ints[local + PROMPT : local + PROMPT + CONTS]
    gain_one = gains[0]
    gain_two = gains[1]

    def head_slots(value):
        first = jnp.where(y == 0, value[:, 0:2], value[:, 4:6])
        slot_a = jnp.where(zh == 0, first[0], first[1])
        slot_c = jnp.where(zh == 0, first[1], first[0])
        slot_b = jnp.where(y == 0, value[0, 2:4], value[1, 2:4])
        return jnp.concatenate([slot_a, slot_b, slot_c], axis=0)

    bias_all = small_all[:, 2, :heads]
    bias_all = jnp.stack(
        [
            jnp.where(zh == 0, bias_all[0], bias_all[1]),
            jnp.where(zh == 0, bias_all[1], bias_all[0]),
        ]
    )
    bias_row = head_slots(bias_all[:, :, None])[:, 0]
    bias_row = jnp.concatenate([bias_row, jnp.zeros((LANES - heads,), F32)])[None]

    proj_a, w_gate, w_up = lax.optimization_barrier((proj_a, w_gate, w_up))
    projects[0] = proj_a
    hid_own = jnp.concatenate(
        [
            lax.dynamic_slice(w, (c * part_d, y * half_units), (part_d, half_units))
            for w in (w_gate, w_up)
        ],
        axis=1,
    )
    hid_there_w = ring.swap(hid_own, "zh")

    dy_all = jnp.array([o[0] for o in ring.offsets], jnp.int32)
    dz_all = jnp.array([o[1] for o in ring.offsets], jnp.int32)
    places = ((y - dy_all) % 2) * zl_count + (zl - dz_all) % zl_count
    unit_no = (places[:, None] * chunk_units + jnp.arange(chunk_units, dtype=jnp.int32)).reshape(-1)
    natural = jnp.arange(pair_unit, dtype=jnp.int32)
    pick = unit_no[:, None] == natural[None, :]
    step = jnp.arange(CLEN, dtype=jnp.int32)
    row_pos = (unit_no[:, None] * CLEN + step[None, :]).reshape(-1)
    seg_rel = jnp.sum(
        jnp.where(pick[:, :, None], segment_row.reshape(1, pair_unit, CLEN), 0), axis=1
    )
    offs_rel = jnp.sum(jnp.where(pick, offset_row[None, :], 0), axis=1)
    last_rel = jnp.sum(
        jnp.where(
            jnp.arange(PROMPT, dtype=jnp.int32)[None, :] == offs_rel[:, None] - 1,
            segment_row[None, :],
            0,
        ),
        axis=1,
    )
    limit = jnp.where(c == 0, unit_no * CLEN, offs_rel)
    doc_row = jnp.where(c == 0, seg_rel, last_rel[:, None]).reshape(-1, 1)
    seg_col = seg_rel.reshape(-1, 1)
    lane = jnp.arange(LANES, dtype=jnp.int32)[None, :]
    unit_col = jnp.repeat(natural, CLEN)[:, None]
    pieces = 3 * heads
    is_doc = (lane >= DOC_LANE) & (lane < DOC_LANE + 4)
    is_unit = (lane >= UNIT_LANE) & (lane < UNIT_LANE + pair_unit)
    limit_lane = jnp.pad(limit, (UNIT_LANE, LANES - UNIT_LANE - pair_unit))[None, :]
    q_base = jnp.where(
        (lane >= FAR_PIECE) & (lane < FAR_PIECE + pieces),
        1.0,
        jnp.where(
            (is_doc & (doc_row != lane - DOC_LANE)) | (is_unit & (unit_col == lane - UNIT_LANE)),
            -NEVER,
            0.0,
        ),
    ).astype(BF)
    near_base = jnp.where(
        (lane < pieces) | (is_doc & (doc_row == lane - DOC_LANE)), 1.0, 0.0
    ).astype(BF)
    far_base = jnp.where(
        (lane < pieces)
        | (is_doc & (seg_col == lane - DOC_LANE))
        | (is_unit & (row_pos[:, None] >= limit_lane)),
        1.0,
        0.0,
    ).astype(BF)
    tri = (step[:, None] >= step[None, :]).astype(F32)
    earlier = (unit_no[None, :] < unit_no[:, None]).astype(F32)
    hot = (row_pos[None, :] == limit[:, None] - 1).astype(F32)
    cont_hot = (row_pos[None, :] == offs_rel[:, None] - 1).astype(F32)

    forget_far = jnp.where(c == 0, forget_own, forget_there)
    flag = c.astype(jnp.int32).reshape(1)
    head_lane = lane < heads

    def keep_log(lin):
        return jnp.where(head_lane, jax.nn.log_sigmoid(lin.astype(F32) + bias_row), 0.0)

    def within(values, matrix):
        return jnp.einsum(
            "ts,ush->uth", matrix, values.reshape(pair_unit, CLEN, LANES), precision=highest
        )

    far_within = within(keep_log(forget_far), tri)
    far_prefix = jnp.dot(earlier, far_within[:, -1], precision=highest)
    cum_far = (far_within + far_prefix[:, None]).reshape(-1, LANES)
    own_base = jnp.dot(hot, cum_far, precision=highest)
    cum_near = (within(keep_log(forget_own), tri) + own_base[:, None]).reshape(-1, LANES)
    keep_slope = jnp.where(
        head_lane, jax.nn.sigmoid(-(forget_own.astype(F32) + bias_row)), 0.0
    )
    gated, attended, logs = attend(
        flag, projects, kv_there, cum_near, cum_far, q_base, near_base, far_base, local, heads
    )
    (
        grad_gated,
        grad_residual,
        grad_residual_all,
        hid_kept,
        hid_there,
        down_kept,
        down_there,
        error_rows,
        gain_two_rows,
    ) = middle_step(
        ring,
        gated,
        w_out_all,
        hid_own,
        hid_there_w,
        w_down,
        tokens_b,
        teacher_prompt[0],
        teacher_cont.reshape(local_conts * CLEN, half_d),
        validity[:, None],
        gain_two[None],
    )
    dqg, dkv_near, dkv_far, row_sum, near_sum, far_sum = attend_back(
        flag,
        projects,
        kv_there,
        cum_near,
        cum_far,
        q_base,
        near_base,
        far_base,
        grad_gated,
        attended,
        logs,
        local,
        heads,
    )

    def low(value):
        return lax.reduce_precision(value, 8, 7).astype(BF)

    def over_zh(value, dim):
        size = value.shape[dim] // 2
        mine = lax.slice_in_dim(value, 0, size, axis=dim)
        theirs = lax.slice_in_dim(value, size, 2 * size, axis=dim)
        return low(mine + ring.swap(theirs.astype(BF), "zh").astype(F32))

    hid_mine = over_zh(hid_kept + hid_there.astype(F32), 1)
    down_mine = over_zh(down_kept + down_there.astype(F32), 0)
    rows_back, proj_all, gate_all, up_all, down_all, out_all, small_sums = last_step(
        ring,
        heads,
        [
            dqg,
            dkv_near,
            dkv_far,
            row_sum,
            near_sum,
            far_sum,
            w_slots,
            normed_all,
            gated,
            grad_residual_all,
            tokens_b,
            grad_residual,
            hid_mine,
            down_mine,
        ],
        [
            gain_one[None],
            w_forget_rows,
            keep_slope,
            cont_hot.T,
            error_rows,
            gain_two_rows,
            validity[:, None],
        ],
    )
    gain_one_sum = small_sums[:, 0].reshape(-1)
    gain_two_sum = small_sums[:, 1].reshape(-1)
    sums = small_sums[0, 2]
    projection_grads = [
        jnp.concatenate(
            [proj_all[:, (4 * s + i) * LANES : (4 * s + i + 1) * LANES] for s in range(slots)],
            axis=1,
        )
        for i in range(4)
    ]
    forget_grad = proj_all[:, 4 * width : 4 * width + heads]
    error_total = sums[0]
    count_total = sums[1]
    groups = ring.sizes["yo"] * ring.sizes["y"] * ring.sizes["c"]
    grad_scale = groups * (PROMPT + CONTS * CLEN) / count_total
    loss_value = error_total / (D * count_total)

    def own_half(value):
        return lax.dynamic_slice_in_dim(value, x * half_d, half_d, value.ndim - 1)

    quarter_no = zh * zl_count + zl
    bias_out = lax.dynamic_slice_in_dim(sums, 2 + quarter_no * heads, heads, 0)

    def scaled(value):
        return value.astype(F32) * grad_scale

    return (
        loss_value,
        scaled(rows_back[0])[None],
        scaled(rows_back[1]).reshape(1, local_conts, CLEN, half_d),
        scaled(own_half(gain_one_sum)),
        scaled(projection_grads[0]),
        scaled(projection_grads[2]),
        scaled(projection_grads[3]),
        scaled(projection_grads[1]),
        scaled(forget_grad),
        scaled(bias_out),
        scaled(out_all),
        scaled(own_half(gain_two_sum)),
        scaled(gate_all),
        scaled(up_all),
        scaled(down_all),
    )


def specs(dp, row, col):
    in_specs = (
        P(dp, col, row),
        P(dp, col, None, row),
        P(dp, col, row),
        P(dp, col, None, row),
        P(dp, None),
        P(dp, None),
        P(dp, col),
        P(dp, col, None),
        P(row),
        P(row, col),
        P(row, col),
        P(row, col),
        P(row, col),
        P(row, col),
        P(col),
        P(col, row),
        P(row),
        P(row, col),
        P(row, col),
        P(col, row),
    )
    out_specs = (
        P(),
        P(dp, col, row),
        P(dp, col, None, row),
        P(row),
        P(row, col),
        P(row, col),
        P(row, col),
        P(row, col),
        P(row, col),
        P(col),
        P(col, row),
        P(row),
        P(row, col),
        P(row, col),
        P(col, row),
    )
    return in_specs, out_specs


def solution(mesh):
    dp, row, col = mesh.shape["dp"], mesh.shape["row"], mesh.shape["col"]
    heads = HEADS // col
    if dp == 4 and row == 2 and col % 2 == 0 and heads == 6:
        sizes = {"yo": dp // 4, "y": 2, "c": 2, "x": 2, "zh": 2, "zl": col // 2}
        ring_mesh = Mesh(mesh.devices.reshape([sizes[a] for a in AX]), AX)
        in_specs, out_specs = specs(("yo", "y", "c"), "x", ("zh", "zl"))
        step = functools.partial(ring_body, Ring(sizes))
        return jax.shard_map(
            step, mesh=ring_mesh, in_specs=in_specs, out_specs=out_specs, check_vma=False
        )
    in_specs, out_specs = specs("dp", "row", "col")
    return jax.shard_map(
        wide_body, mesh=mesh, in_specs=in_specs, out_specs=out_specs, check_vma=False
    )
```

```python
import functools
import itertools

import jax
import jax.numpy as jnp
from jax import lax
from jax.experimental import pallas as pl
from jax.experimental.pallas import tpu as pltpu
from jax.sharding import Mesh, PartitionSpec as P

D = 1536
HEADS = 24
HEAD_DIM = 64
PROMPT = 1024
CONTS = 8
CLEN = 128


epsilon = 1e-06
highest = lax.Precision.HIGHEST
masked = -1e30


def matmul(left_op, right_op):
    return jnp.dot(left_op, right_op, preferred_element_type=jnp.float32)


def by_transpose(left_op, right_op):
    return lax.dot_general(
        left_op, right_op, (((1,), (1,)), ((), ())), preferred_element_type=jnp.float32
    )


def inner_rows(left_op, right_op):
    return lax.dot_general(
        left_op, right_op, (((0,), (0,)), ((), ())), preferred_element_type=jnp.float32
    )


def feature_total(partial_sum):
    return lax.psum(partial_sum, "row")


def group_rows(local_rows):
    return lax.all_gather(local_rows, "col", axis=0, tiled=True)


def token_sums(partial_rows):
    return lax.psum_scatter(
        partial_rows.astype(jnp.bfloat16), "col", scatter_dimension=0, tiled=True
    ).astype(jnp.float32)


def row_partials(partial_rows, col_count, blocks, quarter):
    shaped = partial_rows.reshape(
        col_count, blocks, lax.axis_size("row"), quarter, partial_rows.shape[-1]
    )
    return lax.psum_scatter(
        shaped.astype(jnp.bfloat16), "row", scatter_dimension=2, tiled=True
    ).astype(jnp.float32)


def head_rows(own_rows):
    gathered = lax.all_gather(own_rows, "row", axis=2, tiled=True)
    return gathered.reshape(-1, gathered.shape[-1])


def norm_forward(tokens, gain_vec):
    row_total = feature_total(jnp.sum(tokens * tokens, axis=-1))
    factor = lax.rsqrt(row_total / D + epsilon)
    scaled = tokens * factor[:, None]
    return (factor, scaled, (scaled * gain_vec).astype(jnp.bfloat16))


def norm_backward(grad_normed, factor, scaled, gain_vec):
    grad_scaled = grad_normed * gain_vec
    row_total = feature_total(jnp.sum(grad_scaled * scaled, axis=-1))
    gain_grad = jnp.sum(grad_normed * scaled, axis=0)
    return (gain_grad, factor[:, None] * (grad_scaled - scaled * (row_total / D)[:, None]))


def log_total(scores):
    row_top = jnp.max(scores, axis=-1, keepdims=True)
    return row_top + jnp.log(jnp.sum(jnp.exp(scores - row_top), axis=-1, keepdims=True))


def prompt_scores(queries, key_rows, cum_query, cum_key, allowed):
    raw_scores = jnp.einsum("qhd,khd->hqk", queries, key_rows, preferred_element_type=jnp.float32)
    raw_scores = raw_scores * HEAD_DIM ** (-0.5) + cum_query.T[:, :, None] - cum_key.T[:, None, :]
    return jnp.where(allowed[None], raw_scores, masked)


def cont_scores(queries, key_rows, key_cont, cum_query, cum_key, cum_cont, far_ok, near_ok):
    score_scale = HEAD_DIM ** (-0.5)
    query_cum = cum_query.transpose(0, 2, 1)[:, :, :, None]
    far_scores = jnp.einsum("jqhd,khd->jhqk", queries, key_rows, preferred_element_type=jnp.float32)
    far_scores = far_scores * score_scale + query_cum - cum_key.T[None, :, None, :]
    near_scores = jnp.einsum(
        "jqhd,jkhd->jhqk", queries, key_cont, preferred_element_type=jnp.float32
    )
    near_scores = near_scores * score_scale + query_cum - cum_cont.transpose(0, 2, 1)[:, :, None, :]
    far_scores = jnp.where(far_ok[:, None, None, :], far_scores, masked)
    near_scores = jnp.where(near_ok[None, None], near_scores, masked)
    return jnp.concatenate([far_scores, near_scores], axis=-1)


def wide_body(
    x_prompt,
    x_cont,
    teacher_prompt,
    teacher_cont,
    segment_ids,
    offsets,
    prompt_valid,
    cont_valid,
    first_gain,
    w_query,
    w_key,
    w_value,
    w_outgate,
    w_forget,
    forget_bias,
    w_out,
    second_gain,
    w_gate,
    w_up,
    w_down,
):
    row_count = lax.axis_size("row")
    col_count = lax.axis_size("col")
    row_index = lax.axis_index("row")
    local_prompt = x_prompt.shape[1]
    local_conts = x_cont.shape[1]
    quarter = CLEN // row_count
    local_tokens = local_prompt + local_conts * CLEN
    blocks = local_tokens // CLEN
    prompt_blocks = local_prompt // CLEN
    heads_here = w_forget.shape[1]
    width_here = heads_here * HEAD_DIM
    units_here = w_gate.shape[1]
    score_scale = HEAD_DIM ** (-0.5)
    w_project = jnp.concatenate([w_query, w_key, w_value, w_outgate], axis=1)
    w_hidden = jnp.concatenate([w_gate, w_up], axis=1)
    gain_one = first_gain.astype(jnp.float32)
    gain_two = second_gain.astype(jnp.float32)
    position = jnp.arange(PROMPT, dtype=jnp.int32)
    cont_step = jnp.arange(CLEN, dtype=jnp.int32)
    own_step = row_index * quarter + jnp.arange(quarter, dtype=jnp.int32)
    near_ok = cont_step[None, :] <= own_step[:, None]
    own_position = lax.dynamic_index_in_dim(
        position.reshape(col_count, prompt_blocks, row_count, quarter), row_index, 2, keepdims=False
    ).reshape(-1)

    def own_prompt_part(matrix):
        return matrix[:, :prompt_blocks, 0]

    def one_group(carried, group_data):
        (
            acc_project,
            acc_forget,
            acc_bias,
            acc_out,
            acc_hidden,
            acc_down,
            acc_gain_one,
            acc_gain_two,
            error_sum,
            count_sum,
        ) = carried
        (
            prompt_in,
            cont_in,
            teach_prompt,
            teach_cont,
            segment_row,
            offset_row,
            valid_prompt,
            valid_cont,
        ) = group_data
        tokens = jnp.concatenate(
            [prompt_in, cont_in.reshape(local_conts * CLEN, -1)], axis=0
        ).astype(jnp.float32)
        teacher = jnp.concatenate(
            [teach_prompt, teach_cont.reshape(local_conts * CLEN, -1)], axis=0
        ).astype(jnp.float32)
        validity = jnp.concatenate([valid_prompt, valid_cont.reshape(-1)], axis=0).astype(
            jnp.float32
        )
        branch_mask = position[None, :] == offset_row[:, None] - 1
        branch_hot = branch_mask.astype(jnp.float32)
        last_doc = jnp.sum(jnp.where(branch_mask, segment_row[None, :], 0), axis=1)
        far_ok = (position[None, :] < offset_row[:, None]) & (
            segment_row[None, :] == last_doc[:, None]
        )
        own_doc = lax.dynamic_index_in_dim(
            segment_row.reshape(col_count, prompt_blocks, row_count, quarter),
            row_index,
            2,
            keepdims=False,
        ).reshape(-1)
        prompt_ok = (position[None, :] <= own_position[:, None]) & (
            segment_row[None, :] == own_doc[:, None]
        )
        factor_one, scaled_one, normed_one = norm_forward(tokens, gain_one)
        normed_all = group_rows(normed_one)
        project_part = matmul(normed_all, w_project).reshape(
            col_count, blocks, row_count, quarter, 4 * width_here
        )
        forget_part = matmul(normed_all, w_forget).reshape(
            col_count, blocks, row_count, quarter, heads_here
        )
        own_project, own_forget = (
            lax.psum_scatter(project_part, "row", scatter_dimension=2, tiled=True),
            lax.psum_scatter(forget_part, "row", scatter_dimension=2, tiled=True),
        )
        own_query = own_project[..., :width_here].astype(jnp.bfloat16)
        own_kv = own_project[..., width_here : 3 * width_here].astype(jnp.bfloat16)
        gate_logit = own_project[..., 3 * width_here :]
        kv_all, forget_all = (
            lax.all_gather(own_kv, "row", axis=2, tiled=True),
            lax.all_gather(own_forget.astype(jnp.bfloat16), "row", axis=2, tiled=True),
        )
        kv_all = kv_all.reshape(col_count, local_tokens, 2 * width_here)
        pre_gate = (
            forget_all.reshape(col_count, local_tokens, heads_here).astype(jnp.float32)
            + forget_bias
        )
        log_keep = jax.nn.log_sigmoid(pre_gate)
        cum_prompt = jnp.cumsum(log_keep[:, :local_prompt].reshape(PROMPT, heads_here), axis=0)
        branch_cum = jnp.dot(branch_hot, cum_prompt, precision=highest)
        cum_cont = branch_cum[:, None, :] + jnp.cumsum(
            log_keep[:, local_prompt:].reshape(CONTS, CLEN, heads_here), axis=1
        )
        kv_prompt = kv_all[:, :local_prompt].reshape(PROMPT, 2, heads_here, HEAD_DIM)
        key_prompt = kv_prompt[:, 0]
        value_prompt = kv_prompt[:, 1]
        kv_cont = kv_all[:, local_prompt:].reshape(CONTS, CLEN, 2, heads_here, HEAD_DIM)
        key_cont = kv_cont[:, :, 0]
        value_cont = kv_cont[:, :, 1]
        cum_query_prompt = lax.dynamic_index_in_dim(
            cum_prompt.reshape(col_count, prompt_blocks, row_count, quarter, heads_here),
            row_index,
            2,
            keepdims=False,
        ).reshape(-1, heads_here)
        cum_query_cont = lax.dynamic_index_in_dim(
            cum_cont.reshape(CONTS, row_count, quarter, heads_here), row_index, 1, keepdims=False
        )
        query_prompt = own_prompt_part(own_query).reshape(-1, heads_here, HEAD_DIM)
        query_cont = own_query[:, prompt_blocks:, 0].reshape(CONTS, quarter, heads_here, HEAD_DIM)
        scores_prompt = prompt_scores(
            query_prompt, key_prompt, cum_query_prompt, cum_prompt, prompt_ok
        )
        total_prompt = log_total(scores_prompt)
        probs_prompt = jnp.exp(scores_prompt - total_prompt).astype(jnp.bfloat16)
        out_prompt = jnp.einsum(
            "hqk,khd->qhd", probs_prompt, value_prompt, preferred_element_type=jnp.float32
        )
        scores_cont = cont_scores(
            query_cont, key_prompt, key_cont, cum_query_cont, cum_prompt, cum_cont, far_ok, near_ok
        )
        total_cont = log_total(scores_cont)
        probs_cont = jnp.exp(scores_cont - total_cont).astype(jnp.bfloat16)
        out_cont = jnp.einsum(
            "jhqk,khd->jqhd",
            probs_cont[..., :PROMPT],
            value_prompt,
            preferred_element_type=jnp.float32,
        )
        out_cont = out_cont + jnp.einsum(
            "jhqk,jkhd->jqhd",
            probs_cont[..., PROMPT:],
            value_cont,
            preferred_element_type=jnp.float32,
        )
        attended = jnp.concatenate(
            [
                out_prompt.reshape(col_count, prompt_blocks, 1, quarter, width_here),
                out_cont.reshape(col_count, local_conts, 1, quarter, width_here),
            ],
            axis=1,
        )
        gate_sig = jax.nn.sigmoid(gate_logit)
        gated = (attended * gate_sig).astype(jnp.bfloat16)
        gated_all = head_rows(gated)
        residual = tokens + token_sums(matmul(gated_all, w_out))
        factor_two, scaled_two, normed_two = norm_forward(residual, gain_two)
        normed_two_all = group_rows(normed_two)
        hidden_own = row_partials(matmul(normed_two_all, w_hidden), col_count, blocks, quarter)
        gate_rows = hidden_own[..., :units_here]
        up_rows = hidden_own[..., units_here:]
        gate_sig_two = jax.nn.sigmoid(gate_rows)
        silu_rows = gate_rows * gate_sig_two
        hidden_all = head_rows((silu_rows * up_rows).astype(jnp.bfloat16))
        result_rows = residual + token_sums(matmul(hidden_all, w_down))
        deviation = result_rows - teacher
        group_err = 0.5 * jnp.sum(validity[:, None] * deviation * deviation)
        grad_result = validity[:, None] * deviation
        grad_result_all = group_rows(grad_result.astype(jnp.bfloat16))
        grad_down_w = inner_rows(hidden_all, grad_result_all)
        grad_hid = row_partials(by_transpose(grad_result_all, w_down), col_count, blocks, quarter)
        grad_gate = grad_hid * up_rows * gate_sig_two * (1.0 + gate_rows * (1.0 - gate_sig_two))
        grad_up = grad_hid * silu_rows
        grad_hidden_all = head_rows(
            jnp.concatenate([grad_gate, grad_up], axis=-1).astype(jnp.bfloat16)
        )
        grad_hidden_w = inner_rows(normed_two_all, grad_hidden_all)
        grad_normed_two = token_sums(by_transpose(grad_hidden_all, w_hidden))
        gain_two_grad, grad_residual = norm_backward(
            grad_normed_two, factor_two, scaled_two, gain_two
        )
        grad_residual = grad_residual + grad_result
        grad_residual_all = group_rows(grad_residual.astype(jnp.bfloat16))
        grad_out_w = inner_rows(gated_all, grad_residual_all)
        grad_gated = row_partials(
            by_transpose(grad_residual_all, w_out), col_count, blocks, quarter
        )
        grad_attended = (grad_gated * gate_sig).astype(jnp.bfloat16)
        grad_logit = (grad_gated * attended * gate_sig * (1.0 - gate_sig)).astype(jnp.bfloat16)
        grad_att_prompt = own_prompt_part(grad_attended).reshape(-1, heads_here, HEAD_DIM)
        grad_att_cont = grad_attended[:, prompt_blocks:, 0].reshape(
            CONTS, quarter, heads_here, HEAD_DIM
        )
        again_prompt = jnp.exp(
            prompt_scores(query_prompt, key_prompt, cum_query_prompt, cum_prompt, prompt_ok)
            - total_prompt
        )
        grad_prob_prompt = jnp.einsum(
            "qhd,khd->hqk", grad_att_prompt, value_prompt, preferred_element_type=jnp.float32
        )
        grad_score_prompt = (
            again_prompt
            * (grad_prob_prompt - jnp.sum(again_prompt * grad_prob_prompt, axis=-1, keepdims=True))
        ).astype(jnp.bfloat16)
        again_prompt_b = again_prompt.astype(jnp.bfloat16)
        grad_query_prompt = (
            jnp.einsum(
                "hqk,khd->qhd", grad_score_prompt, key_prompt, preferred_element_type=jnp.float32
            )
            * score_scale
        )
        grad_key_prompt = (
            jnp.einsum(
                "hqk,qhd->khd", grad_score_prompt, query_prompt, preferred_element_type=jnp.float32
            )
            * score_scale
        )
        grad_value_prompt = jnp.einsum(
            "hqk,qhd->khd", again_prompt_b, grad_att_prompt, preferred_element_type=jnp.float32
        )
        cum_grad_query_p = jnp.sum(grad_score_prompt, axis=-1, dtype=jnp.float32).T
        cum_grad_key_p = -jnp.sum(grad_score_prompt, axis=1, dtype=jnp.float32).T
        again_cont = jnp.exp(
            cont_scores(
                query_cont,
                key_prompt,
                key_cont,
                cum_query_cont,
                cum_prompt,
                cum_cont,
                far_ok,
                near_ok,
            )
            - total_cont
        )
        grad_prob_cont = jnp.concatenate(
            [
                jnp.einsum(
                    "jqhd,khd->jhqk",
                    grad_att_cont,
                    value_prompt,
                    preferred_element_type=jnp.float32,
                ),
                jnp.einsum(
                    "jqhd,jkhd->jhqk", grad_att_cont, value_cont, preferred_element_type=jnp.float32
                ),
            ],
            axis=-1,
        )
        grad_score_cont = (
            again_cont
            * (grad_prob_cont - jnp.sum(again_cont * grad_prob_cont, axis=-1, keepdims=True))
        ).astype(jnp.bfloat16)
        again_cont_b = again_cont.astype(jnp.bfloat16)
        far_grad = grad_score_cont[..., :PROMPT]
        near_grad = grad_score_cont[..., PROMPT:]
        grad_query_cont = (
            jnp.einsum("jhqk,khd->jqhd", far_grad, key_prompt, preferred_element_type=jnp.float32)
            + jnp.einsum("jhqk,jkhd->jqhd", near_grad, key_cont, preferred_element_type=jnp.float32)
        ) * score_scale
        grad_key_far = (
            jnp.einsum("jhqk,jqhd->khd", far_grad, query_cont, preferred_element_type=jnp.float32)
            * score_scale
        )
        grad_key_near = (
            jnp.einsum("jhqk,jqhd->jkhd", near_grad, query_cont, preferred_element_type=jnp.float32)
            * score_scale
        )
        grad_value_far = jnp.einsum(
            "jhqk,jqhd->khd",
            again_cont_b[..., :PROMPT],
            grad_att_cont,
            preferred_element_type=jnp.float32,
        )
        grad_value_near = jnp.einsum(
            "jhqk,jqhd->jkhd",
            again_cont_b[..., PROMPT:],
            grad_att_cont,
            preferred_element_type=jnp.float32,
        )
        cum_grad_query_c = jnp.sum(grad_score_cont, axis=-1, dtype=jnp.float32).transpose(0, 2, 1)
        cum_grad_key_far = -jnp.sum(far_grad, axis=(0, 2), dtype=jnp.float32).T
        cum_grad_key_near = -jnp.sum(near_grad, axis=2, dtype=jnp.float32).transpose(0, 2, 1)
        kv_grad_prompt = jnp.stack(
            [grad_key_prompt + grad_key_far, grad_value_prompt + grad_value_far], axis=1
        ).reshape(col_count, local_prompt, 2 * width_here)
        kv_grad_cont = jnp.stack([grad_key_near, grad_value_near], axis=2).reshape(
            col_count, local_conts * CLEN, 2 * width_here
        )
        kv_grad_part = jnp.concatenate([kv_grad_prompt, kv_grad_cont], axis=1)
        query_place = lax.dynamic_update_slice_in_dim(
            jnp.zeros((col_count, prompt_blocks, row_count, quarter, heads_here), jnp.float32),
            cum_grad_query_p.reshape(col_count, prompt_blocks, 1, quarter, heads_here),
            row_index,
            axis=2,
        ).reshape(PROMPT, heads_here)
        cont_place = lax.dynamic_update_slice_in_dim(
            jnp.zeros((CONTS, row_count, quarter, heads_here), jnp.float32),
            cum_grad_query_c.reshape(CONTS, 1, quarter, heads_here),
            row_index,
            axis=1,
        ).reshape(CONTS, CLEN, heads_here)
        cum_grad_part = jnp.concatenate(
            [
                (cum_grad_key_p + cum_grad_key_far + query_place).reshape(
                    col_count, local_prompt, heads_here
                ),
                (cum_grad_key_near + cont_place).reshape(col_count, local_conts * CLEN, heads_here),
            ],
            axis=1,
        )
        kv_grad_full, cum_grad_full = lax.psum((kv_grad_part, cum_grad_part), "row")
        cum_grad_cont = cum_grad_full[:, local_prompt:].reshape(CONTS, CLEN, heads_here)
        cum_grad_prompt = cum_grad_full[:, :local_prompt].reshape(PROMPT, heads_here)
        cum_grad_prompt = cum_grad_prompt + jnp.dot(
            branch_hot.T, jnp.sum(cum_grad_cont, axis=1), precision=highest
        )
        log_grad_prompt = lax.cumsum(cum_grad_prompt, axis=0, reverse=True)
        log_grad_cont = lax.cumsum(cum_grad_cont, axis=1, reverse=True)
        log_grad = jnp.concatenate(
            [
                log_grad_prompt.reshape(col_count, local_prompt, heads_here),
                log_grad_cont.reshape(col_count, local_conts * CLEN, heads_here),
            ],
            axis=1,
        )
        pre_grad = log_grad * jax.nn.sigmoid(-pre_gate)
        bias_grad = jnp.sum(pre_grad, axis=(0, 1))
        forget_grad_b = pre_grad.reshape(-1, heads_here).astype(jnp.bfloat16)
        query_grad_own = jnp.concatenate(
            [
                grad_query_prompt.reshape(col_count, prompt_blocks, 1, quarter, width_here),
                grad_query_cont.reshape(col_count, local_conts, 1, quarter, width_here),
            ],
            axis=1,
        )
        qg_grad_all = head_rows(
            jnp.concatenate([query_grad_own.astype(jnp.bfloat16), grad_logit], axis=-1)
        )
        kv_grad_rows = kv_grad_full.reshape(-1, 2 * width_here).astype(jnp.bfloat16)
        project_grad_rows = jnp.concatenate(
            [qg_grad_all[:, :width_here], kv_grad_rows, qg_grad_all[:, width_here:]], axis=-1
        )
        grad_project_w = inner_rows(normed_all, project_grad_rows)
        grad_forget_w = inner_rows(normed_all, forget_grad_b)
        grad_normed_one = token_sums(
            by_transpose(project_grad_rows, w_project) + by_transpose(forget_grad_b, w_forget)
        )
        gain_one_grad, grad_tokens = norm_backward(
            grad_normed_one, factor_one, scaled_one, gain_one
        )
        grad_tokens = grad_tokens + grad_residual
        grad_prompt_one = grad_tokens[:local_prompt]
        grad_cont_one = grad_tokens[local_prompt:].reshape(local_conts, CLEN, -1)
        group_count = jnp.sum(validity) * (row_index == 0).astype(jnp.float32)
        new_carry = (
            acc_project + grad_project_w,
            acc_forget + grad_forget_w,
            acc_bias + bias_grad,
            acc_out + grad_out_w,
            acc_hidden + grad_hidden_w,
            acc_down + grad_down_w,
            acc_gain_one + gain_one_grad,
            acc_gain_two + gain_two_grad,
            error_sum + group_err,
            count_sum + group_count,
        )
        return (new_carry, (grad_prompt_one, grad_cont_one))

    start = (
        jnp.zeros(w_project.shape, jnp.float32),
        jnp.zeros(w_forget.shape, jnp.float32),
        jnp.zeros(forget_bias.shape, jnp.float32),
        jnp.zeros(w_out.shape, jnp.float32),
        jnp.zeros(w_hidden.shape, jnp.float32),
        jnp.zeros(w_down.shape, jnp.float32),
        jnp.zeros(first_gain.shape, jnp.float32),
        jnp.zeros(second_gain.shape, jnp.float32),
        jnp.zeros((), jnp.float32),
        jnp.zeros((), jnp.float32),
    )
    finished, (grad_prompt, grad_cont) = lax.scan(
        one_group,
        start,
        (
            x_prompt,
            x_cont,
            teacher_prompt,
            teacher_cont,
            segment_ids,
            offsets,
            prompt_valid,
            cont_valid,
        ),
    )
    (
        acc_project,
        acc_forget,
        acc_bias,
        acc_out,
        acc_hidden,
        acc_down,
        acc_gain_one,
        acc_gain_two,
        error_sum,
        count_sum,
    ) = finished
    acc_project, acc_forget, acc_bias, acc_out, acc_hidden, acc_down = (
        lax.psum(acc_project.astype(jnp.bfloat16), "dp").astype(jnp.float32),
        lax.psum(acc_forget.astype(jnp.bfloat16), "dp").astype(jnp.float32),
        lax.psum(acc_bias.astype(jnp.bfloat16), "dp").astype(jnp.float32),
        lax.psum(acc_out.astype(jnp.bfloat16), "dp").astype(jnp.float32),
        lax.psum(acc_hidden.astype(jnp.bfloat16), "dp").astype(jnp.float32),
        lax.psum(acc_down.astype(jnp.bfloat16), "dp").astype(jnp.float32),
    )
    gain_one_total, gain_two_total = lax.psum((acc_gain_one, acc_gain_two), ("dp", "col"))
    error_total, count_total = lax.psum((error_sum, count_sum), ("dp", "row", "col"))
    grad_scale = x_prompt.shape[0] * lax.axis_size("dp") * (PROMPT + CONTS * CLEN) / count_total
    loss_value = error_total / (D * count_total)
    width_here = w_query.shape[1]
    units_here = w_gate.shape[1]
    return (
        loss_value,
        grad_prompt * grad_scale,
        grad_cont * grad_scale,
        gain_one_total * grad_scale,
        acc_project[:, :width_here] * grad_scale,
        acc_project[:, width_here : 2 * width_here] * grad_scale,
        acc_project[:, 2 * width_here : 3 * width_here] * grad_scale,
        acc_project[:, 3 * width_here :] * grad_scale,
        acc_forget * grad_scale,
        acc_bias * grad_scale,
        acc_out * grad_scale,
        gain_two_total * grad_scale,
        acc_hidden[:, :units_here] * grad_scale,
        acc_hidden[:, units_here:] * grad_scale,
        acc_down * grad_scale,
    )


AX = ("yo", "y", "c", "x", "zh", "zl")
FAR_PIECE = 18
DOC_LANE = 36
UNIT_LANE = 40
NEVER = 1e12
LANES = 128
BF = jnp.bfloat16
F32 = jnp.float32


class Ring:
    def __init__(self, sizes):
        self.sizes = sizes
        self.zl_count = sizes["zl"]
        self.offsets = [(dy, dz) for dy in range(2) for dz in range(self.zl_count)]
        self.back = [
            self.offsets.index(((-dy) % 2, (-dz) % self.zl_count)) for dy, dz in self.offsets
        ]

    def pairs(self, target, source_ok=None):
        ranges = [range(self.sizes[a]) for a in AX]
        number = {}
        for place, coords in enumerate(itertools.product(*ranges)):
            number[coords] = place
        out = []
        for coords in number:
            here = dict(zip(AX, coords))
            if source_ok is not None and not source_ok(here):
                continue
            there = dict(here, **target(here))
            out.append((number[coords], number[tuple(there[a] for a in AX)]))
        return out

    def move(self, value, target, source_ok=None):
        return lax.ppermute(value, AX, self.pairs(target, source_ok))

    def swap(self, value, axis, source_ok=None):
        return self.move(value, lambda h: {axis: 1 - h[axis]}, source_ok)

    def to_peer(self, value, k):
        dy, dz = self.offsets[k]
        return self.move(
            value, lambda h: {"y": (h["y"] + dy) % 2, "zl": (h["zl"] + dz) % self.zl_count}
        )

    def to_group(self, value, flip):
        return self.move(
            value,
            lambda h: {
                "y": h["zh"],
                "c": h["x"] ^ flip,
                "x": h["y"],
                "zh": h["c"],
            },
        )

    def from_group(self, value, flip):
        return self.move(
            value,
            lambda h: {"y": h["x"], "c": h["zh"], "x": h["c"] ^ flip, "zh": h["y"]},
        )

    def total(self, value):
        for axis in ("c", "y", "x", "zh"):
            value = value + self.swap(value, axis)
        if self.zl_count == 2:
            value = value + self.swap(value, "zl")
        elif self.zl_count > 2:
            value = lax.psum(value, "zl")
        if self.sizes["yo"] > 1:
            value = lax.psum(value, "yo")
        return value

    def gather(self, rows):
        return [rows] + [self.to_peer(rows, k) for k in range(1, len(self.offsets))]

    def scatter_sum(self, partial_of):
        arrived = []
        for k in range(1, len(self.offsets)):
            arrived.append(self.to_peer(partial_of(self.back[k]).astype(BF), k))
        total = partial_of(0)
        for part in arrived:
            total = total + part.astype(F32)
        return total


def nt_dot(left_op, right_op):
    return lax.dot_general(
        left_op, right_op, (((1,), (1,)), ((), ())), preferred_element_type=F32
    )


def tn_dot(left_op, right_op):
    return lax.dot_general(
        left_op, right_op, (((0,), (0,)), ((), ())), preferred_element_type=F32
    )


def nn_dot(left_op, right_op):
    return jnp.dot(left_op, right_op, preferred_element_type=F32)


def split_pieces(values, shift, heads):
    high = values.astype(BF).astype(F32)
    rest = values - high
    mid = rest.astype(BF).astype(F32)
    low = (rest - mid).astype(BF).astype(F32)
    out = None
    for place, piece in enumerate((high, mid, low)):
        amount = shift + place * heads
        moved = pltpu.roll(piece, amount, 1) if amount else piece
        out = moved if out is None else out + moved
    return out


def head_lanes(shape, head, heads):
    lane = lax.broadcasted_iota(jnp.int32, shape, len(shape) - 1)
    keep = lane >= DOC_LANE
    for place in range(3):
        keep = keep | (lane == place * heads + head) | (lane == FAR_PIECE + place * heads + head)
    return keep


def half_lanes(shape, half):
    lane = lax.broadcasted_iota(jnp.int32, shape, len(shape) - 1)
    return (lane >= HEAD_DIM * half) & (lane < HEAD_DIM * (half + 1))


def near_visible(rows):
    key_row = lax.broadcasted_iota(jnp.int32, (rows, rows), 0)
    query_row = lax.broadcasted_iota(jnp.int32, (rows, rows), 1)
    same = (key_row // CLEN) == (query_row // CLEN)
    return same & (key_row <= query_row)


def fill_keys(
    keys, flag, far_own, far_there, kv_near, cum_far, cum_near, far_base, near_base, far_rows, heads
):
    slots = heads // 2

    @pl.when(pl.program_id(0) == 0)
    def _():
        aug = (far_base[...].astype(F32) + split_pieces(-cum_far[...], FAR_PIECE, heads)).astype(BF)
        for s in range(slots):
            keys[s, :far_rows, LANES:] = aug

        @pl.when(flag[0] == 0)
        def _():
            for s in range(slots):
                keys[s, :far_rows, :LANES] = far_own[s][:, :LANES]

        @pl.when(flag[0] != 0)
        def _():
            for s in range(slots):
                keys[s, :far_rows, :LANES] = far_there[s][:, :LANES]

    aug = (near_base[...].astype(F32) + split_pieces(-cum_near[...], FAR_PIECE, heads)).astype(BF)
    for s in range(slots):
        keys[s, far_rows:, :LANES] = kv_near[s][:, :LANES]
        keys[s, far_rows:, LANES:] = aug


def attend_kernel(
    heads,
    flag,
    qg_a,
    qg_b,
    qg_c,
    near_a,
    near_b,
    near_c,
    own_a,
    own_b,
    own_c,
    there_a,
    there_b,
    there_c,
    cum_near,
    cum_far,
    q_base,
    near_base,
    far_base,
    gated_ref,
    att_ref,
    log_ref,
    keys,
    vals,
):
    qg = (qg_a, qg_b, qg_c)
    kv_near = (near_a, near_b, near_c)
    far_own = (own_a, own_b, own_c)
    far_there = (there_a, there_b, there_c)
    rows = qg_a.shape[0]
    far_rows = own_a.shape[0]
    slots = heads // 2
    fill_keys(
        keys,
        flag,
        far_own,
        far_there,
        kv_near,
        cum_far,
        cum_near,
        far_base,
        near_base,
        far_rows,
        heads,
    )

    @pl.when(pl.program_id(0) == 0)
    def _():
        def fill(source):
            for s in range(slots):
                moved = source[s][:, LANES:].T
                for half in range(2):
                    vals[2 * s + half, :HEAD_DIM, :far_rows] = moved[
                        HEAD_DIM * half : HEAD_DIM * (half + 1)
                    ]

        @pl.when(flag[0] == 0)
        def _():
            fill(far_own)

        @pl.when(flag[0] != 0)
        def _():
            fill(far_there)

        for h in range(heads):
            vals[h, HEAD_DIM:, :] = jnp.ones((16, far_rows + rows), BF)

    for s in range(slots):
        moved = kv_near[s][:, LANES:].T
        for half in range(2):
            vals[2 * s + half, :HEAD_DIM, far_rows:] = moved[
                HEAD_DIM * half : HEAD_DIM * (half + 1)
            ]
    q_aug = (q_base[...].astype(F32) + split_pieces(cum_near[...], 0, heads)).astype(BF)
    visible = near_visible(rows)
    outs = []
    logs = []
    for h in range(heads):
        s, half = h // 2, h % 2
        query = qg[s][:, :LANES]
        query = jnp.where(half_lanes(query.shape, half), query * BF(HEAD_DIM**-0.5), BF(0))
        aug = jnp.where(head_lanes(q_aug.shape, h, heads), q_aug, BF(0))
        q_cat = jnp.concatenate([query, aug], axis=1)
        far = nt_dot(keys[s, :far_rows], q_cat)
        near = jnp.where(visible, nt_dot(keys[s, far_rows:], q_cat), -NEVER)
        top = jnp.maximum(
            jnp.max(far, axis=0, keepdims=True), jnp.max(near, axis=0, keepdims=True)
        )
        far_p = jnp.exp(far - top).astype(BF)
        near_p = jnp.exp(near - top).astype(BF)
        out = nn_dot(vals[h, :, :far_rows], far_p) + nn_dot(vals[h, :, far_rows:], near_p)
        total = out[HEAD_DIM : HEAD_DIM + 1]
        outs.append(out[:HEAD_DIM] / total)
        logs.append(top + jnp.log(total))
    att = jnp.concatenate(outs, axis=0).T
    att_ref[...] = att
    for s in range(slots):
        gate = qg[s][:, LANES:].astype(F32)
        cols = slice(s * LANES, (s + 1) * LANES)
        gated_ref[:, cols] = (att[:, cols] * jax.nn.sigmoid(gate)).astype(BF)
    log_rows = jnp.concatenate(logs + [jnp.zeros((LANES - heads, rows), F32)], axis=0)
    log_ref[...] = log_rows.T


def row_block(rows, cols, place=0):
    return pl.BlockSpec((rows, cols), lambda i: (i, place))


def whole_block(rows, cols):
    return pl.BlockSpec((rows, cols), lambda i: (0, 0))


def slot_inputs(flag, projects, kv_there, rows):
    far_rows = projects[0].shape[0]
    specs_in = [pl.BlockSpec(memory_space=pltpu.SMEM)]
    for spec in (
        row_block(rows, 2 * LANES),
        row_block(rows, 2 * LANES, 1),
        pl.BlockSpec((far_rows, 2 * LANES), lambda i: (0, 1)),
        whole_block(far_rows, 2 * LANES),
    ):
        specs_in += [spec] * len(projects)
    return specs_in, [flag, *projects, *projects, *projects, *kv_there]


def cum_specs(rows, far_rows):
    return [
        row_block(rows, LANES),
        whole_block(far_rows, LANES),
        row_block(rows, LANES),
        row_block(rows, LANES),
        whole_block(far_rows, LANES),
    ]


def attend(flag, projects, kv_there, cum_near, cum_far, q_base, near_base, far_base, rows, heads):
    total = projects[0].shape[0]
    width = heads * HEAD_DIM
    steps = total // rows
    flops = 2 * total * (total + rows) * heads * 384
    slot_specs, slot_values = slot_inputs(flag, projects, kv_there, rows)
    return pl.pallas_call(
        functools.partial(attend_kernel, heads),
        grid=(steps,),
        out_shape=(
            jax.ShapeDtypeStruct((total, width), BF),
            jax.ShapeDtypeStruct((total, width), F32),
            jax.ShapeDtypeStruct((total, LANES), F32),
        ),
        in_specs=slot_specs + cum_specs(rows, total),
        out_specs=(row_block(rows, width), row_block(rows, width), row_block(rows, LANES)),
        scratch_shapes=[
            pltpu.VMEM((heads // 2, total + rows, 2 * LANES), BF),
            pltpu.VMEM((heads, HEAD_DIM + 16, total + rows), BF),
        ],
        compiler_params=pltpu.CompilerParams(vmem_limit_bytes=60 << 20),
        cost_estimate=pl.CostEstimate(
            flops=flops, bytes_accessed=total * width * 20, transcendentals=total * total * heads
        ),
    )(*slot_values, cum_near, cum_far, q_base, near_base, far_base)


def attend_back_kernel(
    heads,
    flag,
    qg_a,
    qg_b,
    qg_c,
    near_a,
    near_b,
    near_c,
    own_a,
    own_b,
    own_c,
    there_a,
    there_b,
    there_c,
    cum_near,
    cum_far,
    q_base,
    near_base,
    far_base,
    grad_ref,
    att_ref,
    log_ref,
    dqg_ref,
    near_ref,
    far_out,
    row_ref,
    near_col,
    far_col,
    keys,
    vals,
    far_ref,
):
    qg = (qg_a, qg_b, qg_c)
    kv_near = (near_a, near_b, near_c)
    far_own = (own_a, own_b, own_c)
    far_there = (there_a, there_b, there_c)
    rows = qg_a.shape[0]
    far_rows = own_a.shape[0]
    slots = heads // 2
    fill_keys(
        keys,
        flag,
        far_own,
        far_there,
        kv_near,
        cum_far,
        cum_near,
        far_base,
        near_base,
        far_rows,
        heads,
    )

    @pl.when(pl.program_id(0) == 0)
    def _():
        lane = lax.broadcasted_iota(jnp.int32, (far_rows + rows, LANES), 1)
        ones = (lane < 3).astype(F32).astype(BF)
        for s in range(slots):
            vals[s, :, LANES:] = ones

        @pl.when(flag[0] == 0)
        def _():
            for s in range(slots):
                vals[s, :far_rows, :LANES] = far_own[s][:, LANES:]

        @pl.when(flag[0] != 0)
        def _():
            for s in range(slots):
                vals[s, :far_rows, :LANES] = far_there[s][:, LANES:]

        far_ref[...] = jnp.zeros(far_ref.shape, F32)
        far_col[...] = jnp.zeros(far_col.shape, F32)

    for s in range(slots):
        vals[s, far_rows:, :LANES] = kv_near[s][:, LANES:]
    q_aug = (q_base[...].astype(F32) + split_pieces(cum_near[...] - log_ref[...], 0, heads)).astype(
        BF
    )
    visible = near_visible(rows)
    lane = lax.broadcasted_iota(jnp.int32, (rows, LANES), 1)
    row_total = jnp.zeros((rows, LANES), F32)
    col_total = jnp.zeros((rows, LANES), F32)
    for s in range(slots):
        cols = slice(s * LANES, (s + 1) * LANES)
        kcols = slice(2 * s * LANES, (2 * s + 1) * LANES)
        vcols = slice((2 * s + 1) * LANES, (2 * s + 2) * LANES)
        gate_sig = jax.nn.sigmoid(qg[s][:, LANES:].astype(F32))
        grad = grad_ref[:, cols].astype(F32)
        att = att_ref[:, cols]
        grad_att = (grad * gate_sig).astype(BF)
        dqg_ref[:, vcols] = (grad * att * gate_sig * (1.0 - gate_sig)).astype(BF)
        weighed = grad_att.astype(F32) * att
        dq_total = jnp.zeros((rows, LANES), F32)
        dk_near = jnp.zeros((rows, LANES), F32)
        dv_near = jnp.zeros((rows, LANES), F32)
        for half in range(2):
            h = 2 * s + half
            mine = half_lanes((rows, LANES), half)
            query = jnp.where(mine, qg[s][:, :LANES] * BF(HEAD_DIM**-0.5), BF(0))
            aug = jnp.where(head_lanes(q_aug.shape, h, heads), q_aug, BF(0))
            q_cat = jnp.concatenate([query, aug], axis=1)
            ga = jnp.where(mine, grad_att, BF(0))
            delta = -jnp.sum(jnp.where(mine, weighed, 0.0), axis=1, keepdims=True)
            high = delta.astype(BF).astype(F32)
            mid = (delta - high).astype(BF).astype(F32)
            low = delta - high - mid
            d_aug = jnp.where(
                lane == 0, high, jnp.where(lane == 1, mid, jnp.where(lane == 2, low, 0.0))
            ).astype(BF)
            ga_cat = jnp.concatenate([ga, d_aug], axis=1)
            for part in range(2):
                span = slice(0, far_rows) if part == 0 else slice(far_rows, far_rows + rows)
                prob = jnp.exp(nt_dot(keys[s, span], q_cat))
                if part == 1:
                    prob = jnp.where(visible, prob, 0.0)
                ds = (prob * nt_dot(vals[s, span], ga_cat)).astype(BF)
                dv = nn_dot(prob.astype(BF), ga)
                dk = nn_dot(ds, q_cat)
                dq = tn_dot(ds, keys[s, span])
                dq_total += jnp.where(mine, dq[:, :LANES], 0.0)
                row_total += jnp.where(lane == h, dq[:, LANES:], 0.0)
                if part == 0:
                    far_ref[:, kcols] += dk[:, :LANES]
                    far_ref[:, vcols] += dv
                    far_col[...] += dk[:, LANES:]
                else:
                    dk_near += dk[:, :LANES]
                    dv_near += dv
                    col_total += dk[:, LANES:]
        dqg_ref[:, kcols] = (dq_total * HEAD_DIM**-0.5).astype(BF)
        near_ref[:, kcols] = dk_near
        near_ref[:, vcols] = dv_near
    row_ref[...] = row_total
    near_col[...] = col_total

    @pl.when(pl.program_id(0) == pl.num_programs(0) - 1)
    def _():
        far_out[...] = far_ref[...].astype(BF)


def attend_back(
    flag,
    projects,
    kv_there,
    cum_near,
    cum_far,
    q_base,
    near_base,
    far_base,
    grad,
    att,
    logs,
    rows,
    heads,
):
    total = projects[0].shape[0]
    width = heads * HEAD_DIM
    steps = total // rows
    flops = 2 * total * (total + rows) * heads * 1152
    slot_specs, slot_values = slot_inputs(flag, projects, kv_there, rows)
    return pl.pallas_call(
        functools.partial(attend_back_kernel, heads),
        grid=(steps,),
        out_shape=(
            jax.ShapeDtypeStruct((total, 2 * width), BF),
            jax.ShapeDtypeStruct((total, 2 * width), F32),
            jax.ShapeDtypeStruct((total, 2 * width), BF),
            jax.ShapeDtypeStruct((total, LANES), F32),
            jax.ShapeDtypeStruct((total, LANES), F32),
            jax.ShapeDtypeStruct((total, LANES), F32),
        ),
        in_specs=slot_specs
        + cum_specs(rows, total)
        + [row_block(rows, width), row_block(rows, width), row_block(rows, LANES)],
        out_specs=(
            row_block(rows, 2 * width),
            row_block(rows, 2 * width),
            whole_block(total, 2 * width),
            row_block(rows, LANES),
            row_block(rows, LANES),
            whole_block(total, LANES),
        ),
        scratch_shapes=[
            pltpu.VMEM((heads // 2, total + rows, 2 * LANES), BF),
            pltpu.VMEM((heads // 2, total + rows, 2 * LANES), BF),
            pltpu.VMEM((total, 2 * width), F32),
        ],
        compiler_params=pltpu.CompilerParams(vmem_limit_bytes=60 << 20),
        cost_estimate=pl.CostEstimate(
            flops=flops, bytes_accessed=total * width * 40, transcendentals=total * total * heads
        ),
    )(*slot_values, cum_near, cum_far, q_base, near_base, far_base, grad, att, logs)


def full_norm(tokens, gain_vec):
    factor = lax.rsqrt(jnp.mean(tokens * tokens, axis=-1, keepdims=True) + epsilon)
    scaled = tokens * factor
    return factor, scaled, (scaled * gain_vec).astype(BF)


def full_norm_back(grad_normed, factor, scaled, gain_vec):
    e = grad_normed * gain_vec
    mean = jnp.mean(e * scaled, axis=-1, keepdims=True)
    return jnp.sum(grad_normed * scaled, axis=0), factor * (e - scaled * mean)


MESH_ID = pl.DeviceIdType.MESH


class Here:
    def __init__(self, ring):
        self.ring = ring
        self.at = {a: lax.axis_index(a) for a in AX}

    def other(self, axis):
        return {axis: 1 - self.at[axis]}

    def peer(self, k):
        dy, dz = self.ring.offsets[k]
        return {
            "y": lax.rem(self.at["y"] + dy, 2),
            "zl": lax.rem(self.at["zl"] + dz, self.ring.zl_count),
        }

    def group_to(self, flip):
        at = self.at
        return {"y": at["zh"], "c": at["x"] ^ flip, "x": at["y"], "zh": at["c"]}

    def group_from(self, flip):
        at = self.at
        return {"y": at["x"], "c": at["zh"], "x": at["c"] ^ flip, "zh": at["y"]}

    def group_away(self):
        at = self.at
        return ~((at["y"] == at["zh"]) & (at["y"] == at["x"]) & (at["y"] == at["c"]))

    def greet_group(self, targets):
        away = self.group_away()
        self.greet(
            targets + [self.group_to(1), self.group_from(1)],
            [(self.group_to(0), away), (self.group_from(0), away)],
        )

    def greet(self, targets, extra=()):
        barrier = pltpu.get_barrier_semaphore()
        for target in targets:
            pl.semaphore_signal(barrier, inc=1, device_id=target, device_id_type=MESH_ID)
        count = len(targets)
        for target, away in extra:
            @pl.when(away)
            def _():
                pl.semaphore_signal(barrier, inc=1, device_id=target, device_id_type=MESH_ID)

            count = count + away.astype(jnp.int32)
        pl.semaphore_wait(barrier, count)


def remote(src, dst, send_sem, recv_sem, target):
    return pltpu.make_async_remote_copy(
        src_ref=src,
        dst_ref=dst,
        send_sem=send_sem,
        recv_sem=recv_sem,
        device_id=target,
        device_id_type=MESH_ID,
    )


def last_kernel(
    ring,
    heads,
    dqg_in,
    near_in,
    far_in,
    row_in,
    near_col_in,
    far_col_in,
    weight_in,
    normed_in,
    gated_in,
    mixed_in,
    tokens_in,
    residual_in,
    hid_in,
    down_kept_in,
    down_there_in,
    gain_ref,
    forget_w,
    sig_ref,
    hot_ref,
    error_ref,
    gain_two_ref,
    valid_ref,
    back_out,
    proj_out,
    gate_out,
    up_out,
    down_out,
    out_out,
    small_out,
    grads,
    near,
    far_own,
    far_land,
    row_sum,
    near_col,
    far_col,
    far_col_land,
    cum,
    tot_send,
    tot_land,
    weight,
    normed,
    gated,
    mixed,
    tokens,
    residual,
    rs_send,
    rs_land,
    total,
    c_send,
    c_land,
    kept,
    x_send,
    x_land,
    z_send,
    z_land,
    final,
    kept_f,
    xf_send,
    xf_land,
    zf_send,
    zf_land,
    final_f,
    yf_land,
    full_f,
    co_send,
    co_land,
    kept_d,
    there_d,
    zd_send,
    zd_land,
    final_d,
    kept_o,
    xo_send,
    xo_land,
    zo_send,
    zo_land,
    final_o,
    blocks,
    gain_sum,
    gain_nat,
    gain_land,
    load_sem,
    local_sem,
    swap_send_sem,
    swap_recv_sem,
    y_send_sem,
    y_recv_sem,
    c2_send_sem,
    c2_recv_sem,
    rs_send_sem,
    rs_recv_sem,
    c_send_sem,
    c_recv_sem,
    x_send_sem,
    x_recv_sem,
    z_send_sem,
    z_recv_sem,
    back_send_sem,
    back_recv_sem,
    gain_send_sem,
    gain_recv_sem,
):
    here = Here(ring)
    y, c, x, zh, zl = (here.at[a] for a in ("y", "c", "x", "zh", "zl"))
    local, features = tokens.shape
    rows_all = normed.shape[0]
    part = features // 4
    slot_w = 4 * LANES
    slots = heads // 2
    all_w = slots * slot_w
    units = down_kept_in.shape[0] // 2
    owner = zh == y
    peers = len(ring.offsets)
    away = here.group_away()
    all_loads = [
        (row_in, row_sum),
        (near_col_in, near_col),
        (far_col_in, far_col),
        (far_in, far_own),
        (near_in, near),
    ]
    for s in range(slots):
        all_loads.append(
            (
                dqg_in.at[:, 2 * s * LANES : 2 * (s + 1) * LANES],
                grads.at[:, s * slot_w : s * slot_w + 2 * LANES],
            )
        )
    all_loads += [
        (down_kept_in, kept_d),
        (down_there_in, there_d),
        (normed_in, normed),
        (weight_in, weight),
        (gated_in, gated),
        (mixed_in, mixed),
        (tokens_in, tokens),
        (residual_in, residual),
    ]
    loads = [
        pltpu.make_async_copy(a, b, load_sem.at[i]) for i, (a, b) in enumerate(all_loads)
    ]
    first_loads = 8 + slots
    for copy in loads[:first_loads]:
        copy.start()
    load_row, load_near_col, load_far_col, load_far, load_near = loads[:5]
    load_dqg = loads[5 : 5 + slots]
    load_kept_d, load_there_d = loads[5 + slots : 7 + slots]
    load_normed, load_weight, load_gated, load_mixed, load_tokens, load_residual = loads[7 + slots :]

    here.greet_group(
        [here.peer(k) for k in range(1, peers)]
        + [here.other("c"), here.other("x"), here.other("zh")]
    )
    far_swap = remote(
        far_in, far_land, swap_send_sem.at[0], swap_recv_sem.at[0], here.other("c")
    )
    far_swap.start()
    col_swap = remote(
        far_col_in, far_col_land, swap_send_sem.at[1], swap_recv_sem.at[1], here.other("c")
    )
    col_swap.start()

    row0 = pl.multiple_of(c * part, part)

    def rows_of(ref, col, width):
        return ref.at[pl.ds(row0, part), pl.ds(pl.multiple_of(col, LANES), width)]

    def cols_of(ref, row, height):
        return ref.at[pl.ds(pl.multiple_of(row, LANES), height), pl.ds(row0, part)]

    def y_copy(i, src, dst):
        return remote(src, dst, y_send_sem.at[i], y_recv_sem.at[i], here.other("y"))

    pieces = [
        (hid_in.at[:, :units], rows_of(gate_out, y * units, units)),
        (hid_in.at[:, units:], rows_of(up_out, y * units, units)),
        (final_d, cols_of(down_out, y * units, units)),
    ]
    own_pieces = [
        pltpu.make_async_copy(src, dst, local_sem.at[i]) for i, (src, dst) in enumerate(pieces)
    ]
    y_pieces = [y_copy(i, src, dst) for i, (src, dst) in enumerate(pieces)]
    for copy in own_pieces[:2] + y_pieces[:2]:
        copy.start()

    lane = lax.broadcasted_iota(jnp.int32, (CLEN, LANES), 1)
    head_lane = lane < heads
    all_units = rows_all // CLEN
    chunk_units = local // CLEN

    def unit_rows(u):
        return slice(u * CLEN, (u + 1) * CLEN)

    load_row.wait()
    load_near_col.wait()
    for u in range(all_units):
        value = row_sum[unit_rows(u), :] - pltpu.roll(
            near_col[unit_rows(u), :], LANES - FAR_PIECE, 1
        )
        value = jnp.where(head_lane, value, 0.0)
        cum[unit_rows(u), :] = value
        tot_send[u : u + 1, :] = jnp.sum(value, axis=0, keepdims=True)
    tot_swap = remote(
        tot_send.at[:all_units],
        tot_land.at[:all_units],
        swap_send_sem.at[2],
        swap_recv_sem.at[2],
        here.other("c"),
    )
    tot_swap.start()

    load_kept_d.wait()
    load_there_d.wait()
    zd_send[...] = (kept_d[units:, :] + there_d[units:, :].astype(F32)).astype(BF)
    zd_copy = remote(zd_send, zd_land, z_send_sem.at[5], z_recv_sem.at[5], here.other("zh"))
    zd_copy.start()

    load_far.wait()
    load_near.wait()
    for copy in load_dqg:
        copy.wait()
    for copy in loads[first_loads:]:
        copy.start()
    far_swap.wait_recv()
    on_prompt = jnp.where(c == 0, 1.0, 0.0)

    def merge(i, carry):
        rows = pl.ds(pl.multiple_of(i * CLEN, CLEN), CLEN)
        value = near[rows, :] + on_prompt * (
            far_own[rows, :].astype(F32) + far_land[rows, :].astype(F32)
        )
        value = value.astype(BF)
        for s in range(slots):
            grads[rows, s * slot_w + 2 * LANES : (s + 1) * slot_w] = value[
                :, 2 * s * LANES : 2 * (s + 1) * LANES
            ]
        return carry

    lax.fori_loop(0, all_units, merge, 0)
    load_far_col.wait()
    col_swap.wait_recv()
    tot_swap.wait_recv()

    @pl.when(c == 0)
    def _():
        for u in range(all_units):
            both = far_col[unit_rows(u), :] + far_col_land[unit_rows(u), :]
            value = cum[unit_rows(u), :] - jnp.where(
                head_lane, pltpu.roll(both, LANES - FAR_PIECE, 1), 0.0
            )
            for j in range(all_units):
                value = value + hot_ref[unit_rows(u), j : j + 1] * tot_land[j : j + 1, :]
            cum[unit_rows(u), :] = value

    step_row = lax.broadcasted_iota(jnp.int32, (CLEN, CLEN), 0)
    step_col = lax.broadcasted_iota(jnp.int32, (CLEN, CLEN), 1)
    tri_back = (step_col >= step_row).astype(F32)
    for u in range(all_units):
        value = jnp.dot(
            tri_back,
            cum[unit_rows(u), :],
            precision=highest,
            preferred_element_type=F32,
        )
        cum[unit_rows(u), :] = value
        tot_send[all_units + u : all_units + u + 1, :] = value[0:1, :]
    places = []
    for dy, dz in ring.offsets:
        place = lax.rem(y + 2 - dy, 2) * ring.zl_count + lax.rem(
            zl + ring.zl_count - dz, ring.zl_count
        )
        for i in range(chunk_units):
            places.append(place * chunk_units + i)
    bias = jnp.zeros((1, LANES), F32)
    for u in range(all_units):
        suffix = jnp.zeros((1, LANES), F32)
        for other in range(all_units):
            if other != u:
                seen = jnp.where((places[other] > places[u]) & (c == 0), 1.0, 0.0)
                suffix = suffix + seen * tot_send[all_units + other : all_units + other + 1, :]
        value = (cum[unit_rows(u), :] + suffix) * sig_ref[unit_rows(u), :]
        grads[unit_rows(u), all_w:] = value.astype(BF)
        bias = bias + jnp.sum(value, axis=0, keepdims=True)

    load_normed.wait()
    tile_r = LANES
    per_part = part // tile_r

    def weight_tile(first, i):
        cols = pl.ds(pl.multiple_of(first + i * tile_r, LANES), tile_r)
        return tn_dot(normed[:, cols], grads[...])

    def c_step(i, carry):
        rows = pl.ds(pl.multiple_of(i * tile_r, tile_r), tile_r)
        c_send[rows, :] = weight_tile(2 * part, i).astype(BF)
        return carry

    lax.fori_loop(0, 2 * per_part, c_step, 0)
    c_copy = remote(c_send, c_land, c_send_sem.at[0], c_recv_sem.at[0], here.other("c"))
    c_copy.start()

    load_gated.wait()
    load_mixed.wait()
    out_rows = slots * LANES

    def out_tile(s, cols):
        return tn_dot(gated[:, s * LANES : (s + 1) * LANES], mixed[:, cols])

    for s in range(slots):
        co_send[s * LANES : (s + 1) * LANES, :] = out_tile(
            s, slice(2 * part, features)
        ).astype(BF)
    co_copy = remote(co_send, co_land, c_send_sem.at[1], c_recv_sem.at[1], here.other("c"))
    co_copy.start()

    zd_copy.wait_recv()
    final_d[...] = (
        kept_d[:units, :] + there_d[:units, :].astype(F32) + zd_land[...].astype(F32)
    ).astype(BF)
    for copy in own_pieces[2:] + y_pieces[2:]:
        copy.start()

    load_weight.wait()
    tiles = 3
    tile_w = features // tiles

    def partial_rows(chunk_no, store):
        rows = slice(chunk_no * local, (chunk_no + 1) * local)

        def step(i, carry):
            cols = pl.ds(pl.multiple_of(i * tile_w, LANES), tile_w)
            value = nn_dot(grads[rows, all_w:], forget_w[:, cols])
            for s in range(slots):
                value = value + nt_dot(
                    grads[rows, s * slot_w : (s + 1) * slot_w], weight[s, cols, :]
                )
            store(cols, value)
            return carry

        lax.fori_loop(0, tiles, step, 0)

    moves = RingRows(here, local)

    def rs_copy(i):
        return moves.sum_copy(rs_send, rs_land, rs_send_sem, rs_recv_sem, i)

    for k in (3, 1, 2):

        def store_out(cols, value, k=k):
            rs_send[k - 1, :, cols] = value.astype(BF)

        partial_rows(k, store_out)
        for i in SUM_STARTS[k]:
            rs_copy(i).start()

    c_copy.wait_recv()

    def x_step(i, carry):
        rows = pl.ds(pl.multiple_of(i * tile_r, tile_r), tile_r)
        land = pl.ds(pl.multiple_of(part + i * tile_r, tile_r), tile_r)
        value = weight_tile(part, i) + c_land[land, :].astype(F32)
        for s in range(slots):
            x_send[s, rows, :] = value[:, s * slot_w : (s + 1) * slot_w].astype(BF)
        xf_send[rows, :] = value[:, all_w:].astype(BF)
        return carry

    lax.fori_loop(0, per_part, x_step, 0)
    x_copies = {}
    for s in (2, 1, 0):
        x_copies[s] = remote(
            x_send.at[s], x_land.at[s], x_send_sem.at[s], x_recv_sem.at[s], here.other("x")
        )
        x_copies[s].start()
    xf_copy = remote(xf_send, xf_land, x_send_sem.at[3], x_recv_sem.at[3], here.other("x"))
    xf_copy.start()
    co_copy.wait_recv()
    for s in range(slots):
        rows = slice(s * LANES, (s + 1) * LANES)
        xo_send[rows, :] = (
            out_tile(s, slice(part, 2 * part)) + co_land[rows, part:].astype(F32)
        ).astype(BF)
    xo_copy = remote(xo_send, xo_land, x_send_sem.at[4], x_recv_sem.at[4], here.other("x"))
    xo_copy.start()

    def own_step(i, carry):
        rows = pl.ds(pl.multiple_of(i * tile_r, tile_r), tile_r)
        value = weight_tile(0, i) + c_land[rows, :].astype(F32)
        for s in range(slots):
            kept[s, rows, :] = value[:, s * slot_w : (s + 1) * slot_w]
        kept_f[rows, :] = value[:, all_w:]
        return carry

    lax.fori_loop(0, per_part, own_step, 0)
    for s in range(slots):
        rows = slice(s * LANES, (s + 1) * LANES)
        kept_o[rows, :] = out_tile(s, slice(0, part)) + co_land[rows, :part].astype(F32)

    def store_own(cols, value):
        total[:, cols] = value

    partial_rows(0, store_own)

    def z_copy(i, src, dst):
        return remote(src, dst, z_send_sem.at[i], z_recv_sem.at[i], here.other("zh"))

    z_first = z_copy(0, z_send.at[0], z_land.at[0])
    z_mid = z_copy(1, z_send.at[1], z_land.at[1])
    z_forget = z_copy(2, zf_send, zf_land)
    zo_first = z_copy(3, zo_send.at[0], zo_land.at[0])
    zo_mid = z_copy(4, zo_send.at[1], zo_land.at[1])
    moves.hand_on(rs_send, rs_land, rs_send_sem, rs_recv_sem)
    x_copies[2].wait_recv()
    z_send[0] = (kept[2] + x_land[2].astype(F32)).astype(BF)
    z_first.start()
    x_copies[1].wait_recv()

    @pl.when(~owner)
    def _():
        z_send[1] = (kept[1] + x_land[1].astype(F32)).astype(BF)
        z_mid.start()


    load_tokens.wait()
    load_residual.wait()
    for i in (0, 2, 4, 5):
        rs_copy(i).wait_recv()
    gain_sum[...] = jnp.zeros(gain_sum.shape, F32)
    tile_n = 32

    def norm_step(i, carry):
        rows = pl.ds(pl.multiple_of(i * tile_n, tile_n), tile_n)
        tok = tokens[rows, :].astype(F32)
        grad = total[rows, :]
        for k in (0, 2):
            grad = grad + rs_land[k, rows, :].astype(F32)
        factor = lax.rsqrt(jnp.mean(tok * tok, axis=-1, keepdims=True) + epsilon)
        scaled_tok = tok * factor
        e = grad * gain_ref[...]
        mean = jnp.mean(e * scaled_tok, axis=-1, keepdims=True)
        out = factor * (e - scaled_tok * mean) + residual[rows, :]
        weighed = jnp.sum(grad * scaled_tok, axis=0, keepdims=True)
        for b in range(4):
            blocks[b, rows, :] = out[:, b * part : (b + 1) * part].astype(BF)
            gain_sum[b, 0:1, :] += weighed[:, b * part : (b + 1) * part]
        return carry

    lax.fori_loop(0, local // tile_n, norm_step, 0)

    def block_no(half, low_high):
        return (half ^ x) + 2 * (low_high ^ c)

    def back_copy(flip, p):
        return remote(
            blocks.at[block_no(c ^ flip, p)],
            back_out.at[c, :, p * part : (p + 1) * part],
            back_send_sem.at[flip, p],
            back_recv_sem.at[flip, p],
            here.group_from(flip),
        )

    def back_own(flip, p):
        return pltpu.make_async_copy(
            blocks.at[block_no(c ^ flip, p)],
            back_out.at[c, :, p * part : (p + 1) * part],
            local_sem.at[5 + p],
        )

    for p in range(2):
        back_copy(1, p).start()

    @pl.when(away)
    def _():
        for p in range(2):
            back_copy(0, p).start()

    @pl.when(~away)
    def _():
        for p in range(2):
            back_own(0, p).start()

    for b in range(4):
        gain_sum[b, 1:2, :] = gain_two_ref[0:1, b * part : (b + 1) * part]
    for b in range(4):
        gain_nat[0, b] = gain_sum[block_no(b // 2, b % 2)]
    wide_lane = lax.broadcasted_iota(jnp.int32, (1, part), 1)
    scalars = jnp.where(
        wide_lane == 0, jnp.sum(error_ref[0:1, :], axis=1, keepdims=True), 0.0
    ) + jnp.where(wide_lane == 1, jnp.sum(valid_ref[...], axis=0, keepdims=True), 0.0)
    small_lane = lax.broadcasted_iota(jnp.int32, (1, LANES), 1)
    for j in range(heads):
        if j < 2:
            quarter, head = zh, 4 * y + j
        elif j < 4:
            quarter, head = y, j
        else:
            quarter, head = 1 - zh, 4 * y + j - 4
        dest = 2 + (quarter * ring.zl_count + zl) * heads + head
        value = jnp.sum(jnp.where(small_lane == j, bias, 0.0), axis=1, keepdims=True)
        scalars = scalars + jnp.where(wide_lane == dest, value, 0.0)
    gain_nat[0, 0, 2:3, :] = scalars
    gain_axes = ("c", "y", "x", "zl", "zh")

    def gain_step(place):
        return remote(
            gain_nat.at[place],
            gain_land.at[place],
            gain_send_sem.at[place],
            gain_recv_sem.at[place],
            here.other(gain_axes[place]),
        )

    def gain_next(place):
        gain_step(place).wait_recv()
        gain_nat[place + 1] = gain_nat[place] + gain_land[place]
        if place < 4:
            gain_step(place + 1).start()

    gain_step(0).start()

    x_copies[0].wait_recv()
    kept[0] += x_land[0].astype(F32)
    gain_next(0)
    xf_copy.wait_recv()
    kept_f[...] += xf_land[...].astype(F32)
    zf_send[...] = kept_f[...].astype(BF)
    z_forget.start()
    xo_copy.wait_recv()
    kept_o[...] += xo_land[...].astype(F32)
    gain_next(1)
    zo_send[0] = kept_o[2 * LANES :, :].astype(BF)
    zo_first.start()

    @pl.when(~owner)
    def _():
        zo_send[1] = kept_o[LANES : 2 * LANES, :].astype(BF)
        zo_mid.start()

    first_dst = rows_of(proj_out, 2 * y * slot_w, slot_w)
    mid_dst = rows_of(proj_out, slot_w, slot_w)
    out_first_dst = cols_of(out_out, 2 * LANES * y, LANES)
    out_mid_dst = cols_of(out_out, LANES, LANES)
    y_first = y_copy(3, final.at[0], first_dst)
    y_mid = y_copy(4, final.at[1], mid_dst)
    y_forget = y_copy(5, final_f, yf_land)
    yo_first = y_copy(6, final_o.at[0], out_first_dst)
    yo_mid = y_copy(7, final_o.at[1], out_mid_dst)
    own_first = pltpu.make_async_copy(final.at[0], first_dst, local_sem.at[8])
    own_mid = pltpu.make_async_copy(final.at[1], mid_dst, local_sem.at[9])
    own_out_first = pltpu.make_async_copy(final_o.at[0], out_first_dst, local_sem.at[10])
    own_out_mid = pltpu.make_async_copy(final_o.at[1], out_mid_dst, local_sem.at[11])
    own_forget = pltpu.make_async_copy(
        full_f, proj_out.at[pl.ds(row0, part), all_w : all_w + LANES], local_sem.at[12]
    )
    z_first.wait_recv()
    final[0] = (kept[0] + z_land[0].astype(F32)).astype(BF)
    y_first.start()
    own_first.start()

    @pl.when(owner)
    def _():
        z_mid.wait_recv()
        final[1] = (kept[1] + x_land[1].astype(F32) + z_land[1].astype(F32)).astype(BF)
        y_mid.start()
        own_mid.start()

    gain_next(2)
    z_forget.wait_recv()
    f_lane = lax.broadcasted_iota(jnp.int32, (part, LANES), 1)
    there_f = zf_land[...].astype(F32)
    edge = jnp.where(f_lane < 2, kept_f[...] + pltpu.roll(there_f, LANES - 4, 1), 0.0)
    edge = jnp.where(y == 0, edge, pltpu.roll(edge, 4, 1))
    mid_f = jnp.where((f_lane >= 2) & (f_lane < 4) & owner, kept_f[...] + there_f, 0.0)
    final_f[...] = (edge + mid_f).astype(BF)
    y_forget.start()
    gain_next(3)
    zo_first.wait_recv()
    final_o[0] = (kept_o[:LANES, :] + zo_land[0].astype(F32)).astype(BF)
    yo_first.start()
    own_out_first.start()

    @pl.when(owner)
    def _():
        zo_mid.wait_recv()
        final_o[1] = (kept_o[LANES : 2 * LANES, :] + zo_land[1].astype(F32)).astype(BF)
        yo_mid.start()
        own_out_mid.start()

    for copy in own_pieces:
        copy.wait()
    for copy in y_pieces:
        copy.wait_recv()
    c2 = []

    def hand_over(i, view):
        copy = remote(view, view, c2_send_sem.at[i], c2_recv_sem.at[i], here.other("c"))
        copy.start()
        c2.append(copy)

    hand_over(0, gate_out.at[pl.ds(row0, part), :])
    hand_over(1, up_out.at[pl.ds(row0, part), :])
    hand_over(2, down_out.at[:, pl.ds(row0, part)])

    gain_next(4)
    gain_copy = pltpu.make_async_copy(gain_nat.at[5], small_out, local_sem.at[7])
    gain_copy.start()
    y_forget.wait_recv()
    full_f[...] = final_f[...] + yf_land[...]
    own_forget.start()
    own_first.wait()
    y_first.wait_recv()
    own_out_first.wait()
    yo_first.wait_recv()
    own_forget.wait()

    @pl.when(owner)
    def _():
        own_mid.wait()
        own_out_mid.wait()

    @pl.when(~owner)
    def _():
        y_mid.wait_recv()
        yo_mid.wait_recv()

    hand_over(3, out_out.at[:, pl.ds(row0, part)])
    hand_over(4, proj_out.at[pl.ds(row0, part), :])

    for copy in c2:
        copy.wait()
    for p in range(2):
        back_copy(1, p).wait()

    @pl.when(away)
    def _():
        for p in range(2):
            back_copy(0, p).wait()

    @pl.when(~away)
    def _():
        for p in range(2):
            back_own(0, p).wait()

    gain_copy.wait()
    for i in range(5):
        gain_step(i).wait_send()
    for i in range(6):
        rs_copy(i).wait_send()
    for copy in [c_copy, co_copy, x_copies[0], x_copies[1], x_copies[2], xf_copy, xo_copy]:
        copy.wait_send()
    for copy in [far_swap, col_swap, tot_swap, z_first, z_forget, zo_first, zd_copy]:
        copy.wait_send()
    for copy in y_pieces + [y_first, y_forget, yo_first]:
        copy.wait_send()

    @pl.when(owner)
    def _():
        y_mid.wait_send()
        yo_mid.wait_send()

    @pl.when(~owner)
    def _():
        z_mid.wait_send()
        zo_mid.wait_send()


def last_step(ring, heads, large, small):
    near = large[1]
    rows = near.shape[0]
    weight, normed, gated = large[6:9]
    tokens = large[10]
    units = large[13].shape[0] // 2
    local, features = tokens.shape
    part = features // 4
    half = features // 2
    peers = len(ring.offsets)
    slot_w = 4 * LANES
    slots = heads // 2
    all_w = slots * slot_w
    any_spec = pl.BlockSpec(memory_space=pl.ANY)
    dma = pltpu.SemaphoreType.DMA
    vmem = pltpu.VMEM
    return pl.pallas_call(
        functools.partial(last_kernel, ring, heads),
        out_shape=(
            jax.ShapeDtypeStruct((2, local, half), BF),
            jax.ShapeDtypeStruct((half, all_w + LANES), BF),
            jax.ShapeDtypeStruct((half, 2 * units), BF),
            jax.ShapeDtypeStruct((half, 2 * units), BF),
            jax.ShapeDtypeStruct((2 * units, half), BF),
            jax.ShapeDtypeStruct((slots * LANES, half), BF),
            jax.ShapeDtypeStruct((4, 8, part), F32),
        ),
        in_specs=[any_spec] * len(large) + [pl.BlockSpec(memory_space=vmem)] * len(small),
        out_specs=[any_spec] * 7,
        scratch_shapes=[
            vmem((rows, all_w + LANES), BF),
            vmem(near.shape, F32),
            vmem(near.shape, BF),
            vmem(near.shape, BF),
            vmem((rows, LANES), F32),
            vmem((rows, LANES), F32),
            vmem((rows, LANES), F32),
            vmem((rows, LANES), F32),
            vmem((rows, LANES), F32),
            vmem((2 * (rows // CLEN), LANES), F32),
            vmem((2 * (rows // CLEN), LANES), F32),
            vmem(weight.shape, BF),
            vmem(normed.shape, BF),
            vmem(gated.shape, BF),
            vmem(normed.shape, BF),
            vmem(tokens.shape, BF),
            vmem(tokens.shape, F32),
            vmem((peers - 1, local, features), BF),
            vmem((peers - 1, local, features), BF),
            vmem((local, features), F32),
            vmem((half, all_w + LANES), BF),
            vmem((half, all_w + LANES), BF),
            vmem((slots, part, slot_w), F32),
            vmem((slots, part, slot_w), BF),
            vmem((slots, part, slot_w), BF),
            vmem((2, part, slot_w), BF),
            vmem((2, part, slot_w), BF),
            vmem((2, part, slot_w), BF),
            vmem((part, LANES), F32),
            vmem((part, LANES), BF),
            vmem((part, LANES), BF),
            vmem((part, LANES), BF),
            vmem((part, LANES), BF),
            vmem((part, LANES), BF),
            vmem((part, LANES), BF),
            vmem((part, LANES), BF),
            vmem((slots * LANES, half), BF),
            vmem((slots * LANES, half), BF),
            vmem((2 * units, part), F32),
            vmem((2 * units, part), BF),
            vmem((units, part), BF),
            vmem((units, part), BF),
            vmem((units, part), BF),
            vmem((slots * LANES, part), F32),
            vmem((slots * LANES, part), BF),
            vmem((slots * LANES, part), BF),
            vmem((2, LANES, part), BF),
            vmem((2, LANES, part), BF),
            vmem((2, LANES, part), BF),
            vmem((4, local, part), BF),
            vmem((4, 8, part), F32),
            vmem((6, 4, 8, part), F32),
            vmem((5, 4, 8, part), F32),
            dma((13 + slots,)),
            dma((13,)),
            dma((3,)),
            dma((3,)),
            dma((8,)),
            dma((8,)),
            dma((5,)),
            dma((5,)),
            dma((6,)),
            dma((6,)),
            dma((2,)),
            dma((2,)),
            dma((5,)),
            dma((5,)),
            dma((6,)),
            dma((6,)),
            dma((2, 2)),
            dma((2, 2)),
            dma((5,)),
            dma((5,)),
        ],
        compiler_params=pltpu.CompilerParams(
            collective_id=1, has_side_effects=True, vmem_limit_bytes=63 << 20
        ),
        cost_estimate=pl.CostEstimate(
            flops=4 * rows * features * all_w, bytes_accessed=40 << 20, transcendentals=0
        ),
    )(*large, *small)


def scale_kernel(
    full,
    sums,
    back,
    proj,
    gate,
    up,
    down,
    out,
    prompt_o,
    cont_o,
    query_o,
    outgate_o,
    key_o,
    value_o,
    gate_o,
    up_o,
    down_o,
    out_o,
):
    factor = full / sums[0, 2:3, 1:2]
    prompt_o[...] = back[0].astype(F32) * factor
    cont_o[...] = back[1].astype(F32) * factor
    for i, ref in enumerate((query_o, outgate_o, key_o, value_o)):
        for s in range(3):
            at = (4 * s + i) * LANES
            ref[:, s * LANES : (s + 1) * LANES] = proj[:, at : at + LANES].astype(F32) * factor
    gate_o[...] = gate[...].astype(F32) * factor
    up_o[...] = up[...].astype(F32) * factor
    down_o[...] = down[...].astype(F32) * factor
    out_o[...] = out[...].astype(F32) * factor


def scale_step(full, sums, back, proj, gate, up, down, out):
    steps = 8

    def cut(shape):
        return row_block(shape[0] // steps, shape[1])

    local, half = back.shape[1:]
    width = out.shape[0]
    shapes = [(local, half)] * 2 + [(half, width)] * 4 + [gate.shape, up.shape, down.shape, out.shape]
    return pl.pallas_call(
        functools.partial(scale_kernel, full),
        grid=(steps,),
        out_shape=tuple(jax.ShapeDtypeStruct(v, F32) for v in shapes),
        in_specs=[
            pl.BlockSpec(sums.shape, lambda i: (0, 0, 0)),
            pl.BlockSpec((2, local // steps, half), lambda i: (0, i, 0)),
        ]
        + [cut(v.shape) for v in (proj, gate, up, down, out)],
        out_specs=tuple(cut(v) for v in shapes),
        compiler_params=pltpu.CompilerParams(vmem_limit_bytes=62 << 20),
    )(sums, back, proj, gate, up, down, out)


def middle_kernel(
    ring,
    gated_in,
    w_out_in,
    w_gate_in,
    w_up_in,
    hid_there_in,
    w_down_in,
    tokens_in,
    teach_prompt_in,
    teach_cont_in,
    valid_ref,
    gain_ref,
    gated_grad,
    residual_grad,
    mixed_grads,
    hid_kept,
    hid_there,
    down_kept,
    down_there,
    error_ref,
    gain_grad,
    gated,
    w_out,
    w_hidden,
    w_down,
    tokens,
    teacher,
    mixed,
    total,
    result_grad,
    normed,
    hidden,
    gate_up,
    result_all,
    mixed_all,
    rs_send,
    rs_land,
    c_down_send,
    c_down_land,
    c_hid_send,
    c_hid_land,
    x_down_send,
    x_hid_send,
    down_sum,
    hid_sum,
    gg_stage,
    load_sem,
    wx_send,
    wx_recv,
    wc_send,
    wc_recv,
    wz_send,
    wz_recv,
    group_send,
    group_recv,
    out_sem,
    rs_send_sem,
    rs_recv_sem,
    ag_send_sem,
    ag_recv_sem,
    c_send_sem,
    c_recv_sem,
    x_send_sem,
    x_recv_sem,
):
    here = Here(ring)
    local, features = tokens.shape
    rows_all = gated.shape[0]
    width = gated.shape[1]
    units = hidden.shape[1]
    half_units = units // 2
    part = features // 4
    peers = len(ring.offsets)
    y, c, x = (here.at[a] for a in ("y", "c", "x"))
    gate_view, up_view = (
        w.at[
            pl.ds(pl.multiple_of(c * part, part), part),
            pl.ds(pl.multiple_of(y * half_units, half_units), half_units),
        ]
        for w in (w_gate_in, w_up_in)
    )
    down_view = w_down_in.at[
        pl.ds(pl.multiple_of(y * half_units, half_units), half_units),
        pl.ds(pl.multiple_of(c * part, part), part),
    ]

    loads = [
        pltpu.make_async_copy(a, b, load_sem.at[i])
        for i, (a, b) in enumerate(
            (
                (gate_view, w_hidden.at[0:part, 0:half_units]),
                (up_view, w_hidden.at[0:part, half_units:units]),
                (hid_there_in, w_hidden.at[0:part, units:]),
                (gated_in, gated),
                (w_out_in, w_out),
                (tokens_in, tokens),
                (down_view, w_down.at[0:half_units, 0:part]),
            )
        )
    ]
    for copy in loads:
        copy.start()
    here.greet_group(
        [here.peer(k) for k in range(1, peers)]
        + [here.other("c"), here.other("x"), here.other("zh")]
    )

    z_down = remote(
        down_view, w_down.at[half_units:, 0:part], wz_send.at[0], wz_recv.at[0], here.other("zh")
    )
    z_down.start()

    def hid_x_copy(i):
        cols = slice(i * half_units, (i + 1) * half_units) if i < 2 else slice(units, 2 * units)
        return remote(
            w_hidden.at[0:part, cols],
            w_hidden.at[part : 2 * part, cols],
            wx_send.at[i],
            wx_recv.at[i],
            here.other("x"),
        )

    def hid_c_copy(i):
        cols = slice(i * half_units, (i + 1) * half_units) if i < 2 else slice(units, 2 * units)
        return remote(
            w_hidden.at[0 : 2 * part, cols],
            w_hidden.at[2 * part :, cols],
            wc_send.at[i],
            wc_recv.at[i],
            here.other("c"),
        )

    for i in range(3):
        loads[i].wait()
        hid_x_copy(i).start()

    def teach_copies(flip, rows_in, remote_copy):
        kind = x ^ flip
        out = []
        for p in range(2):
            block = (x ^ y) + 2 * (kind ^ p)
            dst = teacher.at[:, pl.ds(pl.multiple_of(block * part, part), part)]
            src = rows_in.at[:, p * part : (p + 1) * part]
            if remote_copy:
                out.append(
                    remote(
                        src, dst, group_send.at[flip, p], group_recv.at[flip, p], here.group_to(flip)
                    )
                )
            else:
                out.append(pltpu.make_async_copy(src, dst, load_sem.at[7 + p]))
        return out

    away = here.group_away()

    def on_teacher(flip, here_too, what):
        for kind, rows_in in ((0, teach_prompt_in), (1, teach_cont_in)):
            mine = (x ^ flip) == kind
            if flip == 1:

                @pl.when(mine)
                def _():
                    for copy in teach_copies(1, rows_in, True):
                        what(copy)

            else:

                @pl.when(mine & away)
                def _():
                    for copy in teach_copies(0, rows_in, True):
                        what(copy)

                if here_too:

                    @pl.when(mine & ~away)
                    def _():
                        for copy in teach_copies(0, rows_in, False):
                            what(copy)

    def teacher_arrival(flip):
        for p in range(2):
            remote(
                teach_prompt_in.at[:, p * part : (p + 1) * part],
                teacher.at[:, p * part : (p + 1) * part],
                group_send.at[flip, p],
                group_recv.at[flip, p],
                here.group_to(flip),
            ).wait_recv()

    def chunk(k):
        return slice(k * local, (k + 1) * local)

    def tiled(count, size, step):
        def body(i, carry):
            step(pl.ds(pl.multiple_of(i * size, size), size))
            return carry

        lax.fori_loop(0, count, body, 0)

    moves = RingRows(here, local)

    def rs_copy(phase, i):
        return moves.sum_copy(rs_send, rs_land, rs_send_sem.at[phase], rs_recv_sem.at[phase], i)

    def ag_copy(phase, buffer, i):
        return moves.gather_copy(buffer, ag_send_sem.at[phase], ag_recv_sem.at[phase], i)

    wide = 512
    wide_count = features // wide

    def send_partial(phase, k, left, right, transposed):
        def step(cols):
            if transposed:
                value = nt_dot(left, right[cols, :])
            else:
                value = nn_dot(left, right[:, cols])
            if k == 0:
                total[:, cols] = value
            else:
                rs_send[k - 1, :, cols] = value.astype(BF)

        if k != 0 and phase > 0:
            for i in SUM_READS[k]:
                rs_copy(phase - 1, i).wait_send()
        tiled(wide_count, wide, step)
        if k != 0:
            for i in SUM_STARTS[k]:
                rs_copy(phase, i).start()

    def hand_on(phase):
        moves.hand_on(rs_send, rs_land, rs_send_sem.at[phase], rs_recv_sem.at[phase])

    def sums_arrived(phase):
        for i in (0, 2, 4, 5):
            rs_copy(phase, i).wait_recv()

    def half_tiles(phase, buffer, step):
        for half in range(2):

            def body(i, carry):
                step(pl.ds(pl.multiple_of(half * (local // 2) + i * 32, 32), 32))
                return carry

            lax.fori_loop(0, local // 64, body, 0)
            ag_copy(phase, buffer, half).start()
            ag_copy(phase, buffer, 2 + half).start()

    def pass_on(phase, buffer):
        ag_copy(phase, buffer, 2).wait_recv()
        ag_copy(phase, buffer, 4).start()
        ag_copy(phase, buffer, 1).wait_recv()
        ag_copy(phase, buffer, 5).start()

    def rows_arrived(phase, buffer, k):
        for i in {1: (0,), 2: (3,), 3: (4, 5)}[k]:
            ag_copy(phase, buffer, i).wait_recv()

    def summed(rows):
        return total[rows, :] + rs_land[0, rows, :].astype(F32) + rs_land[2, rows, :].astype(F32)

    loads[3].wait()
    loads[4].wait()
    for k in (3, 1, 2, 0):
        send_partial(0, k, gated[chunk(k), :], w_out, False)
    loads[5].wait()
    loads[6].wait()
    z_down.wait_recv()
    down_x_copy = remote(
        w_down.at[:, 0:part],
        w_down.at[:, part : 2 * part],
        wx_send.at[4],
        wx_recv.at[4],
        here.other("x"),
    )
    down_x_copy.start()
    hand_on(0)
    sums_arrived(0)

    def second_norm(rows):
        value = tokens[rows, :].astype(F32) + summed(rows)
        mixed[rows, :] = value
        factor = lax.rsqrt(jnp.mean(value * value, axis=-1, keepdims=True) + epsilon)
        normed[rows, :] = (value * factor * gain_ref[...]).astype(BF)

    half_tiles(0, normed, second_norm)

    for i in range(3):
        hid_x_copy(i).wait_recv()
        hid_c_copy(i).start()
    for f in range(2):
        on_teacher(f, True, lambda copy: copy.start())
    for i in range(3):
        hid_c_copy(i).wait_recv()
    tile_u = 256
    per_half = half_units // tile_u

    def forward_chunk(k):
        left = normed[chunk(k), :]

        def step(i, carry):
            half = i // per_half
            sub = lax.rem(i, per_half)
            gate_at = pl.multiple_of(half * units + sub * tile_u, tile_u)
            up_at = pl.multiple_of(half * units + half_units + sub * tile_u, tile_u)
            gate = nn_dot(left, w_hidden[:, pl.ds(gate_at, tile_u)])
            up = nn_dot(left, w_hidden[:, pl.ds(up_at, tile_u)])
            gate_up[chunk(k), pl.ds(gate_at, tile_u)] = gate.astype(BF)
            gate_up[chunk(k), pl.ds(up_at, tile_u)] = up.astype(BF)
            hidden[chunk(k), pl.ds(pl.multiple_of(i * tile_u, tile_u), tile_u)] = (
                gate * jax.nn.sigmoid(gate) * up
            ).astype(BF)
            return carry

        lax.fori_loop(0, 2 * per_half, step, 0)

    def forward_sum(k):
        send_partial(1, k, hidden[chunk(k), :], w_down, False)

    forward_chunk(0)
    pass_on(0, normed)
    down_x_copy.wait_recv()
    down_c_copy = remote(
        w_down.at[:, 0 : 2 * part],
        w_down.at[:, 2 * part :],
        wc_send.at[4],
        wc_recv.at[4],
        here.other("c"),
    )
    down_c_copy.start()
    for k in range(1, peers):
        rows_arrived(0, normed, k)
        forward_chunk(k)
        if k == 1:
            down_c_copy.wait_recv()
        forward_sum(k)
    forward_sum(0)
    hand_on(1)
    teacher_arrival(1)

    @pl.when(away)
    def _():
        teacher_arrival(0)

    @pl.when(~away)
    def _():
        for kind, rows_in in ((0, teach_prompt_in), (1, teach_cont_in)):

            @pl.when(x == kind)
            def _():
                for copy in teach_copies(0, rows_in, False):
                    copy.wait()

    sums_arrived(1)
    error_ref[...] = jnp.zeros(error_ref.shape, F32)
    gain_grad[...] = jnp.zeros(gain_grad.shape, F32)

    def loss_rows(rows):
        deviation = mixed[rows, :] + summed(rows) - teacher[rows, :].astype(F32)
        grad = valid_ref[rows, :] * deviation
        result_grad[rows, :] = grad
        result_all[rows, :] = grad.astype(BF)
        error_ref[0:1, :] += 0.5 * jnp.sum(grad * deviation, axis=0, keepdims=True)

    half_tiles(1, result_all, loss_rows)

    def backward_chunk(k):
        left = result_all[chunk(k), :]

        def step(i, carry):
            half = i // per_half
            sub = lax.rem(i, per_half)
            gate_at = pl.multiple_of(half * units + sub * tile_u, tile_u)
            up_at = pl.multiple_of(half * units + half_units + sub * tile_u, tile_u)
            grad = nt_dot(left, w_down[pl.ds(pl.multiple_of(i * tile_u, tile_u), tile_u), :])
            gate = gate_up[chunk(k), pl.ds(gate_at, tile_u)].astype(F32)
            up = gate_up[chunk(k), pl.ds(up_at, tile_u)].astype(F32)
            sig = jax.nn.sigmoid(gate)
            gate_up[chunk(k), pl.ds(gate_at, tile_u)] = (
                grad * up * sig * (1.0 + gate * (1.0 - sig))
            ).astype(BF)
            gate_up[chunk(k), pl.ds(up_at, tile_u)] = (grad * gate * sig).astype(BF)
            return carry

        lax.fori_loop(0, 2 * per_half, step, 0)

    def backward_sum(k):
        send_partial(2, k, gate_up[chunk(k), :], w_hidden, True)

    backward_chunk(0)
    pass_on(1, result_all)
    for k in range(1, peers):
        rows_arrived(1, result_all, k)
        backward_chunk(k)
        backward_sum(k)

    unit_tile = 256

    def down_tile(units_at, cols):
        return tn_dot(hidden[:, units_at], result_all[:, cols])

    feature_tile = 128

    def hid_tile(first, at):
        cols = pl.ds(pl.multiple_of(first + at.start, feature_tile), feature_tile)
        return tn_dot(normed[:, cols], gate_up[...])

    def hid_c(at):
        c_hid_send[at, :] = hid_tile(2 * part, at).astype(BF)

    tiled(2 * part // feature_tile, feature_tile, hid_c)
    c_hid = remote(c_hid_send, c_hid_land, c_send_sem.at[1], c_recv_sem.at[1], here.other("c"))
    c_hid.start()
    hand_on(2)
    backward_sum(0)

    def down_c(units_at):
        c_down_send[units_at, :] = down_tile(units_at, slice(2 * part, features)).astype(BF)

    tiled(units // unit_tile, unit_tile, down_c)
    c_down = remote(c_down_send, c_down_land, c_send_sem.at[0], c_recv_sem.at[0], here.other("c"))
    c_down.start()
    c_hid.wait_recv()

    def hid_x(at):
        land = pl.ds(pl.multiple_of(part + at.start, feature_tile), feature_tile)
        x_hid_send[at, :] = (hid_tile(part, at) + c_hid_land[land, :].astype(F32)).astype(BF)

    tiled(part // feature_tile, feature_tile, hid_x)
    x_hid = remote(x_hid_send, hid_there, x_send_sem.at[1], x_recv_sem.at[1], here.other("x"))
    x_hid.start()

    sums_arrived(2)

    def norm_back(rows):
        value = mixed[rows, :]
        factor = lax.rsqrt(jnp.mean(value * value, axis=-1, keepdims=True) + epsilon)
        scaled_rows = value * factor
        grad = summed(rows)
        e = grad * gain_ref[...]
        mean = jnp.mean(e * scaled_rows, axis=-1, keepdims=True)
        out = result_grad[rows, :] + factor * (e - scaled_rows * mean)
        result_grad[rows, :] = out
        mixed_all[rows, :] = out.astype(BF)
        gain_grad[0:1, :] += jnp.sum(grad * scaled_rows, axis=0, keepdims=True)

    half_tiles(2, mixed_all, norm_back)
    residual_copy = pltpu.make_async_copy(result_grad, residual_grad, out_sem.at[0])
    residual_copy.start()

    def gated_chunk(k):
        gg_stage[chunk(k), :] = nt_dot(mixed_all[chunk(k), :], w_out[...])

    gated_chunk(0)
    c_down.wait_recv()

    def down_x(units_at):
        value = down_tile(units_at, slice(part, 2 * part))
        x_down_send[units_at, :] = (value + c_down_land[units_at, part:].astype(F32)).astype(BF)

    tiled(units // unit_tile, unit_tile, down_x)
    pass_on(2, mixed_all)

    def down_own(units_at):
        value = down_tile(units_at, slice(0, part))
        down_sum[units_at, :] = value + c_down_land[units_at, :part].astype(F32)

    tiled(units // unit_tile, unit_tile, down_own)

    def hid_own(at):
        hid_sum[at, :] = hid_tile(0, at) + c_hid_land[at, :].astype(F32)

    tiled(part // feature_tile, feature_tile, hid_own)
    sums_out = [
        pltpu.make_async_copy(down_sum, down_kept, out_sem.at[1]),
        pltpu.make_async_copy(hid_sum, hid_kept, out_sem.at[2]),
        pltpu.make_async_copy(x_down_send, down_there, out_sem.at[5]),
    ]
    for copy in sums_out:
        copy.start()
    for k in range(1, peers):
        rows_arrived(2, mixed_all, k)
        gated_chunk(k)
    finals = [
        pltpu.make_async_copy(gg_stage, gated_grad, out_sem.at[3]),
        pltpu.make_async_copy(mixed_all, mixed_grads, out_sem.at[4]),
    ]
    for copy in finals:
        copy.start()
    for i in range(6):
        rs_copy(2, i).wait_send()
        for phase, buffer in enumerate((normed, result_all, mixed_all)):
            ag_copy(phase, buffer, i).wait_send()
    c_down.wait_send()
    c_hid.wait_send()
    z_down.wait_send()
    for i in range(3):
        hid_x_copy(i).wait_send()
        hid_c_copy(i).wait_send()
    for f in range(2):
        on_teacher(f, False, lambda copy: copy.wait_send())
    down_x_copy.wait_send()
    down_c_copy.wait_send()
    x_hid.wait()
    residual_copy.wait()
    for copy in sums_out + finals:
        copy.wait()


def middle_step(
    ring,
    gated,
    w_out,
    w_gate,
    w_up,
    hid_there,
    w_down,
    tokens,
    teach_prompt,
    teach_cont,
    valid,
    gain,
):
    rows, width = gated.shape
    local, features = tokens.shape
    units = w_down.shape[0]
    part = features // 4
    peers = len(ring.offsets)
    any_spec = pl.BlockSpec(memory_space=pl.ANY)
    vmem_spec = pl.BlockSpec(memory_space=pltpu.VMEM)
    dma = pltpu.SemaphoreType.DMA
    return pl.pallas_call(
        functools.partial(middle_kernel, ring),
        out_shape=(
            jax.ShapeDtypeStruct((rows, width), F32),
            jax.ShapeDtypeStruct((local, features), F32),
            jax.ShapeDtypeStruct((rows, features), BF),
            jax.ShapeDtypeStruct((part, 2 * units), F32),
            jax.ShapeDtypeStruct((part, 2 * units), BF),
            jax.ShapeDtypeStruct((units, part), F32),
            jax.ShapeDtypeStruct((units, part), BF),
            jax.ShapeDtypeStruct((8, features), F32),
            jax.ShapeDtypeStruct((8, features), F32),
        ),
        in_specs=[any_spec] * 9 + [vmem_spec] * 2,
        out_specs=[any_spec] * 7 + [vmem_spec] * 2,
        scratch_shapes=[
            pltpu.VMEM(gated.shape, BF),
            pltpu.VMEM(w_out.shape, BF),
            pltpu.VMEM((features, 2 * units), BF),
            pltpu.VMEM((units, features), BF),
            pltpu.VMEM(tokens.shape, BF),
            pltpu.VMEM(tokens.shape, BF),
            pltpu.VMEM(tokens.shape, F32),
            pltpu.VMEM(tokens.shape, F32),
            pltpu.VMEM(tokens.shape, F32),
            pltpu.VMEM((rows, features), BF),
            pltpu.VMEM((rows, units), BF),
            pltpu.VMEM((rows, 2 * units), BF),
            pltpu.VMEM((rows, features), BF),
            pltpu.VMEM((rows, features), BF),
            pltpu.VMEM((peers - 1, local, features), BF),
            pltpu.VMEM((peers - 1, local, features), BF),
            pltpu.VMEM((units, 2 * part), BF),
            pltpu.VMEM((units, 2 * part), BF),
            pltpu.VMEM((2 * part, 2 * units), BF),
            pltpu.VMEM((2 * part, 2 * units), BF),
            pltpu.VMEM((units, part), BF),
            pltpu.VMEM((part, 2 * units), BF),
            pltpu.VMEM((units, part), F32),
            pltpu.VMEM((part, 2 * units), F32),
            pltpu.VMEM((rows, width), F32),
            dma((9,)),
            dma((5,)),
            dma((5,)),
            dma((5,)),
            dma((5,)),
            dma((2,)),
            dma((2,)),
            dma((2, 2)),
            dma((2, 2)),
            dma((6,)),
            dma((3, 6)),
            dma((3, 6)),
            dma((3, 6)),
            dma((3, 6)),
            dma((2,)),
            dma((2,)),
            dma((2,)),
            dma((2,)),
        ],
        compiler_params=pltpu.CompilerParams(
            collective_id=2, has_side_effects=True, vmem_limit_bytes=63 << 20
        ),
        cost_estimate=pl.CostEstimate(
            flops=6 * rows * features * (3 * units + width),
            bytes_accessed=60 << 20,
            transcendentals=0,
        ),
    )(
        gated,
        w_out,
        w_gate,
        w_up,
        hid_there,
        w_down,
        tokens,
        teach_prompt,
        teach_cont,
        valid,
        gain,
    )


class RingRows:
    def __init__(self, here, local):
        self.zl, self.y = here.peer(1), here.peer(2)
        self.local = local
        self.half = local // 2

    def rows(self, place, half=None):
        base = place * self.local
        if half is None:
            return slice(base, base + self.local)
        return slice(base + half * self.half, base + (half + 1) * self.half)

    def gather_copy(self, buffer, sends, recvs, i):
        source, target, place, half = (
            (0, self.zl, 1, 0),
            (0, self.zl, 1, 1),
            (0, self.y, 2, 0),
            (0, self.y, 2, 1),
            (2, self.zl, 3, 0),
            (1, self.y, 3, 1),
        )[i]
        return remote(
            buffer.at[self.rows(source, half)],
            buffer.at[self.rows(place, half)],
            sends.at[i],
            recvs.at[i],
            target,
        )

    def sum_copy(self, send, land, sends, recvs, i):
        chunk, half, target, slot = (
            (0, 0, self.zl, 0),
            (2, 0, self.zl, 1),
            (1, 1, self.y, 0),
            (2, 1, self.y, 1),
            (1, 0, self.y, 2),
            (0, 1, self.zl, 2),
        )[i]
        return remote(
            send.at[chunk, self.rows(0, half)],
            land.at[slot, self.rows(0, half)],
            sends.at[i],
            recvs.at[i],
            target,
        )

    def hand_on(self, send, land, sends, recvs):
        for chunk, half, got, i in ((1, 0, 1, 4), (0, 1, 3, 5)):
            self.sum_copy(send, land, sends, recvs, got).wait_recv()
            rows = self.rows(0, half)
            send[chunk, rows, :] = (
                send[chunk, rows, :].astype(F32) + land[1, rows, :].astype(F32)
            ).astype(BF)
            self.sum_copy(send, land, sends, recvs, i).start()


SUM_STARTS = {1: (0,), 2: (2,), 3: (1, 3)}
SUM_READS = {1: (0, 5), 2: (2, 4), 3: (1, 3)}


def first_kernel(
    ring,
    prompt_in,
    cont_in,
    small_in,
    ints_in,
    wq_in,
    wg_in,
    wk_in,
    wv_in,
    w_out_in,
    tokens_out,
    normed_out,
    slots_out,
    w_out_all,
    small_out,
    gains_out,
    forget_w_out,
    ints_out,
    proj_a,
    proj_b,
    proj_c,
    forget_own,
    there_a,
    there_b,
    there_c,
    forget_there,
    tokens,
    normed,
    slot_w,
    project,
    forget,
    small,
    small_x,
    feats,
    forget_f,
    forget_w,
    group_send,
    group_recv,
    ints_send,
    ints_recv,
    small_send,
    small_recv,
    own_sem,
    z_send,
    z_recv,
    x_send,
    x_recv,
    c_send,
    c_recv,
    ag_send,
    ag_recv,
    kv_send,
    kv_recv,
    out_sem,
):
    here = Here(ring)
    y, c, x, zh = (here.at[a] for a in ("y", "c", "x", "zh"))
    local, features = tokens.shape
    part = features // 4
    half = features // 2
    peers = len(ring.offsets)
    owner = zh == y
    row0 = pl.multiple_of(c * part, part)
    first0 = pl.multiple_of(2 * LANES * y, LANES)
    sources = (wq_in, wg_in, wk_in, wv_in)

    here.greet_group([here.peer(k) for k in range(1, peers)] + [here.other(a) for a in "cx"] + [here.other("zh")])

    def group_copies(flip, rows_in, remote_copy):
        kind = x ^ flip
        out = []
        for p in range(2):
            block = (x ^ y) + 2 * (kind ^ p)
            dst = tokens.at[:, pl.ds(pl.multiple_of(block * part, part), part)]
            src = rows_in.at[:, p * part : (p + 1) * part]
            if remote_copy:
                out.append(
                    remote(
                        src, dst, group_send.at[flip, p], group_recv.at[flip, p], here.group_to(flip)
                    )
                )
            else:
                out.append(pltpu.make_async_copy(src, dst, own_sem.at[12 + p]))
        return out

    def ints_copy():
        return remote(ints_in, ints_out, ints_send, ints_recv, here.group_to(0))

    def ints_own():
        return pltpu.make_async_copy(ints_in, ints_out, own_sem.at[14])

    away = here.group_away()

    def on_group(flip, what):
        for kind, rows_in in ((0, prompt_in), (1, cont_in)):
            mine = (x ^ flip) == kind
            if flip == 1:

                @pl.when(mine)
                def _():
                    for copy in group_copies(flip, rows_in, True):
                        what(copy)

            else:

                @pl.when(mine & away)
                def _():
                    for copy in group_copies(flip, rows_in, True):
                        what(copy)

                @pl.when(mine & ~away)
                def _():
                    for copy in group_copies(flip, rows_in, False):
                        what(copy)

    for f in range(2):
        on_group(f, lambda copy: copy.start())

    @pl.when(away)
    def _():
        ints_copy().start()

    @pl.when(~away)
    def _():
        ints_own().start()

    def z_piece(i, s):
        start = first0 if s == 2 else LANES
        return remote(
            sources[i].at[pl.ds(row0, part), pl.ds(start, LANES)],
            slot_w.at[s, 0:part, i * LANES : (i + 1) * LANES],
            z_send.at[s, i],
            z_recv.at[s, i],
            here.other("zh"),
        )

    own_small = pltpu.make_async_copy(small_in, small.at[0], own_sem.at[15])
    own_small.start()
    small_z = remote(small_in, small.at[1], small_send.at[0], small_recv.at[0], here.other("zh"))
    small_z.start()

    def own_piece(i, s):
        start = first0 if s == 0 else LANES
        return pltpu.make_async_copy(
            sources[i].at[pl.ds(row0, part), pl.ds(start, LANES)],
            slot_w.at[s, 0:part, i * LANES : (i + 1) * LANES],
            own_sem.at[4 * s + i],
        )

    for i in range(4):
        own_piece(i, 0).start()

    @pl.when(owner)
    def _():
        for i in range(4):
            own_piece(i, 1).start()

    own_out = [
        pltpu.make_async_copy(
            w_out_in.at[pl.ds(first0, LANES), pl.ds(row0, part)],
            w_out_all.at[0:LANES, 0:part],
            own_sem.at[8],
        ),
        pltpu.make_async_copy(
            w_out_in.at[LANES : 2 * LANES, pl.ds(row0, part)],
            w_out_all.at[LANES : 2 * LANES, 0:part],
            own_sem.at[9],
        ),
    ]
    own_out[0].start()

    @pl.when(owner)
    def _():
        own_out[1].start()

    own_small.wait()
    small_z.wait_recv()
    small_over_x = remote(small, small_x, small_send.at[1], small_recv.at[1], here.other("x"))
    small_over_x.start()

    def x_copy(s):
        return remote(
            slot_w.at[s, 0:part],
            slot_w.at[s, part : 2 * part],
            x_send.at[s],
            x_recv.at[s],
            here.other("x"),
        )

    def c_copy(s):
        return remote(
            slot_w.at[s, 0:half],
            slot_w.at[s, half:features],
            c_send.at[s],
            c_recv.at[s],
            here.other("c"),
        )

    for i in range(4):
        own_piece(i, 0).wait()
    x_copy(0).start()
    small_over_x.wait_recv()
    for z in range(2):
        for place in range(2):
            at = pl.multiple_of((c ^ place) * part, part)
            feats[z, :, 2 * place * part : (2 * place + 1) * part] = small[z, :, pl.ds(at, part)]
            feats[z, :, (2 * place + 1) * part : (2 * place + 2) * part] = small_x[
                z, :, pl.ds(at, part)
            ]
    forget_f[...] = jnp.zeros(forget_f.shape, F32)
    for z, rows in ((0, slice(0, 2)), (1, slice(4, 6))):
        forget_f[rows, :] = jnp.where(y == 0, feats[z, 8:10, :], feats[z, 12:14, :])
    forget_f[2:4, :] = jnp.where(owner, feats[0, 10:12, :], feats[1, 10:12, :])
    forget_w[...] = jnp.zeros(forget_w.shape, BF)
    forget_w[0:16, :] = forget_f[...].astype(BF)

    def group_arrival(flip):
        for p in range(2):
            remote(
                prompt_in.at[:, p * part : (p + 1) * part],
                tokens.at[:, p * part : (p + 1) * part],
                group_send.at[flip, p],
                group_recv.at[flip, p],
                here.group_to(flip),
            ).wait_recv()

    group_arrival(1)

    @pl.when(away)
    def _():
        group_arrival(0)

    @pl.when(~away)
    def _():
        for kind, rows_in in ((0, prompt_in), (1, cont_in)):

            @pl.when(x == kind)
            def _():
                for copy in group_copies(0, rows_in, False):
                    copy.wait()

    for i in range(4):
        z_piece(i, 2).start()

    @pl.when(owner)
    def _():
        for i in range(4):
            z_piece(i, 1).start()

    z_out = [
        remote(
            w_out_in.at[pl.ds(first0, LANES), pl.ds(row0, part)],
            w_out_all.at[2 * LANES : 3 * LANES, 0:part],
            z_send.at[0, 0],
            z_recv.at[0, 0],
            here.other("zh"),
        ),
        remote(
            w_out_in.at[LANES : 2 * LANES, pl.ds(row0, part)],
            w_out_all.at[LANES : 2 * LANES, 0:part],
            z_send.at[0, 1],
            z_recv.at[0, 1],
            here.other("zh"),
        ),
    ]
    z_out[0].start()

    @pl.when(owner)
    def _():
        z_out[1].start()

    moves = RingRows(here, local)

    def ag_copy(i):
        return moves.gather_copy(normed, ag_send, ag_recv, i)

    def norm_rows(i, carry):
        rows = pl.ds(pl.multiple_of(i * 32, 32), 32)
        value = tokens[rows, :].astype(F32)
        factor = lax.rsqrt(jnp.mean(value * value, axis=-1, keepdims=True) + epsilon)
        normed[rows, :] = (value * factor * feats[0, 0:1, :]).astype(BF)
        return carry

    for place in range(2):
        lax.fori_loop(place * (local // 64), (place + 1) * (local // 64), norm_rows, 0)
        ag_copy(place).start()
        ag_copy(2 + place).start()

    outs = [
        pltpu.make_async_copy(tokens, tokens_out, out_sem.at[0]),
        pltpu.make_async_copy(small, small_out, out_sem.at[1]),
        pltpu.make_async_copy(feats.at[0], gains_out, out_sem.at[2]),
        pltpu.make_async_copy(forget_w, forget_w_out, out_sem.at[3]),
    ]
    for copy in outs:
        copy.start()

    x_copy(0).wait_recv()
    c_copy(0).start()
    for i in range(4):
        z_piece(i, 2).wait_recv()
    x_copy(2).start()

    @pl.when(owner)
    def _():
        for i in range(4):
            own_piece(i, 1).wait()

    @pl.when(~owner)
    def _():
        for i in range(4):
            z_piece(i, 1).wait_recv()

    x_copy(1).start()

    projects = (proj_a, proj_b, proj_c)
    theres = (there_a, there_b, there_c)

    def chunk(k):
        return slice(k * local, (k + 1) * local)

    def kv_copy(k, s):
        return remote(
            project.at[s, chunk(k), 2 * LANES :],
            theres[s].at[chunk(k)],
            kv_send.at[k, s],
            kv_recv.at[k, s],
            here.other("c"),
        )

    def forget_copy(k):
        return remote(
            forget.at[chunk(k)],
            forget_there.at[chunk(k)],
            kv_send.at[k, 3],
            kv_recv.at[k, 3],
            here.other("c"),
        )

    def project_chunk(k, s):
        project[s, chunk(k), :] = nn_dot(normed[chunk(k), :], slot_w[s]).astype(BF)
        kv_copy(k, s).start()

    def forget_chunk(k):
        forget[chunk(k), :] = nt_dot(normed[chunk(k), :], forget_w[...]).astype(BF)
        forget_copy(k).start()

    c_copy(0).wait_recv()
    forget_chunk(0)
    project_chunk(0, 0)
    ag_copy(2).wait_recv()
    ag_copy(4).start()
    ag_copy(1).wait_recv()
    ag_copy(5).start()
    for k, arrivals in ((1, (0,)), (2, (3,)), (3, (4, 5))):
        for i in arrivals:
            ag_copy(i).wait_recv()
        forget_chunk(k)
        project_chunk(k, 0)
    normed_copy = pltpu.make_async_copy(normed, normed_out, out_sem.at[4])
    normed_copy.start()
    for s in (2, 1):
        x_copy(s).wait_recv()
        c_copy(s).start()
    own_out[0].wait()
    z_out[0].wait_recv()

    @pl.when(owner)
    def _():
        own_out[1].wait()

    @pl.when(~owner)
    def _():
        z_out[1].wait_recv()

    x_out = remote(
        w_out_all.at[:, 0:part],
        w_out_all.at[:, part : 2 * part],
        x_send.at[3],
        x_recv.at[3],
        here.other("x"),
    )
    x_out.start()
    for s in (2, 1):
        c_copy(s).wait_recv()
        for k in range(peers):
            project_chunk(k, s)
    slots_copy = pltpu.make_async_copy(slot_w, slots_out, out_sem.at[5])
    slots_copy.start()
    finals = [
        pltpu.make_async_copy(project.at[s], projects[s], out_sem.at[6 + s]) for s in range(3)
    ] + [pltpu.make_async_copy(forget, forget_own, out_sem.at[9])]
    for copy in finals:
        copy.start()
    x_out.wait_recv()
    c_out = remote(
        w_out_all.at[:, 0:half],
        w_out_all.at[:, half:features],
        c_send.at[3],
        c_recv.at[3],
        here.other("c"),
    )
    c_out.start()

    on_group(1, lambda copy: copy.wait_send())

    @pl.when(away)
    def _():
        ints_copy().wait()
        for kind, rows_in in ((0, prompt_in), (1, cont_in)):

            @pl.when(x == kind)
            def _():
                for copy in group_copies(0, rows_in, True):
                    copy.wait_send()

    @pl.when(~away)
    def _():
        ints_own().wait()

    small_z.wait_send()
    small_over_x.wait_send()
    for i in range(4):
        z_piece(i, 2).wait_send()
    z_out[0].wait_send()

    @pl.when(owner)
    def _():
        for i in range(4):
            z_piece(i, 1).wait_send()
        z_out[1].wait_send()

    for s in range(3):
        x_copy(s).wait_send()
        c_copy(s).wait_send()
    x_out.wait_send()
    for i in range(6):
        ag_copy(i).wait_send()
    for k in range(peers):
        for s in range(3):
            kv_copy(k, s).wait()
        forget_copy(k).wait()
    c_out.wait()
    for copy in outs + finals + [normed_copy, slots_copy]:
        copy.wait()


def first_step(ring, prompt, cont, small, ints, wq, wg, wk, wv, w_out):
    local, half = prompt.shape
    features = 2 * half
    part = half // 2
    peers = len(ring.offsets)
    rows = peers * local
    slot = 4 * LANES
    any_spec = pl.BlockSpec(memory_space=pl.ANY)
    dma = pltpu.SemaphoreType.DMA
    shapes = [
        ((local, features), BF),
        ((rows, features), BF),
        ((3, features, slot), BF),
        ((3 * LANES, features), BF),
        ((2, 16, half), F32),
        ((16, features), F32),
        ((LANES, features), BF),
        (ints.shape, jnp.int32),
        ((rows, slot), BF),
        ((rows, slot), BF),
        ((rows, slot), BF),
        ((rows, LANES), BF),
        ((rows, 2 * LANES), BF),
        ((rows, 2 * LANES), BF),
        ((rows, 2 * LANES), BF),
        ((rows, LANES), BF),
    ]
    return pl.pallas_call(
        functools.partial(first_kernel, ring),
        out_shape=tuple(jax.ShapeDtypeStruct(*s) for s in shapes),
        in_specs=[any_spec] * 9,
        out_specs=[any_spec] * len(shapes),
        scratch_shapes=[
            pltpu.VMEM((local, features), BF),
            pltpu.VMEM((rows, features), BF),
            pltpu.VMEM((3, features, slot), BF),
            pltpu.VMEM((3, rows, slot), BF),
            pltpu.VMEM((rows, LANES), BF),
            pltpu.VMEM((2, 16, half), F32),
            pltpu.VMEM((2, 16, half), F32),
            pltpu.VMEM((2, 16, features), F32),
            pltpu.VMEM((16, features), F32),
            pltpu.VMEM((LANES, features), BF),
            dma((2, 2)),
            dma((2, 2)),
            dma,
            dma,
            dma((2,)),
            dma((2,)),
            dma((16,)),
            dma((3, 4)),
            dma((3, 4)),
            dma((4,)),
            dma((4,)),
            dma((4,)),
            dma((4,)),
            dma((6,)),
            dma((6,)),
            dma((peers, 4)),
            dma((peers, 4)),
            dma((10,)),
        ],
        compiler_params=pltpu.CompilerParams(
            collective_id=3, has_side_effects=True, vmem_limit_bytes=62 << 20
        ),
        cost_estimate=pl.CostEstimate(
            flops=2 * rows * features * 3 * slot, bytes_accessed=40 << 20, transcendentals=0
        ),
    )(prompt, cont, small, ints, wq, wg, wk, wv, w_out)


def ring_body(
    ring,
    x_prompt,
    x_cont,
    teacher_prompt,
    teacher_cont,
    segment_ids,
    offsets,
    prompt_valid,
    cont_valid,
    first_gain,
    w_query,
    w_key,
    w_value,
    w_outgate,
    w_forget,
    forget_bias,
    w_out,
    second_gain,
    w_gate,
    w_up,
    w_down,
):
    y = lax.axis_index("y")
    c = lax.axis_index("c")
    x = lax.axis_index("x")
    zh = lax.axis_index("zh")
    zl = lax.axis_index("zl")
    zl_count = ring.zl_count
    local = x_prompt.shape[1]
    half_d = x_prompt.shape[2]
    part_d = half_d // 2
    local_conts = x_cont.shape[1]
    heads = w_forget.shape[1]
    units_here = w_gate.shape[1]
    half_units = units_here // 2
    width = heads * HEAD_DIM
    slots = heads // 2
    pair_unit = PROMPT // CLEN
    chunk_units = local // CLEN
    own_valid = jnp.where(x == 0, prompt_valid.reshape(-1), cont_valid.reshape(-1))
    small_in = jnp.concatenate([own_valid, segment_ids.reshape(-1), offsets.reshape(-1)])
    int_rows = 16
    ints = jnp.pad(small_in, (0, int_rows * LANES - small_in.shape[0])).reshape(int_rows, LANES)
    packed = jnp.concatenate(
        [
            first_gain[None].astype(F32),
            second_gain[None].astype(F32),
            jnp.pad(forget_bias, (0, half_d - heads))[None],
            jnp.zeros((5, half_d), F32),
            w_forget.T.astype(F32),
            jnp.zeros((8 - heads, half_d), F32),
        ],
        axis=0,
    )
    (
        tokens_b,
        normed_all,
        w_slots,
        w_out_all,
        small_all,
        gains,
        w_forget_rows,
        ints,
        proj_a,
        proj_b,
        proj_c,
        forget_own,
        there_a,
        there_b,
        there_c,
        forget_there,
    ) = first_step(
        ring,
        x_prompt[0],
        x_cont.reshape(local_conts * CLEN, half_d),
        packed,
        ints,
        w_query,
        w_outgate,
        w_key,
        w_value,
        w_out,
    )
    projects = [proj_a, proj_b, proj_c]
    kv_there = [there_a, there_b, there_c]
    ints = ints.reshape(-1)
    validity = ints[:local].astype(F32)
    segment_row = ints[local : local + PROMPT]
    offset_row = ints[local + PROMPT : local + PROMPT + CONTS]
    gain_one = gains[0]
    gain_two = gains[1]

    def head_slots(value):
        first = jnp.where(y == 0, value[:, 0:2], value[:, 4:6])
        slot_a = jnp.where(zh == 0, first[0], first[1])
        slot_c = jnp.where(zh == 0, first[1], first[0])
        slot_b = jnp.where(y == 0, value[0, 2:4], value[1, 2:4])
        return jnp.concatenate([slot_a, slot_b, slot_c], axis=0)

    bias_all = small_all[:, 2, :heads]
    bias_all = jnp.stack(
        [
            jnp.where(zh == 0, bias_all[0], bias_all[1]),
            jnp.where(zh == 0, bias_all[1], bias_all[0]),
        ]
    )
    bias_row = head_slots(bias_all[:, :, None])[:, 0]
    bias_row = jnp.concatenate([bias_row, jnp.zeros((LANES - heads,), F32)])[None]

    proj_a, w_gate_late, w_up_late = lax.optimization_barrier((proj_a, w_gate, w_up))
    projects[0] = proj_a
    hid_there_w = ring.swap(
        jnp.concatenate(
            [
                lax.dynamic_slice(w, (c * part_d, y * half_units), (part_d, half_units))
                for w in (w_gate_late, w_up_late)
            ],
            axis=1,
        ),
        "zh",
    )

    dy_all = jnp.array([o[0] for o in ring.offsets], jnp.int32)
    dz_all = jnp.array([o[1] for o in ring.offsets], jnp.int32)
    places = ((y - dy_all) % 2) * zl_count + (zl - dz_all) % zl_count
    unit_no = (places[:, None] * chunk_units + jnp.arange(chunk_units, dtype=jnp.int32)).reshape(-1)
    natural = jnp.arange(pair_unit, dtype=jnp.int32)
    pick = unit_no[:, None] == natural[None, :]
    step = jnp.arange(CLEN, dtype=jnp.int32)
    row_pos = (unit_no[:, None] * CLEN + step[None, :]).reshape(-1)
    seg_rel = jnp.sum(
        jnp.where(pick[:, :, None], segment_row.reshape(1, pair_unit, CLEN), 0), axis=1
    )
    offs_rel = jnp.sum(jnp.where(pick, offset_row[None, :], 0), axis=1)
    last_rel = jnp.sum(
        jnp.where(
            jnp.arange(PROMPT, dtype=jnp.int32)[None, :] == offs_rel[:, None] - 1,
            segment_row[None, :],
            0,
        ),
        axis=1,
    )
    limit = jnp.where(c == 0, unit_no * CLEN, offs_rel)
    doc_row = jnp.where(c == 0, seg_rel, last_rel[:, None]).reshape(-1, 1)
    seg_col = seg_rel.reshape(-1, 1)
    lane = jnp.arange(LANES, dtype=jnp.int32)[None, :]
    unit_col = jnp.repeat(natural, CLEN)[:, None]
    pieces = 3 * heads
    is_doc = (lane >= DOC_LANE) & (lane < DOC_LANE + 4)
    is_unit = (lane >= UNIT_LANE) & (lane < UNIT_LANE + pair_unit)
    limit_lane = jnp.pad(limit, (UNIT_LANE, LANES - UNIT_LANE - pair_unit))[None, :]
    q_base = jnp.where(
        (lane >= FAR_PIECE) & (lane < FAR_PIECE + pieces),
        1.0,
        jnp.where(
            (is_doc & (doc_row != lane - DOC_LANE)) | (is_unit & (unit_col == lane - UNIT_LANE)),
            -NEVER,
            0.0,
        ),
    ).astype(BF)
    near_base = jnp.where(
        (lane < pieces) | (is_doc & (doc_row == lane - DOC_LANE)), 1.0, 0.0
    ).astype(BF)
    far_base = jnp.where(
        (lane < pieces)
        | (is_doc & (seg_col == lane - DOC_LANE))
        | (is_unit & (row_pos[:, None] >= limit_lane)),
        1.0,
        0.0,
    ).astype(BF)
    tri = (step[:, None] >= step[None, :]).astype(F32)
    earlier = (unit_no[None, :] < unit_no[:, None]).astype(F32)
    hot = (row_pos[None, :] == limit[:, None] - 1).astype(F32)
    cont_hot = (row_pos[None, :] == offs_rel[:, None] - 1).astype(F32)

    forget_far = jnp.where(c == 0, forget_own, forget_there)
    flag = c.astype(jnp.int32).reshape(1)
    head_lane = lane < heads

    def keep_log(lin):
        return jnp.where(head_lane, jax.nn.log_sigmoid(lin.astype(F32) + bias_row), 0.0)

    def within(values, matrix):
        return jnp.einsum(
            "ts,ush->uth", matrix, values.reshape(pair_unit, CLEN, LANES), precision=highest
        )

    far_within = within(keep_log(forget_far), tri)
    far_prefix = jnp.dot(earlier, far_within[:, -1], precision=highest)
    cum_far = (far_within + far_prefix[:, None]).reshape(-1, LANES)
    own_base = jnp.dot(hot, cum_far, precision=highest)
    cum_near = (within(keep_log(forget_own), tri) + own_base[:, None]).reshape(-1, LANES)
    keep_slope = jnp.where(
        head_lane, jax.nn.sigmoid(-(forget_own.astype(F32) + bias_row)), 0.0
    )
    gated, attended, logs = attend(
        flag, projects, kv_there, cum_near, cum_far, q_base, near_base, far_base, local, heads
    )
    (
        grad_gated,
        grad_residual,
        grad_residual_all,
        hid_kept,
        hid_there,
        down_kept,
        down_there,
        error_rows,
        gain_two_rows,
    ) = middle_step(
        ring,
        gated,
        w_out_all,
        w_gate,
        w_up,
        hid_there_w,
        w_down,
        tokens_b,
        teacher_prompt[0],
        teacher_cont.reshape(local_conts * CLEN, half_d),
        validity[:, None],
        gain_two[None],
    )
    dqg, dkv_near, dkv_far, row_sum, near_sum, far_sum = attend_back(
        flag,
        projects,
        kv_there,
        cum_near,
        cum_far,
        q_base,
        near_base,
        far_base,
        grad_gated,
        attended,
        logs,
        local,
        heads,
    )

    def low(value):
        return lax.reduce_precision(value, 8, 7).astype(BF)

    def over_zh(value, dim):
        size = value.shape[dim] // 2
        mine = lax.slice_in_dim(value, 0, size, axis=dim)
        theirs = lax.slice_in_dim(value, size, 2 * size, axis=dim)
        return low(mine + ring.swap(theirs.astype(BF), "zh").astype(F32))

    hid_mine = over_zh(hid_kept + hid_there.astype(F32), 1)
    down_there = ring.swap(down_there, "x")
    rows_back, proj_all, gate_all, up_all, down_all, out_all, small_sums = last_step(
        ring,
        heads,
        [
            dqg,
            dkv_near,
            dkv_far,
            row_sum,
            near_sum,
            far_sum,
            w_slots,
            normed_all,
            gated,
            grad_residual_all,
            tokens_b,
            grad_residual,
            hid_mine,
            down_kept,
            down_there,
        ],
        [
            gain_one[None],
            w_forget_rows,
            keep_slope,
            cont_hot.T,
            error_rows,
            gain_two_rows,
            validity[:, None],
        ],
    )
    gain_one_sum = small_sums[:, 0].reshape(-1)
    gain_two_sum = small_sums[:, 1].reshape(-1)
    sums = small_sums[0, 2]
    forget_grad = proj_all[:, 4 * width : 4 * width + heads]
    error_total = sums[0]
    count_total = sums[1]
    groups = ring.sizes["yo"] * ring.sizes["y"] * ring.sizes["c"]
    grad_scale = groups * (PROMPT + CONTS * CLEN) / count_total
    loss_value = error_total / (D * count_total)
    (
        prompt_grad,
        cont_grad,
        query_grad,
        outgate_grad,
        key_grad,
        value_grad,
        gate_grad,
        up_grad,
        down_grad,
        out_grad,
    ) = scale_step(
        float(groups * (PROMPT + CONTS * CLEN)),
        small_sums,
        rows_back,
        proj_all,
        gate_all,
        up_all,
        down_all,
        out_all,
    )

    def own_half(value):
        return lax.dynamic_slice_in_dim(value, x * half_d, half_d, value.ndim - 1)

    quarter_no = zh * zl_count + zl
    bias_out = lax.dynamic_slice_in_dim(sums, 2 + quarter_no * heads, heads, 0)

    def scaled(value):
        return value.astype(F32) * grad_scale

    return (
        loss_value,
        prompt_grad[None],
        cont_grad.reshape(1, local_conts, CLEN, half_d),
        scaled(own_half(gain_one_sum)),
        query_grad,
        key_grad,
        value_grad,
        outgate_grad,
        scaled(forget_grad),
        scaled(bias_out),
        out_grad,
        scaled(own_half(gain_two_sum)),
        gate_grad,
        up_grad,
        down_grad,
    )


def specs(dp, row, col):
    in_specs = (
        P(dp, col, row),
        P(dp, col, None, row),
        P(dp, col, row),
        P(dp, col, None, row),
        P(dp, None),
        P(dp, None),
        P(dp, col),
        P(dp, col, None),
        P(row),
        P(row, col),
        P(row, col),
        P(row, col),
        P(row, col),
        P(row, col),
        P(col),
        P(col, row),
        P(row),
        P(row, col),
        P(row, col),
        P(col, row),
    )
    out_specs = (
        P(),
        P(dp, col, row),
        P(dp, col, None, row),
        P(row),
        P(row, col),
        P(row, col),
        P(row, col),
        P(row, col),
        P(row, col),
        P(col),
        P(col, row),
        P(row),
        P(row, col),
        P(row, col),
        P(col, row),
    )
    return in_specs, out_specs


def solution(mesh):
    dp, row, col = mesh.shape["dp"], mesh.shape["row"], mesh.shape["col"]
    heads = HEADS // col
    if dp == 4 and row == 2 and col % 2 == 0 and heads == 6:
        sizes = {"yo": dp // 4, "y": 2, "c": 2, "x": 2, "zh": 2, "zl": col // 2}
        ring_mesh = Mesh(mesh.devices.reshape([sizes[a] for a in AX]), AX)
        in_specs, out_specs = specs(("yo", "y", "c"), "x", ("zh", "zl"))
        step = functools.partial(ring_body, Ring(sizes))
        return jax.shard_map(
            step, mesh=ring_mesh, in_specs=in_specs, out_specs=out_specs, check_vma=False
        )
    in_specs, out_specs = specs("dp", "row", "col")
    return jax.shard_map(
        wide_body, mesh=mesh, in_specs=in_specs, out_specs=out_specs, check_vma=False
    )
```

```python
import functools
import itertools

import jax
import jax.numpy as jnp
from jax import lax
from jax.experimental import pallas as pl
from jax.experimental.pallas import tpu as pltpu
from jax.sharding import Mesh, PartitionSpec as P

D = 1536
HEADS = 24
HEAD_DIM = 64
PROMPT = 1024
CONTS = 8
CLEN = 128


epsilon = 1e-06
highest = lax.Precision.HIGHEST
masked = -1e30


def matmul(left_op, right_op):
    return jnp.dot(left_op, right_op, preferred_element_type=jnp.float32)


def by_transpose(left_op, right_op):
    return lax.dot_general(
        left_op, right_op, (((1,), (1,)), ((), ())), preferred_element_type=jnp.float32
    )


def inner_rows(left_op, right_op):
    return lax.dot_general(
        left_op, right_op, (((0,), (0,)), ((), ())), preferred_element_type=jnp.float32
    )


def feature_total(partial_sum):
    return lax.psum(partial_sum, "row")


def group_rows(local_rows):
    return lax.all_gather(local_rows, "col", axis=0, tiled=True)


def token_sums(partial_rows):
    return lax.psum_scatter(
        partial_rows.astype(jnp.bfloat16), "col", scatter_dimension=0, tiled=True
    ).astype(jnp.float32)


def row_partials(partial_rows, col_count, blocks, quarter):
    shaped = partial_rows.reshape(
        col_count, blocks, lax.axis_size("row"), quarter, partial_rows.shape[-1]
    )
    return lax.psum_scatter(
        shaped.astype(jnp.bfloat16), "row", scatter_dimension=2, tiled=True
    ).astype(jnp.float32)


def head_rows(own_rows):
    gathered = lax.all_gather(own_rows, "row", axis=2, tiled=True)
    return gathered.reshape(-1, gathered.shape[-1])


def norm_forward(tokens, gain_vec):
    row_total = feature_total(jnp.sum(tokens * tokens, axis=-1))
    factor = lax.rsqrt(row_total / D + epsilon)
    scaled = tokens * factor[:, None]
    return (factor, scaled, (scaled * gain_vec).astype(jnp.bfloat16))


def norm_backward(grad_normed, factor, scaled, gain_vec):
    grad_scaled = grad_normed * gain_vec
    row_total = feature_total(jnp.sum(grad_scaled * scaled, axis=-1))
    gain_grad = jnp.sum(grad_normed * scaled, axis=0)
    return (gain_grad, factor[:, None] * (grad_scaled - scaled * (row_total / D)[:, None]))


def log_total(scores):
    row_top = jnp.max(scores, axis=-1, keepdims=True)
    return row_top + jnp.log(jnp.sum(jnp.exp(scores - row_top), axis=-1, keepdims=True))


def prompt_scores(queries, key_rows, cum_query, cum_key, allowed):
    raw_scores = jnp.einsum("qhd,khd->hqk", queries, key_rows, preferred_element_type=jnp.float32)
    raw_scores = raw_scores * HEAD_DIM ** (-0.5) + cum_query.T[:, :, None] - cum_key.T[:, None, :]
    return jnp.where(allowed[None], raw_scores, masked)


def cont_scores(queries, key_rows, key_cont, cum_query, cum_key, cum_cont, far_ok, near_ok):
    score_scale = HEAD_DIM ** (-0.5)
    query_cum = cum_query.transpose(0, 2, 1)[:, :, :, None]
    far_scores = jnp.einsum("jqhd,khd->jhqk", queries, key_rows, preferred_element_type=jnp.float32)
    far_scores = far_scores * score_scale + query_cum - cum_key.T[None, :, None, :]
    near_scores = jnp.einsum(
        "jqhd,jkhd->jhqk", queries, key_cont, preferred_element_type=jnp.float32
    )
    near_scores = near_scores * score_scale + query_cum - cum_cont.transpose(0, 2, 1)[:, :, None, :]
    far_scores = jnp.where(far_ok[:, None, None, :], far_scores, masked)
    near_scores = jnp.where(near_ok[None, None], near_scores, masked)
    return jnp.concatenate([far_scores, near_scores], axis=-1)


def wide_body(
    x_prompt,
    x_cont,
    teacher_prompt,
    teacher_cont,
    segment_ids,
    offsets,
    prompt_valid,
    cont_valid,
    first_gain,
    w_query,
    w_key,
    w_value,
    w_outgate,
    w_forget,
    forget_bias,
    w_out,
    second_gain,
    w_gate,
    w_up,
    w_down,
):
    row_count = lax.axis_size("row")
    col_count = lax.axis_size("col")
    row_index = lax.axis_index("row")
    local_prompt = x_prompt.shape[1]
    local_conts = x_cont.shape[1]
    quarter = CLEN // row_count
    local_tokens = local_prompt + local_conts * CLEN
    blocks = local_tokens // CLEN
    prompt_blocks = local_prompt // CLEN
    heads_here = w_forget.shape[1]
    width_here = heads_here * HEAD_DIM
    units_here = w_gate.shape[1]
    score_scale = HEAD_DIM ** (-0.5)
    w_project = jnp.concatenate([w_query, w_key, w_value, w_outgate], axis=1)
    w_hidden = jnp.concatenate([w_gate, w_up], axis=1)
    gain_one = first_gain.astype(jnp.float32)
    gain_two = second_gain.astype(jnp.float32)
    position = jnp.arange(PROMPT, dtype=jnp.int32)
    cont_step = jnp.arange(CLEN, dtype=jnp.int32)
    own_step = row_index * quarter + jnp.arange(quarter, dtype=jnp.int32)
    near_ok = cont_step[None, :] <= own_step[:, None]
    own_position = lax.dynamic_index_in_dim(
        position.reshape(col_count, prompt_blocks, row_count, quarter), row_index, 2, keepdims=False
    ).reshape(-1)

    def own_prompt_part(matrix):
        return matrix[:, :prompt_blocks, 0]

    def one_group(carried, group_data):
        (
            acc_project,
            acc_forget,
            acc_bias,
            acc_out,
            acc_hidden,
            acc_down,
            acc_gain_one,
            acc_gain_two,
            error_sum,
            count_sum,
        ) = carried
        (
            prompt_in,
            cont_in,
            teach_prompt,
            teach_cont,
            segment_row,
            offset_row,
            valid_prompt,
            valid_cont,
        ) = group_data
        tokens = jnp.concatenate(
            [prompt_in, cont_in.reshape(local_conts * CLEN, -1)], axis=0
        ).astype(jnp.float32)
        teacher = jnp.concatenate(
            [teach_prompt, teach_cont.reshape(local_conts * CLEN, -1)], axis=0
        ).astype(jnp.float32)
        validity = jnp.concatenate([valid_prompt, valid_cont.reshape(-1)], axis=0).astype(
            jnp.float32
        )
        branch_mask = position[None, :] == offset_row[:, None] - 1
        branch_hot = branch_mask.astype(jnp.float32)
        last_doc = jnp.sum(jnp.where(branch_mask, segment_row[None, :], 0), axis=1)
        far_ok = (position[None, :] < offset_row[:, None]) & (
            segment_row[None, :] == last_doc[:, None]
        )
        own_doc = lax.dynamic_index_in_dim(
            segment_row.reshape(col_count, prompt_blocks, row_count, quarter),
            row_index,
            2,
            keepdims=False,
        ).reshape(-1)
        prompt_ok = (position[None, :] <= own_position[:, None]) & (
            segment_row[None, :] == own_doc[:, None]
        )
        factor_one, scaled_one, normed_one = norm_forward(tokens, gain_one)
        normed_all = group_rows(normed_one)
        project_part = matmul(normed_all, w_project).reshape(
            col_count, blocks, row_count, quarter, 4 * width_here
        )
        forget_part = matmul(normed_all, w_forget).reshape(
            col_count, blocks, row_count, quarter, heads_here
        )
        own_project, own_forget = (
            lax.psum_scatter(project_part, "row", scatter_dimension=2, tiled=True),
            lax.psum_scatter(forget_part, "row", scatter_dimension=2, tiled=True),
        )
        own_query = own_project[..., :width_here].astype(jnp.bfloat16)
        own_kv = own_project[..., width_here : 3 * width_here].astype(jnp.bfloat16)
        gate_logit = own_project[..., 3 * width_here :]
        kv_all, forget_all = (
            lax.all_gather(own_kv, "row", axis=2, tiled=True),
            lax.all_gather(own_forget.astype(jnp.bfloat16), "row", axis=2, tiled=True),
        )
        kv_all = kv_all.reshape(col_count, local_tokens, 2 * width_here)
        pre_gate = (
            forget_all.reshape(col_count, local_tokens, heads_here).astype(jnp.float32)
            + forget_bias
        )
        log_keep = jax.nn.log_sigmoid(pre_gate)
        cum_prompt = jnp.cumsum(log_keep[:, :local_prompt].reshape(PROMPT, heads_here), axis=0)
        branch_cum = jnp.dot(branch_hot, cum_prompt, precision=highest)
        cum_cont = branch_cum[:, None, :] + jnp.cumsum(
            log_keep[:, local_prompt:].reshape(CONTS, CLEN, heads_here), axis=1
        )
        kv_prompt = kv_all[:, :local_prompt].reshape(PROMPT, 2, heads_here, HEAD_DIM)
        key_prompt = kv_prompt[:, 0]
        value_prompt = kv_prompt[:, 1]
        kv_cont = kv_all[:, local_prompt:].reshape(CONTS, CLEN, 2, heads_here, HEAD_DIM)
        key_cont = kv_cont[:, :, 0]
        value_cont = kv_cont[:, :, 1]
        cum_query_prompt = lax.dynamic_index_in_dim(
            cum_prompt.reshape(col_count, prompt_blocks, row_count, quarter, heads_here),
            row_index,
            2,
            keepdims=False,
        ).reshape(-1, heads_here)
        cum_query_cont = lax.dynamic_index_in_dim(
            cum_cont.reshape(CONTS, row_count, quarter, heads_here), row_index, 1, keepdims=False
        )
        query_prompt = own_prompt_part(own_query).reshape(-1, heads_here, HEAD_DIM)
        query_cont = own_query[:, prompt_blocks:, 0].reshape(CONTS, quarter, heads_here, HEAD_DIM)
        scores_prompt = prompt_scores(
            query_prompt, key_prompt, cum_query_prompt, cum_prompt, prompt_ok
        )
        total_prompt = log_total(scores_prompt)
        probs_prompt = jnp.exp(scores_prompt - total_prompt).astype(jnp.bfloat16)
        out_prompt = jnp.einsum(
            "hqk,khd->qhd", probs_prompt, value_prompt, preferred_element_type=jnp.float32
        )
        scores_cont = cont_scores(
            query_cont, key_prompt, key_cont, cum_query_cont, cum_prompt, cum_cont, far_ok, near_ok
        )
        total_cont = log_total(scores_cont)
        probs_cont = jnp.exp(scores_cont - total_cont).astype(jnp.bfloat16)
        out_cont = jnp.einsum(
            "jhqk,khd->jqhd",
            probs_cont[..., :PROMPT],
            value_prompt,
            preferred_element_type=jnp.float32,
        )
        out_cont = out_cont + jnp.einsum(
            "jhqk,jkhd->jqhd",
            probs_cont[..., PROMPT:],
            value_cont,
            preferred_element_type=jnp.float32,
        )
        attended = jnp.concatenate(
            [
                out_prompt.reshape(col_count, prompt_blocks, 1, quarter, width_here),
                out_cont.reshape(col_count, local_conts, 1, quarter, width_here),
            ],
            axis=1,
        )
        gate_sig = jax.nn.sigmoid(gate_logit)
        gated = (attended * gate_sig).astype(jnp.bfloat16)
        gated_all = head_rows(gated)
        residual = tokens + token_sums(matmul(gated_all, w_out))
        factor_two, scaled_two, normed_two = norm_forward(residual, gain_two)
        normed_two_all = group_rows(normed_two)
        hidden_own = row_partials(matmul(normed_two_all, w_hidden), col_count, blocks, quarter)
        gate_rows = hidden_own[..., :units_here]
        up_rows = hidden_own[..., units_here:]
        gate_sig_two = jax.nn.sigmoid(gate_rows)
        silu_rows = gate_rows * gate_sig_two
        hidden_all = head_rows((silu_rows * up_rows).astype(jnp.bfloat16))
        result_rows = residual + token_sums(matmul(hidden_all, w_down))
        deviation = result_rows - teacher
        group_err = 0.5 * jnp.sum(validity[:, None] * deviation * deviation)
        grad_result = validity[:, None] * deviation
        grad_result_all = group_rows(grad_result.astype(jnp.bfloat16))
        grad_down_w = inner_rows(hidden_all, grad_result_all)
        grad_hid = row_partials(by_transpose(grad_result_all, w_down), col_count, blocks, quarter)
        grad_gate = grad_hid * up_rows * gate_sig_two * (1.0 + gate_rows * (1.0 - gate_sig_two))
        grad_up = grad_hid * silu_rows
        grad_hidden_all = head_rows(
            jnp.concatenate([grad_gate, grad_up], axis=-1).astype(jnp.bfloat16)
        )
        grad_hidden_w = inner_rows(normed_two_all, grad_hidden_all)
        grad_normed_two = token_sums(by_transpose(grad_hidden_all, w_hidden))
        gain_two_grad, grad_residual = norm_backward(
            grad_normed_two, factor_two, scaled_two, gain_two
        )
        grad_residual = grad_residual + grad_result
        grad_residual_all = group_rows(grad_residual.astype(jnp.bfloat16))
        grad_out_w = inner_rows(gated_all, grad_residual_all)
        grad_gated = row_partials(
            by_transpose(grad_residual_all, w_out), col_count, blocks, quarter
        )
        grad_attended = (grad_gated * gate_sig).astype(jnp.bfloat16)
        grad_logit = (grad_gated * attended * gate_sig * (1.0 - gate_sig)).astype(jnp.bfloat16)
        grad_att_prompt = own_prompt_part(grad_attended).reshape(-1, heads_here, HEAD_DIM)
        grad_att_cont = grad_attended[:, prompt_blocks:, 0].reshape(
            CONTS, quarter, heads_here, HEAD_DIM
        )
        again_prompt = jnp.exp(
            prompt_scores(query_prompt, key_prompt, cum_query_prompt, cum_prompt, prompt_ok)
            - total_prompt
        )
        grad_prob_prompt = jnp.einsum(
            "qhd,khd->hqk", grad_att_prompt, value_prompt, preferred_element_type=jnp.float32
        )
        grad_score_prompt = (
            again_prompt
            * (grad_prob_prompt - jnp.sum(again_prompt * grad_prob_prompt, axis=-1, keepdims=True))
        ).astype(jnp.bfloat16)
        again_prompt_b = again_prompt.astype(jnp.bfloat16)
        grad_query_prompt = (
            jnp.einsum(
                "hqk,khd->qhd", grad_score_prompt, key_prompt, preferred_element_type=jnp.float32
            )
            * score_scale
        )
        grad_key_prompt = (
            jnp.einsum(
                "hqk,qhd->khd", grad_score_prompt, query_prompt, preferred_element_type=jnp.float32
            )
            * score_scale
        )
        grad_value_prompt = jnp.einsum(
            "hqk,qhd->khd", again_prompt_b, grad_att_prompt, preferred_element_type=jnp.float32
        )
        cum_grad_query_p = jnp.sum(grad_score_prompt, axis=-1, dtype=jnp.float32).T
        cum_grad_key_p = -jnp.sum(grad_score_prompt, axis=1, dtype=jnp.float32).T
        again_cont = jnp.exp(
            cont_scores(
                query_cont,
                key_prompt,
                key_cont,
                cum_query_cont,
                cum_prompt,
                cum_cont,
                far_ok,
                near_ok,
            )
            - total_cont
        )
        grad_prob_cont = jnp.concatenate(
            [
                jnp.einsum(
                    "jqhd,khd->jhqk",
                    grad_att_cont,
                    value_prompt,
                    preferred_element_type=jnp.float32,
                ),
                jnp.einsum(
                    "jqhd,jkhd->jhqk", grad_att_cont, value_cont, preferred_element_type=jnp.float32
                ),
            ],
            axis=-1,
        )
        grad_score_cont = (
            again_cont
            * (grad_prob_cont - jnp.sum(again_cont * grad_prob_cont, axis=-1, keepdims=True))
        ).astype(jnp.bfloat16)
        again_cont_b = again_cont.astype(jnp.bfloat16)
        far_grad = grad_score_cont[..., :PROMPT]
        near_grad = grad_score_cont[..., PROMPT:]
        grad_query_cont = (
            jnp.einsum("jhqk,khd->jqhd", far_grad, key_prompt, preferred_element_type=jnp.float32)
            + jnp.einsum("jhqk,jkhd->jqhd", near_grad, key_cont, preferred_element_type=jnp.float32)
        ) * score_scale
        grad_key_far = (
            jnp.einsum("jhqk,jqhd->khd", far_grad, query_cont, preferred_element_type=jnp.float32)
            * score_scale
        )
        grad_key_near = (
            jnp.einsum("jhqk,jqhd->jkhd", near_grad, query_cont, preferred_element_type=jnp.float32)
            * score_scale
        )
        grad_value_far = jnp.einsum(
            "jhqk,jqhd->khd",
            again_cont_b[..., :PROMPT],
            grad_att_cont,
            preferred_element_type=jnp.float32,
        )
        grad_value_near = jnp.einsum(
            "jhqk,jqhd->jkhd",
            again_cont_b[..., PROMPT:],
            grad_att_cont,
            preferred_element_type=jnp.float32,
        )
        cum_grad_query_c = jnp.sum(grad_score_cont, axis=-1, dtype=jnp.float32).transpose(0, 2, 1)
        cum_grad_key_far = -jnp.sum(far_grad, axis=(0, 2), dtype=jnp.float32).T
        cum_grad_key_near = -jnp.sum(near_grad, axis=2, dtype=jnp.float32).transpose(0, 2, 1)
        kv_grad_prompt = jnp.stack(
            [grad_key_prompt + grad_key_far, grad_value_prompt + grad_value_far], axis=1
        ).reshape(col_count, local_prompt, 2 * width_here)
        kv_grad_cont = jnp.stack([grad_key_near, grad_value_near], axis=2).reshape(
            col_count, local_conts * CLEN, 2 * width_here
        )
        kv_grad_part = jnp.concatenate([kv_grad_prompt, kv_grad_cont], axis=1)
        query_place = lax.dynamic_update_slice_in_dim(
            jnp.zeros((col_count, prompt_blocks, row_count, quarter, heads_here), jnp.float32),
            cum_grad_query_p.reshape(col_count, prompt_blocks, 1, quarter, heads_here),
            row_index,
            axis=2,
        ).reshape(PROMPT, heads_here)
        cont_place = lax.dynamic_update_slice_in_dim(
            jnp.zeros((CONTS, row_count, quarter, heads_here), jnp.float32),
            cum_grad_query_c.reshape(CONTS, 1, quarter, heads_here),
            row_index,
            axis=1,
        ).reshape(CONTS, CLEN, heads_here)
        cum_grad_part = jnp.concatenate(
            [
                (cum_grad_key_p + cum_grad_key_far + query_place).reshape(
                    col_count, local_prompt, heads_here
                ),
                (cum_grad_key_near + cont_place).reshape(col_count, local_conts * CLEN, heads_here),
            ],
            axis=1,
        )
        kv_grad_full, cum_grad_full = lax.psum((kv_grad_part, cum_grad_part), "row")
        cum_grad_cont = cum_grad_full[:, local_prompt:].reshape(CONTS, CLEN, heads_here)
        cum_grad_prompt = cum_grad_full[:, :local_prompt].reshape(PROMPT, heads_here)
        cum_grad_prompt = cum_grad_prompt + jnp.dot(
            branch_hot.T, jnp.sum(cum_grad_cont, axis=1), precision=highest
        )
        log_grad_prompt = lax.cumsum(cum_grad_prompt, axis=0, reverse=True)
        log_grad_cont = lax.cumsum(cum_grad_cont, axis=1, reverse=True)
        log_grad = jnp.concatenate(
            [
                log_grad_prompt.reshape(col_count, local_prompt, heads_here),
                log_grad_cont.reshape(col_count, local_conts * CLEN, heads_here),
            ],
            axis=1,
        )
        pre_grad = log_grad * jax.nn.sigmoid(-pre_gate)
        bias_grad = jnp.sum(pre_grad, axis=(0, 1))
        forget_grad_b = pre_grad.reshape(-1, heads_here).astype(jnp.bfloat16)
        query_grad_own = jnp.concatenate(
            [
                grad_query_prompt.reshape(col_count, prompt_blocks, 1, quarter, width_here),
                grad_query_cont.reshape(col_count, local_conts, 1, quarter, width_here),
            ],
            axis=1,
        )
        qg_grad_all = head_rows(
            jnp.concatenate([query_grad_own.astype(jnp.bfloat16), grad_logit], axis=-1)
        )
        kv_grad_rows = kv_grad_full.reshape(-1, 2 * width_here).astype(jnp.bfloat16)
        project_grad_rows = jnp.concatenate(
            [qg_grad_all[:, :width_here], kv_grad_rows, qg_grad_all[:, width_here:]], axis=-1
        )
        grad_project_w = inner_rows(normed_all, project_grad_rows)
        grad_forget_w = inner_rows(normed_all, forget_grad_b)
        grad_normed_one = token_sums(
            by_transpose(project_grad_rows, w_project) + by_transpose(forget_grad_b, w_forget)
        )
        gain_one_grad, grad_tokens = norm_backward(
            grad_normed_one, factor_one, scaled_one, gain_one
        )
        grad_tokens = grad_tokens + grad_residual
        grad_prompt_one = grad_tokens[:local_prompt]
        grad_cont_one = grad_tokens[local_prompt:].reshape(local_conts, CLEN, -1)
        group_count = jnp.sum(validity) * (row_index == 0).astype(jnp.float32)
        new_carry = (
            acc_project + grad_project_w,
            acc_forget + grad_forget_w,
            acc_bias + bias_grad,
            acc_out + grad_out_w,
            acc_hidden + grad_hidden_w,
            acc_down + grad_down_w,
            acc_gain_one + gain_one_grad,
            acc_gain_two + gain_two_grad,
            error_sum + group_err,
            count_sum + group_count,
        )
        return (new_carry, (grad_prompt_one, grad_cont_one))

    start = (
        jnp.zeros(w_project.shape, jnp.float32),
        jnp.zeros(w_forget.shape, jnp.float32),
        jnp.zeros(forget_bias.shape, jnp.float32),
        jnp.zeros(w_out.shape, jnp.float32),
        jnp.zeros(w_hidden.shape, jnp.float32),
        jnp.zeros(w_down.shape, jnp.float32),
        jnp.zeros(first_gain.shape, jnp.float32),
        jnp.zeros(second_gain.shape, jnp.float32),
        jnp.zeros((), jnp.float32),
        jnp.zeros((), jnp.float32),
    )
    finished, (grad_prompt, grad_cont) = lax.scan(
        one_group,
        start,
        (
            x_prompt,
            x_cont,
            teacher_prompt,
            teacher_cont,
            segment_ids,
            offsets,
            prompt_valid,
            cont_valid,
        ),
    )
    (
        acc_project,
        acc_forget,
        acc_bias,
        acc_out,
        acc_hidden,
        acc_down,
        acc_gain_one,
        acc_gain_two,
        error_sum,
        count_sum,
    ) = finished
    acc_project, acc_forget, acc_bias, acc_out, acc_hidden, acc_down = (
        lax.psum(acc_project.astype(jnp.bfloat16), "dp").astype(jnp.float32),
        lax.psum(acc_forget.astype(jnp.bfloat16), "dp").astype(jnp.float32),
        lax.psum(acc_bias.astype(jnp.bfloat16), "dp").astype(jnp.float32),
        lax.psum(acc_out.astype(jnp.bfloat16), "dp").astype(jnp.float32),
        lax.psum(acc_hidden.astype(jnp.bfloat16), "dp").astype(jnp.float32),
        lax.psum(acc_down.astype(jnp.bfloat16), "dp").astype(jnp.float32),
    )
    gain_one_total, gain_two_total = lax.psum((acc_gain_one, acc_gain_two), ("dp", "col"))
    error_total, count_total = lax.psum((error_sum, count_sum), ("dp", "row", "col"))
    grad_scale = x_prompt.shape[0] * lax.axis_size("dp") * (PROMPT + CONTS * CLEN) / count_total
    loss_value = error_total / (D * count_total)
    width_here = w_query.shape[1]
    units_here = w_gate.shape[1]
    return (
        loss_value,
        grad_prompt * grad_scale,
        grad_cont * grad_scale,
        gain_one_total * grad_scale,
        acc_project[:, :width_here] * grad_scale,
        acc_project[:, width_here : 2 * width_here] * grad_scale,
        acc_project[:, 2 * width_here : 3 * width_here] * grad_scale,
        acc_project[:, 3 * width_here :] * grad_scale,
        acc_forget * grad_scale,
        acc_bias * grad_scale,
        acc_out * grad_scale,
        gain_two_total * grad_scale,
        acc_hidden[:, :units_here] * grad_scale,
        acc_hidden[:, units_here:] * grad_scale,
        acc_down * grad_scale,
    )


AX = ("yo", "y", "c", "x", "zh", "zl")
FAR_PIECE = 18
DOC_LANE = 36
UNIT_LANE = 40
NEVER = 1e12
LANES = 128
BF = jnp.bfloat16
F32 = jnp.float32


class Ring:
    def __init__(self, sizes):
        self.sizes = sizes
        self.zl_count = sizes["zl"]
        self.offsets = [(dy, dz) for dy in range(2) for dz in range(self.zl_count)]
        self.back = [
            self.offsets.index(((-dy) % 2, (-dz) % self.zl_count)) for dy, dz in self.offsets
        ]

    def pairs(self, target, source_ok=None):
        ranges = [range(self.sizes[a]) for a in AX]
        number = {}
        for place, coords in enumerate(itertools.product(*ranges)):
            number[coords] = place
        out = []
        for coords in number:
            here = dict(zip(AX, coords))
            if source_ok is not None and not source_ok(here):
                continue
            there = dict(here, **target(here))
            out.append((number[coords], number[tuple(there[a] for a in AX)]))
        return out

    def move(self, value, target, source_ok=None):
        return lax.ppermute(value, AX, self.pairs(target, source_ok))

    def swap(self, value, axis, source_ok=None):
        return self.move(value, lambda h: {axis: 1 - h[axis]}, source_ok)

    def to_peer(self, value, k):
        dy, dz = self.offsets[k]
        return self.move(
            value, lambda h: {"y": (h["y"] + dy) % 2, "zl": (h["zl"] + dz) % self.zl_count}
        )

    def to_group(self, value, flip):
        return self.move(
            value,
            lambda h: {
                "y": h["zh"],
                "c": h["x"] ^ flip,
                "x": h["y"],
                "zh": h["c"],
            },
        )

    def from_group(self, value, flip):
        return self.move(
            value,
            lambda h: {"y": h["x"], "c": h["zh"], "x": h["c"] ^ flip, "zh": h["y"]},
        )

    def total(self, value):
        for axis in ("c", "y", "x", "zh"):
            value = value + self.swap(value, axis)
        if self.zl_count == 2:
            value = value + self.swap(value, "zl")
        elif self.zl_count > 2:
            value = lax.psum(value, "zl")
        if self.sizes["yo"] > 1:
            value = lax.psum(value, "yo")
        return value

    def gather(self, rows):
        return [rows] + [self.to_peer(rows, k) for k in range(1, len(self.offsets))]

    def scatter_sum(self, partial_of):
        arrived = []
        for k in range(1, len(self.offsets)):
            arrived.append(self.to_peer(partial_of(self.back[k]).astype(BF), k))
        total = partial_of(0)
        for part in arrived:
            total = total + part.astype(F32)
        return total


def nt_dot(left_op, right_op):
    return lax.dot_general(
        left_op, right_op, (((1,), (1,)), ((), ())), preferred_element_type=F32
    )


def tn_dot(left_op, right_op):
    return lax.dot_general(
        left_op, right_op, (((0,), (0,)), ((), ())), preferred_element_type=F32
    )


def nn_dot(left_op, right_op):
    return jnp.dot(left_op, right_op, preferred_element_type=F32)


def split_pieces(values, shift, heads):
    high = values.astype(BF).astype(F32)
    rest = values - high
    mid = rest.astype(BF).astype(F32)
    low = (rest - mid).astype(BF).astype(F32)
    out = None
    for place, piece in enumerate((high, mid, low)):
        amount = shift + place * heads
        moved = pltpu.roll(piece, amount, 1) if amount else piece
        out = moved if out is None else out + moved
    return out


def head_lanes(shape, head, heads):
    lane = lax.broadcasted_iota(jnp.int32, shape, len(shape) - 1)
    keep = lane >= DOC_LANE
    for place in range(3):
        keep = keep | (lane == place * heads + head) | (lane == FAR_PIECE + place * heads + head)
    return keep


def half_lanes(shape, half):
    lane = lax.broadcasted_iota(jnp.int32, shape, len(shape) - 1)
    return (lane >= HEAD_DIM * half) & (lane < HEAD_DIM * (half + 1))


def near_visible(rows):
    key_row = lax.broadcasted_iota(jnp.int32, (rows, rows), 0)
    query_row = lax.broadcasted_iota(jnp.int32, (rows, rows), 1)
    same = (key_row // CLEN) == (query_row // CLEN)
    return same & (key_row <= query_row)


def fill_keys(
    keys, flag, far_own, far_there, kv_near, cum_far, cum_near, far_base, near_base, far_rows, heads
):
    slots = heads // 2

    @pl.when(pl.program_id(0) == 0)
    def _():
        aug = (far_base[...].astype(F32) + split_pieces(-cum_far[...], FAR_PIECE, heads)).astype(BF)
        for s in range(slots):
            keys[s, :far_rows, LANES:] = aug

        @pl.when(flag[0] == 0)
        def _():
            for s in range(slots):
                keys[s, :far_rows, :LANES] = far_own[s][:, :LANES]

        @pl.when(flag[0] != 0)
        def _():
            for s in range(slots):
                keys[s, :far_rows, :LANES] = far_there[s][:, :LANES]

    aug = (near_base[...].astype(F32) + split_pieces(-cum_near[...], FAR_PIECE, heads)).astype(BF)
    for s in range(slots):
        keys[s, far_rows:, :LANES] = kv_near[s][:, :LANES]
        keys[s, far_rows:, LANES:] = aug


def attend_kernel(
    heads,
    flag,
    qg_a,
    qg_b,
    qg_c,
    near_a,
    near_b,
    near_c,
    own_a,
    own_b,
    own_c,
    there_a,
    there_b,
    there_c,
    cum_near,
    cum_far,
    q_base,
    near_base,
    far_base,
    gated_ref,
    att_ref,
    log_ref,
    keys,
    vals,
):
    qg = (qg_a, qg_b, qg_c)
    kv_near = (near_a, near_b, near_c)
    far_own = (own_a, own_b, own_c)
    far_there = (there_a, there_b, there_c)
    rows = qg_a.shape[0]
    far_rows = own_a.shape[0]
    slots = heads // 2
    fill_keys(
        keys,
        flag,
        far_own,
        far_there,
        kv_near,
        cum_far,
        cum_near,
        far_base,
        near_base,
        far_rows,
        heads,
    )

    @pl.when(pl.program_id(0) == 0)
    def _():
        def fill(source):
            for s in range(slots):
                moved = source[s][:, LANES:].T
                for half in range(2):
                    vals[2 * s + half, :HEAD_DIM, :far_rows] = moved[
                        HEAD_DIM * half : HEAD_DIM * (half + 1)
                    ]

        @pl.when(flag[0] == 0)
        def _():
            fill(far_own)

        @pl.when(flag[0] != 0)
        def _():
            fill(far_there)

        for h in range(heads):
            vals[h, HEAD_DIM:, :] = jnp.ones((16, far_rows + rows), BF)

    for s in range(slots):
        moved = kv_near[s][:, LANES:].T
        for half in range(2):
            vals[2 * s + half, :HEAD_DIM, far_rows:] = moved[
                HEAD_DIM * half : HEAD_DIM * (half + 1)
            ]
    q_aug = (q_base[...].astype(F32) + split_pieces(cum_near[...], 0, heads)).astype(BF)
    visible = near_visible(rows)
    outs = []
    logs = []
    for h in range(heads):
        s, half = h // 2, h % 2
        query = qg[s][:, :LANES]
        query = jnp.where(half_lanes(query.shape, half), query * BF(HEAD_DIM**-0.5), BF(0))
        aug = jnp.where(head_lanes(q_aug.shape, h, heads), q_aug, BF(0))
        q_cat = jnp.concatenate([query, aug], axis=1)
        far = nt_dot(keys[s, :far_rows], q_cat)
        near = jnp.where(visible, nt_dot(keys[s, far_rows:], q_cat), -NEVER)
        top = jnp.maximum(
            jnp.max(far, axis=0, keepdims=True), jnp.max(near, axis=0, keepdims=True)
        )
        far_p = jnp.exp(far - top).astype(BF)
        near_p = jnp.exp(near - top).astype(BF)
        out = nn_dot(vals[h, :, :far_rows], far_p) + nn_dot(vals[h, :, far_rows:], near_p)
        total = out[HEAD_DIM : HEAD_DIM + 1]
        outs.append(out[:HEAD_DIM] / total)
        logs.append(top + jnp.log(total))
    att = jnp.concatenate(outs, axis=0).T
    att_ref[...] = att
    for s in range(slots):
        gate = qg[s][:, LANES:].astype(F32)
        cols = slice(s * LANES, (s + 1) * LANES)
        gated_ref[:, cols] = (att[:, cols] * jax.nn.sigmoid(gate)).astype(BF)
    log_rows = jnp.concatenate(logs + [jnp.zeros((LANES - heads, rows), F32)], axis=0)
    log_ref[...] = log_rows.T


def row_block(rows, cols, place=0):
    return pl.BlockSpec((rows, cols), lambda i: (i, place))


def whole_block(rows, cols):
    return pl.BlockSpec((rows, cols), lambda i: (0, 0))


def slot_inputs(flag, projects, kv_there, rows):
    far_rows = projects[0].shape[0]
    specs_in = [pl.BlockSpec(memory_space=pltpu.SMEM)]
    for spec in (
        row_block(rows, 2 * LANES),
        row_block(rows, 2 * LANES, 1),
        pl.BlockSpec((far_rows, 2 * LANES), lambda i: (0, 1)),
        whole_block(far_rows, 2 * LANES),
    ):
        specs_in += [spec] * len(projects)
    return specs_in, [flag, *projects, *projects, *projects, *kv_there]


def cum_specs(rows, far_rows):
    return [
        row_block(rows, LANES),
        whole_block(far_rows, LANES),
        row_block(rows, LANES),
        row_block(rows, LANES),
        whole_block(far_rows, LANES),
    ]


def attend(flag, projects, kv_there, cum_near, cum_far, q_base, near_base, far_base, rows, heads):
    total = projects[0].shape[0]
    width = heads * HEAD_DIM
    steps = total // rows
    flops = 2 * total * (total + rows) * heads * 384
    slot_specs, slot_values = slot_inputs(flag, projects, kv_there, rows)
    return pl.pallas_call(
        functools.partial(attend_kernel, heads),
        grid=(steps,),
        out_shape=(
            jax.ShapeDtypeStruct((total, width), BF),
            jax.ShapeDtypeStruct((total, width), F32),
            jax.ShapeDtypeStruct((total, LANES), F32),
        ),
        in_specs=slot_specs + cum_specs(rows, total),
        out_specs=(row_block(rows, width), row_block(rows, width), row_block(rows, LANES)),
        scratch_shapes=[
            pltpu.VMEM((heads // 2, total + rows, 2 * LANES), BF),
            pltpu.VMEM((heads, HEAD_DIM + 16, total + rows), BF),
        ],
        compiler_params=pltpu.CompilerParams(vmem_limit_bytes=60 << 20),
        cost_estimate=pl.CostEstimate(
            flops=flops, bytes_accessed=total * width * 20, transcendentals=total * total * heads
        ),
    )(*slot_values, cum_near, cum_far, q_base, near_base, far_base)


def attend_back_kernel(
    heads,
    flag,
    qg_a,
    qg_b,
    qg_c,
    near_a,
    near_b,
    near_c,
    own_a,
    own_b,
    own_c,
    there_a,
    there_b,
    there_c,
    cum_near,
    cum_far,
    q_base,
    near_base,
    far_base,
    grad_ref,
    att_ref,
    log_ref,
    dqg_ref,
    near_ref,
    far_out,
    row_ref,
    near_col,
    far_col,
    keys,
    vals,
    far_ref,
):
    qg = (qg_a, qg_b, qg_c)
    kv_near = (near_a, near_b, near_c)
    far_own = (own_a, own_b, own_c)
    far_there = (there_a, there_b, there_c)
    rows = qg_a.shape[0]
    far_rows = own_a.shape[0]
    slots = heads // 2
    fill_keys(
        keys,
        flag,
        far_own,
        far_there,
        kv_near,
        cum_far,
        cum_near,
        far_base,
        near_base,
        far_rows,
        heads,
    )

    @pl.when(pl.program_id(0) == 0)
    def _():
        lane = lax.broadcasted_iota(jnp.int32, (far_rows + rows, LANES), 1)
        ones = (lane < 3).astype(F32).astype(BF)
        for s in range(slots):
            vals[s, :, LANES:] = ones

        @pl.when(flag[0] == 0)
        def _():
            for s in range(slots):
                vals[s, :far_rows, :LANES] = far_own[s][:, LANES:]

        @pl.when(flag[0] != 0)
        def _():
            for s in range(slots):
                vals[s, :far_rows, :LANES] = far_there[s][:, LANES:]

        far_ref[...] = jnp.zeros(far_ref.shape, F32)
        far_col[...] = jnp.zeros(far_col.shape, F32)

    for s in range(slots):
        vals[s, far_rows:, :LANES] = kv_near[s][:, LANES:]
    q_aug = (q_base[...].astype(F32) + split_pieces(cum_near[...] - log_ref[...], 0, heads)).astype(
        BF
    )
    visible = near_visible(rows)
    lane = lax.broadcasted_iota(jnp.int32, (rows, LANES), 1)
    row_total = jnp.zeros((rows, LANES), F32)
    col_total = jnp.zeros((rows, LANES), F32)
    for s in range(slots):
        cols = slice(s * LANES, (s + 1) * LANES)
        kcols = slice(2 * s * LANES, (2 * s + 1) * LANES)
        vcols = slice((2 * s + 1) * LANES, (2 * s + 2) * LANES)
        gate_sig = jax.nn.sigmoid(qg[s][:, LANES:].astype(F32))
        grad = grad_ref[:, cols].astype(F32)
        att = att_ref[:, cols]
        grad_att = (grad * gate_sig).astype(BF)
        dqg_ref[:, vcols] = (grad * att * gate_sig * (1.0 - gate_sig)).astype(BF)
        weighed = grad_att.astype(F32) * att
        dq_total = jnp.zeros((rows, LANES), F32)
        dk_near = jnp.zeros((rows, LANES), F32)
        dv_near = jnp.zeros((rows, LANES), F32)
        for half in range(2):
            h = 2 * s + half
            mine = half_lanes((rows, LANES), half)
            query = jnp.where(mine, qg[s][:, :LANES] * BF(HEAD_DIM**-0.5), BF(0))
            aug = jnp.where(head_lanes(q_aug.shape, h, heads), q_aug, BF(0))
            q_cat = jnp.concatenate([query, aug], axis=1)
            ga = jnp.where(mine, grad_att, BF(0))
            delta = -jnp.sum(jnp.where(mine, weighed, 0.0), axis=1, keepdims=True)
            high = delta.astype(BF).astype(F32)
            mid = (delta - high).astype(BF).astype(F32)
            low = delta - high - mid
            d_aug = jnp.where(
                lane == 0, high, jnp.where(lane == 1, mid, jnp.where(lane == 2, low, 0.0))
            ).astype(BF)
            ga_cat = jnp.concatenate([ga, d_aug], axis=1)
            for part in range(2):
                span = slice(0, far_rows) if part == 0 else slice(far_rows, far_rows + rows)
                prob = jnp.exp(nt_dot(keys[s, span], q_cat))
                if part == 1:
                    prob = jnp.where(visible, prob, 0.0)
                ds = (prob * nt_dot(vals[s, span], ga_cat)).astype(BF)
                dv = nn_dot(prob.astype(BF), ga)
                dk = nn_dot(ds, q_cat)
                dq = tn_dot(ds, keys[s, span])
                dq_total += jnp.where(mine, dq[:, :LANES], 0.0)
                row_total += jnp.where(lane == h, dq[:, LANES:], 0.0)
                if part == 0:
                    far_ref[:, kcols] += dk[:, :LANES]
                    far_ref[:, vcols] += dv
                    far_col[...] += dk[:, LANES:]
                else:
                    dk_near += dk[:, :LANES]
                    dv_near += dv
                    col_total += dk[:, LANES:]
        dqg_ref[:, kcols] = (dq_total * HEAD_DIM**-0.5).astype(BF)
        near_ref[:, kcols] = dk_near
        near_ref[:, vcols] = dv_near
    row_ref[...] = row_total
    near_col[...] = col_total

    @pl.when(pl.program_id(0) == pl.num_programs(0) - 1)
    def _():
        far_out[...] = far_ref[...].astype(BF)


def attend_back(
    flag,
    projects,
    kv_there,
    cum_near,
    cum_far,
    q_base,
    near_base,
    far_base,
    grad,
    att,
    logs,
    rows,
    heads,
):
    total = projects[0].shape[0]
    width = heads * HEAD_DIM
    steps = total // rows
    flops = 2 * total * (total + rows) * heads * 1152
    slot_specs, slot_values = slot_inputs(flag, projects, kv_there, rows)
    return pl.pallas_call(
        functools.partial(attend_back_kernel, heads),
        grid=(steps,),
        out_shape=(
            jax.ShapeDtypeStruct((total, 2 * width), BF),
            jax.ShapeDtypeStruct((total, 2 * width), F32),
            jax.ShapeDtypeStruct((total, 2 * width), BF),
            jax.ShapeDtypeStruct((total, LANES), F32),
            jax.ShapeDtypeStruct((total, LANES), F32),
            jax.ShapeDtypeStruct((total, LANES), F32),
        ),
        in_specs=slot_specs
        + cum_specs(rows, total)
        + [row_block(rows, width), row_block(rows, width), row_block(rows, LANES)],
        out_specs=(
            row_block(rows, 2 * width),
            row_block(rows, 2 * width),
            whole_block(total, 2 * width),
            row_block(rows, LANES),
            row_block(rows, LANES),
            whole_block(total, LANES),
        ),
        scratch_shapes=[
            pltpu.VMEM((heads // 2, total + rows, 2 * LANES), BF),
            pltpu.VMEM((heads // 2, total + rows, 2 * LANES), BF),
            pltpu.VMEM((total, 2 * width), F32),
        ],
        compiler_params=pltpu.CompilerParams(vmem_limit_bytes=60 << 20),
        cost_estimate=pl.CostEstimate(
            flops=flops, bytes_accessed=total * width * 40, transcendentals=total * total * heads
        ),
    )(*slot_values, cum_near, cum_far, q_base, near_base, far_base, grad, att, logs)


def full_norm(tokens, gain_vec):
    factor = lax.rsqrt(jnp.mean(tokens * tokens, axis=-1, keepdims=True) + epsilon)
    scaled = tokens * factor
    return factor, scaled, (scaled * gain_vec).astype(BF)


def full_norm_back(grad_normed, factor, scaled, gain_vec):
    e = grad_normed * gain_vec
    mean = jnp.mean(e * scaled, axis=-1, keepdims=True)
    return jnp.sum(grad_normed * scaled, axis=0), factor * (e - scaled * mean)


MESH_ID = pl.DeviceIdType.MESH


class Here:
    def __init__(self, ring):
        self.ring = ring
        self.at = {a: lax.axis_index(a) for a in AX}

    def other(self, axis):
        return {axis: 1 - self.at[axis]}

    def mid_home(self):
        return lax.rem(self.at["y"] + self.at["zl"], 2)

    def peer(self, k):
        dy, dz = self.ring.offsets[k]
        return {
            "y": lax.rem(self.at["y"] + dy, 2),
            "zl": lax.rem(self.at["zl"] + dz, self.ring.zl_count),
        }

    def group_to(self, flip):
        at = self.at
        return {"y": at["zh"], "c": at["x"] ^ flip, "x": at["y"], "zh": at["c"]}

    def group_from(self, flip):
        at = self.at
        return {"y": at["x"], "c": at["zh"], "x": at["c"] ^ flip, "zh": at["y"]}

    def group_away(self):
        at = self.at
        return ~((at["y"] == at["zh"]) & (at["y"] == at["x"]) & (at["y"] == at["c"]))

    def greet_group(self, targets):
        away = self.group_away()
        self.greet(
            targets + [self.group_to(1), self.group_from(1)],
            [(self.group_to(0), away), (self.group_from(0), away)],
        )

    def greet(self, targets, extra=()):
        barrier = pltpu.get_barrier_semaphore()
        for target in targets:
            pl.semaphore_signal(barrier, inc=1, device_id=target, device_id_type=MESH_ID)
        count = len(targets)
        for target, away in extra:
            @pl.when(away)
            def _():
                pl.semaphore_signal(barrier, inc=1, device_id=target, device_id_type=MESH_ID)

            count = count + away.astype(jnp.int32)
        pl.semaphore_wait(barrier, count)


def remote(src, dst, send_sem, recv_sem, target):
    return pltpu.make_async_remote_copy(
        src_ref=src,
        dst_ref=dst,
        send_sem=send_sem,
        recv_sem=recv_sem,
        device_id=target,
        device_id_type=MESH_ID,
    )


def last_kernel(
    ring,
    heads,
    dqg_in,
    near_in,
    far_in,
    row_in,
    near_col_in,
    far_col_in,
    weight_in,
    normed_in,
    gated_in,
    mixed_in,
    tokens_in,
    residual_in,
    hid_in,
    down_kept_in,
    down_there_in,
    gain_ref,
    forget_w,
    sig_ref,
    hot_ref,
    error_ref,
    gain_two_ref,
    valid_ref,
    back_out,
    proj_out,
    gate_out,
    up_out,
    down_out,
    out_out,
    small_out,
    grads,
    near,
    far_own,
    far_land,
    row_sum,
    near_col,
    far_col,
    far_col_land,
    cum,
    tot_send,
    tot_land,
    weight,
    normed,
    gated,
    mixed,
    tokens,
    residual,
    rs_send,
    rs_land,
    total,
    c_send,
    c_land,
    kept,
    x_send,
    x_land,
    z_send,
    z_land,
    final,
    kept_f,
    xf_send,
    xf_land,
    zf_send,
    zf_land,
    final_f,
    yf_land,
    full_f,
    co_send,
    co_land,
    kept_d,
    there_d,
    zd_send,
    zd_land,
    final_d,
    kept_o,
    xo_send,
    xo_land,
    zo_send,
    zo_land,
    final_o,
    blocks,
    gain_sum,
    gain_nat,
    gain_land,
    load_sem,
    local_sem,
    swap_send_sem,
    swap_recv_sem,
    y_send_sem,
    y_recv_sem,
    c2_send_sem,
    c2_recv_sem,
    rs_send_sem,
    rs_recv_sem,
    c_send_sem,
    c_recv_sem,
    x_send_sem,
    x_recv_sem,
    z_send_sem,
    z_recv_sem,
    back_send_sem,
    back_recv_sem,
    gain_send_sem,
    gain_recv_sem,
):
    here = Here(ring)
    y, c, x, zh, zl = (here.at[a] for a in ("y", "c", "x", "zh", "zl"))
    local, features = tokens.shape
    rows_all = normed.shape[0]
    part = features // 4
    slot_w = 4 * LANES
    slots = heads // 2
    all_w = slots * slot_w
    units = down_kept_in.shape[0] // 2
    owner = zh == here.mid_home()
    peers = len(ring.offsets)
    away = here.group_away()
    all_loads = [
        (row_in, row_sum),
        (near_col_in, near_col),
        (far_col_in, far_col),
        (far_in, far_own),
        (near_in, near),
    ]
    for s in range(slots):
        all_loads.append(
            (
                dqg_in.at[:, 2 * s * LANES : 2 * (s + 1) * LANES],
                grads.at[:, s * slot_w : s * slot_w + 2 * LANES],
            )
        )
    all_loads += [
        (down_kept_in, kept_d),
        (down_there_in, there_d),
        (normed_in, normed),
        (weight_in, weight),
        (gated_in, gated),
        (mixed_in, mixed),
        (tokens_in, tokens),
        (residual_in, residual),
    ]
    loads = [
        pltpu.make_async_copy(a, b, load_sem.at[i]) for i, (a, b) in enumerate(all_loads)
    ]
    first_loads = 8 + slots
    for copy in loads[:first_loads]:
        copy.start()
    load_row, load_near_col, load_far_col, load_far, load_near = loads[:5]
    load_dqg = loads[5 : 5 + slots]
    load_kept_d, load_there_d = loads[5 + slots : 7 + slots]
    load_normed, load_weight, load_gated, load_mixed, load_tokens, load_residual = loads[7 + slots :]

    here.greet_group(
        [here.peer(k) for k in range(1, peers)]
        + [here.other("c"), here.other("x"), here.other("zh")]
    )
    far_swap = remote(
        far_in, far_land, swap_send_sem.at[0], swap_recv_sem.at[0], here.other("c")
    )
    far_swap.start()
    col_swap = remote(
        far_col_in, far_col_land, swap_send_sem.at[1], swap_recv_sem.at[1], here.other("c")
    )
    col_swap.start()

    row0 = pl.multiple_of(c * part, part)

    def rows_of(ref, col, width):
        return ref.at[pl.ds(row0, part), pl.ds(pl.multiple_of(col, LANES), width)]

    def cols_of(ref, row, height):
        return ref.at[pl.ds(pl.multiple_of(row, LANES), height), pl.ds(row0, part)]

    def y_copy(i, src, dst):
        return remote(src, dst, y_send_sem.at[i], y_recv_sem.at[i], here.other("y"))

    pieces = [
        (hid_in.at[:, :units], rows_of(gate_out, y * units, units)),
        (hid_in.at[:, units:], rows_of(up_out, y * units, units)),
        (final_d, cols_of(down_out, y * units, units)),
    ]
    own_pieces = [
        pltpu.make_async_copy(src, dst, local_sem.at[i]) for i, (src, dst) in enumerate(pieces)
    ]
    y_pieces = [y_copy(i, src, dst) for i, (src, dst) in enumerate(pieces)]
    for copy in own_pieces[:2] + y_pieces[:2]:
        copy.start()

    lane = lax.broadcasted_iota(jnp.int32, (CLEN, LANES), 1)
    head_lane = lane < heads
    all_units = rows_all // CLEN
    chunk_units = local // CLEN

    def unit_rows(u):
        return slice(u * CLEN, (u + 1) * CLEN)

    load_row.wait()
    load_near_col.wait()
    for u in range(all_units):
        value = row_sum[unit_rows(u), :] - pltpu.roll(
            near_col[unit_rows(u), :], LANES - FAR_PIECE, 1
        )
        value = jnp.where(head_lane, value, 0.0)
        cum[unit_rows(u), :] = value
        tot_send[u : u + 1, :] = jnp.sum(value, axis=0, keepdims=True)
    tot_swap = remote(
        tot_send.at[:all_units],
        tot_land.at[:all_units],
        swap_send_sem.at[2],
        swap_recv_sem.at[2],
        here.other("c"),
    )
    tot_swap.start()

    load_kept_d.wait()
    load_there_d.wait()
    zd_send[...] = (kept_d[units:, :] + there_d[units:, :].astype(F32)).astype(BF)
    zd_copy = remote(zd_send, zd_land, z_send_sem.at[5], z_recv_sem.at[5], here.other("zh"))
    zd_copy.start()

    load_far.wait()
    load_near.wait()
    for copy in load_dqg:
        copy.wait()
    for copy in loads[first_loads:]:
        copy.start()
    far_swap.wait_recv()
    on_prompt = jnp.where(c == 0, 1.0, 0.0)

    def merge(i, carry):
        rows = pl.ds(pl.multiple_of(i * CLEN, CLEN), CLEN)
        value = near[rows, :] + on_prompt * (
            far_own[rows, :].astype(F32) + far_land[rows, :].astype(F32)
        )
        value = value.astype(BF)
        for s in range(slots):
            grads[rows, s * slot_w + 2 * LANES : (s + 1) * slot_w] = value[
                :, 2 * s * LANES : 2 * (s + 1) * LANES
            ]
        return carry

    lax.fori_loop(0, all_units, merge, 0)
    load_far_col.wait()
    col_swap.wait_recv()
    tot_swap.wait_recv()

    @pl.when(c == 0)
    def _():
        for u in range(all_units):
            both = far_col[unit_rows(u), :] + far_col_land[unit_rows(u), :]
            value = cum[unit_rows(u), :] - jnp.where(
                head_lane, pltpu.roll(both, LANES - FAR_PIECE, 1), 0.0
            )
            for j in range(all_units):
                value = value + hot_ref[unit_rows(u), j : j + 1] * tot_land[j : j + 1, :]
            cum[unit_rows(u), :] = value

    step_row = lax.broadcasted_iota(jnp.int32, (CLEN, CLEN), 0)
    step_col = lax.broadcasted_iota(jnp.int32, (CLEN, CLEN), 1)
    tri_back = (step_col >= step_row).astype(F32)
    for u in range(all_units):
        value = jnp.dot(
            tri_back,
            cum[unit_rows(u), :],
            precision=highest,
            preferred_element_type=F32,
        )
        cum[unit_rows(u), :] = value
        tot_send[all_units + u : all_units + u + 1, :] = value[0:1, :]
    places = []
    for dy, dz in ring.offsets:
        place = lax.rem(y + 2 - dy, 2) * ring.zl_count + lax.rem(
            zl + ring.zl_count - dz, ring.zl_count
        )
        for i in range(chunk_units):
            places.append(place * chunk_units + i)
    bias = jnp.zeros((1, LANES), F32)
    for u in range(all_units):
        suffix = jnp.zeros((1, LANES), F32)
        for other in range(all_units):
            if other != u:
                seen = jnp.where((places[other] > places[u]) & (c == 0), 1.0, 0.0)
                suffix = suffix + seen * tot_send[all_units + other : all_units + other + 1, :]
        value = (cum[unit_rows(u), :] + suffix) * sig_ref[unit_rows(u), :]
        grads[unit_rows(u), all_w:] = value.astype(BF)
        bias = bias + jnp.sum(value, axis=0, keepdims=True)

    load_normed.wait()
    tile_r = LANES
    per_part = part // tile_r

    def weight_tile(first, i):
        cols = pl.ds(pl.multiple_of(first + i * tile_r, LANES), tile_r)
        return tn_dot(normed[:, cols], grads[...])

    def c_step(i, carry):
        rows = pl.ds(pl.multiple_of(i * tile_r, tile_r), tile_r)
        c_send[rows, :] = weight_tile(2 * part, i).astype(BF)
        return carry

    lax.fori_loop(0, 2 * per_part, c_step, 0)
    c_copy = remote(c_send, c_land, c_send_sem.at[0], c_recv_sem.at[0], here.other("c"))
    c_copy.start()

    load_gated.wait()
    load_mixed.wait()
    out_rows = slots * LANES

    def out_tile(s, cols):
        return tn_dot(gated[:, s * LANES : (s + 1) * LANES], mixed[:, cols])

    for s in range(slots):
        co_send[s * LANES : (s + 1) * LANES, :] = out_tile(
            s, slice(2 * part, features)
        ).astype(BF)
    co_copy = remote(co_send, co_land, c_send_sem.at[1], c_recv_sem.at[1], here.other("c"))
    co_copy.start()

    zd_copy.wait_recv()
    final_d[...] = (
        kept_d[:units, :] + there_d[:units, :].astype(F32) + zd_land[...].astype(F32)
    ).astype(BF)
    for copy in own_pieces[2:] + y_pieces[2:]:
        copy.start()

    c_copy.wait_recv()

    def x_step(i, carry):
        rows = pl.ds(pl.multiple_of(i * tile_r, tile_r), tile_r)
        land = pl.ds(pl.multiple_of(part + i * tile_r, tile_r), tile_r)
        value = weight_tile(part, i) + c_land[land, :].astype(F32)
        for s in range(slots):
            x_send[s, rows, :] = value[:, s * slot_w : (s + 1) * slot_w].astype(BF)
        xf_send[rows, :] = value[:, all_w:].astype(BF)
        return carry

    lax.fori_loop(0, per_part, x_step, 0)
    x_copies = {}
    for s in (2, 1, 0):
        x_copies[s] = remote(
            x_send.at[s], x_land.at[s], x_send_sem.at[s], x_recv_sem.at[s], here.other("x")
        )
        x_copies[s].start()
    xf_copy = remote(xf_send, xf_land, x_send_sem.at[3], x_recv_sem.at[3], here.other("x"))
    xf_copy.start()
    load_weight.wait()
    tiles = 3
    tile_w = features // tiles

    def partial_rows(chunk_no, store):
        rows = slice(chunk_no * local, (chunk_no + 1) * local)

        def step(i, carry):
            cols = pl.ds(pl.multiple_of(i * tile_w, LANES), tile_w)
            value = nn_dot(grads[rows, all_w:], forget_w[:, cols])
            for s in range(slots):
                value = value + nt_dot(
                    grads[rows, s * slot_w : (s + 1) * slot_w], weight[s, cols, :]
                )
            store(cols, value)
            return carry

        lax.fori_loop(0, tiles, step, 0)

    moves = RingRows(here, local)

    def rs_copy(i):
        return moves.sum_copy(rs_send, rs_land, rs_send_sem, rs_recv_sem, i)

    for k in (3, 1, 2):

        def store_out(cols, value, k=k):
            rs_send[k - 1, :, cols] = value.astype(BF)

        partial_rows(k, store_out)
        for i in SUM_STARTS[k]:
            rs_copy(i).start()

    co_copy.wait_recv()
    for s in range(slots):
        rows = slice(s * LANES, (s + 1) * LANES)
        xo_send[rows, :] = (
            out_tile(s, slice(part, 2 * part)) + co_land[rows, part:].astype(F32)
        ).astype(BF)
    xo_copy = remote(xo_send, xo_land, x_send_sem.at[4], x_recv_sem.at[4], here.other("x"))
    xo_copy.start()

    def own_step(i, carry):
        rows = pl.ds(pl.multiple_of(i * tile_r, tile_r), tile_r)
        value = weight_tile(0, i) + c_land[rows, :].astype(F32)
        for s in range(slots):
            kept[s, rows, :] = value[:, s * slot_w : (s + 1) * slot_w]
        kept_f[rows, :] = value[:, all_w:]
        return carry

    lax.fori_loop(0, per_part, own_step, 0)
    for s in range(slots):
        rows = slice(s * LANES, (s + 1) * LANES)
        kept_o[rows, :] = out_tile(s, slice(0, part)) + co_land[rows, :part].astype(F32)

    def store_own(cols, value):
        total[:, cols] = value

    partial_rows(0, store_own)

    def z_copy(i, src, dst):
        return remote(src, dst, z_send_sem.at[i], z_recv_sem.at[i], here.other("zh"))

    z_first = z_copy(0, z_send.at[0], z_land.at[0])
    z_mid = z_copy(1, z_send.at[1], z_land.at[1])
    z_forget = z_copy(2, zf_send, zf_land)
    zo_first = z_copy(3, zo_send.at[0], zo_land.at[0])
    zo_mid = z_copy(4, zo_send.at[1], zo_land.at[1])
    moves.hand_on(rs_send, rs_land, rs_send_sem, rs_recv_sem)
    x_copies[2].wait_recv()
    z_send[0] = (kept[2] + x_land[2].astype(F32)).astype(BF)
    z_first.start()
    x_copies[1].wait_recv()

    @pl.when(~owner)
    def _():
        z_send[1] = (kept[1] + x_land[1].astype(F32)).astype(BF)
        z_mid.start()


    load_tokens.wait()
    load_residual.wait()
    for i in (0, 2, 4, 5):
        rs_copy(i).wait_recv()
    gain_sum[...] = jnp.zeros(gain_sum.shape, F32)
    tile_n = 32

    def norm_step(i, carry):
        rows = pl.ds(pl.multiple_of(i * tile_n, tile_n), tile_n)
        tok = tokens[rows, :].astype(F32)
        grad = total[rows, :]
        for k in (0, 2):
            grad = grad + rs_land[k, rows, :].astype(F32)
        factor = lax.rsqrt(jnp.mean(tok * tok, axis=-1, keepdims=True) + epsilon)
        scaled_tok = tok * factor
        e = grad * gain_ref[...]
        mean = jnp.mean(e * scaled_tok, axis=-1, keepdims=True)
        out = factor * (e - scaled_tok * mean) + residual[rows, :]
        weighed = jnp.sum(grad * scaled_tok, axis=0, keepdims=True)
        for b in range(4):
            blocks[b, rows, :] = out[:, b * part : (b + 1) * part].astype(BF)
            gain_sum[b, 0:1, :] += weighed[:, b * part : (b + 1) * part]
        return carry

    lax.fori_loop(0, local // tile_n, norm_step, 0)

    def block_no(half, low_high):
        return (half ^ x) + 2 * (low_high ^ c)

    def back_copy(flip, p):
        return remote(
            blocks.at[block_no(c ^ flip, p)],
            back_out.at[c, :, p * part : (p + 1) * part],
            back_send_sem.at[flip, p],
            back_recv_sem.at[flip, p],
            here.group_from(flip),
        )

    def back_own(flip, p):
        return pltpu.make_async_copy(
            blocks.at[block_no(c ^ flip, p)],
            back_out.at[c, :, p * part : (p + 1) * part],
            local_sem.at[5 + p],
        )

    for p in range(2):
        back_copy(1, p).start()

    @pl.when(away)
    def _():
        for p in range(2):
            back_copy(0, p).start()

    @pl.when(~away)
    def _():
        for p in range(2):
            back_own(0, p).start()

    for b in range(4):
        gain_sum[b, 1:2, :] = gain_two_ref[0:1, b * part : (b + 1) * part]
    for b in range(4):
        gain_nat[0, b] = gain_sum[block_no(b // 2, b % 2)]
    wide_lane = lax.broadcasted_iota(jnp.int32, (1, part), 1)
    scalars = jnp.where(
        wide_lane == 0, jnp.sum(error_ref[0:1, :], axis=1, keepdims=True), 0.0
    ) + jnp.where(wide_lane == 1, jnp.sum(valid_ref[...], axis=0, keepdims=True), 0.0)
    small_lane = lax.broadcasted_iota(jnp.int32, (1, LANES), 1)
    for j in range(heads):
        if j < 2:
            quarter, head = zh, 4 * y + j
        elif j < 4:
            quarter, head = here.mid_home(), j
        else:
            quarter, head = 1 - zh, 4 * y + j - 4
        dest = 2 + (quarter * ring.zl_count + zl) * heads + head
        value = jnp.sum(jnp.where(small_lane == j, bias, 0.0), axis=1, keepdims=True)
        scalars = scalars + jnp.where(wide_lane == dest, value, 0.0)
    gain_nat[0, 0, 2:3, :] = scalars
    gain_axes = ("c", "y", "x", "zl", "zh")

    def gain_step(place):
        return remote(
            gain_nat.at[place],
            gain_land.at[place],
            gain_send_sem.at[place],
            gain_recv_sem.at[place],
            here.other(gain_axes[place]),
        )

    def gain_next(place):
        gain_step(place).wait_recv()
        gain_nat[place + 1] = gain_nat[place] + gain_land[place]
        if place < 4:
            gain_step(place + 1).start()

    gain_step(0).start()

    x_copies[0].wait_recv()
    kept[0] += x_land[0].astype(F32)
    gain_next(0)
    xf_copy.wait_recv()
    kept_f[...] += xf_land[...].astype(F32)
    zf_send[...] = kept_f[...].astype(BF)
    z_forget.start()
    xo_copy.wait_recv()
    kept_o[...] += xo_land[...].astype(F32)
    gain_next(1)
    zo_send[0] = kept_o[2 * LANES :, :].astype(BF)
    zo_first.start()

    @pl.when(~owner)
    def _():
        zo_send[1] = kept_o[LANES : 2 * LANES, :].astype(BF)
        zo_mid.start()

    first_dst = rows_of(proj_out, 2 * y * slot_w, slot_w)
    mid_dst = rows_of(proj_out, slot_w, slot_w)
    out_first_dst = cols_of(out_out, 2 * LANES * y, LANES)
    out_mid_dst = cols_of(out_out, LANES, LANES)
    y_first = y_copy(3, final.at[0], first_dst)
    y_mid = y_copy(4, final.at[1], mid_dst)
    y_forget = y_copy(5, final_f, yf_land)
    yo_first = y_copy(6, final_o.at[0], out_first_dst)
    yo_mid = y_copy(7, final_o.at[1], out_mid_dst)
    own_first = pltpu.make_async_copy(final.at[0], first_dst, local_sem.at[8])
    own_mid = pltpu.make_async_copy(final.at[1], mid_dst, local_sem.at[9])
    own_out_first = pltpu.make_async_copy(final_o.at[0], out_first_dst, local_sem.at[10])
    own_out_mid = pltpu.make_async_copy(final_o.at[1], out_mid_dst, local_sem.at[11])
    own_forget = pltpu.make_async_copy(
        full_f, proj_out.at[pl.ds(row0, part), all_w : all_w + LANES], local_sem.at[12]
    )
    z_first.wait_recv()
    final[0] = (kept[0] + z_land[0].astype(F32)).astype(BF)
    y_first.start()
    own_first.start()

    @pl.when(owner)
    def _():
        z_mid.wait_recv()
        final[1] = (kept[1] + x_land[1].astype(F32) + z_land[1].astype(F32)).astype(BF)
        y_mid.start()
        own_mid.start()

    gain_next(2)
    z_forget.wait_recv()
    f_lane = lax.broadcasted_iota(jnp.int32, (part, LANES), 1)
    there_f = zf_land[...].astype(F32)
    edge = jnp.where(f_lane < 2, kept_f[...] + pltpu.roll(there_f, LANES - 4, 1), 0.0)
    edge = jnp.where(y == 0, edge, pltpu.roll(edge, 4, 1))
    mid_f = jnp.where((f_lane >= 2) & (f_lane < 4) & owner, kept_f[...] + there_f, 0.0)
    final_f[...] = (edge + mid_f).astype(BF)
    y_forget.start()
    gain_next(3)
    zo_first.wait_recv()
    final_o[0] = (kept_o[:LANES, :] + zo_land[0].astype(F32)).astype(BF)
    yo_first.start()
    own_out_first.start()

    @pl.when(owner)
    def _():
        zo_mid.wait_recv()
        final_o[1] = (kept_o[LANES : 2 * LANES, :] + zo_land[1].astype(F32)).astype(BF)
        yo_mid.start()
        own_out_mid.start()

    for copy in own_pieces:
        copy.wait()
    for copy in y_pieces:
        copy.wait_recv()
    c2 = []

    def hand_over(i, view):
        copy = remote(view, view, c2_send_sem.at[i], c2_recv_sem.at[i], here.other("c"))
        copy.start()
        c2.append(copy)

    hand_over(0, gate_out.at[pl.ds(row0, part), :])
    hand_over(1, up_out.at[pl.ds(row0, part), :])
    hand_over(2, down_out.at[:, pl.ds(row0, part)])

    gain_next(4)
    gain_copy = pltpu.make_async_copy(gain_nat.at[5], small_out, local_sem.at[7])
    gain_copy.start()
    y_forget.wait_recv()
    full_f[...] = final_f[...] + yf_land[...]
    own_forget.start()
    own_first.wait()
    y_first.wait_recv()
    own_out_first.wait()
    yo_first.wait_recv()
    own_forget.wait()

    @pl.when(owner)
    def _():
        own_mid.wait()
        own_out_mid.wait()

    @pl.when(~owner)
    def _():
        y_mid.wait_recv()
        yo_mid.wait_recv()

    hand_over(3, out_out.at[:, pl.ds(row0, part)])
    hand_over(4, proj_out.at[pl.ds(row0, part), :])

    for copy in c2:
        copy.wait()
    for p in range(2):
        back_copy(1, p).wait()

    @pl.when(away)
    def _():
        for p in range(2):
            back_copy(0, p).wait()

    @pl.when(~away)
    def _():
        for p in range(2):
            back_own(0, p).wait()

    gain_copy.wait()
    for i in range(5):
        gain_step(i).wait_send()
    for i in range(6):
        rs_copy(i).wait_send()
    for copy in [c_copy, co_copy, x_copies[0], x_copies[1], x_copies[2], xf_copy, xo_copy]:
        copy.wait_send()
    for copy in [far_swap, col_swap, tot_swap, z_first, z_forget, zo_first, zd_copy]:
        copy.wait_send()
    for copy in y_pieces + [y_first, y_forget, yo_first]:
        copy.wait_send()

    @pl.when(owner)
    def _():
        y_mid.wait_send()
        yo_mid.wait_send()

    @pl.when(~owner)
    def _():
        z_mid.wait_send()
        zo_mid.wait_send()


def last_step(ring, heads, large, small):
    near = large[1]
    rows = near.shape[0]
    weight, normed, gated = large[6:9]
    tokens = large[10]
    units = large[13].shape[0] // 2
    local, features = tokens.shape
    part = features // 4
    half = features // 2
    peers = len(ring.offsets)
    slot_w = 4 * LANES
    slots = heads // 2
    all_w = slots * slot_w
    any_spec = pl.BlockSpec(memory_space=pl.ANY)
    dma = pltpu.SemaphoreType.DMA
    vmem = pltpu.VMEM
    return pl.pallas_call(
        functools.partial(last_kernel, ring, heads),
        out_shape=(
            jax.ShapeDtypeStruct((2, local, half), BF),
            jax.ShapeDtypeStruct((half, all_w + LANES), BF),
            jax.ShapeDtypeStruct((half, 2 * units), BF),
            jax.ShapeDtypeStruct((half, 2 * units), BF),
            jax.ShapeDtypeStruct((2 * units, half), BF),
            jax.ShapeDtypeStruct((slots * LANES, half), BF),
            jax.ShapeDtypeStruct((4, 8, part), F32),
        ),
        in_specs=[any_spec] * len(large) + [pl.BlockSpec(memory_space=vmem)] * len(small),
        out_specs=[any_spec] * 7,
        scratch_shapes=[
            vmem((rows, all_w + LANES), BF),
            vmem(near.shape, F32),
            vmem(near.shape, BF),
            vmem(near.shape, BF),
            vmem((rows, LANES), F32),
            vmem((rows, LANES), F32),
            vmem((rows, LANES), F32),
            vmem((rows, LANES), F32),
            vmem((rows, LANES), F32),
            vmem((2 * (rows // CLEN), LANES), F32),
            vmem((2 * (rows // CLEN), LANES), F32),
            vmem(weight.shape, BF),
            vmem(normed.shape, BF),
            vmem(gated.shape, BF),
            vmem(normed.shape, BF),
            vmem(tokens.shape, BF),
            vmem(tokens.shape, F32),
            vmem((peers - 1, local, features), BF),
            vmem((peers - 1, local, features), BF),
            vmem((local, features), F32),
            vmem((half, all_w + LANES), BF),
            vmem((half, all_w + LANES), BF),
            vmem((slots, part, slot_w), F32),
            vmem((slots, part, slot_w), BF),
            vmem((slots, part, slot_w), BF),
            vmem((2, part, slot_w), BF),
            vmem((2, part, slot_w), BF),
            vmem((2, part, slot_w), BF),
            vmem((part, LANES), F32),
            vmem((part, LANES), BF),
            vmem((part, LANES), BF),
            vmem((part, LANES), BF),
            vmem((part, LANES), BF),
            vmem((part, LANES), BF),
            vmem((part, LANES), BF),
            vmem((part, LANES), BF),
            vmem((slots * LANES, half), BF),
            vmem((slots * LANES, half), BF),
            vmem((2 * units, part), F32),
            vmem((2 * units, part), BF),
            vmem((units, part), BF),
            vmem((units, part), BF),
            vmem((units, part), BF),
            vmem((slots * LANES, part), F32),
            vmem((slots * LANES, part), BF),
            vmem((slots * LANES, part), BF),
            vmem((2, LANES, part), BF),
            vmem((2, LANES, part), BF),
            vmem((2, LANES, part), BF),
            vmem((4, local, part), BF),
            vmem((4, 8, part), F32),
            vmem((6, 4, 8, part), F32),
            vmem((5, 4, 8, part), F32),
            dma((13 + slots,)),
            dma((13,)),
            dma((3,)),
            dma((3,)),
            dma((8,)),
            dma((8,)),
            dma((5,)),
            dma((5,)),
            dma((6,)),
            dma((6,)),
            dma((2,)),
            dma((2,)),
            dma((5,)),
            dma((5,)),
            dma((6,)),
            dma((6,)),
            dma((2, 2)),
            dma((2, 2)),
            dma((5,)),
            dma((5,)),
        ],
        compiler_params=pltpu.CompilerParams(
            collective_id=1, has_side_effects=True, vmem_limit_bytes=63 << 20
        ),
        cost_estimate=pl.CostEstimate(
            flops=4 * rows * features * all_w, bytes_accessed=40 << 20, transcendentals=0
        ),
    )(*large, *small)


def scale_kernel(
    full,
    sums,
    back,
    proj,
    gate,
    up,
    down,
    out,
    prompt_o,
    cont_o,
    query_o,
    outgate_o,
    key_o,
    value_o,
    gate_o,
    up_o,
    down_o,
    out_o,
):
    factor = full / sums[0, 2:3, 1:2]
    prompt_o[...] = back[0].astype(F32) * factor
    cont_o[...] = back[1].astype(F32) * factor
    for i, ref in enumerate((query_o, outgate_o, key_o, value_o)):
        for s in range(3):
            at = (4 * s + i) * LANES
            ref[:, s * LANES : (s + 1) * LANES] = proj[:, at : at + LANES].astype(F32) * factor
    gate_o[...] = gate[...].astype(F32) * factor
    up_o[...] = up[...].astype(F32) * factor
    down_o[...] = down[...].astype(F32) * factor
    out_o[...] = out[...].astype(F32) * factor


def scale_step(full, sums, back, proj, gate, up, down, out):
    steps = 8

    def cut(shape):
        return row_block(shape[0] // steps, shape[1])

    local, half = back.shape[1:]
    width = out.shape[0]
    shapes = [(local, half)] * 2 + [(half, width)] * 4 + [gate.shape, up.shape, down.shape, out.shape]
    return pl.pallas_call(
        functools.partial(scale_kernel, full),
        grid=(steps,),
        out_shape=tuple(jax.ShapeDtypeStruct(v, F32) for v in shapes),
        in_specs=[
            pl.BlockSpec(sums.shape, lambda i: (0, 0, 0)),
            pl.BlockSpec((2, local // steps, half), lambda i: (0, i, 0)),
        ]
        + [cut(v.shape) for v in (proj, gate, up, down, out)],
        out_specs=tuple(cut(v) for v in shapes),
        compiler_params=pltpu.CompilerParams(vmem_limit_bytes=62 << 20),
    )(sums, back, proj, gate, up, down, out)


def middle_kernel(
    ring,
    gated_in,
    w_out_in,
    w_gate_in,
    w_up_in,
    hid_there_in,
    w_down_in,
    tokens_in,
    teach_prompt_in,
    teach_cont_in,
    valid_ref,
    gain_ref,
    gated_grad,
    residual_grad,
    mixed_grads,
    hid_kept,
    hid_there,
    down_kept,
    down_there,
    error_ref,
    gain_grad,
    gated,
    w_out,
    w_hidden,
    w_down,
    tokens,
    teacher,
    mixed,
    total,
    result_grad,
    normed,
    hidden,
    gate_up,
    result_all,
    mixed_all,
    rs_send,
    rs_land,
    c_down_send,
    c_down_land,
    c_hid_send,
    c_hid_land,
    x_down_send,
    x_hid_send,
    down_sum,
    hid_sum,
    gg_stage,
    load_sem,
    wx_send,
    wx_recv,
    wc_send,
    wc_recv,
    wz_send,
    wz_recv,
    group_send,
    group_recv,
    out_sem,
    rs_send_sem,
    rs_recv_sem,
    ag_send_sem,
    ag_recv_sem,
    c_send_sem,
    c_recv_sem,
    x_send_sem,
    x_recv_sem,
):
    here = Here(ring)
    local, features = tokens.shape
    rows_all = gated.shape[0]
    width = gated.shape[1]
    units = hidden.shape[1]
    half_units = units // 2
    part = features // 4
    peers = len(ring.offsets)
    y, c, x = (here.at[a] for a in ("y", "c", "x"))
    gate_view, up_view = (
        w.at[
            pl.ds(pl.multiple_of(c * part, part), part),
            pl.ds(pl.multiple_of(y * half_units, half_units), half_units),
        ]
        for w in (w_gate_in, w_up_in)
    )
    down_view = w_down_in.at[
        pl.ds(pl.multiple_of(y * half_units, half_units), half_units),
        pl.ds(pl.multiple_of(c * part, part), part),
    ]

    loads = [
        pltpu.make_async_copy(a, b, load_sem.at[i])
        for i, (a, b) in enumerate(
            (
                (gate_view, w_hidden.at[0:part, 0:half_units]),
                (up_view, w_hidden.at[0:part, half_units:units]),
                (hid_there_in, w_hidden.at[0:part, units:]),
                (gated_in, gated),
                (w_out_in, w_out),
                (tokens_in, tokens),
                (down_view, w_down.at[0:half_units, 0:part]),
            )
        )
    ]
    for copy in loads:
        copy.start()
    here.greet_group(
        [here.peer(k) for k in range(1, peers)]
        + [here.other("c"), here.other("x"), here.other("zh")]
    )

    z_down = remote(
        down_view, w_down.at[half_units:, 0:part], wz_send.at[0], wz_recv.at[0], here.other("zh")
    )
    z_down.start()

    def hid_x_copy(i):
        cols = slice(i * half_units, (i + 1) * half_units) if i < 2 else slice(units, 2 * units)
        return remote(
            w_hidden.at[0:part, cols],
            w_hidden.at[part : 2 * part, cols],
            wx_send.at[i],
            wx_recv.at[i],
            here.other("x"),
        )

    def hid_c_copy(i):
        cols = slice(i * half_units, (i + 1) * half_units) if i < 2 else slice(units, 2 * units)
        return remote(
            w_hidden.at[0 : 2 * part, cols],
            w_hidden.at[2 * part :, cols],
            wc_send.at[i],
            wc_recv.at[i],
            here.other("c"),
        )

    for i in range(3):
        loads[i].wait()
        hid_x_copy(i).start()

    def teach_copies(flip, rows_in, remote_copy):
        kind = x ^ flip
        out = []
        for p in range(2):
            block = (x ^ y) + 2 * (kind ^ p)
            dst = teacher.at[:, pl.ds(pl.multiple_of(block * part, part), part)]
            src = rows_in.at[:, p * part : (p + 1) * part]
            if remote_copy:
                out.append(
                    remote(
                        src, dst, group_send.at[flip, p], group_recv.at[flip, p], here.group_to(flip)
                    )
                )
            else:
                out.append(pltpu.make_async_copy(src, dst, load_sem.at[7 + p]))
        return out

    away = here.group_away()

    def on_teacher(flip, here_too, what):
        for kind, rows_in in ((0, teach_prompt_in), (1, teach_cont_in)):
            mine = (x ^ flip) == kind
            if flip == 1:

                @pl.when(mine)
                def _():
                    for copy in teach_copies(1, rows_in, True):
                        what(copy)

            else:

                @pl.when(mine & away)
                def _():
                    for copy in teach_copies(0, rows_in, True):
                        what(copy)

                if here_too:

                    @pl.when(mine & ~away)
                    def _():
                        for copy in teach_copies(0, rows_in, False):
                            what(copy)

    def teacher_arrival(flip):
        for p in range(2):
            remote(
                teach_prompt_in.at[:, p * part : (p + 1) * part],
                teacher.at[:, p * part : (p + 1) * part],
                group_send.at[flip, p],
                group_recv.at[flip, p],
                here.group_to(flip),
            ).wait_recv()

    def chunk(k):
        return slice(k * local, (k + 1) * local)

    def tiled(count, size, step):
        def body(i, carry):
            step(pl.ds(pl.multiple_of(i * size, size), size))
            return carry

        lax.fori_loop(0, count, body, 0)

    moves = RingRows(here, local)

    def rs_copy(phase, i):
        return moves.sum_copy(rs_send, rs_land, rs_send_sem.at[phase], rs_recv_sem.at[phase], i)

    def ag_copy(phase, buffer, i):
        return moves.gather_copy(buffer, ag_send_sem.at[phase], ag_recv_sem.at[phase], i)

    wide = 512
    wide_count = features // wide

    def send_partial(phase, k, left, right, transposed):
        def step(cols):
            if transposed:
                value = nt_dot(left, right[cols, :])
            else:
                value = nn_dot(left, right[:, cols])
            if k == 0:
                total[:, cols] = value
            else:
                rs_send[k - 1, :, cols] = value.astype(BF)

        if k != 0 and phase > 0:
            for i in SUM_READS[k]:
                rs_copy(phase - 1, i).wait_send()
        tiled(wide_count, wide, step)
        if k != 0:
            for i in SUM_STARTS[k]:
                rs_copy(phase, i).start()

    def hand_on(phase):
        moves.hand_on(rs_send, rs_land, rs_send_sem.at[phase], rs_recv_sem.at[phase])

    def sums_arrived(phase):
        for i in (0, 2, 4, 5):
            rs_copy(phase, i).wait_recv()

    def half_tiles(phase, buffer, step):
        for half in range(2):

            def body(i, carry):
                step(pl.ds(pl.multiple_of(half * (local // 2) + i * 32, 32), 32))
                return carry

            lax.fori_loop(0, local // 64, body, 0)
            ag_copy(phase, buffer, half).start()
            ag_copy(phase, buffer, 2 + half).start()

    def pass_on(phase, buffer):
        ag_copy(phase, buffer, 2).wait_recv()
        ag_copy(phase, buffer, 4).start()
        ag_copy(phase, buffer, 1).wait_recv()
        ag_copy(phase, buffer, 5).start()

    def rows_arrived(phase, buffer, k):
        for i in {1: (0,), 2: (3,), 3: (4, 5)}[k]:
            ag_copy(phase, buffer, i).wait_recv()

    def summed(rows):
        return total[rows, :] + rs_land[0, rows, :].astype(F32) + rs_land[2, rows, :].astype(F32)

    loads[3].wait()
    loads[4].wait()
    for k in (3, 1, 2, 0):
        send_partial(0, k, gated[chunk(k), :], w_out, False)
    loads[5].wait()
    loads[6].wait()
    z_down.wait_recv()
    down_x_copy = remote(
        w_down.at[:, 0:part],
        w_down.at[:, part : 2 * part],
        wx_send.at[4],
        wx_recv.at[4],
        here.other("x"),
    )
    down_x_copy.start()
    hand_on(0)
    sums_arrived(0)

    def second_norm(rows):
        value = tokens[rows, :].astype(F32) + summed(rows)
        mixed[rows, :] = value
        factor = lax.rsqrt(jnp.mean(value * value, axis=-1, keepdims=True) + epsilon)
        normed[rows, :] = (value * factor * gain_ref[...]).astype(BF)

    half_tiles(0, normed, second_norm)

    for i in range(3):
        hid_x_copy(i).wait_recv()
        hid_c_copy(i).start()
    for f in range(2):
        on_teacher(f, True, lambda copy: copy.start())
    for i in range(3):
        hid_c_copy(i).wait_recv()
    tile_u = 256
    per_half = half_units // tile_u

    def forward_chunk(k):
        left = normed[chunk(k), :]

        def step(i, carry):
            half = i // per_half
            sub = lax.rem(i, per_half)
            gate_at = pl.multiple_of(half * units + sub * tile_u, tile_u)
            up_at = pl.multiple_of(half * units + half_units + sub * tile_u, tile_u)
            gate = nn_dot(left, w_hidden[:, pl.ds(gate_at, tile_u)])
            up = nn_dot(left, w_hidden[:, pl.ds(up_at, tile_u)])
            gate_up[chunk(k), pl.ds(gate_at, tile_u)] = gate.astype(BF)
            gate_up[chunk(k), pl.ds(up_at, tile_u)] = up.astype(BF)
            hidden[chunk(k), pl.ds(pl.multiple_of(i * tile_u, tile_u), tile_u)] = (
                gate * jax.nn.sigmoid(gate) * up
            ).astype(BF)
            return carry

        lax.fori_loop(0, 2 * per_half, step, 0)

    def forward_sum(k):
        send_partial(1, k, hidden[chunk(k), :], w_down, False)

    forward_chunk(0)
    pass_on(0, normed)
    down_x_copy.wait_recv()
    down_c_copy = remote(
        w_down.at[:, 0 : 2 * part],
        w_down.at[:, 2 * part :],
        wc_send.at[4],
        wc_recv.at[4],
        here.other("c"),
    )
    down_c_copy.start()
    for k in range(1, peers):
        rows_arrived(0, normed, k)
        forward_chunk(k)
        if k == 1:
            down_c_copy.wait_recv()
        forward_sum(k)
    forward_sum(0)
    hand_on(1)
    teacher_arrival(1)

    @pl.when(away)
    def _():
        teacher_arrival(0)

    @pl.when(~away)
    def _():
        for kind, rows_in in ((0, teach_prompt_in), (1, teach_cont_in)):

            @pl.when(x == kind)
            def _():
                for copy in teach_copies(0, rows_in, False):
                    copy.wait()

    sums_arrived(1)
    error_ref[...] = jnp.zeros(error_ref.shape, F32)
    gain_grad[...] = jnp.zeros(gain_grad.shape, F32)

    def loss_rows(rows):
        deviation = mixed[rows, :] + summed(rows) - teacher[rows, :].astype(F32)
        grad = valid_ref[rows, :] * deviation
        result_grad[rows, :] = grad
        result_all[rows, :] = grad.astype(BF)
        error_ref[0:1, :] += 0.5 * jnp.sum(grad * deviation, axis=0, keepdims=True)

    half_tiles(1, result_all, loss_rows)

    def backward_chunk(k):
        left = result_all[chunk(k), :]

        def step(i, carry):
            half = i // per_half
            sub = lax.rem(i, per_half)
            gate_at = pl.multiple_of(half * units + sub * tile_u, tile_u)
            up_at = pl.multiple_of(half * units + half_units + sub * tile_u, tile_u)
            grad = nt_dot(left, w_down[pl.ds(pl.multiple_of(i * tile_u, tile_u), tile_u), :])
            gate = gate_up[chunk(k), pl.ds(gate_at, tile_u)].astype(F32)
            up = gate_up[chunk(k), pl.ds(up_at, tile_u)].astype(F32)
            sig = jax.nn.sigmoid(gate)
            gate_up[chunk(k), pl.ds(gate_at, tile_u)] = (
                grad * up * sig * (1.0 + gate * (1.0 - sig))
            ).astype(BF)
            gate_up[chunk(k), pl.ds(up_at, tile_u)] = (grad * gate * sig).astype(BF)
            return carry

        lax.fori_loop(0, 2 * per_half, step, 0)

    def backward_sum(k):
        send_partial(2, k, gate_up[chunk(k), :], w_hidden, True)

    backward_chunk(0)
    pass_on(1, result_all)
    for k in range(1, peers):
        rows_arrived(1, result_all, k)
        backward_chunk(k)
        backward_sum(k)

    unit_tile = 256

    def down_tile(units_at, cols):
        return tn_dot(hidden[:, units_at], result_all[:, cols])

    feature_tile = 128

    def hid_tile(first, at):
        cols = pl.ds(pl.multiple_of(first + at.start, feature_tile), feature_tile)
        return tn_dot(normed[:, cols], gate_up[...])

    def hid_c(at):
        c_hid_send[at, :] = hid_tile(2 * part, at).astype(BF)

    tiled(2 * part // feature_tile, feature_tile, hid_c)
    c_hid = remote(c_hid_send, c_hid_land, c_send_sem.at[1], c_recv_sem.at[1], here.other("c"))
    c_hid.start()
    hand_on(2)
    backward_sum(0)

    def down_c(units_at):
        c_down_send[units_at, :] = down_tile(units_at, slice(2 * part, features)).astype(BF)

    tiled(units // unit_tile, unit_tile, down_c)
    c_down = remote(c_down_send, c_down_land, c_send_sem.at[0], c_recv_sem.at[0], here.other("c"))
    c_down.start()
    c_hid.wait_recv()

    def hid_x(at):
        land = pl.ds(pl.multiple_of(part + at.start, feature_tile), feature_tile)
        x_hid_send[at, :] = (hid_tile(part, at) + c_hid_land[land, :].astype(F32)).astype(BF)

    tiled(part // feature_tile, feature_tile, hid_x)
    x_hid = remote(x_hid_send, hid_there, x_send_sem.at[1], x_recv_sem.at[1], here.other("x"))
    x_hid.start()

    sums_arrived(2)

    def norm_back(rows):
        value = mixed[rows, :]
        factor = lax.rsqrt(jnp.mean(value * value, axis=-1, keepdims=True) + epsilon)
        scaled_rows = value * factor
        grad = summed(rows)
        e = grad * gain_ref[...]
        mean = jnp.mean(e * scaled_rows, axis=-1, keepdims=True)
        out = result_grad[rows, :] + factor * (e - scaled_rows * mean)
        result_grad[rows, :] = out
        mixed_all[rows, :] = out.astype(BF)
        gain_grad[0:1, :] += jnp.sum(grad * scaled_rows, axis=0, keepdims=True)

    half_tiles(2, mixed_all, norm_back)
    residual_copy = pltpu.make_async_copy(result_grad, residual_grad, out_sem.at[0])
    residual_copy.start()

    def gated_chunk(k):
        gg_stage[chunk(k), :] = nt_dot(mixed_all[chunk(k), :], w_out[...])

    gated_chunk(0)
    c_down.wait_recv()

    def down_x(units_at):
        value = down_tile(units_at, slice(part, 2 * part))
        x_down_send[units_at, :] = (value + c_down_land[units_at, part:].astype(F32)).astype(BF)

    tiled(units // unit_tile, unit_tile, down_x)
    pass_on(2, mixed_all)

    def down_own(units_at):
        value = down_tile(units_at, slice(0, part))
        down_sum[units_at, :] = value + c_down_land[units_at, :part].astype(F32)

    tiled(units // unit_tile, unit_tile, down_own)

    def hid_own(at):
        hid_sum[at, :] = hid_tile(0, at) + c_hid_land[at, :].astype(F32)

    tiled(part // feature_tile, feature_tile, hid_own)
    sums_out = [
        pltpu.make_async_copy(down_sum, down_kept, out_sem.at[1]),
        pltpu.make_async_copy(hid_sum, hid_kept, out_sem.at[2]),
        pltpu.make_async_copy(x_down_send, down_there, out_sem.at[5]),
    ]
    for copy in sums_out:
        copy.start()
    for k in range(1, peers):
        rows_arrived(2, mixed_all, k)
        gated_chunk(k)
    finals = [
        pltpu.make_async_copy(gg_stage, gated_grad, out_sem.at[3]),
        pltpu.make_async_copy(mixed_all, mixed_grads, out_sem.at[4]),
    ]
    for copy in finals:
        copy.start()
    for i in range(6):
        rs_copy(2, i).wait_send()
        for phase, buffer in enumerate((normed, result_all, mixed_all)):
            ag_copy(phase, buffer, i).wait_send()
    c_down.wait_send()
    c_hid.wait_send()
    z_down.wait_send()
    for i in range(3):
        hid_x_copy(i).wait_send()
        hid_c_copy(i).wait_send()
    for f in range(2):
        on_teacher(f, False, lambda copy: copy.wait_send())
    down_x_copy.wait_send()
    down_c_copy.wait_send()
    x_hid.wait()
    residual_copy.wait()
    for copy in sums_out + finals:
        copy.wait()


def middle_step(
    ring,
    gated,
    w_out,
    w_gate,
    w_up,
    hid_there,
    w_down,
    tokens,
    teach_prompt,
    teach_cont,
    valid,
    gain,
):
    rows, width = gated.shape
    local, features = tokens.shape
    units = w_down.shape[0]
    part = features // 4
    peers = len(ring.offsets)
    any_spec = pl.BlockSpec(memory_space=pl.ANY)
    vmem_spec = pl.BlockSpec(memory_space=pltpu.VMEM)
    dma = pltpu.SemaphoreType.DMA
    return pl.pallas_call(
        functools.partial(middle_kernel, ring),
        out_shape=(
            jax.ShapeDtypeStruct((rows, width), F32),
            jax.ShapeDtypeStruct((local, features), F32),
            jax.ShapeDtypeStruct((rows, features), BF),
            jax.ShapeDtypeStruct((part, 2 * units), F32),
            jax.ShapeDtypeStruct((part, 2 * units), BF),
            jax.ShapeDtypeStruct((units, part), F32),
            jax.ShapeDtypeStruct((units, part), BF),
            jax.ShapeDtypeStruct((8, features), F32),
            jax.ShapeDtypeStruct((8, features), F32),
        ),
        in_specs=[any_spec] * 9 + [vmem_spec] * 2,
        out_specs=[any_spec] * 7 + [vmem_spec] * 2,
        scratch_shapes=[
            pltpu.VMEM(gated.shape, BF),
            pltpu.VMEM(w_out.shape, BF),
            pltpu.VMEM((features, 2 * units), BF),
            pltpu.VMEM((units, features), BF),
            pltpu.VMEM(tokens.shape, BF),
            pltpu.VMEM(tokens.shape, BF),
            pltpu.VMEM(tokens.shape, F32),
            pltpu.VMEM(tokens.shape, F32),
            pltpu.VMEM(tokens.shape, F32),
            pltpu.VMEM((rows, features), BF),
            pltpu.VMEM((rows, units), BF),
            pltpu.VMEM((rows, 2 * units), BF),
            pltpu.VMEM((rows, features), BF),
            pltpu.VMEM((rows, features), BF),
            pltpu.VMEM((peers - 1, local, features), BF),
            pltpu.VMEM((peers - 1, local, features), BF),
            pltpu.VMEM((units, 2 * part), BF),
            pltpu.VMEM((units, 2 * part), BF),
            pltpu.VMEM((2 * part, 2 * units), BF),
            pltpu.VMEM((2 * part, 2 * units), BF),
            pltpu.VMEM((units, part), BF),
            pltpu.VMEM((part, 2 * units), BF),
            pltpu.VMEM((units, part), F32),
            pltpu.VMEM((part, 2 * units), F32),
            pltpu.VMEM((rows, width), F32),
            dma((9,)),
            dma((5,)),
            dma((5,)),
            dma((5,)),
            dma((5,)),
            dma((2,)),
            dma((2,)),
            dma((2, 2)),
            dma((2, 2)),
            dma((6,)),
            dma((3, 6)),
            dma((3, 6)),
            dma((3, 6)),
            dma((3, 6)),
            dma((2,)),
            dma((2,)),
            dma((2,)),
            dma((2,)),
        ],
        compiler_params=pltpu.CompilerParams(
            collective_id=2, has_side_effects=True, vmem_limit_bytes=63 << 20
        ),
        cost_estimate=pl.CostEstimate(
            flops=6 * rows * features * (3 * units + width),
            bytes_accessed=60 << 20,
            transcendentals=0,
        ),
    )(
        gated,
        w_out,
        w_gate,
        w_up,
        hid_there,
        w_down,
        tokens,
        teach_prompt,
        teach_cont,
        valid,
        gain,
    )


class RingRows:
    def __init__(self, here, local):
        self.zl, self.y = here.peer(1), here.peer(2)
        self.local = local
        self.half = local // 2

    def rows(self, place, half=None):
        base = place * self.local
        if half is None:
            return slice(base, base + self.local)
        return slice(base + half * self.half, base + (half + 1) * self.half)

    def gather_copy(self, buffer, sends, recvs, i):
        source, target, place, half = (
            (0, self.zl, 1, 0),
            (0, self.zl, 1, 1),
            (0, self.y, 2, 0),
            (0, self.y, 2, 1),
            (2, self.zl, 3, 0),
            (1, self.y, 3, 1),
        )[i]
        return remote(
            buffer.at[self.rows(source, half)],
            buffer.at[self.rows(place, half)],
            sends.at[i],
            recvs.at[i],
            target,
        )

    def sum_copy(self, send, land, sends, recvs, i):
        chunk, half, target, slot = (
            (0, 0, self.zl, 0),
            (2, 0, self.zl, 1),
            (1, 1, self.y, 0),
            (2, 1, self.y, 1),
            (1, 0, self.y, 2),
            (0, 1, self.zl, 2),
        )[i]
        return remote(
            send.at[chunk, self.rows(0, half)],
            land.at[slot, self.rows(0, half)],
            sends.at[i],
            recvs.at[i],
            target,
        )

    def hand_on(self, send, land, sends, recvs):
        for chunk, half, got, i in ((1, 0, 1, 4), (0, 1, 3, 5)):
            self.sum_copy(send, land, sends, recvs, got).wait_recv()
            rows = self.rows(0, half)
            send[chunk, rows, :] = (
                send[chunk, rows, :].astype(F32) + land[1, rows, :].astype(F32)
            ).astype(BF)
            self.sum_copy(send, land, sends, recvs, i).start()


SUM_STARTS = {1: (0,), 2: (2,), 3: (1, 3)}
SUM_READS = {1: (0, 5), 2: (2, 4), 3: (1, 3)}


def first_kernel(
    ring,
    prompt_in,
    cont_in,
    small_in,
    ints_in,
    wq_in,
    wg_in,
    wk_in,
    wv_in,
    w_out_in,
    tokens_out,
    normed_out,
    slots_out,
    w_out_all,
    small_out,
    gains_out,
    forget_w_out,
    ints_out,
    proj_a,
    proj_b,
    proj_c,
    forget_own,
    there_a,
    there_b,
    there_c,
    forget_there,
    tokens,
    normed,
    slot_w,
    project,
    forget,
    small,
    small_x,
    feats,
    forget_f,
    forget_w,
    group_send,
    group_recv,
    ints_send,
    ints_recv,
    small_send,
    small_recv,
    own_sem,
    z_send,
    z_recv,
    x_send,
    x_recv,
    c_send,
    c_recv,
    ag_send,
    ag_recv,
    kv_send,
    kv_recv,
    out_sem,
):
    here = Here(ring)
    y, c, x, zh = (here.at[a] for a in ("y", "c", "x", "zh"))
    local, features = tokens.shape
    part = features // 4
    half = features // 2
    peers = len(ring.offsets)
    owner = zh == here.mid_home()
    row0 = pl.multiple_of(c * part, part)
    first0 = pl.multiple_of(2 * LANES * y, LANES)
    sources = (wq_in, wg_in, wk_in, wv_in)

    here.greet_group([here.peer(k) for k in range(1, peers)] + [here.other(a) for a in "cx"] + [here.other("zh")])

    def group_copies(flip, rows_in, remote_copy):
        kind = x ^ flip
        out = []
        for p in range(2):
            block = (x ^ y) + 2 * (kind ^ p)
            dst = tokens.at[:, pl.ds(pl.multiple_of(block * part, part), part)]
            src = rows_in.at[:, p * part : (p + 1) * part]
            if remote_copy:
                out.append(
                    remote(
                        src, dst, group_send.at[flip, p], group_recv.at[flip, p], here.group_to(flip)
                    )
                )
            else:
                out.append(pltpu.make_async_copy(src, dst, own_sem.at[12 + p]))
        return out

    def ints_copy():
        return remote(ints_in, ints_out, ints_send, ints_recv, here.group_to(0))

    def ints_own():
        return pltpu.make_async_copy(ints_in, ints_out, own_sem.at[14])

    away = here.group_away()

    def on_group(flip, what):
        for kind, rows_in in ((0, prompt_in), (1, cont_in)):
            mine = (x ^ flip) == kind
            if flip == 1:

                @pl.when(mine)
                def _():
                    for copy in group_copies(flip, rows_in, True):
                        what(copy)

            else:

                @pl.when(mine & away)
                def _():
                    for copy in group_copies(flip, rows_in, True):
                        what(copy)

                @pl.when(mine & ~away)
                def _():
                    for copy in group_copies(flip, rows_in, False):
                        what(copy)

    for f in range(2):
        on_group(f, lambda copy: copy.start())

    @pl.when(away)
    def _():
        ints_copy().start()

    @pl.when(~away)
    def _():
        ints_own().start()

    def z_piece(i, s):
        start = first0 if s == 2 else LANES
        return remote(
            sources[i].at[pl.ds(row0, part), pl.ds(start, LANES)],
            slot_w.at[s, 0:part, i * LANES : (i + 1) * LANES],
            z_send.at[s, i],
            z_recv.at[s, i],
            here.other("zh"),
        )

    own_small = pltpu.make_async_copy(small_in, small.at[0], own_sem.at[15])
    own_small.start()
    small_z = remote(small_in, small.at[1], small_send.at[0], small_recv.at[0], here.other("zh"))
    small_z.start()

    def own_piece(i, s):
        start = first0 if s == 0 else LANES
        return pltpu.make_async_copy(
            sources[i].at[pl.ds(row0, part), pl.ds(start, LANES)],
            slot_w.at[s, 0:part, i * LANES : (i + 1) * LANES],
            own_sem.at[4 * s + i],
        )

    for i in range(4):
        own_piece(i, 0).start()

    @pl.when(owner)
    def _():
        for i in range(4):
            own_piece(i, 1).start()

    own_out = [
        pltpu.make_async_copy(
            w_out_in.at[pl.ds(first0, LANES), pl.ds(row0, part)],
            w_out_all.at[0:LANES, 0:part],
            own_sem.at[8],
        ),
        pltpu.make_async_copy(
            w_out_in.at[LANES : 2 * LANES, pl.ds(row0, part)],
            w_out_all.at[LANES : 2 * LANES, 0:part],
            own_sem.at[9],
        ),
    ]
    own_out[0].start()

    @pl.when(owner)
    def _():
        own_out[1].start()

    own_small.wait()
    small_z.wait_recv()
    small_over_x = remote(small, small_x, small_send.at[1], small_recv.at[1], here.other("x"))
    small_over_x.start()

    def x_copy(s):
        return remote(
            slot_w.at[s, 0:part],
            slot_w.at[s, part : 2 * part],
            x_send.at[s],
            x_recv.at[s],
            here.other("x"),
        )

    def c_copy(s):
        return remote(
            slot_w.at[s, 0:half],
            slot_w.at[s, half:features],
            c_send.at[s],
            c_recv.at[s],
            here.other("c"),
        )

    for i in range(4):
        own_piece(i, 0).wait()
    x_copy(0).start()
    small_over_x.wait_recv()
    for z in range(2):
        for place in range(2):
            at = pl.multiple_of((c ^ place) * part, part)
            feats[z, :, 2 * place * part : (2 * place + 1) * part] = small[z, :, pl.ds(at, part)]
            feats[z, :, (2 * place + 1) * part : (2 * place + 2) * part] = small_x[
                z, :, pl.ds(at, part)
            ]
    forget_f[...] = jnp.zeros(forget_f.shape, F32)
    for z, rows in ((0, slice(0, 2)), (1, slice(4, 6))):
        forget_f[rows, :] = jnp.where(y == 0, feats[z, 8:10, :], feats[z, 12:14, :])
    forget_f[2:4, :] = jnp.where(owner, feats[0, 10:12, :], feats[1, 10:12, :])
    forget_w[...] = jnp.zeros(forget_w.shape, BF)
    forget_w[0:16, :] = forget_f[...].astype(BF)

    def group_arrival(flip):
        for p in range(2):
            remote(
                prompt_in.at[:, p * part : (p + 1) * part],
                tokens.at[:, p * part : (p + 1) * part],
                group_send.at[flip, p],
                group_recv.at[flip, p],
                here.group_to(flip),
            ).wait_recv()

    group_arrival(1)

    @pl.when(away)
    def _():
        group_arrival(0)

    @pl.when(~away)
    def _():
        for kind, rows_in in ((0, prompt_in), (1, cont_in)):

            @pl.when(x == kind)
            def _():
                for copy in group_copies(0, rows_in, False):
                    copy.wait()

    for i in range(4):
        z_piece(i, 2).start()

    @pl.when(owner)
    def _():
        for i in range(4):
            z_piece(i, 1).start()

    z_out = [
        remote(
            w_out_in.at[pl.ds(first0, LANES), pl.ds(row0, part)],
            w_out_all.at[2 * LANES : 3 * LANES, 0:part],
            z_send.at[0, 0],
            z_recv.at[0, 0],
            here.other("zh"),
        ),
        remote(
            w_out_in.at[LANES : 2 * LANES, pl.ds(row0, part)],
            w_out_all.at[LANES : 2 * LANES, 0:part],
            z_send.at[0, 1],
            z_recv.at[0, 1],
            here.other("zh"),
        ),
    ]
    z_out[0].start()

    @pl.when(owner)
    def _():
        z_out[1].start()

    moves = RingRows(here, local)

    def ag_copy(i):
        return moves.gather_copy(normed, ag_send, ag_recv, i)

    def norm_rows(i, carry):
        rows = pl.ds(pl.multiple_of(i * 32, 32), 32)
        value = tokens[rows, :].astype(F32)
        factor = lax.rsqrt(jnp.mean(value * value, axis=-1, keepdims=True) + epsilon)
        normed[rows, :] = (value * factor * feats[0, 0:1, :]).astype(BF)
        return carry

    for place in range(2):
        lax.fori_loop(place * (local // 64), (place + 1) * (local // 64), norm_rows, 0)
        ag_copy(place).start()
        ag_copy(2 + place).start()

    outs = [
        pltpu.make_async_copy(tokens, tokens_out, out_sem.at[0]),
        pltpu.make_async_copy(small, small_out, out_sem.at[1]),
        pltpu.make_async_copy(feats.at[0], gains_out, out_sem.at[2]),
        pltpu.make_async_copy(forget_w, forget_w_out, out_sem.at[3]),
    ]
    for copy in outs:
        copy.start()

    x_copy(0).wait_recv()
    c_copy(0).start()
    for i in range(4):
        z_piece(i, 2).wait_recv()
    x_copy(2).start()

    @pl.when(owner)
    def _():
        for i in range(4):
            own_piece(i, 1).wait()

    @pl.when(~owner)
    def _():
        for i in range(4):
            z_piece(i, 1).wait_recv()

    x_copy(1).start()

    projects = (proj_a, proj_b, proj_c)
    theres = (there_a, there_b, there_c)

    def chunk(k):
        return slice(k * local, (k + 1) * local)

    def kv_copy(k, s):
        return remote(
            project.at[s, chunk(k), 2 * LANES :],
            theres[s].at[chunk(k)],
            kv_send.at[k, s],
            kv_recv.at[k, s],
            here.other("c"),
        )

    def forget_copy(k):
        return remote(
            forget.at[chunk(k)],
            forget_there.at[chunk(k)],
            kv_send.at[k, 3],
            kv_recv.at[k, 3],
            here.other("c"),
        )

    def project_chunk(k, s):
        project[s, chunk(k), :] = nn_dot(normed[chunk(k), :], slot_w[s]).astype(BF)
        kv_copy(k, s).start()

    def forget_chunk(k):
        forget[chunk(k), :] = nt_dot(normed[chunk(k), :], forget_w[...]).astype(BF)
        forget_copy(k).start()

    c_copy(0).wait_recv()
    forget_chunk(0)
    project_chunk(0, 0)
    ag_copy(2).wait_recv()
    ag_copy(4).start()
    ag_copy(1).wait_recv()
    ag_copy(5).start()
    for k, arrivals in ((1, (0,)), (2, (3,)), (3, (4, 5))):
        for i in arrivals:
            ag_copy(i).wait_recv()
        forget_chunk(k)
        project_chunk(k, 0)
    normed_copy = pltpu.make_async_copy(normed, normed_out, out_sem.at[4])
    normed_copy.start()
    for s in (2, 1):
        x_copy(s).wait_recv()
        c_copy(s).start()
    own_out[0].wait()
    z_out[0].wait_recv()

    @pl.when(owner)
    def _():
        own_out[1].wait()

    @pl.when(~owner)
    def _():
        z_out[1].wait_recv()

    x_out = remote(
        w_out_all.at[:, 0:part],
        w_out_all.at[:, part : 2 * part],
        x_send.at[3],
        x_recv.at[3],
        here.other("x"),
    )
    x_out.start()
    for s in (2, 1):
        c_copy(s).wait_recv()
        for k in range(peers):
            project_chunk(k, s)
    slots_copy = pltpu.make_async_copy(slot_w, slots_out, out_sem.at[5])
    slots_copy.start()
    finals = [
        pltpu.make_async_copy(project.at[s], projects[s], out_sem.at[6 + s]) for s in range(3)
    ] + [pltpu.make_async_copy(forget, forget_own, out_sem.at[9])]
    for copy in finals:
        copy.start()
    x_out.wait_recv()
    c_out = remote(
        w_out_all.at[:, 0:half],
        w_out_all.at[:, half:features],
        c_send.at[3],
        c_recv.at[3],
        here.other("c"),
    )
    c_out.start()

    on_group(1, lambda copy: copy.wait_send())

    @pl.when(away)
    def _():
        ints_copy().wait()
        for kind, rows_in in ((0, prompt_in), (1, cont_in)):

            @pl.when(x == kind)
            def _():
                for copy in group_copies(0, rows_in, True):
                    copy.wait_send()

    @pl.when(~away)
    def _():
        ints_own().wait()

    small_z.wait_send()
    small_over_x.wait_send()
    for i in range(4):
        z_piece(i, 2).wait_send()
    z_out[0].wait_send()

    @pl.when(owner)
    def _():
        for i in range(4):
            z_piece(i, 1).wait_send()
        z_out[1].wait_send()

    for s in range(3):
        x_copy(s).wait_send()
        c_copy(s).wait_send()
    x_out.wait_send()
    for i in range(6):
        ag_copy(i).wait_send()
    for k in range(peers):
        for s in range(3):
            kv_copy(k, s).wait()
        forget_copy(k).wait()
    c_out.wait()
    for copy in outs + finals + [normed_copy, slots_copy]:
        copy.wait()


def first_step(ring, prompt, cont, small, ints, wq, wg, wk, wv, w_out):
    local, half = prompt.shape
    features = 2 * half
    part = half // 2
    peers = len(ring.offsets)
    rows = peers * local
    slot = 4 * LANES
    any_spec = pl.BlockSpec(memory_space=pl.ANY)
    dma = pltpu.SemaphoreType.DMA
    shapes = [
        ((local, features), BF),
        ((rows, features), BF),
        ((3, features, slot), BF),
        ((3 * LANES, features), BF),
        ((2, 16, half), F32),
        ((16, features), F32),
        ((LANES, features), BF),
        (ints.shape, jnp.int32),
        ((rows, slot), BF),
        ((rows, slot), BF),
        ((rows, slot), BF),
        ((rows, LANES), BF),
        ((rows, 2 * LANES), BF),
        ((rows, 2 * LANES), BF),
        ((rows, 2 * LANES), BF),
        ((rows, LANES), BF),
    ]
    return pl.pallas_call(
        functools.partial(first_kernel, ring),
        out_shape=tuple(jax.ShapeDtypeStruct(*s) for s in shapes),
        in_specs=[any_spec] * 9,
        out_specs=[any_spec] * len(shapes),
        scratch_shapes=[
            pltpu.VMEM((local, features), BF),
            pltpu.VMEM((rows, features), BF),
            pltpu.VMEM((3, features, slot), BF),
            pltpu.VMEM((3, rows, slot), BF),
            pltpu.VMEM((rows, LANES), BF),
            pltpu.VMEM((2, 16, half), F32),
            pltpu.VMEM((2, 16, half), F32),
            pltpu.VMEM((2, 16, features), F32),
            pltpu.VMEM((16, features), F32),
            pltpu.VMEM((LANES, features), BF),
            dma((2, 2)),
            dma((2, 2)),
            dma,
            dma,
            dma((2,)),
            dma((2,)),
            dma((16,)),
            dma((3, 4)),
            dma((3, 4)),
            dma((4,)),
            dma((4,)),
            dma((4,)),
            dma((4,)),
            dma((6,)),
            dma((6,)),
            dma((peers, 4)),
            dma((peers, 4)),
            dma((10,)),
        ],
        compiler_params=pltpu.CompilerParams(
            collective_id=3, has_side_effects=True, vmem_limit_bytes=62 << 20
        ),
        cost_estimate=pl.CostEstimate(
            flops=2 * rows * features * 3 * slot, bytes_accessed=40 << 20, transcendentals=0
        ),
    )(prompt, cont, small, ints, wq, wg, wk, wv, w_out)


def ring_body(
    ring,
    x_prompt,
    x_cont,
    teacher_prompt,
    teacher_cont,
    segment_ids,
    offsets,
    prompt_valid,
    cont_valid,
    first_gain,
    w_query,
    w_key,
    w_value,
    w_outgate,
    w_forget,
    forget_bias,
    w_out,
    second_gain,
    w_gate,
    w_up,
    w_down,
):
    y = lax.axis_index("y")
    c = lax.axis_index("c")
    x = lax.axis_index("x")
    zh = lax.axis_index("zh")
    zl = lax.axis_index("zl")
    zl_count = ring.zl_count
    local = x_prompt.shape[1]
    half_d = x_prompt.shape[2]
    part_d = half_d // 2
    local_conts = x_cont.shape[1]
    heads = w_forget.shape[1]
    units_here = w_gate.shape[1]
    half_units = units_here // 2
    width = heads * HEAD_DIM
    slots = heads // 2
    pair_unit = PROMPT // CLEN
    chunk_units = local // CLEN
    own_valid = jnp.where(x == 0, prompt_valid.reshape(-1), cont_valid.reshape(-1))
    small_in = jnp.concatenate([own_valid, segment_ids.reshape(-1), offsets.reshape(-1)])
    int_rows = 16
    ints = jnp.pad(small_in, (0, int_rows * LANES - small_in.shape[0])).reshape(int_rows, LANES)
    packed = jnp.concatenate(
        [
            first_gain[None].astype(F32),
            second_gain[None].astype(F32),
            jnp.pad(forget_bias, (0, half_d - heads))[None],
            jnp.zeros((5, half_d), F32),
            w_forget.T.astype(F32),
            jnp.zeros((8 - heads, half_d), F32),
        ],
        axis=0,
    )
    (
        tokens_b,
        normed_all,
        w_slots,
        w_out_all,
        small_all,
        gains,
        w_forget_rows,
        ints,
        proj_a,
        proj_b,
        proj_c,
        forget_own,
        there_a,
        there_b,
        there_c,
        forget_there,
    ) = first_step(
        ring,
        x_prompt[0],
        x_cont.reshape(local_conts * CLEN, half_d),
        packed,
        ints,
        w_query,
        w_outgate,
        w_key,
        w_value,
        w_out,
    )
    projects = [proj_a, proj_b, proj_c]
    kv_there = [there_a, there_b, there_c]
    ints = ints.reshape(-1)
    validity = ints[:local].astype(F32)
    segment_row = ints[local : local + PROMPT]
    offset_row = ints[local + PROMPT : local + PROMPT + CONTS]
    gain_one = gains[0]
    gain_two = gains[1]

    def head_slots(value):
        first = jnp.where(y == 0, value[:, 0:2], value[:, 4:6])
        slot_a = jnp.where(zh == 0, first[0], first[1])
        slot_c = jnp.where(zh == 0, first[1], first[0])
        slot_b = jnp.where((y + zl) % 2 == 0, value[0, 2:4], value[1, 2:4])
        return jnp.concatenate([slot_a, slot_b, slot_c], axis=0)

    bias_all = small_all[:, 2, :heads]
    bias_all = jnp.stack(
        [
            jnp.where(zh == 0, bias_all[0], bias_all[1]),
            jnp.where(zh == 0, bias_all[1], bias_all[0]),
        ]
    )
    bias_row = head_slots(bias_all[:, :, None])[:, 0]
    bias_row = jnp.concatenate([bias_row, jnp.zeros((LANES - heads,), F32)])[None]

    proj_a, w_gate_late, w_up_late = lax.optimization_barrier((proj_a, w_gate, w_up))
    projects[0] = proj_a
    hid_there_w = ring.swap(
        jnp.concatenate(
            [
                lax.dynamic_slice(w, (c * part_d, y * half_units), (part_d, half_units))
                for w in (w_gate_late, w_up_late)
            ],
            axis=1,
        ),
        "zh",
    )

    dy_all = jnp.array([o[0] for o in ring.offsets], jnp.int32)
    dz_all = jnp.array([o[1] for o in ring.offsets], jnp.int32)
    places = ((y - dy_all) % 2) * zl_count + (zl - dz_all) % zl_count
    unit_no = (places[:, None] * chunk_units + jnp.arange(chunk_units, dtype=jnp.int32)).reshape(-1)
    natural = jnp.arange(pair_unit, dtype=jnp.int32)
    pick = unit_no[:, None] == natural[None, :]
    step = jnp.arange(CLEN, dtype=jnp.int32)
    row_pos = (unit_no[:, None] * CLEN + step[None, :]).reshape(-1)
    seg_rel = jnp.sum(
        jnp.where(pick[:, :, None], segment_row.reshape(1, pair_unit, CLEN), 0), axis=1
    )
    offs_rel = jnp.sum(jnp.where(pick, offset_row[None, :], 0), axis=1)
    last_rel = jnp.sum(
        jnp.where(
            jnp.arange(PROMPT, dtype=jnp.int32)[None, :] == offs_rel[:, None] - 1,
            segment_row[None, :],
            0,
        ),
        axis=1,
    )
    limit = jnp.where(c == 0, unit_no * CLEN, offs_rel)
    doc_row = jnp.where(c == 0, seg_rel, last_rel[:, None]).reshape(-1, 1)
    seg_col = seg_rel.reshape(-1, 1)
    lane = jnp.arange(LANES, dtype=jnp.int32)[None, :]
    unit_col = jnp.repeat(natural, CLEN)[:, None]
    pieces = 3 * heads
    is_doc = (lane >= DOC_LANE) & (lane < DOC_LANE + 4)
    is_unit = (lane >= UNIT_LANE) & (lane < UNIT_LANE + pair_unit)
    limit_lane = jnp.pad(limit, (UNIT_LANE, LANES - UNIT_LANE - pair_unit))[None, :]
    q_base = jnp.where(
        (lane >= FAR_PIECE) & (lane < FAR_PIECE + pieces),
        1.0,
        jnp.where(
            (is_doc & (doc_row != lane - DOC_LANE)) | (is_unit & (unit_col == lane - UNIT_LANE)),
            -NEVER,
            0.0,
        ),
    ).astype(BF)
    near_base = jnp.where(
        (lane < pieces) | (is_doc & (doc_row == lane - DOC_LANE)), 1.0, 0.0
    ).astype(BF)
    far_base = jnp.where(
        (lane < pieces)
        | (is_doc & (seg_col == lane - DOC_LANE))
        | (is_unit & (row_pos[:, None] >= limit_lane)),
        1.0,
        0.0,
    ).astype(BF)
    tri = (step[:, None] >= step[None, :]).astype(F32)
    earlier = (unit_no[None, :] < unit_no[:, None]).astype(F32)
    hot = (row_pos[None, :] == limit[:, None] - 1).astype(F32)
    cont_hot = (row_pos[None, :] == offs_rel[:, None] - 1).astype(F32)

    forget_far = jnp.where(c == 0, forget_own, forget_there)
    flag = c.astype(jnp.int32).reshape(1)
    head_lane = lane < heads

    def keep_log(lin):
        return jnp.where(head_lane, jax.nn.log_sigmoid(lin.astype(F32) + bias_row), 0.0)

    def within(values, matrix):
        return jnp.einsum(
            "ts,ush->uth", matrix, values.reshape(pair_unit, CLEN, LANES), precision=highest
        )

    far_within = within(keep_log(forget_far), tri)
    far_prefix = jnp.dot(earlier, far_within[:, -1], precision=highest)
    cum_far = (far_within + far_prefix[:, None]).reshape(-1, LANES)
    own_base = jnp.dot(hot, cum_far, precision=highest)
    cum_near = (within(keep_log(forget_own), tri) + own_base[:, None]).reshape(-1, LANES)
    keep_slope = jnp.where(
        head_lane, jax.nn.sigmoid(-(forget_own.astype(F32) + bias_row)), 0.0
    )
    gated, attended, logs = attend(
        flag, projects, kv_there, cum_near, cum_far, q_base, near_base, far_base, local, heads
    )
    (
        grad_gated,
        grad_residual,
        grad_residual_all,
        hid_kept,
        hid_there,
        down_kept,
        down_there,
        error_rows,
        gain_two_rows,
    ) = middle_step(
        ring,
        gated,
        w_out_all,
        w_gate,
        w_up,
        hid_there_w,
        w_down,
        tokens_b,
        teacher_prompt[0],
        teacher_cont.reshape(local_conts * CLEN, half_d),
        validity[:, None],
        gain_two[None],
    )
    dqg, dkv_near, dkv_far, row_sum, near_sum, far_sum = attend_back(
        flag,
        projects,
        kv_there,
        cum_near,
        cum_far,
        q_base,
        near_base,
        far_base,
        grad_gated,
        attended,
        logs,
        local,
        heads,
    )

    def low(value):
        return lax.reduce_precision(value, 8, 7).astype(BF)

    def over_zh(value, dim):
        size = value.shape[dim] // 2
        mine = lax.slice_in_dim(value, 0, size, axis=dim)
        theirs = lax.slice_in_dim(value, size, 2 * size, axis=dim)
        return low(mine + ring.swap(theirs.astype(BF), "zh").astype(F32))

    hid_mine = over_zh(hid_kept + hid_there.astype(F32), 1)
    down_there = ring.swap(down_there, "x")
    rows_back, proj_all, gate_all, up_all, down_all, out_all, small_sums = last_step(
        ring,
        heads,
        [
            dqg,
            dkv_near,
            dkv_far,
            row_sum,
            near_sum,
            far_sum,
            w_slots,
            normed_all,
            gated,
            grad_residual_all,
            tokens_b,
            grad_residual,
            hid_mine,
            down_kept,
            down_there,
        ],
        [
            gain_one[None],
            w_forget_rows,
            keep_slope,
            cont_hot.T,
            error_rows,
            gain_two_rows,
            validity[:, None],
        ],
    )
    gain_one_sum = small_sums[:, 0].reshape(-1)
    gain_two_sum = small_sums[:, 1].reshape(-1)
    sums = small_sums[0, 2]
    forget_grad = proj_all[:, 4 * width : 4 * width + heads]
    error_total = sums[0]
    count_total = sums[1]
    groups = ring.sizes["yo"] * ring.sizes["y"] * ring.sizes["c"]
    grad_scale = groups * (PROMPT + CONTS * CLEN) / count_total
    loss_value = error_total / (D * count_total)
    (
        prompt_grad,
        cont_grad,
        query_grad,
        outgate_grad,
        key_grad,
        value_grad,
        gate_grad,
        up_grad,
        down_grad,
        out_grad,
    ) = scale_step(
        float(groups * (PROMPT + CONTS * CLEN)),
        small_sums,
        rows_back,
        proj_all,
        gate_all,
        up_all,
        down_all,
        out_all,
    )

    def own_half(value):
        return lax.dynamic_slice_in_dim(value, x * half_d, half_d, value.ndim - 1)

    quarter_no = zh * zl_count + zl
    bias_out = lax.dynamic_slice_in_dim(sums, 2 + quarter_no * heads, heads, 0)

    def scaled(value):
        return value.astype(F32) * grad_scale

    return (
        loss_value,
        prompt_grad[None],
        cont_grad.reshape(1, local_conts, CLEN, half_d),
        scaled(own_half(gain_one_sum)),
        query_grad,
        key_grad,
        value_grad,
        outgate_grad,
        scaled(forget_grad),
        scaled(bias_out),
        out_grad,
        scaled(own_half(gain_two_sum)),
        gate_grad,
        up_grad,
        down_grad,
    )


def specs(dp, row, col):
    in_specs = (
        P(dp, col, row),
        P(dp, col, None, row),
        P(dp, col, row),
        P(dp, col, None, row),
        P(dp, None),
        P(dp, None),
        P(dp, col),
        P(dp, col, None),
        P(row),
        P(row, col),
        P(row, col),
        P(row, col),
        P(row, col),
        P(row, col),
        P(col),
        P(col, row),
        P(row),
        P(row, col),
        P(row, col),
        P(col, row),
    )
    out_specs = (
        P(),
        P(dp, col, row),
        P(dp, col, None, row),
        P(row),
        P(row, col),
        P(row, col),
        P(row, col),
        P(row, col),
        P(row, col),
        P(col),
        P(col, row),
        P(row),
        P(row, col),
        P(row, col),
        P(col, row),
    )
    return in_specs, out_specs


def solution(mesh):
    dp, row, col = mesh.shape["dp"], mesh.shape["row"], mesh.shape["col"]
    heads = HEADS // col
    if dp == 4 and row == 2 and col % 2 == 0 and heads == 6:
        sizes = {"yo": dp // 4, "y": 2, "c": 2, "x": 2, "zh": 2, "zl": col // 2}
        ring_mesh = Mesh(mesh.devices.reshape([sizes[a] for a in AX]), AX)
        in_specs, out_specs = specs(("yo", "y", "c"), "x", ("zh", "zl"))
        step = functools.partial(ring_body, Ring(sizes))
        return jax.shard_map(
            step, mesh=ring_mesh, in_specs=in_specs, out_specs=out_specs, check_vma=False
        )
    in_specs, out_specs = specs("dp", "row", "col")
    return jax.shard_map(
        wide_body, mesh=mesh, in_specs=in_specs, out_specs=out_specs, check_vma=False
    )
```

```python
import functools
import itertools

import jax
import jax.numpy as jnp
from jax import lax
from jax.experimental import pallas as pl
from jax.experimental.pallas import tpu as pltpu
from jax.sharding import Mesh, PartitionSpec as P

D = 1536
HEADS = 24
HEAD_DIM = 64
PROMPT = 1024
CONTS = 8
CLEN = 128


epsilon = 1e-06
highest = lax.Precision.HIGHEST
masked = -1e30


def matmul(left_op, right_op):
    return jnp.dot(left_op, right_op, preferred_element_type=jnp.float32)


def by_transpose(left_op, right_op):
    return lax.dot_general(
        left_op, right_op, (((1,), (1,)), ((), ())), preferred_element_type=jnp.float32
    )


def inner_rows(left_op, right_op):
    return lax.dot_general(
        left_op, right_op, (((0,), (0,)), ((), ())), preferred_element_type=jnp.float32
    )


def feature_total(partial_sum):
    return lax.psum(partial_sum, "row")


def group_rows(local_rows):
    return lax.all_gather(local_rows, "col", axis=0, tiled=True)


def token_sums(partial_rows):
    return lax.psum_scatter(
        partial_rows.astype(jnp.bfloat16), "col", scatter_dimension=0, tiled=True
    ).astype(jnp.float32)


def row_partials(partial_rows, col_count, blocks, quarter):
    shaped = partial_rows.reshape(
        col_count, blocks, lax.axis_size("row"), quarter, partial_rows.shape[-1]
    )
    return lax.psum_scatter(
        shaped.astype(jnp.bfloat16), "row", scatter_dimension=2, tiled=True
    ).astype(jnp.float32)


def head_rows(own_rows):
    gathered = lax.all_gather(own_rows, "row", axis=2, tiled=True)
    return gathered.reshape(-1, gathered.shape[-1])


def norm_forward(tokens, gain_vec):
    row_total = feature_total(jnp.sum(tokens * tokens, axis=-1))
    factor = lax.rsqrt(row_total / D + epsilon)
    scaled = tokens * factor[:, None]
    return (factor, scaled, (scaled * gain_vec).astype(jnp.bfloat16))


def norm_backward(grad_normed, factor, scaled, gain_vec):
    grad_scaled = grad_normed * gain_vec
    row_total = feature_total(jnp.sum(grad_scaled * scaled, axis=-1))
    gain_grad = jnp.sum(grad_normed * scaled, axis=0)
    return (gain_grad, factor[:, None] * (grad_scaled - scaled * (row_total / D)[:, None]))


def log_total(scores):
    row_top = jnp.max(scores, axis=-1, keepdims=True)
    return row_top + jnp.log(jnp.sum(jnp.exp(scores - row_top), axis=-1, keepdims=True))


def prompt_scores(queries, key_rows, cum_query, cum_key, allowed):
    raw_scores = jnp.einsum("qhd,khd->hqk", queries, key_rows, preferred_element_type=jnp.float32)
    raw_scores = raw_scores * HEAD_DIM ** (-0.5) + cum_query.T[:, :, None] - cum_key.T[:, None, :]
    return jnp.where(allowed[None], raw_scores, masked)


def cont_scores(queries, key_rows, key_cont, cum_query, cum_key, cum_cont, far_ok, near_ok):
    score_scale = HEAD_DIM ** (-0.5)
    query_cum = cum_query.transpose(0, 2, 1)[:, :, :, None]
    far_scores = jnp.einsum("jqhd,khd->jhqk", queries, key_rows, preferred_element_type=jnp.float32)
    far_scores = far_scores * score_scale + query_cum - cum_key.T[None, :, None, :]
    near_scores = jnp.einsum(
        "jqhd,jkhd->jhqk", queries, key_cont, preferred_element_type=jnp.float32
    )
    near_scores = near_scores * score_scale + query_cum - cum_cont.transpose(0, 2, 1)[:, :, None, :]
    far_scores = jnp.where(far_ok[:, None, None, :], far_scores, masked)
    near_scores = jnp.where(near_ok[None, None], near_scores, masked)
    return jnp.concatenate([far_scores, near_scores], axis=-1)


def wide_body(
    x_prompt,
    x_cont,
    teacher_prompt,
    teacher_cont,
    segment_ids,
    offsets,
    prompt_valid,
    cont_valid,
    first_gain,
    w_query,
    w_key,
    w_value,
    w_outgate,
    w_forget,
    forget_bias,
    w_out,
    second_gain,
    w_gate,
    w_up,
    w_down,
):
    row_count = lax.axis_size("row")
    col_count = lax.axis_size("col")
    row_index = lax.axis_index("row")
    local_prompt = x_prompt.shape[1]
    local_conts = x_cont.shape[1]
    quarter = CLEN // row_count
    local_tokens = local_prompt + local_conts * CLEN
    blocks = local_tokens // CLEN
    prompt_blocks = local_prompt // CLEN
    heads_here = w_forget.shape[1]
    width_here = heads_here * HEAD_DIM
    units_here = w_gate.shape[1]
    score_scale = HEAD_DIM ** (-0.5)
    w_project = jnp.concatenate([w_query, w_key, w_value, w_outgate], axis=1)
    w_hidden = jnp.concatenate([w_gate, w_up], axis=1)
    gain_one = first_gain.astype(jnp.float32)
    gain_two = second_gain.astype(jnp.float32)
    position = jnp.arange(PROMPT, dtype=jnp.int32)
    cont_step = jnp.arange(CLEN, dtype=jnp.int32)
    own_step = row_index * quarter + jnp.arange(quarter, dtype=jnp.int32)
    near_ok = cont_step[None, :] <= own_step[:, None]
    own_position = lax.dynamic_index_in_dim(
        position.reshape(col_count, prompt_blocks, row_count, quarter), row_index, 2, keepdims=False
    ).reshape(-1)

    def own_prompt_part(matrix):
        return matrix[:, :prompt_blocks, 0]

    def one_group(carried, group_data):
        (
            acc_project,
            acc_forget,
            acc_bias,
            acc_out,
            acc_hidden,
            acc_down,
            acc_gain_one,
            acc_gain_two,
            error_sum,
            count_sum,
        ) = carried
        (
            prompt_in,
            cont_in,
            teach_prompt,
            teach_cont,
            segment_row,
            offset_row,
            valid_prompt,
            valid_cont,
        ) = group_data
        tokens = jnp.concatenate(
            [prompt_in, cont_in.reshape(local_conts * CLEN, -1)], axis=0
        ).astype(jnp.float32)
        teacher = jnp.concatenate(
            [teach_prompt, teach_cont.reshape(local_conts * CLEN, -1)], axis=0
        ).astype(jnp.float32)
        validity = jnp.concatenate([valid_prompt, valid_cont.reshape(-1)], axis=0).astype(
            jnp.float32
        )
        branch_mask = position[None, :] == offset_row[:, None] - 1
        branch_hot = branch_mask.astype(jnp.float32)
        last_doc = jnp.sum(jnp.where(branch_mask, segment_row[None, :], 0), axis=1)
        far_ok = (position[None, :] < offset_row[:, None]) & (
            segment_row[None, :] == last_doc[:, None]
        )
        own_doc = lax.dynamic_index_in_dim(
            segment_row.reshape(col_count, prompt_blocks, row_count, quarter),
            row_index,
            2,
            keepdims=False,
        ).reshape(-1)
        prompt_ok = (position[None, :] <= own_position[:, None]) & (
            segment_row[None, :] == own_doc[:, None]
        )
        factor_one, scaled_one, normed_one = norm_forward(tokens, gain_one)
        normed_all = group_rows(normed_one)
        project_part = matmul(normed_all, w_project).reshape(
            col_count, blocks, row_count, quarter, 4 * width_here
        )
        forget_part = matmul(normed_all, w_forget).reshape(
            col_count, blocks, row_count, quarter, heads_here
        )
        own_project, own_forget = (
            lax.psum_scatter(project_part, "row", scatter_dimension=2, tiled=True),
            lax.psum_scatter(forget_part, "row", scatter_dimension=2, tiled=True),
        )
        own_query = own_project[..., :width_here].astype(jnp.bfloat16)
        own_kv = own_project[..., width_here : 3 * width_here].astype(jnp.bfloat16)
        gate_logit = own_project[..., 3 * width_here :]
        kv_all, forget_all = (
            lax.all_gather(own_kv, "row", axis=2, tiled=True),
            lax.all_gather(own_forget.astype(jnp.bfloat16), "row", axis=2, tiled=True),
        )
        kv_all = kv_all.reshape(col_count, local_tokens, 2 * width_here)
        pre_gate = (
            forget_all.reshape(col_count, local_tokens, heads_here).astype(jnp.float32)
            + forget_bias
        )
        log_keep = jax.nn.log_sigmoid(pre_gate)
        cum_prompt = jnp.cumsum(log_keep[:, :local_prompt].reshape(PROMPT, heads_here), axis=0)
        branch_cum = jnp.dot(branch_hot, cum_prompt, precision=highest)
        cum_cont = branch_cum[:, None, :] + jnp.cumsum(
            log_keep[:, local_prompt:].reshape(CONTS, CLEN, heads_here), axis=1
        )
        kv_prompt = kv_all[:, :local_prompt].reshape(PROMPT, 2, heads_here, HEAD_DIM)
        key_prompt = kv_prompt[:, 0]
        value_prompt = kv_prompt[:, 1]
        kv_cont = kv_all[:, local_prompt:].reshape(CONTS, CLEN, 2, heads_here, HEAD_DIM)
        key_cont = kv_cont[:, :, 0]
        value_cont = kv_cont[:, :, 1]
        cum_query_prompt = lax.dynamic_index_in_dim(
            cum_prompt.reshape(col_count, prompt_blocks, row_count, quarter, heads_here),
            row_index,
            2,
            keepdims=False,
        ).reshape(-1, heads_here)
        cum_query_cont = lax.dynamic_index_in_dim(
            cum_cont.reshape(CONTS, row_count, quarter, heads_here), row_index, 1, keepdims=False
        )
        query_prompt = own_prompt_part(own_query).reshape(-1, heads_here, HEAD_DIM)
        query_cont = own_query[:, prompt_blocks:, 0].reshape(CONTS, quarter, heads_here, HEAD_DIM)
        scores_prompt = prompt_scores(
            query_prompt, key_prompt, cum_query_prompt, cum_prompt, prompt_ok
        )
        total_prompt = log_total(scores_prompt)
        probs_prompt = jnp.exp(scores_prompt - total_prompt).astype(jnp.bfloat16)
        out_prompt = jnp.einsum(
            "hqk,khd->qhd", probs_prompt, value_prompt, preferred_element_type=jnp.float32
        )
        scores_cont = cont_scores(
            query_cont, key_prompt, key_cont, cum_query_cont, cum_prompt, cum_cont, far_ok, near_ok
        )
        total_cont = log_total(scores_cont)
        probs_cont = jnp.exp(scores_cont - total_cont).astype(jnp.bfloat16)
        out_cont = jnp.einsum(
            "jhqk,khd->jqhd",
            probs_cont[..., :PROMPT],
            value_prompt,
            preferred_element_type=jnp.float32,
        )
        out_cont = out_cont + jnp.einsum(
            "jhqk,jkhd->jqhd",
            probs_cont[..., PROMPT:],
            value_cont,
            preferred_element_type=jnp.float32,
        )
        attended = jnp.concatenate(
            [
                out_prompt.reshape(col_count, prompt_blocks, 1, quarter, width_here),
                out_cont.reshape(col_count, local_conts, 1, quarter, width_here),
            ],
            axis=1,
        )
        gate_sig = jax.nn.sigmoid(gate_logit)
        gated = (attended * gate_sig).astype(jnp.bfloat16)
        gated_all = head_rows(gated)
        residual = tokens + token_sums(matmul(gated_all, w_out))
        factor_two, scaled_two, normed_two = norm_forward(residual, gain_two)
        normed_two_all = group_rows(normed_two)
        hidden_own = row_partials(matmul(normed_two_all, w_hidden), col_count, blocks, quarter)
        gate_rows = hidden_own[..., :units_here]
        up_rows = hidden_own[..., units_here:]
        gate_sig_two = jax.nn.sigmoid(gate_rows)
        silu_rows = gate_rows * gate_sig_two
        hidden_all = head_rows((silu_rows * up_rows).astype(jnp.bfloat16))
        result_rows = residual + token_sums(matmul(hidden_all, w_down))
        deviation = result_rows - teacher
        group_err = 0.5 * jnp.sum(validity[:, None] * deviation * deviation)
        grad_result = validity[:, None] * deviation
        grad_result_all = group_rows(grad_result.astype(jnp.bfloat16))
        grad_down_w = inner_rows(hidden_all, grad_result_all)
        grad_hid = row_partials(by_transpose(grad_result_all, w_down), col_count, blocks, quarter)
        grad_gate = grad_hid * up_rows * gate_sig_two * (1.0 + gate_rows * (1.0 - gate_sig_two))
        grad_up = grad_hid * silu_rows
        grad_hidden_all = head_rows(
            jnp.concatenate([grad_gate, grad_up], axis=-1).astype(jnp.bfloat16)
        )
        grad_hidden_w = inner_rows(normed_two_all, grad_hidden_all)
        grad_normed_two = token_sums(by_transpose(grad_hidden_all, w_hidden))
        gain_two_grad, grad_residual = norm_backward(
            grad_normed_two, factor_two, scaled_two, gain_two
        )
        grad_residual = grad_residual + grad_result
        grad_residual_all = group_rows(grad_residual.astype(jnp.bfloat16))
        grad_out_w = inner_rows(gated_all, grad_residual_all)
        grad_gated = row_partials(
            by_transpose(grad_residual_all, w_out), col_count, blocks, quarter
        )
        grad_attended = (grad_gated * gate_sig).astype(jnp.bfloat16)
        grad_logit = (grad_gated * attended * gate_sig * (1.0 - gate_sig)).astype(jnp.bfloat16)
        grad_att_prompt = own_prompt_part(grad_attended).reshape(-1, heads_here, HEAD_DIM)
        grad_att_cont = grad_attended[:, prompt_blocks:, 0].reshape(
            CONTS, quarter, heads_here, HEAD_DIM
        )
        again_prompt = jnp.exp(
            prompt_scores(query_prompt, key_prompt, cum_query_prompt, cum_prompt, prompt_ok)
            - total_prompt
        )
        grad_prob_prompt = jnp.einsum(
            "qhd,khd->hqk", grad_att_prompt, value_prompt, preferred_element_type=jnp.float32
        )
        grad_score_prompt = (
            again_prompt
            * (grad_prob_prompt - jnp.sum(again_prompt * grad_prob_prompt, axis=-1, keepdims=True))
        ).astype(jnp.bfloat16)
        again_prompt_b = again_prompt.astype(jnp.bfloat16)
        grad_query_prompt = (
            jnp.einsum(
                "hqk,khd->qhd", grad_score_prompt, key_prompt, preferred_element_type=jnp.float32
            )
            * score_scale
        )
        grad_key_prompt = (
            jnp.einsum(
                "hqk,qhd->khd", grad_score_prompt, query_prompt, preferred_element_type=jnp.float32
            )
            * score_scale
        )
        grad_value_prompt = jnp.einsum(
            "hqk,qhd->khd", again_prompt_b, grad_att_prompt, preferred_element_type=jnp.float32
        )
        cum_grad_query_p = jnp.sum(grad_score_prompt, axis=-1, dtype=jnp.float32).T
        cum_grad_key_p = -jnp.sum(grad_score_prompt, axis=1, dtype=jnp.float32).T
        again_cont = jnp.exp(
            cont_scores(
                query_cont,
                key_prompt,
                key_cont,
                cum_query_cont,
                cum_prompt,
                cum_cont,
                far_ok,
                near_ok,
            )
            - total_cont
        )
        grad_prob_cont = jnp.concatenate(
            [
                jnp.einsum(
                    "jqhd,khd->jhqk",
                    grad_att_cont,
                    value_prompt,
                    preferred_element_type=jnp.float32,
                ),
                jnp.einsum(
                    "jqhd,jkhd->jhqk", grad_att_cont, value_cont, preferred_element_type=jnp.float32
                ),
            ],
            axis=-1,
        )
        grad_score_cont = (
            again_cont
            * (grad_prob_cont - jnp.sum(again_cont * grad_prob_cont, axis=-1, keepdims=True))
        ).astype(jnp.bfloat16)
        again_cont_b = again_cont.astype(jnp.bfloat16)
        far_grad = grad_score_cont[..., :PROMPT]
        near_grad = grad_score_cont[..., PROMPT:]
        grad_query_cont = (
            jnp.einsum("jhqk,khd->jqhd", far_grad, key_prompt, preferred_element_type=jnp.float32)
            + jnp.einsum("jhqk,jkhd->jqhd", near_grad, key_cont, preferred_element_type=jnp.float32)
        ) * score_scale
        grad_key_far = (
            jnp.einsum("jhqk,jqhd->khd", far_grad, query_cont, preferred_element_type=jnp.float32)
            * score_scale
        )
        grad_key_near = (
            jnp.einsum("jhqk,jqhd->jkhd", near_grad, query_cont, preferred_element_type=jnp.float32)
            * score_scale
        )
        grad_value_far = jnp.einsum(
            "jhqk,jqhd->khd",
            again_cont_b[..., :PROMPT],
            grad_att_cont,
            preferred_element_type=jnp.float32,
        )
        grad_value_near = jnp.einsum(
            "jhqk,jqhd->jkhd",
            again_cont_b[..., PROMPT:],
            grad_att_cont,
            preferred_element_type=jnp.float32,
        )
        cum_grad_query_c = jnp.sum(grad_score_cont, axis=-1, dtype=jnp.float32).transpose(0, 2, 1)
        cum_grad_key_far = -jnp.sum(far_grad, axis=(0, 2), dtype=jnp.float32).T
        cum_grad_key_near = -jnp.sum(near_grad, axis=2, dtype=jnp.float32).transpose(0, 2, 1)
        kv_grad_prompt = jnp.stack(
            [grad_key_prompt + grad_key_far, grad_value_prompt + grad_value_far], axis=1
        ).reshape(col_count, local_prompt, 2 * width_here)
        kv_grad_cont = jnp.stack([grad_key_near, grad_value_near], axis=2).reshape(
            col_count, local_conts * CLEN, 2 * width_here
        )
        kv_grad_part = jnp.concatenate([kv_grad_prompt, kv_grad_cont], axis=1)
        query_place = lax.dynamic_update_slice_in_dim(
            jnp.zeros((col_count, prompt_blocks, row_count, quarter, heads_here), jnp.float32),
            cum_grad_query_p.reshape(col_count, prompt_blocks, 1, quarter, heads_here),
            row_index,
            axis=2,
        ).reshape(PROMPT, heads_here)
        cont_place = lax.dynamic_update_slice_in_dim(
            jnp.zeros((CONTS, row_count, quarter, heads_here), jnp.float32),
            cum_grad_query_c.reshape(CONTS, 1, quarter, heads_here),
            row_index,
            axis=1,
        ).reshape(CONTS, CLEN, heads_here)
        cum_grad_part = jnp.concatenate(
            [
                (cum_grad_key_p + cum_grad_key_far + query_place).reshape(
                    col_count, local_prompt, heads_here
                ),
                (cum_grad_key_near + cont_place).reshape(col_count, local_conts * CLEN, heads_here),
            ],
            axis=1,
        )
        kv_grad_full, cum_grad_full = lax.psum((kv_grad_part, cum_grad_part), "row")
        cum_grad_cont = cum_grad_full[:, local_prompt:].reshape(CONTS, CLEN, heads_here)
        cum_grad_prompt = cum_grad_full[:, :local_prompt].reshape(PROMPT, heads_here)
        cum_grad_prompt = cum_grad_prompt + jnp.dot(
            branch_hot.T, jnp.sum(cum_grad_cont, axis=1), precision=highest
        )
        log_grad_prompt = lax.cumsum(cum_grad_prompt, axis=0, reverse=True)
        log_grad_cont = lax.cumsum(cum_grad_cont, axis=1, reverse=True)
        log_grad = jnp.concatenate(
            [
                log_grad_prompt.reshape(col_count, local_prompt, heads_here),
                log_grad_cont.reshape(col_count, local_conts * CLEN, heads_here),
            ],
            axis=1,
        )
        pre_grad = log_grad * jax.nn.sigmoid(-pre_gate)
        bias_grad = jnp.sum(pre_grad, axis=(0, 1))
        forget_grad_b = pre_grad.reshape(-1, heads_here).astype(jnp.bfloat16)
        query_grad_own = jnp.concatenate(
            [
                grad_query_prompt.reshape(col_count, prompt_blocks, 1, quarter, width_here),
                grad_query_cont.reshape(col_count, local_conts, 1, quarter, width_here),
            ],
            axis=1,
        )
        qg_grad_all = head_rows(
            jnp.concatenate([query_grad_own.astype(jnp.bfloat16), grad_logit], axis=-1)
        )
        kv_grad_rows = kv_grad_full.reshape(-1, 2 * width_here).astype(jnp.bfloat16)
        project_grad_rows = jnp.concatenate(
            [qg_grad_all[:, :width_here], kv_grad_rows, qg_grad_all[:, width_here:]], axis=-1
        )
        grad_project_w = inner_rows(normed_all, project_grad_rows)
        grad_forget_w = inner_rows(normed_all, forget_grad_b)
        grad_normed_one = token_sums(
            by_transpose(project_grad_rows, w_project) + by_transpose(forget_grad_b, w_forget)
        )
        gain_one_grad, grad_tokens = norm_backward(
            grad_normed_one, factor_one, scaled_one, gain_one
        )
        grad_tokens = grad_tokens + grad_residual
        grad_prompt_one = grad_tokens[:local_prompt]
        grad_cont_one = grad_tokens[local_prompt:].reshape(local_conts, CLEN, -1)
        group_count = jnp.sum(validity) * (row_index == 0).astype(jnp.float32)
        new_carry = (
            acc_project + grad_project_w,
            acc_forget + grad_forget_w,
            acc_bias + bias_grad,
            acc_out + grad_out_w,
            acc_hidden + grad_hidden_w,
            acc_down + grad_down_w,
            acc_gain_one + gain_one_grad,
            acc_gain_two + gain_two_grad,
            error_sum + group_err,
            count_sum + group_count,
        )
        return (new_carry, (grad_prompt_one, grad_cont_one))

    start = (
        jnp.zeros(w_project.shape, jnp.float32),
        jnp.zeros(w_forget.shape, jnp.float32),
        jnp.zeros(forget_bias.shape, jnp.float32),
        jnp.zeros(w_out.shape, jnp.float32),
        jnp.zeros(w_hidden.shape, jnp.float32),
        jnp.zeros(w_down.shape, jnp.float32),
        jnp.zeros(first_gain.shape, jnp.float32),
        jnp.zeros(second_gain.shape, jnp.float32),
        jnp.zeros((), jnp.float32),
        jnp.zeros((), jnp.float32),
    )
    finished, (grad_prompt, grad_cont) = lax.scan(
        one_group,
        start,
        (
            x_prompt,
            x_cont,
            teacher_prompt,
            teacher_cont,
            segment_ids,
            offsets,
            prompt_valid,
            cont_valid,
        ),
    )
    (
        acc_project,
        acc_forget,
        acc_bias,
        acc_out,
        acc_hidden,
        acc_down,
        acc_gain_one,
        acc_gain_two,
        error_sum,
        count_sum,
    ) = finished
    acc_project, acc_forget, acc_bias, acc_out, acc_hidden, acc_down = (
        lax.psum(acc_project.astype(jnp.bfloat16), "dp").astype(jnp.float32),
        lax.psum(acc_forget.astype(jnp.bfloat16), "dp").astype(jnp.float32),
        lax.psum(acc_bias.astype(jnp.bfloat16), "dp").astype(jnp.float32),
        lax.psum(acc_out.astype(jnp.bfloat16), "dp").astype(jnp.float32),
        lax.psum(acc_hidden.astype(jnp.bfloat16), "dp").astype(jnp.float32),
        lax.psum(acc_down.astype(jnp.bfloat16), "dp").astype(jnp.float32),
    )
    gain_one_total, gain_two_total = lax.psum((acc_gain_one, acc_gain_two), ("dp", "col"))
    error_total, count_total = lax.psum((error_sum, count_sum), ("dp", "row", "col"))
    grad_scale = x_prompt.shape[0] * lax.axis_size("dp") * (PROMPT + CONTS * CLEN) / count_total
    loss_value = error_total / (D * count_total)
    width_here = w_query.shape[1]
    units_here = w_gate.shape[1]
    return (
        loss_value,
        grad_prompt * grad_scale,
        grad_cont * grad_scale,
        gain_one_total * grad_scale,
        acc_project[:, :width_here] * grad_scale,
        acc_project[:, width_here : 2 * width_here] * grad_scale,
        acc_project[:, 2 * width_here : 3 * width_here] * grad_scale,
        acc_project[:, 3 * width_here :] * grad_scale,
        acc_forget * grad_scale,
        acc_bias * grad_scale,
        acc_out * grad_scale,
        gain_two_total * grad_scale,
        acc_hidden[:, :units_here] * grad_scale,
        acc_hidden[:, units_here:] * grad_scale,
        acc_down * grad_scale,
    )


AX = ("yo", "y", "c", "x", "zh", "zl")
FAR_PIECE = 18
DOC_LANE = 36
UNIT_LANE = 40
NEVER = 1e12
LANES = 128
BF = jnp.bfloat16
F32 = jnp.float32


class Ring:
    def __init__(self, sizes):
        self.sizes = sizes
        self.zl_count = sizes["zl"]
        self.offsets = [(dy, dz) for dy in range(2) for dz in range(self.zl_count)]
        self.back = [
            self.offsets.index(((-dy) % 2, (-dz) % self.zl_count)) for dy, dz in self.offsets
        ]

    def pairs(self, target, source_ok=None):
        ranges = [range(self.sizes[a]) for a in AX]
        number = {}
        for place, coords in enumerate(itertools.product(*ranges)):
            number[coords] = place
        out = []
        for coords in number:
            here = dict(zip(AX, coords))
            if source_ok is not None and not source_ok(here):
                continue
            there = dict(here, **target(here))
            out.append((number[coords], number[tuple(there[a] for a in AX)]))
        return out

    def move(self, value, target, source_ok=None):
        return lax.ppermute(value, AX, self.pairs(target, source_ok))

    def swap(self, value, axis, source_ok=None):
        return self.move(value, lambda h: {axis: 1 - h[axis]}, source_ok)

    def to_peer(self, value, k):
        dy, dz = self.offsets[k]
        return self.move(
            value, lambda h: {"y": (h["y"] + dy) % 2, "zl": (h["zl"] + dz) % self.zl_count}
        )

    def to_group(self, value, flip):
        return self.move(
            value,
            lambda h: {
                "y": h["zh"],
                "c": h["x"] ^ flip,
                "x": h["y"],
                "zh": h["c"],
            },
        )

    def from_group(self, value, flip):
        return self.move(
            value,
            lambda h: {"y": h["x"], "c": h["zh"], "x": h["c"] ^ flip, "zh": h["y"]},
        )

    def total(self, value):
        for axis in ("c", "y", "x", "zh"):
            value = value + self.swap(value, axis)
        if self.zl_count == 2:
            value = value + self.swap(value, "zl")
        elif self.zl_count > 2:
            value = lax.psum(value, "zl")
        if self.sizes["yo"] > 1:
            value = lax.psum(value, "yo")
        return value

    def gather(self, rows):
        return [rows] + [self.to_peer(rows, k) for k in range(1, len(self.offsets))]

    def scatter_sum(self, partial_of):
        arrived = []
        for k in range(1, len(self.offsets)):
            arrived.append(self.to_peer(partial_of(self.back[k]).astype(BF), k))
        total = partial_of(0)
        for part in arrived:
            total = total + part.astype(F32)
        return total


def nt_dot(left_op, right_op):
    return lax.dot_general(
        left_op, right_op, (((1,), (1,)), ((), ())), preferred_element_type=F32
    )


def tn_dot(left_op, right_op):
    return lax.dot_general(
        left_op, right_op, (((0,), (0,)), ((), ())), preferred_element_type=F32
    )


def nn_dot(left_op, right_op):
    return jnp.dot(left_op, right_op, preferred_element_type=F32)


def split_pieces(values, shift, heads):
    high = values.astype(BF).astype(F32)
    rest = values - high
    mid = rest.astype(BF).astype(F32)
    low = (rest - mid).astype(BF).astype(F32)
    out = None
    for place, piece in enumerate((high, mid, low)):
        amount = shift + place * heads
        moved = pltpu.roll(piece, amount, 1) if amount else piece
        out = moved if out is None else out + moved
    return out


def head_lanes(shape, head, heads):
    lane = lax.broadcasted_iota(jnp.int32, shape, len(shape) - 1)
    keep = lane >= DOC_LANE
    for place in range(3):
        keep = keep | (lane == place * heads + head) | (lane == FAR_PIECE + place * heads + head)
    return keep


def half_lanes(shape, half):
    lane = lax.broadcasted_iota(jnp.int32, shape, len(shape) - 1)
    return (lane >= HEAD_DIM * half) & (lane < HEAD_DIM * (half + 1))


def near_visible(rows):
    key_row = lax.broadcasted_iota(jnp.int32, (rows, rows), 0)
    query_row = lax.broadcasted_iota(jnp.int32, (rows, rows), 1)
    same = (key_row // CLEN) == (query_row // CLEN)
    return same & (key_row <= query_row)


def fill_keys(
    keys, flag, far_own, far_there, kv_near, cum_far, cum_near, far_base, near_base, far_rows, heads
):
    slots = heads // 2

    @pl.when(pl.program_id(0) == 0)
    def _():
        aug = (far_base[...].astype(F32) + split_pieces(-cum_far[...], FAR_PIECE, heads)).astype(BF)
        for s in range(slots):
            keys[s, :far_rows, LANES:] = aug

        @pl.when(flag[0] == 0)
        def _():
            for s in range(slots):
                keys[s, :far_rows, :LANES] = far_own[s][:, :LANES]

        @pl.when(flag[0] != 0)
        def _():
            for s in range(slots):
                keys[s, :far_rows, :LANES] = far_there[s][:, :LANES]

    aug = (near_base[...].astype(F32) + split_pieces(-cum_near[...], FAR_PIECE, heads)).astype(BF)
    for s in range(slots):
        keys[s, far_rows:, :LANES] = kv_near[s][:, :LANES]
        keys[s, far_rows:, LANES:] = aug


def attend_kernel(
    heads,
    flag,
    qg_a,
    qg_b,
    qg_c,
    near_a,
    near_b,
    near_c,
    own_a,
    own_b,
    own_c,
    there_a,
    there_b,
    there_c,
    cum_near,
    cum_far,
    q_base,
    near_base,
    far_base,
    gated_ref,
    att_ref,
    log_ref,
    keys,
    vals,
):
    qg = (qg_a, qg_b, qg_c)
    kv_near = (near_a, near_b, near_c)
    far_own = (own_a, own_b, own_c)
    far_there = (there_a, there_b, there_c)
    rows = qg_a.shape[0]
    far_rows = own_a.shape[0]
    slots = heads // 2
    fill_keys(
        keys,
        flag,
        far_own,
        far_there,
        kv_near,
        cum_far,
        cum_near,
        far_base,
        near_base,
        far_rows,
        heads,
    )

    @pl.when(pl.program_id(0) == 0)
    def _():
        def fill(source):
            for s in range(slots):
                moved = source[s][:, LANES:].T
                for half in range(2):
                    vals[2 * s + half, :HEAD_DIM, :far_rows] = moved[
                        HEAD_DIM * half : HEAD_DIM * (half + 1)
                    ]

        @pl.when(flag[0] == 0)
        def _():
            fill(far_own)

        @pl.when(flag[0] != 0)
        def _():
            fill(far_there)

        for h in range(heads):
            vals[h, HEAD_DIM:, :] = jnp.ones((16, far_rows + rows), BF)

    for s in range(slots):
        moved = kv_near[s][:, LANES:].T
        for half in range(2):
            vals[2 * s + half, :HEAD_DIM, far_rows:] = moved[
                HEAD_DIM * half : HEAD_DIM * (half + 1)
            ]
    q_aug = (q_base[...].astype(F32) + split_pieces(cum_near[...], 0, heads)).astype(BF)
    visible = near_visible(rows)
    outs = []
    logs = []
    for h in range(heads):
        s, half = h // 2, h % 2
        query = qg[s][:, :LANES]
        query = jnp.where(half_lanes(query.shape, half), query * BF(HEAD_DIM**-0.5), BF(0))
        aug = jnp.where(head_lanes(q_aug.shape, h, heads), q_aug, BF(0))
        q_cat = jnp.concatenate([query, aug], axis=1)
        far = nt_dot(keys[s, :far_rows], q_cat)
        near = jnp.where(visible, nt_dot(keys[s, far_rows:], q_cat), -NEVER)
        top = jnp.maximum(
            jnp.max(far, axis=0, keepdims=True), jnp.max(near, axis=0, keepdims=True)
        )
        far_p = jnp.exp(far - top).astype(BF)
        near_p = jnp.exp(near - top).astype(BF)
        out = nn_dot(vals[h, :, :far_rows], far_p) + nn_dot(vals[h, :, far_rows:], near_p)
        total = out[HEAD_DIM : HEAD_DIM + 1]
        outs.append(out[:HEAD_DIM] / total)
        logs.append(top + jnp.log(total))
    att = jnp.concatenate(outs, axis=0).T
    att_ref[...] = att
    for s in range(slots):
        gate = qg[s][:, LANES:].astype(F32)
        cols = slice(s * LANES, (s + 1) * LANES)
        gated_ref[:, cols] = (att[:, cols] * jax.nn.sigmoid(gate)).astype(BF)
    log_rows = jnp.concatenate(logs + [jnp.zeros((LANES - heads, rows), F32)], axis=0)
    log_ref[...] = log_rows.T


def row_block(rows, cols, place=0):
    return pl.BlockSpec((rows, cols), lambda i: (i, place))


def whole_block(rows, cols):
    return pl.BlockSpec((rows, cols), lambda i: (0, 0))


def slot_inputs(flag, projects, kv_there, rows):
    far_rows = projects[0].shape[0]
    specs_in = [pl.BlockSpec(memory_space=pltpu.SMEM)]
    for spec in (
        row_block(rows, 2 * LANES),
        row_block(rows, 2 * LANES, 1),
        pl.BlockSpec((far_rows, 2 * LANES), lambda i: (0, 1)),
        whole_block(far_rows, 2 * LANES),
    ):
        specs_in += [spec] * len(projects)
    return specs_in, [flag, *projects, *projects, *projects, *kv_there]


def cum_specs(rows, far_rows):
    return [
        row_block(rows, LANES),
        whole_block(far_rows, LANES),
        row_block(rows, LANES),
        row_block(rows, LANES),
        whole_block(far_rows, LANES),
    ]


def attend(flag, projects, kv_there, cum_near, cum_far, q_base, near_base, far_base, rows, heads):
    total = projects[0].shape[0]
    width = heads * HEAD_DIM
    steps = total // rows
    flops = 2 * total * (total + rows) * heads * 384
    slot_specs, slot_values = slot_inputs(flag, projects, kv_there, rows)
    return pl.pallas_call(
        functools.partial(attend_kernel, heads),
        grid=(steps,),
        out_shape=(
            jax.ShapeDtypeStruct((total, width), BF),
            jax.ShapeDtypeStruct((total, width), F32),
            jax.ShapeDtypeStruct((total, LANES), F32),
        ),
        in_specs=slot_specs + cum_specs(rows, total),
        out_specs=(row_block(rows, width), row_block(rows, width), row_block(rows, LANES)),
        scratch_shapes=[
            pltpu.VMEM((heads // 2, total + rows, 2 * LANES), BF),
            pltpu.VMEM((heads, HEAD_DIM + 16, total + rows), BF),
        ],
        compiler_params=pltpu.CompilerParams(vmem_limit_bytes=60 << 20),
        cost_estimate=pl.CostEstimate(
            flops=flops, bytes_accessed=total * width * 20, transcendentals=total * total * heads
        ),
    )(*slot_values, cum_near, cum_far, q_base, near_base, far_base)


def attend_back_kernel(
    heads,
    flag,
    qg_a,
    qg_b,
    qg_c,
    near_a,
    near_b,
    near_c,
    own_a,
    own_b,
    own_c,
    there_a,
    there_b,
    there_c,
    cum_near,
    cum_far,
    q_base,
    near_base,
    far_base,
    grad_ref,
    att_ref,
    log_ref,
    dqg_ref,
    near_ref,
    far_out,
    row_ref,
    near_col,
    far_col,
    keys,
    vals,
    far_ref,
):
    qg = (qg_a, qg_b, qg_c)
    kv_near = (near_a, near_b, near_c)
    far_own = (own_a, own_b, own_c)
    far_there = (there_a, there_b, there_c)
    rows = qg_a.shape[0]
    far_rows = own_a.shape[0]
    slots = heads // 2
    fill_keys(
        keys,
        flag,
        far_own,
        far_there,
        kv_near,
        cum_far,
        cum_near,
        far_base,
        near_base,
        far_rows,
        heads,
    )

    @pl.when(pl.program_id(0) == 0)
    def _():
        lane = lax.broadcasted_iota(jnp.int32, (far_rows + rows, LANES), 1)
        ones = (lane < 3).astype(F32).astype(BF)
        for s in range(slots):
            vals[s, :, LANES:] = ones

        @pl.when(flag[0] == 0)
        def _():
            for s in range(slots):
                vals[s, :far_rows, :LANES] = far_own[s][:, LANES:]

        @pl.when(flag[0] != 0)
        def _():
            for s in range(slots):
                vals[s, :far_rows, :LANES] = far_there[s][:, LANES:]

        far_ref[...] = jnp.zeros(far_ref.shape, F32)
        far_col[...] = jnp.zeros(far_col.shape, F32)

    for s in range(slots):
        vals[s, far_rows:, :LANES] = kv_near[s][:, LANES:]
    q_aug = (q_base[...].astype(F32) + split_pieces(cum_near[...] - log_ref[...], 0, heads)).astype(
        BF
    )
    visible = near_visible(rows)
    lane = lax.broadcasted_iota(jnp.int32, (rows, LANES), 1)
    row_total = jnp.zeros((rows, LANES), F32)
    col_total = jnp.zeros((rows, LANES), F32)
    for s in range(slots):
        cols = slice(s * LANES, (s + 1) * LANES)
        kcols = slice(2 * s * LANES, (2 * s + 1) * LANES)
        vcols = slice((2 * s + 1) * LANES, (2 * s + 2) * LANES)
        gate_sig = jax.nn.sigmoid(qg[s][:, LANES:].astype(F32))
        grad = grad_ref[:, cols].astype(F32)
        att = att_ref[:, cols]
        grad_att = (grad * gate_sig).astype(BF)
        dqg_ref[:, vcols] = (grad * att * gate_sig * (1.0 - gate_sig)).astype(BF)
        weighed = grad_att.astype(F32) * att
        dq_total = jnp.zeros((rows, LANES), F32)
        dk_near = jnp.zeros((rows, LANES), F32)
        dv_near = jnp.zeros((rows, LANES), F32)
        for half in range(2):
            h = 2 * s + half
            mine = half_lanes((rows, LANES), half)
            query = jnp.where(mine, qg[s][:, :LANES] * BF(HEAD_DIM**-0.5), BF(0))
            aug = jnp.where(head_lanes(q_aug.shape, h, heads), q_aug, BF(0))
            q_cat = jnp.concatenate([query, aug], axis=1)
            ga = jnp.where(mine, grad_att, BF(0))
            delta = -jnp.sum(jnp.where(mine, weighed, 0.0), axis=1, keepdims=True)
            high = delta.astype(BF).astype(F32)
            mid = (delta - high).astype(BF).astype(F32)
            low = delta - high - mid
            d_aug = jnp.where(
                lane == 0, high, jnp.where(lane == 1, mid, jnp.where(lane == 2, low, 0.0))
            ).astype(BF)
            ga_cat = jnp.concatenate([ga, d_aug], axis=1)
            for part in range(2):
                span = slice(0, far_rows) if part == 0 else slice(far_rows, far_rows + rows)
                prob = jnp.exp(nt_dot(keys[s, span], q_cat))
                if part == 1:
                    prob = jnp.where(visible, prob, 0.0)
                ds = (prob * nt_dot(vals[s, span], ga_cat)).astype(BF)
                dv = nn_dot(prob.astype(BF), ga)
                dk = nn_dot(ds, q_cat)
                dq = tn_dot(ds, keys[s, span])
                dq_total += jnp.where(mine, dq[:, :LANES], 0.0)
                row_total += jnp.where(lane == h, dq[:, LANES:], 0.0)
                if part == 0:
                    far_ref[:, kcols] += dk[:, :LANES]
                    far_ref[:, vcols] += dv
                    far_col[...] += dk[:, LANES:]
                else:
                    dk_near += dk[:, :LANES]
                    dv_near += dv
                    col_total += dk[:, LANES:]
        dqg_ref[:, kcols] = (dq_total * HEAD_DIM**-0.5).astype(BF)
        near_ref[:, kcols] = dk_near
        near_ref[:, vcols] = dv_near
    row_ref[...] = row_total
    near_col[...] = col_total

    @pl.when(pl.program_id(0) == pl.num_programs(0) - 1)
    def _():
        far_out[...] = far_ref[...].astype(BF)


def attend_back(
    flag,
    projects,
    kv_there,
    cum_near,
    cum_far,
    q_base,
    near_base,
    far_base,
    grad,
    att,
    logs,
    rows,
    heads,
):
    total = projects[0].shape[0]
    width = heads * HEAD_DIM
    steps = total // rows
    flops = 2 * total * (total + rows) * heads * 1152
    slot_specs, slot_values = slot_inputs(flag, projects, kv_there, rows)
    return pl.pallas_call(
        functools.partial(attend_back_kernel, heads),
        grid=(steps,),
        out_shape=(
            jax.ShapeDtypeStruct((total, 2 * width), BF),
            jax.ShapeDtypeStruct((total, 2 * width), F32),
            jax.ShapeDtypeStruct((total, 2 * width), BF),
            jax.ShapeDtypeStruct((total, LANES), F32),
            jax.ShapeDtypeStruct((total, LANES), F32),
            jax.ShapeDtypeStruct((total, LANES), F32),
        ),
        in_specs=slot_specs
        + cum_specs(rows, total)
        + [row_block(rows, width), row_block(rows, width), row_block(rows, LANES)],
        out_specs=(
            row_block(rows, 2 * width),
            row_block(rows, 2 * width),
            whole_block(total, 2 * width),
            row_block(rows, LANES),
            row_block(rows, LANES),
            whole_block(total, LANES),
        ),
        scratch_shapes=[
            pltpu.VMEM((heads // 2, total + rows, 2 * LANES), BF),
            pltpu.VMEM((heads // 2, total + rows, 2 * LANES), BF),
            pltpu.VMEM((total, 2 * width), F32),
        ],
        compiler_params=pltpu.CompilerParams(vmem_limit_bytes=60 << 20),
        cost_estimate=pl.CostEstimate(
            flops=flops, bytes_accessed=total * width * 40, transcendentals=total * total * heads
        ),
    )(*slot_values, cum_near, cum_far, q_base, near_base, far_base, grad, att, logs)


def full_norm(tokens, gain_vec):
    factor = lax.rsqrt(jnp.mean(tokens * tokens, axis=-1, keepdims=True) + epsilon)
    scaled = tokens * factor
    return factor, scaled, (scaled * gain_vec).astype(BF)


def full_norm_back(grad_normed, factor, scaled, gain_vec):
    e = grad_normed * gain_vec
    mean = jnp.mean(e * scaled, axis=-1, keepdims=True)
    return jnp.sum(grad_normed * scaled, axis=0), factor * (e - scaled * mean)


MESH_ID = pl.DeviceIdType.MESH


class Here:
    def __init__(self, ring):
        self.ring = ring
        self.at = {a: lax.axis_index(a) for a in AX}

    def other(self, axis):
        return {axis: 1 - self.at[axis]}

    def mid_home(self):
        return lax.rem(self.at["y"] + self.at["zl"], 2)

    def peer(self, k):
        dy, dz = self.ring.offsets[k]
        return {
            "y": lax.rem(self.at["y"] + dy, 2),
            "zl": lax.rem(self.at["zl"] + dz, self.ring.zl_count),
        }

    def group_to(self, flip):
        at = self.at
        return {"y": at["zh"], "c": at["x"] ^ flip, "x": at["y"], "zh": at["c"]}

    def group_from(self, flip):
        at = self.at
        return {"y": at["x"], "c": at["zh"], "x": at["c"] ^ flip, "zh": at["y"]}

    def group_away(self):
        at = self.at
        return ~((at["y"] == at["zh"]) & (at["y"] == at["x"]) & (at["y"] == at["c"]))

    def greet_group(self, targets):
        away = self.group_away()
        self.greet(
            targets + [self.group_to(1), self.group_from(1)],
            [(self.group_to(0), away), (self.group_from(0), away)],
        )

    def greet(self, targets, extra=()):
        barrier = pltpu.get_barrier_semaphore()
        for target in targets:
            pl.semaphore_signal(barrier, inc=1, device_id=target, device_id_type=MESH_ID)
        count = len(targets)
        for target, away in extra:
            @pl.when(away)
            def _():
                pl.semaphore_signal(barrier, inc=1, device_id=target, device_id_type=MESH_ID)

            count = count + away.astype(jnp.int32)
        pl.semaphore_wait(barrier, count)


def remote(src, dst, send_sem, recv_sem, target):
    return pltpu.make_async_remote_copy(
        src_ref=src,
        dst_ref=dst,
        send_sem=send_sem,
        recv_sem=recv_sem,
        device_id=target,
        device_id_type=MESH_ID,
    )


def last_kernel(
    ring,
    heads,
    dqg_in,
    near_in,
    far_in,
    row_in,
    near_col_in,
    far_col_in,
    weight_in,
    normed_in,
    gated_in,
    mixed_in,
    tokens_in,
    residual_in,
    hid_kept_in,
    hid_there_in,
    hid_z_in,
    down_kept_in,
    down_there_in,
    gain_ref,
    forget_w,
    sig_ref,
    hot_ref,
    error_ref,
    gain_two_ref,
    valid_ref,
    back_out,
    proj_out,
    gate_out,
    up_out,
    down_out,
    out_out,
    small_out,
    grads,
    near,
    far_own,
    far_land,
    row_sum,
    near_col,
    far_col,
    far_col_land,
    cum,
    tot_send,
    tot_land,
    weight,
    normed,
    gated,
    mixed,
    tokens,
    residual,
    rs_send,
    rs_land,
    total,
    c_send,
    c_land,
    cf_send,
    cf_land,
    kept,
    x_send,
    x_land,
    z_send,
    z_land,
    final,
    kept_f,
    xf_send,
    xf_land,
    zf_send,
    zf_land,
    final_f,
    yf_land,
    full_f,
    co_send,
    co_land,
    kept_h,
    there_h,
    z_h,
    final_h,
    kept_d,
    there_d,
    zd_send,
    zd_land,
    final_d,
    kept_o,
    xo_send,
    xo_land,
    zo_send,
    zo_land,
    final_o,
    blocks,
    gain_sum,
    gain_nat,
    gain_land,
    load_sem,
    local_sem,
    swap_send_sem,
    swap_recv_sem,
    y_send_sem,
    y_recv_sem,
    c2_send_sem,
    c2_recv_sem,
    rs_send_sem,
    rs_recv_sem,
    c_send_sem,
    c_recv_sem,
    x_send_sem,
    x_recv_sem,
    z_send_sem,
    z_recv_sem,
    back_send_sem,
    back_recv_sem,
    gain_send_sem,
    gain_recv_sem,
):
    here = Here(ring)
    y, c, x, zh, zl = (here.at[a] for a in ("y", "c", "x", "zh", "zl"))
    local, features = tokens.shape
    rows_all = normed.shape[0]
    part = features // 4
    slot_w = 4 * LANES
    slots = heads // 2
    all_w = slots * slot_w
    units = down_kept_in.shape[0] // 2
    owner = zh == here.mid_home()
    peers = len(ring.offsets)
    away = here.group_away()
    all_loads = [
        (row_in, row_sum),
        (near_col_in, near_col),
        (far_col_in, far_col),
        (far_in, far_own),
        (near_in, near),
    ]
    for s in range(slots):
        all_loads.append(
            (
                dqg_in.at[:, 2 * s * LANES : 2 * (s + 1) * LANES],
                grads.at[:, s * slot_w : s * slot_w + 2 * LANES],
            )
        )
    all_loads += [
        (hid_kept_in.at[:, : 2 * units], kept_h),
        (hid_there_in.at[:, : 2 * units], there_h),
        (hid_z_in, z_h),
        (down_kept_in, kept_d),
        (down_there_in, there_d),
        (normed_in, normed),
        (weight_in, weight),
        (gated_in, gated),
        (mixed_in, mixed),
        (tokens_in, tokens),
        (residual_in, residual),
    ]
    loads = [
        pltpu.make_async_copy(a, b, load_sem.at[i]) for i, (a, b) in enumerate(all_loads)
    ]
    first_loads = 11 + slots
    for copy in loads[:first_loads]:
        copy.start()
    load_row, load_near_col, load_far_col, load_far, load_near = loads[:5]
    load_dqg = loads[5 : 5 + slots]
    load_hid = loads[5 + slots : 8 + slots]
    load_kept_d, load_there_d = loads[8 + slots : 10 + slots]
    load_normed, load_weight, load_gated, load_mixed, load_tokens, load_residual = loads[10 + slots :]

    here.greet_group(
        [here.peer(k) for k in range(1, peers)]
        + [here.other("c"), here.other("x"), here.other("zh")]
    )
    far_swap = remote(
        far_in, far_land, swap_send_sem.at[0], swap_recv_sem.at[0], here.other("c")
    )
    far_swap.start()
    col_swap = remote(
        far_col_in, far_col_land, swap_send_sem.at[1], swap_recv_sem.at[1], here.other("c")
    )
    col_swap.start()

    row0 = pl.multiple_of(c * part, part)

    def rows_of(ref, col, width):
        return ref.at[pl.ds(row0, part), pl.ds(pl.multiple_of(col, LANES), width)]

    def cols_of(ref, row, height):
        return ref.at[pl.ds(pl.multiple_of(row, LANES), height), pl.ds(row0, part)]

    def y_copy(i, src, dst):
        return remote(src, dst, y_send_sem.at[i], y_recv_sem.at[i], here.other("y"))

    pieces = [
        (final_h.at[0], rows_of(gate_out, y * units, units)),
        (final_h.at[1], rows_of(up_out, y * units, units)),
        (final_d, cols_of(down_out, y * units, units)),
    ]
    own_pieces = [
        pltpu.make_async_copy(src, dst, local_sem.at[i]) for i, (src, dst) in enumerate(pieces)
    ]
    y_pieces = [y_copy(i, src, dst) for i, (src, dst) in enumerate(pieces)]
    for copy in load_hid:
        copy.wait()
    for i in range(2):
        cols = slice(i * units, (i + 1) * units)
        final_h[i] = (
            kept_h[:, cols] + there_h[:, cols].astype(F32) + z_h[:, cols].astype(F32)
        ).astype(BF)
    for copy in own_pieces[:2] + y_pieces[:2]:
        copy.start()

    lane = lax.broadcasted_iota(jnp.int32, (CLEN, LANES), 1)
    head_lane = lane < heads
    all_units = rows_all // CLEN
    chunk_units = local // CLEN

    def unit_rows(u):
        return slice(u * CLEN, (u + 1) * CLEN)

    load_row.wait()
    load_near_col.wait()
    for u in range(all_units):
        value = row_sum[unit_rows(u), :] - pltpu.roll(
            near_col[unit_rows(u), :], LANES - FAR_PIECE, 1
        )
        value = jnp.where(head_lane, value, 0.0)
        cum[unit_rows(u), :] = value
        tot_send[u : u + 1, :] = jnp.sum(value, axis=0, keepdims=True)
    tot_swap = remote(
        tot_send.at[:all_units],
        tot_land.at[:all_units],
        swap_send_sem.at[2],
        swap_recv_sem.at[2],
        here.other("c"),
    )
    tot_swap.start()

    load_kept_d.wait()
    load_there_d.wait()
    zd_send[...] = (kept_d[units:, :] + there_d[units:, :].astype(F32)).astype(BF)
    zd_copy = remote(zd_send, zd_land, z_send_sem.at[5], z_recv_sem.at[5], here.other("zh"))
    zd_copy.start()

    load_far.wait()
    load_near.wait()
    for copy in load_dqg:
        copy.wait()
    for copy in loads[first_loads:]:
        copy.start()
    far_swap.wait_recv()
    on_prompt = jnp.where(c == 0, 1.0, 0.0)

    def merge(i, carry):
        rows = pl.ds(pl.multiple_of(i * CLEN, CLEN), CLEN)
        value = near[rows, :] + on_prompt * (
            far_own[rows, :].astype(F32) + far_land[rows, :].astype(F32)
        )
        value = value.astype(BF)
        for s in range(slots):
            grads[rows, s * slot_w + 2 * LANES : (s + 1) * slot_w] = value[
                :, 2 * s * LANES : 2 * (s + 1) * LANES
            ]
        return carry

    lax.fori_loop(0, all_units, merge, 0)
    load_normed.wait()
    tile_r = LANES
    per_part = part // tile_r

    def weight_tile(first, i):
        cols = pl.ds(pl.multiple_of(first + i * tile_r, LANES), tile_r)
        return tn_dot(normed[:, cols], grads[:, :all_w])

    def forget_tile(first, i):
        cols = pl.ds(pl.multiple_of(first + i * tile_r, LANES), tile_r)
        return tn_dot(normed[:, cols], grads[:, all_w:])

    def c_step(i, carry):
        rows = pl.ds(pl.multiple_of(i * tile_r, tile_r), tile_r)
        c_send[rows, :] = weight_tile(2 * part, i).astype(BF)
        return carry

    lax.fori_loop(0, 2 * per_part, c_step, 0)
    c_copy = remote(c_send, c_land, c_send_sem.at[0], c_recv_sem.at[0], here.other("c"))
    c_copy.start()

    load_far_col.wait()
    col_swap.wait_recv()
    tot_swap.wait_recv()

    @pl.when(c == 0)
    def _():
        for u in range(all_units):
            both = far_col[unit_rows(u), :] + far_col_land[unit_rows(u), :]
            value = cum[unit_rows(u), :] - jnp.where(
                head_lane, pltpu.roll(both, LANES - FAR_PIECE, 1), 0.0
            )
            for j in range(all_units):
                value = value + hot_ref[unit_rows(u), j : j + 1] * tot_land[j : j + 1, :]
            cum[unit_rows(u), :] = value

    step_row = lax.broadcasted_iota(jnp.int32, (CLEN, CLEN), 0)
    step_col = lax.broadcasted_iota(jnp.int32, (CLEN, CLEN), 1)
    tri_back = (step_col >= step_row).astype(F32)
    for u in range(all_units):
        value = jnp.dot(
            tri_back,
            cum[unit_rows(u), :],
            precision=highest,
            preferred_element_type=F32,
        )
        cum[unit_rows(u), :] = value
        tot_send[all_units + u : all_units + u + 1, :] = value[0:1, :]
    places = []
    for dy, dz in ring.offsets:
        place = lax.rem(y + 2 - dy, 2) * ring.zl_count + lax.rem(
            zl + ring.zl_count - dz, ring.zl_count
        )
        for i in range(chunk_units):
            places.append(place * chunk_units + i)
    bias = jnp.zeros((1, LANES), F32)
    for u in range(all_units):
        suffix = jnp.zeros((1, LANES), F32)
        for other in range(all_units):
            if other != u:
                seen = jnp.where((places[other] > places[u]) & (c == 0), 1.0, 0.0)
                suffix = suffix + seen * tot_send[all_units + other : all_units + other + 1, :]
        value = (cum[unit_rows(u), :] + suffix) * sig_ref[unit_rows(u), :]
        grads[unit_rows(u), all_w:] = value.astype(BF)
        bias = bias + jnp.sum(value, axis=0, keepdims=True)

    zd_copy.wait_recv()
    final_d[...] = (
        kept_d[:units, :] + there_d[:units, :].astype(F32) + zd_land[...].astype(F32)
    ).astype(BF)
    for copy in own_pieces[2:] + y_pieces[2:]:
        copy.start()

    c_copy.wait_recv()

    def x_step(i, carry):
        rows = pl.ds(pl.multiple_of(i * tile_r, tile_r), tile_r)
        land = pl.ds(pl.multiple_of(part + i * tile_r, tile_r), tile_r)
        value = weight_tile(part, i) + c_land[land, :].astype(F32)
        for s in range(slots):
            x_send[s, rows, :] = value[:, s * slot_w : (s + 1) * slot_w].astype(BF)
        return carry

    lax.fori_loop(0, per_part, x_step, 0)
    x_copies = {}
    for s in (2, 1, 0):
        x_copies[s] = remote(
            x_send.at[s], x_land.at[s], x_send_sem.at[s], x_recv_sem.at[s], here.other("x")
        )
        x_copies[s].start()
    load_weight.wait()
    tiles = 3
    tile_w = features // tiles

    def partial_rows(chunk_no, store):
        rows = slice(chunk_no * local, (chunk_no + 1) * local)

        def step(i, carry):
            cols = pl.ds(pl.multiple_of(i * tile_w, LANES), tile_w)
            value = nn_dot(grads[rows, all_w:], forget_w[:, cols])
            for s in range(slots):
                value = value + nt_dot(
                    grads[rows, s * slot_w : (s + 1) * slot_w], weight[s, cols, :]
                )
            store(cols, value)
            return carry

        lax.fori_loop(0, tiles, step, 0)

    moves = RingRows(here, local)

    def rs_copy(i):
        return moves.sum_copy(rs_send, rs_land, rs_send_sem, rs_recv_sem, i)

    for k in (3, 1, 2):

        def store_out(cols, value, k=k):
            rs_send[k - 1, :, cols] = value.astype(BF)

        partial_rows(k, store_out)
        for i in SUM_STARTS[k]:
            rs_copy(i).start()

    def cf_step(i, carry):
        rows = pl.ds(pl.multiple_of(i * tile_r, tile_r), tile_r)
        cf_send[rows, :] = forget_tile(2 * part, i).astype(BF)
        return carry

    lax.fori_loop(0, 2 * per_part, cf_step, 0)
    cf_copy = remote(cf_send, cf_land, c_send_sem.at[2], c_recv_sem.at[2], here.other("c"))
    cf_copy.start()

    load_gated.wait()
    load_mixed.wait()
    out_rows = slots * LANES

    def out_tile(s, cols):
        return tn_dot(gated[:, s * LANES : (s + 1) * LANES], mixed[:, cols])

    for s in range(slots):
        co_send[s * LANES : (s + 1) * LANES, :] = out_tile(
            s, slice(2 * part, features)
        ).astype(BF)
    co_copy = remote(co_send, co_land, c_send_sem.at[1], c_recv_sem.at[1], here.other("c"))
    co_copy.start()

    cf_copy.wait_recv()

    def xf_step(i, carry):
        rows = pl.ds(pl.multiple_of(i * tile_r, tile_r), tile_r)
        land = pl.ds(pl.multiple_of(part + i * tile_r, tile_r), tile_r)
        xf_send[rows, :] = (forget_tile(part, i) + cf_land[land, :].astype(F32)).astype(BF)
        return carry

    lax.fori_loop(0, per_part, xf_step, 0)
    xf_copy = remote(xf_send, xf_land, x_send_sem.at[3], x_recv_sem.at[3], here.other("x"))
    xf_copy.start()
    co_copy.wait_recv()
    for s in range(slots):
        rows = slice(s * LANES, (s + 1) * LANES)
        xo_send[rows, :] = (
            out_tile(s, slice(part, 2 * part)) + co_land[rows, part:].astype(F32)
        ).astype(BF)
    xo_copy = remote(xo_send, xo_land, x_send_sem.at[4], x_recv_sem.at[4], here.other("x"))
    xo_copy.start()

    def own_step(i, carry):
        rows = pl.ds(pl.multiple_of(i * tile_r, tile_r), tile_r)
        value = weight_tile(0, i) + c_land[rows, :].astype(F32)
        for s in range(slots):
            kept[s, rows, :] = value[:, s * slot_w : (s + 1) * slot_w]
        kept_f[rows, :] = forget_tile(0, i) + cf_land[rows, :].astype(F32)
        return carry

    lax.fori_loop(0, per_part, own_step, 0)
    for s in range(slots):
        rows = slice(s * LANES, (s + 1) * LANES)
        kept_o[rows, :] = out_tile(s, slice(0, part)) + co_land[rows, :part].astype(F32)

    def store_own(cols, value):
        total[:, cols] = value

    partial_rows(0, store_own)

    def z_copy(i, src, dst):
        return remote(src, dst, z_send_sem.at[i], z_recv_sem.at[i], here.other("zh"))

    z_first = z_copy(0, z_send.at[0], z_land.at[0])
    z_mid = z_copy(1, z_send.at[1], z_land.at[1])
    z_forget = z_copy(2, zf_send, zf_land)
    zo_first = z_copy(3, zo_send.at[0], zo_land.at[0])
    zo_mid = z_copy(4, zo_send.at[1], zo_land.at[1])
    moves.hand_on(rs_send, rs_land, rs_send_sem, rs_recv_sem)
    x_copies[2].wait_recv()
    z_send[0] = (kept[2] + x_land[2].astype(F32)).astype(BF)
    z_first.start()
    x_copies[1].wait_recv()

    @pl.when(~owner)
    def _():
        z_send[1] = (kept[1] + x_land[1].astype(F32)).astype(BF)
        z_mid.start()


    load_tokens.wait()
    load_residual.wait()
    for i in (0, 2, 4, 5):
        rs_copy(i).wait_recv()
    gain_sum[...] = jnp.zeros(gain_sum.shape, F32)
    tile_n = 32

    def norm_step(i, carry):
        rows = pl.ds(pl.multiple_of(i * tile_n, tile_n), tile_n)
        tok = tokens[rows, :].astype(F32)
        grad = total[rows, :]
        for k in (0, 2):
            grad = grad + rs_land[k, rows, :].astype(F32)
        factor = lax.rsqrt(jnp.mean(tok * tok, axis=-1, keepdims=True) + epsilon)
        scaled_tok = tok * factor
        e = grad * gain_ref[...]
        mean = jnp.mean(e * scaled_tok, axis=-1, keepdims=True)
        out = factor * (e - scaled_tok * mean) + residual[rows, :]
        weighed = jnp.sum(grad * scaled_tok, axis=0, keepdims=True)
        for b in range(4):
            blocks[b, rows, :] = out[:, b * part : (b + 1) * part].astype(BF)
            gain_sum[b, 0:1, :] += weighed[:, b * part : (b + 1) * part]
        return carry

    lax.fori_loop(0, local // tile_n, norm_step, 0)

    def block_no(half, low_high):
        return (half ^ x) + 2 * (low_high ^ c)

    def back_copy(flip, p):
        return remote(
            blocks.at[block_no(c ^ flip, p)],
            back_out.at[c, :, p * part : (p + 1) * part],
            back_send_sem.at[flip, p],
            back_recv_sem.at[flip, p],
            here.group_from(flip),
        )

    def back_own(flip, p):
        return pltpu.make_async_copy(
            blocks.at[block_no(c ^ flip, p)],
            back_out.at[c, :, p * part : (p + 1) * part],
            local_sem.at[5 + p],
        )

    for p in range(2):
        back_copy(1, p).start()

    @pl.when(away)
    def _():
        for p in range(2):
            back_copy(0, p).start()

    @pl.when(~away)
    def _():
        for p in range(2):
            back_own(0, p).start()

    for b in range(4):
        gain_sum[b, 1:2, :] = gain_two_ref[0:1, b * part : (b + 1) * part]
    for b in range(4):
        gain_nat[0, b] = gain_sum[block_no(b // 2, b % 2)]
    wide_lane = lax.broadcasted_iota(jnp.int32, (1, part), 1)
    scalars = jnp.where(
        wide_lane == 0, jnp.sum(error_ref[0:1, :], axis=1, keepdims=True), 0.0
    ) + jnp.where(wide_lane == 1, jnp.sum(valid_ref[...], axis=0, keepdims=True), 0.0)
    small_lane = lax.broadcasted_iota(jnp.int32, (1, LANES), 1)
    for j in range(heads):
        if j < 2:
            quarter, head = zh, 4 * y + j
        elif j < 4:
            quarter, head = here.mid_home(), j
        else:
            quarter, head = 1 - zh, 4 * y + j - 4
        dest = 2 + (quarter * ring.zl_count + zl) * heads + head
        value = jnp.sum(jnp.where(small_lane == j, bias, 0.0), axis=1, keepdims=True)
        scalars = scalars + jnp.where(wide_lane == dest, value, 0.0)
    gain_nat[0, 0, 2:3, :] = scalars
    gain_axes = ("c", "y", "x", "zl", "zh")

    def gain_step(place):
        return remote(
            gain_nat.at[place],
            gain_land.at[place],
            gain_send_sem.at[place],
            gain_recv_sem.at[place],
            here.other(gain_axes[place]),
        )

    def gain_next(place):
        gain_step(place).wait_recv()
        gain_nat[place + 1] = gain_nat[place] + gain_land[place]
        if place < 4:
            gain_step(place + 1).start()

    gain_step(0).start()

    x_copies[0].wait_recv()
    kept[0] += x_land[0].astype(F32)
    gain_next(0)
    xf_copy.wait_recv()
    kept_f[...] += xf_land[...].astype(F32)
    zf_send[...] = kept_f[...].astype(BF)
    z_forget.start()
    xo_copy.wait_recv()
    kept_o[...] += xo_land[...].astype(F32)
    gain_next(1)
    zo_send[0] = kept_o[2 * LANES :, :].astype(BF)
    zo_first.start()

    @pl.when(~owner)
    def _():
        zo_send[1] = kept_o[LANES : 2 * LANES, :].astype(BF)
        zo_mid.start()

    first_dst = rows_of(proj_out, 2 * y * slot_w, slot_w)
    mid_dst = rows_of(proj_out, slot_w, slot_w)
    out_first_dst = cols_of(out_out, 2 * LANES * y, LANES)
    out_mid_dst = cols_of(out_out, LANES, LANES)
    y_first = y_copy(3, final.at[0], first_dst)
    y_mid = y_copy(4, final.at[1], mid_dst)
    y_forget = y_copy(5, final_f, yf_land)
    yo_first = y_copy(6, final_o.at[0], out_first_dst)
    yo_mid = y_copy(7, final_o.at[1], out_mid_dst)
    own_first = pltpu.make_async_copy(final.at[0], first_dst, local_sem.at[8])
    own_mid = pltpu.make_async_copy(final.at[1], mid_dst, local_sem.at[9])
    own_out_first = pltpu.make_async_copy(final_o.at[0], out_first_dst, local_sem.at[10])
    own_out_mid = pltpu.make_async_copy(final_o.at[1], out_mid_dst, local_sem.at[11])
    own_forget = pltpu.make_async_copy(
        full_f, proj_out.at[pl.ds(row0, part), all_w : all_w + LANES], local_sem.at[12]
    )
    z_first.wait_recv()
    final[0] = (kept[0] + z_land[0].astype(F32)).astype(BF)
    y_first.start()
    own_first.start()

    @pl.when(owner)
    def _():
        z_mid.wait_recv()
        final[1] = (kept[1] + x_land[1].astype(F32) + z_land[1].astype(F32)).astype(BF)
        y_mid.start()
        own_mid.start()

    gain_next(2)
    z_forget.wait_recv()
    f_lane = lax.broadcasted_iota(jnp.int32, (part, LANES), 1)
    there_f = zf_land[...].astype(F32)
    edge = jnp.where(f_lane < 2, kept_f[...] + pltpu.roll(there_f, LANES - 4, 1), 0.0)
    edge = jnp.where(y == 0, edge, pltpu.roll(edge, 4, 1))
    mid_f = jnp.where((f_lane >= 2) & (f_lane < 4) & owner, kept_f[...] + there_f, 0.0)
    final_f[...] = (edge + mid_f).astype(BF)
    y_forget.start()
    gain_next(3)
    zo_first.wait_recv()
    final_o[0] = (kept_o[:LANES, :] + zo_land[0].astype(F32)).astype(BF)
    yo_first.start()
    own_out_first.start()

    @pl.when(owner)
    def _():
        zo_mid.wait_recv()
        final_o[1] = (kept_o[LANES : 2 * LANES, :] + zo_land[1].astype(F32)).astype(BF)
        yo_mid.start()
        own_out_mid.start()

    for copy in own_pieces:
        copy.wait()
    for copy in y_pieces:
        copy.wait_recv()
    c2 = []

    def hand_over(i, view):
        copy = remote(view, view, c2_send_sem.at[i], c2_recv_sem.at[i], here.other("c"))
        copy.start()
        c2.append(copy)

    hand_over(0, gate_out.at[pl.ds(row0, part), :])
    hand_over(1, up_out.at[pl.ds(row0, part), :])
    hand_over(2, down_out.at[:, pl.ds(row0, part)])

    gain_next(4)
    gain_copy = pltpu.make_async_copy(gain_nat.at[5], small_out, local_sem.at[7])
    gain_copy.start()
    y_forget.wait_recv()
    full_f[...] = final_f[...] + yf_land[...]
    own_forget.start()
    own_first.wait()
    y_first.wait_recv()
    own_out_first.wait()
    yo_first.wait_recv()
    own_forget.wait()

    @pl.when(owner)
    def _():
        own_mid.wait()
        own_out_mid.wait()

    @pl.when(~owner)
    def _():
        y_mid.wait_recv()
        yo_mid.wait_recv()

    hand_over(3, out_out.at[:, pl.ds(row0, part)])
    hand_over(4, proj_out.at[pl.ds(row0, part), :])

    for copy in c2:
        copy.wait()
    for p in range(2):
        back_copy(1, p).wait()

    @pl.when(away)
    def _():
        for p in range(2):
            back_copy(0, p).wait()

    @pl.when(~away)
    def _():
        for p in range(2):
            back_own(0, p).wait()

    gain_copy.wait()
    for i in range(5):
        gain_step(i).wait_send()
    for i in range(6):
        rs_copy(i).wait_send()
    for copy in [c_copy, cf_copy, co_copy, x_copies[0], x_copies[1], x_copies[2], xf_copy, xo_copy]:
        copy.wait_send()
    for copy in [far_swap, col_swap, tot_swap, z_first, z_forget, zo_first, zd_copy]:
        copy.wait_send()
    for copy in y_pieces + [y_first, y_forget, yo_first]:
        copy.wait_send()

    @pl.when(owner)
    def _():
        y_mid.wait_send()
        yo_mid.wait_send()

    @pl.when(~owner)
    def _():
        z_mid.wait_send()
        zo_mid.wait_send()


def last_step(ring, heads, large, small):
    near = large[1]
    rows = near.shape[0]
    weight, normed, gated = large[6:9]
    tokens = large[10]
    units = large[15].shape[0] // 2
    local, features = tokens.shape
    part = features // 4
    half = features // 2
    peers = len(ring.offsets)
    slot_w = 4 * LANES
    slots = heads // 2
    all_w = slots * slot_w
    any_spec = pl.BlockSpec(memory_space=pl.ANY)
    dma = pltpu.SemaphoreType.DMA
    vmem = pltpu.VMEM
    return pl.pallas_call(
        functools.partial(last_kernel, ring, heads),
        out_shape=(
            jax.ShapeDtypeStruct((2, local, half), BF),
            jax.ShapeDtypeStruct((half, all_w + LANES), BF),
            jax.ShapeDtypeStruct((half, 2 * units), BF),
            jax.ShapeDtypeStruct((half, 2 * units), BF),
            jax.ShapeDtypeStruct((2 * units, half), BF),
            jax.ShapeDtypeStruct((slots * LANES, half), BF),
            jax.ShapeDtypeStruct((4, 8, part), F32),
        ),
        in_specs=[any_spec] * len(large) + [pl.BlockSpec(memory_space=vmem)] * len(small),
        out_specs=[any_spec] * 7,
        scratch_shapes=[
            vmem((rows, all_w + LANES), BF),
            vmem(near.shape, F32),
            vmem(near.shape, BF),
            vmem(near.shape, BF),
            vmem((rows, LANES), F32),
            vmem((rows, LANES), F32),
            vmem((rows, LANES), F32),
            vmem((rows, LANES), F32),
            vmem((rows, LANES), F32),
            vmem((2 * (rows // CLEN), LANES), F32),
            vmem((2 * (rows // CLEN), LANES), F32),
            vmem(weight.shape, BF),
            vmem(normed.shape, BF),
            vmem(gated.shape, BF),
            vmem(normed.shape, BF),
            vmem(tokens.shape, BF),
            vmem(tokens.shape, F32),
            vmem((peers - 1, local, features), BF),
            vmem((peers - 1, local, features), BF),
            vmem((local, features), F32),
            vmem((half, all_w), BF),
            vmem((half, all_w), BF),
            vmem((half, LANES), BF),
            vmem((half, LANES), BF),
            vmem((slots, part, slot_w), F32),
            vmem((slots, part, slot_w), BF),
            vmem((slots, part, slot_w), BF),
            vmem((2, part, slot_w), BF),
            vmem((2, part, slot_w), BF),
            vmem((2, part, slot_w), BF),
            vmem((part, LANES), F32),
            vmem((part, LANES), BF),
            vmem((part, LANES), BF),
            vmem((part, LANES), BF),
            vmem((part, LANES), BF),
            vmem((part, LANES), BF),
            vmem((part, LANES), BF),
            vmem((part, LANES), BF),
            vmem((slots * LANES, half), BF),
            vmem((slots * LANES, half), BF),
            vmem((part, 2 * units), F32),
            vmem((part, 2 * units), BF),
            vmem((part, 2 * units), BF),
            vmem((2, part, units), BF),
            vmem((2 * units, part), F32),
            vmem((2 * units, part), BF),
            vmem((units, part), BF),
            vmem((units, part), BF),
            vmem((units, part), BF),
            vmem((slots * LANES, part), F32),
            vmem((slots * LANES, part), BF),
            vmem((slots * LANES, part), BF),
            vmem((2, LANES, part), BF),
            vmem((2, LANES, part), BF),
            vmem((2, LANES, part), BF),
            vmem((4, local, part), BF),
            vmem((4, 8, part), F32),
            vmem((6, 4, 8, part), F32),
            vmem((5, 4, 8, part), F32),
            dma((16 + slots,)),
            dma((13,)),
            dma((3,)),
            dma((3,)),
            dma((8,)),
            dma((8,)),
            dma((5,)),
            dma((5,)),
            dma((6,)),
            dma((6,)),
            dma((3,)),
            dma((3,)),
            dma((5,)),
            dma((5,)),
            dma((6,)),
            dma((6,)),
            dma((2, 2)),
            dma((2, 2)),
            dma((5,)),
            dma((5,)),
        ],
        compiler_params=pltpu.CompilerParams(
            collective_id=1, has_side_effects=True, vmem_limit_bytes=63 << 20
        ),
        cost_estimate=pl.CostEstimate(
            flops=4 * rows * features * all_w, bytes_accessed=40 << 20, transcendentals=0
        ),
    )(*large, *small)


def scale_kernel(
    full,
    sums,
    back,
    proj,
    gate,
    up,
    down,
    out,
    prompt_o,
    cont_o,
    query_o,
    outgate_o,
    key_o,
    value_o,
    gate_o,
    up_o,
    down_o,
    out_o,
):
    factor = full / sums[0, 2:3, 1:2]
    prompt_o[...] = back[0].astype(F32) * factor
    cont_o[...] = back[1].astype(F32) * factor
    for i, ref in enumerate((query_o, outgate_o, key_o, value_o)):
        for s in range(3):
            at = (4 * s + i) * LANES
            ref[:, s * LANES : (s + 1) * LANES] = proj[:, at : at + LANES].astype(F32) * factor
    gate_o[...] = gate[...].astype(F32) * factor
    up_o[...] = up[...].astype(F32) * factor
    down_o[...] = down[...].astype(F32) * factor
    out_o[...] = out[...].astype(F32) * factor


def scale_step(full, sums, back, proj, gate, up, down, out):
    steps = 8

    def cut(shape):
        return row_block(shape[0] // steps, shape[1])

    local, half = back.shape[1:]
    width = out.shape[0]
    shapes = [(local, half)] * 2 + [(half, width)] * 4 + [gate.shape, up.shape, down.shape, out.shape]
    return pl.pallas_call(
        functools.partial(scale_kernel, full),
        grid=(steps,),
        out_shape=tuple(jax.ShapeDtypeStruct(v, F32) for v in shapes),
        in_specs=[
            pl.BlockSpec(sums.shape, lambda i: (0, 0, 0)),
            pl.BlockSpec((2, local // steps, half), lambda i: (0, i, 0)),
        ]
        + [cut(v.shape) for v in (proj, gate, up, down, out)],
        out_specs=tuple(cut(v) for v in shapes),
        compiler_params=pltpu.CompilerParams(vmem_limit_bytes=62 << 20),
    )(sums, back, proj, gate, up, down, out)


def middle_kernel(
    ring,
    gated_in,
    w_out_in,
    w_gate_in,
    w_up_in,
    hid_there_in,
    w_down_in,
    tokens_in,
    teach_prompt_in,
    teach_cont_in,
    valid_ref,
    gain_ref,
    gated_grad,
    residual_grad,
    mixed_grads,
    hid_kept,
    hid_there,
    down_kept,
    down_there,
    error_ref,
    gain_grad,
    gated,
    w_out,
    w_hidden,
    w_down,
    tokens,
    teacher,
    mixed,
    total,
    result_grad,
    normed,
    hidden,
    gate_up,
    result_all,
    mixed_all,
    rs_send,
    rs_land,
    c_down_send,
    c_down_land,
    c_hid_send,
    c_hid_land,
    x_down_send,
    x_hid_send,
    down_sum,
    hid_sum,
    gg_stage,
    load_sem,
    wx_send,
    wx_recv,
    wc_send,
    wc_recv,
    wz_send,
    wz_recv,
    group_send,
    group_recv,
    out_sem,
    rs_send_sem,
    rs_recv_sem,
    ag_send_sem,
    ag_recv_sem,
    c_send_sem,
    c_recv_sem,
    x_send_sem,
    x_recv_sem,
):
    here = Here(ring)
    local, features = tokens.shape
    rows_all = gated.shape[0]
    width = gated.shape[1]
    units = hidden.shape[1]
    half_units = units // 2
    part = features // 4
    peers = len(ring.offsets)
    y, c, x = (here.at[a] for a in ("y", "c", "x"))
    gate_view, up_view = (
        w.at[
            pl.ds(pl.multiple_of(c * part, part), part),
            pl.ds(pl.multiple_of(y * half_units, half_units), half_units),
        ]
        for w in (w_gate_in, w_up_in)
    )
    down_view = w_down_in.at[
        pl.ds(pl.multiple_of(y * half_units, half_units), half_units),
        pl.ds(pl.multiple_of(c * part, part), part),
    ]

    loads = [
        pltpu.make_async_copy(a, b, load_sem.at[i])
        for i, (a, b) in enumerate(
            (
                (gate_view, w_hidden.at[0:part, 0:half_units]),
                (up_view, w_hidden.at[0:part, half_units:units]),
                (hid_there_in, w_hidden.at[0:part, units:]),
                (gated_in, gated),
                (w_out_in, w_out),
                (tokens_in, tokens),
                (down_view, w_down.at[0:half_units, 0:part]),
            )
        )
    ]
    for copy in loads:
        copy.start()
    here.greet_group(
        [here.peer(k) for k in range(1, peers)]
        + [here.other("c"), here.other("x"), here.other("zh")]
    )

    z_down = remote(
        down_view, w_down.at[half_units:, 0:part], wz_send.at[0], wz_recv.at[0], here.other("zh")
    )
    z_down.start()

    def hid_x_copy(i):
        cols = slice(i * half_units, (i + 1) * half_units) if i < 2 else slice(units, 2 * units)
        return remote(
            w_hidden.at[0:part, cols],
            w_hidden.at[part : 2 * part, cols],
            wx_send.at[i],
            wx_recv.at[i],
            here.other("x"),
        )

    def hid_c_copy(i):
        cols = slice(i * half_units, (i + 1) * half_units) if i < 2 else slice(units, 2 * units)
        return remote(
            w_hidden.at[0 : 2 * part, cols],
            w_hidden.at[2 * part :, cols],
            wc_send.at[i],
            wc_recv.at[i],
            here.other("c"),
        )

    for i in range(3):
        loads[i].wait()
        hid_x_copy(i).start()

    def teach_copies(flip, rows_in, remote_copy):
        kind = x ^ flip
        out = []
        for p in range(2):
            block = (x ^ y) + 2 * (kind ^ p)
            dst = teacher.at[:, pl.ds(pl.multiple_of(block * part, part), part)]
            src = rows_in.at[:, p * part : (p + 1) * part]
            if remote_copy:
                out.append(
                    remote(
                        src, dst, group_send.at[flip, p], group_recv.at[flip, p], here.group_to(flip)
                    )
                )
            else:
                out.append(pltpu.make_async_copy(src, dst, load_sem.at[7 + p]))
        return out

    away = here.group_away()

    def on_teacher(flip, here_too, what):
        for kind, rows_in in ((0, teach_prompt_in), (1, teach_cont_in)):
            mine = (x ^ flip) == kind
            if flip == 1:

                @pl.when(mine)
                def _():
                    for copy in teach_copies(1, rows_in, True):
                        what(copy)

            else:

                @pl.when(mine & away)
                def _():
                    for copy in teach_copies(0, rows_in, True):
                        what(copy)

                if here_too:

                    @pl.when(mine & ~away)
                    def _():
                        for copy in teach_copies(0, rows_in, False):
                            what(copy)

    def teacher_arrival(flip):
        for p in range(2):
            remote(
                teach_prompt_in.at[:, p * part : (p + 1) * part],
                teacher.at[:, p * part : (p + 1) * part],
                group_send.at[flip, p],
                group_recv.at[flip, p],
                here.group_to(flip),
            ).wait_recv()

    def chunk(k):
        return slice(k * local, (k + 1) * local)

    def tiled(count, size, step):
        def body(i, carry):
            step(pl.ds(pl.multiple_of(i * size, size), size))
            return carry

        lax.fori_loop(0, count, body, 0)

    moves = RingRows(here, local)

    def rs_copy(phase, i):
        return moves.sum_copy(rs_send, rs_land, rs_send_sem.at[phase], rs_recv_sem.at[phase], i)

    def ag_copy(phase, buffer, i):
        return moves.gather_copy(buffer, ag_send_sem.at[phase], ag_recv_sem.at[phase], i)

    wide = 512
    wide_count = features // wide

    def send_partial(phase, k, left, right, transposed):
        def step(cols):
            if transposed:
                value = nt_dot(left, right[cols, :])
            else:
                value = nn_dot(left, right[:, cols])
            if k == 0:
                total[:, cols] = value
            else:
                rs_send[k - 1, :, cols] = value.astype(BF)

        if k != 0 and phase > 0:
            for i in SUM_READS[k]:
                rs_copy(phase - 1, i).wait_send()
        tiled(wide_count, wide, step)
        if k != 0:
            for i in SUM_STARTS[k]:
                rs_copy(phase, i).start()

    def hand_on(phase):
        moves.hand_on(rs_send, rs_land, rs_send_sem.at[phase], rs_recv_sem.at[phase])

    def sums_arrived(phase):
        for i in (0, 2, 4, 5):
            rs_copy(phase, i).wait_recv()

    def half_tiles(phase, buffer, step):
        for half in range(2):

            def body(i, carry):
                step(pl.ds(pl.multiple_of(half * (local // 2) + i * 32, 32), 32))
                return carry

            lax.fori_loop(0, local // 64, body, 0)
            ag_copy(phase, buffer, half).start()
            ag_copy(phase, buffer, 2 + half).start()

    def pass_on(phase, buffer):
        ag_copy(phase, buffer, 2).wait_recv()
        ag_copy(phase, buffer, 4).start()
        ag_copy(phase, buffer, 1).wait_recv()
        ag_copy(phase, buffer, 5).start()

    def rows_arrived(phase, buffer, k):
        for i in {1: (0,), 2: (3,), 3: (4, 5)}[k]:
            ag_copy(phase, buffer, i).wait_recv()

    def summed(rows):
        return total[rows, :] + rs_land[0, rows, :].astype(F32) + rs_land[2, rows, :].astype(F32)

    loads[3].wait()
    loads[4].wait()
    for k in (3, 1, 2, 0):
        send_partial(0, k, gated[chunk(k), :], w_out, False)
    loads[5].wait()
    loads[6].wait()
    z_down.wait_recv()
    down_x_copy = remote(
        w_down.at[:, 0:part],
        w_down.at[:, part : 2 * part],
        wx_send.at[4],
        wx_recv.at[4],
        here.other("x"),
    )
    down_x_copy.start()
    hand_on(0)
    sums_arrived(0)

    def second_norm(rows):
        value = tokens[rows, :].astype(F32) + summed(rows)
        mixed[rows, :] = value
        factor = lax.rsqrt(jnp.mean(value * value, axis=-1, keepdims=True) + epsilon)
        normed[rows, :] = (value * factor * gain_ref[...]).astype(BF)

    half_tiles(0, normed, second_norm)

    for i in range(3):
        hid_x_copy(i).wait_recv()
        hid_c_copy(i).start()
    for f in range(2):
        on_teacher(f, True, lambda copy: copy.start())
    for i in range(3):
        hid_c_copy(i).wait_recv()
    tile_u = 256
    per_half = half_units // tile_u

    def forward_chunk(k):
        left = normed[chunk(k), :]

        def step(i, carry):
            half = i // per_half
            sub = lax.rem(i, per_half)
            gate_at = pl.multiple_of(half * units + sub * tile_u, tile_u)
            up_at = pl.multiple_of(half * units + half_units + sub * tile_u, tile_u)
            gate = nn_dot(left, w_hidden[:, pl.ds(gate_at, tile_u)])
            up = nn_dot(left, w_hidden[:, pl.ds(up_at, tile_u)])
            gate_up[chunk(k), pl.ds(gate_at, tile_u)] = gate.astype(BF)
            gate_up[chunk(k), pl.ds(up_at, tile_u)] = up.astype(BF)
            hidden[chunk(k), pl.ds(pl.multiple_of(i * tile_u, tile_u), tile_u)] = (
                gate * jax.nn.sigmoid(gate) * up
            ).astype(BF)
            return carry

        lax.fori_loop(0, 2 * per_half, step, 0)

    def forward_sum(k):
        send_partial(1, k, hidden[chunk(k), :], w_down, False)

    forward_chunk(0)
    pass_on(0, normed)
    down_x_copy.wait_recv()
    down_c_copy = remote(
        w_down.at[:, 0 : 2 * part],
        w_down.at[:, 2 * part :],
        wc_send.at[4],
        wc_recv.at[4],
        here.other("c"),
    )
    down_c_copy.start()
    for k in range(1, peers):
        rows_arrived(0, normed, k)
        forward_chunk(k)
        if k == 1:
            down_c_copy.wait_recv()
        forward_sum(k)
    forward_sum(0)
    hand_on(1)
    teacher_arrival(1)

    @pl.when(away)
    def _():
        teacher_arrival(0)

    @pl.when(~away)
    def _():
        for kind, rows_in in ((0, teach_prompt_in), (1, teach_cont_in)):

            @pl.when(x == kind)
            def _():
                for copy in teach_copies(0, rows_in, False):
                    copy.wait()

    sums_arrived(1)
    error_ref[...] = jnp.zeros(error_ref.shape, F32)
    gain_grad[...] = jnp.zeros(gain_grad.shape, F32)

    def loss_rows(rows):
        deviation = mixed[rows, :] + summed(rows) - teacher[rows, :].astype(F32)
        grad = valid_ref[rows, :] * deviation
        result_grad[rows, :] = grad
        result_all[rows, :] = grad.astype(BF)
        error_ref[0:1, :] += 0.5 * jnp.sum(grad * deviation, axis=0, keepdims=True)

    half_tiles(1, result_all, loss_rows)

    def backward_chunk(k):
        left = result_all[chunk(k), :]

        def step(i, carry):
            half = i // per_half
            sub = lax.rem(i, per_half)
            gate_at = pl.multiple_of(half * units + sub * tile_u, tile_u)
            up_at = pl.multiple_of(half * units + half_units + sub * tile_u, tile_u)
            grad = nt_dot(left, w_down[pl.ds(pl.multiple_of(i * tile_u, tile_u), tile_u), :])
            gate = gate_up[chunk(k), pl.ds(gate_at, tile_u)].astype(F32)
            up = gate_up[chunk(k), pl.ds(up_at, tile_u)].astype(F32)
            sig = jax.nn.sigmoid(gate)
            gate_up[chunk(k), pl.ds(gate_at, tile_u)] = (
                grad * up * sig * (1.0 + gate * (1.0 - sig))
            ).astype(BF)
            gate_up[chunk(k), pl.ds(up_at, tile_u)] = (grad * gate * sig).astype(BF)
            return carry

        lax.fori_loop(0, 2 * per_half, step, 0)

    def backward_sum(k):
        send_partial(2, k, gate_up[chunk(k), :], w_hidden, True)

    backward_chunk(0)
    pass_on(1, result_all)
    for k in range(1, peers):
        rows_arrived(1, result_all, k)
        backward_chunk(k)
        backward_sum(k)

    unit_tile = 256

    def down_tile(units_at, cols):
        return tn_dot(hidden[:, units_at], result_all[:, cols])

    feature_tile = 128

    def hid_tile(first, at):
        cols = pl.ds(pl.multiple_of(first + at.start, feature_tile), feature_tile)
        return tn_dot(normed[:, cols], gate_up[...])

    def hid_c(at):
        c_hid_send[at, :] = hid_tile(2 * part, at).astype(BF)

    tiled(2 * part // feature_tile, feature_tile, hid_c)
    c_hid = remote(c_hid_send, c_hid_land, c_send_sem.at[1], c_recv_sem.at[1], here.other("c"))
    c_hid.start()
    hand_on(2)
    backward_sum(0)

    def down_c(units_at):
        c_down_send[units_at, :] = down_tile(units_at, slice(2 * part, features)).astype(BF)

    tiled(units // unit_tile, unit_tile, down_c)
    c_down = remote(c_down_send, c_down_land, c_send_sem.at[0], c_recv_sem.at[0], here.other("c"))
    c_down.start()
    c_hid.wait_recv()

    def hid_x(at):
        land = pl.ds(pl.multiple_of(part + at.start, feature_tile), feature_tile)
        x_hid_send[at, :] = (hid_tile(part, at) + c_hid_land[land, :].astype(F32)).astype(BF)

    tiled(part // feature_tile, feature_tile, hid_x)
    x_hid = remote(x_hid_send, hid_there, x_send_sem.at[1], x_recv_sem.at[1], here.other("x"))
    x_hid.start()

    sums_arrived(2)

    def norm_back(rows):
        value = mixed[rows, :]
        factor = lax.rsqrt(jnp.mean(value * value, axis=-1, keepdims=True) + epsilon)
        scaled_rows = value * factor
        grad = summed(rows)
        e = grad * gain_ref[...]
        mean = jnp.mean(e * scaled_rows, axis=-1, keepdims=True)
        out = result_grad[rows, :] + factor * (e - scaled_rows * mean)
        result_grad[rows, :] = out
        mixed_all[rows, :] = out.astype(BF)
        gain_grad[0:1, :] += jnp.sum(grad * scaled_rows, axis=0, keepdims=True)

    half_tiles(2, mixed_all, norm_back)
    residual_copy = pltpu.make_async_copy(result_grad, residual_grad, out_sem.at[0])
    residual_copy.start()

    def gated_chunk(k):
        gg_stage[chunk(k), :] = nt_dot(mixed_all[chunk(k), :], w_out[...])

    gated_chunk(0)
    c_down.wait_recv()

    def down_x(units_at):
        value = down_tile(units_at, slice(part, 2 * part))
        x_down_send[units_at, :] = (value + c_down_land[units_at, part:].astype(F32)).astype(BF)

    tiled(units // unit_tile, unit_tile, down_x)
    pass_on(2, mixed_all)

    def down_own(units_at):
        value = down_tile(units_at, slice(0, part))
        down_sum[units_at, :] = value + c_down_land[units_at, :part].astype(F32)

    tiled(units // unit_tile, unit_tile, down_own)

    def hid_own(at):
        hid_sum[at, :] = hid_tile(0, at) + c_hid_land[at, :].astype(F32)

    tiled(part // feature_tile, feature_tile, hid_own)
    sums_out = [
        pltpu.make_async_copy(down_sum, down_kept, out_sem.at[1]),
        pltpu.make_async_copy(hid_sum, hid_kept, out_sem.at[2]),
        pltpu.make_async_copy(x_down_send, down_there, out_sem.at[5]),
    ]
    for copy in sums_out:
        copy.start()
    for k in range(1, peers):
        rows_arrived(2, mixed_all, k)
        gated_chunk(k)
    finals = [
        pltpu.make_async_copy(gg_stage, gated_grad, out_sem.at[3]),
        pltpu.make_async_copy(mixed_all, mixed_grads, out_sem.at[4]),
    ]
    for copy in finals:
        copy.start()
    for i in range(6):
        rs_copy(2, i).wait_send()
        for phase, buffer in enumerate((normed, result_all, mixed_all)):
            ag_copy(phase, buffer, i).wait_send()
    c_down.wait_send()
    c_hid.wait_send()
    z_down.wait_send()
    for i in range(3):
        hid_x_copy(i).wait_send()
        hid_c_copy(i).wait_send()
    for f in range(2):
        on_teacher(f, False, lambda copy: copy.wait_send())
    down_x_copy.wait_send()
    down_c_copy.wait_send()
    x_hid.wait()
    residual_copy.wait()
    for copy in sums_out + finals:
        copy.wait()


def middle_step(
    ring,
    gated,
    w_out,
    w_gate,
    w_up,
    hid_there,
    w_down,
    tokens,
    teach_prompt,
    teach_cont,
    valid,
    gain,
):
    rows, width = gated.shape
    local, features = tokens.shape
    units = w_down.shape[0]
    part = features // 4
    peers = len(ring.offsets)
    any_spec = pl.BlockSpec(memory_space=pl.ANY)
    vmem_spec = pl.BlockSpec(memory_space=pltpu.VMEM)
    dma = pltpu.SemaphoreType.DMA
    return pl.pallas_call(
        functools.partial(middle_kernel, ring),
        out_shape=(
            jax.ShapeDtypeStruct((rows, width), F32),
            jax.ShapeDtypeStruct((local, features), F32),
            jax.ShapeDtypeStruct((rows, features), BF),
            jax.ShapeDtypeStruct((part, 2 * units), F32),
            jax.ShapeDtypeStruct((part, 2 * units), BF),
            jax.ShapeDtypeStruct((units, part), F32),
            jax.ShapeDtypeStruct((units, part), BF),
            jax.ShapeDtypeStruct((8, features), F32),
            jax.ShapeDtypeStruct((8, features), F32),
        ),
        in_specs=[any_spec] * 9 + [vmem_spec] * 2,
        out_specs=[any_spec] * 7 + [vmem_spec] * 2,
        scratch_shapes=[
            pltpu.VMEM(gated.shape, BF),
            pltpu.VMEM(w_out.shape, BF),
            pltpu.VMEM((features, 2 * units), BF),
            pltpu.VMEM((units, features), BF),
            pltpu.VMEM(tokens.shape, BF),
            pltpu.VMEM(tokens.shape, BF),
            pltpu.VMEM(tokens.shape, F32),
            pltpu.VMEM(tokens.shape, F32),
            pltpu.VMEM(tokens.shape, F32),
            pltpu.VMEM((rows, features), BF),
            pltpu.VMEM((rows, units), BF),
            pltpu.VMEM((rows, 2 * units), BF),
            pltpu.VMEM((rows, features), BF),
            pltpu.VMEM((rows, features), BF),
            pltpu.VMEM((peers - 1, local, features), BF),
            pltpu.VMEM((peers - 1, local, features), BF),
            pltpu.VMEM((units, 2 * part), BF),
            pltpu.VMEM((units, 2 * part), BF),
            pltpu.VMEM((2 * part, 2 * units), BF),
            pltpu.VMEM((2 * part, 2 * units), BF),
            pltpu.VMEM((units, part), BF),
            pltpu.VMEM((part, 2 * units), BF),
            pltpu.VMEM((units, part), F32),
            pltpu.VMEM((part, 2 * units), F32),
            pltpu.VMEM((rows, width), F32),
            dma((9,)),
            dma((5,)),
            dma((5,)),
            dma((5,)),
            dma((5,)),
            dma((2,)),
            dma((2,)),
            dma((2, 2)),
            dma((2, 2)),
            dma((6,)),
            dma((3, 6)),
            dma((3, 6)),
            dma((3, 6)),
            dma((3, 6)),
            dma((2,)),
            dma((2,)),
            dma((2,)),
            dma((2,)),
        ],
        compiler_params=pltpu.CompilerParams(
            collective_id=2, has_side_effects=True, vmem_limit_bytes=63 << 20
        ),
        cost_estimate=pl.CostEstimate(
            flops=6 * rows * features * (3 * units + width),
            bytes_accessed=60 << 20,
            transcendentals=0,
        ),
    )(
        gated,
        w_out,
        w_gate,
        w_up,
        hid_there,
        w_down,
        tokens,
        teach_prompt,
        teach_cont,
        valid,
        gain,
    )


class RingRows:
    def __init__(self, here, local):
        self.zl, self.y = here.peer(1), here.peer(2)
        self.local = local
        self.half = local // 2

    def rows(self, place, half=None):
        base = place * self.local
        if half is None:
            return slice(base, base + self.local)
        return slice(base + half * self.half, base + (half + 1) * self.half)

    def gather_copy(self, buffer, sends, recvs, i):
        source, target, place, half = (
            (0, self.zl, 1, 0),
            (0, self.zl, 1, 1),
            (0, self.y, 2, 0),
            (0, self.y, 2, 1),
            (2, self.zl, 3, 0),
            (1, self.y, 3, 1),
        )[i]
        return remote(
            buffer.at[self.rows(source, half)],
            buffer.at[self.rows(place, half)],
            sends.at[i],
            recvs.at[i],
            target,
        )

    def sum_copy(self, send, land, sends, recvs, i):
        chunk, half, target, slot = (
            (0, 0, self.zl, 0),
            (2, 0, self.zl, 1),
            (1, 1, self.y, 0),
            (2, 1, self.y, 1),
            (1, 0, self.y, 2),
            (0, 1, self.zl, 2),
        )[i]
        return remote(
            send.at[chunk, self.rows(0, half)],
            land.at[slot, self.rows(0, half)],
            sends.at[i],
            recvs.at[i],
            target,
        )

    def hand_on(self, send, land, sends, recvs):
        for chunk, half, got, i in ((1, 0, 1, 4), (0, 1, 3, 5)):
            self.sum_copy(send, land, sends, recvs, got).wait_recv()
            rows = self.rows(0, half)
            send[chunk, rows, :] = (
                send[chunk, rows, :].astype(F32) + land[1, rows, :].astype(F32)
            ).astype(BF)
            self.sum_copy(send, land, sends, recvs, i).start()


SUM_STARTS = {1: (0,), 2: (2,), 3: (1, 3)}
SUM_READS = {1: (0, 5), 2: (2, 4), 3: (1, 3)}


def first_kernel(
    ring,
    prompt_in,
    cont_in,
    small_in,
    ints_in,
    wq_in,
    wg_in,
    wk_in,
    wv_in,
    w_out_in,
    tokens_out,
    normed_out,
    slots_out,
    w_out_all,
    small_out,
    gains_out,
    forget_w_out,
    ints_out,
    proj_a,
    proj_b,
    proj_c,
    forget_own,
    there_a,
    there_b,
    there_c,
    forget_there,
    tokens,
    normed,
    slot_w,
    project,
    forget,
    small,
    small_x,
    feats,
    forget_f,
    forget_w,
    group_send,
    group_recv,
    ints_send,
    ints_recv,
    small_send,
    small_recv,
    own_sem,
    z_send,
    z_recv,
    x_send,
    x_recv,
    c_send,
    c_recv,
    ag_send,
    ag_recv,
    kv_send,
    kv_recv,
    out_sem,
):
    here = Here(ring)
    y, c, x, zh = (here.at[a] for a in ("y", "c", "x", "zh"))
    local, features = tokens.shape
    part = features // 4
    half = features // 2
    peers = len(ring.offsets)
    owner = zh == here.mid_home()
    row0 = pl.multiple_of(c * part, part)
    first0 = pl.multiple_of(2 * LANES * y, LANES)
    sources = (wq_in, wg_in, wk_in, wv_in)

    here.greet_group([here.peer(k) for k in range(1, peers)] + [here.other(a) for a in "cx"] + [here.other("zh")])

    def group_copies(flip, rows_in, remote_copy):
        kind = x ^ flip
        out = []
        for p in range(2):
            block = (x ^ y) + 2 * (kind ^ p)
            dst = tokens.at[:, pl.ds(pl.multiple_of(block * part, part), part)]
            src = rows_in.at[:, p * part : (p + 1) * part]
            if remote_copy:
                out.append(
                    remote(
                        src, dst, group_send.at[flip, p], group_recv.at[flip, p], here.group_to(flip)
                    )
                )
            else:
                out.append(pltpu.make_async_copy(src, dst, own_sem.at[12 + p]))
        return out

    def ints_copy():
        return remote(ints_in, ints_out, ints_send, ints_recv, here.group_to(0))

    def ints_own():
        return pltpu.make_async_copy(ints_in, ints_out, own_sem.at[14])

    away = here.group_away()

    def on_group(flip, what):
        for kind, rows_in in ((0, prompt_in), (1, cont_in)):
            mine = (x ^ flip) == kind
            if flip == 1:

                @pl.when(mine)
                def _():
                    for copy in group_copies(flip, rows_in, True):
                        what(copy)

            else:

                @pl.when(mine & away)
                def _():
                    for copy in group_copies(flip, rows_in, True):
                        what(copy)

                @pl.when(mine & ~away)
                def _():
                    for copy in group_copies(flip, rows_in, False):
                        what(copy)

    for f in range(2):
        on_group(f, lambda copy: copy.start())

    @pl.when(away)
    def _():
        ints_copy().start()

    @pl.when(~away)
    def _():
        ints_own().start()

    def z_piece(i, s):
        start = first0 if s == 2 else LANES
        return remote(
            sources[i].at[pl.ds(row0, part), pl.ds(start, LANES)],
            slot_w.at[s, 0:part, i * LANES : (i + 1) * LANES],
            z_send.at[s, i],
            z_recv.at[s, i],
            here.other("zh"),
        )

    own_small = pltpu.make_async_copy(small_in, small.at[0], own_sem.at[15])
    own_small.start()
    small_z = remote(small_in, small.at[1], small_send.at[0], small_recv.at[0], here.other("zh"))
    small_z.start()

    def own_piece(i, s):
        start = first0 if s == 0 else LANES
        return pltpu.make_async_copy(
            sources[i].at[pl.ds(row0, part), pl.ds(start, LANES)],
            slot_w.at[s, 0:part, i * LANES : (i + 1) * LANES],
            own_sem.at[4 * s + i],
        )

    for i in range(4):
        own_piece(i, 0).start()

    @pl.when(owner)
    def _():
        for i in range(4):
            own_piece(i, 1).start()

    own_out = [
        pltpu.make_async_copy(
            w_out_in.at[pl.ds(first0, LANES), pl.ds(row0, part)],
            w_out_all.at[0:LANES, 0:part],
            own_sem.at[8],
        ),
        pltpu.make_async_copy(
            w_out_in.at[LANES : 2 * LANES, pl.ds(row0, part)],
            w_out_all.at[LANES : 2 * LANES, 0:part],
            own_sem.at[9],
        ),
    ]
    own_out[0].start()

    @pl.when(owner)
    def _():
        own_out[1].start()

    own_small.wait()
    small_z.wait_recv()
    small_over_x = remote(small, small_x, small_send.at[1], small_recv.at[1], here.other("x"))
    small_over_x.start()

    def x_copy(s):
        return remote(
            slot_w.at[s, 0:part],
            slot_w.at[s, part : 2 * part],
            x_send.at[s],
            x_recv.at[s],
            here.other("x"),
        )

    def c_copy(s):
        return remote(
            slot_w.at[s, 0:half],
            slot_w.at[s, half:features],
            c_send.at[s],
            c_recv.at[s],
            here.other("c"),
        )

    for i in range(4):
        own_piece(i, 0).wait()
    x_copy(0).start()
    small_over_x.wait_recv()
    for z in range(2):
        for place in range(2):
            at = pl.multiple_of((c ^ place) * part, part)
            feats[z, :, 2 * place * part : (2 * place + 1) * part] = small[z, :, pl.ds(at, part)]
            feats[z, :, (2 * place + 1) * part : (2 * place + 2) * part] = small_x[
                z, :, pl.ds(at, part)
            ]
    forget_f[...] = jnp.zeros(forget_f.shape, F32)
    for z, rows in ((0, slice(0, 2)), (1, slice(4, 6))):
        forget_f[rows, :] = jnp.where(y == 0, feats[z, 8:10, :], feats[z, 12:14, :])
    forget_f[2:4, :] = jnp.where(owner, feats[0, 10:12, :], feats[1, 10:12, :])
    forget_w[...] = jnp.zeros(forget_w.shape, BF)
    forget_w[0:16, :] = forget_f[...].astype(BF)

    def group_arrival(flip):
        for p in range(2):
            remote(
                prompt_in.at[:, p * part : (p + 1) * part],
                tokens.at[:, p * part : (p + 1) * part],
                group_send.at[flip, p],
                group_recv.at[flip, p],
                here.group_to(flip),
            ).wait_recv()

    group_arrival(1)

    @pl.when(away)
    def _():
        group_arrival(0)

    @pl.when(~away)
    def _():
        for kind, rows_in in ((0, prompt_in), (1, cont_in)):

            @pl.when(x == kind)
            def _():
                for copy in group_copies(0, rows_in, False):
                    copy.wait()

    for i in range(4):
        z_piece(i, 2).start()

    @pl.when(owner)
    def _():
        for i in range(4):
            z_piece(i, 1).start()

    z_out = [
        remote(
            w_out_in.at[pl.ds(first0, LANES), pl.ds(row0, part)],
            w_out_all.at[2 * LANES : 3 * LANES, 0:part],
            z_send.at[0, 0],
            z_recv.at[0, 0],
            here.other("zh"),
        ),
        remote(
            w_out_in.at[LANES : 2 * LANES, pl.ds(row0, part)],
            w_out_all.at[LANES : 2 * LANES, 0:part],
            z_send.at[0, 1],
            z_recv.at[0, 1],
            here.other("zh"),
        ),
    ]
    z_out[0].start()

    @pl.when(owner)
    def _():
        z_out[1].start()

    moves = RingRows(here, local)

    def ag_copy(i):
        return moves.gather_copy(normed, ag_send, ag_recv, i)

    def norm_rows(i, carry):
        rows = pl.ds(pl.multiple_of(i * 32, 32), 32)
        value = tokens[rows, :].astype(F32)
        factor = lax.rsqrt(jnp.mean(value * value, axis=-1, keepdims=True) + epsilon)
        normed[rows, :] = (value * factor * feats[0, 0:1, :]).astype(BF)
        return carry

    for place in range(2):
        lax.fori_loop(place * (local // 64), (place + 1) * (local // 64), norm_rows, 0)
        ag_copy(place).start()
        ag_copy(2 + place).start()

    outs = [
        pltpu.make_async_copy(tokens, tokens_out, out_sem.at[0]),
        pltpu.make_async_copy(small, small_out, out_sem.at[1]),
        pltpu.make_async_copy(feats.at[0], gains_out, out_sem.at[2]),
        pltpu.make_async_copy(forget_w, forget_w_out, out_sem.at[3]),
    ]
    for copy in outs:
        copy.start()

    x_copy(0).wait_recv()
    c_copy(0).start()
    for i in range(4):
        z_piece(i, 2).wait_recv()
    x_copy(2).start()

    @pl.when(owner)
    def _():
        for i in range(4):
            own_piece(i, 1).wait()

    @pl.when(~owner)
    def _():
        for i in range(4):
            z_piece(i, 1).wait_recv()

    x_copy(1).start()

    projects = (proj_a, proj_b, proj_c)
    theres = (there_a, there_b, there_c)

    def chunk(k):
        return slice(k * local, (k + 1) * local)

    def kv_copy(k, s):
        return remote(
            project.at[s, chunk(k), 2 * LANES :],
            theres[s].at[chunk(k)],
            kv_send.at[k, s],
            kv_recv.at[k, s],
            here.other("c"),
        )

    def forget_copy(k):
        return remote(
            forget.at[chunk(k)],
            forget_there.at[chunk(k)],
            kv_send.at[k, 3],
            kv_recv.at[k, 3],
            here.other("c"),
        )

    def project_chunk(k, s):
        project[s, chunk(k), :] = nn_dot(normed[chunk(k), :], slot_w[s]).astype(BF)
        kv_copy(k, s).start()

    def forget_chunk(k):
        forget[chunk(k), :] = nt_dot(normed[chunk(k), :], forget_w[...]).astype(BF)
        forget_copy(k).start()

    c_copy(0).wait_recv()
    forget_chunk(0)
    project_chunk(0, 0)
    ag_copy(2).wait_recv()
    ag_copy(4).start()
    ag_copy(1).wait_recv()
    ag_copy(5).start()
    for k, arrivals in ((1, (0,)), (2, (3,)), (3, (4, 5))):
        for i in arrivals:
            ag_copy(i).wait_recv()
        forget_chunk(k)
        project_chunk(k, 0)
    normed_copy = pltpu.make_async_copy(normed, normed_out, out_sem.at[4])
    normed_copy.start()
    for s in (2, 1):
        x_copy(s).wait_recv()
        c_copy(s).start()
    own_out[0].wait()
    z_out[0].wait_recv()

    @pl.when(owner)
    def _():
        own_out[1].wait()

    @pl.when(~owner)
    def _():
        z_out[1].wait_recv()

    x_out = remote(
        w_out_all.at[:, 0:part],
        w_out_all.at[:, part : 2 * part],
        x_send.at[3],
        x_recv.at[3],
        here.other("x"),
    )
    x_out.start()
    for s in (2, 1):
        c_copy(s).wait_recv()
        for k in range(peers):
            project_chunk(k, s)
    slots_copy = pltpu.make_async_copy(slot_w, slots_out, out_sem.at[5])
    slots_copy.start()
    finals = [
        pltpu.make_async_copy(project.at[s], projects[s], out_sem.at[6 + s]) for s in range(3)
    ] + [pltpu.make_async_copy(forget, forget_own, out_sem.at[9])]
    for copy in finals:
        copy.start()
    x_out.wait_recv()
    c_out = remote(
        w_out_all.at[:, 0:half],
        w_out_all.at[:, half:features],
        c_send.at[3],
        c_recv.at[3],
        here.other("c"),
    )
    c_out.start()

    on_group(1, lambda copy: copy.wait_send())

    @pl.when(away)
    def _():
        ints_copy().wait()
        for kind, rows_in in ((0, prompt_in), (1, cont_in)):

            @pl.when(x == kind)
            def _():
                for copy in group_copies(0, rows_in, True):
                    copy.wait_send()

    @pl.when(~away)
    def _():
        ints_own().wait()

    small_z.wait_send()
    small_over_x.wait_send()
    for i in range(4):
        z_piece(i, 2).wait_send()
    z_out[0].wait_send()

    @pl.when(owner)
    def _():
        for i in range(4):
            z_piece(i, 1).wait_send()
        z_out[1].wait_send()

    for s in range(3):
        x_copy(s).wait_send()
        c_copy(s).wait_send()
    x_out.wait_send()
    for i in range(6):
        ag_copy(i).wait_send()
    for k in range(peers):
        for s in range(3):
            kv_copy(k, s).wait()
        forget_copy(k).wait()
    c_out.wait()
    for copy in outs + finals + [normed_copy, slots_copy]:
        copy.wait()


def first_step(ring, prompt, cont, small, ints, wq, wg, wk, wv, w_out):
    local, half = prompt.shape
    features = 2 * half
    part = half // 2
    peers = len(ring.offsets)
    rows = peers * local
    slot = 4 * LANES
    any_spec = pl.BlockSpec(memory_space=pl.ANY)
    dma = pltpu.SemaphoreType.DMA
    shapes = [
        ((local, features), BF),
        ((rows, features), BF),
        ((3, features, slot), BF),
        ((3 * LANES, features), BF),
        ((2, 16, half), F32),
        ((16, features), F32),
        ((LANES, features), BF),
        (ints.shape, jnp.int32),
        ((rows, slot), BF),
        ((rows, slot), BF),
        ((rows, slot), BF),
        ((rows, LANES), BF),
        ((rows, 2 * LANES), BF),
        ((rows, 2 * LANES), BF),
        ((rows, 2 * LANES), BF),
        ((rows, LANES), BF),
    ]
    return pl.pallas_call(
        functools.partial(first_kernel, ring),
        out_shape=tuple(jax.ShapeDtypeStruct(*s) for s in shapes),
        in_specs=[any_spec] * 9,
        out_specs=[any_spec] * len(shapes),
        scratch_shapes=[
            pltpu.VMEM((local, features), BF),
            pltpu.VMEM((rows, features), BF),
            pltpu.VMEM((3, features, slot), BF),
            pltpu.VMEM((3, rows, slot), BF),
            pltpu.VMEM((rows, LANES), BF),
            pltpu.VMEM((2, 16, half), F32),
            pltpu.VMEM((2, 16, half), F32),
            pltpu.VMEM((2, 16, features), F32),
            pltpu.VMEM((16, features), F32),
            pltpu.VMEM((LANES, features), BF),
            dma((2, 2)),
            dma((2, 2)),
            dma,
            dma,
            dma((2,)),
            dma((2,)),
            dma((16,)),
            dma((3, 4)),
            dma((3, 4)),
            dma((4,)),
            dma((4,)),
            dma((4,)),
            dma((4,)),
            dma((6,)),
            dma((6,)),
            dma((peers, 4)),
            dma((peers, 4)),
            dma((10,)),
        ],
        compiler_params=pltpu.CompilerParams(
            collective_id=3, has_side_effects=True, vmem_limit_bytes=62 << 20
        ),
        cost_estimate=pl.CostEstimate(
            flops=2 * rows * features * 3 * slot, bytes_accessed=40 << 20, transcendentals=0
        ),
    )(prompt, cont, small, ints, wq, wg, wk, wv, w_out)


def ring_body(
    ring,
    x_prompt,
    x_cont,
    teacher_prompt,
    teacher_cont,
    segment_ids,
    offsets,
    prompt_valid,
    cont_valid,
    first_gain,
    w_query,
    w_key,
    w_value,
    w_outgate,
    w_forget,
    forget_bias,
    w_out,
    second_gain,
    w_gate,
    w_up,
    w_down,
):
    y = lax.axis_index("y")
    c = lax.axis_index("c")
    x = lax.axis_index("x")
    zh = lax.axis_index("zh")
    zl = lax.axis_index("zl")
    zl_count = ring.zl_count
    local = x_prompt.shape[1]
    half_d = x_prompt.shape[2]
    part_d = half_d // 2
    local_conts = x_cont.shape[1]
    heads = w_forget.shape[1]
    units_here = w_gate.shape[1]
    half_units = units_here // 2
    width = heads * HEAD_DIM
    slots = heads // 2
    pair_unit = PROMPT // CLEN
    chunk_units = local // CLEN
    own_valid = jnp.where(x == 0, prompt_valid.reshape(-1), cont_valid.reshape(-1))
    small_in = jnp.concatenate([own_valid, segment_ids.reshape(-1), offsets.reshape(-1)])
    int_rows = 16
    ints = jnp.pad(small_in, (0, int_rows * LANES - small_in.shape[0])).reshape(int_rows, LANES)
    packed = jnp.concatenate(
        [
            first_gain[None].astype(F32),
            second_gain[None].astype(F32),
            jnp.pad(forget_bias, (0, half_d - heads))[None],
            jnp.zeros((5, half_d), F32),
            w_forget.T.astype(F32),
            jnp.zeros((8 - heads, half_d), F32),
        ],
        axis=0,
    )
    (
        tokens_b,
        normed_all,
        w_slots,
        w_out_all,
        small_all,
        gains,
        w_forget_rows,
        ints,
        proj_a,
        proj_b,
        proj_c,
        forget_own,
        there_a,
        there_b,
        there_c,
        forget_there,
    ) = first_step(
        ring,
        x_prompt[0],
        x_cont.reshape(local_conts * CLEN, half_d),
        packed,
        ints,
        w_query,
        w_outgate,
        w_key,
        w_value,
        w_out,
    )
    projects = [proj_a, proj_b, proj_c]
    kv_there = [there_a, there_b, there_c]
    ints = ints.reshape(-1)
    validity = ints[:local].astype(F32)
    segment_row = ints[local : local + PROMPT]
    offset_row = ints[local + PROMPT : local + PROMPT + CONTS]
    gain_one = gains[0]
    gain_two = gains[1]

    def head_slots(value):
        first = jnp.where(y == 0, value[:, 0:2], value[:, 4:6])
        slot_a = jnp.where(zh == 0, first[0], first[1])
        slot_c = jnp.where(zh == 0, first[1], first[0])
        slot_b = jnp.where((y + zl) % 2 == 0, value[0, 2:4], value[1, 2:4])
        return jnp.concatenate([slot_a, slot_b, slot_c], axis=0)

    bias_all = small_all[:, 2, :heads]
    bias_all = jnp.stack(
        [
            jnp.where(zh == 0, bias_all[0], bias_all[1]),
            jnp.where(zh == 0, bias_all[1], bias_all[0]),
        ]
    )
    bias_row = head_slots(bias_all[:, :, None])[:, 0]
    bias_row = jnp.concatenate([bias_row, jnp.zeros((LANES - heads,), F32)])[None]

    proj_a, w_gate_late, w_up_late = lax.optimization_barrier((proj_a, w_gate, w_up))
    projects[0] = proj_a
    hid_there_w = ring.swap(
        jnp.concatenate(
            [
                lax.dynamic_slice(w, (c * part_d, y * half_units), (part_d, half_units))
                for w in (w_gate_late, w_up_late)
            ],
            axis=1,
        ),
        "zh",
    )

    dy_all = jnp.array([o[0] for o in ring.offsets], jnp.int32)
    dz_all = jnp.array([o[1] for o in ring.offsets], jnp.int32)
    places = ((y - dy_all) % 2) * zl_count + (zl - dz_all) % zl_count
    unit_no = (places[:, None] * chunk_units + jnp.arange(chunk_units, dtype=jnp.int32)).reshape(-1)
    natural = jnp.arange(pair_unit, dtype=jnp.int32)
    pick = unit_no[:, None] == natural[None, :]
    step = jnp.arange(CLEN, dtype=jnp.int32)
    row_pos = (unit_no[:, None] * CLEN + step[None, :]).reshape(-1)
    seg_rel = jnp.sum(
        jnp.where(pick[:, :, None], segment_row.reshape(1, pair_unit, CLEN), 0), axis=1
    )
    offs_rel = jnp.sum(jnp.where(pick, offset_row[None, :], 0), axis=1)
    last_rel = jnp.sum(
        jnp.where(
            jnp.arange(PROMPT, dtype=jnp.int32)[None, :] == offs_rel[:, None] - 1,
            segment_row[None, :],
            0,
        ),
        axis=1,
    )
    limit = jnp.where(c == 0, unit_no * CLEN, offs_rel)
    doc_row = jnp.where(c == 0, seg_rel, last_rel[:, None]).reshape(-1, 1)
    seg_col = seg_rel.reshape(-1, 1)
    lane = jnp.arange(LANES, dtype=jnp.int32)[None, :]
    unit_col = jnp.repeat(natural, CLEN)[:, None]
    pieces = 3 * heads
    is_doc = (lane >= DOC_LANE) & (lane < DOC_LANE + 4)
    is_unit = (lane >= UNIT_LANE) & (lane < UNIT_LANE + pair_unit)
    limit_lane = jnp.pad(limit, (UNIT_LANE, LANES - UNIT_LANE - pair_unit))[None, :]
    q_base = jnp.where(
        (lane >= FAR_PIECE) & (lane < FAR_PIECE + pieces),
        1.0,
        jnp.where(
            (is_doc & (doc_row != lane - DOC_LANE)) | (is_unit & (unit_col == lane - UNIT_LANE)),
            -NEVER,
            0.0,
        ),
    ).astype(BF)
    near_base = jnp.where(
        (lane < pieces) | (is_doc & (doc_row == lane - DOC_LANE)), 1.0, 0.0
    ).astype(BF)
    far_base = jnp.where(
        (lane < pieces)
        | (is_doc & (seg_col == lane - DOC_LANE))
        | (is_unit & (row_pos[:, None] >= limit_lane)),
        1.0,
        0.0,
    ).astype(BF)
    tri = (step[:, None] >= step[None, :]).astype(F32)
    earlier = (unit_no[None, :] < unit_no[:, None]).astype(F32)
    hot = (row_pos[None, :] == limit[:, None] - 1).astype(F32)
    cont_hot = (row_pos[None, :] == offs_rel[:, None] - 1).astype(F32)

    forget_far = jnp.where(c == 0, forget_own, forget_there)
    flag = c.astype(jnp.int32).reshape(1)
    head_lane = lane < heads

    def keep_log(lin):
        return jnp.where(head_lane, jax.nn.log_sigmoid(lin.astype(F32) + bias_row), 0.0)

    def within(values, matrix):
        return jnp.einsum(
            "ts,ush->uth", matrix, values.reshape(pair_unit, CLEN, LANES), precision=highest
        )

    far_within = within(keep_log(forget_far), tri)
    far_prefix = jnp.dot(earlier, far_within[:, -1], precision=highest)
    cum_far = (far_within + far_prefix[:, None]).reshape(-1, LANES)
    own_base = jnp.dot(hot, cum_far, precision=highest)
    cum_near = (within(keep_log(forget_own), tri) + own_base[:, None]).reshape(-1, LANES)
    keep_slope = jnp.where(
        head_lane, jax.nn.sigmoid(-(forget_own.astype(F32) + bias_row)), 0.0
    )
    gated, attended, logs = attend(
        flag, projects, kv_there, cum_near, cum_far, q_base, near_base, far_base, local, heads
    )
    (
        grad_gated,
        grad_residual,
        grad_residual_all,
        hid_kept,
        hid_there,
        down_kept,
        down_there,
        error_rows,
        gain_two_rows,
    ) = middle_step(
        ring,
        gated,
        w_out_all,
        w_gate,
        w_up,
        hid_there_w,
        w_down,
        tokens_b,
        teacher_prompt[0],
        teacher_cont.reshape(local_conts * CLEN, half_d),
        validity[:, None],
        gain_two[None],
    )
    dqg, dkv_near, dkv_far, row_sum, near_sum, far_sum = attend_back(
        flag,
        projects,
        kv_there,
        cum_near,
        cum_far,
        q_base,
        near_base,
        far_base,
        grad_gated,
        attended,
        logs,
        local,
        heads,
    )

    edge = 2 * half_units
    hid_z = ring.swap((hid_kept[:, edge:] + hid_there[:, edge:].astype(F32)).astype(BF), "zh")
    down_there = ring.swap(down_there, "x")
    rows_back, proj_all, gate_all, up_all, down_all, out_all, small_sums = last_step(
        ring,
        heads,
        [
            dqg,
            dkv_near,
            dkv_far,
            row_sum,
            near_sum,
            far_sum,
            w_slots,
            normed_all,
            gated,
            grad_residual_all,
            tokens_b,
            grad_residual,
            hid_kept,
            hid_there,
            hid_z,
            down_kept,
            down_there,
        ],
        [
            gain_one[None],
            w_forget_rows,
            keep_slope,
            cont_hot.T,
            error_rows,
            gain_two_rows,
            validity[:, None],
        ],
    )
    gain_one_sum = small_sums[:, 0].reshape(-1)
    gain_two_sum = small_sums[:, 1].reshape(-1)
    sums = small_sums[0, 2]
    forget_grad = proj_all[:, 4 * width : 4 * width + heads]
    error_total = sums[0]
    count_total = sums[1]
    groups = ring.sizes["yo"] * ring.sizes["y"] * ring.sizes["c"]
    grad_scale = groups * (PROMPT + CONTS * CLEN) / count_total
    loss_value = error_total / (D * count_total)
    (
        prompt_grad,
        cont_grad,
        query_grad,
        outgate_grad,
        key_grad,
        value_grad,
        gate_grad,
        up_grad,
        down_grad,
        out_grad,
    ) = scale_step(
        float(groups * (PROMPT + CONTS * CLEN)),
        small_sums,
        rows_back,
        proj_all,
        gate_all,
        up_all,
        down_all,
        out_all,
    )

    def own_half(value):
        return lax.dynamic_slice_in_dim(value, x * half_d, half_d, value.ndim - 1)

    quarter_no = zh * zl_count + zl
    bias_out = lax.dynamic_slice_in_dim(sums, 2 + quarter_no * heads, heads, 0)

    def scaled(value):
        return value.astype(F32) * grad_scale

    return (
        loss_value,
        prompt_grad[None],
        cont_grad.reshape(1, local_conts, CLEN, half_d),
        scaled(own_half(gain_one_sum)),
        query_grad,
        key_grad,
        value_grad,
        outgate_grad,
        scaled(forget_grad),
        scaled(bias_out),
        out_grad,
        scaled(own_half(gain_two_sum)),
        gate_grad,
        up_grad,
        down_grad,
    )


def specs(dp, row, col):
    in_specs = (
        P(dp, col, row),
        P(dp, col, None, row),
        P(dp, col, row),
        P(dp, col, None, row),
        P(dp, None),
        P(dp, None),
        P(dp, col),
        P(dp, col, None),
        P(row),
        P(row, col),
        P(row, col),
        P(row, col),
        P(row, col),
        P(row, col),
        P(col),
        P(col, row),
        P(row),
        P(row, col),
        P(row, col),
        P(col, row),
    )
    out_specs = (
        P(),
        P(dp, col, row),
        P(dp, col, None, row),
        P(row),
        P(row, col),
        P(row, col),
        P(row, col),
        P(row, col),
        P(row, col),
        P(col),
        P(col, row),
        P(row),
        P(row, col),
        P(row, col),
        P(col, row),
    )
    return in_specs, out_specs


def solution(mesh):
    dp, row, col = mesh.shape["dp"], mesh.shape["row"], mesh.shape["col"]
    heads = HEADS // col
    if dp == 4 and row == 2 and col % 2 == 0 and heads == 6:
        sizes = {"yo": dp // 4, "y": 2, "c": 2, "x": 2, "zh": 2, "zl": col // 2}
        ring_mesh = Mesh(mesh.devices.reshape([sizes[a] for a in AX]), AX)
        in_specs, out_specs = specs(("yo", "y", "c"), "x", ("zh", "zl"))
        step = functools.partial(ring_body, Ring(sizes))
        return jax.shard_map(
            step, mesh=ring_mesh, in_specs=in_specs, out_specs=out_specs, check_vma=False
        )
    in_specs, out_specs = specs("dp", "row", "col")
    return jax.shard_map(
        wide_body, mesh=mesh, in_specs=in_specs, out_specs=out_specs, check_vma=False
    )
```

```python
import functools
import itertools

import jax
import jax.numpy as jnp
from jax import lax
from jax.experimental import pallas as pl
from jax.experimental.pallas import tpu as pltpu
from jax.sharding import Mesh, PartitionSpec as P

D = 1536
HEADS = 24
HEAD_DIM = 64
PROMPT = 1024
CONTS = 8
CLEN = 128


epsilon = 1e-06
highest = lax.Precision.HIGHEST
masked = -1e30


def matmul(left_op, right_op):
    return jnp.dot(left_op, right_op, preferred_element_type=jnp.float32)


def by_transpose(left_op, right_op):
    return lax.dot_general(
        left_op, right_op, (((1,), (1,)), ((), ())), preferred_element_type=jnp.float32
    )


def inner_rows(left_op, right_op):
    return lax.dot_general(
        left_op, right_op, (((0,), (0,)), ((), ())), preferred_element_type=jnp.float32
    )


def feature_total(partial_sum):
    return lax.psum(partial_sum, "row")


def group_rows(local_rows):
    return lax.all_gather(local_rows, "col", axis=0, tiled=True)


def token_sums(partial_rows):
    return lax.psum_scatter(
        partial_rows.astype(jnp.bfloat16), "col", scatter_dimension=0, tiled=True
    ).astype(jnp.float32)


def row_partials(partial_rows, col_count, blocks, quarter):
    shaped = partial_rows.reshape(
        col_count, blocks, lax.axis_size("row"), quarter, partial_rows.shape[-1]
    )
    return lax.psum_scatter(
        shaped.astype(jnp.bfloat16), "row", scatter_dimension=2, tiled=True
    ).astype(jnp.float32)


def head_rows(own_rows):
    gathered = lax.all_gather(own_rows, "row", axis=2, tiled=True)
    return gathered.reshape(-1, gathered.shape[-1])


def norm_forward(tokens, gain_vec):
    row_total = feature_total(jnp.sum(tokens * tokens, axis=-1))
    factor = lax.rsqrt(row_total / D + epsilon)
    scaled = tokens * factor[:, None]
    return (factor, scaled, (scaled * gain_vec).astype(jnp.bfloat16))


def norm_backward(grad_normed, factor, scaled, gain_vec):
    grad_scaled = grad_normed * gain_vec
    row_total = feature_total(jnp.sum(grad_scaled * scaled, axis=-1))
    gain_grad = jnp.sum(grad_normed * scaled, axis=0)
    return (gain_grad, factor[:, None] * (grad_scaled - scaled * (row_total / D)[:, None]))


def log_total(scores):
    row_top = jnp.max(scores, axis=-1, keepdims=True)
    return row_top + jnp.log(jnp.sum(jnp.exp(scores - row_top), axis=-1, keepdims=True))


def prompt_scores(queries, key_rows, cum_query, cum_key, allowed):
    raw_scores = jnp.einsum("qhd,khd->hqk", queries, key_rows, preferred_element_type=jnp.float32)
    raw_scores = raw_scores * HEAD_DIM ** (-0.5) + cum_query.T[:, :, None] - cum_key.T[:, None, :]
    return jnp.where(allowed[None], raw_scores, masked)


def cont_scores(queries, key_rows, key_cont, cum_query, cum_key, cum_cont, far_ok, near_ok):
    score_scale = HEAD_DIM ** (-0.5)
    query_cum = cum_query.transpose(0, 2, 1)[:, :, :, None]
    far_scores = jnp.einsum("jqhd,khd->jhqk", queries, key_rows, preferred_element_type=jnp.float32)
    far_scores = far_scores * score_scale + query_cum - cum_key.T[None, :, None, :]
    near_scores = jnp.einsum(
        "jqhd,jkhd->jhqk", queries, key_cont, preferred_element_type=jnp.float32
    )
    near_scores = near_scores * score_scale + query_cum - cum_cont.transpose(0, 2, 1)[:, :, None, :]
    far_scores = jnp.where(far_ok[:, None, None, :], far_scores, masked)
    near_scores = jnp.where(near_ok[None, None], near_scores, masked)
    return jnp.concatenate([far_scores, near_scores], axis=-1)


def wide_body(
    x_prompt,
    x_cont,
    teacher_prompt,
    teacher_cont,
    segment_ids,
    offsets,
    prompt_valid,
    cont_valid,
    first_gain,
    w_query,
    w_key,
    w_value,
    w_outgate,
    w_forget,
    forget_bias,
    w_out,
    second_gain,
    w_gate,
    w_up,
    w_down,
):
    row_count = lax.axis_size("row")
    col_count = lax.axis_size("col")
    row_index = lax.axis_index("row")
    local_prompt = x_prompt.shape[1]
    local_conts = x_cont.shape[1]
    quarter = CLEN // row_count
    local_tokens = local_prompt + local_conts * CLEN
    blocks = local_tokens // CLEN
    prompt_blocks = local_prompt // CLEN
    heads_here = w_forget.shape[1]
    width_here = heads_here * HEAD_DIM
    units_here = w_gate.shape[1]
    score_scale = HEAD_DIM ** (-0.5)
    w_project = jnp.concatenate([w_query, w_key, w_value, w_outgate], axis=1)
    w_hidden = jnp.concatenate([w_gate, w_up], axis=1)
    gain_one = first_gain.astype(jnp.float32)
    gain_two = second_gain.astype(jnp.float32)
    position = jnp.arange(PROMPT, dtype=jnp.int32)
    cont_step = jnp.arange(CLEN, dtype=jnp.int32)
    own_step = row_index * quarter + jnp.arange(quarter, dtype=jnp.int32)
    near_ok = cont_step[None, :] <= own_step[:, None]
    own_position = lax.dynamic_index_in_dim(
        position.reshape(col_count, prompt_blocks, row_count, quarter), row_index, 2, keepdims=False
    ).reshape(-1)

    def own_prompt_part(matrix):
        return matrix[:, :prompt_blocks, 0]

    def one_group(carried, group_data):
        (
            acc_project,
            acc_forget,
            acc_bias,
            acc_out,
            acc_hidden,
            acc_down,
            acc_gain_one,
            acc_gain_two,
            error_sum,
            count_sum,
        ) = carried
        (
            prompt_in,
            cont_in,
            teach_prompt,
            teach_cont,
            segment_row,
            offset_row,
            valid_prompt,
            valid_cont,
        ) = group_data
        tokens = jnp.concatenate(
            [prompt_in, cont_in.reshape(local_conts * CLEN, -1)], axis=0
        ).astype(jnp.float32)
        teacher = jnp.concatenate(
            [teach_prompt, teach_cont.reshape(local_conts * CLEN, -1)], axis=0
        ).astype(jnp.float32)
        validity = jnp.concatenate([valid_prompt, valid_cont.reshape(-1)], axis=0).astype(
            jnp.float32
        )
        branch_mask = position[None, :] == offset_row[:, None] - 1
        branch_hot = branch_mask.astype(jnp.float32)
        last_doc = jnp.sum(jnp.where(branch_mask, segment_row[None, :], 0), axis=1)
        far_ok = (position[None, :] < offset_row[:, None]) & (
            segment_row[None, :] == last_doc[:, None]
        )
        own_doc = lax.dynamic_index_in_dim(
            segment_row.reshape(col_count, prompt_blocks, row_count, quarter),
            row_index,
            2,
            keepdims=False,
        ).reshape(-1)
        prompt_ok = (position[None, :] <= own_position[:, None]) & (
            segment_row[None, :] == own_doc[:, None]
        )
        factor_one, scaled_one, normed_one = norm_forward(tokens, gain_one)
        normed_all = group_rows(normed_one)
        project_part = matmul(normed_all, w_project).reshape(
            col_count, blocks, row_count, quarter, 4 * width_here
        )
        forget_part = matmul(normed_all, w_forget).reshape(
            col_count, blocks, row_count, quarter, heads_here
        )
        own_project, own_forget = (
            lax.psum_scatter(project_part, "row", scatter_dimension=2, tiled=True),
            lax.psum_scatter(forget_part, "row", scatter_dimension=2, tiled=True),
        )
        own_query = own_project[..., :width_here].astype(jnp.bfloat16)
        own_kv = own_project[..., width_here : 3 * width_here].astype(jnp.bfloat16)
        gate_logit = own_project[..., 3 * width_here :]
        kv_all, forget_all = (
            lax.all_gather(own_kv, "row", axis=2, tiled=True),
            lax.all_gather(own_forget.astype(jnp.bfloat16), "row", axis=2, tiled=True),
        )
        kv_all = kv_all.reshape(col_count, local_tokens, 2 * width_here)
        pre_gate = (
            forget_all.reshape(col_count, local_tokens, heads_here).astype(jnp.float32)
            + forget_bias
        )
        log_keep = jax.nn.log_sigmoid(pre_gate)
        cum_prompt = jnp.cumsum(log_keep[:, :local_prompt].reshape(PROMPT, heads_here), axis=0)
        branch_cum = jnp.dot(branch_hot, cum_prompt, precision=highest)
        cum_cont = branch_cum[:, None, :] + jnp.cumsum(
            log_keep[:, local_prompt:].reshape(CONTS, CLEN, heads_here), axis=1
        )
        kv_prompt = kv_all[:, :local_prompt].reshape(PROMPT, 2, heads_here, HEAD_DIM)
        key_prompt = kv_prompt[:, 0]
        value_prompt = kv_prompt[:, 1]
        kv_cont = kv_all[:, local_prompt:].reshape(CONTS, CLEN, 2, heads_here, HEAD_DIM)
        key_cont = kv_cont[:, :, 0]
        value_cont = kv_cont[:, :, 1]
        cum_query_prompt = lax.dynamic_index_in_dim(
            cum_prompt.reshape(col_count, prompt_blocks, row_count, quarter, heads_here),
            row_index,
            2,
            keepdims=False,
        ).reshape(-1, heads_here)
        cum_query_cont = lax.dynamic_index_in_dim(
            cum_cont.reshape(CONTS, row_count, quarter, heads_here), row_index, 1, keepdims=False
        )
        query_prompt = own_prompt_part(own_query).reshape(-1, heads_here, HEAD_DIM)
        query_cont = own_query[:, prompt_blocks:, 0].reshape(CONTS, quarter, heads_here, HEAD_DIM)
        scores_prompt = prompt_scores(
            query_prompt, key_prompt, cum_query_prompt, cum_prompt, prompt_ok
        )
        total_prompt = log_total(scores_prompt)
        probs_prompt = jnp.exp(scores_prompt - total_prompt).astype(jnp.bfloat16)
        out_prompt = jnp.einsum(
            "hqk,khd->qhd", probs_prompt, value_prompt, preferred_element_type=jnp.float32
        )
        scores_cont = cont_scores(
            query_cont, key_prompt, key_cont, cum_query_cont, cum_prompt, cum_cont, far_ok, near_ok
        )
        total_cont = log_total(scores_cont)
        probs_cont = jnp.exp(scores_cont - total_cont).astype(jnp.bfloat16)
        out_cont = jnp.einsum(
            "jhqk,khd->jqhd",
            probs_cont[..., :PROMPT],
            value_prompt,
            preferred_element_type=jnp.float32,
        )
        out_cont = out_cont + jnp.einsum(
            "jhqk,jkhd->jqhd",
            probs_cont[..., PROMPT:],
            value_cont,
            preferred_element_type=jnp.float32,
        )
        attended = jnp.concatenate(
            [
                out_prompt.reshape(col_count, prompt_blocks, 1, quarter, width_here),
                out_cont.reshape(col_count, local_conts, 1, quarter, width_here),
            ],
            axis=1,
        )
        gate_sig = jax.nn.sigmoid(gate_logit)
        gated = (attended * gate_sig).astype(jnp.bfloat16)
        gated_all = head_rows(gated)
        residual = tokens + token_sums(matmul(gated_all, w_out))
        factor_two, scaled_two, normed_two = norm_forward(residual, gain_two)
        normed_two_all = group_rows(normed_two)
        hidden_own = row_partials(matmul(normed_two_all, w_hidden), col_count, blocks, quarter)
        gate_rows = hidden_own[..., :units_here]
        up_rows = hidden_own[..., units_here:]
        gate_sig_two = jax.nn.sigmoid(gate_rows)
        silu_rows = gate_rows * gate_sig_two
        hidden_all = head_rows((silu_rows * up_rows).astype(jnp.bfloat16))
        result_rows = residual + token_sums(matmul(hidden_all, w_down))
        deviation = result_rows - teacher
        group_err = 0.5 * jnp.sum(validity[:, None] * deviation * deviation)
        grad_result = validity[:, None] * deviation
        grad_result_all = group_rows(grad_result.astype(jnp.bfloat16))
        grad_down_w = inner_rows(hidden_all, grad_result_all)
        grad_hid = row_partials(by_transpose(grad_result_all, w_down), col_count, blocks, quarter)
        grad_gate = grad_hid * up_rows * gate_sig_two * (1.0 + gate_rows * (1.0 - gate_sig_two))
        grad_up = grad_hid * silu_rows
        grad_hidden_all = head_rows(
            jnp.concatenate([grad_gate, grad_up], axis=-1).astype(jnp.bfloat16)
        )
        grad_hidden_w = inner_rows(normed_two_all, grad_hidden_all)
        grad_normed_two = token_sums(by_transpose(grad_hidden_all, w_hidden))
        gain_two_grad, grad_residual = norm_backward(
            grad_normed_two, factor_two, scaled_two, gain_two
        )
        grad_residual = grad_residual + grad_result
        grad_residual_all = group_rows(grad_residual.astype(jnp.bfloat16))
        grad_out_w = inner_rows(gated_all, grad_residual_all)
        grad_gated = row_partials(
            by_transpose(grad_residual_all, w_out), col_count, blocks, quarter
        )
        grad_attended = (grad_gated * gate_sig).astype(jnp.bfloat16)
        grad_logit = (grad_gated * attended * gate_sig * (1.0 - gate_sig)).astype(jnp.bfloat16)
        grad_att_prompt = own_prompt_part(grad_attended).reshape(-1, heads_here, HEAD_DIM)
        grad_att_cont = grad_attended[:, prompt_blocks:, 0].reshape(
            CONTS, quarter, heads_here, HEAD_DIM
        )
        again_prompt = jnp.exp(
            prompt_scores(query_prompt, key_prompt, cum_query_prompt, cum_prompt, prompt_ok)
            - total_prompt
        )
        grad_prob_prompt = jnp.einsum(
            "qhd,khd->hqk", grad_att_prompt, value_prompt, preferred_element_type=jnp.float32
        )
        grad_score_prompt = (
            again_prompt
            * (grad_prob_prompt - jnp.sum(again_prompt * grad_prob_prompt, axis=-1, keepdims=True))
        ).astype(jnp.bfloat16)
        again_prompt_b = again_prompt.astype(jnp.bfloat16)
        grad_query_prompt = (
            jnp.einsum(
                "hqk,khd->qhd", grad_score_prompt, key_prompt, preferred_element_type=jnp.float32
            )
            * score_scale
        )
        grad_key_prompt = (
            jnp.einsum(
                "hqk,qhd->khd", grad_score_prompt, query_prompt, preferred_element_type=jnp.float32
            )
            * score_scale
        )
        grad_value_prompt = jnp.einsum(
            "hqk,qhd->khd", again_prompt_b, grad_att_prompt, preferred_element_type=jnp.float32
        )
        cum_grad_query_p = jnp.sum(grad_score_prompt, axis=-1, dtype=jnp.float32).T
        cum_grad_key_p = -jnp.sum(grad_score_prompt, axis=1, dtype=jnp.float32).T
        again_cont = jnp.exp(
            cont_scores(
                query_cont,
                key_prompt,
                key_cont,
                cum_query_cont,
                cum_prompt,
                cum_cont,
                far_ok,
                near_ok,
            )
            - total_cont
        )
        grad_prob_cont = jnp.concatenate(
            [
                jnp.einsum(
                    "jqhd,khd->jhqk",
                    grad_att_cont,
                    value_prompt,
                    preferred_element_type=jnp.float32,
                ),
                jnp.einsum(
                    "jqhd,jkhd->jhqk", grad_att_cont, value_cont, preferred_element_type=jnp.float32
                ),
            ],
            axis=-1,
        )
        grad_score_cont = (
            again_cont
            * (grad_prob_cont - jnp.sum(again_cont * grad_prob_cont, axis=-1, keepdims=True))
        ).astype(jnp.bfloat16)
        again_cont_b = again_cont.astype(jnp.bfloat16)
        far_grad = grad_score_cont[..., :PROMPT]
        near_grad = grad_score_cont[..., PROMPT:]
        grad_query_cont = (
            jnp.einsum("jhqk,khd->jqhd", far_grad, key_prompt, preferred_element_type=jnp.float32)
            + jnp.einsum("jhqk,jkhd->jqhd", near_grad, key_cont, preferred_element_type=jnp.float32)
        ) * score_scale
        grad_key_far = (
            jnp.einsum("jhqk,jqhd->khd", far_grad, query_cont, preferred_element_type=jnp.float32)
            * score_scale
        )
        grad_key_near = (
            jnp.einsum("jhqk,jqhd->jkhd", near_grad, query_cont, preferred_element_type=jnp.float32)
            * score_scale
        )
        grad_value_far = jnp.einsum(
            "jhqk,jqhd->khd",
            again_cont_b[..., :PROMPT],
            grad_att_cont,
            preferred_element_type=jnp.float32,
        )
        grad_value_near = jnp.einsum(
            "jhqk,jqhd->jkhd",
            again_cont_b[..., PROMPT:],
            grad_att_cont,
            preferred_element_type=jnp.float32,
        )
        cum_grad_query_c = jnp.sum(grad_score_cont, axis=-1, dtype=jnp.float32).transpose(0, 2, 1)
        cum_grad_key_far = -jnp.sum(far_grad, axis=(0, 2), dtype=jnp.float32).T
        cum_grad_key_near = -jnp.sum(near_grad, axis=2, dtype=jnp.float32).transpose(0, 2, 1)
        kv_grad_prompt = jnp.stack(
            [grad_key_prompt + grad_key_far, grad_value_prompt + grad_value_far], axis=1
        ).reshape(col_count, local_prompt, 2 * width_here)
        kv_grad_cont = jnp.stack([grad_key_near, grad_value_near], axis=2).reshape(
            col_count, local_conts * CLEN, 2 * width_here
        )
        kv_grad_part = jnp.concatenate([kv_grad_prompt, kv_grad_cont], axis=1)
        query_place = lax.dynamic_update_slice_in_dim(
            jnp.zeros((col_count, prompt_blocks, row_count, quarter, heads_here), jnp.float32),
            cum_grad_query_p.reshape(col_count, prompt_blocks, 1, quarter, heads_here),
            row_index,
            axis=2,
        ).reshape(PROMPT, heads_here)
        cont_place = lax.dynamic_update_slice_in_dim(
            jnp.zeros((CONTS, row_count, quarter, heads_here), jnp.float32),
            cum_grad_query_c.reshape(CONTS, 1, quarter, heads_here),
            row_index,
            axis=1,
        ).reshape(CONTS, CLEN, heads_here)
        cum_grad_part = jnp.concatenate(
            [
                (cum_grad_key_p + cum_grad_key_far + query_place).reshape(
                    col_count, local_prompt, heads_here
                ),
                (cum_grad_key_near + cont_place).reshape(col_count, local_conts * CLEN, heads_here),
            ],
            axis=1,
        )
        kv_grad_full, cum_grad_full = lax.psum((kv_grad_part, cum_grad_part), "row")
        cum_grad_cont = cum_grad_full[:, local_prompt:].reshape(CONTS, CLEN, heads_here)
        cum_grad_prompt = cum_grad_full[:, :local_prompt].reshape(PROMPT, heads_here)
        cum_grad_prompt = cum_grad_prompt + jnp.dot(
            branch_hot.T, jnp.sum(cum_grad_cont, axis=1), precision=highest
        )
        log_grad_prompt = lax.cumsum(cum_grad_prompt, axis=0, reverse=True)
        log_grad_cont = lax.cumsum(cum_grad_cont, axis=1, reverse=True)
        log_grad = jnp.concatenate(
            [
                log_grad_prompt.reshape(col_count, local_prompt, heads_here),
                log_grad_cont.reshape(col_count, local_conts * CLEN, heads_here),
            ],
            axis=1,
        )
        pre_grad = log_grad * jax.nn.sigmoid(-pre_gate)
        bias_grad = jnp.sum(pre_grad, axis=(0, 1))
        forget_grad_b = pre_grad.reshape(-1, heads_here).astype(jnp.bfloat16)
        query_grad_own = jnp.concatenate(
            [
                grad_query_prompt.reshape(col_count, prompt_blocks, 1, quarter, width_here),
                grad_query_cont.reshape(col_count, local_conts, 1, quarter, width_here),
            ],
            axis=1,
        )
        qg_grad_all = head_rows(
            jnp.concatenate([query_grad_own.astype(jnp.bfloat16), grad_logit], axis=-1)
        )
        kv_grad_rows = kv_grad_full.reshape(-1, 2 * width_here).astype(jnp.bfloat16)
        project_grad_rows = jnp.concatenate(
            [qg_grad_all[:, :width_here], kv_grad_rows, qg_grad_all[:, width_here:]], axis=-1
        )
        grad_project_w = inner_rows(normed_all, project_grad_rows)
        grad_forget_w = inner_rows(normed_all, forget_grad_b)
        grad_normed_one = token_sums(
            by_transpose(project_grad_rows, w_project) + by_transpose(forget_grad_b, w_forget)
        )
        gain_one_grad, grad_tokens = norm_backward(
            grad_normed_one, factor_one, scaled_one, gain_one
        )
        grad_tokens = grad_tokens + grad_residual
        grad_prompt_one = grad_tokens[:local_prompt]
        grad_cont_one = grad_tokens[local_prompt:].reshape(local_conts, CLEN, -1)
        group_count = jnp.sum(validity) * (row_index == 0).astype(jnp.float32)
        new_carry = (
            acc_project + grad_project_w,
            acc_forget + grad_forget_w,
            acc_bias + bias_grad,
            acc_out + grad_out_w,
            acc_hidden + grad_hidden_w,
            acc_down + grad_down_w,
            acc_gain_one + gain_one_grad,
            acc_gain_two + gain_two_grad,
            error_sum + group_err,
            count_sum + group_count,
        )
        return (new_carry, (grad_prompt_one, grad_cont_one))

    start = (
        jnp.zeros(w_project.shape, jnp.float32),
        jnp.zeros(w_forget.shape, jnp.float32),
        jnp.zeros(forget_bias.shape, jnp.float32),
        jnp.zeros(w_out.shape, jnp.float32),
        jnp.zeros(w_hidden.shape, jnp.float32),
        jnp.zeros(w_down.shape, jnp.float32),
        jnp.zeros(first_gain.shape, jnp.float32),
        jnp.zeros(second_gain.shape, jnp.float32),
        jnp.zeros((), jnp.float32),
        jnp.zeros((), jnp.float32),
    )
    finished, (grad_prompt, grad_cont) = lax.scan(
        one_group,
        start,
        (
            x_prompt,
            x_cont,
            teacher_prompt,
            teacher_cont,
            segment_ids,
            offsets,
            prompt_valid,
            cont_valid,
        ),
    )
    (
        acc_project,
        acc_forget,
        acc_bias,
        acc_out,
        acc_hidden,
        acc_down,
        acc_gain_one,
        acc_gain_two,
        error_sum,
        count_sum,
    ) = finished
    acc_project, acc_forget, acc_bias, acc_out, acc_hidden, acc_down = (
        lax.psum(acc_project.astype(jnp.bfloat16), "dp").astype(jnp.float32),
        lax.psum(acc_forget.astype(jnp.bfloat16), "dp").astype(jnp.float32),
        lax.psum(acc_bias.astype(jnp.bfloat16), "dp").astype(jnp.float32),
        lax.psum(acc_out.astype(jnp.bfloat16), "dp").astype(jnp.float32),
        lax.psum(acc_hidden.astype(jnp.bfloat16), "dp").astype(jnp.float32),
        lax.psum(acc_down.astype(jnp.bfloat16), "dp").astype(jnp.float32),
    )
    gain_one_total, gain_two_total = lax.psum((acc_gain_one, acc_gain_two), ("dp", "col"))
    error_total, count_total = lax.psum((error_sum, count_sum), ("dp", "row", "col"))
    grad_scale = x_prompt.shape[0] * lax.axis_size("dp") * (PROMPT + CONTS * CLEN) / count_total
    loss_value = error_total / (D * count_total)
    width_here = w_query.shape[1]
    units_here = w_gate.shape[1]
    return (
        loss_value,
        grad_prompt * grad_scale,
        grad_cont * grad_scale,
        gain_one_total * grad_scale,
        acc_project[:, :width_here] * grad_scale,
        acc_project[:, width_here : 2 * width_here] * grad_scale,
        acc_project[:, 2 * width_here : 3 * width_here] * grad_scale,
        acc_project[:, 3 * width_here :] * grad_scale,
        acc_forget * grad_scale,
        acc_bias * grad_scale,
        acc_out * grad_scale,
        gain_two_total * grad_scale,
        acc_hidden[:, :units_here] * grad_scale,
        acc_hidden[:, units_here:] * grad_scale,
        acc_down * grad_scale,
    )


AX = ("yo", "y", "c", "x", "zh", "zl")
FAR_PIECE = 18
DOC_LANE = 36
UNIT_LANE = 40
NEVER = 1e12
LANES = 128
BF = jnp.bfloat16
F32 = jnp.float32


class Ring:
    def __init__(self, sizes):
        self.sizes = sizes
        self.zl_count = sizes["zl"]
        self.offsets = [(dy, dz) for dy in range(2) for dz in range(self.zl_count)]
        self.back = [
            self.offsets.index(((-dy) % 2, (-dz) % self.zl_count)) for dy, dz in self.offsets
        ]

    def pairs(self, target, source_ok=None):
        ranges = [range(self.sizes[a]) for a in AX]
        number = {}
        for place, coords in enumerate(itertools.product(*ranges)):
            number[coords] = place
        out = []
        for coords in number:
            here = dict(zip(AX, coords))
            if source_ok is not None and not source_ok(here):
                continue
            there = dict(here, **target(here))
            out.append((number[coords], number[tuple(there[a] for a in AX)]))
        return out

    def move(self, value, target, source_ok=None):
        return lax.ppermute(value, AX, self.pairs(target, source_ok))

    def swap(self, value, axis, source_ok=None):
        return self.move(value, lambda h: {axis: 1 - h[axis]}, source_ok)

    def to_peer(self, value, k):
        dy, dz = self.offsets[k]
        return self.move(
            value, lambda h: {"y": (h["y"] + dy) % 2, "zl": (h["zl"] + dz) % self.zl_count}
        )

    def to_group(self, value, flip):
        return self.move(
            value,
            lambda h: {
                "y": h["zh"],
                "c": h["x"] ^ flip,
                "x": h["y"],
                "zh": h["c"],
            },
        )

    def from_group(self, value, flip):
        return self.move(
            value,
            lambda h: {"y": h["x"], "c": h["zh"], "x": h["c"] ^ flip, "zh": h["y"]},
        )

    def total(self, value):
        for axis in ("c", "y", "x", "zh"):
            value = value + self.swap(value, axis)
        if self.zl_count == 2:
            value = value + self.swap(value, "zl")
        elif self.zl_count > 2:
            value = lax.psum(value, "zl")
        if self.sizes["yo"] > 1:
            value = lax.psum(value, "yo")
        return value

    def gather(self, rows):
        return [rows] + [self.to_peer(rows, k) for k in range(1, len(self.offsets))]

    def scatter_sum(self, partial_of):
        arrived = []
        for k in range(1, len(self.offsets)):
            arrived.append(self.to_peer(partial_of(self.back[k]).astype(BF), k))
        total = partial_of(0)
        for part in arrived:
            total = total + part.astype(F32)
        return total


def nt_dot(left_op, right_op):
    return lax.dot_general(
        left_op, right_op, (((1,), (1,)), ((), ())), preferred_element_type=F32
    )


def tn_dot(left_op, right_op):
    return lax.dot_general(
        left_op, right_op, (((0,), (0,)), ((), ())), preferred_element_type=F32
    )


def nn_dot(left_op, right_op):
    return jnp.dot(left_op, right_op, preferred_element_type=F32)


def split_pieces(values, shift, heads):
    high = values.astype(BF).astype(F32)
    rest = values - high
    mid = rest.astype(BF).astype(F32)
    low = (rest - mid).astype(BF).astype(F32)
    out = None
    for place, piece in enumerate((high, mid, low)):
        amount = shift + place * heads
        moved = pltpu.roll(piece, amount, 1) if amount else piece
        out = moved if out is None else out + moved
    return out


def head_lanes(shape, head, heads):
    lane = lax.broadcasted_iota(jnp.int32, shape, len(shape) - 1)
    keep = lane >= DOC_LANE
    for place in range(3):
        keep = keep | (lane == place * heads + head) | (lane == FAR_PIECE + place * heads + head)
    return keep


def half_lanes(shape, half):
    lane = lax.broadcasted_iota(jnp.int32, shape, len(shape) - 1)
    return (lane >= HEAD_DIM * half) & (lane < HEAD_DIM * (half + 1))


def near_visible(rows):
    key_row = lax.broadcasted_iota(jnp.int32, (rows, rows), 0)
    query_row = lax.broadcasted_iota(jnp.int32, (rows, rows), 1)
    same = (key_row // CLEN) == (query_row // CLEN)
    return same & (key_row <= query_row)


def fill_keys(
    keys, flag, far_own, far_there, kv_near, cum_far, cum_near, far_base, near_base, far_rows, heads
):
    slots = heads // 2

    @pl.when(pl.program_id(0) == 0)
    def _():
        aug = (far_base[...].astype(F32) + split_pieces(-cum_far[...], FAR_PIECE, heads)).astype(BF)
        for s in range(slots):
            keys[s, :far_rows, LANES:] = aug

        @pl.when(flag[0] == 0)
        def _():
            for s in range(slots):
                keys[s, :far_rows, :LANES] = far_own[s][:, :LANES]

        @pl.when(flag[0] != 0)
        def _():
            for s in range(slots):
                keys[s, :far_rows, :LANES] = far_there[s][:, :LANES]

    aug = (near_base[...].astype(F32) + split_pieces(-cum_near[...], FAR_PIECE, heads)).astype(BF)
    for s in range(slots):
        keys[s, far_rows:, :LANES] = kv_near[s][:, :LANES]
        keys[s, far_rows:, LANES:] = aug


def attend_kernel(
    heads,
    flag,
    qg_a,
    qg_b,
    qg_c,
    near_a,
    near_b,
    near_c,
    own_a,
    own_b,
    own_c,
    there_a,
    there_b,
    there_c,
    cum_near,
    cum_far,
    q_base,
    near_base,
    far_base,
    gated_ref,
    att_ref,
    log_ref,
    keys,
    vals,
):
    qg = (qg_a, qg_b, qg_c)
    kv_near = (near_a, near_b, near_c)
    far_own = (own_a, own_b, own_c)
    far_there = (there_a, there_b, there_c)
    rows = qg_a.shape[0]
    far_rows = own_a.shape[0]
    slots = heads // 2
    fill_keys(
        keys,
        flag,
        far_own,
        far_there,
        kv_near,
        cum_far,
        cum_near,
        far_base,
        near_base,
        far_rows,
        heads,
    )

    @pl.when(pl.program_id(0) == 0)
    def _():
        def fill(source):
            for s in range(slots):
                moved = source[s][:, LANES:].T
                for half in range(2):
                    vals[2 * s + half, :HEAD_DIM, :far_rows] = moved[
                        HEAD_DIM * half : HEAD_DIM * (half + 1)
                    ]

        @pl.when(flag[0] == 0)
        def _():
            fill(far_own)

        @pl.when(flag[0] != 0)
        def _():
            fill(far_there)

        for h in range(heads):
            vals[h, HEAD_DIM:, :] = jnp.ones((16, far_rows + rows), BF)

    for s in range(slots):
        moved = kv_near[s][:, LANES:].T
        for half in range(2):
            vals[2 * s + half, :HEAD_DIM, far_rows:] = moved[
                HEAD_DIM * half : HEAD_DIM * (half + 1)
            ]
    q_aug = (q_base[...].astype(F32) + split_pieces(cum_near[...], 0, heads)).astype(BF)
    visible = near_visible(rows)
    outs = []
    logs = []
    for h in range(heads):
        s, half = h // 2, h % 2
        query = qg[s][:, :LANES]
        query = jnp.where(half_lanes(query.shape, half), query * BF(HEAD_DIM**-0.5), BF(0))
        aug = jnp.where(head_lanes(q_aug.shape, h, heads), q_aug, BF(0))
        q_cat = jnp.concatenate([query, aug], axis=1)
        far = nt_dot(keys[s, :far_rows], q_cat)
        near = jnp.where(visible, nt_dot(keys[s, far_rows:], q_cat), -NEVER)
        top = jnp.maximum(
            jnp.max(far, axis=0, keepdims=True), jnp.max(near, axis=0, keepdims=True)
        )
        far_p = jnp.exp(far - top).astype(BF)
        near_p = jnp.exp(near - top).astype(BF)
        out = nn_dot(vals[h, :, :far_rows], far_p) + nn_dot(vals[h, :, far_rows:], near_p)
        total = out[HEAD_DIM : HEAD_DIM + 1]
        outs.append(out[:HEAD_DIM] / total)
        logs.append(top + jnp.log(total))
    att = jnp.concatenate(outs, axis=0).T
    att_ref[...] = att
    for s in range(slots):
        gate = qg[s][:, LANES:].astype(F32)
        cols = slice(s * LANES, (s + 1) * LANES)
        gated_ref[:, cols] = (att[:, cols] * jax.nn.sigmoid(gate)).astype(BF)
    log_rows = jnp.concatenate(logs + [jnp.zeros((LANES - heads, rows), F32)], axis=0)
    log_ref[...] = log_rows.T


def row_block(rows, cols, place=0):
    return pl.BlockSpec((rows, cols), lambda i: (i, place))


def whole_block(rows, cols):
    return pl.BlockSpec((rows, cols), lambda i: (0, 0))


def slot_inputs(flag, projects, kv_there, rows):
    far_rows = projects[0].shape[0]
    specs_in = [pl.BlockSpec(memory_space=pltpu.SMEM)]
    for spec in (
        row_block(rows, 2 * LANES),
        row_block(rows, 2 * LANES, 1),
        pl.BlockSpec((far_rows, 2 * LANES), lambda i: (0, 1)),
        whole_block(far_rows, 2 * LANES),
    ):
        specs_in += [spec] * len(projects)
    return specs_in, [flag, *projects, *projects, *projects, *kv_there]


def cum_specs(rows, far_rows):
    return [
        row_block(rows, LANES),
        whole_block(far_rows, LANES),
        row_block(rows, LANES),
        row_block(rows, LANES),
        whole_block(far_rows, LANES),
    ]


def attend(flag, projects, kv_there, cum_near, cum_far, q_base, near_base, far_base, rows, heads):
    total = projects[0].shape[0]
    width = heads * HEAD_DIM
    steps = total // rows
    flops = 2 * total * (total + rows) * heads * 384
    slot_specs, slot_values = slot_inputs(flag, projects, kv_there, rows)
    return pl.pallas_call(
        functools.partial(attend_kernel, heads),
        grid=(steps,),
        out_shape=(
            jax.ShapeDtypeStruct((total, width), BF),
            jax.ShapeDtypeStruct((total, width), F32),
            jax.ShapeDtypeStruct((total, LANES), F32),
        ),
        in_specs=slot_specs + cum_specs(rows, total),
        out_specs=(row_block(rows, width), row_block(rows, width), row_block(rows, LANES)),
        scratch_shapes=[
            pltpu.VMEM((heads // 2, total + rows, 2 * LANES), BF),
            pltpu.VMEM((heads, HEAD_DIM + 16, total + rows), BF),
        ],
        compiler_params=pltpu.CompilerParams(vmem_limit_bytes=60 << 20),
        cost_estimate=pl.CostEstimate(
            flops=flops, bytes_accessed=total * width * 20, transcendentals=total * total * heads
        ),
    )(*slot_values, cum_near, cum_far, q_base, near_base, far_base)


def attend_back_kernel(
    heads,
    flag,
    qg_a,
    qg_b,
    qg_c,
    near_a,
    near_b,
    near_c,
    own_a,
    own_b,
    own_c,
    there_a,
    there_b,
    there_c,
    cum_near,
    cum_far,
    q_base,
    near_base,
    far_base,
    grad_ref,
    att_ref,
    log_ref,
    dqg_ref,
    near_ref,
    far_out,
    row_ref,
    near_col,
    far_col,
    keys,
    vals,
    far_ref,
):
    qg = (qg_a, qg_b, qg_c)
    kv_near = (near_a, near_b, near_c)
    far_own = (own_a, own_b, own_c)
    far_there = (there_a, there_b, there_c)
    rows = qg_a.shape[0]
    far_rows = own_a.shape[0]
    slots = heads // 2
    fill_keys(
        keys,
        flag,
        far_own,
        far_there,
        kv_near,
        cum_far,
        cum_near,
        far_base,
        near_base,
        far_rows,
        heads,
    )

    @pl.when(pl.program_id(0) == 0)
    def _():
        lane = lax.broadcasted_iota(jnp.int32, (far_rows + rows, LANES), 1)
        ones = (lane < 3).astype(F32).astype(BF)
        for s in range(slots):
            vals[s, :, LANES:] = ones

        @pl.when(flag[0] == 0)
        def _():
            for s in range(slots):
                vals[s, :far_rows, :LANES] = far_own[s][:, LANES:]

        @pl.when(flag[0] != 0)
        def _():
            for s in range(slots):
                vals[s, :far_rows, :LANES] = far_there[s][:, LANES:]

        far_ref[...] = jnp.zeros(far_ref.shape, F32)
        far_col[...] = jnp.zeros(far_col.shape, F32)

    for s in range(slots):
        vals[s, far_rows:, :LANES] = kv_near[s][:, LANES:]
    q_aug = (q_base[...].astype(F32) + split_pieces(cum_near[...] - log_ref[...], 0, heads)).astype(
        BF
    )
    visible = near_visible(rows)
    lane = lax.broadcasted_iota(jnp.int32, (rows, LANES), 1)
    row_total = jnp.zeros((rows, LANES), F32)
    col_total = jnp.zeros((rows, LANES), F32)
    for s in range(slots):
        cols = slice(s * LANES, (s + 1) * LANES)
        kcols = slice(2 * s * LANES, (2 * s + 1) * LANES)
        vcols = slice((2 * s + 1) * LANES, (2 * s + 2) * LANES)
        gate_sig = jax.nn.sigmoid(qg[s][:, LANES:].astype(F32))
        grad = grad_ref[:, cols].astype(F32)
        att = att_ref[:, cols]
        grad_att = (grad * gate_sig).astype(BF)
        dqg_ref[:, vcols] = (grad * att * gate_sig * (1.0 - gate_sig)).astype(BF)
        weighed = grad_att.astype(F32) * att
        dq_total = jnp.zeros((rows, LANES), F32)
        dk_near = jnp.zeros((rows, LANES), F32)
        dv_near = jnp.zeros((rows, LANES), F32)
        for half in range(2):
            h = 2 * s + half
            mine = half_lanes((rows, LANES), half)
            query = jnp.where(mine, qg[s][:, :LANES] * BF(HEAD_DIM**-0.5), BF(0))
            aug = jnp.where(head_lanes(q_aug.shape, h, heads), q_aug, BF(0))
            q_cat = jnp.concatenate([query, aug], axis=1)
            ga = jnp.where(mine, grad_att, BF(0))
            delta = -jnp.sum(jnp.where(mine, weighed, 0.0), axis=1, keepdims=True)
            high = delta.astype(BF).astype(F32)
            mid = (delta - high).astype(BF).astype(F32)
            low = delta - high - mid
            d_aug = jnp.where(
                lane == 0, high, jnp.where(lane == 1, mid, jnp.where(lane == 2, low, 0.0))
            ).astype(BF)
            ga_cat = jnp.concatenate([ga, d_aug], axis=1)
            for part in range(2):
                span = slice(0, far_rows) if part == 0 else slice(far_rows, far_rows + rows)
                prob = jnp.exp(nt_dot(keys[s, span], q_cat))
                if part == 1:
                    prob = jnp.where(visible, prob, 0.0)
                ds = (prob * nt_dot(vals[s, span], ga_cat)).astype(BF)
                dv = nn_dot(prob.astype(BF), ga)
                dk = nn_dot(ds, q_cat)
                dq = tn_dot(ds, keys[s, span])
                dq_total += jnp.where(mine, dq[:, :LANES], 0.0)
                row_total += jnp.where(lane == h, dq[:, LANES:], 0.0)
                if part == 0:
                    far_ref[:, kcols] += dk[:, :LANES]
                    far_ref[:, vcols] += dv
                    far_col[...] += dk[:, LANES:]
                else:
                    dk_near += dk[:, :LANES]
                    dv_near += dv
                    col_total += dk[:, LANES:]
        dqg_ref[:, kcols] = (dq_total * HEAD_DIM**-0.5).astype(BF)
        near_ref[:, kcols] = dk_near
        near_ref[:, vcols] = dv_near
    row_ref[...] = row_total
    near_col[...] = col_total

    @pl.when(pl.program_id(0) == pl.num_programs(0) - 1)
    def _():
        far_out[...] = far_ref[...].astype(BF)


def attend_back(
    flag,
    projects,
    kv_there,
    cum_near,
    cum_far,
    q_base,
    near_base,
    far_base,
    grad,
    att,
    logs,
    rows,
    heads,
):
    total = projects[0].shape[0]
    width = heads * HEAD_DIM
    steps = total // rows
    flops = 2 * total * (total + rows) * heads * 1152
    slot_specs, slot_values = slot_inputs(flag, projects, kv_there, rows)
    return pl.pallas_call(
        functools.partial(attend_back_kernel, heads),
        grid=(steps,),
        out_shape=(
            jax.ShapeDtypeStruct((total, 2 * width), BF),
            jax.ShapeDtypeStruct((total, 2 * width), F32),
            jax.ShapeDtypeStruct((total, 2 * width), BF),
            jax.ShapeDtypeStruct((total, LANES), F32),
            jax.ShapeDtypeStruct((total, LANES), F32),
            jax.ShapeDtypeStruct((total, LANES), F32),
        ),
        in_specs=slot_specs
        + cum_specs(rows, total)
        + [row_block(rows, width), row_block(rows, width), row_block(rows, LANES)],
        out_specs=(
            row_block(rows, 2 * width),
            row_block(rows, 2 * width),
            whole_block(total, 2 * width),
            row_block(rows, LANES),
            row_block(rows, LANES),
            whole_block(total, LANES),
        ),
        scratch_shapes=[
            pltpu.VMEM((heads // 2, total + rows, 2 * LANES), BF),
            pltpu.VMEM((heads // 2, total + rows, 2 * LANES), BF),
            pltpu.VMEM((total, 2 * width), F32),
        ],
        compiler_params=pltpu.CompilerParams(vmem_limit_bytes=60 << 20),
        cost_estimate=pl.CostEstimate(
            flops=flops, bytes_accessed=total * width * 40, transcendentals=total * total * heads
        ),
    )(*slot_values, cum_near, cum_far, q_base, near_base, far_base, grad, att, logs)


def full_norm(tokens, gain_vec):
    factor = lax.rsqrt(jnp.mean(tokens * tokens, axis=-1, keepdims=True) + epsilon)
    scaled = tokens * factor
    return factor, scaled, (scaled * gain_vec).astype(BF)


def full_norm_back(grad_normed, factor, scaled, gain_vec):
    e = grad_normed * gain_vec
    mean = jnp.mean(e * scaled, axis=-1, keepdims=True)
    return jnp.sum(grad_normed * scaled, axis=0), factor * (e - scaled * mean)


MESH_ID = pl.DeviceIdType.MESH


class Here:
    def __init__(self, ring):
        self.ring = ring
        self.at = {a: lax.axis_index(a) for a in AX}

    def other(self, axis):
        return {axis: 1 - self.at[axis]}

    def mid_home(self):
        return lax.rem(self.at["y"] + self.at["zl"], 2)

    def peer(self, k):
        dy, dz = self.ring.offsets[k]
        return {
            "y": lax.rem(self.at["y"] + dy, 2),
            "zl": lax.rem(self.at["zl"] + dz, self.ring.zl_count),
        }

    def group_to(self, flip):
        at = self.at
        return {"y": at["zh"], "c": at["x"] ^ flip, "x": at["y"], "zh": at["c"]}

    def group_from(self, flip):
        at = self.at
        return {"y": at["x"], "c": at["zh"], "x": at["c"] ^ flip, "zh": at["y"]}

    def group_away(self):
        at = self.at
        return ~((at["y"] == at["zh"]) & (at["y"] == at["x"]) & (at["y"] == at["c"]))

    def greet_group(self, targets):
        away = self.group_away()
        self.greet(
            targets + [self.group_to(1), self.group_from(1)],
            [(self.group_to(0), away), (self.group_from(0), away)],
        )

    def greet(self, targets, extra=()):
        barrier = pltpu.get_barrier_semaphore()
        for target in targets:
            pl.semaphore_signal(barrier, inc=1, device_id=target, device_id_type=MESH_ID)
        count = len(targets)
        for target, away in extra:
            @pl.when(away)
            def _():
                pl.semaphore_signal(barrier, inc=1, device_id=target, device_id_type=MESH_ID)

            count = count + away.astype(jnp.int32)
        pl.semaphore_wait(barrier, count)


def remote(src, dst, send_sem, recv_sem, target):
    return pltpu.make_async_remote_copy(
        src_ref=src,
        dst_ref=dst,
        send_sem=send_sem,
        recv_sem=recv_sem,
        device_id=target,
        device_id_type=MESH_ID,
    )


def last_kernel(
    ring,
    heads,
    dqg_in,
    near_in,
    far_in,
    row_in,
    near_col_in,
    far_col_in,
    weight_in,
    normed_in,
    gated_in,
    mixed_in,
    tokens_in,
    residual_in,
    hid_kept_in,
    hid_there_in,
    hid_z_in,
    down_kept_in,
    down_there_in,
    gain_ref,
    forget_w,
    sig_ref,
    hot_ref,
    error_ref,
    gain_two_ref,
    valid_ref,
    back_out,
    proj_out,
    gate_out,
    up_out,
    down_out,
    out_out,
    small_out,
    grads,
    near,
    far_own,
    far_land,
    row_sum,
    near_col,
    far_col,
    far_col_land,
    cum,
    tot_send,
    tot_land,
    weight,
    normed,
    gated,
    mixed,
    tokens,
    residual,
    rs_send,
    rs_land,
    total,
    c_send,
    c_land,
    cf_send,
    cf_land,
    kept,
    x_send,
    x_land,
    z_send,
    z_land,
    final,
    kept_f,
    xf_send,
    xf_land,
    zf_send,
    zf_land,
    final_f,
    yf_land,
    full_f,
    co_send,
    co_land,
    kept_h,
    there_h,
    z_h,
    final_h,
    kept_d,
    there_d,
    zd_send,
    zd_land,
    final_d,
    kept_o,
    xo_send,
    xo_land,
    zo_send,
    zo_land,
    final_o,
    blocks,
    gain_sum,
    gain_nat,
    gain_land,
    load_sem,
    local_sem,
    swap_send_sem,
    swap_recv_sem,
    y_send_sem,
    y_recv_sem,
    c2_send_sem,
    c2_recv_sem,
    rs_send_sem,
    rs_recv_sem,
    c_send_sem,
    c_recv_sem,
    x_send_sem,
    x_recv_sem,
    z_send_sem,
    z_recv_sem,
    back_send_sem,
    back_recv_sem,
    gain_send_sem,
    gain_recv_sem,
):
    here = Here(ring)
    y, c, x, zh, zl = (here.at[a] for a in ("y", "c", "x", "zh", "zl"))
    local, features = tokens.shape
    rows_all = normed.shape[0]
    part = features // 4
    slot_w = 4 * LANES
    slots = heads // 2
    all_w = slots * slot_w
    units = down_kept_in.shape[0] // 2
    owner = zh == here.mid_home()
    peers = len(ring.offsets)
    away = here.group_away()
    all_loads = [
        (row_in, row_sum),
        (near_col_in, near_col),
        (far_col_in, far_col),
        (far_in, far_own),
        (near_in, near),
    ]
    for s in range(slots):
        all_loads.append(
            (
                dqg_in.at[:, 2 * s * LANES : 2 * (s + 1) * LANES],
                grads.at[:, s * slot_w : s * slot_w + 2 * LANES],
            )
        )
    all_loads += [
        (hid_kept_in.at[:, : 2 * units], kept_h),
        (hid_there_in.at[:, : 2 * units], there_h),
        (hid_z_in, z_h),
        (down_kept_in, kept_d),
        (down_there_in, there_d),
        (normed_in, normed),
        (weight_in, weight),
        (gated_in, gated),
        (mixed_in, mixed),
        (tokens_in, tokens),
        (residual_in, residual),
    ]
    loads = [
        pltpu.make_async_copy(a, b, load_sem.at[i]) for i, (a, b) in enumerate(all_loads)
    ]
    first_loads = 11 + slots
    for copy in loads[:first_loads]:
        copy.start()
    load_row, load_near_col, load_far_col, load_far, load_near = loads[:5]
    load_dqg = loads[5 : 5 + slots]
    load_hid = loads[5 + slots : 8 + slots]
    load_kept_d, load_there_d = loads[8 + slots : 10 + slots]
    load_normed, load_weight, load_gated, load_mixed, load_tokens, load_residual = loads[10 + slots :]

    here.greet_group(
        [here.peer(k) for k in range(1, peers)]
        + [here.other("c"), here.other("x"), here.other("zh")]
    )
    far_swap = remote(
        far_in, far_land, swap_send_sem.at[0], swap_recv_sem.at[0], here.other("c")
    )
    far_swap.start()
    col_swap = remote(
        far_col_in, far_col_land, swap_send_sem.at[1], swap_recv_sem.at[1], here.other("c")
    )
    col_swap.start()

    row0 = pl.multiple_of(c * part, part)

    def rows_of(ref, col, width):
        return ref.at[pl.ds(row0, part), pl.ds(pl.multiple_of(col, LANES), width)]

    def cols_of(ref, row, height):
        return ref.at[pl.ds(pl.multiple_of(row, LANES), height), pl.ds(row0, part)]

    def y_copy(i, src, dst):
        return remote(src, dst, y_send_sem.at[i], y_recv_sem.at[i], here.other("y"))

    pieces = [
        (final_h.at[0], rows_of(gate_out, y * units, units)),
        (final_h.at[1], rows_of(up_out, y * units, units)),
        (final_d, cols_of(down_out, y * units, units)),
    ]
    own_pieces = [
        pltpu.make_async_copy(src, dst, local_sem.at[i]) for i, (src, dst) in enumerate(pieces)
    ]
    y_pieces = [y_copy(i, src, dst) for i, (src, dst) in enumerate(pieces)]
    for copy in load_hid:
        copy.wait()
    for i in range(2):
        cols = slice(i * units, (i + 1) * units)
        final_h[i] = (
            kept_h[:, cols] + there_h[:, cols].astype(F32) + z_h[:, cols].astype(F32)
        ).astype(BF)
    for copy in own_pieces[:2] + y_pieces[:2]:
        copy.start()

    lane = lax.broadcasted_iota(jnp.int32, (CLEN, LANES), 1)
    head_lane = lane < heads
    all_units = rows_all // CLEN
    chunk_units = local // CLEN

    def unit_rows(u):
        return slice(u * CLEN, (u + 1) * CLEN)

    load_row.wait()
    load_near_col.wait()
    for u in range(all_units):
        value = row_sum[unit_rows(u), :] - pltpu.roll(
            near_col[unit_rows(u), :], LANES - FAR_PIECE, 1
        )
        value = jnp.where(head_lane, value, 0.0)
        cum[unit_rows(u), :] = value
        tot_send[u : u + 1, :] = jnp.sum(value, axis=0, keepdims=True)
    tot_swap = remote(
        tot_send.at[:all_units],
        tot_land.at[:all_units],
        swap_send_sem.at[2],
        swap_recv_sem.at[2],
        here.other("c"),
    )
    tot_swap.start()

    load_kept_d.wait()
    load_there_d.wait()
    zd_send[...] = (kept_d[units:, :] + there_d[units:, :].astype(F32)).astype(BF)
    zd_copy = remote(zd_send, zd_land, z_send_sem.at[5], z_recv_sem.at[5], here.other("zh"))
    zd_copy.start()

    load_far.wait()
    load_near.wait()
    for copy in load_dqg:
        copy.wait()
    for copy in loads[first_loads:]:
        copy.start()
    far_swap.wait_recv()
    on_prompt = jnp.where(c == 0, 1.0, 0.0)

    def merge(i, carry):
        rows = pl.ds(pl.multiple_of(i * CLEN, CLEN), CLEN)
        value = near[rows, :] + on_prompt * (
            far_own[rows, :].astype(F32) + far_land[rows, :].astype(F32)
        )
        value = value.astype(BF)
        for s in range(slots):
            grads[rows, s * slot_w + 2 * LANES : (s + 1) * slot_w] = value[
                :, 2 * s * LANES : 2 * (s + 1) * LANES
            ]
        return carry

    lax.fori_loop(0, all_units, merge, 0)
    load_normed.wait()
    tile_r = LANES
    per_part = part // tile_r

    def weight_tile(first, i):
        cols = pl.ds(pl.multiple_of(first + i * tile_r, LANES), tile_r)
        return tn_dot(normed[:, cols], grads[:, :all_w])

    def forget_tile(first, i):
        cols = pl.ds(pl.multiple_of(first + i * tile_r, LANES), tile_r)
        return tn_dot(normed[:, cols], grads[:, all_w:])

    def c_step(i, carry):
        rows = pl.ds(pl.multiple_of(i * tile_r, tile_r), tile_r)
        c_send[rows, :] = weight_tile(2 * part, i).astype(BF)
        return carry

    lax.fori_loop(0, 2 * per_part, c_step, 0)
    c_copy = remote(c_send, c_land, c_send_sem.at[0], c_recv_sem.at[0], here.other("c"))
    c_copy.start()

    load_far_col.wait()
    col_swap.wait_recv()
    tot_swap.wait_recv()

    @pl.when(c == 0)
    def _():
        for u in range(all_units):
            both = far_col[unit_rows(u), :] + far_col_land[unit_rows(u), :]
            value = cum[unit_rows(u), :] - jnp.where(
                head_lane, pltpu.roll(both, LANES - FAR_PIECE, 1), 0.0
            )
            for j in range(all_units):
                value = value + hot_ref[unit_rows(u), j : j + 1] * tot_land[j : j + 1, :]
            cum[unit_rows(u), :] = value

    step_row = lax.broadcasted_iota(jnp.int32, (CLEN, CLEN), 0)
    step_col = lax.broadcasted_iota(jnp.int32, (CLEN, CLEN), 1)
    tri_back = (step_col >= step_row).astype(F32)
    for u in range(all_units):
        value = jnp.dot(
            tri_back,
            cum[unit_rows(u), :],
            precision=highest,
            preferred_element_type=F32,
        )
        cum[unit_rows(u), :] = value
        tot_send[all_units + u : all_units + u + 1, :] = value[0:1, :]
    places = []
    for dy, dz in ring.offsets:
        place = lax.rem(y + 2 - dy, 2) * ring.zl_count + lax.rem(
            zl + ring.zl_count - dz, ring.zl_count
        )
        for i in range(chunk_units):
            places.append(place * chunk_units + i)
    bias = jnp.zeros((1, LANES), F32)
    for u in range(all_units):
        suffix = jnp.zeros((1, LANES), F32)
        for other in range(all_units):
            if other != u:
                seen = jnp.where((places[other] > places[u]) & (c == 0), 1.0, 0.0)
                suffix = suffix + seen * tot_send[all_units + other : all_units + other + 1, :]
        value = (cum[unit_rows(u), :] + suffix) * sig_ref[unit_rows(u), :]
        grads[unit_rows(u), all_w:] = value.astype(BF)
        bias = bias + jnp.sum(value, axis=0, keepdims=True)

    zd_copy.wait_recv()
    final_d[...] = (
        kept_d[:units, :] + there_d[:units, :].astype(F32) + zd_land[...].astype(F32)
    ).astype(BF)
    for copy in own_pieces[2:] + y_pieces[2:]:
        copy.start()

    c_copy.wait_recv()

    def x_step(i, carry):
        rows = pl.ds(pl.multiple_of(i * tile_r, tile_r), tile_r)
        land = pl.ds(pl.multiple_of(part + i * tile_r, tile_r), tile_r)
        value = weight_tile(part, i) + c_land[land, :].astype(F32)
        for s in range(slots):
            x_send[s, rows, :] = value[:, s * slot_w : (s + 1) * slot_w].astype(BF)
        return carry

    lax.fori_loop(0, per_part, x_step, 0)
    x_copies = {}
    for s in (2, 1, 0):
        x_copies[s] = remote(
            x_send.at[s], x_land.at[s], x_send_sem.at[s], x_recv_sem.at[s], here.other("x")
        )
        x_copies[s].start()
    load_weight.wait()
    tiles = 3
    tile_w = features // tiles

    def partial_rows(chunk_no, store):
        rows = slice(chunk_no * local, (chunk_no + 1) * local)

        def step(i, carry):
            cols = pl.ds(pl.multiple_of(i * tile_w, LANES), tile_w)
            value = nn_dot(grads[rows, all_w:], forget_w[:, cols])
            for s in range(slots):
                value = value + nt_dot(
                    grads[rows, s * slot_w : (s + 1) * slot_w], weight[s, cols, :]
                )
            store(cols, value)
            return carry

        lax.fori_loop(0, tiles, step, 0)

    moves = RingRows(here, local)

    def rs_copy(i):
        return moves.sum_copy(rs_send, rs_land, rs_send_sem, rs_recv_sem, i)

    for k in (3, 1, 2):

        def store_out(cols, value, k=k):
            rs_send[k - 1, :, cols] = value.astype(BF)

        partial_rows(k, store_out)
        for i in SUM_STARTS[k]:
            rs_copy(i).start()

    def cf_step(i, carry):
        rows = pl.ds(pl.multiple_of(i * tile_r, tile_r), tile_r)
        cf_send[rows, :] = forget_tile(2 * part, i).astype(BF)
        return carry

    lax.fori_loop(0, 2 * per_part, cf_step, 0)
    cf_copy = remote(cf_send, cf_land, c_send_sem.at[2], c_recv_sem.at[2], here.other("c"))
    cf_copy.start()

    load_gated.wait()
    load_mixed.wait()
    out_rows = slots * LANES

    def out_tile(s, cols):
        return tn_dot(gated[:, s * LANES : (s + 1) * LANES], mixed[:, cols])

    for s in range(slots):
        co_send[s * LANES : (s + 1) * LANES, :] = out_tile(
            s, slice(2 * part, features)
        ).astype(BF)
    co_copy = remote(co_send, co_land, c_send_sem.at[1], c_recv_sem.at[1], here.other("c"))
    co_copy.start()

    cf_copy.wait_recv()

    def xf_step(i, carry):
        rows = pl.ds(pl.multiple_of(i * tile_r, tile_r), tile_r)
        land = pl.ds(pl.multiple_of(part + i * tile_r, tile_r), tile_r)
        xf_send[rows, :] = (forget_tile(part, i) + cf_land[land, :].astype(F32)).astype(BF)
        return carry

    lax.fori_loop(0, per_part, xf_step, 0)
    xf_copy = remote(xf_send, xf_land, x_send_sem.at[3], x_recv_sem.at[3], here.other("x"))
    xf_copy.start()
    co_copy.wait_recv()
    for s in range(slots):
        rows = slice(s * LANES, (s + 1) * LANES)
        xo_send[rows, :] = (
            out_tile(s, slice(part, 2 * part)) + co_land[rows, part:].astype(F32)
        ).astype(BF)
    xo_copy = remote(xo_send, xo_land, x_send_sem.at[4], x_recv_sem.at[4], here.other("x"))
    xo_copy.start()

    def own_step(i, carry):
        rows = pl.ds(pl.multiple_of(i * tile_r, tile_r), tile_r)
        value = weight_tile(0, i) + c_land[rows, :].astype(F32)
        for s in range(slots):
            kept[s, rows, :] = value[:, s * slot_w : (s + 1) * slot_w]
        kept_f[rows, :] = forget_tile(0, i) + cf_land[rows, :].astype(F32)
        return carry

    lax.fori_loop(0, per_part, own_step, 0)
    for s in range(slots):
        rows = slice(s * LANES, (s + 1) * LANES)
        kept_o[rows, :] = out_tile(s, slice(0, part)) + co_land[rows, :part].astype(F32)

    def store_own(cols, value):
        total[:, cols] = value

    partial_rows(0, store_own)

    def z_copy(i, src, dst):
        return remote(src, dst, z_send_sem.at[i], z_recv_sem.at[i], here.other("zh"))

    z_first = z_copy(0, z_send.at[0], z_land.at[0])
    z_mid = z_copy(1, z_send.at[1], z_land.at[1])
    z_forget = z_copy(2, zf_send, zf_land)
    zo_first = z_copy(3, zo_send.at[0], zo_land.at[0])
    zo_mid = z_copy(4, zo_send.at[1], zo_land.at[1])
    moves.hand_on(rs_send, rs_land, rs_send_sem, rs_recv_sem)
    x_copies[2].wait_recv()
    z_send[0] = (kept[2] + x_land[2].astype(F32)).astype(BF)
    z_first.start()
    x_copies[1].wait_recv()

    @pl.when(~owner)
    def _():
        z_send[1] = (kept[1] + x_land[1].astype(F32)).astype(BF)
        z_mid.start()


    load_tokens.wait()
    load_residual.wait()
    for i in (0, 2, 4, 5):
        rs_copy(i).wait_recv()
    gain_sum[...] = jnp.zeros(gain_sum.shape, F32)
    tile_n = 32

    def norm_step(i, carry):
        rows = pl.ds(pl.multiple_of(i * tile_n, tile_n), tile_n)
        tok = tokens[rows, :].astype(F32)
        grad = total[rows, :]
        for k in (0, 2):
            grad = grad + rs_land[k, rows, :].astype(F32)
        factor = lax.rsqrt(jnp.mean(tok * tok, axis=-1, keepdims=True) + epsilon)
        scaled_tok = tok * factor
        e = grad * gain_ref[...]
        mean = jnp.mean(e * scaled_tok, axis=-1, keepdims=True)
        out = factor * (e - scaled_tok * mean) + residual[rows, :]
        weighed = jnp.sum(grad * scaled_tok, axis=0, keepdims=True)
        for b in range(4):
            blocks[b, rows, :] = out[:, b * part : (b + 1) * part].astype(BF)
            gain_sum[b, 0:1, :] += weighed[:, b * part : (b + 1) * part]
        return carry

    lax.fori_loop(0, local // tile_n, norm_step, 0)

    def block_no(half, low_high):
        return (half ^ x) + 2 * (low_high ^ c)

    def back_copy(flip, p):
        return remote(
            blocks.at[block_no(c ^ flip, p)],
            back_out.at[c, :, p * part : (p + 1) * part],
            back_send_sem.at[flip, p],
            back_recv_sem.at[flip, p],
            here.group_from(flip),
        )

    def back_own(flip, p):
        return pltpu.make_async_copy(
            blocks.at[block_no(c ^ flip, p)],
            back_out.at[c, :, p * part : (p + 1) * part],
            local_sem.at[5 + p],
        )

    for p in range(2):
        back_copy(1, p).start()

    @pl.when(away)
    def _():
        for p in range(2):
            back_copy(0, p).start()

    @pl.when(~away)
    def _():
        for p in range(2):
            back_own(0, p).start()

    for b in range(4):
        gain_sum[b, 1:2, :] = gain_two_ref[0:1, b * part : (b + 1) * part]
    for b in range(4):
        gain_nat[0, b] = gain_sum[block_no(b // 2, b % 2)]
    wide_lane = lax.broadcasted_iota(jnp.int32, (1, part), 1)
    scalars = jnp.where(
        wide_lane == 0, jnp.sum(error_ref[0:1, :], axis=1, keepdims=True), 0.0
    ) + jnp.where(wide_lane == 1, jnp.sum(valid_ref[...], axis=0, keepdims=True), 0.0)
    small_lane = lax.broadcasted_iota(jnp.int32, (1, LANES), 1)
    for j in range(heads):
        if j < 2:
            quarter, head = zh, 4 * y + j
        elif j < 4:
            quarter, head = here.mid_home(), j
        else:
            quarter, head = 1 - zh, 4 * y + j - 4
        dest = 2 + (quarter * ring.zl_count + zl) * heads + head
        value = jnp.sum(jnp.where(small_lane == j, bias, 0.0), axis=1, keepdims=True)
        scalars = scalars + jnp.where(wide_lane == dest, value, 0.0)
    gain_nat[0, 0, 2:3, :] = scalars
    gain_axes = ("c", "y", "x", "zl", "zh")

    def gain_step(place):
        return remote(
            gain_nat.at[place],
            gain_land.at[place],
            gain_send_sem.at[place],
            gain_recv_sem.at[place],
            here.other(gain_axes[place]),
        )

    def gain_next(place):
        gain_step(place).wait_recv()
        gain_nat[place + 1] = gain_nat[place] + gain_land[place]
        if place < 4:
            gain_step(place + 1).start()

    gain_step(0).start()

    x_copies[0].wait_recv()
    kept[0] += x_land[0].astype(F32)
    gain_next(0)
    xf_copy.wait_recv()
    kept_f[...] += xf_land[...].astype(F32)
    zf_send[...] = kept_f[...].astype(BF)
    z_forget.start()
    xo_copy.wait_recv()
    kept_o[...] += xo_land[...].astype(F32)
    gain_next(1)
    zo_send[0] = kept_o[2 * LANES :, :].astype(BF)
    zo_first.start()

    @pl.when(~owner)
    def _():
        zo_send[1] = kept_o[LANES : 2 * LANES, :].astype(BF)
        zo_mid.start()

    first_dst = rows_of(proj_out, 2 * y * slot_w, slot_w)
    mid_dst = rows_of(proj_out, slot_w, slot_w)
    out_first_dst = cols_of(out_out, 2 * LANES * y, LANES)
    out_mid_dst = cols_of(out_out, LANES, LANES)
    y_first = y_copy(3, final.at[0], first_dst)
    y_mid = y_copy(4, final.at[1], mid_dst)
    y_forget = y_copy(5, final_f, yf_land)
    yo_first = y_copy(6, final_o.at[0], out_first_dst)
    yo_mid = y_copy(7, final_o.at[1], out_mid_dst)
    own_first = pltpu.make_async_copy(final.at[0], first_dst, local_sem.at[8])
    own_mid = pltpu.make_async_copy(final.at[1], mid_dst, local_sem.at[9])
    own_out_first = pltpu.make_async_copy(final_o.at[0], out_first_dst, local_sem.at[10])
    own_out_mid = pltpu.make_async_copy(final_o.at[1], out_mid_dst, local_sem.at[11])
    own_forget = pltpu.make_async_copy(
        full_f, proj_out.at[pl.ds(row0, part), all_w : all_w + LANES], local_sem.at[12]
    )
    z_first.wait_recv()
    final[0] = (kept[0] + z_land[0].astype(F32)).astype(BF)
    y_first.start()
    own_first.start()

    @pl.when(owner)
    def _():
        z_mid.wait_recv()
        final[1] = (kept[1] + x_land[1].astype(F32) + z_land[1].astype(F32)).astype(BF)
        y_mid.start()
        own_mid.start()

    gain_next(2)
    z_forget.wait_recv()
    f_lane = lax.broadcasted_iota(jnp.int32, (part, LANES), 1)
    there_f = zf_land[...].astype(F32)
    edge = jnp.where(f_lane < 2, kept_f[...] + pltpu.roll(there_f, LANES - 4, 1), 0.0)
    edge = jnp.where(y == 0, edge, pltpu.roll(edge, 4, 1))
    mid_f = jnp.where((f_lane >= 2) & (f_lane < 4) & owner, kept_f[...] + there_f, 0.0)
    final_f[...] = (edge + mid_f).astype(BF)
    y_forget.start()
    gain_next(3)
    zo_first.wait_recv()
    final_o[0] = (kept_o[:LANES, :] + zo_land[0].astype(F32)).astype(BF)
    yo_first.start()
    own_out_first.start()

    @pl.when(owner)
    def _():
        zo_mid.wait_recv()
        final_o[1] = (kept_o[LANES : 2 * LANES, :] + zo_land[1].astype(F32)).astype(BF)
        yo_mid.start()
        own_out_mid.start()

    for copy in own_pieces:
        copy.wait()
    for copy in y_pieces:
        copy.wait_recv()
    c2 = []

    def hand_over(i, view):
        copy = remote(view, view, c2_send_sem.at[i], c2_recv_sem.at[i], here.other("c"))
        copy.start()
        c2.append(copy)

    hand_over(0, gate_out.at[pl.ds(row0, part), :])
    hand_over(1, up_out.at[pl.ds(row0, part), :])
    hand_over(2, down_out.at[:, pl.ds(row0, part)])

    gain_next(4)
    gain_copy = pltpu.make_async_copy(gain_nat.at[5], small_out, local_sem.at[7])
    gain_copy.start()
    y_forget.wait_recv()
    full_f[...] = final_f[...] + yf_land[...]
    own_forget.start()
    own_first.wait()
    y_first.wait_recv()
    own_out_first.wait()
    yo_first.wait_recv()
    own_forget.wait()

    @pl.when(owner)
    def _():
        own_mid.wait()
        own_out_mid.wait()

    @pl.when(~owner)
    def _():
        y_mid.wait_recv()
        yo_mid.wait_recv()

    hand_over(3, out_out.at[:, pl.ds(row0, part)])
    hand_over(4, proj_out.at[pl.ds(row0, part), :])

    for copy in c2:
        copy.wait()
    for p in range(2):
        back_copy(1, p).wait()

    @pl.when(away)
    def _():
        for p in range(2):
            back_copy(0, p).wait()

    @pl.when(~away)
    def _():
        for p in range(2):
            back_own(0, p).wait()

    gain_copy.wait()
    for i in range(5):
        gain_step(i).wait_send()
    for i in range(6):
        rs_copy(i).wait_send()
    for copy in [c_copy, cf_copy, co_copy, x_copies[0], x_copies[1], x_copies[2], xf_copy, xo_copy]:
        copy.wait_send()
    for copy in [far_swap, col_swap, tot_swap, z_first, z_forget, zo_first, zd_copy]:
        copy.wait_send()
    for copy in y_pieces + [y_first, y_forget, yo_first]:
        copy.wait_send()

    @pl.when(owner)
    def _():
        y_mid.wait_send()
        yo_mid.wait_send()

    @pl.when(~owner)
    def _():
        z_mid.wait_send()
        zo_mid.wait_send()


def last_step(ring, heads, large, small):
    near = large[1]
    rows = near.shape[0]
    weight, normed, gated = large[6:9]
    tokens = large[10]
    units = large[15].shape[0] // 2
    local, features = tokens.shape
    part = features // 4
    half = features // 2
    peers = len(ring.offsets)
    slot_w = 4 * LANES
    slots = heads // 2
    all_w = slots * slot_w
    any_spec = pl.BlockSpec(memory_space=pl.ANY)
    dma = pltpu.SemaphoreType.DMA
    vmem = pltpu.VMEM
    return pl.pallas_call(
        functools.partial(last_kernel, ring, heads),
        out_shape=(
            jax.ShapeDtypeStruct((2, local, half), BF),
            jax.ShapeDtypeStruct((half, all_w + LANES), BF),
            jax.ShapeDtypeStruct((half, 2 * units), BF),
            jax.ShapeDtypeStruct((half, 2 * units), BF),
            jax.ShapeDtypeStruct((2 * units, half), BF),
            jax.ShapeDtypeStruct((slots * LANES, half), BF),
            jax.ShapeDtypeStruct((4, 8, part), F32),
        ),
        in_specs=[any_spec] * len(large) + [pl.BlockSpec(memory_space=vmem)] * len(small),
        out_specs=[any_spec] * 7,
        scratch_shapes=[
            vmem((rows, all_w + LANES), BF),
            vmem(near.shape, F32),
            vmem(near.shape, BF),
            vmem(near.shape, BF),
            vmem((rows, LANES), F32),
            vmem((rows, LANES), F32),
            vmem((rows, LANES), F32),
            vmem((rows, LANES), F32),
            vmem((rows, LANES), F32),
            vmem((2 * (rows // CLEN), LANES), F32),
            vmem((2 * (rows // CLEN), LANES), F32),
            vmem(weight.shape, BF),
            vmem(normed.shape, BF),
            vmem(gated.shape, BF),
            vmem(normed.shape, BF),
            vmem(tokens.shape, BF),
            vmem(tokens.shape, F32),
            vmem((peers - 1, local, features), BF),
            vmem((peers - 1, local, features), BF),
            vmem((local, features), F32),
            vmem((half, all_w), BF),
            vmem((half, all_w), BF),
            vmem((half, LANES), BF),
            vmem((half, LANES), BF),
            vmem((slots, part, slot_w), F32),
            vmem((slots, part, slot_w), BF),
            vmem((slots, part, slot_w), BF),
            vmem((2, part, slot_w), BF),
            vmem((2, part, slot_w), BF),
            vmem((2, part, slot_w), BF),
            vmem((part, LANES), F32),
            vmem((part, LANES), BF),
            vmem((part, LANES), BF),
            vmem((part, LANES), BF),
            vmem((part, LANES), BF),
            vmem((part, LANES), BF),
            vmem((part, LANES), BF),
            vmem((part, LANES), BF),
            vmem((slots * LANES, half), BF),
            vmem((slots * LANES, half), BF),
            vmem((part, 2 * units), F32),
            vmem((part, 2 * units), BF),
            vmem((part, 2 * units), BF),
            vmem((2, part, units), BF),
            vmem((2 * units, part), F32),
            vmem((2 * units, part), BF),
            vmem((units, part), BF),
            vmem((units, part), BF),
            vmem((units, part), BF),
            vmem((slots * LANES, part), F32),
            vmem((slots * LANES, part), BF),
            vmem((slots * LANES, part), BF),
            vmem((2, LANES, part), BF),
            vmem((2, LANES, part), BF),
            vmem((2, LANES, part), BF),
            vmem((4, local, part), BF),
            vmem((4, 8, part), F32),
            vmem((6, 4, 8, part), F32),
            vmem((5, 4, 8, part), F32),
            dma((16 + slots,)),
            dma((13,)),
            dma((3,)),
            dma((3,)),
            dma((8,)),
            dma((8,)),
            dma((5,)),
            dma((5,)),
            dma((6,)),
            dma((6,)),
            dma((3,)),
            dma((3,)),
            dma((5,)),
            dma((5,)),
            dma((6,)),
            dma((6,)),
            dma((2, 2)),
            dma((2, 2)),
            dma((5,)),
            dma((5,)),
        ],
        compiler_params=pltpu.CompilerParams(
            collective_id=1, has_side_effects=True, vmem_limit_bytes=63 << 20
        ),
        cost_estimate=pl.CostEstimate(
            flops=4 * rows * features * all_w, bytes_accessed=40 << 20, transcendentals=0
        ),
    )(*large, *small)


def scale_kernel(
    full,
    sums,
    back,
    proj,
    gate,
    up,
    down,
    out,
    prompt_o,
    cont_o,
    query_o,
    outgate_o,
    key_o,
    value_o,
    gate_o,
    up_o,
    down_o,
    out_o,
):
    factor = full / sums[0, 2:3, 1:2]
    prompt_o[...] = back[0].astype(F32) * factor
    cont_o[...] = back[1].astype(F32) * factor
    for i, ref in enumerate((query_o, outgate_o, key_o, value_o)):
        for s in range(3):
            at = (4 * s + i) * LANES
            ref[:, s * LANES : (s + 1) * LANES] = proj[:, at : at + LANES].astype(F32) * factor
    gate_o[...] = gate[...].astype(F32) * factor
    up_o[...] = up[...].astype(F32) * factor
    down_o[...] = down[...].astype(F32) * factor
    out_o[...] = out[...].astype(F32) * factor


def scale_step(full, sums, back, proj, gate, up, down, out):
    steps = 8

    def cut(shape):
        return row_block(shape[0] // steps, shape[1])

    local, half = back.shape[1:]
    width = out.shape[0]
    shapes = [(local, half)] * 2 + [(half, width)] * 4 + [gate.shape, up.shape, down.shape, out.shape]
    return pl.pallas_call(
        functools.partial(scale_kernel, full),
        grid=(steps,),
        out_shape=tuple(jax.ShapeDtypeStruct(v, F32) for v in shapes),
        in_specs=[
            pl.BlockSpec(sums.shape, lambda i: (0, 0, 0)),
            pl.BlockSpec((2, local // steps, half), lambda i: (0, i, 0)),
        ]
        + [cut(v.shape) for v in (proj, gate, up, down, out)],
        out_specs=tuple(cut(v) for v in shapes),
        compiler_params=pltpu.CompilerParams(vmem_limit_bytes=62 << 20),
    )(sums, back, proj, gate, up, down, out)


def middle_kernel(
    ring,
    gated_in,
    w_out_in,
    w_gate_in,
    w_up_in,
    hid_there_in,
    w_down_in,
    tokens_in,
    teach_prompt_in,
    teach_cont_in,
    valid_ref,
    gain_ref,
    gated_grad,
    residual_grad,
    mixed_grads,
    hid_kept,
    hid_there,
    down_kept,
    down_there,
    error_ref,
    gain_grad,
    gated,
    w_out,
    w_hidden,
    w_down,
    tokens,
    teacher,
    mixed,
    total,
    result_grad,
    normed,
    hidden,
    gate_up,
    result_all,
    mixed_all,
    rs_send,
    rs_land,
    c_down_send,
    c_down_land,
    c_hid_send,
    c_hid_land,
    x_down_send,
    x_hid_send,
    down_sum,
    hid_sum,
    gg_stage,
    load_sem,
    wx_send,
    wx_recv,
    wc_send,
    wc_recv,
    wz_send,
    wz_recv,
    group_send,
    group_recv,
    out_sem,
    rs_send_sem,
    rs_recv_sem,
    ag_send_sem,
    ag_recv_sem,
    c_send_sem,
    c_recv_sem,
    x_send_sem,
    x_recv_sem,
):
    here = Here(ring)
    local, features = tokens.shape
    rows_all = gated.shape[0]
    width = gated.shape[1]
    units = hidden.shape[1]
    half_units = units // 2
    part = features // 4
    peers = len(ring.offsets)
    y, c, x = (here.at[a] for a in ("y", "c", "x"))
    gate_view, up_view = (
        w.at[
            pl.ds(pl.multiple_of(c * part, part), part),
            pl.ds(pl.multiple_of(y * half_units, half_units), half_units),
        ]
        for w in (w_gate_in, w_up_in)
    )
    down_view = w_down_in.at[
        pl.ds(pl.multiple_of(y * half_units, half_units), half_units),
        pl.ds(pl.multiple_of(c * part, part), part),
    ]

    loads = [
        pltpu.make_async_copy(a, b, load_sem.at[i])
        for i, (a, b) in enumerate(
            (
                (gate_view, w_hidden.at[0:part, 0:half_units]),
                (up_view, w_hidden.at[0:part, half_units:units]),
                (hid_there_in, w_hidden.at[0:part, units:]),
                (gated_in, gated),
                (w_out_in, w_out),
                (tokens_in, tokens),
                (down_view, w_down.at[0:half_units, 0:part]),
            )
        )
    ]
    for copy in loads:
        copy.start()
    here.greet_group(
        [here.peer(k) for k in range(1, peers)]
        + [here.other("c"), here.other("x"), here.other("zh")]
    )

    z_down = remote(
        down_view, w_down.at[half_units:, 0:part], wz_send.at[0], wz_recv.at[0], here.other("zh")
    )
    z_down.start()

    def hid_x_copy(i):
        cols = slice(i * half_units, (i + 1) * half_units) if i < 2 else slice(units, 2 * units)
        return remote(
            w_hidden.at[0:part, cols],
            w_hidden.at[part : 2 * part, cols],
            wx_send.at[i],
            wx_recv.at[i],
            here.other("x"),
        )

    def hid_c_copy(i):
        cols = slice(i * half_units, (i + 1) * half_units) if i < 2 else slice(units, 2 * units)
        return remote(
            w_hidden.at[0 : 2 * part, cols],
            w_hidden.at[2 * part :, cols],
            wc_send.at[i],
            wc_recv.at[i],
            here.other("c"),
        )

    for i in range(3):
        loads[i].wait()
        hid_x_copy(i).start()

    def teach_copies(flip, rows_in, remote_copy):
        kind = x ^ flip
        out = []
        for p in range(2):
            block = (x ^ y) + 2 * (kind ^ p)
            dst = teacher.at[:, pl.ds(pl.multiple_of(block * part, part), part)]
            src = rows_in.at[:, p * part : (p + 1) * part]
            if remote_copy:
                out.append(
                    remote(
                        src, dst, group_send.at[flip, p], group_recv.at[flip, p], here.group_to(flip)
                    )
                )
            else:
                out.append(pltpu.make_async_copy(src, dst, load_sem.at[7 + p]))
        return out

    away = here.group_away()

    def on_teacher(flip, here_too, what):
        for kind, rows_in in ((0, teach_prompt_in), (1, teach_cont_in)):
            mine = (x ^ flip) == kind
            if flip == 1:

                @pl.when(mine)
                def _():
                    for copy in teach_copies(1, rows_in, True):
                        what(copy)

            else:

                @pl.when(mine & away)
                def _():
                    for copy in teach_copies(0, rows_in, True):
                        what(copy)

                if here_too:

                    @pl.when(mine & ~away)
                    def _():
                        for copy in teach_copies(0, rows_in, False):
                            what(copy)

    def teacher_arrival(flip):
        for p in range(2):
            remote(
                teach_prompt_in.at[:, p * part : (p + 1) * part],
                teacher.at[:, p * part : (p + 1) * part],
                group_send.at[flip, p],
                group_recv.at[flip, p],
                here.group_to(flip),
            ).wait_recv()

    def chunk(k):
        return slice(k * local, (k + 1) * local)

    def tiled(count, size, step):
        def body(i, carry):
            step(pl.ds(pl.multiple_of(i * size, size), size))
            return carry

        lax.fori_loop(0, count, body, 0)

    moves = RingRows(here, local)

    def rs_copy(phase, i):
        return moves.sum_copy(rs_send, rs_land, rs_send_sem.at[phase], rs_recv_sem.at[phase], i)

    def ag_copy(phase, buffer, i):
        return moves.gather_copy(buffer, ag_send_sem.at[phase], ag_recv_sem.at[phase], i)

    wide = 512
    wide_count = features // wide

    def send_partial(phase, k, left, right, transposed):
        def step(cols):
            if transposed:
                value = nt_dot(left, right[cols, :])
            else:
                value = nn_dot(left, right[:, cols])
            if k == 0:
                total[:, cols] = value
            else:
                rs_send[k - 1, :, cols] = value.astype(BF)

        if k != 0 and phase > 0:
            for i in SUM_READS[k]:
                rs_copy(phase - 1, i).wait_send()
        tiled(wide_count, wide, step)
        if k != 0:
            for i in SUM_STARTS[k]:
                rs_copy(phase, i).start()

    def hand_on(phase):
        moves.hand_on(rs_send, rs_land, rs_send_sem.at[phase], rs_recv_sem.at[phase])

    def sums_arrived(phase):
        for i in (0, 2, 4, 5):
            rs_copy(phase, i).wait_recv()

    def half_tiles(phase, buffer, step):
        for half in range(2):

            def body(i, carry):
                step(pl.ds(pl.multiple_of(half * (local // 2) + i * 32, 32), 32))
                return carry

            lax.fori_loop(0, local // 64, body, 0)
            ag_copy(phase, buffer, half).start()
            ag_copy(phase, buffer, 2 + half).start()

    def pass_on(phase, buffer):
        ag_copy(phase, buffer, 2).wait_recv()
        ag_copy(phase, buffer, 4).start()
        ag_copy(phase, buffer, 1).wait_recv()
        ag_copy(phase, buffer, 5).start()

    def rows_arrived(phase, buffer, k):
        for i in {1: (0,), 2: (3,), 3: (4, 5)}[k]:
            ag_copy(phase, buffer, i).wait_recv()

    def summed(rows):
        return total[rows, :] + rs_land[0, rows, :].astype(F32) + rs_land[2, rows, :].astype(F32)

    loads[3].wait()
    loads[4].wait()
    for k in (3, 1, 2, 0):
        send_partial(0, k, gated[chunk(k), :], w_out, False)
    loads[5].wait()
    loads[6].wait()
    z_down.wait_recv()
    down_x_copy = remote(
        w_down.at[:, 0:part],
        w_down.at[:, part : 2 * part],
        wx_send.at[4],
        wx_recv.at[4],
        here.other("x"),
    )
    down_x_copy.start()
    hand_on(0)
    sums_arrived(0)

    def second_norm(rows):
        value = tokens[rows, :].astype(F32) + summed(rows)
        mixed[rows, :] = value
        factor = lax.rsqrt(jnp.mean(value * value, axis=-1, keepdims=True) + epsilon)
        normed[rows, :] = (value * factor * gain_ref[...]).astype(BF)

    half_tiles(0, normed, second_norm)

    for i in range(3):
        hid_x_copy(i).wait_recv()
        hid_c_copy(i).start()
    for f in range(2):
        on_teacher(f, True, lambda copy: copy.start())
    for i in range(3):
        hid_c_copy(i).wait_recv()
    tile_u = 256
    per_half = half_units // tile_u

    def forward_chunk(k):
        left = normed[chunk(k), :]

        def step(i, carry):
            half = i // per_half
            sub = lax.rem(i, per_half)
            gate_at = pl.multiple_of(half * units + sub * tile_u, tile_u)
            up_at = pl.multiple_of(half * units + half_units + sub * tile_u, tile_u)
            gate = nn_dot(left, w_hidden[:, pl.ds(gate_at, tile_u)])
            up = nn_dot(left, w_hidden[:, pl.ds(up_at, tile_u)])
            gate_up[chunk(k), pl.ds(gate_at, tile_u)] = gate.astype(BF)
            gate_up[chunk(k), pl.ds(up_at, tile_u)] = up.astype(BF)
            hidden[chunk(k), pl.ds(pl.multiple_of(i * tile_u, tile_u), tile_u)] = (
                gate * jax.nn.sigmoid(gate) * up
            ).astype(BF)
            return carry

        lax.fori_loop(0, 2 * per_half, step, 0)

    def forward_sum(k):
        send_partial(1, k, hidden[chunk(k), :], w_down, False)

    forward_chunk(0)
    pass_on(0, normed)
    down_x_copy.wait_recv()
    down_c_copy = remote(
        w_down.at[:, 0 : 2 * part],
        w_down.at[:, 2 * part :],
        wc_send.at[4],
        wc_recv.at[4],
        here.other("c"),
    )
    down_c_copy.start()
    for k in range(1, peers):
        rows_arrived(0, normed, k)
        forward_chunk(k)
        if k == 1:
            down_c_copy.wait_recv()
        forward_sum(k)
    forward_sum(0)
    hand_on(1)
    teacher_arrival(1)

    @pl.when(away)
    def _():
        teacher_arrival(0)

    @pl.when(~away)
    def _():
        for kind, rows_in in ((0, teach_prompt_in), (1, teach_cont_in)):

            @pl.when(x == kind)
            def _():
                for copy in teach_copies(0, rows_in, False):
                    copy.wait()

    sums_arrived(1)
    error_ref[...] = jnp.zeros(error_ref.shape, F32)
    gain_grad[...] = jnp.zeros(gain_grad.shape, F32)

    def loss_rows(rows):
        deviation = mixed[rows, :] + summed(rows) - teacher[rows, :].astype(F32)
        grad = valid_ref[rows, :] * deviation
        result_grad[rows, :] = grad
        result_all[rows, :] = grad.astype(BF)
        error_ref[0:1, :] += 0.5 * jnp.sum(grad * deviation, axis=0, keepdims=True)

    half_tiles(1, result_all, loss_rows)

    def backward_chunk(k):
        left = result_all[chunk(k), :]

        def step(i, carry):
            half = i // per_half
            sub = lax.rem(i, per_half)
            gate_at = pl.multiple_of(half * units + sub * tile_u, tile_u)
            up_at = pl.multiple_of(half * units + half_units + sub * tile_u, tile_u)
            grad = nt_dot(left, w_down[pl.ds(pl.multiple_of(i * tile_u, tile_u), tile_u), :])
            gate = gate_up[chunk(k), pl.ds(gate_at, tile_u)].astype(F32)
            up = gate_up[chunk(k), pl.ds(up_at, tile_u)].astype(F32)
            sig = jax.nn.sigmoid(gate)
            gate_up[chunk(k), pl.ds(gate_at, tile_u)] = (
                grad * up * sig * (1.0 + gate * (1.0 - sig))
            ).astype(BF)
            gate_up[chunk(k), pl.ds(up_at, tile_u)] = (grad * gate * sig).astype(BF)
            return carry

        lax.fori_loop(0, 2 * per_half, step, 0)

    def backward_sum(k):
        send_partial(2, k, gate_up[chunk(k), :], w_hidden, True)

    backward_chunk(0)
    pass_on(1, result_all)
    for k in range(1, peers):
        rows_arrived(1, result_all, k)
        backward_chunk(k)
        backward_sum(k)

    unit_tile = 256

    def down_tile(units_at, cols):
        return tn_dot(hidden[:, units_at], result_all[:, cols])

    feature_tile = 128

    def hid_tile(first, at):
        cols = pl.ds(pl.multiple_of(first + at.start, feature_tile), feature_tile)
        return tn_dot(normed[:, cols], gate_up[...])

    def hid_c(at):
        c_hid_send[at, :] = hid_tile(2 * part, at).astype(BF)

    tiled(2 * part // feature_tile, feature_tile, hid_c)
    c_hid = remote(c_hid_send, c_hid_land, c_send_sem.at[1], c_recv_sem.at[1], here.other("c"))
    c_hid.start()
    hand_on(2)
    backward_sum(0)

    def down_c(units_at):
        c_down_send[units_at, :] = down_tile(units_at, slice(2 * part, features)).astype(BF)

    tiled(units // unit_tile, unit_tile, down_c)
    c_down = remote(c_down_send, c_down_land, c_send_sem.at[0], c_recv_sem.at[0], here.other("c"))
    c_down.start()
    c_hid.wait_recv()

    def hid_x(at):
        land = pl.ds(pl.multiple_of(part + at.start, feature_tile), feature_tile)
        x_hid_send[at, :] = (hid_tile(part, at) + c_hid_land[land, :].astype(F32)).astype(BF)

    tiled(part // feature_tile, feature_tile, hid_x)
    x_hid = remote(x_hid_send, hid_there, x_send_sem.at[1], x_recv_sem.at[1], here.other("x"))
    x_hid.start()

    sums_arrived(2)

    def norm_back(rows):
        value = mixed[rows, :]
        factor = lax.rsqrt(jnp.mean(value * value, axis=-1, keepdims=True) + epsilon)
        scaled_rows = value * factor
        grad = summed(rows)
        e = grad * gain_ref[...]
        mean = jnp.mean(e * scaled_rows, axis=-1, keepdims=True)
        out = result_grad[rows, :] + factor * (e - scaled_rows * mean)
        result_grad[rows, :] = out
        mixed_all[rows, :] = out.astype(BF)
        gain_grad[0:1, :] += jnp.sum(grad * scaled_rows, axis=0, keepdims=True)

    half_tiles(2, mixed_all, norm_back)
    residual_copy = pltpu.make_async_copy(result_grad, residual_grad, out_sem.at[0])
    residual_copy.start()

    def gated_chunk(k):
        gg_stage[chunk(k), :] = nt_dot(mixed_all[chunk(k), :], w_out[...])

    gated_chunk(0)
    c_down.wait_recv()

    def down_x(units_at):
        value = down_tile(units_at, slice(part, 2 * part))
        x_down_send[units_at, :] = (value + c_down_land[units_at, part:].astype(F32)).astype(BF)

    tiled(units // unit_tile, unit_tile, down_x)
    pass_on(2, mixed_all)

    def down_own(units_at):
        value = down_tile(units_at, slice(0, part))
        down_sum[units_at, :] = value + c_down_land[units_at, :part].astype(F32)

    tiled(units // unit_tile, unit_tile, down_own)

    def hid_own(at):
        hid_sum[at, :] = hid_tile(0, at) + c_hid_land[at, :].astype(F32)

    tiled(part // feature_tile, feature_tile, hid_own)
    sums_out = [
        pltpu.make_async_copy(down_sum, down_kept, out_sem.at[1]),
        pltpu.make_async_copy(hid_sum, hid_kept, out_sem.at[2]),
        pltpu.make_async_copy(x_down_send, down_there, out_sem.at[5]),
    ]
    for copy in sums_out:
        copy.start()
    for k in range(1, peers):
        rows_arrived(2, mixed_all, k)
        gated_chunk(k)
    finals = [
        pltpu.make_async_copy(gg_stage, gated_grad, out_sem.at[3]),
        pltpu.make_async_copy(mixed_all, mixed_grads, out_sem.at[4]),
    ]
    for copy in finals:
        copy.start()
    for i in range(6):
        rs_copy(2, i).wait_send()
        for phase, buffer in enumerate((normed, result_all, mixed_all)):
            ag_copy(phase, buffer, i).wait_send()
    c_down.wait_send()
    c_hid.wait_send()
    z_down.wait_send()
    for i in range(3):
        hid_x_copy(i).wait_send()
        hid_c_copy(i).wait_send()
    for f in range(2):
        on_teacher(f, False, lambda copy: copy.wait_send())
    down_x_copy.wait_send()
    down_c_copy.wait_send()
    x_hid.wait()
    residual_copy.wait()
    for copy in sums_out + finals:
        copy.wait()


def middle_step(
    ring,
    gated,
    w_out,
    w_gate,
    w_up,
    hid_there,
    w_down,
    tokens,
    teach_prompt,
    teach_cont,
    valid,
    gain,
):
    rows, width = gated.shape
    local, features = tokens.shape
    units = w_down.shape[0]
    part = features // 4
    peers = len(ring.offsets)
    any_spec = pl.BlockSpec(memory_space=pl.ANY)
    vmem_spec = pl.BlockSpec(memory_space=pltpu.VMEM)
    dma = pltpu.SemaphoreType.DMA
    return pl.pallas_call(
        functools.partial(middle_kernel, ring),
        out_shape=(
            jax.ShapeDtypeStruct((rows, width), F32),
            jax.ShapeDtypeStruct((local, features), F32),
            jax.ShapeDtypeStruct((rows, features), BF),
            jax.ShapeDtypeStruct((part, 2 * units), F32),
            jax.ShapeDtypeStruct((part, 2 * units), BF),
            jax.ShapeDtypeStruct((units, part), F32),
            jax.ShapeDtypeStruct((units, part), BF),
            jax.ShapeDtypeStruct((8, features), F32),
            jax.ShapeDtypeStruct((8, features), F32),
        ),
        in_specs=[any_spec] * 9 + [vmem_spec] * 2,
        out_specs=[any_spec] * 7 + [vmem_spec] * 2,
        scratch_shapes=[
            pltpu.VMEM(gated.shape, BF),
            pltpu.VMEM(w_out.shape, BF),
            pltpu.VMEM((features, 2 * units), BF),
            pltpu.VMEM((units, features), BF),
            pltpu.VMEM(tokens.shape, BF),
            pltpu.VMEM(tokens.shape, BF),
            pltpu.VMEM(tokens.shape, F32),
            pltpu.VMEM(tokens.shape, F32),
            pltpu.VMEM(tokens.shape, F32),
            pltpu.VMEM((rows, features), BF),
            pltpu.VMEM((rows, units), BF),
            pltpu.VMEM((rows, 2 * units), BF),
            pltpu.VMEM((rows, features), BF),
            pltpu.VMEM((rows, features), BF),
            pltpu.VMEM((peers - 1, local, features), BF),
            pltpu.VMEM((peers - 1, local, features), BF),
            pltpu.VMEM((units, 2 * part), BF),
            pltpu.VMEM((units, 2 * part), BF),
            pltpu.VMEM((2 * part, 2 * units), BF),
            pltpu.VMEM((2 * part, 2 * units), BF),
            pltpu.VMEM((units, part), BF),
            pltpu.VMEM((part, 2 * units), BF),
            pltpu.VMEM((units, part), F32),
            pltpu.VMEM((part, 2 * units), F32),
            pltpu.VMEM((rows, width), F32),
            dma((9,)),
            dma((5,)),
            dma((5,)),
            dma((5,)),
            dma((5,)),
            dma((2,)),
            dma((2,)),
            dma((2, 2)),
            dma((2, 2)),
            dma((6,)),
            dma((3, 6)),
            dma((3, 6)),
            dma((3, 6)),
            dma((3, 6)),
            dma((2,)),
            dma((2,)),
            dma((2,)),
            dma((2,)),
        ],
        compiler_params=pltpu.CompilerParams(
            collective_id=2, has_side_effects=True, vmem_limit_bytes=63 << 20
        ),
        cost_estimate=pl.CostEstimate(
            flops=6 * rows * features * (3 * units + width),
            bytes_accessed=60 << 20,
            transcendentals=0,
        ),
    )(
        gated,
        w_out,
        w_gate,
        w_up,
        hid_there,
        w_down,
        tokens,
        teach_prompt,
        teach_cont,
        valid,
        gain,
    )


class RingRows:
    def __init__(self, here, local):
        self.zl, self.y = here.peer(1), here.peer(2)
        self.local = local
        self.half = local // 2

    def rows(self, place, half=None):
        base = place * self.local
        if half is None:
            return slice(base, base + self.local)
        return slice(base + half * self.half, base + (half + 1) * self.half)

    def gather_copy(self, buffer, sends, recvs, i):
        source, target, place, half = (
            (0, self.zl, 1, 0),
            (0, self.zl, 1, 1),
            (0, self.y, 2, 0),
            (0, self.y, 2, 1),
            (2, self.zl, 3, 0),
            (1, self.y, 3, 1),
        )[i]
        return remote(
            buffer.at[self.rows(source, half)],
            buffer.at[self.rows(place, half)],
            sends.at[i],
            recvs.at[i],
            target,
        )

    def sum_copy(self, send, land, sends, recvs, i):
        chunk, half, target, slot = (
            (0, 0, self.zl, 0),
            (2, 0, self.zl, 1),
            (1, 1, self.y, 0),
            (2, 1, self.y, 1),
            (1, 0, self.y, 2),
            (0, 1, self.zl, 2),
        )[i]
        return remote(
            send.at[chunk, self.rows(0, half)],
            land.at[slot, self.rows(0, half)],
            sends.at[i],
            recvs.at[i],
            target,
        )

    def hand_on(self, send, land, sends, recvs):
        for chunk, half, got, i in ((1, 0, 1, 4), (0, 1, 3, 5)):
            self.sum_copy(send, land, sends, recvs, got).wait_recv()
            rows = self.rows(0, half)
            send[chunk, rows, :] = (
                send[chunk, rows, :].astype(F32) + land[1, rows, :].astype(F32)
            ).astype(BF)
            self.sum_copy(send, land, sends, recvs, i).start()


SUM_STARTS = {1: (0,), 2: (2,), 3: (1, 3)}
SUM_READS = {1: (0, 5), 2: (2, 4), 3: (1, 3)}


def first_kernel(
    ring,
    prompt_in,
    cont_in,
    small_in,
    ints_in,
    wq_in,
    wg_in,
    wk_in,
    wv_in,
    w_out_in,
    tokens_out,
    normed_out,
    slots_out,
    w_out_all,
    small_out,
    gains_out,
    forget_w_out,
    ints_out,
    proj_a,
    proj_b,
    proj_c,
    forget_own,
    there_a,
    there_b,
    there_c,
    forget_there,
    tokens,
    normed,
    slot_w,
    project,
    forget,
    small,
    small_x,
    feats,
    forget_f,
    forget_w,
    group_send,
    group_recv,
    ints_send,
    ints_recv,
    small_send,
    small_recv,
    own_sem,
    z_send,
    z_recv,
    x_send,
    x_recv,
    c_send,
    c_recv,
    ag_send,
    ag_recv,
    kv_send,
    kv_recv,
    out_sem,
):
    here = Here(ring)
    y, c, x, zh = (here.at[a] for a in ("y", "c", "x", "zh"))
    local, features = tokens.shape
    part = features // 4
    half = features // 2
    peers = len(ring.offsets)
    owner = zh == here.mid_home()
    row0 = pl.multiple_of(c * part, part)
    first0 = pl.multiple_of(2 * LANES * y, LANES)
    sources = (wq_in, wg_in, wk_in, wv_in)

    here.greet_group([here.peer(k) for k in range(1, peers)] + [here.other(a) for a in "cx"] + [here.other("zh")])

    def group_copies(flip, rows_in, remote_copy):
        kind = x ^ flip
        out = []
        for p in range(2):
            block = (x ^ y) + 2 * (kind ^ p)
            dst = tokens.at[:, pl.ds(pl.multiple_of(block * part, part), part)]
            src = rows_in.at[:, p * part : (p + 1) * part]
            if remote_copy:
                out.append(
                    remote(
                        src, dst, group_send.at[flip, p], group_recv.at[flip, p], here.group_to(flip)
                    )
                )
            else:
                out.append(pltpu.make_async_copy(src, dst, own_sem.at[12 + p]))
        return out

    def ints_copy():
        return remote(ints_in, ints_out, ints_send, ints_recv, here.group_to(0))

    def ints_own():
        return pltpu.make_async_copy(ints_in, ints_out, own_sem.at[14])

    away = here.group_away()

    def on_group(flip, what):
        for kind, rows_in in ((0, prompt_in), (1, cont_in)):
            mine = (x ^ flip) == kind
            if flip == 1:

                @pl.when(mine)
                def _():
                    for copy in group_copies(flip, rows_in, True):
                        what(copy)

            else:

                @pl.when(mine & away)
                def _():
                    for copy in group_copies(flip, rows_in, True):
                        what(copy)

                @pl.when(mine & ~away)
                def _():
                    for copy in group_copies(flip, rows_in, False):
                        what(copy)

    for f in range(2):
        on_group(f, lambda copy: copy.start())

    @pl.when(away)
    def _():
        ints_copy().start()

    @pl.when(~away)
    def _():
        ints_own().start()

    def z_piece(i, s):
        start = first0 if s == 2 else LANES
        return remote(
            sources[i].at[pl.ds(row0, part), pl.ds(start, LANES)],
            slot_w.at[s, 0:part, i * LANES : (i + 1) * LANES],
            z_send.at[s, i],
            z_recv.at[s, i],
            here.other("zh"),
        )

    own_small = pltpu.make_async_copy(small_in, small.at[0], own_sem.at[15])
    own_small.start()
    small_z = remote(small_in, small.at[1], small_send.at[0], small_recv.at[0], here.other("zh"))
    small_z.start()

    def own_piece(i, s):
        start = first0 if s == 0 else LANES
        return pltpu.make_async_copy(
            sources[i].at[pl.ds(row0, part), pl.ds(start, LANES)],
            slot_w.at[s, 0:part, i * LANES : (i + 1) * LANES],
            own_sem.at[4 * s + i],
        )

    for i in range(4):
        own_piece(i, 0).start()

    @pl.when(owner)
    def _():
        for i in range(4):
            own_piece(i, 1).start()

    own_out = [
        pltpu.make_async_copy(
            w_out_in.at[pl.ds(first0, LANES), pl.ds(row0, part)],
            w_out_all.at[0:LANES, 0:part],
            own_sem.at[8],
        ),
        pltpu.make_async_copy(
            w_out_in.at[LANES : 2 * LANES, pl.ds(row0, part)],
            w_out_all.at[LANES : 2 * LANES, 0:part],
            own_sem.at[9],
        ),
    ]
    own_out[0].start()

    @pl.when(owner)
    def _():
        own_out[1].start()

    own_small.wait()
    small_z.wait_recv()
    small_over_x = remote(small, small_x, small_send.at[1], small_recv.at[1], here.other("x"))
    small_over_x.start()

    def x_copy(s):
        return remote(
            slot_w.at[s, 0:part],
            slot_w.at[s, part : 2 * part],
            x_send.at[s],
            x_recv.at[s],
            here.other("x"),
        )

    def c_copy(s):
        return remote(
            slot_w.at[s, 0:half],
            slot_w.at[s, half:features],
            c_send.at[s],
            c_recv.at[s],
            here.other("c"),
        )

    for i in range(4):
        own_piece(i, 0).wait()
    x_copy(0).start()
    small_over_x.wait_recv()
    for z in range(2):
        for place in range(2):
            at = pl.multiple_of((c ^ place) * part, part)
            feats[z, :, 2 * place * part : (2 * place + 1) * part] = small[z, :, pl.ds(at, part)]
            feats[z, :, (2 * place + 1) * part : (2 * place + 2) * part] = small_x[
                z, :, pl.ds(at, part)
            ]
    forget_f[...] = jnp.zeros(forget_f.shape, F32)
    for z, rows in ((0, slice(0, 2)), (1, slice(4, 6))):
        forget_f[rows, :] = jnp.where(y == 0, feats[z, 8:10, :], feats[z, 12:14, :])
    forget_f[2:4, :] = jnp.where(owner, feats[0, 10:12, :], feats[1, 10:12, :])
    forget_w[...] = jnp.zeros(forget_w.shape, BF)
    forget_w[0:16, :] = forget_f[...].astype(BF)

    def group_arrival(flip):
        for p in range(2):
            remote(
                prompt_in.at[:, p * part : (p + 1) * part],
                tokens.at[:, p * part : (p + 1) * part],
                group_send.at[flip, p],
                group_recv.at[flip, p],
                here.group_to(flip),
            ).wait_recv()

    group_arrival(1)

    @pl.when(away)
    def _():
        group_arrival(0)

    @pl.when(~away)
    def _():
        for kind, rows_in in ((0, prompt_in), (1, cont_in)):

            @pl.when(x == kind)
            def _():
                for copy in group_copies(0, rows_in, False):
                    copy.wait()

    for i in range(4):
        z_piece(i, 2).start()

    z_out = [
        remote(
            w_out_in.at[pl.ds(first0, LANES), pl.ds(row0, part)],
            w_out_all.at[2 * LANES : 3 * LANES, 0:part],
            z_send.at[0, 0],
            z_recv.at[0, 0],
            here.other("zh"),
        ),
        remote(
            w_out_in.at[LANES : 2 * LANES, pl.ds(row0, part)],
            w_out_all.at[LANES : 2 * LANES, 0:part],
            z_send.at[0, 1],
            z_recv.at[0, 1],
            here.other("zh"),
        ),
    ]
    z_out[0].start()

    @pl.when(owner)
    def _():
        z_out[1].start()

    moves = RingRows(here, local)

    def ag_copy(i):
        return moves.gather_copy(normed, ag_send, ag_recv, i)

    def norm_rows(i, carry):
        rows = pl.ds(pl.multiple_of(i * 32, 32), 32)
        value = tokens[rows, :].astype(F32)
        factor = lax.rsqrt(jnp.mean(value * value, axis=-1, keepdims=True) + epsilon)
        normed[rows, :] = (value * factor * feats[0, 0:1, :]).astype(BF)
        return carry

    for place in range(2):
        lax.fori_loop(place * (local // 64), (place + 1) * (local // 64), norm_rows, 0)
        ag_copy(place).start()
        ag_copy(2 + place).start()

    outs = [
        pltpu.make_async_copy(tokens, tokens_out, out_sem.at[0]),
        pltpu.make_async_copy(small, small_out, out_sem.at[1]),
        pltpu.make_async_copy(feats.at[0], gains_out, out_sem.at[2]),
        pltpu.make_async_copy(forget_w, forget_w_out, out_sem.at[3]),
    ]
    for copy in outs:
        copy.start()

    x_copy(0).wait_recv()
    c_copy(0).start()
    for i in range(4):
        z_piece(i, 2).wait_recv()
    @pl.when(owner)
    def _():
        for i in range(4):
            z_piece(i, 1).start()

    x_copy(2).start()

    @pl.when(owner)
    def _():
        for i in range(4):
            own_piece(i, 1).wait()

    @pl.when(~owner)
    def _():
        for i in range(4):
            z_piece(i, 1).wait_recv()

    x_copy(1).start()

    projects = (proj_a, proj_b, proj_c)
    theres = (there_a, there_b, there_c)

    def chunk(k):
        return slice(k * local, (k + 1) * local)

    def kv_copy(k, s):
        return remote(
            project.at[s, chunk(k), 2 * LANES :],
            theres[s].at[chunk(k)],
            kv_send.at[k, s],
            kv_recv.at[k, s],
            here.other("c"),
        )

    def forget_copy(k):
        return remote(
            forget.at[chunk(k)],
            forget_there.at[chunk(k)],
            kv_send.at[k, 3],
            kv_recv.at[k, 3],
            here.other("c"),
        )

    def project_chunk(k, s):
        project[s, chunk(k), :] = nn_dot(normed[chunk(k), :], slot_w[s]).astype(BF)
        kv_copy(k, s).start()

    def forget_chunk(k):
        forget[chunk(k), :] = nt_dot(normed[chunk(k), :], forget_w[...]).astype(BF)
        forget_copy(k).start()

    c_copy(0).wait_recv()
    forget_chunk(0)
    project_chunk(0, 0)
    ag_copy(2).wait_recv()
    ag_copy(4).start()
    ag_copy(1).wait_recv()
    ag_copy(5).start()
    for k, arrivals in ((1, (0,)), (2, (3,)), (3, (4, 5))):
        for i in arrivals:
            ag_copy(i).wait_recv()
        forget_chunk(k)
        project_chunk(k, 0)
    normed_copy = pltpu.make_async_copy(normed, normed_out, out_sem.at[4])
    normed_copy.start()
    for s in (2, 1):
        x_copy(s).wait_recv()
        c_copy(s).start()
    own_out[0].wait()
    z_out[0].wait_recv()

    @pl.when(owner)
    def _():
        own_out[1].wait()

    @pl.when(~owner)
    def _():
        z_out[1].wait_recv()

    x_out = remote(
        w_out_all.at[:, 0:part],
        w_out_all.at[:, part : 2 * part],
        x_send.at[3],
        x_recv.at[3],
        here.other("x"),
    )
    x_out.start()
    for s in (2, 1):
        c_copy(s).wait_recv()
        for k in range(peers):
            project_chunk(k, s)
    slots_copy = pltpu.make_async_copy(slot_w, slots_out, out_sem.at[5])
    slots_copy.start()
    finals = [
        pltpu.make_async_copy(project.at[s], projects[s], out_sem.at[6 + s]) for s in range(3)
    ] + [pltpu.make_async_copy(forget, forget_own, out_sem.at[9])]
    for copy in finals:
        copy.start()
    x_out.wait_recv()
    c_out = remote(
        w_out_all.at[:, 0:half],
        w_out_all.at[:, half:features],
        c_send.at[3],
        c_recv.at[3],
        here.other("c"),
    )
    c_out.start()

    on_group(1, lambda copy: copy.wait_send())

    @pl.when(away)
    def _():
        ints_copy().wait()
        for kind, rows_in in ((0, prompt_in), (1, cont_in)):

            @pl.when(x == kind)
            def _():
                for copy in group_copies(0, rows_in, True):
                    copy.wait_send()

    @pl.when(~away)
    def _():
        ints_own().wait()

    small_z.wait_send()
    small_over_x.wait_send()
    for i in range(4):
        z_piece(i, 2).wait_send()
    z_out[0].wait_send()

    @pl.when(owner)
    def _():
        for i in range(4):
            z_piece(i, 1).wait_send()
        z_out[1].wait_send()

    for s in range(3):
        x_copy(s).wait_send()
        c_copy(s).wait_send()
    x_out.wait_send()
    for i in range(6):
        ag_copy(i).wait_send()
    for k in range(peers):
        for s in range(3):
            kv_copy(k, s).wait()
        forget_copy(k).wait()
    c_out.wait()
    for copy in outs + finals + [normed_copy, slots_copy]:
        copy.wait()


def first_step(ring, prompt, cont, small, ints, wq, wg, wk, wv, w_out):
    local, half = prompt.shape
    features = 2 * half
    part = half // 2
    peers = len(ring.offsets)
    rows = peers * local
    slot = 4 * LANES
    any_spec = pl.BlockSpec(memory_space=pl.ANY)
    dma = pltpu.SemaphoreType.DMA
    shapes = [
        ((local, features), BF),
        ((rows, features), BF),
        ((3, features, slot), BF),
        ((3 * LANES, features), BF),
        ((2, 16, half), F32),
        ((16, features), F32),
        ((LANES, features), BF),
        (ints.shape, jnp.int32),
        ((rows, slot), BF),
        ((rows, slot), BF),
        ((rows, slot), BF),
        ((rows, LANES), BF),
        ((rows, 2 * LANES), BF),
        ((rows, 2 * LANES), BF),
        ((rows, 2 * LANES), BF),
        ((rows, LANES), BF),
    ]
    return pl.pallas_call(
        functools.partial(first_kernel, ring),
        out_shape=tuple(jax.ShapeDtypeStruct(*s) for s in shapes),
        in_specs=[any_spec] * 9,
        out_specs=[any_spec] * len(shapes),
        scratch_shapes=[
            pltpu.VMEM((local, features), BF),
            pltpu.VMEM((rows, features), BF),
            pltpu.VMEM((3, features, slot), BF),
            pltpu.VMEM((3, rows, slot), BF),
            pltpu.VMEM((rows, LANES), BF),
            pltpu.VMEM((2, 16, half), F32),
            pltpu.VMEM((2, 16, half), F32),
            pltpu.VMEM((2, 16, features), F32),
            pltpu.VMEM((16, features), F32),
            pltpu.VMEM((LANES, features), BF),
            dma((2, 2)),
            dma((2, 2)),
            dma,
            dma,
            dma((2,)),
            dma((2,)),
            dma((16,)),
            dma((3, 4)),
            dma((3, 4)),
            dma((4,)),
            dma((4,)),
            dma((4,)),
            dma((4,)),
            dma((6,)),
            dma((6,)),
            dma((peers, 4)),
            dma((peers, 4)),
            dma((10,)),
        ],
        compiler_params=pltpu.CompilerParams(
            collective_id=3, has_side_effects=True, vmem_limit_bytes=62 << 20
        ),
        cost_estimate=pl.CostEstimate(
            flops=2 * rows * features * 3 * slot, bytes_accessed=40 << 20, transcendentals=0
        ),
    )(prompt, cont, small, ints, wq, wg, wk, wv, w_out)


def ring_body(
    ring,
    x_prompt,
    x_cont,
    teacher_prompt,
    teacher_cont,
    segment_ids,
    offsets,
    prompt_valid,
    cont_valid,
    first_gain,
    w_query,
    w_key,
    w_value,
    w_outgate,
    w_forget,
    forget_bias,
    w_out,
    second_gain,
    w_gate,
    w_up,
    w_down,
):
    y = lax.axis_index("y")
    c = lax.axis_index("c")
    x = lax.axis_index("x")
    zh = lax.axis_index("zh")
    zl = lax.axis_index("zl")
    zl_count = ring.zl_count
    local = x_prompt.shape[1]
    half_d = x_prompt.shape[2]
    part_d = half_d // 2
    local_conts = x_cont.shape[1]
    heads = w_forget.shape[1]
    units_here = w_gate.shape[1]
    half_units = units_here // 2
    width = heads * HEAD_DIM
    slots = heads // 2
    pair_unit = PROMPT // CLEN
    chunk_units = local // CLEN
    own_valid = jnp.where(x == 0, prompt_valid.reshape(-1), cont_valid.reshape(-1))
    small_in = jnp.concatenate([own_valid, segment_ids.reshape(-1), offsets.reshape(-1)])
    int_rows = 16
    ints = jnp.pad(small_in, (0, int_rows * LANES - small_in.shape[0])).reshape(int_rows, LANES)
    packed = jnp.concatenate(
        [
            first_gain[None].astype(F32),
            second_gain[None].astype(F32),
            jnp.pad(forget_bias, (0, half_d - heads))[None],
            jnp.zeros((5, half_d), F32),
            w_forget.T.astype(F32),
            jnp.zeros((8 - heads, half_d), F32),
        ],
        axis=0,
    )
    (
        tokens_b,
        normed_all,
        w_slots,
        w_out_all,
        small_all,
        gains,
        w_forget_rows,
        ints,
        proj_a,
        proj_b,
        proj_c,
        forget_own,
        there_a,
        there_b,
        there_c,
        forget_there,
    ) = first_step(
        ring,
        x_prompt[0],
        x_cont.reshape(local_conts * CLEN, half_d),
        packed,
        ints,
        w_query,
        w_outgate,
        w_key,
        w_value,
        w_out,
    )
    projects = [proj_a, proj_b, proj_c]
    kv_there = [there_a, there_b, there_c]
    ints = ints.reshape(-1)
    validity = ints[:local].astype(F32)
    segment_row = ints[local : local + PROMPT]
    offset_row = ints[local + PROMPT : local + PROMPT + CONTS]
    gain_one = gains[0]
    gain_two = gains[1]

    def head_slots(value):
        first = jnp.where(y == 0, value[:, 0:2], value[:, 4:6])
        slot_a = jnp.where(zh == 0, first[0], first[1])
        slot_c = jnp.where(zh == 0, first[1], first[0])
        slot_b = jnp.where((y + zl) % 2 == 0, value[0, 2:4], value[1, 2:4])
        return jnp.concatenate([slot_a, slot_b, slot_c], axis=0)

    bias_all = small_all[:, 2, :heads]
    bias_all = jnp.stack(
        [
            jnp.where(zh == 0, bias_all[0], bias_all[1]),
            jnp.where(zh == 0, bias_all[1], bias_all[0]),
        ]
    )
    bias_row = head_slots(bias_all[:, :, None])[:, 0]
    bias_row = jnp.concatenate([bias_row, jnp.zeros((LANES - heads,), F32)])[None]

    proj_a, w_gate_late, w_up_late = lax.optimization_barrier((proj_a, w_gate, w_up))
    projects[0] = proj_a
    hid_there_w = ring.swap(
        jnp.concatenate(
            [
                lax.dynamic_slice(w, (c * part_d, y * half_units), (part_d, half_units))
                for w in (w_gate_late, w_up_late)
            ],
            axis=1,
        ),
        "zh",
    )

    dy_all = jnp.array([o[0] for o in ring.offsets], jnp.int32)
    dz_all = jnp.array([o[1] for o in ring.offsets], jnp.int32)
    places = ((y - dy_all) % 2) * zl_count + (zl - dz_all) % zl_count
    unit_no = (places[:, None] * chunk_units + jnp.arange(chunk_units, dtype=jnp.int32)).reshape(-1)
    natural = jnp.arange(pair_unit, dtype=jnp.int32)
    pick = unit_no[:, None] == natural[None, :]
    step = jnp.arange(CLEN, dtype=jnp.int32)
    row_pos = (unit_no[:, None] * CLEN + step[None, :]).reshape(-1)
    seg_rel = jnp.sum(
        jnp.where(pick[:, :, None], segment_row.reshape(1, pair_unit, CLEN), 0), axis=1
    )
    offs_rel = jnp.sum(jnp.where(pick, offset_row[None, :], 0), axis=1)
    last_rel = jnp.sum(
        jnp.where(
            jnp.arange(PROMPT, dtype=jnp.int32)[None, :] == offs_rel[:, None] - 1,
            segment_row[None, :],
            0,
        ),
        axis=1,
    )
    limit = jnp.where(c == 0, unit_no * CLEN, offs_rel)
    doc_row = jnp.where(c == 0, seg_rel, last_rel[:, None]).reshape(-1, 1)
    seg_col = seg_rel.reshape(-1, 1)
    lane = jnp.arange(LANES, dtype=jnp.int32)[None, :]
    unit_col = jnp.repeat(natural, CLEN)[:, None]
    pieces = 3 * heads
    is_doc = (lane >= DOC_LANE) & (lane < DOC_LANE + 4)
    is_unit = (lane >= UNIT_LANE) & (lane < UNIT_LANE + pair_unit)
    limit_lane = jnp.pad(limit, (UNIT_LANE, LANES - UNIT_LANE - pair_unit))[None, :]
    q_base = jnp.where(
        (lane >= FAR_PIECE) & (lane < FAR_PIECE + pieces),
        1.0,
        jnp.where(
            (is_doc & (doc_row != lane - DOC_LANE)) | (is_unit & (unit_col == lane - UNIT_LANE)),
            -NEVER,
            0.0,
        ),
    ).astype(BF)
    near_base = jnp.where(
        (lane < pieces) | (is_doc & (doc_row == lane - DOC_LANE)), 1.0, 0.0
    ).astype(BF)
    far_base = jnp.where(
        (lane < pieces)
        | (is_doc & (seg_col == lane - DOC_LANE))
        | (is_unit & (row_pos[:, None] >= limit_lane)),
        1.0,
        0.0,
    ).astype(BF)
    tri = (step[:, None] >= step[None, :]).astype(F32)
    earlier = (unit_no[None, :] < unit_no[:, None]).astype(F32)
    hot = (row_pos[None, :] == limit[:, None] - 1).astype(F32)
    cont_hot = (row_pos[None, :] == offs_rel[:, None] - 1).astype(F32)

    forget_far = jnp.where(c == 0, forget_own, forget_there)
    flag = c.astype(jnp.int32).reshape(1)
    head_lane = lane < heads

    def keep_log(lin):
        return jnp.where(head_lane, jax.nn.log_sigmoid(lin.astype(F32) + bias_row), 0.0)

    def within(values, matrix):
        return jnp.einsum(
            "ts,ush->uth", matrix, values.reshape(pair_unit, CLEN, LANES), precision=highest
        )

    far_within = within(keep_log(forget_far), tri)
    far_prefix = jnp.dot(earlier, far_within[:, -1], precision=highest)
    cum_far = (far_within + far_prefix[:, None]).reshape(-1, LANES)
    own_base = jnp.dot(hot, cum_far, precision=highest)
    cum_near = (within(keep_log(forget_own), tri) + own_base[:, None]).reshape(-1, LANES)
    keep_slope = jnp.where(
        head_lane, jax.nn.sigmoid(-(forget_own.astype(F32) + bias_row)), 0.0
    )
    gated, attended, logs = attend(
        flag, projects, kv_there, cum_near, cum_far, q_base, near_base, far_base, local, heads
    )
    (
        grad_gated,
        grad_residual,
        grad_residual_all,
        hid_kept,
        hid_there,
        down_kept,
        down_there,
        error_rows,
        gain_two_rows,
    ) = middle_step(
        ring,
        gated,
        w_out_all,
        w_gate,
        w_up,
        hid_there_w,
        w_down,
        tokens_b,
        teacher_prompt[0],
        teacher_cont.reshape(local_conts * CLEN, half_d),
        validity[:, None],
        gain_two[None],
    )
    dqg, dkv_near, dkv_far, row_sum, near_sum, far_sum = attend_back(
        flag,
        projects,
        kv_there,
        cum_near,
        cum_far,
        q_base,
        near_base,
        far_base,
        grad_gated,
        attended,
        logs,
        local,
        heads,
    )

    edge = 2 * half_units
    hid_z = ring.swap((hid_kept[:, edge:] + hid_there[:, edge:].astype(F32)).astype(BF), "zh")
    down_there = ring.swap(down_there, "x")
    rows_back, proj_all, gate_all, up_all, down_all, out_all, small_sums = last_step(
        ring,
        heads,
        [
            dqg,
            dkv_near,
            dkv_far,
            row_sum,
            near_sum,
            far_sum,
            w_slots,
            normed_all,
            gated,
            grad_residual_all,
            tokens_b,
            grad_residual,
            hid_kept,
            hid_there,
            hid_z,
            down_kept,
            down_there,
        ],
        [
            gain_one[None],
            w_forget_rows,
            keep_slope,
            cont_hot.T,
            error_rows,
            gain_two_rows,
            validity[:, None],
        ],
    )
    gain_one_sum = small_sums[:, 0].reshape(-1)
    gain_two_sum = small_sums[:, 1].reshape(-1)
    sums = small_sums[0, 2]
    forget_grad = proj_all[:, 4 * width : 4 * width + heads]
    error_total = sums[0]
    count_total = sums[1]
    groups = ring.sizes["yo"] * ring.sizes["y"] * ring.sizes["c"]
    grad_scale = groups * (PROMPT + CONTS * CLEN) / count_total
    loss_value = error_total / (D * count_total)
    (
        prompt_grad,
        cont_grad,
        query_grad,
        outgate_grad,
        key_grad,
        value_grad,
        gate_grad,
        up_grad,
        down_grad,
        out_grad,
    ) = scale_step(
        float(groups * (PROMPT + CONTS * CLEN)),
        small_sums,
        rows_back,
        proj_all,
        gate_all,
        up_all,
        down_all,
        out_all,
    )

    def own_half(value):
        return lax.dynamic_slice_in_dim(value, x * half_d, half_d, value.ndim - 1)

    quarter_no = zh * zl_count + zl
    bias_out = lax.dynamic_slice_in_dim(sums, 2 + quarter_no * heads, heads, 0)

    def scaled(value):
        return value.astype(F32) * grad_scale

    return (
        loss_value,
        prompt_grad[None],
        cont_grad.reshape(1, local_conts, CLEN, half_d),
        scaled(own_half(gain_one_sum)),
        query_grad,
        key_grad,
        value_grad,
        outgate_grad,
        scaled(forget_grad),
        scaled(bias_out),
        out_grad,
        scaled(own_half(gain_two_sum)),
        gate_grad,
        up_grad,
        down_grad,
    )


def specs(dp, row, col):
    in_specs = (
        P(dp, col, row),
        P(dp, col, None, row),
        P(dp, col, row),
        P(dp, col, None, row),
        P(dp, None),
        P(dp, None),
        P(dp, col),
        P(dp, col, None),
        P(row),
        P(row, col),
        P(row, col),
        P(row, col),
        P(row, col),
        P(row, col),
        P(col),
        P(col, row),
        P(row),
        P(row, col),
        P(row, col),
        P(col, row),
    )
    out_specs = (
        P(),
        P(dp, col, row),
        P(dp, col, None, row),
        P(row),
        P(row, col),
        P(row, col),
        P(row, col),
        P(row, col),
        P(row, col),
        P(col),
        P(col, row),
        P(row),
        P(row, col),
        P(row, col),
        P(col, row),
    )
    return in_specs, out_specs


def solution(mesh):
    dp, row, col = mesh.shape["dp"], mesh.shape["row"], mesh.shape["col"]
    heads = HEADS // col
    if dp == 4 and row == 2 and col % 2 == 0 and heads == 6:
        sizes = {"yo": dp // 4, "y": 2, "c": 2, "x": 2, "zh": 2, "zl": col // 2}
        ring_mesh = Mesh(mesh.devices.reshape([sizes[a] for a in AX]), AX)
        in_specs, out_specs = specs(("yo", "y", "c"), "x", ("zh", "zl"))
        step = functools.partial(ring_body, Ring(sizes))
        return jax.shard_map(
            step, mesh=ring_mesh, in_specs=in_specs, out_specs=out_specs, check_vma=False
        )
    in_specs, out_specs = specs("dp", "row", "col")
    return jax.shard_map(
        wide_body, mesh=mesh, in_specs=in_specs, out_specs=out_specs, check_vma=False
    )
```
